32 devices in a mesh: dp: 8 (over z, y), tensor: 4 (over x, core).
Axes of the slice: x: 2, y: 2, z: 4, core: 2. Of those that a mesh axis runs over, the one named last changes fastest.
Arguments:
- tokens: bfloat16 [16384, 768], P('dp'), may hold values from -6 to 6
- first_gain: float32 [768], replicated, may hold values from 0.5 to 1.5
- first_bias: float32 [768], replicated, may hold values from -1.5 to 1.5
- query_weight: bfloat16 [768, 768], P(None, 'tensor'), may hold values from -0.21875 to 0.21875
- key_weight: bfloat16 [768, 768], P(None, 'tensor'), may hold values from -0.21875 to 0.21875
- value_weight: bfloat16 [768, 768], P(None, 'tensor'), may hold values from -0.21875 to 0.21875
- output_weight: bfloat16 [768, 768], P('tensor'), may hold values from -3.5 to 3.5
- second_gain: float32 [768], replicated, may hold values from 0.5 to 1.5
- second_bias: float32 [768], replicated, may hold values from -1.5 to 1.5
- expert_up: bfloat16 [8, 768, 3072], P('dp'), may hold values from -0.21875 to 0.21875
- expert_down: bfloat16 [8, 3072, 768], P('dp'), may hold values from -0.109375 to 0.109375
- item_lengths: int32 [8, 5], P('dp'), may hold values from 64 to 1024, as said below
- routes: int32 [16384, 1], P(('dp', 'tensor')), may hold values from 0 to 7
- slot_order: int32 [32, 512], P(('dp', 'tensor')), may hold values from 0 to 511, each once within a row
- cotangent: bfloat16 [16384, 768], P(('dp', 'tensor')), may hold values from -6 to 6
Outputs:
- block_out: float32 [16384, 768], P(('dp', 'tensor'))
- token_grad: float32 [16384, 768], P(('dp', 'tensor'))
- first_gain_grad: float32 [768], replicated
- first_bias_grad: float32 [768], replicated
- query_grad: float32 [768, 768], P(None, 'tensor')
- key_grad: float32 [768, 768], P(None, 'tensor')
- value_grad: float32 [768, 768], P(None, 'tensor')
- output_grad: float32 [768, 768], P('tensor')
- second_gain_grad: float32 [768], replicated
- second_bias_grad: float32 [768], replicated
- expert_up_grad: float32 [8, 768, 3072], P('dp', None, 'tensor')
- expert_down_grad: float32 [8, 3072, 768], P('dp', 'tensor')
The draws below stay inside these ranges and needn't reach their ends.
Inputs may be any that keep to these rules, and one draw needn't show every extreme that they name: `item_lengths`: each dp index holds 5 items laid end to end from its first slot, their lengths summing to at most 2048; its remaining slots are padding. In every draw some item has exactly 1024 slots and some exactly 64. Padding slots have routes too. `slot_order`: each row is a permutation of the numbers 0 to 511.
All inputs are finite; a program needn't handle non-finite values.
Results may differ from the reference program's by a relative error of at most 0.019.
Values may be sent and summed in bfloat16 or wider, within the bound.
No kernel may reach another device: no remote copies, remote signals or barrier semaphores. Data moves between devices by JAX's collectives and lax.ppermute only.
A program may use at most 128 MiB of HBM per device.

```python
import jax
import jax.numpy as jnp
from jax import lax

D = 768
HEADS = 12
HEAD_DIM = 64
FF = 3072
SLOTS = 2048
ITEMS = 5
LEN_MIN = 64
EXPERTS = 8
MAXLEN = 1024
SHARD = 512
CAP = 64
TOKENS = 16384
N_DP = 8
N_TENSOR = 4


def draw_item_lengths(key, part):
    places = jnp.arange(N_DP, dtype=jnp.int32)
    chosen = jax.random.randint(jax.random.fold_in(key, 101), (), 0, N_DP)
    occupied = jnp.zeros((N_DP,), jnp.int32)
    columns = []
    for column in range(ITEMS):
        ceiling = SLOTS - occupied - LEN_MIN * (ITEMS - 1 - column)
        sampled = jax.random.randint(jax.random.fold_in(key, column), (N_DP,), LEN_MIN, MAXLEN + 1)
        sampled = jnp.minimum(sampled, ceiling)
        if column == 0:
            sampled = jnp.where(places == chosen, MAXLEN, sampled)
        if column == 1:
            sampled = jnp.where(places == chosen, LEN_MIN, sampled)
        occupied = occupied + sampled
        columns.append(sampled)
    return jnp.stack(columns, axis=1).astype(jnp.int32)


def levels(own_key, dims, cuts, low, high):
    def one(position, parts):
        heights = jax.random.uniform(jax.random.fold_in(jax.random.fold_in(own_key, 6), position), (parts,), jnp.float32, low / len(cuts), high / len(cuts))
        return jnp.repeat(jnp.exp(heights), dims[position] // parts).reshape((-1,) + (1,) * (len(dims) - position - 1))

    factor_of = one(*cuts[0])
    for cut in cuts[1:]:
        factor_of = factor_of * one(*cut)
    return factor_of


def choose_distinct(rng, rows, amount, top, lift):
    sequence = jax.random.permutation(jax.random.fold_in(rng, 1), amount)
    favour = sequence
    for power in range(3):
        favour = favour * favour // amount
    favour = favour * lift // amount
    chance = jax.random.randint(jax.random.fold_in(rng, 2), (rows, amount), 0, 4096) + favour
    holders = jax.random.permutation(jax.random.fold_in(rng, 3), rows)[jnp.arange(amount) % rows]
    chance = jnp.where(jnp.arange(rows)[:, None] == holders[None, :], 1 << 14, chance)
    score = chance * amount + jnp.arange(amount)
    return lax.top_k(score.astype(jnp.int32), top)[1].astype(jnp.int32)


def gaussian(own_key, extent, width, limit, shards=(), kind=jnp.bfloat16):
    array = jax.random.normal(own_key, extent, jnp.float32) * width
    if len(shards) > 0:
        array = levels(own_key, extent, shards, -0.22, 0.18) * array
    return jnp.clip(array, min=-limit, max=limit).astype(kind)


def setup_inputs(seed: int = 0) -> dict:
    streams_of = jax.random.split(jax.random.key(seed), 16)
    return {
        "tokens": gaussian(streams_of[0], (TOKENS, D), 1.0, 6.0, ((0, 8),)),
        "first_gain": jnp.clip(1.0 + 0.1 * jax.random.normal(streams_of[1], (D,), jnp.float32), 0.5, 1.5),
        "first_bias": gaussian(streams_of[2], (D,), 0.3, 1.5, (), jnp.float32),
        "query_weight": gaussian(streams_of[3], (D, HEADS * HEAD_DIM), D ** -0.5, 0.21875, ((1, 4),)),
        "key_weight": gaussian(streams_of[4], (D, HEADS * HEAD_DIM), D ** -0.5, 0.21875, ((1, 4),)),
        "value_weight": gaussian(streams_of[5], (D, HEADS * HEAD_DIM), D ** -0.5, 0.21875, ((1, 4),)),
        "output_weight": gaussian(streams_of[6], (HEADS * HEAD_DIM, D), (max(1, D // 256)) ** -0.5, 3.5, ((0, 4),)),
        "second_gain": jnp.clip(1.0 + 0.1 * jax.random.normal(streams_of[7], (D,), jnp.float32), 0.5, 1.5),
        "second_bias": gaussian(streams_of[8], (D,), 0.3, 1.5, (), jnp.float32),
        "expert_up": gaussian(streams_of[9], (EXPERTS, D, FF), D ** -0.5, 0.21875, ((0, 8),)),
        "expert_down": gaussian(streams_of[10], (EXPERTS, FF, D), FF ** -0.5, 0.109375, ((0, 8),)),
        "item_lengths": draw_item_lengths(jax.random.fold_in(streams_of[15], 71), 0),
        "routes": choose_distinct(streams_of[12], TOKENS, EXPERTS, 1, 1024),
        "slot_order": jax.vmap(lambda own: jax.random.permutation(own, SHARD))(jax.random.split(streams_of[13], (N_DP * N_TENSOR))).reshape((N_DP * N_TENSOR, SHARD)).astype(jnp.int32),
        "cotangent": gaussian(streams_of[14], (TOKENS, D), 1.0, 6.0, ((0, 32),)),
    }


@jax.custom_vjp
def low(v):
    return lax.optimization_barrier(v.astype(jnp.bfloat16)).astype(jnp.float32)

@jax.custom_vjp
def low_back(v):
    return v

def low_keep(v):
    return (low(v), None)

def low_pass(kept, grad):
    return (grad,)

def back_keep(v):
    return (v, None)

def back_low(kept, grad):
    return (low(grad),)
low.defvjp(low_keep, low_pass)
low_back.defvjp(back_keep, back_low)
EPSILON = 1e-05
NEGATIVE = -1e+30
HIGHEST = lax.Precision.HIGHEST

def layer_norm(values, gain, shift):
    average = lax.optimization_barrier(jnp.mean(values, axis=-1, keepdims=True))
    centred = values - average
    variance = lax.optimization_barrier(jnp.mean(centred * centred, axis=-1, keepdims=True))
    return centred * lax.rsqrt(variance + EPSILON) * gain + shift

def gelu_exact(values):
    return jax.nn.gelu(values, approximate=False)

def segment_of(lengths, count):
    ends = jnp.cumsum(lengths).astype(jnp.int32)
    places = jnp.arange(count, dtype=jnp.int32)
    return lax.optimization_barrier(jnp.sum((places[:, None] >= ends[None, :]).astype(jnp.int32), axis=1))

def plan_shard(pieces):
    chosen, order, alive_rows = pieces
    matches = (chosen[:, None] == chosen[None, :]) & (order[None, :] < order[:, None]) & alive_rows[None, :]
    ranked = lax.optimization_barrier(jnp.sum(matches.astype(jnp.int32), axis=1))
    kept_rows = alive_rows & (ranked < CAP)
    slot_index = jnp.where(kept_rows, chosen * CAP + ranked, EXPERTS * CAP).astype(jnp.int32)
    return slot_index

def reference(tokens, first_gain, first_bias, query_weight, key_weight, value_weight, output_weight, second_gain, second_bias, expert_up, expert_down, item_lengths, routes, slot_order, cotangent):
    shard_count = N_DP * N_TENSOR
    head_cols = HEADS * HEAD_DIM
    block_rows = min(512, SLOTS)
    block_count = SLOTS // block_rows
    scale = HEAD_DIM ** (-0.5)
    segments = jnp.stack([segment_of(item_lengths[group], SLOTS) for group in range(N_DP)])
    alive_table = segments < ITEMS
    slot_table = lax.map(plan_shard, (routes[:, 0].reshape(shard_count, SHARD), slot_order, alive_table.reshape(shard_count, SHARD)))
    shard_index = jnp.arange(shard_count, dtype=jnp.int32)[:, None]

    def forward(token_values, gain_one, bias_one, query_mat, key_mat, value_mat, output_mat, gain_two, bias_two, up_all, down_all):
        normed_in = low(layer_norm(token_values, gain_one, bias_one))
        query = low(low_back(jnp.dot(normed_in, query_mat, precision=HIGHEST)))
        key_all = low(low_back(jnp.dot(normed_in, key_mat, precision=HIGHEST)))
        value_all = low(low_back(jnp.dot(normed_in, value_mat, precision=HIGHEST)))

        def group_attend(pieces):
            query_group, key_group, value_group, seg_group, alive_group = pieces
            key_heads = key_group.reshape(SLOTS, HEADS, HEAD_DIM)
            value_heads = value_group.reshape(SLOTS, HEADS, HEAD_DIM)

            def block_attend(block_pieces):
                query_block, seg_block = block_pieces
                scores = low_back(jnp.einsum('qhd,khd->hqk', query_block, key_heads, precision=HIGHEST) * scale)
                matches = seg_block[:, None] == seg_group[None, :]
                scores = jnp.where(matches[None], scores, NEGATIVE)
                soft = jax.nn.softmax(scores, axis=-1)
                return jnp.einsum('hqk,khd->qhd', low(soft), value_heads, precision=HIGHEST)
            blocks = lax.map(jax.checkpoint(block_attend), (query_group.reshape(block_count, block_rows, HEADS, HEAD_DIM), seg_group.reshape(block_count, block_rows)))
            heads_out = blocks.reshape(SLOTS, head_cols) * alive_group[:, None].astype(jnp.float32)
            heads_low = low(low_back(heads_out))
            return low_back(jnp.dot(heads_low, output_mat, precision=HIGHEST))
        attended = lax.map(jax.checkpoint(group_attend), (query.reshape(N_DP, SLOTS, head_cols), key_all.reshape(N_DP, SLOTS, head_cols), value_all.reshape(N_DP, SLOTS, head_cols), segments, alive_table))
        residual = token_values + attended.reshape(TOKENS, D)
        normed_mid = low(low_back(layer_norm(residual, gain_two, bias_two)))
        shard_values = normed_mid.reshape(shard_count, SHARD, D)
        buffer = jnp.zeros((shard_count, EXPERTS * CAP + 1, D), jnp.float32).at[shard_index, slot_table].add(shard_values)
        expert_rows = buffer[:, :EXPERTS * CAP].reshape(shard_count, EXPERTS, CAP, D).transpose(1, 0, 2, 3).reshape(EXPERTS, shard_count * CAP, D)

        def expert_apply(pieces):
            rows_in, up_one, down_one = pieces
            pre_act = low_back(jnp.dot(rows_in, up_one, precision=HIGHEST))
            activated = low(gelu_exact(pre_act))
            return low(jnp.dot(activated, down_one, precision=HIGHEST))
        produced = lax.map(jax.checkpoint(expert_apply), (expert_rows, up_all, down_all))
        produced = produced.reshape(EXPERTS, shard_count, CAP, D).transpose(1, 0, 2, 3).reshape(shard_count, EXPERTS * CAP, D)
        produced = jnp.concatenate([produced, jnp.zeros((shard_count, 1, D), jnp.float32)], axis=1)
        returned = jnp.take_along_axis(produced, slot_table[:, :, None], axis=1)
        return residual + returned.reshape(TOKENS, D)
    block_out, pull = jax.vjp(forward, tokens.astype(jnp.float32), first_gain.astype(jnp.float32), first_bias.astype(jnp.float32), query_weight.astype(jnp.float32), key_weight.astype(jnp.float32), value_weight.astype(jnp.float32), output_weight.astype(jnp.float32), second_gain.astype(jnp.float32), second_bias.astype(jnp.float32), expert_up.astype(jnp.float32), expert_down.astype(jnp.float32))
    grads = pull(cotangent.astype(jnp.float32))
    return (block_out, grads[0], grads[1], grads[2], grads[3], grads[4], grads[5], grads[6], grads[7], grads[8], grads[9], grads[10])
```

```python
import functools

import jax
import jax.numpy as jnp
from jax import lax
from jax.experimental import pallas as pl
from jax.experimental.pallas import tpu as pltpu
from jax.sharding import PartitionSpec as P

HEAD_DIM = 64
EPSILON = 1e-05
NEGATIVE = -1e30
f32 = jnp.float32
bf16 = jnp.bfloat16
VMEM = pl.BlockSpec(memory_space=pltpu.VMEM)
SMEM = pl.BlockSpec(memory_space=pltpu.SMEM)


def layer_norm(values, gain, shift):
    average = jnp.mean(values, axis=-1, keepdims=True)
    centred = values - average
    variance = jnp.mean(centred * centred, axis=-1, keepdims=True)
    return centred * lax.rsqrt(variance + EPSILON) * gain + shift


def segment_of(lengths, places):
    ends = jnp.cumsum(lengths)
    return jnp.sum((places[:, None] >= ends[None, :]).astype(jnp.int32), axis=1)


def slot_plan(chosen, order, alive_rows, capacity, experts_all):
    matches = (
        (chosen[:, None] == chosen[None, :])
        & (order[None, :] < order[:, None])
        & alive_rows[None, :]
    )
    ranked = jnp.sum(matches.astype(jnp.int32), axis=1)
    kept_rows = alive_rows & (ranked < capacity)
    return jnp.where(kept_rows, chosen * capacity + ranked, experts_all * capacity)


def contract_rows(left, right):
    return lax.dot_general(
        left, right, (((0,), (0,)), ((), ())), preferred_element_type=f32
    )


def swap(values, axis, step):
    count = lax.axis_size(axis)
    return lax.ppermute(values, axis, [(i, i ^ step) for i in range(count)])


def steps_of(count):
    steps = []
    step = 1
    while step < count:
        steps.append(step)
        step *= 2
    return steps


def lane_masked(values, head):
    lane = lax.broadcasted_iota(jnp.int32, values.shape, 1)
    inside = (lane >= head * HEAD_DIM) & (lane < (head + 1) * HEAD_DIM)
    return jnp.where(inside, values, jnp.zeros_like(values))


def item_ends(lens_ref):
    ends = []
    total = jnp.int32(0)
    for i in range(lens_ref.shape[1]):
        total = total + lens_ref[0, i]
        ends.append(total)
    return ends


def segments_at(place, ends):
    segment = jnp.zeros_like(place)
    for end in ends:
        segment = segment + (place >= end).astype(jnp.int32)
    return segment


def block_span(block, size, ends):
    first = block * size
    last = jnp.minimum(first + size, ends[-1]) - 1
    low = jnp.int32(0)
    high = ends[-1]
    for end in ends:
        low = jnp.where(first >= end, end, low)
    for end in reversed(ends):
        high = jnp.where(last < end, end, high)
    empty = first >= ends[-1]
    low_block = jnp.where(empty, 0, low // size)
    high_block = jnp.where(empty, 0, (high + size - 1) // size)
    return low_block, high_block


def rows_at(block, size):
    return pl.ds(pl.multiple_of(block * size, size), size)


def forward_kernel(
    lens_ref, rank_ref, qt_ref, k_ref, vt_ref, out_ref, log_ref, masked_ref
):
    size = out_ref.shape[2]
    blocks = out_ref.shape[0]
    heads = qt_ref.shape[0] // HEAD_DIM
    rank = rank_ref[0, 0]
    ends = item_ends(lens_ref)
    keys = k_ref[...]
    for h in range(heads):
        masked_ref[h] = lane_masked(keys, h)

    def query_block(i, unused):
        at = i ^ rank
        cols = rows_at(at, size)
        seg_q = segments_at(
            i * size + lax.broadcasted_iota(jnp.int32, (1, size), 1), ends
        )
        queries = qt_ref[:, cols]

        def key_block(j, carry):
            rows = rows_at(j ^ rank, size)
            seg_k = segments_at(
                j * size + lax.broadcasted_iota(jnp.int32, (size, 1), 0), ends
            )
            same = seg_k == seg_q
            result = []
            for h in range(heads):
                highest, summed, total = carry[h]
                scores = jnp.dot(
                    masked_ref[h, rows, :], queries, preferred_element_type=f32
                )
                scores = jnp.where(same, scores, NEGATIVE)
                raised = jnp.maximum(highest, jnp.max(scores, axis=0, keepdims=True))
                shrink = jnp.exp(highest - raised)
                soft = jnp.exp(scores - raised)
                summed = summed * shrink + jnp.sum(soft, axis=0, keepdims=True)
                total = total * shrink + jnp.dot(
                    vt_ref[pl.ds(h * HEAD_DIM, HEAD_DIM), rows],
                    soft.astype(bf16),
                    preferred_element_type=f32,
                )
                result.append((raised, summed, total))
            return tuple(result)

        start = tuple(
            (
                jnp.full((1, size), NEGATIVE, f32),
                jnp.zeros((1, size), f32),
                jnp.zeros((HEAD_DIM, size), f32),
            )
            for h in range(heads)
        )
        low, high = block_span(i, size, ends)
        done = lax.fori_loop(low, high, key_block, start)
        live = seg_q < len(ends)
        for h in range(heads):
            highest, summed, total = done[h]
            summed = jnp.where(live, summed, 1.0)
            out_ref[at, pl.ds(h * HEAD_DIM, HEAD_DIM), :] = jnp.where(
                live, total / summed, 0.0
            ).astype(bf16)
            log_ref[at, pl.ds(h, 1), :] = jnp.where(
                live, highest + jnp.log(summed), -NEGATIVE
            )
        return unused

    lax.fori_loop(0, blocks, query_block, 0)


def attend(lens, rank, qt, k, vt, blocks):
    width, slots = qt.shape
    size = slots // blocks
    heads = width // HEAD_DIM
    return pl.pallas_call(
        forward_kernel,
        out_shape=(
            jax.ShapeDtypeStruct((blocks, width, size), bf16),
            jax.ShapeDtypeStruct((blocks, 8, size), f32),
        ),
        in_specs=[SMEM, SMEM, VMEM, VMEM, VMEM],
        out_specs=(VMEM, VMEM),
        scratch_shapes=[pltpu.VMEM((heads, slots, width), bf16)],
        name="attend",
        compiler_params=pltpu.CompilerParams(vmem_limit_bytes=60 * 2**20),
        cost_estimate=pl.CostEstimate(
            flops=slots * slots * width * 3, bytes_accessed=6 * slots * width,
            transcendentals=slots * slots * heads // 2,
        ),
    )(lens, rank, qt, k, vt)


def backward_kernel(
    lens_ref, rank_ref, qt_ref, kt_ref, q_ref, k_ref, v_ref, out_ref, log_ref, *rest
):
    blocks, width, size = out_ref.shape
    grad_refs = rest[:blocks]
    dqt_ref, dk_ref, dv_ref = rest[blocks : blocks + 3]
    km_ref, vm_ref, qm_ref, gm_ref, gt_ref, inner_ref, dq_ref = rest[blocks + 3 :]
    heads = width // HEAD_DIM
    rank = rank_ref[0, 0]
    ends = item_ends(lens_ref)
    q = q_ref[...]
    k = k_ref[...]
    v = v_ref[...]
    for h in range(heads):
        km_ref[h] = lane_masked(k, h)
        vm_ref[h] = lane_masked(v, h)
        qm_ref[h] = lane_masked(q, h)
    for b in range(blocks):
        grad_t = grad_refs[b][...]
        gt_ref[:, pl.ds(b * size, size)] = grad_t
        grad = jnp.transpose(grad_t, (1, 0))
        for h in range(heads):
            gm_ref[h, pl.ds(b * size, size), :] = lane_masked(grad, h)
            part = slice(h * HEAD_DIM, (h + 1) * HEAD_DIM)
            inner_ref[b, pl.ds(h, 1), :] = jnp.sum(
                out_ref[b, part, :].astype(f32) * grad_t[part, :].astype(f32),
                axis=0,
                keepdims=True,
            )
    dq_ref[...] = jnp.zeros_like(dq_ref)

    def key_block(j, unused):
        rows = rows_at(j ^ rank, size)
        seg_k = segments_at(
            j * size + lax.broadcasted_iota(jnp.int32, (size, 1), 0), ends
        )

        def query_block(i, carry):
            dk, dv = carry
            at = i ^ rank
            cols = rows_at(at, size)
            seg_q = segments_at(
                i * size + lax.broadcasted_iota(jnp.int32, (1, size), 1), ends
            )
            same = seg_k == seg_q
            queries = qt_ref[:, cols]
            grads = gt_ref[:, cols]
            for h in range(heads):
                part = pl.ds(h * HEAD_DIM, HEAD_DIM)
                scores = jnp.dot(km_ref[h, rows, :], queries, preferred_element_type=f32)
                soft = jnp.where(
                    same, jnp.exp(scores - log_ref[at, pl.ds(h, 1), :]), 0.0
                )
                grad_soft = jnp.dot(vm_ref[h, rows, :], grads, preferred_element_type=f32)
                grad_scores = (
                    soft * (grad_soft - inner_ref[at, pl.ds(h, 1), :])
                ).astype(bf16)
                dv = dv + jnp.dot(
                    soft.astype(bf16), gm_ref[h, cols, :], preferred_element_type=f32
                )
                dk = dk + jnp.dot(
                    grad_scores, qm_ref[h, cols, :], preferred_element_type=f32
                )
                dq_ref[part, cols] += jnp.dot(
                    kt_ref[part, rows], grad_scores, preferred_element_type=f32
                )
            return dk, dv

        low, high = block_span(j, size, ends)
        zero = jnp.zeros((size, width), f32)
        dk, dv = lax.fori_loop(low, high, query_block, (zero, zero))
        dk_ref[rows, :] = dk.astype(bf16)
        dv_ref[rows, :] = dv.astype(bf16)
        return unused

    lax.fori_loop(0, blocks, key_block, 0)
    dqt_ref[...] = (dq_ref[...] * HEAD_DIM ** (-0.5)).astype(bf16)


def attend_back(lens, rank, qt, kt, q, k, v, out, logs, grads):
    blocks, width, size = out.shape
    slots = blocks * size
    heads = width // HEAD_DIM
    return pl.pallas_call(
        backward_kernel,
        out_shape=(
            jax.ShapeDtypeStruct((width, slots), bf16),
            jax.ShapeDtypeStruct((slots, width), bf16),
            jax.ShapeDtypeStruct((slots, width), bf16),
        ),
        in_specs=[SMEM, SMEM] + [VMEM] * (7 + blocks),
        out_specs=(VMEM, VMEM, VMEM),
        scratch_shapes=[pltpu.VMEM((heads, slots, width), bf16)] * 4
        + [
            pltpu.VMEM((width, slots), bf16),
            pltpu.VMEM((blocks, 8, size), f32),
            pltpu.VMEM((width, slots), f32),
        ],
        name="attend_back",
        compiler_params=pltpu.CompilerParams(vmem_limit_bytes=60 * 2**20),
        cost_estimate=pl.CostEstimate(
            flops=slots * slots * width * 6, bytes_accessed=14 * slots * width,
            transcendentals=slots * slots * heads // 2,
        ),
    )(lens, rank, qt, kt, q, k, v, out, logs, *grads)


def gelu_parts(values):
    below = 0.5 + 0.5 * lax.erf(values * (0.5**0.5))
    density = jnp.exp(-0.5 * values * values) * (0.5 / jnp.pi) ** 0.5
    return values * below, below + values * density


def expert_kernel(in_ref, grad_ref, up_ref, down_ref, act_ref, mid_ref, sum_ref):
    step = pl.program_id(0)
    pre = jnp.dot(in_ref[...], up_ref[...], preferred_element_type=f32)
    grad_act = lax.dot_general(
        grad_ref[...], down_ref[...], (((1,), (1,)), ((), ())),
        preferred_element_type=f32,
    )
    act, slope = gelu_parts(pre)
    act_ref[...] = act.astype(bf16)
    grad_pre = (grad_act * slope).astype(bf16)
    mid = lax.dot_general(
        grad_pre, up_ref[...], (((1,), (1,)), ((), ())), preferred_element_type=f32
    )

    @pl.when(step == 0)
    def first():
        sum_ref[...] = mid

    @pl.when(step > 0)
    def later():
        sum_ref[...] += mid

    @pl.when(step == pl.num_programs(0) - 1)
    def last():
        mid_ref[...] = sum_ref[...].astype(bf16)


def expert(rows, grads, up, down):
    count, width = rows.shape
    hidden = up.shape[1]
    size = min(512, hidden)
    return pl.pallas_call(
        expert_kernel,
        grid=(hidden // size,),
        out_shape=(
            jax.ShapeDtypeStruct((count, hidden), bf16),
            jax.ShapeDtypeStruct((count, width), bf16),
        ),
        in_specs=[
            pl.BlockSpec((count, width), lambda i: (0, 0)),
            pl.BlockSpec((count, width), lambda i: (0, 0)),
            pl.BlockSpec((width, size), lambda i: (0, i)),
            pl.BlockSpec((size, width), lambda i: (i, 0)),
        ],
        out_specs=(
            pl.BlockSpec((count, size), lambda i: (0, i)),
            pl.BlockSpec((count, width), lambda i: (0, 0)),
        ),
        scratch_shapes=[pltpu.VMEM((count, width), f32)],
        name="expert",
        cost_estimate=pl.CostEstimate(
            flops=6 * count * width * hidden, bytes_accessed=4 * width * hidden,
            transcendentals=2 * count * hidden,
        ),
    )(rows, grads, up, down)


def weight_kernel(rank_ref, in_ref, grad_ref, up_ref, down_ref, dup_ref, ddown_ref):
    step = pl.program_id(1)
    pre = jnp.dot(in_ref[...], up_ref[...], preferred_element_type=f32)
    grad_act = lax.dot_general(
        grad_ref[...], down_ref[...], (((1,), (1,)), ((), ())),
        preferred_element_type=f32,
    )
    act, slope = gelu_parts(pre)
    dup = contract_rows(in_ref[...], (grad_act * slope).astype(bf16))
    ddown = contract_rows(act.astype(bf16), grad_ref[...])

    @pl.when(step == 0)
    def first():
        dup_ref[...] = dup
        ddown_ref[...] = ddown

    @pl.when(step > 0)
    def later():
        dup_ref[...] += dup
        ddown_ref[...] += ddown


def expert_weights(rank, rows, grads, up, down, parts):
    count, width = rows.shape
    hidden = up.shape[1] // parts
    size = min(384, hidden)
    chunk = min(512, count)
    blocks = hidden // size
    return pl.pallas_call(
        weight_kernel,
        grid_spec=pltpu.PrefetchScalarGridSpec(
            num_scalar_prefetch=1,
            grid=(blocks, count // chunk),
            in_specs=[
                pl.BlockSpec((chunk, width), lambda i, j, r: (j, 0)),
                pl.BlockSpec((chunk, width), lambda i, j, r: (j, 0)),
                pl.BlockSpec((width, size), lambda i, j, r: (0, r[0] * blocks + i)),
                pl.BlockSpec((size, width), lambda i, j, r: (r[0] * blocks + i, 0)),
            ],
            out_specs=(
                pl.BlockSpec((width, size), lambda i, j, r: (0, i)),
                pl.BlockSpec((size, width), lambda i, j, r: (i, 0)),
            ),
        ),
        out_shape=(
            jax.ShapeDtypeStruct((width, hidden), f32),
            jax.ShapeDtypeStruct((hidden, width), f32),
        ),
        name="expert_weights",
        cost_estimate=pl.CostEstimate(
            flops=8 * count * width * hidden, bytes_accessed=16 * width * hidden,
            transcendentals=2 * count * hidden,
        ),
    )(rank, rows, grads, up, down)


def sum_rows_over(values, axis):
    count = lax.axis_size(axis)
    rows, cols = values.shape
    parts = values.astype(bf16).reshape(count, rows // count, cols)
    arrived = lax.all_to_all(parts, axis, split_axis=0, concat_axis=0, tiled=True)
    mine = jnp.sum(arrived.astype(f32), axis=0).astype(bf16)
    spread = jnp.broadcast_to(mine[None], parts.shape)
    full = lax.all_to_all(spread, axis, split_axis=0, concat_axis=0, tiled=True)
    return full.reshape(rows, cols).astype(f32)


def sum_small(values, axes):
    for axis in axes:
        for step in steps_of(lax.axis_size(axis)):
            values = values + swap(values, axis, step)
    return values


def on_device(
    tokens,
    first_gain,
    first_bias,
    query_weight,
    key_weight,
    value_weight,
    output_weight,
    second_gain,
    second_bias,
    expert_up,
    expert_down,
    item_lengths,
    routes,
    slot_order,
    cotangent,
):
    slots_all, width = tokens.shape
    members = lax.axis_size("tensor")
    shard_rows = slots_all // members
    rank = lax.axis_index("tensor")
    sources = lax.axis_size("dp")
    experts_all = sources * expert_up.shape[0]
    capacity = shard_rows // experts_all
    head_cols = query_weight.shape[1]
    scale = HEAD_DIM ** (-0.5)
    up_matrix = expert_up[0]
    down_matrix = expert_down[0]
    rank_cell = rank.astype(jnp.int32).reshape(1, 1)

    tokens_x = jnp.concatenate(
        [
            lax.dynamic_slice_in_dim(tokens, (rank ^ k) * shard_rows, shard_rows)
            for k in range(members)
        ]
    )
    tokens_mine = tokens_x[:shard_rows].astype(f32)
    places = rank * shard_rows + jnp.arange(shard_rows, dtype=jnp.int32)
    alive_mine = segment_of(item_lengths[0], places) < item_lengths.shape[1]
    slot_index = slot_plan(routes[:, 0], slot_order[0], alive_mine, capacity, experts_all)
    slot_ids = jnp.arange(experts_all * capacity, dtype=jnp.int32)
    dispatch = (slot_ids[:, None] == slot_index[None, :]).astype(bf16)

    grad_slots = jnp.dot(dispatch, cotangent, preferred_element_type=f32).astype(bf16)
    flat_grad = lax.all_to_all(
        grad_slots.reshape(experts_all, capacity, width),
        "dp", split_axis=0, concat_axis=0, tiled=True,
    ).reshape(-1, width)
    output_x = jnp.concatenate(
        [output_weight]
        + [swap(output_weight, "tensor", k) for k in range(1, members)]
    )

    normed_in = layer_norm(tokens_x.astype(f32), first_gain, first_bias).astype(bf16)
    joined = jnp.concatenate([query_weight, key_weight, value_weight], axis=1)
    column_scale = jnp.where(jnp.arange(3 * head_cols) < head_cols, scale, 1.0)
    natural = jnp.dot(normed_in, joined, preferred_element_type=f32).astype(bf16)
    natural = natural * column_scale[None, :].astype(bf16)
    turned = lax.dot_general(
        joined, normed_in, (((0,), (1,)), ((), ())), preferred_element_type=f32
    ).astype(bf16)
    turned = turned * column_scale[:, None].astype(bf16)
    q, k, v = (natural[:, i * head_cols : (i + 1) * head_cols] for i in range(3))
    qt, kt, vt = (turned[i * head_cols : (i + 1) * head_cols] for i in range(3))

    heads_t, logs = attend(item_lengths, rank_cell, qt, k, vt, members)
    heads_x = jnp.concatenate(
        [heads_t[0]] + [swap(heads_t[j], "tensor", j) for j in range(1, members)]
    )
    residual = tokens_mine + contract_rows(heads_x, output_x)
    normed_low = layer_norm(residual, second_gain, second_bias).astype(bf16)
    outgoing = jnp.dot(dispatch, normed_low, preferred_element_type=f32).astype(bf16)
    flat_in = lax.all_to_all(
        outgoing.reshape(experts_all, capacity, width),
        "dp", split_axis=0, concat_axis=0, tiled=True,
    ).reshape(-1, width)

    act, grad_mid = expert(flat_in, flat_grad, up_matrix, down_matrix)
    grad_back = lax.all_to_all(
        grad_mid.reshape(sources, capacity, width),
        "dp", split_axis=0, concat_axis=0, tiled=True,
    ).reshape(-1, width)
    made = jnp.dot(act, down_matrix, preferred_element_type=f32).astype(bf16)

    grad_normed = contract_rows(dispatch, grad_back)
    unused_mid, pull_mid = jax.vjp(layer_norm, residual, second_gain, second_bias)
    grad_res_norm, second_gain_part, second_bias_part = pull_mid(grad_normed)
    grad_res = cotangent.astype(f32) + grad_res_norm
    grad_low = grad_res.astype(bf16)
    grad_heads = (
        lax.dot_general(
            output_x, grad_low, (((1,), (1,)), ((), ())), preferred_element_type=f32
        )
        * alive_mine[None, :].astype(f32)
    ).astype(bf16)
    grad_parts = [grad_heads[:head_cols]] + [
        swap(grad_heads[j * head_cols : (j + 1) * head_cols], "tensor", j)
        for j in range(1, members)
    ]
    dqt, dk, dv = attend_back(
        item_lengths, rank_cell, qt, kt, q, k, v, heads_t, logs, grad_parts
    )

    partial = (
        lax.dot_general(
            dqt, query_weight, (((0,), (1,)), ((), ())), preferred_element_type=f32
        )
        + lax.dot_general(
            dk, key_weight, (((1,), (1,)), ((), ())), preferred_element_type=f32
        )
        + lax.dot_general(
            dv, value_weight, (((1,), (1,)), ((), ())), preferred_element_type=f32
        )
    ).astype(bf16).reshape(members, shard_rows, width)
    for step in steps_of(members):
        stride = 2 * step
        arrived = swap(partial[1::2], "tensor", step)
        partial = (partial[0::2].astype(f32) + arrived.astype(f32)).astype(
            bf16 if stride < members else f32
        )
    grad_in = partial[0]
    unused_first, pull_first = jax.vjp(layer_norm, tokens_mine, first_gain, first_bias)
    grad_tok_norm, first_gain_part, first_bias_part = pull_first(grad_in)
    token_grad = grad_res + grad_tok_norm

    query_grad = lax.dot_general(
        normed_in, dqt, (((0,), (1,)), ((), ())), preferred_element_type=f32
    )
    key_grad = contract_rows(normed_in, dk)
    value_grad = contract_rows(normed_in, dv)
    head_sum = sum_rows_over(
        jnp.concatenate([query_grad, key_grad, value_grad], axis=1), "dp"
    )

    output_part = jnp.dot(heads_x, grad_low, preferred_element_type=f32).astype(bf16)
    output_mine = output_part[:head_cols].astype(f32)
    for j in range(1, members):
        output_mine = output_mine + swap(
            output_part[j * head_cols : (j + 1) * head_cols], "tensor", j
        ).astype(f32)
    output_grad = sum_rows_over(output_mine, "dp")

    returned = lax.all_to_all(
        made.reshape(sources, capacity, width),
        "dp", split_axis=0, concat_axis=0, tiled=True,
    ).reshape(-1, width)
    block_out = residual + contract_rows(dispatch, returned)

    rows_all = flat_in[None]
    grads_all = flat_grad[None]
    for step in reversed(steps_of(members)):
        rows_all = jnp.concatenate([rows_all, swap(rows_all, "tensor", step)])
        grads_all = jnp.concatenate([grads_all, swap(grads_all, "tensor", step)])
    up_grad, down_grad = expert_weights(
        rank_cell[0], rows_all.reshape(-1, width), grads_all.reshape(-1, width),
        up_matrix, down_matrix, members,
    )

    norm_sums = sum_small(
        jnp.stack([first_gain_part, first_bias_part, second_gain_part, second_bias_part]),
        ("tensor", "dp"),
    )
    return (
        block_out,
        token_grad,
        norm_sums[0],
        norm_sums[1],
        head_sum[:, :head_cols],
        head_sum[:, head_cols : 2 * head_cols],
        head_sum[:, 2 * head_cols :],
        output_grad,
        norm_sums[2],
        norm_sums[3],
        up_grad[None],
        down_grad[None],
    )


def solution(mesh):
    in_specs = (
        P("dp", None),
        P(),
        P(),
        P(None, "tensor"),
        P(None, "tensor"),
        P(None, "tensor"),
        P("tensor", None),
        P(),
        P(),
        P("dp", None, None),
        P("dp", None, None),
        P("dp", None),
        P(("dp", "tensor"), None),
        P(("dp", "tensor"), None),
        P(("dp", "tensor"), None),
    )
    out_specs = (
        P(("dp", "tensor"), None),
        P(("dp", "tensor"), None),
        P(),
        P(),
        P(None, "tensor"),
        P(None, "tensor"),
        P(None, "tensor"),
        P("tensor", None),
        P(),
        P(),
        P("dp", None, "tensor"),
        P("dp", "tensor", None),
    )
    return jax.shard_map(
        on_device, mesh=mesh, in_specs=in_specs, out_specs=out_specs, check_vma=False
    )
```

```python
import functools

import jax
import jax.numpy as jnp
from jax import lax
from jax.experimental import pallas as pl
from jax.experimental.pallas import tpu as pltpu
from jax.sharding import PartitionSpec as P

HEAD_DIM = 64
EPSILON = 1e-05
NEGATIVE = -1e30
f32 = jnp.float32
bf16 = jnp.bfloat16
VMEM = pl.BlockSpec(memory_space=pltpu.VMEM)
SMEM = pl.BlockSpec(memory_space=pltpu.SMEM)


def layer_norm(values, gain, shift):
    average = jnp.mean(values, axis=-1, keepdims=True)
    centred = values - average
    variance = jnp.mean(centred * centred, axis=-1, keepdims=True)
    return centred * lax.rsqrt(variance + EPSILON) * gain + shift


def contract_rows(left, right):
    return lax.dot_general(
        left, right, (((0,), (0,)), ((), ())), preferred_element_type=f32
    )


def swap(values, axis, step):
    count = lax.axis_size(axis)
    return lax.ppermute(values, axis, [(i, i ^ step) for i in range(count)])


def steps_of(count):
    steps = []
    step = 1
    while step < count:
        steps.append(step)
        step *= 2
    return steps


def normalized(values):
    average = jnp.mean(values, axis=-1, keepdims=True)
    centred = values - average
    variance = jnp.mean(centred * centred, axis=-1, keepdims=True)
    return centred * lax.rsqrt(variance + EPSILON)


def project_kernel(
    rank_ref, tokens_ref, gain_ref, bias_ref, qw_ref, kw_ref, vw_ref,
    normed_ref, qt_ref, kt_ref, vt_ref,
):
    values = tokens_ref[...].astype(f32)
    normed = (normalized(values) * gain_ref[...] + bias_ref[...]).astype(bf16)
    normed_ref[...] = normed
    for weight_ref, out_ref, factor in (
        (qw_ref, qt_ref, HEAD_DIM ** (-0.5)), (kw_ref, kt_ref, None), (vw_ref, vt_ref, None)
    ):
        made = jnp.dot(normed, weight_ref[...], preferred_element_type=f32).astype(bf16)
        if factor is not None:
            made = made * jnp.asarray(factor, bf16)
        out_ref[...] = jnp.transpose(made, (1, 0))


def project(rank, tokens, gain, bias, qw, kw, vw, blocks):
    slots, width = tokens.shape
    cols = qw.shape[1]
    size = slots // blocks
    fixed = lambda i, r: (0, 0)
    return pl.pallas_call(
        project_kernel,
        grid_spec=pltpu.PrefetchScalarGridSpec(
            num_scalar_prefetch=1,
            grid=(blocks,),
            in_specs=[
                pl.BlockSpec((size, width), lambda i, r: (i ^ r[0], 0)),
                pl.BlockSpec((1, width), fixed),
                pl.BlockSpec((1, width), fixed),
                pl.BlockSpec((width, cols), fixed),
                pl.BlockSpec((width, cols), fixed),
                pl.BlockSpec((width, cols), fixed),
            ],
            out_specs=(
                pl.BlockSpec((size, width), lambda i, r: (i, 0)),
                pl.BlockSpec((cols, size), lambda i, r: (0, i)),
                pl.BlockSpec((cols, size), lambda i, r: (0, i)),
                pl.BlockSpec((cols, size), lambda i, r: (0, i)),
            ),
        ),
        out_shape=(jax.ShapeDtypeStruct((slots, width), bf16),)
        + (jax.ShapeDtypeStruct((cols, slots), bf16),) * 3,
        name="project",
        cost_estimate=pl.CostEstimate(
            flops=6 * slots * width * cols, bytes_accessed=6 * slots * width,
            transcendentals=slots,
        ),
    )(rank, tokens, gain[None], bias[None], qw, kw, vw)


def item_ends(lens_ref):
    ends = []
    total = jnp.int32(0)
    for i in range(lens_ref.shape[1]):
        total = total + lens_ref[0, i]
        ends.append(total)
    return ends


def segments_at(place, ends):
    segment = jnp.zeros_like(place)
    for end in ends:
        segment = segment + (place >= end).astype(jnp.int32)
    return segment


def block_span(first, size, unit, ends):
    last = jnp.minimum(first + size, ends[-1]) - 1
    low = jnp.int32(0)
    high = ends[-1]
    for end in ends:
        low = jnp.where(first >= end, end, low)
    for end in reversed(ends):
        high = jnp.where(last < end, end, high)
    empty = first >= ends[-1]
    low_block = jnp.where(empty, 0, low // unit)
    high_block = jnp.where(empty, 0, (high + unit - 1) // unit)
    return low_block, high_block


def rows_at(block, size):
    return pl.ds(pl.multiple_of(block * size, size), size)


def memory_segments(block, size, shard, rank, ends, axis):
    shape = (1, size) if axis else (size, 1)
    at = block * size + lax.broadcasted_iota(jnp.int32, shape, axis)
    place = ((at // shard) ^ rank) * shard + at % shard
    return segments_at(place, ends)


def lane_masked(values, head):
    lane = lax.broadcasted_iota(jnp.int32, values.shape, 1)
    inside = (lane >= head * HEAD_DIM) & (lane < (head + 1) * HEAD_DIM)
    return jnp.where(inside, values, jnp.zeros_like(values))


def forward_kernel(
    lens_ref, rank_ref, qt_ref, kt_ref, vt_ref, out_ref, log_ref, masked_ref
):
    blocks, width, shard = out_ref.shape
    heads = width // HEAD_DIM
    pair = 2 if blocks % 2 == 0 else 1
    size = shard * pair
    rank = rank_ref[0, 0]
    ends = item_ends(lens_ref)
    keys = jnp.transpose(kt_ref[...], (1, 0))
    for h in range(heads):
        masked_ref[h] = lane_masked(keys, h)

    def query_block(i, unused):
        at = i ^ (rank // pair)
        cols = rows_at(at, size)
        seg_q = memory_segments(at, size, shard, rank, ends, 1)
        queries = qt_ref[:, cols]

        def key_block(j, carry):
            rows = rows_at(j ^ rank, shard)
            seg_k = memory_segments(j ^ rank, shard, shard, rank, ends, 0)
            same = seg_k == seg_q
            result = []
            for h in range(heads):
                highest, summed, total = carry[h]
                scores = jnp.dot(
                    masked_ref[h, rows, :], queries, preferred_element_type=f32
                )
                scores = jnp.where(same, scores, NEGATIVE)
                raised = jnp.maximum(highest, jnp.max(scores, axis=0, keepdims=True))
                shrink = jnp.exp(highest - raised)
                soft = jnp.exp(scores - raised)
                summed = summed * shrink + jnp.sum(soft, axis=0, keepdims=True)
                total = total * shrink + jnp.dot(
                    vt_ref[pl.ds(h * HEAD_DIM, HEAD_DIM), rows],
                    soft.astype(bf16),
                    preferred_element_type=f32,
                )
                result.append((raised, summed, total))
            return tuple(result)

        start = tuple(
            (
                jnp.full((1, size), NEGATIVE, f32),
                jnp.zeros((1, size), f32),
                jnp.zeros((HEAD_DIM, size), f32),
            )
            for h in range(heads)
        )
        low, high = block_span(i * size, size, shard, ends)
        done = lax.fori_loop(low, high, key_block, start)
        live = seg_q < len(ends)
        for h in range(heads):
            highest, summed, total = done[h]
            summed = jnp.where(live, summed, 1.0)
            result = jnp.where(live, total / summed, 0.0).astype(bf16)
            logs = jnp.where(live, highest + jnp.log(summed), -NEGATIVE)
            for p in range(pair):
                part = slice(p * shard, (p + 1) * shard)
                out_ref[at * pair + p, pl.ds(h * HEAD_DIM, HEAD_DIM), :] = result[:, part]
            log_ref[h, :, cols] = logs
        return unused

    lax.fori_loop(0, blocks // pair, query_block, 0)


def attend(lens, rank, qt, kt, vt, blocks):
    width, slots = qt.shape
    size = slots // blocks
    heads = width // HEAD_DIM
    return pl.pallas_call(
        forward_kernel,
        out_shape=(
            jax.ShapeDtypeStruct((blocks, width, size), bf16),
            jax.ShapeDtypeStruct((heads, 1, slots), f32),
        ),
        in_specs=[SMEM, SMEM, VMEM, VMEM, VMEM],
        out_specs=(VMEM, VMEM),
        scratch_shapes=[pltpu.VMEM((heads, slots, width), bf16)],
        name="attend",
        compiler_params=pltpu.CompilerParams(vmem_limit_bytes=60 * 2**20),
        cost_estimate=pl.CostEstimate(
            flops=slots * slots * width * 3, bytes_accessed=6 * slots * width,
            transcendentals=slots * slots * heads // 2,
        ),
    )(lens, rank, qt, kt, vt)


def backward_kernel(lens_ref, rank_ref, qt_ref, kt_ref, vt_ref, out_ref, log_ref, *rest):
    blocks, dim, shard = out_ref.shape
    grad_refs = rest[:blocks]
    joint_ref, kv_ref, q0_ref, og_ref, right_ref, inner_ref, dq_ref = rest[blocks:]
    slots = blocks * shard
    pair = 2 if blocks % 2 == 0 else 1
    size = shard * pair
    rank = rank_ref[0, 0]
    ends = item_ends(lens_ref)
    zero = jnp.zeros((dim, slots), bf16)
    kv_ref[...] = jnp.transpose(jnp.concatenate([kt_ref[...], vt_ref[...]], axis=0), (1, 0))
    padded = jnp.concatenate([qt_ref[...], zero], axis=0)
    q0_ref[...] = jnp.transpose(padded, (1, 0))
    right_ref[0] = padded
    for b in range(blocks):
        grad = grad_refs[b][...]
        cols = pl.ds(b * shard, shard)
        padded = jnp.concatenate([zero[:, :shard], grad], axis=0)
        og_ref[cols, :] = jnp.transpose(padded, (1, 0))
        right_ref[1, :, cols] = padded
        inner_ref[:, cols] = jnp.sum(
            out_ref[b].astype(f32) * grad.astype(f32), axis=0, keepdims=True
        )
    dq_ref[...] = jnp.zeros_like(dq_ref)

    def key_block(j, unused):
        rows = rows_at(j ^ rank, shard)
        seg_k = memory_segments(j ^ rank, shard, shard, rank, ends, 0)

        def query_block(i, total):
            at = i ^ (rank // pair)
            cols = rows_at(at, size)
            same = seg_k == memory_segments(at, size, shard, rank, ends, 1)
            kv = kv_ref[rows, :]
            scores = jnp.dot(kv, right_ref[0, :, cols], preferred_element_type=f32)
            grad_soft = jnp.dot(kv, right_ref[1, :, cols], preferred_element_type=f32)
            soft = jnp.where(same, jnp.exp(scores - log_ref[0, :, cols]), 0.0)
            grad_scores = (soft * (grad_soft - inner_ref[:, cols])).astype(bf16)
            total = total + jnp.dot(
                soft.astype(bf16), og_ref[cols, :], preferred_element_type=f32
            )
            total = total + jnp.dot(
                grad_scores, q0_ref[cols, :], preferred_element_type=f32
            )
            dq_ref[:, cols] += jnp.dot(
                kt_ref[:, rows], grad_scores, preferred_element_type=f32
            )
            return total

        low, high = block_span(j * shard, shard, size, ends)
        total = lax.fori_loop(low, high, query_block, jnp.zeros((shard, 2 * dim), f32))
        joint_ref[rows, : 2 * dim] = total.astype(bf16)
        return unused

    lax.fori_loop(0, blocks, key_block, 0)
    dq = (dq_ref[...] * HEAD_DIM ** (-0.5)).astype(bf16)
    joint_ref[:, 2 * dim :] = jnp.transpose(dq, (1, 0))


def attend_back(head, lens, rank, qt, kt, vt, out, logs, grads):
    blocks, width, size = out.shape
    slots = blocks * size
    dim = HEAD_DIM
    own = pl.BlockSpec((dim, slots), lambda i: (head, 0))
    return pl.pallas_call(
        backward_kernel,
        grid=(1,),
        out_shape=jax.ShapeDtypeStruct((slots, 3 * dim), bf16),
        in_specs=[SMEM, SMEM, own, own, own]
        + [
            pl.BlockSpec((blocks, dim, size), lambda i: (0, head, 0)),
            pl.BlockSpec((1, 1, slots), lambda i: (head, 0, 0)),
        ]
        + [pl.BlockSpec((dim, size), lambda i: (head, 0))] * blocks,
        out_specs=pl.BlockSpec((slots, 3 * dim), lambda i: (0, 0)),
        scratch_shapes=[pltpu.VMEM((slots, 2 * dim), bf16)] * 3
        + [
            pltpu.VMEM((2, 2 * dim, slots), bf16),
            pltpu.VMEM((1, slots), f32),
            pltpu.VMEM((dim, slots), f32),
        ],
        name="attend_back",
        compiler_params=pltpu.CompilerParams(vmem_limit_bytes=60 * 2**20),
        cost_estimate=pl.CostEstimate(
            flops=slots * slots * dim * 8, bytes_accessed=14 * slots * dim,
            transcendentals=slots * slots // 2,
        ),
    )(lens, rank, qt, kt, vt, out, logs, *grads)


def plan_kernel(capacity, lens_ref, rank_ref, routes_ref, order_ref, grad_ref,
                dispatch_ref, slots_ref):
    shard = routes_ref.shape[0]
    first = rank_ref[0, 0] * shard
    ends = item_ends(lens_ref)
    across = (shard, 128)
    chosen_col = routes_ref[...]
    chosen_row = jnp.transpose(jnp.broadcast_to(chosen_col, across), (1, 0))[0:1]
    order_row = order_ref[...]
    order_col = jnp.transpose(jnp.broadcast_to(order_row, (128, shard)), (1, 0))[:, 0:1]
    alive_row = segments_at(
        first + lax.broadcasted_iota(jnp.int32, (1, shard), 1), ends
    ) < len(ends)
    alive_col = segments_at(
        first + lax.broadcasted_iota(jnp.int32, (shard, 1), 0), ends
    ) < len(ends)
    ahead = (chosen_col == chosen_row) & (order_col < order_row) & alive_col
    ranked = jnp.sum(ahead.astype(jnp.int32), axis=0, keepdims=True)
    kept = alive_row & (ranked < capacity)
    slot = jnp.where(kept, chosen_row * capacity + ranked, -1)
    dispatch = (
        lax.broadcasted_iota(jnp.int32, dispatch_ref.shape, 0) == slot
    ).astype(f32).astype(bf16)
    dispatch_ref[...] = dispatch
    slots_ref[...] = jnp.dot(
        dispatch, grad_ref[...], preferred_element_type=f32
    ).astype(bf16)


def plan(lens, rank, routes, order, grads, capacity, experts_all):
    shard, width = grads.shape
    count = experts_all * capacity
    return pl.pallas_call(
        functools.partial(plan_kernel, capacity),
        out_shape=(
            jax.ShapeDtypeStruct((count, shard), bf16),
            jax.ShapeDtypeStruct((count, width), bf16),
        ),
        in_specs=[SMEM, SMEM, VMEM, VMEM, VMEM],
        out_specs=(VMEM, VMEM),
        name="plan",
        cost_estimate=pl.CostEstimate(
            flops=2 * count * shard * width, bytes_accessed=4 * shard * width,
            transcendentals=0,
        ),
    )(lens, rank, routes, order, grads)


def gelu_parts(values):
    below = 0.5 + 0.5 * lax.erf(values * (0.5**0.5))
    density = jnp.exp(-0.5 * values * values) * (0.5 / jnp.pi) ** 0.5
    return values * below, below + values * density


def expert_kernel(in_ref, grad_ref, up_ref, down_ref, act_ref, mid_ref, sum_ref):
    step = pl.program_id(0)
    pre = jnp.dot(in_ref[...], up_ref[...], preferred_element_type=f32)
    grad_act = lax.dot_general(
        grad_ref[...], down_ref[...], (((1,), (1,)), ((), ())),
        preferred_element_type=f32,
    )
    act, slope = gelu_parts(pre)
    act_ref[...] = act.astype(bf16)
    grad_pre = (grad_act * slope).astype(bf16)
    mid = lax.dot_general(
        grad_pre, up_ref[...], (((1,), (1,)), ((), ())), preferred_element_type=f32
    )

    @pl.when(step == 0)
    def first():
        sum_ref[...] = mid

    @pl.when(step > 0)
    def later():
        sum_ref[...] += mid

    @pl.when(step == pl.num_programs(0) - 1)
    def last():
        mid_ref[...] = sum_ref[...].astype(bf16)


def expert(rows, grads, up, down):
    count, width = rows.shape
    hidden = up.shape[1]
    size = min(512, hidden)
    return pl.pallas_call(
        expert_kernel,
        grid=(hidden // size,),
        out_shape=(
            jax.ShapeDtypeStruct((count, hidden), bf16),
            jax.ShapeDtypeStruct((count, width), bf16),
        ),
        in_specs=[
            pl.BlockSpec((count, width), lambda i: (0, 0)),
            pl.BlockSpec((count, width), lambda i: (0, 0)),
            pl.BlockSpec((width, size), lambda i: (0, i)),
            pl.BlockSpec((size, width), lambda i: (i, 0)),
        ],
        out_specs=(
            pl.BlockSpec((count, size), lambda i: (0, i)),
            pl.BlockSpec((count, width), lambda i: (0, 0)),
        ),
        scratch_shapes=[pltpu.VMEM((count, width), f32)],
        name="expert",
        cost_estimate=pl.CostEstimate(
            flops=6 * count * width * hidden, bytes_accessed=4 * width * hidden,
            transcendentals=2 * count * hidden,
        ),
    )(rows, grads, up, down)


def weight_kernel(rank_ref, in_ref, grad_ref, up_ref, down_ref, *refs):
    dup_ref, ddown_ref = refs[-2:]
    step = pl.program_id(1)
    pre = jnp.dot(in_ref[...], up_ref[...], preferred_element_type=f32)
    grad_act = lax.dot_general(
        grad_ref[...], down_ref[...], (((1,), (1,)), ((), ())),
        preferred_element_type=f32,
    )
    act, slope = gelu_parts(pre)
    dup = contract_rows(in_ref[...], (grad_act * slope).astype(bf16))
    ddown = contract_rows(act.astype(bf16), grad_ref[...])

    @pl.when(step == 0)
    def first():
        if len(refs) == 4:
            dup_ref[...] = refs[0][...] + dup
            ddown_ref[...] = refs[1][...] + ddown
        else:
            dup_ref[...] = dup
            ddown_ref[...] = ddown

    @pl.when(step > 0)
    def later():
        dup_ref[...] += dup
        ddown_ref[...] += ddown


def expert_weights(rank, rows, grads, up, down, parts, earlier=()):
    count, width = rows.shape
    hidden = up.shape[1] // parts
    size = min(384, hidden)
    chunk = min(512, count)
    blocks = hidden // size
    up_block = pl.BlockSpec((width, size), lambda i, j, r: (0, i))
    down_block = pl.BlockSpec((size, width), lambda i, j, r: (i, 0))
    return pl.pallas_call(
        weight_kernel,
        grid_spec=pltpu.PrefetchScalarGridSpec(
            num_scalar_prefetch=1,
            grid=(blocks, count // chunk),
            in_specs=[
                pl.BlockSpec((chunk, width), lambda i, j, r: (j, 0)),
                pl.BlockSpec((chunk, width), lambda i, j, r: (j, 0)),
                pl.BlockSpec((width, size), lambda i, j, r: (0, r[0] * blocks + i)),
                pl.BlockSpec((size, width), lambda i, j, r: (r[0] * blocks + i, 0)),
            ]
            + ([up_block, down_block] if earlier else []),
            out_specs=(up_block, down_block),
        ),
        out_shape=(
            jax.ShapeDtypeStruct((width, hidden), f32),
            jax.ShapeDtypeStruct((hidden, width), f32),
        ),
        name="expert_weights",
        cost_estimate=pl.CostEstimate(
            flops=8 * count * width * hidden, bytes_accessed=16 * width * hidden,
            transcendentals=2 * count * hidden,
        ),
    )(rank, rows, grads, up, down, *earlier)


def input_grad_kernel(a_ref, b_ref, *refs):
    joint_refs = refs[:-2]
    part_ref, sums_ref = refs[-2:]
    total = jnp.zeros((a_ref.shape[0], a_ref.shape[1]), f32)
    for h, joint_ref in enumerate(joint_refs):
        total = total + jnp.dot(joint_ref[...], b_ref[h], preferred_element_type=f32)
    part_ref[0] = total.astype(bf16)
    gains = jnp.sum(total * a_ref[...].astype(f32), axis=0, keepdims=True)
    shifts = jnp.sum(total, axis=0, keepdims=True)

    @pl.when(pl.program_id(0) == 0)
    def first():
        sums_ref[0:1] = gains
        sums_ref[1:2] = shifts

    @pl.when(pl.program_id(0) > 0)
    def later():
        sums_ref[0:1] += gains
        sums_ref[1:2] += shifts


def input_grad(normed, turned, joints, start, count, blocks):
    slots, width = normed.shape
    size = slots // blocks
    cols = joints[0].shape[1]
    return pl.pallas_call(
        input_grad_kernel,
        grid=(count,),
        out_shape=(
            jax.ShapeDtypeStruct((count, size, width), bf16),
            jax.ShapeDtypeStruct((2, width), f32),
        ),
        in_specs=[
            pl.BlockSpec((size, width), lambda i: (start + i, 0)),
            pl.BlockSpec(turned.shape, lambda i: (0, 0, 0)),
        ]
        + [pl.BlockSpec((size, cols), lambda i: (start + i, 0))] * len(joints),
        out_specs=(
            pl.BlockSpec((1, size, width), lambda i: (i, 0, 0)),
            pl.BlockSpec((2, width), lambda i: (0, 0)),
        ),
        name="input_grad",
        cost_estimate=pl.CostEstimate(
            flops=2 * count * size * width * cols * len(joints),
            bytes_accessed=6 * count * size * width, transcendentals=0,
        ),
    )(normed, turned, *joints)


def sum_halves(values, axis):
    low_bit = lax.axis_index(axis) & 1
    half = values.shape[0] // 2
    own = lax.dynamic_slice_in_dim(values, low_bit * half, half)
    away = lax.dynamic_slice_in_dim(values, (1 - low_bit) * half, half)
    for step in steps_of(lax.axis_size(axis)):
        arrived = swap(away if step == 1 else own, axis, step)
        own = (own.astype(f32) + arrived.astype(f32)).astype(bf16)
    return own, swap(own, axis, 1)


def finish_kernel(bit_ref, *refs):
    own_refs, other_refs = refs[:-4][0::2], refs[:-4][1::2]
    query_ref, key_ref, value_ref, output_ref = refs[-4:]
    bit = bit_ref[0, 0]
    for place, group in ((bit, own_refs), (1 - bit, other_refs)):
        out_half = group[0].shape[0]
        output_ref[rows_at(place, out_half), :] = group[0][...].astype(f32)
        half = group[1].shape[0]
        for target, start in ((key_ref, 0), (value_ref, 1), (query_ref, 2)):
            part = slice(start * HEAD_DIM, (start + 1) * HEAD_DIM)
            target[rows_at(place, half), :] = jnp.concatenate(
                [ref[:, part].astype(f32) for ref in group[1:]], axis=1
            )


def finish(bit, pieces):
    out_half, width = pieces[0][0].shape
    half, cols = pieces[1][0].shape
    wide = jax.ShapeDtypeStruct((2 * half, cols // 3 * (len(pieces) - 1)), f32)
    flat = [half_piece for piece in pieces for half_piece in piece]
    return pl.pallas_call(
        finish_kernel,
        out_shape=(wide, wide, wide, jax.ShapeDtypeStruct((2 * out_half, width), f32)),
        in_specs=[SMEM] + [VMEM] * len(flat),
        out_specs=(VMEM,) * 4,
        name="finish",
    )(bit, *flat)


def sum_small(values, axes):
    for axis in axes:
        for step in steps_of(lax.axis_size(axis)):
            values = values + swap(values, axis, step)
    return values


def on_device(
    tokens,
    first_gain,
    first_bias,
    query_weight,
    key_weight,
    value_weight,
    output_weight,
    second_gain,
    second_bias,
    expert_up,
    expert_down,
    item_lengths,
    routes,
    slot_order,
    cotangent,
):
    slots_all, width = tokens.shape
    members = lax.axis_size("tensor")
    shard_rows = slots_all // members
    rank = lax.axis_index("tensor")
    sources = lax.axis_size("dp")
    experts_all = sources * expert_up.shape[0]
    capacity = shard_rows // experts_all
    head_cols = query_weight.shape[1]
    heads = head_cols // HEAD_DIM
    up_matrix = expert_up[0]
    down_matrix = expert_down[0]
    rank_cell = rank.astype(jnp.int32).reshape(1, 1)

    def exchange(rows):
        return lax.all_to_all(
            rows.reshape(sources, -1, width), "dp", split_axis=0, concat_axis=0, tiled=True
        ).reshape(-1, width)

    dispatch, grad_slots = plan(
        item_lengths, rank_cell, routes, slot_order, cotangent, capacity, experts_all
    )
    flat_grad = exchange(grad_slots)
    output_x = jnp.concatenate(
        [output_weight]
        + [swap(output_weight, "tensor", k) for k in range(1, members)]
    )

    normed_in, qt, kt, vt = project(
        rank_cell[0], tokens, first_gain, first_bias,
        query_weight, key_weight, value_weight, members,
    )
    heads_t, logs = attend(item_lengths, rank_cell, qt, kt, vt, members)
    heads_x = jnp.concatenate(
        [heads_t[0]] + [swap(heads_t[j], "tensor", j) for j in range(1, members)]
    )
    tokens_mine = lax.dynamic_slice_in_dim(tokens, rank * shard_rows, shard_rows).astype(f32)
    residual = tokens_mine + contract_rows(heads_x, output_x)
    normed_low = layer_norm(residual, second_gain, second_bias).astype(bf16)
    outgoing = jnp.dot(dispatch, normed_low, preferred_element_type=f32).astype(bf16)
    flat_in = exchange(outgoing)

    flat_grad, unused = lax.optimization_barrier((flat_grad, outgoing))
    act, grad_mid = expert(flat_in, flat_grad, up_matrix, down_matrix)
    grad_back = exchange(grad_mid)
    gathered = [(flat_in, flat_grad)]
    for step in reversed(steps_of(members)):
        gathered = gathered + [
            (swap(a, "tensor", step), swap(b, "tensor", step)) for a, b in gathered
        ]
    sums = ()
    for group in (gathered[0::2], gathered[1::2]):
        sums = expert_weights(
            rank_cell[0],
            jnp.concatenate([a for a, b in group]),
            jnp.concatenate([b for a, b in group]),
            up_matrix, down_matrix, members, sums,
        )
    up_grad, down_grad = sums
    grad_back, up_grad, down_grad = lax.optimization_barrier((grad_back, up_grad, down_grad))

    grad_normed = contract_rows(dispatch, grad_back)
    unused_mid, pull_mid = jax.vjp(layer_norm, residual, second_gain, second_bias)
    grad_res_norm, second_gain_part, second_bias_part = pull_mid(grad_normed)
    grad_res = cotangent.astype(f32) + grad_res_norm
    grad_low = grad_res.astype(bf16)
    places = rank * shard_rows + jnp.arange(shard_rows, dtype=jnp.int32)
    alive_mine = places < jnp.sum(item_lengths)
    grad_heads = (
        lax.dot_general(
            output_x, grad_low, (((1,), (1,)), ((), ())), preferred_element_type=f32
        )
        * alive_mine[None, :].astype(f32)
    ).astype(bf16)
    grad_parts = [grad_heads[:head_cols]] + [
        swap(grad_heads[j * head_cols : (j + 1) * head_cols], "tensor", j)
        for j in range(1, members)
    ]
    made = jnp.dot(act, down_matrix, preferred_element_type=f32).astype(bf16)
    output_part = jnp.dot(heads_x, grad_low, preferred_element_type=f32).astype(bf16)
    grad_parts, made, output_part = lax.optimization_barrier((grad_parts, made, output_part))
    returned = exchange(made)

    output_mine = output_part[:head_cols].astype(f32)
    for j in range(1, members):
        output_mine = output_mine + swap(
            output_part[j * head_cols : (j + 1) * head_cols], "tensor", j
        ).astype(f32)
    pieces = [sum_halves(output_mine.astype(bf16), "dp")]
    joints = []
    for h in range(heads):
        joint = attend_back(
            h, item_lengths, rank_cell, qt, kt, vt, heads_t, logs, grad_parts
        )
        joints.append(joint)
        pieces.append(sum_halves(contract_rows(normed_in, joint).astype(bf16), "dp"))

    stacked = jnp.stack([key_weight, value_weight, query_weight])
    turned = (
        stacked.reshape(3, width, heads, HEAD_DIM)
        .transpose(2, 0, 3, 1)
        .reshape(heads, 3 * HEAD_DIM, width)
    )
    far = members // 2
    away, sums_far = input_grad(normed_in, turned, joints, far, members - far, members)
    home, sums_near = input_grad(normed_in, turned, joints, 0, far, members)
    partial = [home[j] for j in range(far)] + [away[j] for j in range(members - far)]
    for step in steps_of(members):
        partial = [
            (a.astype(f32) + swap(b, "tensor", step).astype(f32)).astype(
                bf16 if 2 * step < members else f32
            )
            for a, b in zip(partial[0::2], partial[1::2])
        ]
    grad_in = partial[0]
    unused_first, pull_first = jax.vjp(
        lambda values: layer_norm(values, first_gain, first_bias), tokens_mine
    )
    token_grad = grad_res + pull_first(grad_in)[0]

    sums_first = sums_far + sums_near
    first_bias_part = sums_first[1]
    first_gain_part = (sums_first[0] - first_bias * first_bias_part) / first_gain
    norm_sums = sum_small(
        jnp.stack([first_gain_part, first_bias_part, second_gain_part, second_bias_part]),
        ("tensor", "dp"),
    )
    block_out = residual + contract_rows(dispatch, returned)
    bit_cell = (lax.axis_index("dp") & 1).astype(jnp.int32).reshape(1, 1)
    query_grad, key_grad, value_grad, output_grad = finish(bit_cell, pieces)
    return (
        block_out,
        token_grad,
        norm_sums[0],
        norm_sums[1],
        query_grad,
        key_grad,
        value_grad,
        output_grad,
        norm_sums[2],
        norm_sums[3],
        up_grad[None],
        down_grad[None],
    )


def solution(mesh):
    in_specs = (
        P("dp", None),
        P(),
        P(),
        P(None, "tensor"),
        P(None, "tensor"),
        P(None, "tensor"),
        P("tensor", None),
        P(),
        P(),
        P("dp", None, None),
        P("dp", None, None),
        P("dp", None),
        P(("dp", "tensor"), None),
        P(("dp", "tensor"), None),
        P(("dp", "tensor"), None),
    )
    out_specs = (
        P(("dp", "tensor"), None),
        P(("dp", "tensor"), None),
        P(),
        P(),
        P(None, "tensor"),
        P(None, "tensor"),
        P(None, "tensor"),
        P("tensor", None),
        P(),
        P(),
        P("dp", None, "tensor"),
        P("dp", "tensor", None),
    )
    return jax.shard_map(
        on_device, mesh=mesh, in_specs=in_specs, out_specs=out_specs, check_vma=False
    )
```

```python
import functools

import jax
import jax.numpy as jnp
from jax import lax
from jax.experimental import pallas as pl
from jax.experimental.pallas import tpu as pltpu
from jax.sharding import PartitionSpec as P

HEAD_DIM = 64
EPSILON = 1e-05
NEGATIVE = -1e30
f32 = jnp.float32
bf16 = jnp.bfloat16
VMEM = pl.BlockSpec(memory_space=pltpu.VMEM)
SMEM = pl.BlockSpec(memory_space=pltpu.SMEM)


def layer_norm(values, gain, shift):
    average = jnp.mean(values, axis=-1, keepdims=True)
    centred = values - average
    variance = jnp.mean(centred * centred, axis=-1, keepdims=True)
    return centred * lax.rsqrt(variance + EPSILON) * gain + shift


def contract_rows(left, right):
    return lax.dot_general(
        left, right, (((0,), (0,)), ((), ())), preferred_element_type=f32
    )


def swap(values, axis, step):
    count = lax.axis_size(axis)
    return lax.ppermute(values, axis, [(i, i ^ step) for i in range(count)])


def steps_of(count):
    steps = []
    step = 1
    while step < count:
        steps.append(step)
        step *= 2
    return steps


def normalized(values):
    average = jnp.mean(values, axis=-1, keepdims=True)
    centred = values - average
    variance = jnp.mean(centred * centred, axis=-1, keepdims=True)
    return centred * lax.rsqrt(variance + EPSILON)


def project_kernel(
    rank_ref, tokens_ref, gain_ref, bias_ref, qw_ref, kw_ref, vw_ref,
    normed_ref, qt_ref, kt_ref, vt_ref,
):
    values = tokens_ref[...].astype(f32)
    normed = (normalized(values) * gain_ref[...] + bias_ref[...]).astype(bf16)
    normed_ref[...] = normed
    for weight_ref, out_ref, factor in (
        (qw_ref, qt_ref, HEAD_DIM ** (-0.5)), (kw_ref, kt_ref, None), (vw_ref, vt_ref, None)
    ):
        made = lax.dot_general(
            weight_ref[...], normed, (((1,), (1,)), ((), ())), preferred_element_type=f32
        ).astype(bf16)
        if factor is not None:
            made = made * jnp.asarray(factor, bf16)
        out_ref[...] = made


def project(rank, tokens, gain, bias, qw, kw, vw, blocks):
    slots, width = tokens.shape
    cols = qw.shape[0]
    size = slots // blocks
    fixed = lambda i, r: (0, 0)
    return pl.pallas_call(
        project_kernel,
        grid_spec=pltpu.PrefetchScalarGridSpec(
            num_scalar_prefetch=1,
            grid=(blocks,),
            in_specs=[
                pl.BlockSpec((size, width), lambda i, r: (i ^ r[0], 0)),
                pl.BlockSpec((1, width), fixed),
                pl.BlockSpec((1, width), fixed),
                pl.BlockSpec((cols, width), fixed),
                pl.BlockSpec((cols, width), fixed),
                pl.BlockSpec((cols, width), fixed),
            ],
            out_specs=(
                pl.BlockSpec((size, width), lambda i, r: (i, 0)),
                pl.BlockSpec((cols, size), lambda i, r: (0, i)),
                pl.BlockSpec((cols, size), lambda i, r: (0, i)),
                pl.BlockSpec((cols, size), lambda i, r: (0, i)),
            ),
        ),
        out_shape=(jax.ShapeDtypeStruct((slots, width), bf16),)
        + (jax.ShapeDtypeStruct((cols, slots), bf16),) * 3,
        name="project",
        cost_estimate=pl.CostEstimate(
            flops=6 * slots * width * cols, bytes_accessed=6 * slots * width,
            transcendentals=slots,
        ),
    )(rank, tokens, gain[None], bias[None], qw, kw, vw)


def item_ends(lens_ref):
    ends = []
    total = jnp.int32(0)
    for i in range(lens_ref.shape[1]):
        total = total + lens_ref[0, i]
        ends.append(total)
    return ends


def segments_at(place, ends):
    segment = jnp.zeros_like(place)
    for end in ends:
        segment = segment + (place >= end).astype(jnp.int32)
    return segment


def block_span(first, size, unit, ends):
    last = jnp.minimum(first + size, ends[-1]) - 1
    low = jnp.int32(0)
    high = ends[-1]
    for end in ends:
        low = jnp.where(first >= end, end, low)
    for end in reversed(ends):
        high = jnp.where(last < end, end, high)
    empty = first >= ends[-1]
    low_block = jnp.where(empty, 0, low // unit)
    high_block = jnp.where(empty, 0, (high + unit - 1) // unit)
    return low_block, high_block


def rows_at(block, size):
    return pl.ds(pl.multiple_of(block * size, size), size)


def memory_segments(block, size, shard, rank, ends, axis):
    shape = (1, size) if axis else (size, 1)
    at = block * size + lax.broadcasted_iota(jnp.int32, shape, axis)
    place = ((at // shard) ^ rank) * shard + at % shard
    return segments_at(place, ends)


def lane_masked(values, head):
    lane = lax.broadcasted_iota(jnp.int32, values.shape, 1)
    inside = (lane >= head * HEAD_DIM) & (lane < (head + 1) * HEAD_DIM)
    return jnp.where(inside, values, jnp.zeros_like(values))


def forward_kernel(
    lens_ref, rank_ref, qt_ref, kt_ref, vt_ref, out_ref, log_ref, masked_ref
):
    blocks, width, shard = out_ref.shape
    heads = width // HEAD_DIM
    pair = 1
    size = shard * pair
    rank = rank_ref[0, 0]
    ends = item_ends(lens_ref)
    keys = jnp.transpose(kt_ref[...], (1, 0))
    for h in range(heads):
        masked_ref[h] = lane_masked(keys, h)

    def query_block(i, unused):
        at = i ^ (rank // pair)
        cols = rows_at(at, size)
        seg_q = memory_segments(at, size, shard, rank, ends, 1)
        queries = qt_ref[:, cols]

        def key_block(j, carry):
            rows = rows_at(j ^ rank, shard)
            seg_k = memory_segments(j ^ rank, shard, shard, rank, ends, 0)
            same = seg_k == seg_q
            result = []
            for h in range(heads):
                highest, summed, total = carry[h]
                scores = jnp.dot(
                    masked_ref[h, rows, :], queries, preferred_element_type=f32
                )
                scores = jnp.where(same, scores, NEGATIVE)
                raised = jnp.maximum(highest, jnp.max(scores, axis=0, keepdims=True))
                shrink = jnp.exp(highest - raised)
                soft = jnp.exp(scores - raised)
                summed = summed * shrink + jnp.sum(soft, axis=0, keepdims=True)
                total = total * shrink + jnp.dot(
                    vt_ref[pl.ds(h * HEAD_DIM, HEAD_DIM), rows],
                    soft.astype(bf16),
                    preferred_element_type=f32,
                )
                result.append((raised, summed, total))
            return tuple(result)

        start = tuple(
            (
                jnp.full((1, size), NEGATIVE, f32),
                jnp.zeros((1, size), f32),
                jnp.zeros((HEAD_DIM, size), f32),
            )
            for h in range(heads)
        )
        low, high = block_span(i * size, size, shard, ends)
        done = lax.fori_loop(low, high, key_block, start)
        live = seg_q < len(ends)
        for h in range(heads):
            highest, summed, total = done[h]
            summed = jnp.where(live, summed, 1.0)
            result = jnp.where(live, total / summed, 0.0).astype(bf16)
            logs = jnp.where(live, highest + jnp.log(summed), -NEGATIVE)
            for p in range(pair):
                part = slice(p * shard, (p + 1) * shard)
                out_ref[at * pair + p, pl.ds(h * HEAD_DIM, HEAD_DIM), :] = result[:, part]
            log_ref[h, :, cols] = logs
        return unused

    lax.fori_loop(0, blocks // pair, query_block, 0)


def attend(lens, rank, qt, kt, vt, blocks):
    width, slots = qt.shape
    size = slots // blocks
    heads = width // HEAD_DIM
    return pl.pallas_call(
        forward_kernel,
        out_shape=(
            jax.ShapeDtypeStruct((blocks, width, size), bf16),
            jax.ShapeDtypeStruct((heads, 1, slots), f32),
        ),
        in_specs=[SMEM, SMEM, VMEM, VMEM, VMEM],
        out_specs=(VMEM, VMEM),
        scratch_shapes=[pltpu.VMEM((heads, slots, width), bf16)],
        name="attend",
        compiler_params=pltpu.CompilerParams(vmem_limit_bytes=60 * 2**20),
        cost_estimate=pl.CostEstimate(
            flops=slots * slots * width * 3, bytes_accessed=6 * slots * width,
            transcendentals=slots * slots * heads // 2,
        ),
    )(lens, rank, qt, kt, vt)


def backward_kernel(
    first_head, heads, lens_ref, rank_ref, qt_ref, kt_ref, vt_ref, out_ref, log_ref, *rest
):
    blocks, width, shard = out_ref.shape
    dim = HEAD_DIM
    grad_refs = rest[:blocks]
    joint_ref, kv_ref, q0_ref, og_ref, right_ref, inner_ref, dq_ref = rest[blocks:]
    slots = blocks * shard
    unit = shard // 2
    rank = rank_ref[0, 0]
    ends = item_ends(lens_ref)
    zero = jnp.zeros((dim, slots), bf16)
    for n in range(heads):
        part = slice((first_head + n) * dim, (first_head + n + 1) * dim)
        both = jnp.concatenate([kt_ref[part, :], vt_ref[part, :]], axis=0)
        kv_ref[n] = jnp.transpose(both, (1, 0))
        padded = jnp.concatenate([qt_ref[part, :], zero], axis=0)
        q0_ref[n] = jnp.transpose(padded, (1, 0))
        right_ref[n, 0] = padded
        for b in range(blocks):
            grad = grad_refs[b][part, :]
            cols = slice(b * shard, (b + 1) * shard)
            padded = jnp.concatenate([zero[:, :shard], grad], axis=0)
            og_ref[n, cols, :] = jnp.transpose(padded, (1, 0))
            right_ref[n, 1, :, cols] = padded
            inner_ref[n, :, cols] = jnp.sum(
                out_ref[b, part, :].astype(f32) * grad.astype(f32), axis=0, keepdims=True
            )
    dq_ref[...] = jnp.zeros_like(dq_ref)

    def key_block(j, unused):
        at_key = ((j // 2) ^ rank) * 2 + j % 2
        rows = rows_at(at_key, unit)
        seg_k = memory_segments(at_key, unit, shard, rank, ends, 0)

        def query_block(i, totals):
            at = i ^ rank
            cols = rows_at(at, shard)
            same = seg_k == memory_segments(at, shard, shard, rank, ends, 1)
            result = []
            for n in range(heads):
                head = first_head + n
                kv = kv_ref[n, rows, :]
                scores = jnp.dot(kv, right_ref[n, 0, :, cols], preferred_element_type=f32)
                grad_soft = jnp.dot(kv, right_ref[n, 1, :, cols], preferred_element_type=f32)
                soft = jnp.where(same, jnp.exp(scores - log_ref[head, :, cols]), 0.0)
                grad_scores = (soft * (grad_soft - inner_ref[n, :, cols])).astype(bf16)
                total = totals[n] + jnp.dot(
                    soft.astype(bf16), og_ref[n, cols, :], preferred_element_type=f32
                )
                total = total + jnp.dot(
                    grad_scores, q0_ref[n, cols, :], preferred_element_type=f32
                )
                dq_ref[n, :, cols] += jnp.dot(
                    kt_ref[pl.ds(head * dim, dim), rows], grad_scores,
                    preferred_element_type=f32,
                )
                result.append(total)
            return tuple(result)

        low, high = block_span(j * unit, unit, shard, ends)
        start = (jnp.zeros((unit, 2 * dim), f32),) * heads
        totals = lax.fori_loop(low, high, query_block, start)
        for n in range(heads):
            joint_ref[rows, 2 * dim * n : 2 * dim * (n + 1)] = totals[n].astype(bf16)
        return unused

    lax.fori_loop(0, 2 * blocks, key_block, 0)
    dq = (dq_ref[...] * dim ** (-0.5)).astype(bf16).reshape(heads * dim, slots)
    joint_ref[:, 2 * dim * heads :] = jnp.transpose(dq, (1, 0))


def attend_back(first_head, heads, lens, rank, qt, kt, vt, out, logs, grads):
    blocks, width, size = out.shape
    slots = blocks * size
    dim = HEAD_DIM
    return pl.pallas_call(
        functools.partial(backward_kernel, first_head, heads),
        out_shape=jax.ShapeDtypeStruct((slots, 3 * dim * heads), bf16),
        in_specs=[SMEM, SMEM] + [VMEM] * (5 + blocks),
        out_specs=VMEM,
        scratch_shapes=[pltpu.VMEM((heads, slots, 2 * dim), bf16)] * 3
        + [
            pltpu.VMEM((heads, 2, 2 * dim, slots), bf16),
            pltpu.VMEM((heads, 1, slots), f32),
            pltpu.VMEM((heads, dim, slots), f32),
        ],
        name="attend_back",
        compiler_params=pltpu.CompilerParams(vmem_limit_bytes=60 * 2**20),
        cost_estimate=pl.CostEstimate(
            flops=slots * slots * dim * heads * 8, bytes_accessed=14 * slots * dim * heads,
            transcendentals=slots * slots * heads // 2,
        ),
    )(lens, rank, qt, kt, vt, out, logs, *grads)


def plan_kernel(capacity, lens_ref, rank_ref, routes_ref, order_ref, grad_ref,
                dispatch_ref, slots_ref):
    shard = routes_ref.shape[1]
    first = rank_ref[0, 0] * shard
    ends = item_ends(lens_ref)
    chosen_row = routes_ref[...]
    chosen_col = jnp.transpose(jnp.broadcast_to(chosen_row, (128, shard)), (1, 0))[:, 0:1]
    order_row = order_ref[...]
    order_col = jnp.transpose(jnp.broadcast_to(order_row, (128, shard)), (1, 0))[:, 0:1]
    alive_row = segments_at(
        first + lax.broadcasted_iota(jnp.int32, (1, shard), 1), ends
    ) < len(ends)
    alive_col = segments_at(
        first + lax.broadcasted_iota(jnp.int32, (shard, 1), 0), ends
    ) < len(ends)
    ahead = (chosen_col == chosen_row) & (order_col < order_row) & alive_col
    ranked = jnp.sum(ahead.astype(jnp.int32), axis=0, keepdims=True)
    kept = alive_row & (ranked < capacity)
    slot = jnp.where(kept, chosen_row * capacity + ranked, -1)
    dispatch = (
        lax.broadcasted_iota(jnp.int32, dispatch_ref.shape, 0) == slot
    ).astype(f32).astype(bf16)
    dispatch_ref[...] = dispatch
    slots_ref[...] = jnp.dot(
        dispatch, grad_ref[...], preferred_element_type=f32
    ).astype(bf16)


def plan(lens, rank, routes, order, grads, capacity, experts_all):
    shard, width = grads.shape
    count = experts_all * capacity
    return pl.pallas_call(
        functools.partial(plan_kernel, capacity),
        out_shape=(
            jax.ShapeDtypeStruct((count, shard), bf16),
            jax.ShapeDtypeStruct((count, width), bf16),
        ),
        in_specs=[SMEM, SMEM, VMEM, VMEM, VMEM],
        out_specs=(VMEM, VMEM),
        name="plan",
        cost_estimate=pl.CostEstimate(
            flops=2 * count * shard * width, bytes_accessed=4 * shard * width,
            transcendentals=0,
        ),
    )(lens, rank, routes.reshape(1, -1), order, grads)


def gelu_parts(values):
    below = 0.5 + 0.5 * lax.erf(values * (0.5**0.5))
    density = jnp.exp(-0.5 * values * values) * (0.5 / jnp.pi) ** 0.5
    return values * below, below + values * density


def expert_kernel(in_ref, grad_act_ref, up_ref, act_ref, mid_ref, sum_ref):
    step = pl.program_id(0)
    pre = jnp.dot(in_ref[...], up_ref[...], preferred_element_type=f32)
    act, slope = gelu_parts(pre)
    act_ref[...] = act.astype(bf16)
    grad_pre = (grad_act_ref[...] * slope).astype(bf16)
    mid = lax.dot_general(
        grad_pre, up_ref[...], (((1,), (1,)), ((), ())), preferred_element_type=f32
    )

    @pl.when(step == 0)
    def first():
        sum_ref[...] = mid

    @pl.when(step > 0)
    def later():
        sum_ref[...] += mid

    @pl.when(step == pl.num_programs(0) - 1)
    def last():
        mid_ref[...] = sum_ref[...].astype(bf16)


def expert(rows, grad_act, up):
    count, width = rows.shape
    hidden = up.shape[1]
    size = min(512, hidden)
    return pl.pallas_call(
        expert_kernel,
        grid=(hidden // size,),
        out_shape=(
            jax.ShapeDtypeStruct((count, hidden), bf16),
            jax.ShapeDtypeStruct((count, width), bf16),
        ),
        in_specs=[
            pl.BlockSpec((count, width), lambda i: (0, 0)),
            pl.BlockSpec((count, size), lambda i: (0, i)),
            pl.BlockSpec((width, size), lambda i: (0, i)),
        ],
        out_specs=(
            pl.BlockSpec((count, size), lambda i: (0, i)),
            pl.BlockSpec((count, width), lambda i: (0, 0)),
        ),
        scratch_shapes=[pltpu.VMEM((count, width), f32)],
        name="expert",
        cost_estimate=pl.CostEstimate(
            flops=4 * count * width * hidden, bytes_accessed=4 * width * hidden,
            transcendentals=2 * count * hidden,
        ),
    )(rows, grad_act, up)


def product_kernel(a_ref, b_ref, out_ref, sum_ref):
    step = pl.program_id(0)
    made = jnp.dot(a_ref[...], b_ref[...], preferred_element_type=f32)

    @pl.when(step == 0)
    def first():
        sum_ref[...] = made

    @pl.when(step > 0)
    def later():
        sum_ref[...] += made

    @pl.when(step == pl.num_programs(0) - 1)
    def last():
        out_ref[...] = sum_ref[...].astype(bf16)


def product(a, b):
    count, depth = a.shape
    width = b.shape[1]
    size = min(1024, depth)
    return pl.pallas_call(
        product_kernel,
        grid=(depth // size,),
        out_shape=jax.ShapeDtypeStruct((count, width), bf16),
        in_specs=[
            pl.BlockSpec((count, size), lambda i: (0, i)),
            pl.BlockSpec((size, width), lambda i: (i, 0)),
        ],
        out_specs=pl.BlockSpec((count, width), lambda i: (0, 0)),
        scratch_shapes=[pltpu.VMEM((count, width), f32)],
        name="product",
        cost_estimate=pl.CostEstimate(
            flops=2 * count * width * depth, bytes_accessed=2 * width * depth,
            transcendentals=0,
        ),
    )(a, b)


def weight_kernel(groups, rank_ref, up_ref, down_ref, *refs):
    dup_ref, ddown_ref = refs[-2:]
    dup = ddown = 0.0
    for g in range(groups):
        in_ref, grad_ref = refs[2 * g : 2 * g + 2]
        pre = jnp.dot(in_ref[...], up_ref[...], preferred_element_type=f32)
        grad_act = lax.dot_general(
            grad_ref[...], down_ref[...], (((1,), (1,)), ((), ())),
            preferred_element_type=f32,
        )
        act, slope = gelu_parts(pre)
        dup = dup + contract_rows(in_ref[...], (grad_act * slope).astype(bf16))
        ddown = ddown + contract_rows(act.astype(bf16), grad_ref[...])
    if len(refs) > 2 * groups + 2:
        dup = dup + refs[2 * groups][...]
        ddown = ddown + refs[2 * groups + 1][...]
    dup_ref[...] = dup
    ddown_ref[...] = ddown


def expert_weights(rank, group, up, down, parts, earlier=()):
    count, width = group[0][0].shape
    hidden = up.shape[1] // parts
    size = min(256, hidden)
    blocks = hidden // size
    up_block = pl.BlockSpec((width, size), lambda i, r: (0, i))
    down_block = pl.BlockSpec((size, width), lambda i, r: (i, 0))
    rows = [values for both in group for values in both]
    return pl.pallas_call(
        functools.partial(weight_kernel, len(group)),
        grid_spec=pltpu.PrefetchScalarGridSpec(
            num_scalar_prefetch=1,
            grid=(blocks,),
            in_specs=[
                pl.BlockSpec((width, size), lambda i, r: (0, r[0] * blocks + i)),
                pl.BlockSpec((size, width), lambda i, r: (r[0] * blocks + i, 0)),
            ]
            + [pl.BlockSpec((count, width), lambda i, r: (0, 0))] * len(rows)
            + ([up_block, down_block] if earlier else []),
            out_specs=(up_block, down_block),
        ),
        out_shape=(
            jax.ShapeDtypeStruct((width, hidden), f32),
            jax.ShapeDtypeStruct((hidden, width), f32),
        ),
        name="expert_weights",
        cost_estimate=pl.CostEstimate(
            flops=8 * count * width * hidden * len(group),
            bytes_accessed=16 * width * hidden,
            transcendentals=2 * count * hidden * len(group),
        ),
    )(rank, up, down, *rows, *earlier)


def input_grad_kernel(groups, normed_ref, qw_ref, kw_ref, vw_ref, *refs):
    joint_refs = refs[: len(groups)]
    part_ref, sums_ref, turned_ref = refs[len(groups) :]
    step = pl.program_id(0)
    dim = HEAD_DIM

    @pl.when(step == 0)
    def stack():
        at = 0
        for first_head, heads in groups:
            for n in range(first_head, first_head + heads):
                part = slice(n * dim, (n + 1) * dim)
                turned_ref[at : at + dim, :] = kw_ref[part, :]
                turned_ref[at + dim : at + 2 * dim, :] = vw_ref[part, :]
                at += 2 * dim
            part = slice(first_head * dim, (first_head + heads) * dim)
            turned_ref[at : at + heads * dim, :] = qw_ref[part, :]
            at += heads * dim

    total = 0.0
    at = 0
    for joint_ref in joint_refs:
        rows = slice(at, at + joint_ref.shape[1])
        total = total + jnp.dot(
            joint_ref[...], turned_ref[rows, :], preferred_element_type=f32
        )
        at += joint_ref.shape[1]
    part_ref[0] = total.astype(bf16)
    gains = jnp.sum(total * normed_ref[...].astype(f32), axis=0, keepdims=True)
    shifts = jnp.sum(total, axis=0, keepdims=True)

    @pl.when(step == 0)
    def first():
        sums_ref[0:1] = gains
        sums_ref[1:2] = shifts

    @pl.when(step > 0)
    def later():
        sums_ref[0:1] += gains
        sums_ref[1:2] += shifts


def input_grad(groups, normed, qw, kw, vw, joints, blocks):
    slots, width = normed.shape
    size = slots // blocks
    cols = qw.shape[0]
    fixed = pl.BlockSpec((cols, width), lambda i: (0, 0))
    far = blocks // 2
    return pl.pallas_call(
        functools.partial(input_grad_kernel, groups),
        grid=(blocks,),
        out_shape=(
            jax.ShapeDtypeStruct((blocks, size, width), bf16),
            jax.ShapeDtypeStruct((2, width), f32),
        ),
        in_specs=[pl.BlockSpec((size, width), lambda i: (i, 0)), fixed, fixed, fixed]
        + [pl.BlockSpec((size, joint.shape[1]), lambda i: (i, 0)) for joint in joints],
        out_specs=(
            pl.BlockSpec((1, size, width), lambda i: ((i % 2) * far + i // 2, 0, 0)),
            pl.BlockSpec((2, width), lambda i: (0, 0)),
        ),
        scratch_shapes=[pltpu.VMEM((3 * cols, width), bf16)],
        name="input_grad",
        cost_estimate=pl.CostEstimate(
            flops=6 * slots * width * cols,
            bytes_accessed=6 * slots * width, transcendentals=0,
        ),
    )(normed, qw, kw, vw, *joints)


def sum_halves(values, axis):
    low_bit = lax.axis_index(axis) & 1
    half = values.shape[0] // 2
    own = lax.dynamic_slice_in_dim(values, low_bit * half, half)
    away = lax.dynamic_slice_in_dim(values, (1 - low_bit) * half, half)
    for step in steps_of(lax.axis_size(axis)):
        arrived = swap(away if step == 1 else own, axis, step)
        own = (own.astype(f32) + arrived.astype(f32)).astype(bf16)
    return own, swap(own, axis, 1)


def finish_kernel(groups, bit_ref, *refs):
    pieces = refs[: 2 * len(groups)]
    outs = refs[2 * len(groups) : 2 * len(groups) + 3]
    whole_refs = refs[2 * len(groups) + 3 :]
    query_ref, key_ref, value_ref = outs
    dim = HEAD_DIM
    bit = bit_ref[0, 0]
    for g, (first_head, heads) in enumerate(groups):
        whole_ref = whole_refs[g]
        half = whole_ref.shape[0] // 2
        whole_ref[rows_at(bit, half), :] = pieces[2 * g][...].astype(f32)
        whole_ref[rows_at(1 - bit, half), :] = pieces[2 * g + 1][...].astype(f32)
        at = 0
        for n in range(first_head, first_head + heads):
            part = slice(n * dim, (n + 1) * dim)
            key_ref[part, :] = whole_ref[at : at + dim, :]
            value_ref[part, :] = whole_ref[at + dim : at + 2 * dim, :]
            at += 2 * dim
        part = slice(first_head * dim, (first_head + heads) * dim)
        query_ref[part, :] = whole_ref[at : at + heads * dim, :]


def finish(groups, bit, pieces):
    width = pieces[0][0].shape[1]
    cols = sum(heads for first_head, heads in groups) * HEAD_DIM
    flat = [half_piece for piece in pieces for half_piece in piece]
    return pl.pallas_call(
        functools.partial(finish_kernel, groups),
        out_shape=(jax.ShapeDtypeStruct((cols, width), f32),) * 3,
        in_specs=[SMEM] + [VMEM] * len(flat),
        out_specs=(VMEM,) * 3,
        scratch_shapes=[
            pltpu.VMEM((3 * heads * HEAD_DIM, width), f32) for first_head, heads in groups
        ],
        name="finish",
    )(bit, *flat)


def sum_rows_over(values, axis):
    count = lax.axis_size(axis)
    rows, cols = values.shape
    parts = values.reshape(count, rows // count, cols)
    arrived = lax.all_to_all(parts, axis, split_axis=0, concat_axis=0, tiled=True)
    mine = jnp.sum(arrived.astype(f32), axis=0).astype(bf16)
    spread = jnp.broadcast_to(mine[None], parts.shape)
    full = lax.all_to_all(spread, axis, split_axis=0, concat_axis=0, tiled=True)
    return full.reshape(rows, cols).astype(f32)


def pair_sums(parts, axis, last=f32):
    count = len(parts)
    for step in steps_of(count):
        kind = bf16 if 2 * step < count else last
        parts = [
            (a.astype(f32) + swap(b, axis, step).astype(f32)).astype(kind)
            for a, b in zip(parts[0::2], parts[1::2])
        ]
    return parts[0]


def sum_small(values, axes):
    for axis in axes:
        for step in steps_of(lax.axis_size(axis)):
            values = values + swap(values, axis, step)
    return values


def on_device(
    tokens,
    first_gain,
    first_bias,
    query_weight,
    key_weight,
    value_weight,
    output_weight,
    second_gain,
    second_bias,
    expert_up,
    expert_down,
    item_lengths,
    routes,
    slot_order,
    cotangent,
):
    slots_all, width = tokens.shape
    members = lax.axis_size("tensor")
    shard_rows = slots_all // members
    rank = lax.axis_index("tensor")
    sources = lax.axis_size("dp")
    experts_all = sources * expert_up.shape[0]
    capacity = shard_rows // experts_all
    head_cols = query_weight.shape[1]
    heads = head_cols // HEAD_DIM
    up_matrix = expert_up[0]
    down_matrix = expert_down[0]
    rank_cell = rank.astype(jnp.int32).reshape(1, 1)

    def exchange(rows):
        return lax.all_to_all(
            rows.reshape(sources, -1, width), "dp", split_axis=0, concat_axis=0, tiled=True
        ).reshape(-1, width)

    qw, kw, vw = query_weight.T, key_weight.T, value_weight.T

    dispatch, grad_slots = plan(
        item_lengths, rank_cell, routes, slot_order, cotangent, capacity, experts_all
    )
    flat_grad = exchange(grad_slots)
    tokens, grad_slots = lax.optimization_barrier((tokens, grad_slots))
    normed_in, qt, kt, vt = project(
        rank_cell[0], tokens, first_gain, first_bias, qw, kw, vw, members
    )
    output_x = jnp.concatenate(
        [output_weight]
        + [swap(output_weight, "tensor", k) for k in range(1, members)]
    )
    heads_t, logs = attend(item_lengths, rank_cell, qt, kt, vt, members)
    heads_x = jnp.concatenate(
        [heads_t[0]] + [swap(heads_t[j], "tensor", j) for j in range(1, members)]
    )
    tokens_mine = lax.dynamic_slice_in_dim(tokens, rank * shard_rows, shard_rows).astype(f32)
    residual = tokens_mine + contract_rows(heads_x, output_x)
    normed_low = layer_norm(residual, second_gain, second_bias).astype(bf16)
    outgoing = jnp.dot(dispatch, normed_low, preferred_element_type=f32).astype(bf16)
    flat_in = exchange(outgoing)

    flat_grad, unused = lax.optimization_barrier((flat_grad, outgoing))
    grad_act = lax.dot_general(
        flat_grad, down_matrix, (((1,), (1,)), ((), ())), preferred_element_type=f32
    )
    gathered_grads = [flat_grad]
    for step in reversed(steps_of(members)):
        gathered_grads += [swap(a, "tensor", step) for a in gathered_grads]
    flat_in, grad_act = lax.optimization_barrier((flat_in, grad_act))
    act, grad_mid = expert(flat_in, grad_act, up_matrix)
    grad_back = exchange(grad_mid)
    gathered_rows = [flat_in]
    for step in reversed(steps_of(members)):
        gathered_rows += [swap(a, "tensor", step) for a in gathered_rows]

    gathered = list(zip(gathered_rows, gathered_grads))
    act, unused = lax.optimization_barrier((act, grad_mid))
    made = product(act, down_matrix)
    sums = expert_weights(rank_cell[0], gathered[0::2], up_matrix, down_matrix, members)
    grad_back, made, sums = lax.optimization_barrier((grad_back, made, sums))

    grad_normed = contract_rows(dispatch, grad_back)
    unused_mid, pull_mid = jax.vjp(layer_norm, residual, second_gain, second_bias)
    grad_res_norm, second_gain_part, second_bias_part = pull_mid(grad_normed)
    grad_res = cotangent.astype(f32) + grad_res_norm
    grad_low = grad_res.astype(bf16)
    places = rank * shard_rows + jnp.arange(shard_rows, dtype=jnp.int32)
    alive_mine = places < jnp.sum(item_lengths)
    grad_heads = (
        lax.dot_general(
            output_x, grad_low, (((1,), (1,)), ((), ())), preferred_element_type=f32
        )
        * alive_mine[None, :].astype(f32)
    ).astype(bf16)
    grad_parts = [grad_heads[:head_cols]] + [
        swap(grad_heads[j * head_cols : (j + 1) * head_cols], "tensor", j)
        for j in range(1, members)
    ]
    made, sums, grad_heads = lax.optimization_barrier((made, sums, grad_heads))
    returned = exchange(made)
    up_grad, down_grad = expert_weights(
        rank_cell[0], gathered[1::2], up_matrix, down_matrix, members, sums
    )
    output_part = jnp.dot(heads_x, grad_low, preferred_element_type=f32).astype(bf16)
    grad_parts, up_grad, down_grad, output_part = lax.optimization_barrier(
        (grad_parts, up_grad, down_grad, output_part)
    )

    groups = ((0, heads - 1), (heads - 1, 1)) if heads > 1 else ((0, heads),)
    joints = []
    pieces = []
    for first_head, count in groups:
        joint = attend_back(
            first_head, count, item_lengths, rank_cell, qt, kt, vt, heads_t, logs, grad_parts
        )
        weight_part = contract_rows(joint, normed_in).astype(bf16)
        weight_part, grad_parts = lax.optimization_barrier((weight_part, grad_parts))
        joints.append(joint)
        pieces.append(sum_halves(weight_part, "dp"))
    output_grad = sum_rows_over(
        pair_sums(
            [output_part[j * head_cols : (j + 1) * head_cols] for j in range(members)],
            "tensor", bf16,
        ),
        "dp",
    )

    partial, sums_first = input_grad(groups, normed_in, qw, kw, vw, joints, members)
    for step in steps_of(members):
        kept, sent = partial[: len(partial) // 2], partial[len(partial) // 2 :]
        partial = (kept.astype(f32) + swap(sent, "tensor", step).astype(f32)).astype(
            bf16 if 2 * step < members else f32
        )
    grad_in = partial[0]
    unused_first, pull_first = jax.vjp(
        lambda values: layer_norm(values, first_gain, first_bias), tokens_mine
    )
    token_grad = grad_res + pull_first(grad_in)[0]

    first_bias_part = sums_first[1]
    first_gain_part = (sums_first[0] - first_bias * first_bias_part) / first_gain
    norm_sums = sum_small(
        jnp.stack([first_gain_part, first_bias_part, second_gain_part, second_bias_part]),
        ("tensor", "dp"),
    )
    block_out = residual + contract_rows(dispatch, returned)
    bit_cell = (lax.axis_index("dp") & 1).astype(jnp.int32).reshape(1, 1)
    query_grad, key_grad, value_grad = finish(groups, bit_cell, pieces)
    return (
        block_out,
        token_grad,
        norm_sums[0],
        norm_sums[1],
        query_grad.T,
        key_grad.T,
        value_grad.T,
        output_grad,
        norm_sums[2],
        norm_sums[3],
        up_grad[None],
        down_grad[None],
    )


def solution(mesh):
    in_specs = (
        P("dp", None),
        P(),
        P(),
        P(None, "tensor"),
        P(None, "tensor"),
        P(None, "tensor"),
        P("tensor", None),
        P(),
        P(),
        P("dp", None, None),
        P("dp", None, None),
        P("dp", None),
        P(("dp", "tensor"), None),
        P(("dp", "tensor"), None),
        P(("dp", "tensor"), None),
    )
    out_specs = (
        P(("dp", "tensor"), None),
        P(("dp", "tensor"), None),
        P(),
        P(),
        P(None, "tensor"),
        P(None, "tensor"),
        P(None, "tensor"),
        P("tensor", None),
        P(),
        P(),
        P("dp", None, "tensor"),
        P("dp", "tensor", None),
    )
    return jax.shard_map(
        on_device, mesh=mesh, in_specs=in_specs, out_specs=out_specs, check_vma=False
    )
```

```python
import functools

import jax
import jax.numpy as jnp
from jax import lax
from jax.experimental import pallas as pl
from jax.experimental.pallas import tpu as pltpu
from jax.sharding import PartitionSpec as P

HEAD_DIM = 64
EPSILON = 1e-05
NEGATIVE = -1e30
f32 = jnp.float32
bf16 = jnp.bfloat16
VMEM = pl.BlockSpec(memory_space=pltpu.VMEM)
SMEM = pl.BlockSpec(memory_space=pltpu.SMEM)
COST = pl.CostEstimate(flops=2**20, bytes_accessed=2**20, transcendentals=0)


def layer_norm(values, gain, shift):
    average = jnp.mean(values, axis=-1, keepdims=True)
    centred = values - average
    variance = jnp.mean(centred * centred, axis=-1, keepdims=True)
    return centred * lax.rsqrt(variance + EPSILON) * gain + shift


def contract_rows(left, right):
    return lax.dot_general(
        left, right, (((0,), (0,)), ((), ())), preferred_element_type=f32
    )


def swap(values, axis, step):
    count = lax.axis_size(axis)
    return lax.ppermute(values, axis, [(i, i ^ step) for i in range(count)])


def steps_of(count):
    steps = []
    step = 1
    while step < count:
        steps.append(step)
        step *= 2
    return steps


def normalized(values):
    average = jnp.mean(values, axis=-1, keepdims=True)
    centred = values - average
    variance = jnp.mean(centred * centred, axis=-1, keepdims=True)
    return centred * lax.rsqrt(variance + EPSILON)


def project_kernel(
    rank_ref, tokens_ref, gain_ref, bias_ref, qw_ref, kw_ref, vw_ref,
    normed_ref, qt_ref, kt_ref, vt_ref,
):
    values = tokens_ref[...].astype(f32)
    normed = (normalized(values) * gain_ref[...] + bias_ref[...]).astype(bf16)
    normed_ref[...] = normed
    for weight_ref, out_ref, factor in (
        (qw_ref, qt_ref, HEAD_DIM ** (-0.5)), (kw_ref, kt_ref, None), (vw_ref, vt_ref, None)
    ):
        made = lax.dot_general(
            weight_ref[...], normed, (((1,), (1,)), ((), ())), preferred_element_type=f32
        ).astype(bf16)
        if factor is not None:
            made = made * jnp.asarray(factor, bf16)
        out_ref[...] = made


def project(rank, tokens, gain, bias, qw, kw, vw, blocks):
    slots, width = tokens.shape
    cols = qw.shape[0]
    size = slots // blocks
    fixed = lambda i, r: (0, 0)
    return pl.pallas_call(
        project_kernel,
        grid_spec=pltpu.PrefetchScalarGridSpec(
            num_scalar_prefetch=1,
            grid=(blocks,),
            in_specs=[
                pl.BlockSpec((size, width), lambda i, r: (i ^ r[0], 0)),
                pl.BlockSpec((1, width), fixed),
                pl.BlockSpec((1, width), fixed),
                pl.BlockSpec((cols, width), fixed),
                pl.BlockSpec((cols, width), fixed),
                pl.BlockSpec((cols, width), fixed),
            ],
            out_specs=(
                pl.BlockSpec((size, width), lambda i, r: (i, 0)),
                pl.BlockSpec((cols, size), lambda i, r: (0, i)),
                pl.BlockSpec((cols, size), lambda i, r: (0, i)),
                pl.BlockSpec((cols, size), lambda i, r: (0, i)),
            ),
        ),
        out_shape=(jax.ShapeDtypeStruct((slots, width), bf16),)
        + (jax.ShapeDtypeStruct((cols, slots), bf16),) * 3,
        name="project",
        cost_estimate=COST,
    )(rank, tokens, gain.reshape(1, -1), bias.reshape(1, -1), qw, kw, vw)


def item_ends(lens_ref):
    ends = []
    total = jnp.int32(0)
    for i in range(lens_ref.shape[1]):
        total = total + lens_ref[0, i]
        ends.append(total)
    return ends


def segments_at(place, ends):
    segment = jnp.zeros_like(place)
    for end in ends:
        segment = segment + (place >= end).astype(jnp.int32)
    return segment


def block_span(first, size, unit, ends):
    last = jnp.minimum(first + size, ends[-1]) - 1
    low = jnp.int32(0)
    high = ends[-1]
    for end in ends:
        low = jnp.where(first >= end, end, low)
    for end in reversed(ends):
        high = jnp.where(last < end, end, high)
    empty = first >= ends[-1]
    low_block = jnp.where(empty, 0, low // unit)
    high_block = jnp.where(empty, 0, (high + unit - 1) // unit)
    return low_block, high_block


def rows_at(block, size):
    return pl.ds(pl.multiple_of(block * size, size), size)


def memory_segments(block, size, shard, rank, ends, axis):
    shape = (1, size) if axis else (size, 1)
    at = block * size + lax.broadcasted_iota(jnp.int32, shape, axis)
    place = ((at // shard) ^ rank) * shard + at % shard
    return segments_at(place, ends)


def lane_masked(values, head):
    lane = lax.broadcasted_iota(jnp.int32, values.shape, 1)
    inside = (lane >= head * HEAD_DIM) & (lane < (head + 1) * HEAD_DIM)
    return jnp.where(inside, values, jnp.zeros_like(values))


def forward_kernel(
    lens_ref, rank_ref, qt_ref, kt_ref, vt_ref, *refs
):
    *out_refs, log_ref, masked_ref, out_ref = refs
    blocks, width, shard = out_ref.shape
    heads = width // HEAD_DIM
    pair = 1
    size = shard * pair
    rank = rank_ref[0, 0]
    ends = item_ends(lens_ref)
    keys = jnp.transpose(kt_ref[...], (1, 0))
    for h in range(heads):
        masked_ref[h] = lane_masked(keys, h)

    def query_block(i, unused):
        at = i ^ (rank // pair)
        cols = rows_at(at, size)
        seg_q = memory_segments(at, size, shard, rank, ends, 1)
        queries = qt_ref[:, cols]

        def key_block(j, carry):
            rows = rows_at(j ^ rank, shard)
            seg_k = memory_segments(j ^ rank, shard, shard, rank, ends, 0)
            same = seg_k == seg_q
            result = []
            for h in range(heads):
                highest, summed, total = carry[h]
                scores = jnp.dot(
                    masked_ref[h, rows, :], queries, preferred_element_type=f32
                )
                scores = jnp.where(same, scores, NEGATIVE)
                raised = jnp.maximum(highest, jnp.max(scores, axis=0, keepdims=True))
                shrink = jnp.exp(highest - raised)
                soft = jnp.exp(scores - raised)
                summed = summed * shrink + jnp.sum(soft, axis=0, keepdims=True)
                total = total * shrink + jnp.dot(
                    vt_ref[pl.ds(h * HEAD_DIM, HEAD_DIM), rows],
                    soft.astype(bf16),
                    preferred_element_type=f32,
                )
                result.append((raised, summed, total))
            return tuple(result)

        start = tuple(
            (
                jnp.full((1, size), NEGATIVE, f32),
                jnp.zeros((1, size), f32),
                jnp.zeros((HEAD_DIM, size), f32),
            )
            for h in range(heads)
        )
        low, high = block_span(i * size, size, shard, ends)
        done = lax.fori_loop(low, high, key_block, start)
        live = seg_q < len(ends)
        for h in range(heads):
            highest, summed, total = done[h]
            summed = jnp.where(live, summed, 1.0)
            result = jnp.where(live, total / summed, 0.0).astype(bf16)
            logs = jnp.where(live, highest + jnp.log(summed), -NEGATIVE)
            for p in range(pair):
                part = slice(p * shard, (p + 1) * shard)
                out_ref[at * pair + p, pl.ds(h * HEAD_DIM, HEAD_DIM), :] = result[:, part]
            log_ref[h, :, cols] = logs
        return unused

    lax.fori_loop(0, blocks // pair, query_block, 0)
    for b in range(blocks):
        out_refs[b][...] = out_ref[b]


def attend(lens, rank, qt, kt, vt, blocks):
    width, slots = qt.shape
    size = slots // blocks
    heads = width // HEAD_DIM
    return pl.pallas_call(
        forward_kernel,
        out_shape=(jax.ShapeDtypeStruct((width, size), bf16),) * blocks
        + (jax.ShapeDtypeStruct((heads, 1, slots), f32),),
        in_specs=[SMEM, SMEM, VMEM, VMEM, VMEM],
        out_specs=(VMEM,) * (blocks + 1),
        scratch_shapes=[
            pltpu.VMEM((heads, slots, width), bf16),
            pltpu.VMEM((blocks, width, size), bf16),
        ],
        name="attend",
        compiler_params=pltpu.CompilerParams(vmem_limit_bytes=60 * 2**20),
        cost_estimate=COST,
    )(lens, rank, qt, kt, vt)


def backward_kernel(
    first_head, heads, blocks, lens_ref, rank_ref, qt_ref, kt_ref, vt_ref, log_ref,
    normed_ref, *rest
):
    width, slots = qt_ref.shape
    shard = slots // blocks
    dim = HEAD_DIM
    out_refs, grad_refs = rest[:blocks], rest[blocks : 2 * blocks]
    joint_ref, weight_ref, kv_ref, q0_ref, og_ref, right_ref, inner_ref, dq_ref = rest[
        2 * blocks : -3
    ]
    turned_ref, rows_ref, copied = rest[-3:]
    fetch = pltpu.make_async_copy(normed_ref, rows_ref, copied)
    fetch.start()
    unit = shard // 2
    rank = rank_ref[0, 0]
    ends = item_ends(lens_ref)
    zero = jnp.zeros((dim, slots), bf16)
    for n in range(heads):
        part = slice((first_head + n) * dim, (first_head + n + 1) * dim)
        both = jnp.concatenate([kt_ref[part, :], vt_ref[part, :]], axis=0)
        kv_ref[n] = jnp.transpose(both, (1, 0))
        padded = jnp.concatenate([qt_ref[part, :], zero], axis=0)
        q0_ref[n] = jnp.transpose(padded, (1, 0))
        right_ref[n, 0] = padded
        for b in range(blocks):
            grad = grad_refs[b][part, :]
            cols = slice(b * shard, (b + 1) * shard)
            padded = jnp.concatenate([zero[:, :shard], grad], axis=0)
            og_ref[n, cols, :] = jnp.transpose(padded, (1, 0))
            right_ref[n, 1, :, cols] = padded
            inner_ref[n, :, cols] = jnp.sum(
                out_refs[b][part, :].astype(f32) * grad.astype(f32), axis=0, keepdims=True
            )
    dq_ref[...] = jnp.zeros_like(dq_ref)

    def key_block(j, unused):
        at_key = ((j // 2) ^ rank) * 2 + j % 2
        rows = rows_at(at_key, unit)
        seg_k = memory_segments(at_key, unit, shard, rank, ends, 0)

        def query_block(i, totals):
            at = i ^ rank
            cols = rows_at(at, shard)
            same = seg_k == memory_segments(at, shard, shard, rank, ends, 1)
            result = []
            for n in range(heads):
                head = first_head + n
                kv = kv_ref[n, rows, :]
                scores = jnp.dot(kv, right_ref[n, 0, :, cols], preferred_element_type=f32)
                grad_soft = jnp.dot(kv, right_ref[n, 1, :, cols], preferred_element_type=f32)
                soft = jnp.where(same, jnp.exp(scores - log_ref[head, :, cols]), 0.0)
                grad_scores = (soft * (grad_soft - inner_ref[n, :, cols])).astype(bf16)
                total = totals[n] + jnp.dot(
                    soft.astype(bf16), og_ref[n, cols, :], preferred_element_type=f32
                )
                total = total + jnp.dot(
                    grad_scores, q0_ref[n, cols, :], preferred_element_type=f32
                )
                dq_ref[n, :, cols] += jnp.dot(
                    kt_ref[pl.ds(head * dim, dim), rows], grad_scores,
                    preferred_element_type=f32,
                )
                result.append(total)
            return tuple(result)

        low, high = block_span(j * unit, unit, shard, ends)
        start = (jnp.zeros((unit, 2 * dim), f32),) * heads
        totals = lax.fori_loop(low, high, query_block, start)
        for n in range(heads):
            part = slice(2 * dim * n, 2 * dim * (n + 1))
            total = totals[n].astype(bf16)
            joint_ref[rows, part] = total
            turned_ref[part, rows] = jnp.transpose(total, (1, 0))
        return unused

    lax.fori_loop(0, 2 * blocks, key_block, 0)
    dq = (dq_ref[...] * dim ** (-0.5)).astype(bf16).reshape(heads * dim, slots)
    turned_ref[2 * dim * heads :, :] = dq
    joint_ref[:, 2 * dim * heads :] = jnp.transpose(dq, (1, 0))
    fetch.wait()
    weight_ref[...] = jnp.dot(
        turned_ref[...], rows_ref[...], preferred_element_type=f32
    ).astype(bf16)


def attend_back(first_head, heads, lens, rank, qt, kt, vt, logs, normed, outs, grads):
    slots, width = normed.shape
    blocks = len(outs)
    dim = HEAD_DIM
    return pl.pallas_call(
        functools.partial(backward_kernel, first_head, heads, blocks),
        out_shape=(
            jax.ShapeDtypeStruct((slots, 3 * dim * heads), bf16),
            jax.ShapeDtypeStruct((3 * dim * heads, width), bf16),
        ),
        in_specs=[SMEM, SMEM]
        + [VMEM] * 4
        + [pl.BlockSpec(memory_space=pl.ANY)]
        + [VMEM] * (2 * blocks),
        out_specs=(VMEM, VMEM),
        scratch_shapes=[pltpu.VMEM((heads, slots, 2 * dim), bf16)] * 3
        + [
            pltpu.VMEM((heads, 2, 2 * dim, slots), bf16),
            pltpu.VMEM((heads, 1, slots), f32),
            pltpu.VMEM((heads, dim, slots), f32),
            pltpu.VMEM((3 * dim * heads, slots), bf16),
            pltpu.VMEM((slots, width), bf16),
            pltpu.SemaphoreType.DMA,
        ],
        name="attend_back",
        compiler_params=pltpu.CompilerParams(vmem_limit_bytes=60 * 2**20),
        cost_estimate=COST,
    )(lens, rank, qt, kt, vt, logs, normed, *outs, *grads)


def plan_kernel(capacity, lens_ref, rank_ref, routes_ref, order_ref, grad_ref,
                dispatch_ref, slots_ref):
    shard = routes_ref.shape[1]
    first = rank_ref[0, 0] * shard
    ends = item_ends(lens_ref)
    chosen_row = routes_ref[...]
    chosen_col = jnp.transpose(jnp.broadcast_to(chosen_row, (128, shard)), (1, 0))[:, 0:1]
    order_row = order_ref[...]
    order_col = jnp.transpose(jnp.broadcast_to(order_row, (128, shard)), (1, 0))[:, 0:1]
    alive_row = segments_at(
        first + lax.broadcasted_iota(jnp.int32, (1, shard), 1), ends
    ) < len(ends)
    alive_col = segments_at(
        first + lax.broadcasted_iota(jnp.int32, (shard, 1), 0), ends
    ) < len(ends)
    ahead = (chosen_col == chosen_row) & (order_col < order_row) & alive_col
    ranked = jnp.sum(ahead.astype(jnp.int32), axis=0, keepdims=True)
    kept = alive_row & (ranked < capacity)
    slot = jnp.where(kept, chosen_row * capacity + ranked, -1)
    dispatch = (
        lax.broadcasted_iota(jnp.int32, dispatch_ref.shape, 0) == slot
    ).astype(f32).astype(bf16)
    dispatch_ref[...] = dispatch
    slots_ref[...] = jnp.dot(
        dispatch, grad_ref[...], preferred_element_type=f32
    ).astype(bf16)


def plan(lens, rank, routes, order, grads, capacity, experts_all):
    shard, width = grads.shape
    count = experts_all * capacity
    return pl.pallas_call(
        functools.partial(plan_kernel, capacity),
        out_shape=(
            jax.ShapeDtypeStruct((count, shard), bf16),
            jax.ShapeDtypeStruct((count, width), bf16),
        ),
        in_specs=[SMEM, SMEM, VMEM, VMEM, VMEM],
        out_specs=(VMEM, VMEM),
        name="plan",
        cost_estimate=COST,
    )(lens, rank, routes.reshape(1, -1), order, grads)


def across(left, right):
    return lax.dot_general(
        left, right, (((1,), (1,)), ((), ())), preferred_element_type=f32
    )


def middle_kernel(count, rank_ref, tokens_ref, gain_ref, bias_ref, dispatch_ref, *refs):
    head_refs, weight_refs = refs[:count], refs[count : 2 * count]
    residual_ref, rows_ref = refs[2 * count :]
    residual = tokens_ref[...].astype(f32)
    for head_ref, weight_ref in zip(head_refs, weight_refs):
        residual = residual + contract_rows(head_ref[...], weight_ref[...])
    residual_ref[...] = residual
    normed = (normalized(residual) * gain_ref[...] + bias_ref[...]).astype(bf16)
    rows_ref[...] = jnp.dot(
        dispatch_ref[...], normed, preferred_element_type=f32
    ).astype(bf16)


def middle(rank, tokens, gain, bias, dispatch, heads, weights):
    count, shard = dispatch.shape
    width = tokens.shape[1]
    fixed = lambda array: pl.BlockSpec(array.shape, lambda i, r: (0, 0))
    small = [gain.reshape(1, -1), bias.reshape(1, -1), dispatch, *heads, *weights]
    return pl.pallas_call(
        functools.partial(middle_kernel, len(heads)),
        grid_spec=pltpu.PrefetchScalarGridSpec(
            num_scalar_prefetch=1,
            grid=(1,),
            in_specs=[pl.BlockSpec((shard, width), lambda i, r: (r[0], 0))]
            + [fixed(array) for array in small],
            out_specs=(
                pl.BlockSpec((shard, width), lambda i, r: (0, 0)),
                pl.BlockSpec((count, width), lambda i, r: (0, 0)),
            ),
        ),
        out_shape=(
            jax.ShapeDtypeStruct((shard, width), f32),
            jax.ShapeDtypeStruct((count, width), bf16),
        ),
        name="middle",
        cost_estimate=COST,
    )(rank, tokens, *small)


def turn_kernel(
    count, lens_ref, rank_ref, dispatch_ref, back_ref, residual_ref, cotangent_ref,
    gain_ref, *refs
):
    weight_refs = refs[:count]
    grad_ref, low_ref, sums_ref = refs[count : count + 3]
    part_refs = refs[count + 3 :]
    shard = residual_ref.shape[0]
    grad_normed = contract_rows(dispatch_ref[...], back_ref[...])
    values = residual_ref[...]
    centred = values - jnp.mean(values, axis=-1, keepdims=True)
    inverse = lax.rsqrt(jnp.mean(centred * centred, axis=-1, keepdims=True) + EPSILON)
    normed = centred * inverse
    sums_ref[0:1] = jnp.sum(grad_normed * normed, axis=0, keepdims=True)
    sums_ref[1:2] = jnp.sum(grad_normed, axis=0, keepdims=True)
    scaled = grad_normed * gain_ref[...]
    grad = cotangent_ref[...].astype(f32) + inverse * (
        scaled
        - jnp.mean(scaled, axis=-1, keepdims=True)
        - normed * jnp.mean(scaled * normed, axis=-1, keepdims=True)
    )
    grad_ref[...] = grad
    low = grad.astype(bf16)
    low_ref[...] = low
    place = rank_ref[0, 0] * shard + lax.broadcasted_iota(jnp.int32, (1, shard), 1)
    alive = place < item_ends(lens_ref)[-1]
    for weight_ref, part_ref in zip(weight_refs, part_refs):
        part_ref[...] = jnp.where(alive, across(weight_ref[...], low), 0.0).astype(bf16)


def turn(lens, rank, dispatch, back, residual, cotangent, gain, weights):
    shard, width = residual.shape
    cols = weights[0].shape[0]
    count = len(weights)
    return pl.pallas_call(
        functools.partial(turn_kernel, count),
        out_shape=(
            jax.ShapeDtypeStruct((shard, width), f32),
            jax.ShapeDtypeStruct((shard, width), bf16),
            jax.ShapeDtypeStruct((2, width), f32),
        )
        + (jax.ShapeDtypeStruct((cols, shard), bf16),) * count,
        in_specs=[SMEM, SMEM] + [VMEM] * (5 + count),
        out_specs=(VMEM,) * (3 + count),
        name="turn",
        cost_estimate=COST,
    )(lens, rank, dispatch, back, residual, cotangent, gain.reshape(1, -1), *weights)


def output_kernel(low_ref, *refs):
    head_refs, (kept_ref, sent_ref) = refs[:-2], refs[-2:]
    for j, head_ref in enumerate(head_refs):
        made = jnp.dot(head_ref[...], low_ref[...], preferred_element_type=f32)
        (kept_ref, sent_ref)[j % 2][j // 2] = made.astype(bf16)


def output_products(low, heads):
    cols = heads[0].shape[0]
    shape = jax.ShapeDtypeStruct((len(heads) // 2, cols, low.shape[1]), bf16)
    return pl.pallas_call(
        output_kernel,
        out_shape=(shape, shape),
        in_specs=[VMEM] * (1 + len(heads)),
        out_specs=(VMEM, VMEM),
        name="output_products",
        cost_estimate=COST,
    )(low, *heads)


def gelu_parts(values):
    below = 0.5 + 0.5 * lax.erf(values * (0.5**0.5))
    density = jnp.exp(-0.5 * values * values) * (0.5 / jnp.pi) ** 0.5
    return values * below, below + values * density


def expert_kernel(in_ref, grad_act_ref, up_ref, act_ref, mid_ref, sum_ref):
    step = pl.program_id(0)
    pre = jnp.dot(in_ref[...], up_ref[...], preferred_element_type=f32)
    act, slope = gelu_parts(pre)
    act_ref[...] = act.astype(bf16)
    grad_pre = (grad_act_ref[...] * slope).astype(bf16)
    mid = lax.dot_general(
        grad_pre, up_ref[...], (((1,), (1,)), ((), ())), preferred_element_type=f32
    )

    @pl.when(step == 0)
    def first():
        sum_ref[...] = mid

    @pl.when(step > 0)
    def later():
        sum_ref[...] += mid

    @pl.when(step == pl.num_programs(0) - 1)
    def last():
        mid_ref[...] = sum_ref[...].astype(bf16)


def expert(rows, grad_act, up):
    count, width = rows.shape
    hidden = up.shape[1]
    size = min(512, hidden)
    return pl.pallas_call(
        expert_kernel,
        grid=(hidden // size,),
        out_shape=(
            jax.ShapeDtypeStruct((count, hidden), bf16),
            jax.ShapeDtypeStruct((count, width), bf16),
        ),
        in_specs=[
            pl.BlockSpec((count, width), lambda i: (0, 0)),
            pl.BlockSpec((count, size), lambda i: (0, i)),
            pl.BlockSpec((width, size), lambda i: (0, i)),
        ],
        out_specs=(
            pl.BlockSpec((count, size), lambda i: (0, i)),
            pl.BlockSpec((count, width), lambda i: (0, 0)),
        ),
        scratch_shapes=[pltpu.VMEM((count, width), f32)],
        name="expert",
        cost_estimate=COST,
    )(rows, grad_act, up)


def product_kernel(a_ref, b_ref, out_ref, sum_ref):
    step = pl.program_id(0)
    made = jnp.dot(a_ref[...], b_ref[...], preferred_element_type=f32)

    @pl.when(step == 0)
    def first():
        sum_ref[...] = made

    @pl.when(step > 0)
    def later():
        sum_ref[...] += made

    @pl.when(step == pl.num_programs(0) - 1)
    def last():
        out_ref[...] = sum_ref[...].astype(bf16)


def product(a, b):
    count, depth = a.shape
    width = b.shape[1]
    size = min(1024, depth)
    return pl.pallas_call(
        product_kernel,
        grid=(depth // size,),
        out_shape=jax.ShapeDtypeStruct((count, width), bf16),
        in_specs=[
            pl.BlockSpec((count, size), lambda i: (0, i)),
            pl.BlockSpec((size, width), lambda i: (i, 0)),
        ],
        out_specs=pl.BlockSpec((count, width), lambda i: (0, 0)),
        scratch_shapes=[pltpu.VMEM((count, width), f32)],
        name="product",
        cost_estimate=COST,
    )(a, b)


def weight_kernel(groups, rank_ref, up_ref, down_ref, *refs):
    dup_ref, ddown_ref = refs[-2:]
    dup = ddown = 0.0
    for g in range(groups):
        in_ref, grad_ref = refs[2 * g : 2 * g + 2]
        pre = jnp.dot(in_ref[...], up_ref[...], preferred_element_type=f32)
        grad_act = lax.dot_general(
            grad_ref[...], down_ref[...], (((1,), (1,)), ((), ())),
            preferred_element_type=f32,
        )
        act, slope = gelu_parts(pre)
        dup = dup + contract_rows(in_ref[...], (grad_act * slope).astype(bf16))
        ddown = ddown + contract_rows(act.astype(bf16), grad_ref[...])
    if len(refs) > 2 * groups + 2:
        dup = dup + refs[2 * groups][...]
        ddown = ddown + refs[2 * groups + 1][...]
    dup_ref[...] = dup
    ddown_ref[...] = ddown


def expert_weights(rank, group, up, down, parts, earlier=()):
    count, width = group[0][0].shape
    hidden = up.shape[1] // parts
    size = min(256, hidden)
    blocks = hidden // size
    up_block = pl.BlockSpec((width, size), lambda i, r: (0, i))
    down_block = pl.BlockSpec((size, width), lambda i, r: (i, 0))
    rows = [values for both in group for values in both]
    return pl.pallas_call(
        functools.partial(weight_kernel, len(group)),
        grid_spec=pltpu.PrefetchScalarGridSpec(
            num_scalar_prefetch=1,
            grid=(blocks,),
            in_specs=[
                pl.BlockSpec((width, size), lambda i, r: (0, r[0] * blocks + i)),
                pl.BlockSpec((size, width), lambda i, r: (r[0] * blocks + i, 0)),
            ]
            + [pl.BlockSpec((count, width), lambda i, r: (0, 0))] * len(rows)
            + ([up_block, down_block] if earlier else []),
            out_specs=(up_block, down_block),
        ),
        out_shape=(
            jax.ShapeDtypeStruct((width, hidden), f32),
            jax.ShapeDtypeStruct((hidden, width), f32),
        ),
        name="expert_weights",
        cost_estimate=COST,
    )(rank, up, down, *rows, *earlier)


def input_grad_kernel(groups, normed_ref, qw_ref, kw_ref, vw_ref, *refs):
    joint_refs = refs[: len(groups)]
    kept_ref, sent_ref, sums_ref, turned_ref = refs[len(groups) :]
    step = pl.program_id(0)
    dim = HEAD_DIM

    @pl.when(step == 0)
    def stack():
        at = 0
        for first_head, heads in groups:
            for n in range(first_head, first_head + heads):
                part = slice(n * dim, (n + 1) * dim)
                turned_ref[at : at + dim, :] = kw_ref[part, :]
                turned_ref[at + dim : at + 2 * dim, :] = vw_ref[part, :]
                at += 2 * dim
            part = slice(first_head * dim, (first_head + heads) * dim)
            turned_ref[at : at + heads * dim, :] = qw_ref[part, :]
            at += heads * dim

    total = 0.0
    at = 0
    for joint_ref in joint_refs:
        rows = slice(at, at + joint_ref.shape[1])
        total = total + jnp.dot(
            joint_ref[...], turned_ref[rows, :], preferred_element_type=f32
        )
        at += joint_ref.shape[1]
    @pl.when(step % 2 == 0)
    def keep():
        kept_ref[0] = total.astype(bf16)

    @pl.when(step % 2 == 1)
    def send():
        sent_ref[0] = total.astype(bf16)

    gains = jnp.sum(total * normed_ref[...].astype(f32), axis=0, keepdims=True)
    shifts = jnp.sum(total, axis=0, keepdims=True)

    @pl.when(step == 0)
    def first():
        sums_ref[0:1] = gains
        sums_ref[1:2] = shifts

    @pl.when(step > 0)
    def later():
        sums_ref[0:1] += gains
        sums_ref[1:2] += shifts


def input_grad(groups, normed, qw, kw, vw, joints, blocks):
    slots, width = normed.shape
    size = slots // blocks
    cols = qw.shape[0]
    fixed = pl.BlockSpec((cols, width), lambda i: (0, 0))
    return pl.pallas_call(
        functools.partial(input_grad_kernel, groups),
        grid=(blocks,),
        out_shape=(jax.ShapeDtypeStruct((blocks // 2, size, width), bf16),) * 2
        + (jax.ShapeDtypeStruct((2, width), f32),),
        in_specs=[pl.BlockSpec((size, width), lambda i: (i, 0)), fixed, fixed, fixed]
        + [pl.BlockSpec((size, joint.shape[1]), lambda i: (i, 0)) for joint in joints],
        out_specs=(
            pl.BlockSpec((1, size, width), lambda i: (i // 2, 0, 0)),
            pl.BlockSpec((1, size, width), lambda i: (i // 2, 0, 0)),
            pl.BlockSpec((2, width), lambda i: (0, 0)),
        ),
        scratch_shapes=[pltpu.VMEM((3 * cols, width), bf16)],
        name="input_grad",
        cost_estimate=COST,
    )(normed, qw, kw, vw, *joints)


def start_halves(values, axis):
    low_bit = lax.axis_index(axis) & 1
    half = values.shape[0] // 2
    own = lax.dynamic_slice_in_dim(values, low_bit * half, half)
    away = lax.dynamic_slice_in_dim(values, (1 - low_bit) * half, half)
    return add_low(own, swap(away, axis, 1))


def add_low(a, b):
    return (a.astype(f32) + b.astype(f32)).astype(bf16)


def tie(*values):
    return lax.optimization_barrier(values)


def finish_kernel(groups, bit_ref, *refs):
    pieces = refs[: 2 * len(groups)]
    outs = refs[2 * len(groups) : 2 * len(groups) + 3]
    whole_refs = refs[2 * len(groups) + 3 :]
    query_ref, key_ref, value_ref = outs
    dim = HEAD_DIM
    bit = bit_ref[0, 0]
    for g, (first_head, heads) in enumerate(groups):
        whole_ref = whole_refs[g]
        half = whole_ref.shape[0] // 2
        whole_ref[rows_at(bit, half), :] = pieces[2 * g][...].astype(f32)
        whole_ref[rows_at(1 - bit, half), :] = pieces[2 * g + 1][...].astype(f32)
        at = 0
        for n in range(first_head, first_head + heads):
            part = slice(n * dim, (n + 1) * dim)
            key_ref[part, :] = whole_ref[at : at + dim, :]
            value_ref[part, :] = whole_ref[at + dim : at + 2 * dim, :]
            at += 2 * dim
        part = slice(first_head * dim, (first_head + heads) * dim)
        query_ref[part, :] = whole_ref[at : at + heads * dim, :]


def finish(groups, bit, pieces):
    width = pieces[0][0].shape[1]
    cols = sum(heads for first_head, heads in groups) * HEAD_DIM
    flat = [half_piece for piece in pieces for half_piece in piece]
    return pl.pallas_call(
        functools.partial(finish_kernel, groups),
        out_shape=(jax.ShapeDtypeStruct((cols, width), f32),) * 3,
        in_specs=[SMEM] + [VMEM] * len(flat),
        out_specs=(VMEM,) * 3,
        scratch_shapes=[
            pltpu.VMEM((3 * heads * HEAD_DIM, width), f32) for first_head, heads in groups
        ],
        name="finish",
    )(bit, *flat)


def sum_rows_over(values, axis):
    count = lax.axis_size(axis)
    rows, cols = values.shape
    parts = values.reshape(count, rows // count, cols)
    arrived = lax.all_to_all(parts, axis, split_axis=0, concat_axis=0, tiled=True)
    mine = jnp.sum(arrived.astype(f32), axis=0).astype(bf16)
    spread = jnp.broadcast_to(mine[None], parts.shape)
    full = lax.all_to_all(spread, axis, split_axis=0, concat_axis=0, tiled=True)
    return full.reshape(rows, cols).astype(f32)


def sum_small(values, axes):
    for axis in axes:
        for step in steps_of(lax.axis_size(axis)):
            values = values + swap(values, axis, step)
    return values


def on_device(
    tokens,
    first_gain,
    first_bias,
    query_weight,
    key_weight,
    value_weight,
    output_weight,
    second_gain,
    second_bias,
    expert_up,
    expert_down,
    item_lengths,
    routes,
    slot_order,
    cotangent,
):
    slots_all, width = tokens.shape
    members = lax.axis_size("tensor")
    shard_rows = slots_all // members
    rank = lax.axis_index("tensor")
    sources = lax.axis_size("dp")
    experts_all = sources * expert_up.shape[0]
    capacity = shard_rows // experts_all
    head_cols = query_weight.shape[1]
    heads = head_cols // HEAD_DIM
    up_matrix = expert_up[0]
    down_matrix = expert_down[0]
    rank_cell = rank.astype(jnp.int32).reshape(1, 1)

    def exchange(rows):
        return lax.all_to_all(
            rows.reshape(sources, -1, width), "dp", split_axis=0, concat_axis=0, tiled=True
        ).reshape(-1, width)

    qw, kw, vw = query_weight.T, key_weight.T, value_weight.T

    dispatch, grad_slots = plan(
        item_lengths, rank_cell, routes, slot_order, cotangent, capacity, experts_all
    )
    flat_grad = exchange(grad_slots)
    tokens, grad_slots = tie(tokens, grad_slots)
    normed_in, qt, kt, vt = project(
        rank_cell[0], tokens, first_gain, first_bias, qw, kw, vw, members
    )
    outputs = [output_weight] + [
        swap(output_weight, "tensor", k) for k in range(1, members)
    ]
    *own_heads, logs = attend(item_lengths, rank_cell, qt, kt, vt, members)
    own_heads, flat_grad, outputs = tie(own_heads, flat_grad, outputs)
    all_heads = [own_heads[0]] + [
        swap(own_heads[j], "tensor", j) for j in range(1, members)
    ]
    residual, outgoing = middle(
        rank_cell[0], tokens, second_gain, second_bias, dispatch, all_heads, outputs
    )
    flat_in = exchange(outgoing)

    flat_grad, outgoing = tie(flat_grad, outgoing)
    grad_act = across(flat_grad, down_matrix)
    gathered_grads = [flat_grad]
    gathered_rows = [flat_in]
    steps = steps_of(members)
    for step in reversed(steps[1:]):
        gathered_grads += [swap(a, "tensor", step) for a in gathered_grads]
    flat_in, grad_act, gathered_grads = tie(flat_in, grad_act, gathered_grads)
    gathered_rows = [flat_in]
    for step in reversed(steps[1:]):
        gathered_rows += [swap(a, "tensor", step) for a in gathered_rows]
    near_grads = swap(gathered_grads[0], "tensor", 1)
    near_rows = swap(flat_in, "tensor", 1)
    far_grads = [swap(a, "tensor", 1) for a in gathered_grads[1:]]
    act, grad_mid = expert(flat_in, grad_act, up_matrix)
    act, grad_mid, near_rows, near_grads, far_grads = tie(
        act, grad_mid, near_rows, near_grads, far_grads
    )
    grad_back = exchange(grad_mid)

    act, near_rows, grad_mid = tie(act, near_rows, grad_mid)
    made = product(act, down_matrix)
    sums = expert_weights(
        rank_cell[0],
        [(flat_in, gathered_grads[0]), (near_rows, near_grads)],
        up_matrix, down_matrix, members,
    )
    made, sums, gathered_rows = tie(made, sums, gathered_rows)
    far_rows = [swap(a, "tensor", 1) for a in gathered_rows[1:]]
    grad_back, made, sums = tie(grad_back, made, sums)

    grad_res, grad_low, sums_second, *grad_heads = turn(
        item_lengths, rank_cell, dispatch, grad_back, residual, cotangent,
        second_gain, outputs,
    )
    grad_parts = [grad_heads[0]] + [
        swap(grad_heads[j], "tensor", j) for j in range(1, members)
    ]
    made, sums, grad_low, grad_heads = tie(made, sums, grad_low, grad_heads)
    returned = exchange(made)
    kept, sent = output_products(grad_low, all_heads)
    sums, kept, sent = tie(sums, kept, sent)
    output_sum = add_low(kept, swap(sent, "tensor", 1))
    sums = expert_weights(
        rank_cell[0],
        list(zip(gathered_rows[1:], gathered_grads[1:])) + list(zip(far_rows, far_grads)),
        up_matrix, down_matrix, members, sums,
    )
    grad_parts, sums, output_sum = tie(grad_parts, sums, output_sum)
    up_grad, down_grad = sums

    back = functools.partial(
        attend_back, lens=item_lengths, rank=rank_cell, qt=qt, kt=kt, vt=vt, logs=logs,
        normed=normed_in, outs=own_heads,
    )
    groups = ((0, heads - 1), (heads - 1, 1))
    joint_a, part_a = back(*groups[0], grads=grad_parts)
    for step in steps[1:]:
        output_sum = add_low(
            output_sum[: len(output_sum) // 2],
            swap(output_sum[len(output_sum) // 2 :], "tensor", step),
        )
    joint_a, part_a, output_sum, grad_parts = tie(joint_a, part_a, output_sum, grad_parts)
    half_a = start_halves(part_a, "dp")
    joint_b, part_b = back(*groups[1], grads=grad_parts)
    joint_b, part_b, half_a, returned = tie(joint_b, part_b, half_a, returned)
    output_grad = sum_rows_over(output_sum[0], "dp")

    half_b = start_halves(part_b, "dp")
    kept, sent, sums_first = input_grad(
        groups, normed_in, qw, kw, vw, (joint_a, joint_b), members
    )
    for step in steps:
        partial = kept.astype(f32) + swap(sent, "tensor", step).astype(f32)
        count = partial.shape[0] // 2
        kept, sent = partial[:count].astype(bf16), partial[count:].astype(bf16)
    grad_in = partial[0]
    for step in steps_of(sources)[1:]:
        half_a = add_low(half_a, swap(half_a, "dp", step))
        half_b = add_low(half_b, swap(half_b, "dp", step))
    pieces = [(half_a, swap(half_a, "dp", 1)), (half_b, swap(half_b, "dp", 1))]
    tokens_mine = lax.dynamic_slice_in_dim(tokens, rank * shard_rows, shard_rows).astype(f32)
    unused_first, pull_first = jax.vjp(
        lambda values: layer_norm(values, first_gain, first_bias), tokens_mine
    )
    token_grad = grad_res + pull_first(grad_in)[0]

    first_gain_part = (sums_first[0] - first_bias * sums_first[1]) / first_gain
    norm_sums = sum_small(
        jnp.stack([first_gain_part, sums_first[1], sums_second[0], sums_second[1]]),
        ("tensor", "dp"),
    )
    block_out = residual + contract_rows(dispatch, returned)
    bit_cell = (lax.axis_index("dp") & 1).astype(jnp.int32).reshape(1, 1)
    query_grad, key_grad, value_grad = finish(groups, bit_cell, pieces)
    return (
        block_out,
        token_grad,
        norm_sums[0],
        norm_sums[1],
        query_grad.T,
        key_grad.T,
        value_grad.T,
        output_grad,
        norm_sums[2],
        norm_sums[3],
        up_grad[None],
        down_grad[None],
    )


def solution(mesh):
    in_specs = (
        P("dp", None),
        P(),
        P(),
        P(None, "tensor"),
        P(None, "tensor"),
        P(None, "tensor"),
        P("tensor", None),
        P(),
        P(),
        P("dp", None, None),
        P("dp", None, None),
        P("dp", None),
        P(("dp", "tensor"), None),
        P(("dp", "tensor"), None),
        P(("dp", "tensor"), None),
    )
    out_specs = (
        P(("dp", "tensor"), None),
        P(("dp", "tensor"), None),
        P(),
        P(),
        P(None, "tensor"),
        P(None, "tensor"),
        P(None, "tensor"),
        P("tensor", None),
        P(),
        P(),
        P("dp", None, "tensor"),
        P("dp", "tensor", None),
    )
    return jax.shard_map(
        on_device, mesh=mesh, in_specs=in_specs, out_specs=out_specs, check_vma=False
    )
```

```python
import functools

import jax
import jax.numpy as jnp
from jax import lax
from jax.experimental import pallas as pl
from jax.experimental.pallas import tpu as pltpu
from jax.sharding import PartitionSpec as P

HEAD_DIM = 64
EPSILON = 1e-05
NEGATIVE = -1e30
f32 = jnp.float32
bf16 = jnp.bfloat16
VMEM = pl.BlockSpec(memory_space=pltpu.VMEM)
SMEM = pl.BlockSpec(memory_space=pltpu.SMEM)
COST = pl.CostEstimate(flops=2**20, bytes_accessed=2**20, transcendentals=0)


def layer_norm(values, gain, shift):
    average = jnp.mean(values, axis=-1, keepdims=True)
    centred = values - average
    variance = jnp.mean(centred * centred, axis=-1, keepdims=True)
    return centred * lax.rsqrt(variance + EPSILON) * gain + shift


def contract_rows(left, right):
    return lax.dot_general(
        left, right, (((0,), (0,)), ((), ())), preferred_element_type=f32
    )


def swap(values, axis, step):
    count = lax.axis_size(axis)
    return lax.ppermute(values, axis, [(i, i ^ step) for i in range(count)])


def steps_of(count):
    steps = []
    step = 1
    while step < count:
        steps.append(step)
        step *= 2
    return steps


def normalized(values):
    average = jnp.mean(values, axis=-1, keepdims=True)
    centred = values - average
    variance = jnp.mean(centred * centred, axis=-1, keepdims=True)
    return centred * lax.rsqrt(variance + EPSILON)


def project_kernel(
    rank_ref, tokens_ref, gain_ref, bias_ref, qw_ref, kw_ref, vw_ref,
    normed_ref, qt_ref, kt_ref, vt_ref,
):
    values = tokens_ref[...].astype(f32)
    normed = (normalized(values) * gain_ref[...][None] + bias_ref[...][None]).astype(bf16)
    normed_ref[...] = normed
    for weight_ref, out_ref, factor in (
        (qw_ref, qt_ref, HEAD_DIM ** (-0.5)), (kw_ref, kt_ref, None), (vw_ref, vt_ref, None)
    ):
        made = lax.dot_general(
            weight_ref[...], normed, (((1,), (1,)), ((), ())), preferred_element_type=f32
        ).astype(bf16)
        if factor is not None:
            made = made * jnp.asarray(factor, bf16)
        out_ref[...] = made


def project(rank, tokens, gain, bias, qw, kw, vw, blocks):
    slots, width = tokens.shape
    cols = qw.shape[0]
    size = slots // blocks
    fixed = lambda i, r: (0, 0)
    line = pl.BlockSpec((width,), lambda i, r: (0,))
    return pl.pallas_call(
        project_kernel,
        grid_spec=pltpu.PrefetchScalarGridSpec(
            num_scalar_prefetch=1,
            grid=(blocks,),
            in_specs=[
                pl.BlockSpec((size, width), lambda i, r: (i ^ r[0], 0)),
                line,
                line,
                pl.BlockSpec((cols, width), fixed),
                pl.BlockSpec((cols, width), fixed),
                pl.BlockSpec((cols, width), fixed),
            ],
            out_specs=(
                pl.BlockSpec((size, width), lambda i, r: (i, 0)),
                pl.BlockSpec((cols, size), lambda i, r: (0, i)),
                pl.BlockSpec((cols, size), lambda i, r: (0, i)),
                pl.BlockSpec((cols, size), lambda i, r: (0, i)),
            ),
        ),
        out_shape=(jax.ShapeDtypeStruct((slots, width), bf16),)
        + (jax.ShapeDtypeStruct((cols, slots), bf16),) * 3,
        name="project",
        cost_estimate=COST,
    )(rank, tokens, gain, bias, qw, kw, vw)


def item_ends(lens_ref):
    ends = []
    total = jnp.int32(0)
    for i in range(lens_ref.shape[1]):
        total = total + lens_ref[0, i]
        ends.append(total)
    return ends


def segments_at(place, ends):
    segment = jnp.zeros_like(place)
    for end in ends:
        segment = segment + (place >= end).astype(jnp.int32)
    return segment


def block_span(first, size, unit, ends):
    last = jnp.minimum(first + size, ends[-1]) - 1
    low = jnp.int32(0)
    high = ends[-1]
    for end in ends:
        low = jnp.where(first >= end, end, low)
    for end in reversed(ends):
        high = jnp.where(last < end, end, high)
    empty = first >= ends[-1]
    low_block = jnp.where(empty, 0, low // unit)
    high_block = jnp.where(empty, 0, (high + unit - 1) // unit)
    return low_block, high_block


def rows_at(block, size):
    return pl.ds(pl.multiple_of(block * size, size), size)


def memory_segments(block, size, shard, rank, ends, axis):
    shape = (1, size) if axis else (size, 1)
    at = block * size + lax.broadcasted_iota(jnp.int32, shape, axis)
    place = ((at // shard) ^ rank) * shard + at % shard
    return segments_at(place, ends)


def lane_masked(values, head):
    lane = lax.broadcasted_iota(jnp.int32, values.shape, 1)
    inside = (lane >= head * HEAD_DIM) & (lane < (head + 1) * HEAD_DIM)
    return jnp.where(inside, values, jnp.zeros_like(values))


def forward_kernel(
    lens_ref, rank_ref, qt_ref, kt_ref, vt_ref, *refs
):
    *out_refs, log_ref, masked_ref, out_ref = refs
    blocks, width, shard = out_ref.shape
    heads = width // HEAD_DIM
    pair = 1
    size = shard * pair
    rank = rank_ref[0, 0]
    ends = item_ends(lens_ref)
    keys = jnp.transpose(kt_ref[...], (1, 0))
    for h in range(heads):
        masked_ref[h] = lane_masked(keys, h)

    def query_block(i, unused):
        at = i ^ (rank // pair)
        cols = rows_at(at, size)
        seg_q = memory_segments(at, size, shard, rank, ends, 1)
        queries = qt_ref[:, cols]

        def key_block(j, carry):
            rows = rows_at(j ^ rank, shard)
            seg_k = memory_segments(j ^ rank, shard, shard, rank, ends, 0)
            same = seg_k == seg_q
            result = []
            for h in range(heads):
                highest, summed, total = carry[h]
                scores = jnp.dot(
                    masked_ref[h, rows, :], queries, preferred_element_type=f32
                )
                scores = jnp.where(same, scores, NEGATIVE)
                raised = jnp.maximum(highest, jnp.max(scores, axis=0, keepdims=True))
                shrink = jnp.exp(highest - raised)
                soft = jnp.exp(scores - raised)
                summed = summed * shrink + jnp.sum(soft, axis=0, keepdims=True)
                total = total * shrink + jnp.dot(
                    vt_ref[pl.ds(h * HEAD_DIM, HEAD_DIM), rows],
                    soft.astype(bf16),
                    preferred_element_type=f32,
                )
                result.append((raised, summed, total))
            return tuple(result)

        start = tuple(
            (
                jnp.full((1, size), NEGATIVE, f32),
                jnp.zeros((1, size), f32),
                jnp.zeros((HEAD_DIM, size), f32),
            )
            for h in range(heads)
        )
        low, high = block_span(i * size, size, shard, ends)
        done = lax.fori_loop(low, high, key_block, start)
        live = seg_q < len(ends)
        for h in range(heads):
            highest, summed, total = done[h]
            summed = jnp.where(live, summed, 1.0)
            result = jnp.where(live, total / summed, 0.0).astype(bf16)
            logs = jnp.where(live, highest + jnp.log(summed), -NEGATIVE)
            for p in range(pair):
                part = slice(p * shard, (p + 1) * shard)
                out_ref[at * pair + p, pl.ds(h * HEAD_DIM, HEAD_DIM), :] = result[:, part]
            log_ref[h, :, cols] = logs
        return unused

    lax.fori_loop(0, blocks // pair, query_block, 0)
    for b in range(blocks):
        out_refs[b][...] = out_ref[b]


def attend(lens, rank, qt, kt, vt, blocks):
    width, slots = qt.shape
    size = slots // blocks
    heads = width // HEAD_DIM
    return pl.pallas_call(
        forward_kernel,
        out_shape=(jax.ShapeDtypeStruct((width, size), bf16),) * blocks
        + (jax.ShapeDtypeStruct((heads, 1, slots), f32),),
        in_specs=[SMEM, SMEM, VMEM, VMEM, VMEM],
        out_specs=(VMEM,) * (blocks + 1),
        scratch_shapes=[
            pltpu.VMEM((heads, slots, width), bf16),
            pltpu.VMEM((blocks, width, size), bf16),
        ],
        name="attend",
        compiler_params=pltpu.CompilerParams(vmem_limit_bytes=60 * 2**20),
        cost_estimate=COST,
    )(lens, rank, qt, kt, vt)


def stacked_parts(first_head, heads, query, key, value):
    dim = HEAD_DIM
    parts = []
    for n in range(heads):
        first = (first_head + n) * dim
        parts += [(2 * n * dim, key, first, dim), ((2 * n + 1) * dim, value, first, dim)]
    return parts + [(2 * heads * dim, query, first_head * dim, heads * dim)]


def backward_kernel(
    first_head, heads, blocks, halves, lens_ref, rank_ref, bit_ref, qt_ref, kt_ref, vt_ref,
    log_ref, qw_ref, kw_ref, vw_ref, normed_ref, *rest
):
    width, slots = qt_ref.shape
    shard = slots // blocks
    dim = HEAD_DIM
    out_refs, grad_refs = rest[:blocks], rest[blocks : 2 * blocks]
    joint_ref, sums_ref, *part_refs = rest[2 * blocks : 2 * blocks + 2 + halves]
    kv_ref, q0_ref, og_ref, right_ref, inner_ref, dq_ref, made_ref = rest[-10:-3]
    turned_ref, rows_ref, copied = rest[-3:]
    fetch = pltpu.make_async_copy(normed_ref, rows_ref, copied)
    fetch.start()
    unit = shard // 2
    rank = rank_ref[0, 0]
    ends = item_ends(lens_ref)
    zero = jnp.zeros((dim, slots), bf16)
    for n in range(heads):
        part = slice((first_head + n) * dim, (first_head + n + 1) * dim)
        both = jnp.concatenate([kt_ref[part, :], vt_ref[part, :]], axis=0)
        kv_ref[n] = jnp.transpose(both, (1, 0))
        padded = jnp.concatenate([qt_ref[part, :], zero], axis=0)
        q0_ref[n] = jnp.transpose(padded, (1, 0))
        right_ref[n, 0] = padded
        for b in range(blocks):
            grad = grad_refs[b][part, :]
            cols = slice(b * shard, (b + 1) * shard)
            padded = jnp.concatenate([zero[:, :shard], grad], axis=0)
            og_ref[n, cols, :] = jnp.transpose(padded, (1, 0))
            right_ref[n, 1, :, cols] = padded
            inner_ref[n, :, cols] = jnp.sum(
                out_refs[b][part, :].astype(f32) * grad.astype(f32), axis=0, keepdims=True
            )
    dq_ref[...] = jnp.zeros_like(dq_ref)

    def key_block(j, unused):
        at_key = ((j // 2) ^ rank) * 2 + j % 2
        rows = rows_at(at_key, unit)
        seg_k = memory_segments(at_key, unit, shard, rank, ends, 0)

        def query_block(i, totals):
            at = i ^ rank
            cols = rows_at(at, shard)
            same = seg_k == memory_segments(at, shard, shard, rank, ends, 1)
            result = []
            for n in range(heads):
                head = first_head + n
                kv = kv_ref[n, rows, :]
                scores = jnp.dot(kv, right_ref[n, 0, :, cols], preferred_element_type=f32)
                grad_soft = jnp.dot(kv, right_ref[n, 1, :, cols], preferred_element_type=f32)
                soft = jnp.where(same, jnp.exp(scores - log_ref[head, :, cols]), 0.0)
                grad_scores = (soft * (grad_soft - inner_ref[n, :, cols])).astype(bf16)
                total = totals[n] + jnp.dot(
                    soft.astype(bf16), og_ref[n, cols, :], preferred_element_type=f32
                )
                total = total + jnp.dot(
                    grad_scores, q0_ref[n, cols, :], preferred_element_type=f32
                )
                dq_ref[n, :, cols] += jnp.dot(
                    kt_ref[pl.ds(head * dim, dim), rows], grad_scores,
                    preferred_element_type=f32,
                )
                result.append(total)
            return tuple(result)

        low, high = block_span(j * unit, unit, shard, ends)
        start = (jnp.zeros((unit, 2 * dim), f32),) * heads
        totals = lax.fori_loop(low, high, query_block, start)
        for n in range(heads):
            part = slice(2 * dim * n, 2 * dim * (n + 1))
            total = totals[n].astype(bf16)
            joint_ref[rows, part] = total
            turned_ref[part, rows] = jnp.transpose(total, (1, 0))
        return unused

    lax.fori_loop(0, 2 * blocks, key_block, 0)
    dq = (dq_ref[...] * dim ** (-0.5)).astype(bf16).reshape(heads * dim, slots)
    turned_ref[2 * dim * heads :, :] = dq
    joint_ref[:, 2 * dim * heads :] = jnp.transpose(dq, (1, 0))
    fetch.wait()
    made_ref[...] = jnp.dot(turned_ref[...], rows_ref[...], preferred_element_type=f32)
    gains = jnp.zeros((1, rows_ref.shape[1]), f32)
    shifts = jnp.zeros((1, rows_ref.shape[1]), f32)
    for at, weight_ref, first, size in stacked_parts(
        first_head, heads, qw_ref, kw_ref, vw_ref
    ):
        weight = weight_ref[first : first + size, :].astype(f32)
        gains += jnp.sum(weight * made_ref[at : at + size, :], axis=0, keepdims=True)
        total = jnp.sum(turned_ref[at : at + size, :].astype(f32), axis=1, keepdims=True)
        shifts += jnp.sum(weight * total, axis=0, keepdims=True)
    sums_ref[0:1] = gains
    sums_ref[1:2] = shifts
    if halves == 2:
        half = made_ref.shape[0] // 2
        bit = bit_ref[0, 0]
        part_refs[0][...] = made_ref[rows_at(bit, half), :].astype(bf16)
        part_refs[1][...] = made_ref[rows_at(1 - bit, half), :].astype(bf16)
    else:
        part_refs[0][...] = made_ref[...].astype(bf16)


def attend_back(
    first_head, heads, halves, lens, rank, bit, qt, kt, vt, logs, weights, normed, outs, grads
):
    slots, width = normed.shape
    blocks = len(outs)
    dim = HEAD_DIM
    cols = 3 * dim * heads
    return pl.pallas_call(
        functools.partial(backward_kernel, first_head, heads, blocks, halves),
        out_shape=(
            jax.ShapeDtypeStruct((slots, cols), bf16),
            jax.ShapeDtypeStruct((2, width), f32),
        )
        + (jax.ShapeDtypeStruct((cols // halves, width), bf16),) * halves,
        in_specs=[SMEM, SMEM, SMEM]
        + [VMEM] * 7
        + [pl.BlockSpec(memory_space=pl.ANY)]
        + [VMEM] * (2 * blocks),
        out_specs=(VMEM,) * (2 + halves),
        scratch_shapes=[pltpu.VMEM((heads, slots, 2 * dim), bf16)] * 3
        + [
            pltpu.VMEM((heads, 2, 2 * dim, slots), bf16),
            pltpu.VMEM((heads, 1, slots), f32),
            pltpu.VMEM((heads, dim, slots), f32),
            pltpu.VMEM((cols, width), f32),
            pltpu.VMEM((cols, slots), bf16),
            pltpu.VMEM((slots, width), bf16),
            pltpu.SemaphoreType.DMA,
        ],
        name="attend_back",
        compiler_params=pltpu.CompilerParams(vmem_limit_bytes=60 * 2**20),
        cost_estimate=COST,
    )(lens, rank, bit, qt, kt, vt, logs, *weights, normed, *outs, *grads)


def plan_kernel(capacity, lens_ref, rank_ref, routes_ref, order_ref, grad_ref,
                dispatch_ref, slots_ref):
    shard = routes_ref.shape[1]
    first = rank_ref[0, 0] * shard
    ends = item_ends(lens_ref)
    chosen_row = routes_ref[...]
    chosen_col = jnp.transpose(jnp.broadcast_to(chosen_row, (128, shard)), (1, 0))[:, 0:1]
    order_row = order_ref[...]
    order_col = jnp.transpose(jnp.broadcast_to(order_row, (128, shard)), (1, 0))[:, 0:1]
    alive_row = segments_at(
        first + lax.broadcasted_iota(jnp.int32, (1, shard), 1), ends
    ) < len(ends)
    alive_col = segments_at(
        first + lax.broadcasted_iota(jnp.int32, (shard, 1), 0), ends
    ) < len(ends)
    ahead = (chosen_col == chosen_row) & (order_col < order_row) & alive_col
    ranked = jnp.sum(ahead.astype(jnp.int32), axis=0, keepdims=True)
    kept = alive_row & (ranked < capacity)
    slot = jnp.where(kept, chosen_row * capacity + ranked, -1)
    dispatch = (
        lax.broadcasted_iota(jnp.int32, dispatch_ref.shape, 0) == slot
    ).astype(f32).astype(bf16)
    dispatch_ref[...] = dispatch
    slots_ref[...] = jnp.dot(
        dispatch, grad_ref[...], preferred_element_type=f32
    ).astype(bf16)


def plan(lens, rank, routes, order, grads, capacity, experts_all):
    shard, width = grads.shape
    count = experts_all * capacity
    return pl.pallas_call(
        functools.partial(plan_kernel, capacity),
        out_shape=(
            jax.ShapeDtypeStruct((count, shard), bf16),
            jax.ShapeDtypeStruct((count, width), bf16),
        ),
        in_specs=[SMEM, SMEM, VMEM, VMEM, VMEM],
        out_specs=(VMEM, VMEM),
        name="plan",
        cost_estimate=COST,
    )(lens, rank, routes.reshape(1, -1), order, grads)


def across(left, right):
    return lax.dot_general(
        left, right, (((1,), (1,)), ((), ())), preferred_element_type=f32
    )


def middle_kernel(count, rank_ref, tokens_ref, gain_ref, bias_ref, dispatch_ref, *refs):
    head_refs, weight_refs = refs[:count], refs[count : 2 * count]
    residual_ref, rows_ref = refs[2 * count :]
    residual = tokens_ref[...].astype(f32)
    for head_ref, weight_ref in zip(head_refs, weight_refs):
        residual = residual + contract_rows(head_ref[...], weight_ref[...])
    residual_ref[...] = residual
    normed = (normalized(residual) * gain_ref[...][None] + bias_ref[...][None]).astype(bf16)
    rows_ref[...] = jnp.dot(
        dispatch_ref[...], normed, preferred_element_type=f32
    ).astype(bf16)


def middle(rank, tokens, gain, bias, dispatch, heads, weights):
    count, shard = dispatch.shape
    width = tokens.shape[1]
    fixed = lambda array: pl.BlockSpec(array.shape, lambda i, r: (0,) * array.ndim)
    small = [gain, bias, dispatch, *heads, *weights]
    return pl.pallas_call(
        functools.partial(middle_kernel, len(heads)),
        grid_spec=pltpu.PrefetchScalarGridSpec(
            num_scalar_prefetch=1,
            grid=(1,),
            in_specs=[pl.BlockSpec((shard, width), lambda i, r: (r[0], 0))]
            + [fixed(array) for array in small],
            out_specs=(
                pl.BlockSpec((shard, width), lambda i, r: (0, 0)),
                pl.BlockSpec((count, width), lambda i, r: (0, 0)),
            ),
        ),
        out_shape=(
            jax.ShapeDtypeStruct((shard, width), f32),
            jax.ShapeDtypeStruct((count, width), bf16),
        ),
        name="middle",
        cost_estimate=COST,
    )(rank, tokens, *small)


def turn_kernel(
    count, lens_ref, rank_ref, dispatch_ref, back_ref, residual_ref, cotangent_ref,
    gain_ref, *refs
):
    head_refs, weight_refs = refs[:count], refs[count : 2 * count]
    grad_ref, sums_ref, kept_ref, sent_ref = refs[2 * count : 2 * count + 4]
    part_refs = refs[2 * count + 4 :]
    shard = residual_ref.shape[0]
    grad_normed = contract_rows(dispatch_ref[...], back_ref[...])
    values = residual_ref[...]
    centred = values - jnp.mean(values, axis=-1, keepdims=True)
    inverse = lax.rsqrt(jnp.mean(centred * centred, axis=-1, keepdims=True) + EPSILON)
    normed = centred * inverse
    sums_ref[0:1] = jnp.sum(grad_normed * normed, axis=0, keepdims=True)
    sums_ref[1:2] = jnp.sum(grad_normed, axis=0, keepdims=True)
    scaled = grad_normed * gain_ref[...][None]
    grad = cotangent_ref[...].astype(f32) + inverse * (
        scaled
        - jnp.mean(scaled, axis=-1, keepdims=True)
        - normed * jnp.mean(scaled * normed, axis=-1, keepdims=True)
    )
    grad_ref[...] = grad
    low = grad.astype(bf16)
    place = rank_ref[0, 0] * shard + lax.broadcasted_iota(jnp.int32, (1, shard), 1)
    alive = place < item_ends(lens_ref)[-1]
    for weight_ref, part_ref in zip(weight_refs, part_refs):
        part_ref[...] = jnp.where(alive, across(weight_ref[...], low), 0.0).astype(bf16)
    for j, head_ref in enumerate(head_refs):
        made = jnp.dot(head_ref[...], low, preferred_element_type=f32)
        (kept_ref, sent_ref)[j % 2][j // 2] = made.astype(bf16)


def turn(lens, rank, dispatch, back, residual, cotangent, gain, heads, weights):
    shard, width = residual.shape
    cols = weights[0].shape[0]
    count = len(weights)
    return pl.pallas_call(
        functools.partial(turn_kernel, count),
        out_shape=(
            jax.ShapeDtypeStruct((shard, width), f32),
            jax.ShapeDtypeStruct((2, width), f32),
            jax.ShapeDtypeStruct((count // 2, cols, width), bf16),
            jax.ShapeDtypeStruct((count // 2, cols, width), bf16),
        )
        + (jax.ShapeDtypeStruct((cols, shard), bf16),) * count,
        in_specs=[SMEM, SMEM] + [VMEM] * (5 + 2 * count),
        out_specs=(VMEM,) * (4 + count),
        name="turn",
        cost_estimate=COST,
    )(lens, rank, dispatch, back, residual, cotangent, gain, *heads, *weights)


def gelu_parts(values):
    below = 0.5 + 0.5 * lax.erf(values * (0.5**0.5))
    density = jnp.exp(-0.5 * values * values) * (0.5 / jnp.pi) ** 0.5
    return values * below, below + values * density


def expert_kernel(in_ref, grad_act_ref, up_ref, act_ref, mid_ref, sum_ref):
    step = pl.program_id(0)
    pre = jnp.dot(in_ref[...], up_ref[...], preferred_element_type=f32)
    act, slope = gelu_parts(pre)
    act_ref[...] = act.astype(bf16)
    grad_pre = (grad_act_ref[...] * slope).astype(bf16)
    mid = lax.dot_general(
        grad_pre, up_ref[...], (((1,), (1,)), ((), ())), preferred_element_type=f32
    )

    @pl.when(step == 0)
    def first():
        sum_ref[...] = mid

    @pl.when(step > 0)
    def later():
        sum_ref[...] += mid

    @pl.when(step == pl.num_programs(0) - 1)
    def last():
        mid_ref[...] = sum_ref[...].astype(bf16)


def expert(rows, grad_act, up):
    count, width = rows.shape
    hidden = up.shape[1]
    size = min(512, hidden)
    return pl.pallas_call(
        expert_kernel,
        grid=(hidden // size,),
        out_shape=(
            jax.ShapeDtypeStruct((count, hidden), bf16),
            jax.ShapeDtypeStruct((count, width), bf16),
        ),
        in_specs=[
            pl.BlockSpec((count, width), lambda i: (0, 0)),
            pl.BlockSpec((count, size), lambda i: (0, i)),
            pl.BlockSpec((width, size), lambda i: (0, i)),
        ],
        out_specs=(
            pl.BlockSpec((count, size), lambda i: (0, i)),
            pl.BlockSpec((count, width), lambda i: (0, 0)),
        ),
        scratch_shapes=[pltpu.VMEM((count, width), f32)],
        name="expert",
        cost_estimate=COST,
    )(rows, grad_act, up)


def product_kernel(a_ref, b_ref, out_ref, sum_ref):
    step = pl.program_id(0)
    made = jnp.dot(a_ref[...], b_ref[...], preferred_element_type=f32)

    @pl.when(step == 0)
    def first():
        sum_ref[...] = made

    @pl.when(step > 0)
    def later():
        sum_ref[...] += made

    @pl.when(step == pl.num_programs(0) - 1)
    def last():
        out_ref[...] = sum_ref[...].astype(bf16)


def product(a, b):
    count, depth = a.shape
    width = b.shape[1]
    size = min(1024, depth)
    return pl.pallas_call(
        product_kernel,
        grid=(depth // size,),
        out_shape=jax.ShapeDtypeStruct((count, width), bf16),
        in_specs=[
            pl.BlockSpec((count, size), lambda i: (0, i)),
            pl.BlockSpec((size, width), lambda i: (i, 0)),
        ],
        out_specs=pl.BlockSpec((count, width), lambda i: (0, 0)),
        scratch_shapes=[pltpu.VMEM((count, width), f32)],
        name="product",
        cost_estimate=COST,
    )(a, b)


def weight_kernel(groups, rank_ref, up_ref, down_ref, *refs):
    dup_ref, ddown_ref = refs[-2:]
    dup = ddown = 0.0
    for g in range(groups):
        in_ref, grad_ref = refs[2 * g : 2 * g + 2]
        pre = jnp.dot(in_ref[...], up_ref[...], preferred_element_type=f32)
        grad_act = lax.dot_general(
            grad_ref[...], down_ref[...], (((1,), (1,)), ((), ())),
            preferred_element_type=f32,
        )
        act, slope = gelu_parts(pre)
        dup = dup + contract_rows(in_ref[...], (grad_act * slope).astype(bf16))
        ddown = ddown + contract_rows(act.astype(bf16), grad_ref[...])
    if len(refs) > 2 * groups + 2:
        dup = dup + refs[2 * groups][...]
        ddown = ddown + refs[2 * groups + 1][...]
    dup_ref[...] = dup
    ddown_ref[...] = ddown


def expert_weights(rank, group, up, down, parts, earlier=()):
    count, width = group[0][0].shape
    hidden = up.shape[1] // parts
    size = min(256, hidden)
    blocks = hidden // size
    up_block = pl.BlockSpec((width, size), lambda i, r: (0, i))
    down_block = pl.BlockSpec((size, width), lambda i, r: (i, 0))
    rows = [values for both in group for values in both]
    return pl.pallas_call(
        functools.partial(weight_kernel, len(group)),
        grid_spec=pltpu.PrefetchScalarGridSpec(
            num_scalar_prefetch=1,
            grid=(blocks,),
            in_specs=[
                pl.BlockSpec((width, size), lambda i, r: (0, r[0] * blocks + i)),
                pl.BlockSpec((size, width), lambda i, r: (r[0] * blocks + i, 0)),
            ]
            + [pl.BlockSpec((count, width), lambda i, r: (0, 0))] * len(rows)
            + ([up_block, down_block] if earlier else []),
            out_specs=(up_block, down_block),
        ),
        out_shape=(
            jax.ShapeDtypeStruct((width, hidden), f32),
            jax.ShapeDtypeStruct((hidden, width), f32),
        ),
        name="expert_weights",
        cost_estimate=COST,
    )(rank, up, down, *rows, *earlier)


def input_grad_kernel(groups, qw_ref, kw_ref, vw_ref, *refs):
    joint_refs = refs[: len(groups)]
    kept_ref, sent_ref, turned_ref = refs[len(groups) :]
    step = pl.program_id(0)

    @pl.when(step == 0)
    def stack():
        start = 0
        for first_head, heads in groups:
            for at, weight_ref, first, size in stacked_parts(
                first_head, heads, qw_ref, kw_ref, vw_ref
            ):
                turned_ref[start + at : start + at + size, :] = weight_ref[
                    first : first + size, :
                ]
            start += 3 * heads * HEAD_DIM

    total = 0.0
    at = 0
    for joint_ref in joint_refs:
        rows = slice(at, at + joint_ref.shape[1])
        total = total + jnp.dot(
            joint_ref[...], turned_ref[rows, :], preferred_element_type=f32
        )
        at += joint_ref.shape[1]

    @pl.when(step % 2 == 0)
    def keep():
        kept_ref[0] = total.astype(bf16)

    @pl.when(step % 2 == 1)
    def send():
        sent_ref[0] = total.astype(bf16)


def input_grad(groups, weights, joints, first, count, size):
    cols, width = weights[0].shape
    fixed = pl.BlockSpec((cols, width), lambda i: (0, 0))
    return pl.pallas_call(
        functools.partial(input_grad_kernel, groups),
        grid=(count,),
        out_shape=(jax.ShapeDtypeStruct((count // 2, size, width), bf16),) * 2,
        in_specs=[fixed] * 3
        + [
            pl.BlockSpec((size, joint.shape[1]), lambda i: (first + i, 0))
            for joint in joints
        ],
        out_specs=(pl.BlockSpec((1, size, width), lambda i: (i // 2, 0, 0)),) * 2,
        scratch_shapes=[pltpu.VMEM((3 * cols, width), bf16)],
        name="input_grad",
        cost_estimate=COST,
    )(*weights, *joints)


def close_kernel(rank_ref, tokens_ref, gain_ref, grad_ref, *refs):
    *part_refs, out_ref = refs
    grad_in = 0.0
    for part_ref in part_refs:
        grad_in = grad_in + part_ref[...].reshape(out_ref.shape).astype(f32)
    values = tokens_ref[...].astype(f32)
    centred = values - jnp.mean(values, axis=-1, keepdims=True)
    inverse = lax.rsqrt(jnp.mean(centred * centred, axis=-1, keepdims=True) + EPSILON)
    normed = centred * inverse
    scaled = grad_in * gain_ref[...][None]
    out_ref[...] = grad_ref[...] + inverse * (
        scaled
        - jnp.mean(scaled, axis=-1, keepdims=True)
        - normed * jnp.mean(scaled * normed, axis=-1, keepdims=True)
    )


def close(rank, tokens, gain, grad, parts):
    shard, width = grad.shape
    size = shard // 2
    rows = lambda i, r: (i, 0)
    return pl.pallas_call(
        close_kernel,
        grid_spec=pltpu.PrefetchScalarGridSpec(
            num_scalar_prefetch=1,
            grid=(2,),
            in_specs=[
                pl.BlockSpec((size, width), lambda i, r: (2 * r[0] + i, 0)),
                pl.BlockSpec((width,), lambda i, r: (0,)),
                pl.BlockSpec((size, width), rows),
            ]
            + [pl.BlockSpec((1, size, width), lambda i, r: (0, i, 0))] * len(parts),
            out_specs=pl.BlockSpec((size, width), rows),
        ),
        out_shape=jax.ShapeDtypeStruct((shard, width), f32),
        name="close",
        cost_estimate=COST,
    )(rank, tokens, gain, grad, *parts)


def add_low(a, b):
    return (a.astype(f32) + b.astype(f32)).astype(bf16)


def tie(*values):
    return lax.optimization_barrier(values)


def finish_kernel(groups, counts, bit_ref, *refs):
    pieces, refs = refs[: sum(counts)], refs[sum(counts) :]
    query_ref, key_ref, value_ref = refs[:3]
    bit = bit_ref[0, 0]
    for (first_head, heads), count, whole_ref in zip(groups, counts, refs[3:]):
        own, pieces = pieces[:count], pieces[count:]
        if count == 2:
            half = whole_ref.shape[0] // 2
            whole_ref[rows_at(bit, half), :] = own[0][...].astype(f32)
            whole_ref[rows_at(1 - bit, half), :] = own[1][...].astype(f32)
        else:
            whole_ref[...] = own[0][...].astype(f32)
        for at, target_ref, first, size in stacked_parts(
            first_head, heads, query_ref, key_ref, value_ref
        ):
            target_ref[first : first + size, :] = whole_ref[at : at + size, :]


def finish(groups, bit, pieces):
    width = pieces[0][0].shape[1]
    cols = sum(heads for first_head, heads in groups) * HEAD_DIM
    flat = [part for piece in pieces for part in piece]
    return pl.pallas_call(
        functools.partial(finish_kernel, groups, [len(piece) for piece in pieces]),
        out_shape=(jax.ShapeDtypeStruct((cols, width), f32),) * 3,
        in_specs=[SMEM] + [VMEM] * len(flat),
        out_specs=(VMEM,) * 3,
        scratch_shapes=[
            pltpu.VMEM((3 * heads * HEAD_DIM, width), f32) for first_head, heads in groups
        ],
        name="finish",
        cost_estimate=COST,
    )(bit, *flat)


def scatter_rows(values, axis):
    count = lax.axis_size(axis)
    rows, cols = values.shape
    parts = values.reshape(count, rows // count, cols)
    arrived = lax.all_to_all(parts, axis, split_axis=0, concat_axis=0, tiled=True)
    return jnp.sum(arrived.astype(f32), axis=0).astype(bf16)


def gather_rows(values, axis):
    count = lax.axis_size(axis)
    spread = jnp.broadcast_to(values[None], (count,) + values.shape)
    full = lax.all_to_all(spread, axis, split_axis=0, concat_axis=0, tiled=True)
    return full.reshape(count * values.shape[0], values.shape[1]).astype(f32)


def sum_everywhere(values, axes):
    count = 1
    for axis in axes:
        count *= lax.axis_size(axis)
    spread = jnp.broadcast_to(values[None], (count,) + values.shape)
    full = lax.all_to_all(spread, axes, split_axis=0, concat_axis=0, tiled=True)
    return jnp.sum(full, axis=0)


def on_device(
    tokens,
    first_gain,
    first_bias,
    query_weight,
    key_weight,
    value_weight,
    output_weight,
    second_gain,
    second_bias,
    expert_up,
    expert_down,
    item_lengths,
    routes,
    slot_order,
    cotangent,
):
    slots_all, width = tokens.shape
    members = lax.axis_size("tensor")
    shard_rows = slots_all // members
    rank = lax.axis_index("tensor")
    sources = lax.axis_size("dp")
    experts_all = sources * expert_up.shape[0]
    capacity = shard_rows // experts_all
    head_cols = query_weight.shape[1]
    heads = head_cols // HEAD_DIM
    up_matrix = expert_up[0]
    down_matrix = expert_down[0]
    rank_cell = rank.astype(jnp.int32).reshape(1, 1)

    def exchange(rows):
        return lax.all_to_all(
            rows.reshape(sources, -1, width), "dp", split_axis=0, concat_axis=0, tiled=True
        ).reshape(-1, width)

    qw, kw, vw = query_weight.T, key_weight.T, value_weight.T

    dispatch, grad_slots = plan(
        item_lengths, rank_cell, routes, slot_order, cotangent, capacity, experts_all
    )
    flat_grad = exchange(grad_slots)
    tokens, grad_slots = tie(tokens, grad_slots)
    normed_in, qt, kt, vt = project(
        rank_cell[0], tokens, first_gain, first_bias, qw, kw, vw, members
    )
    outputs = [output_weight] + [
        swap(output_weight, "tensor", k) for k in range(1, members)
    ]
    *own_heads, logs = attend(item_lengths, rank_cell, qt, kt, vt, members)
    own_heads, flat_grad, outputs = tie(own_heads, flat_grad, outputs)
    all_heads = [own_heads[0]] + [
        swap(own_heads[j], "tensor", j) for j in range(1, members)
    ]
    grad_act = across(flat_grad, down_matrix)
    all_heads, grad_act = tie(all_heads, grad_act)
    residual, outgoing = middle(
        rank_cell[0], tokens, second_gain, second_bias, dispatch, all_heads, outputs
    )
    flat_in = exchange(outgoing)

    flat_grad, outgoing = tie(flat_grad, outgoing)
    gathered_grads = [flat_grad]
    gathered_rows = [flat_in]
    steps = steps_of(members)
    for step in reversed(steps[1:]):
        gathered_grads += [swap(a, "tensor", step) for a in gathered_grads]
    flat_in, gathered_grads = tie(flat_in, gathered_grads)
    gathered_rows = [flat_in]
    for step in reversed(steps[1:]):
        gathered_rows += [swap(a, "tensor", step) for a in gathered_rows]
    near_grads = swap(gathered_grads[0], "tensor", 1)
    near_rows = swap(flat_in, "tensor", 1)
    far_grads = [swap(a, "tensor", 1) for a in gathered_grads[1:]]
    act, grad_mid = expert(flat_in, grad_act, up_matrix)
    act, grad_mid, near_rows, near_grads, far_grads = tie(
        act, grad_mid, near_rows, near_grads, far_grads
    )
    grad_back = exchange(grad_mid)

    act, near_rows, grad_mid = tie(act, near_rows, grad_mid)
    made = product(act, down_matrix)
    sums = expert_weights(
        rank_cell[0],
        [(flat_in, gathered_grads[0]), (near_rows, near_grads)],
        up_matrix, down_matrix, members,
    )
    made, sums, gathered_rows = tie(made, sums, gathered_rows)
    far_rows = [swap(a, "tensor", 1) for a in gathered_rows[1:]]
    grad_back, made, sums = tie(grad_back, made, sums)

    grad_res, sums_second, kept, sent, *grad_heads = turn(
        item_lengths, rank_cell, dispatch, grad_back, residual, cotangent,
        second_gain, all_heads, outputs,
    )
    grad_parts = [grad_heads[0]] + [
        swap(grad_heads[j], "tensor", j) for j in range(1, members)
    ]
    sums, grad_heads = tie(sums, grad_heads)
    output_sum = add_low(kept, swap(sent, "tensor", 1))
    sums = expert_weights(
        rank_cell[0],
        list(zip(gathered_rows[1:], gathered_grads[1:])) + list(zip(far_rows, far_grads)),
        up_matrix, down_matrix, members, sums,
    )
    grad_parts, sums, output_sum = tie(grad_parts, sums, output_sum)
    up_grad, down_grad = sums
    made, up_grad = tie(made, up_grad)
    returned = exchange(made)

    bit_cell = (lax.axis_index("dp") & 1).astype(jnp.int32).reshape(1, 1)
    weights = (qw, kw, vw)
    back = functools.partial(
        attend_back, lens=item_lengths, rank=rank_cell, bit=bit_cell, qt=qt, kt=kt, vt=vt,
        logs=logs, weights=weights, normed=normed_in, outs=own_heads,
    )
    groups = ((0, heads - 1), (heads - 1, 1))
    joint_a, sums_a, own_a, away_a = back(*groups[0], halves=2, grads=grad_parts)
    for step in steps[1:]:
        output_sum = add_low(
            output_sum[: len(output_sum) // 2],
            swap(output_sum[len(output_sum) // 2 :], "tensor", step),
        )
    joint_a, away_a, output_sum, grad_parts, returned = tie(
        joint_a, away_a, output_sum, grad_parts, returned
    )
    half_a = add_low(own_a, swap(away_a, "dp", 1))
    joint_b, sums_b, part_b = back(*groups[1], halves=1, grads=grad_parts)
    output_part = scatter_rows(output_sum[0], "dp")
    joint_b, part_b, half_a, output_part = tie(joint_b, part_b, half_a, output_part)

    dp_steps = steps_of(sources)
    far = members // 2
    far_kept, far_sent = input_grad(
        groups, weights, (joint_a, joint_b), far, members - far, shard_rows
    )
    near_kept, near_sent = input_grad(
        groups, weights, (joint_a, joint_b), 0, far, shard_rows
    )
    part_b = add_low(part_b, swap(part_b, "dp", dp_steps[0]))
    far_kept = add_low(far_kept, swap(far_sent, "tensor", 1))
    near_core = swap(near_sent, "tensor", 1)
    sums_first = sums_a + sums_b
    far_kept, part_b, sums_first, output_part = tie(
        far_kept, part_b, sums_first, output_part
    )
    near_far = swap(far_kept, "tensor", 2)
    for step in dp_steps[1:]:
        half_a = add_low(half_a, swap(half_a, "dp", step))
        part_b = add_low(part_b, swap(part_b, "dp", step))
    pieces = [(half_a, swap(half_a, "dp", 1)), (part_b,)]
    token_grad = close(
        rank_cell[0], tokens, first_gain, grad_res, (near_kept, near_core, near_far)
    )

    first_gain_part = (sums_first[0] - first_bias * sums_first[1]) / first_gain
    norm_sums = sum_everywhere(
        jnp.stack([first_gain_part, sums_first[1], sums_second[0], sums_second[1]]),
        ("dp", "tensor"),
    )
    output_grad = gather_rows(output_part, "dp")
    block_out = residual + contract_rows(dispatch, returned)
    query_grad, key_grad, value_grad = finish(groups, bit_cell, pieces)
    return (
        block_out,
        token_grad,
        norm_sums[0],
        norm_sums[1],
        query_grad.T,
        key_grad.T,
        value_grad.T,
        output_grad,
        norm_sums[2],
        norm_sums[3],
        up_grad[None],
        down_grad[None],
    )


def solution(mesh):
    in_specs = (
        P("dp", None),
        P(),
        P(),
        P(None, "tensor"),
        P(None, "tensor"),
        P(None, "tensor"),
        P("tensor", None),
        P(),
        P(),
        P("dp", None, None),
        P("dp", None, None),
        P("dp", None),
        P(("dp", "tensor"), None),
        P(("dp", "tensor"), None),
        P(("dp", "tensor"), None),
    )
    out_specs = (
        P(("dp", "tensor"), None),
        P(("dp", "tensor"), None),
        P(),
        P(),
        P(None, "tensor"),
        P(None, "tensor"),
        P(None, "tensor"),
        P("tensor", None),
        P(),
        P(),
        P("dp", None, "tensor"),
        P("dp", "tensor", None),
    )
    return jax.shard_map(
        on_device, mesh=mesh, in_specs=in_specs, out_specs=out_specs, check_vma=False
    )
```

```python
import functools

import jax
import jax.numpy as jnp
from jax import lax
from jax.experimental import pallas as pl
from jax.experimental.pallas import tpu as pltpu
from jax.sharding import PartitionSpec as P

HEAD_DIM = 64
EPSILON = 1e-05
NEGATIVE = -1e30
f32 = jnp.float32
bf16 = jnp.bfloat16
VMEM = pl.BlockSpec(memory_space=pltpu.VMEM)
SMEM = pl.BlockSpec(memory_space=pltpu.SMEM)
SUM_ROWS = 16
COST = pl.CostEstimate(flops=2**20, bytes_accessed=2**20, transcendentals=0)


def layer_norm(values, gain, shift):
    average = jnp.mean(values, axis=-1, keepdims=True)
    centred = values - average
    variance = jnp.mean(centred * centred, axis=-1, keepdims=True)
    return centred * lax.rsqrt(variance + EPSILON) * gain + shift


def contract_rows(left, right):
    return lax.dot_general(
        left, right, (((0,), (0,)), ((), ())), preferred_element_type=f32
    )


def swap(values, axis, step):
    count = lax.axis_size(axis)
    return lax.ppermute(values, axis, [(i, i ^ step) for i in range(count)])


def steps_of(count):
    steps = []
    step = 1
    while step < count:
        steps.append(step)
        step *= 2
    return steps


def normalized(values):
    average = jnp.mean(values, axis=-1, keepdims=True)
    centred = values - average
    variance = jnp.mean(centred * centred, axis=-1, keepdims=True)
    return centred * lax.rsqrt(variance + EPSILON)


def project_kernel(
    rank_ref, tokens_ref, gain_ref, bias_ref, qw_ref, kw_ref, vw_ref,
    normed_ref, qt_ref, kt_ref, vt_ref,
):
    values = tokens_ref[...].astype(f32)
    normed = (normalized(values) * gain_ref[...][None] + bias_ref[...][None]).astype(bf16)
    normed_ref[...] = normed
    for weight_ref, out_ref, factor in (
        (qw_ref, qt_ref, HEAD_DIM ** (-0.5)), (kw_ref, kt_ref, None), (vw_ref, vt_ref, None)
    ):
        made = lax.dot_general(
            weight_ref[...], normed, (((1,), (1,)), ((), ())), preferred_element_type=f32
        ).astype(bf16)
        if factor is not None:
            made = made * jnp.asarray(factor, bf16)
        out_ref[...] = made


def project(rank, tokens, gain, bias, qw, kw, vw, blocks):
    slots, width = tokens.shape
    cols = qw.shape[0]
    size = slots // blocks
    fixed = lambda i, r: (0, 0)
    line = pl.BlockSpec((width,), lambda i, r: (0,))
    return pl.pallas_call(
        project_kernel,
        grid_spec=pltpu.PrefetchScalarGridSpec(
            num_scalar_prefetch=1,
            grid=(blocks,),
            in_specs=[
                pl.BlockSpec((size, width), lambda i, r: (i ^ r[0], 0)),
                line,
                line,
                pl.BlockSpec((cols, width), fixed),
                pl.BlockSpec((cols, width), fixed),
                pl.BlockSpec((cols, width), fixed),
            ],
            out_specs=(
                pl.BlockSpec((size, width), lambda i, r: (i, 0)),
                pl.BlockSpec((cols, size), lambda i, r: (0, i)),
                pl.BlockSpec((cols, size), lambda i, r: (0, i)),
                pl.BlockSpec((cols, size), lambda i, r: (0, i)),
            ),
        ),
        out_shape=(jax.ShapeDtypeStruct((slots, width), bf16),)
        + (jax.ShapeDtypeStruct((cols, slots), bf16),) * 3,
        name="project",
        cost_estimate=COST,
    )(rank, tokens, gain, bias, qw, kw, vw)


def item_ends(lens_ref):
    ends = []
    total = jnp.int32(0)
    for i in range(lens_ref.shape[1]):
        total = total + lens_ref[0, i]
        ends.append(total)
    return ends


def segments_at(place, ends):
    segment = jnp.zeros_like(place)
    for end in ends:
        segment = segment + (place >= end).astype(jnp.int32)
    return segment


def block_span(first, size, unit, ends):
    last = jnp.minimum(first + size, ends[-1]) - 1
    low = jnp.int32(0)
    high = ends[-1]
    for end in ends:
        low = jnp.where(first >= end, end, low)
    for end in reversed(ends):
        high = jnp.where(last < end, end, high)
    empty = first >= ends[-1]
    low_block = jnp.where(empty, 0, low // unit)
    high_block = jnp.where(empty, 0, (high + unit - 1) // unit)
    return low_block, high_block


def rows_at(block, size):
    return pl.ds(pl.multiple_of(block * size, size), size)


def memory_segments(block, size, shard, rank, ends, axis):
    shape = (1, size) if axis else (size, 1)
    at = block * size + lax.broadcasted_iota(jnp.int32, shape, axis)
    place = ((at // shard) ^ rank) * shard + at % shard
    return segments_at(place, ends)


def lane_masked(values, head):
    lane = lax.broadcasted_iota(jnp.int32, values.shape, 1)
    inside = (lane >= head * HEAD_DIM) & (lane < (head + 1) * HEAD_DIM)
    return jnp.where(inside, values, jnp.zeros_like(values))


def forward_kernel(
    lens_ref, rank_ref, qt_ref, kt_ref, vt_ref, *refs
):
    *out_refs, log_ref, masked_ref, out_ref = refs
    blocks, width, shard = out_ref.shape
    heads = width // HEAD_DIM
    pair = 1
    size = shard * pair
    rank = rank_ref[0, 0]
    ends = item_ends(lens_ref)
    keys = jnp.transpose(kt_ref[...], (1, 0))
    for h in range(heads):
        masked_ref[h] = lane_masked(keys, h)

    def query_block(i, unused):
        at = i ^ (rank // pair)
        cols = rows_at(at, size)
        seg_q = memory_segments(at, size, shard, rank, ends, 1)
        queries = qt_ref[:, cols]

        def key_block(j, carry):
            rows = rows_at(j ^ rank, shard)
            seg_k = memory_segments(j ^ rank, shard, shard, rank, ends, 0)
            same = seg_k == seg_q
            result = []
            for h in range(heads):
                highest, summed, total = carry[h]
                scores = jnp.dot(
                    masked_ref[h, rows, :], queries, preferred_element_type=f32
                )
                scores = jnp.where(same, scores, NEGATIVE)
                raised = jnp.maximum(highest, jnp.max(scores, axis=0, keepdims=True))
                shrink = jnp.exp(highest - raised)
                soft = jnp.exp(scores - raised)
                summed = summed * shrink + jnp.sum(soft, axis=0, keepdims=True)
                total = total * shrink + jnp.dot(
                    vt_ref[pl.ds(h * HEAD_DIM, HEAD_DIM), rows],
                    soft.astype(bf16),
                    preferred_element_type=f32,
                )
                result.append((raised, summed, total))
            return tuple(result)

        start = tuple(
            (
                jnp.full((1, size), NEGATIVE, f32),
                jnp.zeros((1, size), f32),
                jnp.zeros((HEAD_DIM, size), f32),
            )
            for h in range(heads)
        )
        low, high = block_span(i * size, size, shard, ends)
        done = lax.fori_loop(low, high, key_block, start)
        live = seg_q < len(ends)
        for h in range(heads):
            highest, summed, total = done[h]
            summed = jnp.where(live, summed, 1.0)
            result = jnp.where(live, total / summed, 0.0).astype(bf16)
            logs = jnp.where(live, highest + jnp.log(summed), -NEGATIVE)
            for p in range(pair):
                part = slice(p * shard, (p + 1) * shard)
                out_ref[at * pair + p, pl.ds(h * HEAD_DIM, HEAD_DIM), :] = result[:, part]
            log_ref[h, :, cols] = logs
        return unused

    lax.fori_loop(0, blocks // pair, query_block, 0)
    for b in range(blocks):
        out_refs[b][...] = out_ref[b]


def attend(lens, rank, qt, kt, vt, blocks):
    width, slots = qt.shape
    size = slots // blocks
    heads = width // HEAD_DIM
    return pl.pallas_call(
        forward_kernel,
        out_shape=(jax.ShapeDtypeStruct((width, size), bf16),) * blocks
        + (jax.ShapeDtypeStruct((heads, 1, slots), f32),),
        in_specs=[SMEM, SMEM, VMEM, VMEM, VMEM],
        out_specs=(VMEM,) * (blocks + 1),
        scratch_shapes=[
            pltpu.VMEM((heads, slots, width), bf16),
            pltpu.VMEM((blocks, width, size), bf16),
        ],
        name="attend",
        compiler_params=pltpu.CompilerParams(vmem_limit_bytes=60 * 2**20),
        cost_estimate=COST,
    )(lens, rank, qt, kt, vt)


def stacked_parts(first_head, heads, query, key, value):
    dim = HEAD_DIM
    parts = []
    for n in range(heads):
        first = (first_head + n) * dim
        parts += [(2 * n * dim, key, first, dim), ((2 * n + 1) * dim, value, first, dim)]
    return parts + [(2 * heads * dim, query, first_head * dim, heads * dim)]


def backward_kernel(
    first_head, heads, blocks, extras, lens_ref, rank_ref, bit_ref, qt_ref, kt_ref, vt_ref,
    log_ref, qw_ref, kw_ref, vw_ref, normed_ref, *rest
):
    extra_refs, rest = rest[:extras], rest[extras:]
    width, slots = qt_ref.shape
    shard = slots // blocks
    dim = HEAD_DIM
    out_refs, grad_refs = rest[:blocks], rest[blocks : 2 * blocks]
    joint_ref, sums_ref, own_ref, away_ref = rest[2 * blocks : 2 * blocks + 4]
    kv_ref, q0_ref, og_ref, right_ref, inner_ref, dq_ref, made_ref = rest[-10:-3]
    turned_ref, rows_ref, copied = rest[-3:]
    fetch = pltpu.make_async_copy(normed_ref, rows_ref, copied)
    fetch.start()
    unit = shard // 2
    rank = rank_ref[0, 0]
    ends = item_ends(lens_ref)
    zero = jnp.zeros((dim, slots), bf16)
    for n in range(heads):
        part = slice((first_head + n) * dim, (first_head + n + 1) * dim)
        both = jnp.concatenate([kt_ref[part, :], vt_ref[part, :]], axis=0)
        kv_ref[n] = jnp.transpose(both, (1, 0))
        padded = jnp.concatenate([qt_ref[part, :], zero], axis=0)
        q0_ref[n] = jnp.transpose(padded, (1, 0))
        right_ref[n, 0] = padded
        for b in range(blocks):
            grad = grad_refs[b][part, :]
            cols = slice(b * shard, (b + 1) * shard)
            padded = jnp.concatenate([zero[:, :shard], grad], axis=0)
            og_ref[n, cols, :] = jnp.transpose(padded, (1, 0))
            right_ref[n, 1, :, cols] = padded
            inner_ref[n, :, cols] = jnp.sum(
                out_refs[b][part, :].astype(f32) * grad.astype(f32), axis=0, keepdims=True
            )
    dq_ref[...] = jnp.zeros_like(dq_ref)

    def key_block(j, unused):
        at_key = ((j // 2) ^ rank) * 2 + j % 2
        rows = rows_at(at_key, unit)
        seg_k = memory_segments(at_key, unit, shard, rank, ends, 0)

        def query_block(i, totals):
            at = i ^ rank
            cols = rows_at(at, shard)
            same = seg_k == memory_segments(at, shard, shard, rank, ends, 1)
            result = []
            for n in range(heads):
                head = first_head + n
                kv = kv_ref[n, rows, :]
                scores = jnp.dot(kv, right_ref[n, 0, :, cols], preferred_element_type=f32)
                grad_soft = jnp.dot(kv, right_ref[n, 1, :, cols], preferred_element_type=f32)
                soft = jnp.where(same, jnp.exp(scores - log_ref[head, :, cols]), 0.0)
                grad_scores = (soft * (grad_soft - inner_ref[n, :, cols])).astype(bf16)
                total = totals[n] + jnp.dot(
                    soft.astype(bf16), og_ref[n, cols, :], preferred_element_type=f32
                )
                total = total + jnp.dot(
                    grad_scores, q0_ref[n, cols, :], preferred_element_type=f32
                )
                dq_ref[n, :, cols] += jnp.dot(
                    kt_ref[pl.ds(head * dim, dim), rows], grad_scores,
                    preferred_element_type=f32,
                )
                result.append(total)
            return tuple(result)

        low, high = block_span(j * unit, unit, shard, ends)
        start = (jnp.zeros((unit, 2 * dim), f32),) * heads
        totals = lax.fori_loop(low, high, query_block, start)
        for n in range(heads):
            part = slice(2 * dim * n, 2 * dim * (n + 1))
            total = totals[n].astype(bf16)
            joint_ref[rows, part] = total
            turned_ref[part, rows] = jnp.transpose(total, (1, 0))
        return unused

    lax.fori_loop(0, 2 * blocks, key_block, 0)
    dq = (dq_ref[...] * dim ** (-0.5)).astype(bf16).reshape(heads * dim, slots)
    turned_ref[2 * dim * heads :, :] = dq
    joint_ref[:, 2 * dim * heads :] = jnp.transpose(dq, (1, 0))
    fetch.wait()
    made_ref[...] = jnp.dot(turned_ref[...], rows_ref[...], preferred_element_type=f32)
    gains = jnp.zeros((1, rows_ref.shape[1]), f32)
    shifts = jnp.zeros((1, rows_ref.shape[1]), f32)
    for at, weight_ref, first, size in stacked_parts(
        first_head, heads, qw_ref, kw_ref, vw_ref
    ):
        weight = weight_ref[first : first + size, :].astype(f32)
        gains += jnp.sum(weight * made_ref[at : at + size, :], axis=0, keepdims=True)
        total = jnp.sum(turned_ref[at : at + size, :].astype(f32), axis=1, keepdims=True)
        shifts += jnp.sum(weight * total, axis=0, keepdims=True)
    sums_ref[0:1] = gains
    sums_ref[1:2] = shifts
    half = made_ref.shape[0] // 2
    bit = bit_ref[0, 0]
    for part_ref, at in ((own_ref, bit), (away_ref, 1 - bit)):
        part_ref[0:half, :] = made_ref[rows_at(at, half), :].astype(bf16)
        if extras:
            lines = [sums_ref[...] + extra_refs[0][...], extra_refs[1][...]]
            lines.append(jnp.zeros((SUM_ROWS - 4, gains.shape[1]), f32))
            part_ref[half:, :] = jnp.concatenate(lines, axis=0).astype(bf16)


def attend_back(
    first_head, heads, extras, lens, rank, bit, qt, kt, vt, logs, weights, normed, outs, grads
):
    slots, width = normed.shape
    blocks = len(outs)
    dim = HEAD_DIM
    cols = 3 * dim * heads
    rows = cols // 2 + (SUM_ROWS if extras else 0)
    return pl.pallas_call(
        functools.partial(backward_kernel, first_head, heads, blocks, len(extras)),
        out_shape=(
            jax.ShapeDtypeStruct((slots, cols), bf16),
            jax.ShapeDtypeStruct((2, width), f32),
        )
        + (jax.ShapeDtypeStruct((rows, width), bf16),) * 2,
        in_specs=[SMEM, SMEM, SMEM]
        + [VMEM] * 7
        + [pl.BlockSpec(memory_space=pl.ANY)]
        + [VMEM] * (len(extras) + 2 * blocks),
        out_specs=(VMEM,) * 4,
        scratch_shapes=[pltpu.VMEM((heads, slots, 2 * dim), bf16)] * 3
        + [
            pltpu.VMEM((heads, 2, 2 * dim, slots), bf16),
            pltpu.VMEM((heads, 1, slots), f32),
            pltpu.VMEM((heads, dim, slots), f32),
            pltpu.VMEM((cols, width), f32),
            pltpu.VMEM((cols, slots), bf16),
            pltpu.VMEM((slots, width), bf16),
            pltpu.SemaphoreType.DMA,
        ],
        name="attend_back",
        compiler_params=pltpu.CompilerParams(vmem_limit_bytes=60 * 2**20),
        cost_estimate=COST,
    )(lens, rank, bit, qt, kt, vt, logs, *weights, normed, *extras, *outs, *grads)


def plan_kernel(capacity, lens_ref, rank_ref, routes_ref, order_ref, grad_ref,
                dispatch_ref, slots_ref):
    shard = routes_ref.shape[1]
    first = rank_ref[0, 0] * shard
    ends = item_ends(lens_ref)
    chosen_row = routes_ref[...]
    chosen_col = jnp.transpose(jnp.broadcast_to(chosen_row, (128, shard)), (1, 0))[:, 0:1]
    order_row = order_ref[...]
    order_col = jnp.transpose(jnp.broadcast_to(order_row, (128, shard)), (1, 0))[:, 0:1]
    alive_row = segments_at(
        first + lax.broadcasted_iota(jnp.int32, (1, shard), 1), ends
    ) < len(ends)
    alive_col = segments_at(
        first + lax.broadcasted_iota(jnp.int32, (shard, 1), 0), ends
    ) < len(ends)
    ahead = (chosen_col == chosen_row) & (order_col < order_row) & alive_col
    ranked = jnp.sum(ahead.astype(jnp.int32), axis=0, keepdims=True)
    kept = alive_row & (ranked < capacity)
    slot = jnp.where(kept, chosen_row * capacity + ranked, -1)
    dispatch = (
        lax.broadcasted_iota(jnp.int32, dispatch_ref.shape, 0) == slot
    ).astype(f32).astype(bf16)
    dispatch_ref[...] = dispatch
    slots_ref[...] = jnp.dot(
        dispatch, grad_ref[...], preferred_element_type=f32
    ).astype(bf16)


def plan(lens, rank, routes, order, grads, capacity, experts_all):
    shard, width = grads.shape
    count = experts_all * capacity
    return pl.pallas_call(
        functools.partial(plan_kernel, capacity),
        out_shape=(
            jax.ShapeDtypeStruct((count, shard), bf16),
            jax.ShapeDtypeStruct((count, width), bf16),
        ),
        in_specs=[SMEM, SMEM, VMEM, VMEM, VMEM],
        out_specs=(VMEM, VMEM),
        name="plan",
        cost_estimate=COST,
    )(lens, rank, routes.reshape(1, -1), order, grads)


def across(left, right):
    return lax.dot_general(
        left, right, (((1,), (1,)), ((), ())), preferred_element_type=f32
    )


def middle_kernel(count, rank_ref, tokens_ref, gain_ref, bias_ref, dispatch_ref, *refs):
    head_refs, weight_refs = refs[:count], refs[count : 2 * count]
    residual_ref, rows_ref = refs[2 * count :]
    residual = tokens_ref[...].astype(f32)
    for head_ref, weight_ref in zip(head_refs, weight_refs):
        residual = residual + contract_rows(head_ref[...], weight_ref[...])
    residual_ref[...] = residual
    normed = (normalized(residual) * gain_ref[...][None] + bias_ref[...][None]).astype(bf16)
    rows_ref[...] = jnp.dot(
        dispatch_ref[...], normed, preferred_element_type=f32
    ).astype(bf16)


def middle(rank, tokens, gain, bias, dispatch, heads, weights):
    count, shard = dispatch.shape
    width = tokens.shape[1]
    fixed = lambda array: pl.BlockSpec(array.shape, lambda i, r: (0,) * array.ndim)
    small = [gain, bias, dispatch, *heads, *weights]
    return pl.pallas_call(
        functools.partial(middle_kernel, len(heads)),
        grid_spec=pltpu.PrefetchScalarGridSpec(
            num_scalar_prefetch=1,
            grid=(1,),
            in_specs=[pl.BlockSpec((shard, width), lambda i, r: (r[0], 0))]
            + [fixed(array) for array in small],
            out_specs=(
                pl.BlockSpec((shard, width), lambda i, r: (0, 0)),
                pl.BlockSpec((count, width), lambda i, r: (0, 0)),
            ),
        ),
        out_shape=(
            jax.ShapeDtypeStruct((shard, width), f32),
            jax.ShapeDtypeStruct((count, width), bf16),
        ),
        name="middle",
        cost_estimate=COST,
    )(rank, tokens, *small)


def turn_kernel(
    count, lens_ref, rank_ref, dispatch_ref, back_ref, residual_ref, cotangent_ref,
    gain_ref, *refs
):
    head_refs, weight_refs = refs[:count], refs[count : 2 * count]
    grad_ref, sums_ref, kept_ref, sent_ref = refs[2 * count : 2 * count + 4]
    part_refs = refs[2 * count + 4 :]
    shard = residual_ref.shape[0]
    grad_normed = contract_rows(dispatch_ref[...], back_ref[...])
    values = residual_ref[...]
    centred = values - jnp.mean(values, axis=-1, keepdims=True)
    inverse = lax.rsqrt(jnp.mean(centred * centred, axis=-1, keepdims=True) + EPSILON)
    normed = centred * inverse
    sums_ref[0:1] = jnp.sum(grad_normed * normed, axis=0, keepdims=True)
    sums_ref[1:2] = jnp.sum(grad_normed, axis=0, keepdims=True)
    scaled = grad_normed * gain_ref[...][None]
    grad = cotangent_ref[...].astype(f32) + inverse * (
        scaled
        - jnp.mean(scaled, axis=-1, keepdims=True)
        - normed * jnp.mean(scaled * normed, axis=-1, keepdims=True)
    )
    grad_ref[...] = grad
    low = grad.astype(bf16)
    place = rank_ref[0, 0] * shard + lax.broadcasted_iota(jnp.int32, (1, shard), 1)
    alive = place < item_ends(lens_ref)[-1]
    for weight_ref, part_ref in zip(weight_refs, part_refs):
        part_ref[...] = jnp.where(alive, across(weight_ref[...], low), 0.0).astype(bf16)
    for j, head_ref in enumerate(head_refs):
        made = jnp.dot(head_ref[...], low, preferred_element_type=f32)
        (kept_ref, sent_ref)[j % 2][j // 2] = made.astype(bf16)


def turn(lens, rank, dispatch, back, residual, cotangent, gain, heads, weights):
    shard, width = residual.shape
    cols = weights[0].shape[0]
    count = len(weights)
    return pl.pallas_call(
        functools.partial(turn_kernel, count),
        out_shape=(
            jax.ShapeDtypeStruct((shard, width), f32),
            jax.ShapeDtypeStruct((2, width), f32),
            jax.ShapeDtypeStruct((count // 2, cols, width), bf16),
            jax.ShapeDtypeStruct((count // 2, cols, width), bf16),
        )
        + (jax.ShapeDtypeStruct((cols, shard), bf16),) * count,
        in_specs=[SMEM, SMEM] + [VMEM] * (5 + 2 * count),
        out_specs=(VMEM,) * (4 + count),
        name="turn",
        cost_estimate=COST,
    )(lens, rank, dispatch, back, residual, cotangent, gain, *heads, *weights)


def gelu_parts(values):
    below = 0.5 + 0.5 * lax.erf(values * (0.5**0.5))
    density = jnp.exp(-0.5 * values * values) * (0.5 / jnp.pi) ** 0.5
    return values * below, below + values * density


def expert_kernel(in_ref, grad_act_ref, up_ref, act_ref, mid_ref, sum_ref):
    step = pl.program_id(0)
    pre = jnp.dot(in_ref[...], up_ref[...], preferred_element_type=f32)
    act, slope = gelu_parts(pre)
    act_ref[...] = act.astype(bf16)
    grad_pre = (grad_act_ref[...] * slope).astype(bf16)
    mid = lax.dot_general(
        grad_pre, up_ref[...], (((1,), (1,)), ((), ())), preferred_element_type=f32
    )

    @pl.when(step == 0)
    def first():
        sum_ref[...] = mid

    @pl.when(step > 0)
    def later():
        sum_ref[...] += mid

    @pl.when(step == pl.num_programs(0) - 1)
    def last():
        mid_ref[...] = sum_ref[...].astype(bf16)


def expert(rows, grad_act, up):
    count, width = rows.shape
    hidden = up.shape[1]
    size = min(512, hidden)
    return pl.pallas_call(
        expert_kernel,
        grid=(hidden // size,),
        out_shape=(
            jax.ShapeDtypeStruct((count, hidden), bf16),
            jax.ShapeDtypeStruct((count, width), bf16),
        ),
        in_specs=[
            pl.BlockSpec((count, width), lambda i: (0, 0)),
            pl.BlockSpec((count, size), lambda i: (0, i)),
            pl.BlockSpec((width, size), lambda i: (0, i)),
        ],
        out_specs=(
            pl.BlockSpec((count, size), lambda i: (0, i)),
            pl.BlockSpec((count, width), lambda i: (0, 0)),
        ),
        scratch_shapes=[pltpu.VMEM((count, width), f32)],
        name="expert",
        cost_estimate=COST,
    )(rows, grad_act, up)


def product_kernel(a_ref, b_ref, out_ref, sum_ref):
    step = pl.program_id(0)
    made = jnp.dot(a_ref[...], b_ref[...], preferred_element_type=f32)

    @pl.when(step == 0)
    def first():
        sum_ref[...] = made

    @pl.when(step > 0)
    def later():
        sum_ref[...] += made

    @pl.when(step == pl.num_programs(0) - 1)
    def last():
        out_ref[...] = sum_ref[...].astype(bf16)


def product(a, b):
    count, depth = a.shape
    width = b.shape[1]
    size = min(1024, depth)
    return pl.pallas_call(
        product_kernel,
        grid=(depth // size,),
        out_shape=jax.ShapeDtypeStruct((count, width), bf16),
        in_specs=[
            pl.BlockSpec((count, size), lambda i: (0, i)),
            pl.BlockSpec((size, width), lambda i: (i, 0)),
        ],
        out_specs=pl.BlockSpec((count, width), lambda i: (0, 0)),
        scratch_shapes=[pltpu.VMEM((count, width), f32)],
        name="product",
        cost_estimate=COST,
    )(a, b)


def weight_kernel(groups, rank_ref, up_ref, down_ref, *refs):
    dup_ref, ddown_ref = refs[-2:]
    dup = ddown = 0.0
    for g in range(groups):
        in_ref, grad_ref = refs[2 * g : 2 * g + 2]
        pre = jnp.dot(in_ref[...], up_ref[...], preferred_element_type=f32)
        grad_act = lax.dot_general(
            grad_ref[...], down_ref[...], (((1,), (1,)), ((), ())),
            preferred_element_type=f32,
        )
        act, slope = gelu_parts(pre)
        dup = dup + contract_rows(in_ref[...], (grad_act * slope).astype(bf16))
        ddown = ddown + contract_rows(act.astype(bf16), grad_ref[...])
    if len(refs) > 2 * groups + 2:
        dup = dup + refs[2 * groups][...]
        ddown = ddown + refs[2 * groups + 1][...]
    dup_ref[...] = dup
    ddown_ref[...] = ddown


def expert_weights(rank, group, up, down, parts, earlier=()):
    count, width = group[0][0].shape
    hidden = up.shape[1] // parts
    size = min(256, hidden)
    blocks = hidden // size
    up_block = pl.BlockSpec((width, size), lambda i, r: (0, i))
    down_block = pl.BlockSpec((size, width), lambda i, r: (i, 0))
    rows = [values for both in group for values in both]
    return pl.pallas_call(
        functools.partial(weight_kernel, len(group)),
        grid_spec=pltpu.PrefetchScalarGridSpec(
            num_scalar_prefetch=1,
            grid=(blocks,),
            in_specs=[
                pl.BlockSpec((width, size), lambda i, r: (0, r[0] * blocks + i)),
                pl.BlockSpec((size, width), lambda i, r: (r[0] * blocks + i, 0)),
            ]
            + [pl.BlockSpec((count, width), lambda i, r: (0, 0))] * len(rows)
            + ([up_block, down_block] if earlier else []),
            out_specs=(up_block, down_block),
        ),
        out_shape=(
            jax.ShapeDtypeStruct((width, hidden), f32),
            jax.ShapeDtypeStruct((hidden, width), f32),
        ),
        name="expert_weights",
        cost_estimate=COST,
    )(rank, up, down, *rows, *earlier)


def input_grad_kernel(groups, qw_ref, kw_ref, vw_ref, *refs):
    joint_refs = refs[: len(groups)]
    kept_ref, sent_ref, turned_ref = refs[len(groups) :]
    step = pl.program_id(0)

    @pl.when(step == 0)
    def stack():
        start = 0
        for first_head, heads in groups:
            for at, weight_ref, first, size in stacked_parts(
                first_head, heads, qw_ref, kw_ref, vw_ref
            ):
                turned_ref[start + at : start + at + size, :] = weight_ref[
                    first : first + size, :
                ]
            start += 3 * heads * HEAD_DIM

    total = 0.0
    at = 0
    for joint_ref in joint_refs:
        rows = slice(at, at + joint_ref.shape[1])
        total = total + jnp.dot(
            joint_ref[...], turned_ref[rows, :], preferred_element_type=f32
        )
        at += joint_ref.shape[1]

    @pl.when(step % 2 == 0)
    def keep():
        kept_ref[0] = total.astype(bf16)

    @pl.when(step % 2 == 1)
    def send():
        sent_ref[0] = total.astype(bf16)


def input_grad(groups, weights, joints, first, count, size):
    cols, width = weights[0].shape
    fixed = pl.BlockSpec((cols, width), lambda i: (0, 0))
    return pl.pallas_call(
        functools.partial(input_grad_kernel, groups),
        grid=(count,),
        out_shape=(jax.ShapeDtypeStruct((count // 2, size, width), bf16),) * 2,
        in_specs=[fixed] * 3
        + [
            pl.BlockSpec((size, joint.shape[1]), lambda i: (first + i, 0))
            for joint in joints
        ],
        out_specs=(pl.BlockSpec((1, size, width), lambda i: (i // 2, 0, 0)),) * 2,
        scratch_shapes=[pltpu.VMEM((3 * cols, width), bf16)],
        name="input_grad",
        cost_estimate=COST,
    )(*weights, *joints)


def close_kernel(rank_ref, tokens_ref, gain_ref, grad_ref, *refs):
    *part_refs, out_ref = refs
    grad_in = 0.0
    for part_ref in part_refs:
        grad_in = grad_in + part_ref[...].reshape(out_ref.shape).astype(f32)
    values = tokens_ref[...].astype(f32)
    centred = values - jnp.mean(values, axis=-1, keepdims=True)
    inverse = lax.rsqrt(jnp.mean(centred * centred, axis=-1, keepdims=True) + EPSILON)
    normed = centred * inverse
    scaled = grad_in * gain_ref[...][None]
    out_ref[...] = grad_ref[...] + inverse * (
        scaled
        - jnp.mean(scaled, axis=-1, keepdims=True)
        - normed * jnp.mean(scaled * normed, axis=-1, keepdims=True)
    )


def close(rank, tokens, gain, grad, parts):
    shard, width = grad.shape
    size = shard // 2
    rows = lambda i, r: (i, 0)
    return pl.pallas_call(
        close_kernel,
        grid_spec=pltpu.PrefetchScalarGridSpec(
            num_scalar_prefetch=1,
            grid=(2,),
            in_specs=[
                pl.BlockSpec((size, width), lambda i, r: (2 * r[0] + i, 0)),
                pl.BlockSpec((width,), lambda i, r: (0,)),
                pl.BlockSpec((size, width), rows),
            ]
            + [pl.BlockSpec((1, size, width), lambda i, r: (0, i, 0))] * len(parts),
            out_specs=pl.BlockSpec((size, width), rows),
        ),
        out_shape=jax.ShapeDtypeStruct((shard, width), f32),
        name="close",
        cost_estimate=COST,
    )(rank, tokens, gain, grad, *parts)


def add_low(a, b):
    return (a.astype(f32) + b.astype(f32)).astype(bf16)


def tie(*values):
    return lax.optimization_barrier(values)


def finish_kernel(groups, bit_ref, *refs):
    pieces, refs = refs[: 2 * len(groups)], refs[2 * len(groups) :]
    query_ref, key_ref, value_ref = refs[:3]
    bit = bit_ref[0, 0]
    for g, ((first_head, heads), whole_ref) in enumerate(zip(groups, refs[3:])):
        half = whole_ref.shape[0] // 2
        for piece_ref, at in ((pieces[2 * g], bit), (pieces[2 * g + 1], 1 - bit)):
            whole_ref[rows_at(at, half), :] = piece_ref[0:half, :].astype(f32)
        for at, target_ref, first, size in stacked_parts(
            first_head, heads, query_ref, key_ref, value_ref
        ):
            target_ref[first : first + size, :] = whole_ref[at : at + size, :]


def finish(groups, bit, pieces):
    width = pieces[0].shape[1]
    cols = sum(heads for first_head, heads in groups) * HEAD_DIM
    return pl.pallas_call(
        functools.partial(finish_kernel, groups),
        out_shape=(jax.ShapeDtypeStruct((cols, width), f32),) * 3,
        in_specs=[SMEM] + [VMEM] * len(pieces),
        out_specs=(VMEM,) * 3,
        scratch_shapes=[
            pltpu.VMEM((3 * heads * HEAD_DIM, width), f32) for first_head, heads in groups
        ],
        name="finish",
        cost_estimate=COST,
    )(bit, *pieces)


def on_device(
    tokens,
    first_gain,
    first_bias,
    query_weight,
    key_weight,
    value_weight,
    output_weight,
    second_gain,
    second_bias,
    expert_up,
    expert_down,
    item_lengths,
    routes,
    slot_order,
    cotangent,
):
    slots_all, width = tokens.shape
    members = lax.axis_size("tensor")
    shard_rows = slots_all // members
    rank = lax.axis_index("tensor")
    sources = lax.axis_size("dp")
    experts_all = sources * expert_up.shape[0]
    capacity = shard_rows // experts_all
    head_cols = query_weight.shape[1]
    heads = head_cols // HEAD_DIM
    up_matrix = expert_up[0]
    down_matrix = expert_down[0]
    rank_cell = rank.astype(jnp.int32).reshape(1, 1)

    def exchange(rows):
        return lax.all_to_all(
            rows.reshape(sources, -1, width), "dp", split_axis=0, concat_axis=0, tiled=True
        ).reshape(-1, width)

    qw, kw, vw = query_weight.T, key_weight.T, value_weight.T

    dispatch, grad_slots = plan(
        item_lengths, rank_cell, routes, slot_order, cotangent, capacity, experts_all
    )
    flat_grad = exchange(grad_slots)
    tokens, grad_slots = tie(tokens, grad_slots)
    normed_in, qt, kt, vt = project(
        rank_cell[0], tokens, first_gain, first_bias, qw, kw, vw, members
    )
    outputs = [output_weight] + [
        swap(output_weight, "tensor", k) for k in range(1, members)
    ]
    *own_heads, logs = attend(item_lengths, rank_cell, qt, kt, vt, members)
    own_heads, flat_grad, outputs = tie(own_heads, flat_grad, outputs)
    all_heads = [own_heads[0]] + [
        swap(own_heads[j], "tensor", j) for j in range(1, members)
    ]
    grad_act = across(flat_grad, down_matrix)
    all_heads, grad_act = tie(all_heads, grad_act)
    residual, outgoing = middle(
        rank_cell[0], tokens, second_gain, second_bias, dispatch, all_heads, outputs
    )
    flat_in = exchange(outgoing)

    flat_grad, outgoing = tie(flat_grad, outgoing)
    gathered_grads = [flat_grad]
    gathered_rows = [flat_in]
    steps = steps_of(members)
    for step in reversed(steps[1:]):
        gathered_grads += [swap(a, "tensor", step) for a in gathered_grads]
    flat_in, gathered_grads = tie(flat_in, gathered_grads)
    gathered_rows = [flat_in]
    for step in reversed(steps[1:]):
        gathered_rows += [swap(a, "tensor", step) for a in gathered_rows]
    near_grads = swap(gathered_grads[0], "tensor", 1)
    near_rows = swap(flat_in, "tensor", 1)
    far_grads = [swap(a, "tensor", 1) for a in gathered_grads[1:]]
    act, grad_mid = expert(flat_in, grad_act, up_matrix)
    act, grad_mid, near_rows, near_grads, far_grads = tie(
        act, grad_mid, near_rows, near_grads, far_grads
    )
    grad_back = exchange(grad_mid)

    act, near_rows, grad_mid = tie(act, near_rows, grad_mid)
    made = product(act, down_matrix)
    sums = expert_weights(
        rank_cell[0],
        [(flat_in, gathered_grads[0]), (near_rows, near_grads)],
        up_matrix, down_matrix, members,
    )
    made, sums, gathered_rows = tie(made, sums, gathered_rows)
    far_rows = [swap(a, "tensor", 1) for a in gathered_rows[1:]]
    grad_back, made, sums = tie(grad_back, made, sums)

    grad_res, sums_second, kept, sent, *grad_heads = turn(
        item_lengths, rank_cell, dispatch, grad_back, residual, cotangent,
        second_gain, all_heads, outputs,
    )
    grad_parts = [grad_heads[0]] + [
        swap(grad_heads[j], "tensor", j) for j in range(1, members)
    ]
    made, grad_heads = tie(made, grad_heads)
    returned = exchange(made)
    output_sum = add_low(kept, swap(sent, "tensor", 1))
    grad_parts, output_sum = tie(grad_parts, output_sum)

    bit_cell = (lax.axis_index("dp") & 1).astype(jnp.int32).reshape(1, 1)
    weights = (qw, kw, vw)
    dp_steps = steps_of(sources)
    back = functools.partial(
        attend_back, lens=item_lengths, rank=rank_cell, bit=bit_cell, qt=qt, kt=kt, vt=vt,
        logs=logs, weights=weights, normed=normed_in, outs=own_heads,
    )
    groups = ((0, heads - 1), (heads - 1, 1))
    joint_a, sums_a, own_a, away_a = back(*groups[0], extras=(), grads=grad_parts)
    for step in steps[1:]:
        output_sum = add_low(
            output_sum[: len(output_sum) // 2],
            swap(output_sum[len(output_sum) // 2 :], "tensor", step),
        )
    joint_a, own_a, away_a, output_sum, grad_parts = tie(
        joint_a, own_a, away_a, output_sum, grad_parts
    )
    own_a = add_low(own_a, swap(away_a, "dp", 1))
    output_sum = add_low(output_sum[0], swap(output_sum[0], "dp", dp_steps[-1]))
    joint_b, unused, own_b, away_b = back(
        *groups[1], extras=(sums_a, sums_second), grads=grad_parts
    )
    joint_b, own_a, own_b, away_b, output_sum, returned = tie(
        joint_b, own_a, own_b, away_b, output_sum, returned
    )

    far = members // 2
    far_kept, far_sent = input_grad(
        groups, weights, (joint_a, joint_b), far, members - far, shard_rows
    )
    near_kept, near_sent = input_grad(
        groups, weights, (joint_a, joint_b), 0, far, shard_rows
    )
    own_b = add_low(own_b, swap(away_b, "dp", 1))
    far_kept = add_low(far_kept, swap(far_sent, "tensor", 1))
    far_kept, own_b, output_sum, near_sent = tie(far_kept, own_b, output_sum, near_sent)
    near_core = swap(near_sent, "tensor", 1)
    near_far = swap(far_kept, "tensor", 2)
    for step in dp_steps[1:]:
        own_a = add_low(own_a, swap(own_a, "dp", step))
        own_b = add_low(own_b, swap(own_b, "dp", step))
        if step == dp_steps[1]:
            own_b, sums, gathered_rows, far_rows = tie(own_b, sums, gathered_rows, far_rows)
    up_grad, down_grad = expert_weights(
        rank_cell[0],
        list(zip(gathered_rows[1:], gathered_grads[1:])) + list(zip(far_rows, far_grads)),
        up_matrix, down_matrix, members, sums,
    )
    own_b, up_grad, down_grad, near_far = tie(own_b, up_grad, down_grad, near_far)
    norm_sums = own_b[3 * HEAD_DIM * groups[1][1] // 2 :][:8].astype(f32)
    for step in steps:
        norm_sums = norm_sums + swap(norm_sums, "tensor", step)
    pieces = (own_a, swap(own_a, "dp", 1), own_b, swap(own_b, "dp", 1))
    token_grad = close(
        rank_cell[0], tokens, first_gain, grad_res, (near_kept, near_core, near_far)
    )
    for step in dp_steps[:-1]:
        output_sum = add_low(output_sum, swap(output_sum, "dp", step))

    block_out = residual + contract_rows(dispatch, returned)
    query_grad, key_grad, value_grad = finish(groups, bit_cell, pieces)
    return (
        block_out,
        token_grad,
        (norm_sums[0] - first_bias * norm_sums[1]) / first_gain,
        norm_sums[1],
        query_grad.T,
        key_grad.T,
        value_grad.T,
        output_sum.astype(f32),
        norm_sums[2],
        norm_sums[3],
        up_grad[None],
        down_grad[None],
    )


def solution(mesh):
    in_specs = (
        P("dp", None),
        P(),
        P(),
        P(None, "tensor"),
        P(None, "tensor"),
        P(None, "tensor"),
        P("tensor", None),
        P(),
        P(),
        P("dp", None, None),
        P("dp", None, None),
        P("dp", None),
        P(("dp", "tensor"), None),
        P(("dp", "tensor"), None),
        P(("dp", "tensor"), None),
    )
    out_specs = (
        P(("dp", "tensor"), None),
        P(("dp", "tensor"), None),
        P(),
        P(),
        P(None, "tensor"),
        P(None, "tensor"),
        P(None, "tensor"),
        P("tensor", None),
        P(),
        P(),
        P("dp", None, "tensor"),
        P("dp", "tensor", None),
    )
    return jax.shard_map(
        on_device, mesh=mesh, in_specs=in_specs, out_specs=out_specs, check_vma=False
    )
```

```python
import functools

import jax
import jax.numpy as jnp
from jax import lax
from jax.experimental import pallas as pl
from jax.experimental.pallas import tpu as pltpu
from jax.sharding import PartitionSpec as P

HEAD_DIM = 64
EPSILON = 1e-05
NEGATIVE = -1e30
f32 = jnp.float32
bf16 = jnp.bfloat16
VMEM = pl.BlockSpec(memory_space=pltpu.VMEM)
SMEM = pl.BlockSpec(memory_space=pltpu.SMEM)
SUM_ROWS = 16
COST = pl.CostEstimate(flops=2**20, bytes_accessed=2**20, transcendentals=0)


def layer_norm(values, gain, shift):
    average = jnp.mean(values, axis=-1, keepdims=True)
    centred = values - average
    variance = jnp.mean(centred * centred, axis=-1, keepdims=True)
    return centred * lax.rsqrt(variance + EPSILON) * gain + shift


def contract_rows(left, right):
    return lax.dot_general(
        left, right, (((0,), (0,)), ((), ())), preferred_element_type=f32
    )


def swap(values, axis, step):
    count = lax.axis_size(axis)
    return lax.ppermute(values, axis, [(i, i ^ step) for i in range(count)])


def steps_of(count):
    steps = []
    step = 1
    while step < count:
        steps.append(step)
        step *= 2
    return steps


def normalized(values):
    average = jnp.mean(values, axis=-1, keepdims=True)
    centred = values - average
    variance = jnp.mean(centred * centred, axis=-1, keepdims=True)
    return centred * lax.rsqrt(variance + EPSILON)


def project_kernel(
    rank_ref, tokens_ref, gain_ref, bias_ref, qw_ref, kw_ref, vw_ref,
    normed_ref, qt_ref, kt_ref, vt_ref,
):
    values = tokens_ref[...].astype(f32)
    normed = (normalized(values) * gain_ref[...][None] + bias_ref[...][None]).astype(bf16)
    normed_ref[...] = normed
    for weight_ref, out_ref, factor in (
        (qw_ref, qt_ref, HEAD_DIM ** (-0.5)), (kw_ref, kt_ref, None), (vw_ref, vt_ref, None)
    ):
        made = lax.dot_general(
            weight_ref[...], normed, (((1,), (1,)), ((), ())), preferred_element_type=f32
        ).astype(bf16)
        if factor is not None:
            made = made * jnp.asarray(factor, bf16)
        out_ref[...] = made


def project(rank, tokens, gain, bias, qw, kw, vw, blocks):
    slots, width = tokens.shape
    cols = qw.shape[0]
    size = slots // blocks
    fixed = lambda i, r: (0, 0)
    line = pl.BlockSpec((width,), lambda i, r: (0,))
    return pl.pallas_call(
        project_kernel,
        grid_spec=pltpu.PrefetchScalarGridSpec(
            num_scalar_prefetch=1,
            grid=(blocks,),
            in_specs=[
                pl.BlockSpec((size, width), lambda i, r: (i ^ r[0], 0)),
                line,
                line,
                pl.BlockSpec((cols, width), fixed),
                pl.BlockSpec((cols, width), fixed),
                pl.BlockSpec((cols, width), fixed),
            ],
            out_specs=(
                pl.BlockSpec((size, width), lambda i, r: (i, 0)),
                pl.BlockSpec((cols, size), lambda i, r: (0, i)),
                pl.BlockSpec((cols, size), lambda i, r: (0, i)),
                pl.BlockSpec((cols, size), lambda i, r: (0, i)),
            ),
        ),
        out_shape=(jax.ShapeDtypeStruct((slots, width), bf16),)
        + (jax.ShapeDtypeStruct((cols, slots), bf16),) * 3,
        name="project",
        cost_estimate=COST,
    )(rank, tokens, gain, bias, qw, kw, vw)


def item_ends(lens_ref):
    ends = []
    total = jnp.int32(0)
    for i in range(lens_ref.shape[1]):
        total = total + lens_ref[0, i]
        ends.append(total)
    return ends


def segments_at(place, ends):
    segment = jnp.zeros_like(place)
    for end in ends:
        segment = segment + (place >= end).astype(jnp.int32)
    return segment


def block_span(first, size, unit, ends):
    last = jnp.minimum(first + size, ends[-1]) - 1
    low = jnp.int32(0)
    high = ends[-1]
    for end in ends:
        low = jnp.where(first >= end, end, low)
    for end in reversed(ends):
        high = jnp.where(last < end, end, high)
    empty = first >= ends[-1]
    low_block = jnp.where(empty, 0, low // unit)
    high_block = jnp.where(empty, 0, (high + unit - 1) // unit)
    return low_block, high_block


def rows_at(block, size):
    return pl.ds(pl.multiple_of(block * size, size), size)


def fill_segments(row_ref, col_ref, shard, rank, ends):
    slots = row_ref.shape[1]
    at = lax.broadcasted_iota(jnp.int32, (1, slots), 1)
    place = ((at // shard) ^ rank) * shard + at % shard
    segments = segments_at(place, ends)
    row_ref[...] = segments
    col_ref[...] = jnp.transpose(jnp.broadcast_to(segments, (128, slots)), (1, 0))


def block_bias(row_ref, col_ref, rows, cols):
    return jnp.where(col_ref[rows, 0:1] == row_ref[:, cols], 0.0, NEGATIVE)


def lane_masked(values, head):
    lane = lax.broadcasted_iota(jnp.int32, values.shape, 1)
    inside = (lane >= head * HEAD_DIM) & (lane < (head + 1) * HEAD_DIM)
    return jnp.where(inside, values, jnp.zeros_like(values))


def forward_kernel(
    first, blocks, lens_ref, rank_ref, qt_ref, kt_ref, vt_ref, *refs
):
    *out_refs, log_ref, masked_ref, out_ref, row_ref, col_ref, score_ref = refs
    count, width, size = out_ref.shape
    heads = width // HEAD_DIM
    shard = size
    rank = rank_ref[0, 0]
    ends = item_ends(lens_ref)
    fill_segments(row_ref, col_ref, shard, rank, ends)
    keys = jnp.transpose(kt_ref[...], (1, 0))
    for h in range(heads):
        masked_ref[h] = lane_masked(keys, h)

    def query_block(b, unused):
        at = first + b
        i = at ^ rank
        cols = rows_at(at, size)
        queries = qt_ref[:, cols]

        def score_block(j, carry):
            rows = rows_at(j ^ rank, shard)
            bias = block_bias(row_ref, col_ref, rows, cols)
            result = []
            for h in range(heads):
                scores = jnp.dot(
                    masked_ref[h, rows, :], queries, preferred_element_type=f32
                )
                scores = scores + bias
                score_ref[h, rows_at(j, shard), :] = scores
                part = jnp.max(scores.reshape(-1, 8, size), axis=0)
                result.append(jnp.maximum(carry[h], part))
            return tuple(result)

        low, high = block_span(i * size, size, shard, ends)
        peaks = lax.fori_loop(
            low, high, score_block, (jnp.full((8, size), NEGATIVE, f32),) * heads
        )
        peaks = [jnp.max(peak, axis=0, keepdims=True) for peak in peaks]

        def key_block(j, carry):
            rows = rows_at(j ^ rank, shard)
            result = []
            for h in range(heads):
                summed, total = carry[h]
                soft = jnp.exp(score_ref[h, rows_at(j, shard), :] - peaks[h])
                summed = summed + jnp.sum(soft.reshape(-1, 8, size), axis=0)
                total = total + jnp.dot(
                    vt_ref[pl.ds(h * HEAD_DIM, HEAD_DIM), rows],
                    soft.astype(bf16),
                    preferred_element_type=f32,
                )
                result.append((summed, total))
            return tuple(result)

        start = ((jnp.zeros((8, size), f32), jnp.zeros((HEAD_DIM, size), f32)),) * heads
        done = lax.fori_loop(low, high, key_block, start)
        live = row_ref[:, cols] < len(ends)
        for h in range(heads):
            summed, total = done[h]
            summed = jnp.sum(summed, axis=0, keepdims=True)
            highest = peaks[h]
            summed = jnp.where(live, summed, 1.0)
            result = jnp.where(live, total / summed, 0.0).astype(bf16)
            logs = jnp.where(live, highest + jnp.log(summed), -NEGATIVE)
            out_ref[b, pl.ds(h * HEAD_DIM, HEAD_DIM), :] = result
            log_ref[h, :, rows_at(b, size)] = logs
        return unused

    lax.fori_loop(0, count, query_block, 0)
    for b in range(count):
        out_refs[b][...] = out_ref[b]


def attend(lens, rank, qt, kt, vt, blocks, first, count):
    width, slots = qt.shape
    size = slots // blocks
    heads = width // HEAD_DIM
    return pl.pallas_call(
        functools.partial(forward_kernel, first, blocks),
        out_shape=(jax.ShapeDtypeStruct((width, size), bf16),) * count
        + (jax.ShapeDtypeStruct((heads, 1, count * size), f32),),
        in_specs=[SMEM, SMEM, VMEM, VMEM, VMEM],
        out_specs=(VMEM,) * (count + 1),
        scratch_shapes=[
            pltpu.VMEM((heads, slots, width), bf16),
            pltpu.VMEM((count, width, size), bf16),
            pltpu.VMEM((1, slots), jnp.int32),
            pltpu.VMEM((slots, 128), jnp.int32),
            pltpu.VMEM((heads, slots, size), f32),
        ],
        name="attend",
        compiler_params=pltpu.CompilerParams(vmem_limit_bytes=60 * 2**20),
        cost_estimate=COST,
    )(lens, rank, qt, kt, vt)


def split_rows(values):
    high = values.astype(bf16)
    return jnp.concatenate([high, (values - high.astype(f32)).astype(bf16)], axis=0)


def add_kernel(a_ref, b_ref, out_ref):
    half = out_ref.shape[0] - SUM_ROWS
    line = SUM_ROWS // 2
    total = a_ref[...].astype(f32) + b_ref[...].astype(f32)
    out_ref[:half, :] = total[:half].astype(bf16)
    out_ref[half:, :] = split_rows(total[half : half + line] + total[half + line :])


def add_parts(a, b):
    return pl.pallas_call(
        add_kernel,
        out_shape=jax.ShapeDtypeStruct(a.shape, bf16),
        in_specs=[VMEM, VMEM],
        out_specs=VMEM,
        name="add_parts",
        cost_estimate=COST,
    )(a, b)


def stacked_parts(first_head, heads, query, key, value):
    dim = HEAD_DIM
    parts = []
    for n in range(heads):
        first = (first_head + n) * dim
        parts += [(2 * n * dim, key, first, dim), ((2 * n + 1) * dim, value, first, dim)]
    return parts + [(2 * heads * dim, query, first_head * dim, heads * dim)]


def backward_kernel(
    first_head, heads, blocks, extras, lens_ref, rank_ref, bit_ref, qt_ref, kt_ref, vt_ref,
    near_ref, far_ref, qw_ref, kw_ref, vw_ref, normed_ref, *rest
):
    extra_refs, rest = rest[:extras], rest[extras:]
    width, slots = qt_ref.shape
    shard = slots // blocks
    dim = HEAD_DIM
    out_refs, grad_refs = rest[:blocks], rest[blocks : 2 * blocks]
    joint_ref, sums_ref, own_ref, away_ref = rest[2 * blocks : 2 * blocks + 4]
    kv_ref, q0_ref, og_ref, right_ref, inner_ref, dq_ref, made_ref = rest[-13:-6]
    log_ref = rest[-6]
    row_ref, col_ref = rest[-5:-3]
    turned_ref, rows_ref, copied = rest[-3:]
    fetch = pltpu.make_async_copy(normed_ref, rows_ref, copied)
    fetch.start()
    unit = shard // 2
    rank = rank_ref[0, 0]
    ends = item_ends(lens_ref)
    fill_segments(row_ref, col_ref, shard, rank, ends)
    near = near_ref.shape[2]
    log_ref[:, :, :near] = near_ref[...]
    log_ref[:, :, near:] = far_ref[...]
    zero = jnp.zeros((dim, slots), bf16)
    for n in range(heads):
        part = slice((first_head + n) * dim, (first_head + n + 1) * dim)
        both = jnp.concatenate([kt_ref[part, :], vt_ref[part, :]], axis=0)
        kv_ref[n] = jnp.transpose(both, (1, 0))
        padded = jnp.concatenate([qt_ref[part, :], zero], axis=0)
        q0_ref[n] = jnp.transpose(padded, (1, 0))
        right_ref[n, 0] = padded
        for b in range(blocks):
            grad = grad_refs[b][part, :]
            cols = slice(b * shard, (b + 1) * shard)
            padded = jnp.concatenate([zero[:, :shard], grad], axis=0)
            og_ref[n, cols, :] = jnp.transpose(padded, (1, 0))
            right_ref[n, 1, :, cols] = padded
            inner_ref[n, :, cols] = jnp.sum(
                out_refs[b][part, :].astype(f32) * grad.astype(f32), axis=0, keepdims=True
            )
    dq_ref[...] = jnp.zeros_like(dq_ref)

    def key_block(j, unused):
        at_key = ((j // 2) ^ rank) * 2 + j % 2
        rows = rows_at(at_key, unit)

        def query_block(i, totals):
            at = i ^ rank
            cols = rows_at(at, shard)
            same = col_ref[rows, 0:1] == row_ref[:, cols]
            result = []
            for n in range(heads):
                head = first_head + n
                kv = kv_ref[n, rows, :]
                scores = jnp.dot(kv, right_ref[n, 0, :, cols], preferred_element_type=f32)
                grad_soft = jnp.dot(kv, right_ref[n, 1, :, cols], preferred_element_type=f32)
                soft = jnp.where(same, jnp.exp(scores - log_ref[head, :, cols]), 0.0)
                grad_scores = (soft * (grad_soft - inner_ref[n, :, cols])).astype(bf16)
                total = totals[n] + jnp.dot(
                    soft.astype(bf16), og_ref[n, cols, :], preferred_element_type=f32
                )
                total = total + jnp.dot(
                    grad_scores, q0_ref[n, cols, :], preferred_element_type=f32
                )
                dq_ref[n, :, cols] += jnp.dot(
                    kt_ref[pl.ds(head * dim, dim), rows], grad_scores,
                    preferred_element_type=f32,
                )
                result.append(total)
            return tuple(result)

        low, high = block_span(j * unit, unit, shard, ends)
        start = (jnp.zeros((unit, 2 * dim), f32),) * heads
        totals = lax.fori_loop(low, high, query_block, start)
        for n in range(heads):
            part = slice(2 * dim * n, 2 * dim * (n + 1))
            total = totals[n].astype(bf16)
            joint_ref[rows, part] = total
            turned_ref[part, rows] = jnp.transpose(total, (1, 0))
        return unused

    lax.fori_loop(0, 2 * blocks, key_block, 0)
    dq = (dq_ref[...] * dim ** (-0.5)).astype(bf16).reshape(heads * dim, slots)
    turned_ref[2 * dim * heads :, :] = dq
    joint_ref[:, 2 * dim * heads :] = jnp.transpose(dq, (1, 0))
    fetch.wait()
    made_ref[...] = jnp.dot(turned_ref[...], rows_ref[...], preferred_element_type=f32)
    gains = jnp.zeros((1, rows_ref.shape[1]), f32)
    shifts = jnp.zeros((1, rows_ref.shape[1]), f32)
    for at, weight_ref, first, size in stacked_parts(
        first_head, heads, qw_ref, kw_ref, vw_ref
    ):
        weight = weight_ref[first : first + size, :].astype(f32)
        gains += jnp.sum(weight * made_ref[at : at + size, :], axis=0, keepdims=True)
        total = jnp.sum(turned_ref[at : at + size, :].astype(f32), axis=1, keepdims=True)
        shifts += jnp.sum(weight * total, axis=0, keepdims=True)
    sums_ref[0:1] = gains
    sums_ref[1:2] = shifts
    half = made_ref.shape[0] // 2
    bit = bit_ref[0, 0]
    for part_ref, at in ((own_ref, bit), (away_ref, 1 - bit)):
        part_ref[0:half, :] = made_ref[rows_at(at, half), :].astype(bf16)
        if extras:
            lines = [sums_ref[...] + extra_refs[0][...], extra_refs[1][...]]
            lines.append(jnp.zeros((SUM_ROWS // 2 - 4, gains.shape[1]), f32))
            part_ref[half:, :] = split_rows(jnp.concatenate(lines, axis=0))


def attend_back(
    first_head, heads, extras, lens, rank, bit, qt, kt, vt, logs, weights, normed, outs, grads
):
    slots, width = normed.shape
    blocks = len(outs)
    dim = HEAD_DIM
    cols = 3 * dim * heads
    rows = cols // 2 + (SUM_ROWS if extras else 0)
    return pl.pallas_call(
        functools.partial(backward_kernel, first_head, heads, blocks, len(extras)),
        out_shape=(
            jax.ShapeDtypeStruct((slots, cols), bf16),
            jax.ShapeDtypeStruct((2, width), f32),
        )
        + (jax.ShapeDtypeStruct((rows, width), bf16),) * 2,
        in_specs=[SMEM, SMEM, SMEM]
        + [VMEM] * 8
        + [pl.BlockSpec(memory_space=pl.ANY)]
        + [VMEM] * (len(extras) + 2 * blocks),
        out_specs=(VMEM,) * 4,
        scratch_shapes=[pltpu.VMEM((heads, slots, 2 * dim), bf16)] * 3
        + [
            pltpu.VMEM((heads, 2, 2 * dim, slots), bf16),
            pltpu.VMEM((heads, 1, slots), f32),
            pltpu.VMEM((heads, dim, slots), f32),
            pltpu.VMEM((cols, width), f32),
            pltpu.VMEM((qt.shape[0] // dim, 1, slots), f32),
            pltpu.VMEM((1, slots), jnp.int32),
            pltpu.VMEM((slots, 128), jnp.int32),
            pltpu.VMEM((cols, slots), bf16),
            pltpu.VMEM((slots, width), bf16),
            pltpu.SemaphoreType.DMA,
        ],
        name="attend_back",
        compiler_params=pltpu.CompilerParams(vmem_limit_bytes=60 * 2**20),
        cost_estimate=COST,
    )(lens, rank, bit, qt, kt, vt, *logs, *weights, normed, *extras, *outs, *grads)


def plan_kernel(capacity, lens_ref, rank_ref, routes_ref, order_ref, grad_ref,
                dispatch_ref, slots_ref):
    shard = routes_ref.shape[1]
    first = rank_ref[0, 0] * shard
    ends = item_ends(lens_ref)
    chosen_row = routes_ref[...]
    chosen_col = jnp.transpose(jnp.broadcast_to(chosen_row, (128, shard)), (1, 0))[:, 0:1]
    order_row = order_ref[...]
    order_col = jnp.transpose(jnp.broadcast_to(order_row, (128, shard)), (1, 0))[:, 0:1]
    alive_row = segments_at(
        first + lax.broadcasted_iota(jnp.int32, (1, shard), 1), ends
    ) < len(ends)
    alive_col = segments_at(
        first + lax.broadcasted_iota(jnp.int32, (shard, 1), 0), ends
    ) < len(ends)
    ahead = (chosen_col == chosen_row) & (order_col < order_row) & alive_col
    ranked = jnp.sum(ahead.astype(jnp.int32), axis=0, keepdims=True)
    kept = alive_row & (ranked < capacity)
    slot = jnp.where(kept, chosen_row * capacity + ranked, -1)
    dispatch = (
        lax.broadcasted_iota(jnp.int32, dispatch_ref.shape, 0) == slot
    ).astype(f32).astype(bf16)
    dispatch_ref[...] = dispatch
    slots_ref[...] = jnp.dot(
        dispatch, grad_ref[...], preferred_element_type=f32
    ).astype(bf16)


def plan(lens, rank, routes, order, grads, capacity, experts_all):
    shard, width = grads.shape
    count = experts_all * capacity
    return pl.pallas_call(
        functools.partial(plan_kernel, capacity),
        out_shape=(
            jax.ShapeDtypeStruct((count, shard), bf16),
            jax.ShapeDtypeStruct((count, width), bf16),
        ),
        in_specs=[SMEM, SMEM, VMEM, VMEM, VMEM],
        out_specs=(VMEM, VMEM),
        name="plan",
        cost_estimate=COST,
    )(lens, rank, routes.reshape(1, -1), order, grads)


def across(left, right):
    return lax.dot_general(
        left, right, (((1,), (1,)), ((), ())), preferred_element_type=f32
    )


def middle_kernel(count, rank_ref, tokens_ref, gain_ref, bias_ref, dispatch_ref, *refs):
    head_refs, weight_refs = refs[:count], refs[count : 2 * count]
    residual_ref, rows_ref = refs[2 * count :]
    residual = tokens_ref[...].astype(f32)
    for head_ref, weight_ref in zip(head_refs, weight_refs):
        residual = residual + contract_rows(head_ref[...], weight_ref[...])
    residual_ref[...] = residual
    normed = (normalized(residual) * gain_ref[...][None] + bias_ref[...][None]).astype(bf16)
    rows_ref[...] = jnp.dot(
        dispatch_ref[...], normed, preferred_element_type=f32
    ).astype(bf16)


def middle(rank, tokens, gain, bias, dispatch, heads, weights):
    count, shard = dispatch.shape
    width = tokens.shape[1]
    fixed = lambda array: pl.BlockSpec(array.shape, lambda i, r: (0,) * array.ndim)
    small = [gain, bias, dispatch, *heads, *weights]
    return pl.pallas_call(
        functools.partial(middle_kernel, len(heads)),
        grid_spec=pltpu.PrefetchScalarGridSpec(
            num_scalar_prefetch=1,
            grid=(1,),
            in_specs=[pl.BlockSpec((shard, width), lambda i, r: (r[0], 0))]
            + [fixed(array) for array in small],
            out_specs=(
                pl.BlockSpec((shard, width), lambda i, r: (0, 0)),
                pl.BlockSpec((count, width), lambda i, r: (0, 0)),
            ),
        ),
        out_shape=(
            jax.ShapeDtypeStruct((shard, width), f32),
            jax.ShapeDtypeStruct((count, width), bf16),
        ),
        name="middle",
        cost_estimate=COST,
    )(rank, tokens, *small)


def turn_kernel(
    count, lens_ref, rank_ref, dispatch_ref, back_ref, residual_ref, cotangent_ref,
    gain_ref, *refs
):
    head_refs, weight_refs = refs[:count], refs[count : 2 * count]
    grad_ref, sums_ref, kept_ref, sent_ref = refs[2 * count : 2 * count + 4]
    part_refs = refs[2 * count + 4 :]
    shard = residual_ref.shape[0]
    grad_normed = contract_rows(dispatch_ref[...], back_ref[...])
    values = residual_ref[...]
    centred = values - jnp.mean(values, axis=-1, keepdims=True)
    inverse = lax.rsqrt(jnp.mean(centred * centred, axis=-1, keepdims=True) + EPSILON)
    normed = centred * inverse
    sums_ref[0:1] = jnp.sum(grad_normed * normed, axis=0, keepdims=True)
    sums_ref[1:2] = jnp.sum(grad_normed, axis=0, keepdims=True)
    scaled = grad_normed * gain_ref[...][None]
    grad = cotangent_ref[...].astype(f32) + inverse * (
        scaled
        - jnp.mean(scaled, axis=-1, keepdims=True)
        - normed * jnp.mean(scaled * normed, axis=-1, keepdims=True)
    )
    grad_ref[...] = grad
    low = grad.astype(bf16)
    place = rank_ref[0, 0] * shard + lax.broadcasted_iota(jnp.int32, (1, shard), 1)
    alive = place < item_ends(lens_ref)[-1]
    for weight_ref, part_ref in zip(weight_refs, part_refs):
        part_ref[...] = jnp.where(alive, across(weight_ref[...], low), 0.0).astype(bf16)
    for j, head_ref in enumerate(head_refs):
        made = jnp.dot(head_ref[...], low, preferred_element_type=f32)
        (kept_ref, sent_ref)[j % 2][j // 2] = made.astype(bf16)


def turn(lens, rank, dispatch, back, residual, cotangent, gain, heads, weights):
    shard, width = residual.shape
    cols = weights[0].shape[0]
    count = len(weights)
    return pl.pallas_call(
        functools.partial(turn_kernel, count),
        out_shape=(
            jax.ShapeDtypeStruct((shard, width), f32),
            jax.ShapeDtypeStruct((2, width), f32),
            jax.ShapeDtypeStruct((count // 2, cols, width), bf16),
            jax.ShapeDtypeStruct((count // 2, cols, width), bf16),
        )
        + (jax.ShapeDtypeStruct((cols, shard), bf16),) * count,
        in_specs=[SMEM, SMEM] + [VMEM] * (5 + 2 * count),
        out_specs=(VMEM,) * (4 + count),
        name="turn",
        cost_estimate=COST,
    )(lens, rank, dispatch, back, residual, cotangent, gain, *heads, *weights)


def gelu_parts(values):
    below = 0.5 + 0.5 * lax.erf(values * (0.5**0.5))
    density = jnp.exp(-0.5 * values * values) * (0.5 / jnp.pi) ** 0.5
    return values * below, below + values * density


def expert_kernel(in_ref, grad_act_ref, up_ref, act_ref, mid_ref, sum_ref):
    step = pl.program_id(0)
    pre = jnp.dot(in_ref[...], up_ref[...], preferred_element_type=f32)
    act, slope = gelu_parts(pre)
    act_ref[...] = act.astype(bf16)
    grad_pre = (grad_act_ref[...] * slope).astype(bf16)
    mid = lax.dot_general(
        grad_pre, up_ref[...], (((1,), (1,)), ((), ())), preferred_element_type=f32
    )

    @pl.when(step == 0)
    def first():
        sum_ref[...] = mid

    @pl.when(step > 0)
    def later():
        sum_ref[...] += mid

    @pl.when(step == pl.num_programs(0) - 1)
    def last():
        mid_ref[...] = sum_ref[...].astype(bf16)


def expert(rows, grad_act, up):
    count, width = rows.shape
    hidden = up.shape[1]
    size = min(512, hidden)
    return pl.pallas_call(
        expert_kernel,
        grid=(hidden // size,),
        out_shape=(
            jax.ShapeDtypeStruct((count, hidden), bf16),
            jax.ShapeDtypeStruct((count, width), bf16),
        ),
        in_specs=[
            pl.BlockSpec((count, width), lambda i: (0, 0)),
            pl.BlockSpec((count, size), lambda i: (0, i)),
            pl.BlockSpec((width, size), lambda i: (0, i)),
        ],
        out_specs=(
            pl.BlockSpec((count, size), lambda i: (0, i)),
            pl.BlockSpec((count, width), lambda i: (0, 0)),
        ),
        scratch_shapes=[pltpu.VMEM((count, width), f32)],
        name="expert",
        cost_estimate=COST,
    )(rows, grad_act, up)


def product_kernel(a_ref, b_ref, out_ref, sum_ref):
    step = pl.program_id(0)
    made = jnp.dot(a_ref[...], b_ref[...], preferred_element_type=f32)

    @pl.when(step == 0)
    def first():
        sum_ref[...] = made

    @pl.when(step > 0)
    def later():
        sum_ref[...] += made

    @pl.when(step == pl.num_programs(0) - 1)
    def last():
        out_ref[...] = sum_ref[...].astype(bf16)


def product(a, b):
    count, depth = a.shape
    width = b.shape[1]
    size = min(1024, depth)
    return pl.pallas_call(
        product_kernel,
        grid=(depth // size,),
        out_shape=jax.ShapeDtypeStruct((count, width), bf16),
        in_specs=[
            pl.BlockSpec((count, size), lambda i: (0, i)),
            pl.BlockSpec((size, width), lambda i: (i, 0)),
        ],
        out_specs=pl.BlockSpec((count, width), lambda i: (0, 0)),
        scratch_shapes=[pltpu.VMEM((count, width), f32)],
        name="product",
        cost_estimate=COST,
    )(a, b)


def weight_kernel(groups, rank_ref, up_ref, down_ref, *refs):
    dup_ref, ddown_ref = refs[-2:]
    dup = ddown = 0.0
    for g in range(groups):
        in_ref, grad_ref = refs[2 * g : 2 * g + 2]
        pre = jnp.dot(in_ref[...], up_ref[...], preferred_element_type=f32)
        grad_act = lax.dot_general(
            grad_ref[...], down_ref[...], (((1,), (1,)), ((), ())),
            preferred_element_type=f32,
        )
        act, slope = gelu_parts(pre)
        dup = dup + contract_rows(in_ref[...], (grad_act * slope).astype(bf16))
        ddown = ddown + contract_rows(act.astype(bf16), grad_ref[...])
    if len(refs) > 2 * groups + 2:
        dup = dup + refs[2 * groups][...]
        ddown = ddown + refs[2 * groups + 1][...]
    dup_ref[...] = dup
    ddown_ref[...] = ddown


def expert_weights(rank, group, up, down, parts, earlier=()):
    count, width = group[0][0].shape
    hidden = up.shape[1] // parts
    size = min(256, hidden)
    blocks = hidden // size
    up_block = pl.BlockSpec((width, size), lambda i, r: (0, i))
    down_block = pl.BlockSpec((size, width), lambda i, r: (i, 0))
    rows = [values for both in group for values in both]
    return pl.pallas_call(
        functools.partial(weight_kernel, len(group)),
        grid_spec=pltpu.PrefetchScalarGridSpec(
            num_scalar_prefetch=1,
            grid=(blocks,),
            in_specs=[
                pl.BlockSpec((width, size), lambda i, r: (0, r[0] * blocks + i)),
                pl.BlockSpec((size, width), lambda i, r: (r[0] * blocks + i, 0)),
            ]
            + [pl.BlockSpec((count, width), lambda i, r: (0, 0))] * len(rows)
            + ([up_block, down_block] if earlier else []),
            out_specs=(up_block, down_block),
        ),
        out_shape=(
            jax.ShapeDtypeStruct((width, hidden), f32),
            jax.ShapeDtypeStruct((hidden, width), f32),
        ),
        name="expert_weights",
        cost_estimate=COST,
    )(rank, up, down, *rows, *earlier)


def input_grad_kernel(groups, qw_ref, kw_ref, vw_ref, *refs):
    joint_refs = refs[: len(groups)]
    kept_ref, sent_ref, turned_ref = refs[len(groups) :]
    step = pl.program_id(0)

    @pl.when(step == 0)
    def stack():
        start = 0
        for first_head, heads in groups:
            for at, weight_ref, first, size in stacked_parts(
                first_head, heads, qw_ref, kw_ref, vw_ref
            ):
                turned_ref[start + at : start + at + size, :] = weight_ref[
                    first : first + size, :
                ]
            start += 3 * heads * HEAD_DIM

    total = 0.0
    at = 0
    for joint_ref in joint_refs:
        rows = slice(at, at + joint_ref.shape[1])
        total = total + jnp.dot(
            joint_ref[...], turned_ref[rows, :], preferred_element_type=f32
        )
        at += joint_ref.shape[1]

    @pl.when(step % 2 == 0)
    def keep():
        kept_ref[0] = total.astype(bf16)

    @pl.when(step % 2 == 1)
    def send():
        sent_ref[0] = total.astype(bf16)


def input_grad(groups, weights, joints, first, count, size):
    cols, width = weights[0].shape
    fixed = pl.BlockSpec((cols, width), lambda i: (0, 0))
    return pl.pallas_call(
        functools.partial(input_grad_kernel, groups),
        grid=(count,),
        out_shape=(jax.ShapeDtypeStruct((count // 2, size, width), bf16),) * 2,
        in_specs=[fixed] * 3
        + [
            pl.BlockSpec((size, joint.shape[1]), lambda i: (first + i, 0))
            for joint in joints
        ],
        out_specs=(pl.BlockSpec((1, size, width), lambda i: (i // 2, 0, 0)),) * 2,
        scratch_shapes=[pltpu.VMEM((3 * cols, width), bf16)],
        name="input_grad",
        cost_estimate=COST,
    )(*weights, *joints)


def close_kernel(rank_ref, tokens_ref, gain_ref, grad_ref, *refs):
    *part_refs, out_ref = refs
    grad_in = 0.0
    for part_ref in part_refs:
        grad_in = grad_in + part_ref[...].reshape(out_ref.shape).astype(f32)
    values = tokens_ref[...].astype(f32)
    centred = values - jnp.mean(values, axis=-1, keepdims=True)
    inverse = lax.rsqrt(jnp.mean(centred * centred, axis=-1, keepdims=True) + EPSILON)
    normed = centred * inverse
    scaled = grad_in * gain_ref[...][None]
    out_ref[...] = grad_ref[...] + inverse * (
        scaled
        - jnp.mean(scaled, axis=-1, keepdims=True)
        - normed * jnp.mean(scaled * normed, axis=-1, keepdims=True)
    )


def close(rank, tokens, gain, grad, parts):
    shard, width = grad.shape
    size = shard // 2
    rows = lambda i, r: (i, 0)
    return pl.pallas_call(
        close_kernel,
        grid_spec=pltpu.PrefetchScalarGridSpec(
            num_scalar_prefetch=1,
            grid=(2,),
            in_specs=[
                pl.BlockSpec((size, width), lambda i, r: (2 * r[0] + i, 0)),
                pl.BlockSpec((width,), lambda i, r: (0,)),
                pl.BlockSpec((size, width), rows),
            ]
            + [pl.BlockSpec((1, size, width), lambda i, r: (0, i, 0))] * len(parts),
            out_specs=pl.BlockSpec((size, width), rows),
        ),
        out_shape=jax.ShapeDtypeStruct((shard, width), f32),
        name="close",
        cost_estimate=COST,
    )(rank, tokens, gain, grad, *parts)


def add_low(a, b):
    return (a.astype(f32) + b.astype(f32)).astype(bf16)


def tie(*values):
    return lax.optimization_barrier(values)


def finish_kernel(groups, bit_ref, *refs):
    pieces, refs = refs[: 2 * len(groups)], refs[2 * len(groups) :]
    query_ref, key_ref, value_ref = refs[:3]
    bit = bit_ref[0, 0]
    for g, ((first_head, heads), whole_ref) in enumerate(zip(groups, refs[3:])):
        half = whole_ref.shape[0] // 2
        for piece_ref, at in ((pieces[2 * g], bit), (pieces[2 * g + 1], 1 - bit)):
            whole_ref[rows_at(at, half), :] = piece_ref[0:half, :].astype(f32)
        for at, target_ref, first, size in stacked_parts(
            first_head, heads, query_ref, key_ref, value_ref
        ):
            target_ref[first : first + size, :] = whole_ref[at : at + size, :]


def finish(groups, bit, pieces):
    width = pieces[0].shape[1]
    cols = sum(heads for first_head, heads in groups) * HEAD_DIM
    return pl.pallas_call(
        functools.partial(finish_kernel, groups),
        out_shape=(jax.ShapeDtypeStruct((cols, width), f32),) * 3,
        in_specs=[SMEM] + [VMEM] * len(pieces),
        out_specs=(VMEM,) * 3,
        scratch_shapes=[
            pltpu.VMEM((3 * heads * HEAD_DIM, width), f32) for first_head, heads in groups
        ],
        name="finish",
        cost_estimate=COST,
    )(bit, *pieces)


def on_device(
    tokens,
    first_gain,
    first_bias,
    query_weight,
    key_weight,
    value_weight,
    output_weight,
    second_gain,
    second_bias,
    expert_up,
    expert_down,
    item_lengths,
    routes,
    slot_order,
    cotangent,
):
    slots_all, width = tokens.shape
    members = lax.axis_size("tensor")
    shard_rows = slots_all // members
    rank = lax.axis_index("tensor")
    sources = lax.axis_size("dp")
    experts_all = sources * expert_up.shape[0]
    capacity = shard_rows // experts_all
    head_cols = query_weight.shape[1]
    heads = head_cols // HEAD_DIM
    up_matrix = expert_up[0]
    down_matrix = expert_down[0]
    rank_cell = rank.astype(jnp.int32).reshape(1, 1)

    def exchange(rows):
        return lax.all_to_all(
            rows.reshape(sources, -1, width), "dp", split_axis=0, concat_axis=0, tiled=True
        ).reshape(-1, width)

    qw, kw, vw = query_weight.T, key_weight.T, value_weight.T

    dispatch, grad_slots = plan(
        item_lengths, rank_cell, routes, slot_order, cotangent, capacity, experts_all
    )
    flat_grad = exchange(grad_slots)
    tokens, grad_slots = tie(tokens, grad_slots)
    normed_in, qt, kt, vt = project(
        rank_cell[0], tokens, first_gain, first_bias, qw, kw, vw, members
    )
    outputs = [output_weight] + [
        swap(output_weight, "tensor", k) for k in range(1, members)
    ]
    far = members // 2
    *far_heads, far_logs = attend(
        item_lengths, rank_cell, qt, kt, vt, members, far, members - far
    )
    far_heads, kt = tie(far_heads, kt)
    far_arrived = [swap(far_heads[j - far], "tensor", j) for j in range(far, members)]
    *near_heads, near_logs = attend(item_lengths, rank_cell, qt, kt, vt, members, 0, far)
    near_heads, far_arrived, outputs = tie(near_heads, far_arrived, outputs)
    own_heads = near_heads + far_heads
    logs = (near_logs, far_logs)
    all_heads = (
        near_heads[:1]
        + [swap(near_heads[j], "tensor", j) for j in range(1, far)]
        + far_arrived
    )
    residual, outgoing = middle(
        rank_cell[0], tokens, second_gain, second_bias, dispatch, all_heads, outputs
    )
    flat_in = exchange(outgoing)

    flat_grad, outgoing = tie(flat_grad, outgoing)
    grad_act = across(flat_grad, down_matrix)
    gathered_grads = [flat_grad]
    gathered_rows = [flat_in]
    steps = steps_of(members)
    for step in reversed(steps[1:]):
        gathered_grads += [swap(a, "tensor", step) for a in gathered_grads]
    flat_in, grad_act, gathered_grads = tie(flat_in, grad_act, gathered_grads)
    gathered_rows = [flat_in]
    for step in reversed(steps[1:]):
        gathered_rows += [swap(a, "tensor", step) for a in gathered_rows]
    near_grads = swap(gathered_grads[0], "tensor", 1)
    near_rows = swap(flat_in, "tensor", 1)
    far_grads = [swap(a, "tensor", 1) for a in gathered_grads[1:]]
    act, grad_mid = expert(flat_in, grad_act, up_matrix)
    act, grad_mid, near_rows, near_grads, far_grads = tie(
        act, grad_mid, near_rows, near_grads, far_grads
    )
    grad_back = exchange(grad_mid)

    act, near_rows, grad_mid = tie(act, near_rows, grad_mid)
    made = product(act, down_matrix)
    sums = expert_weights(
        rank_cell[0],
        [(flat_in, gathered_grads[0]), (near_rows, near_grads)],
        up_matrix, down_matrix, members,
    )
    made, sums, gathered_rows = tie(made, sums, gathered_rows)
    far_rows = [swap(a, "tensor", 1) for a in gathered_rows[1:]]
    grad_back, made, sums = tie(grad_back, made, sums)

    grad_res, sums_second, kept, sent, *grad_heads = turn(
        item_lengths, rank_cell, dispatch, grad_back, residual, cotangent,
        second_gain, all_heads, outputs,
    )
    grad_parts = [grad_heads[0]] + [
        swap(grad_heads[j], "tensor", j) for j in range(1, members)
    ]
    made, grad_heads = tie(made, grad_heads)
    returned = exchange(made)
    output_sum = add_low(kept, swap(sent, "tensor", 1))
    grad_parts, output_sum = tie(grad_parts, output_sum)

    bit_cell = (lax.axis_index("dp") & 1).astype(jnp.int32).reshape(1, 1)
    weights = (qw, kw, vw)
    dp_steps = steps_of(sources)
    back = functools.partial(
        attend_back, lens=item_lengths, rank=rank_cell, bit=bit_cell, qt=qt, kt=kt, vt=vt,
        logs=logs, weights=weights, normed=normed_in, outs=own_heads,
    )
    groups = ((0, heads - 1), (heads - 1, 1))
    joint_a, sums_a, own_a, away_a = back(*groups[0], extras=(), grads=grad_parts)
    for step in steps[1:]:
        output_sum = add_low(
            output_sum[: len(output_sum) // 2],
            swap(output_sum[len(output_sum) // 2 :], "tensor", step),
        )
    joint_a, own_a, away_a, output_sum, grad_parts = tie(
        joint_a, own_a, away_a, output_sum, grad_parts
    )
    own_a = add_low(own_a, swap(away_a, "dp", 1))
    output_sum = add_low(output_sum[0], swap(output_sum[0], "dp", dp_steps[-1]))
    joint_b, unused, own_b, away_b = back(
        *groups[1], extras=(sums_a, sums_second), grads=grad_parts
    )
    joint_b, own_a, own_b, away_b, output_sum, returned = tie(
        joint_b, own_a, own_b, away_b, output_sum, returned
    )

    far_kept, far_sent = input_grad(
        groups, weights, (joint_a, joint_b), far, members - far, shard_rows
    )
    near_kept, near_sent = input_grad(
        groups, weights, (joint_a, joint_b), 0, far, shard_rows
    )
    own_b = add_parts(own_b, swap(away_b, "dp", 1))
    far_kept = add_low(far_kept, swap(far_sent, "tensor", 1))
    far_kept, own_b, output_sum, near_sent = tie(far_kept, own_b, output_sum, near_sent)
    near_core = swap(near_sent, "tensor", 1)
    near_far = swap(far_kept, "tensor", 2)
    for step in dp_steps[1:]:
        own_a = add_low(own_a, swap(own_a, "dp", step))
        own_b = add_parts(own_b, swap(own_b, "dp", step))
        if step == dp_steps[1]:
            own_b, sums, gathered_rows, far_rows = tie(own_b, sums, gathered_rows, far_rows)
    up_grad, down_grad = expert_weights(
        rank_cell[0],
        list(zip(gathered_rows[1:], gathered_grads[1:])) + list(zip(far_rows, far_grads)),
        up_matrix, down_matrix, members, sums,
    )
    own_b, up_grad, down_grad, near_far = tie(own_b, up_grad, down_grad, near_far)
    norm_sums = own_b[-SUM_ROWS:].astype(f32)
    norm_sums = norm_sums[: SUM_ROWS // 2] + norm_sums[SUM_ROWS // 2 :]
    for step in steps:
        norm_sums = norm_sums + swap(norm_sums, "tensor", step)
    pieces = (own_a, swap(own_a, "dp", 1), own_b, swap(own_b, "dp", 1))
    token_grad = close(
        rank_cell[0], tokens, first_gain, grad_res, (near_kept, near_core, near_far)
    )
    for step in dp_steps[:-1]:
        output_sum = add_low(output_sum, swap(output_sum, "dp", step))

    block_out = residual + contract_rows(dispatch, returned)
    query_grad, key_grad, value_grad = finish(groups, bit_cell, pieces)
    return (
        block_out,
        token_grad,
        (norm_sums[0] - first_bias * norm_sums[1]) / first_gain,
        norm_sums[1],
        query_grad.T,
        key_grad.T,
        value_grad.T,
        output_sum.astype(f32),
        norm_sums[2],
        norm_sums[3],
        up_grad[None],
        down_grad[None],
    )


def solution(mesh):
    in_specs = (
        P("dp", None),
        P(),
        P(),
        P(None, "tensor"),
        P(None, "tensor"),
        P(None, "tensor"),
        P("tensor", None),
        P(),
        P(),
        P("dp", None, None),
        P("dp", None, None),
        P("dp", None),
        P(("dp", "tensor"), None),
        P(("dp", "tensor"), None),
        P(("dp", "tensor"), None),
    )
    out_specs = (
        P(("dp", "tensor"), None),
        P(("dp", "tensor"), None),
        P(),
        P(),
        P(None, "tensor"),
        P(None, "tensor"),
        P(None, "tensor"),
        P("tensor", None),
        P(),
        P(),
        P("dp", None, "tensor"),
        P("dp", "tensor", None),
    )
    return jax.shard_map(
        on_device, mesh=mesh, in_specs=in_specs, out_specs=out_specs, check_vma=False
    )
```

```python
import functools

import jax
import jax.numpy as jnp
from jax import lax
from jax.experimental import pallas as pl
from jax.experimental.pallas import tpu as pltpu
from jax.sharding import PartitionSpec as P

HEAD_DIM = 64
EPSILON = 1e-05
NEGATIVE = -1e30
f32 = jnp.float32
bf16 = jnp.bfloat16
VMEM = pl.BlockSpec(memory_space=pltpu.VMEM)
SMEM = pl.BlockSpec(memory_space=pltpu.SMEM)
SUM_ROWS = 16
COST = pl.CostEstimate(flops=2**20, bytes_accessed=2**20, transcendentals=0)
LONG = pl.CostEstimate(flops=2**34, bytes_accessed=2**24, transcendentals=0)


def layer_norm(values, gain, shift):
    average = jnp.mean(values, axis=-1, keepdims=True)
    centred = values - average
    variance = jnp.mean(centred * centred, axis=-1, keepdims=True)
    return centred * lax.rsqrt(variance + EPSILON) * gain + shift


def contract_rows(left, right):
    return lax.dot_general(
        left, right, (((0,), (0,)), ((), ())), preferred_element_type=f32
    )


def swap(values, axis, step):
    count = lax.axis_size(axis)
    return lax.ppermute(values, axis, [(i, i ^ step) for i in range(count)])


def steps_of(count):
    steps = []
    step = 1
    while step < count:
        steps.append(step)
        step *= 2
    return steps


def normalized(values):
    average = jnp.mean(values, axis=-1, keepdims=True)
    centred = values - average
    variance = jnp.mean(centred * centred, axis=-1, keepdims=True)
    return centred * lax.rsqrt(variance + EPSILON)


def project_kernel(
    rank_ref, tokens_ref, gain_ref, bias_ref, qw_ref, kw_ref, vw_ref,
    normed_ref, qt_ref, kt_ref, vt_ref,
):
    values = tokens_ref[...].astype(f32)
    normed = (normalized(values) * gain_ref[...][None] + bias_ref[...][None]).astype(bf16)
    normed_ref[...] = normed
    for weight_ref, out_ref, factor in (
        (qw_ref, qt_ref, HEAD_DIM ** (-0.5)), (kw_ref, kt_ref, None), (vw_ref, vt_ref, None)
    ):
        made = lax.dot_general(
            weight_ref[...], normed, (((1,), (1,)), ((), ())), preferred_element_type=f32
        ).astype(bf16)
        if factor is not None:
            made = made * jnp.asarray(factor, bf16)
        out_ref[...] = made


def project(rank, tokens, gain, bias, qw, kw, vw, blocks):
    slots, width = tokens.shape
    cols = qw.shape[0]
    size = slots // blocks
    fixed = lambda i, r: (0, 0)
    line = pl.BlockSpec((width,), lambda i, r: (0,))
    return pl.pallas_call(
        project_kernel,
        grid_spec=pltpu.PrefetchScalarGridSpec(
            num_scalar_prefetch=1,
            grid=(blocks,),
            in_specs=[
                pl.BlockSpec((size, width), lambda i, r: (i ^ r[0], 0)),
                line,
                line,
                pl.BlockSpec((cols, width), fixed),
                pl.BlockSpec((cols, width), fixed),
                pl.BlockSpec((cols, width), fixed),
            ],
            out_specs=(
                pl.BlockSpec((size, width), lambda i, r: (i, 0)),
                pl.BlockSpec((cols, size), lambda i, r: (0, i)),
                pl.BlockSpec((cols, size), lambda i, r: (0, i)),
                pl.BlockSpec((cols, size), lambda i, r: (0, i)),
            ),
        ),
        out_shape=(jax.ShapeDtypeStruct((slots, width), bf16),)
        + (jax.ShapeDtypeStruct((cols, slots), bf16),) * 3,
        name="project",
        cost_estimate=COST,
    )(rank, tokens, gain, bias, qw, kw, vw)


def item_ends(lens_ref):
    ends = []
    total = jnp.int32(0)
    for i in range(lens_ref.shape[1]):
        total = total + lens_ref[0, i]
        ends.append(total)
    return ends


def segments_at(place, ends):
    segment = jnp.zeros_like(place)
    for end in ends:
        segment = segment + (place >= end).astype(jnp.int32)
    return segment


def block_span(first, size, unit, ends):
    last = jnp.minimum(first + size, ends[-1]) - 1
    low = jnp.int32(0)
    high = ends[-1]
    for end in ends:
        low = jnp.where(first >= end, end, low)
    for end in reversed(ends):
        high = jnp.where(last < end, end, high)
    empty = first >= ends[-1]
    low_block = jnp.where(empty, 0, low // unit)
    high_block = jnp.where(empty, 0, (high + unit - 1) // unit)
    return low_block, high_block


def rows_at(block, size):
    return pl.ds(pl.multiple_of(block * size, size), size)


def fill_segments(row_ref, col_ref, shard, rank, ends):
    slots = row_ref.shape[1]
    at = lax.broadcasted_iota(jnp.int32, (1, slots), 1)
    place = ((at // shard) ^ rank) * shard + at % shard
    segments = segments_at(place, ends)
    row_ref[...] = segments
    col_ref[...] = jnp.transpose(jnp.broadcast_to(segments, (128, slots)), (1, 0))


def block_bias(row_ref, col_ref, rows, cols):
    return jnp.where(col_ref[rows, 0:1] == row_ref[:, cols], 0.0, NEGATIVE)


def lane_masked(values, head):
    lane = lax.broadcasted_iota(jnp.int32, values.shape, 1)
    inside = (lane >= head * HEAD_DIM) & (lane < (head + 1) * HEAD_DIM)
    return jnp.where(inside, values, jnp.zeros_like(values))


def forward_kernel(
    first, blocks, lens_ref, rank_ref, qt_ref, kt_ref, vt_ref, *refs
):
    *out_refs, log_ref, masked_ref, out_ref, row_ref, col_ref, score_ref = refs
    count, width, size = out_ref.shape
    heads = width // HEAD_DIM
    shard = size
    rank = rank_ref[0, 0]
    ends = item_ends(lens_ref)
    fill_segments(row_ref, col_ref, shard, rank, ends)
    keys = jnp.transpose(kt_ref[...], (1, 0))
    for h in range(heads):
        masked_ref[h] = lane_masked(keys, h)

    def query_block(b, unused):
        at = first + b
        i = at ^ rank
        cols = rows_at(at, size)
        queries = qt_ref[:, cols]

        def score_block(j, carry):
            rows = rows_at(j ^ rank, shard)
            bias = block_bias(row_ref, col_ref, rows, cols)
            result = []
            for h in range(heads):
                scores = jnp.dot(
                    masked_ref[h, rows, :], queries, preferred_element_type=f32
                )
                scores = scores + bias
                score_ref[h, rows_at(j, shard), :] = scores
                part = jnp.max(scores.reshape(-1, 8, size), axis=0)
                result.append(jnp.maximum(carry[h], part))
            return tuple(result)

        low, high = block_span(i * size, size, shard, ends)
        peaks = lax.fori_loop(
            low, high, score_block, (jnp.full((8, size), NEGATIVE, f32),) * heads
        )
        peaks = [jnp.max(peak, axis=0, keepdims=True) for peak in peaks]

        def key_block(j, carry):
            rows = rows_at(j ^ rank, shard)
            result = []
            for h in range(heads):
                summed, total = carry[h]
                soft = jnp.exp(score_ref[h, rows_at(j, shard), :] - peaks[h])
                summed = summed + jnp.sum(soft.reshape(-1, 8, size), axis=0)
                total = total + jnp.dot(
                    vt_ref[pl.ds(h * HEAD_DIM, HEAD_DIM), rows],
                    soft.astype(bf16),
                    preferred_element_type=f32,
                )
                result.append((summed, total))
            return tuple(result)

        start = ((jnp.zeros((8, size), f32), jnp.zeros((HEAD_DIM, size), f32)),) * heads
        done = lax.fori_loop(low, high, key_block, start)
        live = row_ref[:, cols] < len(ends)
        for h in range(heads):
            summed, total = done[h]
            summed = jnp.sum(summed, axis=0, keepdims=True)
            highest = peaks[h]
            summed = jnp.where(live, summed, 1.0)
            result = jnp.where(live, total / summed, 0.0).astype(bf16)
            logs = jnp.where(live, highest + jnp.log(summed), -NEGATIVE)
            out_ref[b, pl.ds(h * HEAD_DIM, HEAD_DIM), :] = result
            log_ref[h, :, rows_at(b, size)] = logs
        return unused

    lax.fori_loop(0, count, query_block, 0)
    for b in range(count):
        out_refs[b][...] = out_ref[b]


def attend(lens, rank, qt, kt, vt, blocks, first, count):
    width, slots = qt.shape
    size = slots // blocks
    heads = width // HEAD_DIM
    return pl.pallas_call(
        functools.partial(forward_kernel, first, blocks),
        out_shape=(jax.ShapeDtypeStruct((width, size), bf16),) * count
        + (jax.ShapeDtypeStruct((heads, 1, count * size), f32),),
        in_specs=[SMEM, SMEM, VMEM, VMEM, VMEM],
        out_specs=(VMEM,) * (count + 1),
        scratch_shapes=[
            pltpu.VMEM((heads, slots, width), bf16),
            pltpu.VMEM((count, width, size), bf16),
            pltpu.VMEM((1, slots), jnp.int32),
            pltpu.VMEM((slots, 128), jnp.int32),
            pltpu.VMEM((heads, slots, size), f32),
        ],
        name="attend",
        compiler_params=pltpu.CompilerParams(vmem_limit_bytes=60 * 2**20),
        cost_estimate=COST,
    )(lens, rank, qt, kt, vt)


def split_rows(values):
    high = values.astype(bf16)
    return jnp.concatenate([high, (values - high.astype(f32)).astype(bf16)], axis=0)


def add_kernel(a_ref, b_ref, out_ref):
    half = out_ref.shape[0] - SUM_ROWS
    line = SUM_ROWS // 2
    total = a_ref[...].astype(f32) + b_ref[...].astype(f32)
    out_ref[:half, :] = total[:half].astype(bf16)
    out_ref[half:, :] = split_rows(total[half : half + line] + total[half + line :])


def add_parts(a, b):
    return pl.pallas_call(
        add_kernel,
        out_shape=jax.ShapeDtypeStruct(a.shape, bf16),
        in_specs=[VMEM, VMEM],
        out_specs=VMEM,
        name="add_parts",
        cost_estimate=COST,
    )(a, b)


def stacked_parts(first_head, heads, query, key, value):
    dim = HEAD_DIM
    parts = []
    for n in range(heads):
        first = (first_head + n) * dim
        parts += [(2 * n * dim, key, first, dim), ((2 * n + 1) * dim, value, first, dim)]
    return parts + [(2 * heads * dim, query, first_head * dim, heads * dim)]


def backward_kernel(
    first_head, heads, blocks, extras, lens_ref, rank_ref, bit_ref, qt_ref, kt_ref, vt_ref,
    near_ref, far_ref, qw_ref, kw_ref, vw_ref, normed_ref, *rest
):
    extra_refs, rest = rest[:extras], rest[extras:]
    width, slots = qt_ref.shape
    shard = slots // blocks
    dim = HEAD_DIM
    out_refs, grad_refs = rest[:blocks], rest[blocks : 2 * blocks]
    joint_ref, sums_ref, own_ref, away_ref = rest[2 * blocks : 2 * blocks + 4]
    kv_ref, q0_ref, og_ref, right_ref, inner_ref, dq_ref, made_ref = rest[-13:-6]
    log_ref = rest[-6]
    row_ref, col_ref = rest[-5:-3]
    turned_ref, rows_ref, copied = rest[-3:]
    fetch = pltpu.make_async_copy(normed_ref, rows_ref, copied)
    fetch.start()
    unit = shard // 2
    rank = rank_ref[0, 0]
    ends = item_ends(lens_ref)
    fill_segments(row_ref, col_ref, shard, rank, ends)
    near = near_ref.shape[2]
    log_ref[:, :, :near] = near_ref[...]
    log_ref[:, :, near:] = far_ref[...]
    zero = jnp.zeros((dim, slots), bf16)
    for n in range(heads):
        part = slice((first_head + n) * dim, (first_head + n + 1) * dim)
        both = jnp.concatenate([kt_ref[part, :], vt_ref[part, :]], axis=0)
        kv_ref[n] = jnp.transpose(both, (1, 0))
        padded = jnp.concatenate([qt_ref[part, :], zero], axis=0)
        q0_ref[n] = jnp.transpose(padded, (1, 0))
        right_ref[n, 0] = padded
        for b in range(blocks):
            grad = grad_refs[b][part, :]
            cols = slice(b * shard, (b + 1) * shard)
            padded = jnp.concatenate([zero[:, :shard], grad], axis=0)
            og_ref[n, cols, :] = jnp.transpose(padded, (1, 0))
            right_ref[n, 1, :, cols] = padded
            inner_ref[n, :, cols] = jnp.sum(
                out_refs[b][part, :].astype(f32) * grad.astype(f32), axis=0, keepdims=True
            )
    dq_ref[...] = jnp.zeros_like(dq_ref)

    def key_block(j, unused):
        at_key = ((j // 2) ^ rank) * 2 + j % 2
        rows = rows_at(at_key, unit)

        def query_block(i, totals):
            at = i ^ rank
            cols = rows_at(at, shard)
            same = col_ref[rows, 0:1] == row_ref[:, cols]
            result = []
            for n in range(heads):
                head = first_head + n
                kv = kv_ref[n, rows, :]
                scores = jnp.dot(kv, right_ref[n, 0, :, cols], preferred_element_type=f32)
                grad_soft = jnp.dot(kv, right_ref[n, 1, :, cols], preferred_element_type=f32)
                soft = jnp.where(same, jnp.exp(scores - log_ref[head, :, cols]), 0.0)
                grad_scores = (soft * (grad_soft - inner_ref[n, :, cols])).astype(bf16)
                total = totals[n] + jnp.dot(
                    soft.astype(bf16), og_ref[n, cols, :], preferred_element_type=f32
                )
                total = total + jnp.dot(
                    grad_scores, q0_ref[n, cols, :], preferred_element_type=f32
                )
                dq_ref[n, :, cols] += jnp.dot(
                    kt_ref[pl.ds(head * dim, dim), rows], grad_scores,
                    preferred_element_type=f32,
                )
                result.append(total)
            return tuple(result)

        low, high = block_span(j * unit, unit, shard, ends)
        start = (jnp.zeros((unit, 2 * dim), f32),) * heads
        totals = lax.fori_loop(low, high, query_block, start)
        for n in range(heads):
            part = slice(2 * dim * n, 2 * dim * (n + 1))
            total = totals[n].astype(bf16)
            joint_ref[rows, part] = total
            turned_ref[part, rows] = jnp.transpose(total, (1, 0))
        return unused

    lax.fori_loop(0, 2 * blocks, key_block, 0)
    dq = (dq_ref[...] * dim ** (-0.5)).astype(bf16).reshape(heads * dim, slots)
    turned_ref[2 * dim * heads :, :] = dq
    joint_ref[:, 2 * dim * heads :] = jnp.transpose(dq, (1, 0))
    fetch.wait()
    made_ref[...] = jnp.dot(turned_ref[...], rows_ref[...], preferred_element_type=f32)
    gains = jnp.zeros((1, rows_ref.shape[1]), f32)
    shifts = jnp.zeros((1, rows_ref.shape[1]), f32)
    for at, weight_ref, first, size in stacked_parts(
        first_head, heads, qw_ref, kw_ref, vw_ref
    ):
        weight = weight_ref[first : first + size, :].astype(f32)
        gains += jnp.sum(weight * made_ref[at : at + size, :], axis=0, keepdims=True)
        total = jnp.sum(turned_ref[at : at + size, :].astype(f32), axis=1, keepdims=True)
        shifts += jnp.sum(weight * total, axis=0, keepdims=True)
    sums_ref[0:1] = gains
    sums_ref[1:2] = shifts
    half = made_ref.shape[0] // 2
    bit = bit_ref[0, 0]
    for part_ref, at in ((own_ref, bit), (away_ref, 1 - bit)):
        part_ref[0:half, :] = made_ref[rows_at(at, half), :].astype(bf16)
        if extras:
            lines = [sums_ref[...] + extra_refs[0][...], extra_refs[1][...]]
            lines.append(jnp.zeros((SUM_ROWS // 2 - 4, gains.shape[1]), f32))
            part_ref[half:, :] = split_rows(jnp.concatenate(lines, axis=0))


def attend_back(
    first_head, heads, extras, lens, rank, bit, qt, kt, vt, logs, weights, normed, outs, grads
):
    slots, width = normed.shape
    blocks = len(outs)
    dim = HEAD_DIM
    cols = 3 * dim * heads
    rows = cols // 2 + (SUM_ROWS if extras else 0)
    return pl.pallas_call(
        functools.partial(backward_kernel, first_head, heads, blocks, len(extras)),
        out_shape=(
            jax.ShapeDtypeStruct((slots, cols), bf16),
            jax.ShapeDtypeStruct((2, width), f32),
        )
        + (jax.ShapeDtypeStruct((rows, width), bf16),) * 2,
        in_specs=[SMEM, SMEM, SMEM]
        + [VMEM] * 8
        + [pl.BlockSpec(memory_space=pl.ANY)]
        + [VMEM] * (len(extras) + 2 * blocks),
        out_specs=(VMEM,) * 4,
        scratch_shapes=[pltpu.VMEM((heads, slots, 2 * dim), bf16)] * 3
        + [
            pltpu.VMEM((heads, 2, 2 * dim, slots), bf16),
            pltpu.VMEM((heads, 1, slots), f32),
            pltpu.VMEM((heads, dim, slots), f32),
            pltpu.VMEM((cols, width), f32),
            pltpu.VMEM((qt.shape[0] // dim, 1, slots), f32),
            pltpu.VMEM((1, slots), jnp.int32),
            pltpu.VMEM((slots, 128), jnp.int32),
            pltpu.VMEM((cols, slots), bf16),
            pltpu.VMEM((slots, width), bf16),
            pltpu.SemaphoreType.DMA,
        ],
        name="attend_back",
        compiler_params=pltpu.CompilerParams(vmem_limit_bytes=60 * 2**20),
        cost_estimate=COST,
    )(lens, rank, bit, qt, kt, vt, *logs, *weights, normed, *extras, *outs, *grads)


def plan_kernel(capacity, lens_ref, rank_ref, routes_ref, order_ref, grad_ref,
                dispatch_ref, slots_ref):
    shard = routes_ref.shape[1]
    first = rank_ref[0, 0] * shard
    ends = item_ends(lens_ref)
    chosen_row = routes_ref[...]
    chosen_col = jnp.transpose(jnp.broadcast_to(chosen_row, (128, shard)), (1, 0))[:, 0:1]
    order_row = order_ref[...]
    order_col = jnp.transpose(jnp.broadcast_to(order_row, (128, shard)), (1, 0))[:, 0:1]
    alive_row = segments_at(
        first + lax.broadcasted_iota(jnp.int32, (1, shard), 1), ends
    ) < len(ends)
    alive_col = segments_at(
        first + lax.broadcasted_iota(jnp.int32, (shard, 1), 0), ends
    ) < len(ends)
    ahead = (chosen_col == chosen_row) & (order_col < order_row) & alive_col
    ranked = jnp.sum(ahead.astype(jnp.int32), axis=0, keepdims=True)
    kept = alive_row & (ranked < capacity)
    slot = jnp.where(kept, chosen_row * capacity + ranked, -1)
    dispatch = (
        lax.broadcasted_iota(jnp.int32, dispatch_ref.shape, 0) == slot
    ).astype(f32).astype(bf16)
    dispatch_ref[...] = dispatch
    slots_ref[...] = jnp.dot(
        dispatch, grad_ref[...], preferred_element_type=f32
    ).astype(bf16)


def plan(lens, rank, routes, order, grads, capacity, experts_all):
    shard, width = grads.shape
    count = experts_all * capacity
    return pl.pallas_call(
        functools.partial(plan_kernel, capacity),
        out_shape=(
            jax.ShapeDtypeStruct((count, shard), bf16),
            jax.ShapeDtypeStruct((count, width), bf16),
        ),
        in_specs=[SMEM, SMEM, VMEM, VMEM, VMEM],
        out_specs=(VMEM, VMEM),
        name="plan",
        cost_estimate=COST,
    )(lens, rank, routes.reshape(1, -1), order, grads)


def across(left, right):
    return lax.dot_general(
        left, right, (((1,), (1,)), ((), ())), preferred_element_type=f32
    )


def middle_kernel(count, rank_ref, tokens_ref, gain_ref, bias_ref, dispatch_ref, *refs):
    head_refs, weight_refs = refs[:count], refs[count : 2 * count]
    residual_ref, rows_ref = refs[2 * count :]
    residual = tokens_ref[...].astype(f32)
    for head_ref, weight_ref in zip(head_refs, weight_refs):
        residual = residual + contract_rows(head_ref[...], weight_ref[...])
    residual_ref[...] = residual
    normed = (normalized(residual) * gain_ref[...][None] + bias_ref[...][None]).astype(bf16)
    rows_ref[...] = jnp.dot(
        dispatch_ref[...], normed, preferred_element_type=f32
    ).astype(bf16)


def middle(rank, tokens, gain, bias, dispatch, heads, weights):
    count, shard = dispatch.shape
    width = tokens.shape[1]
    fixed = lambda array: pl.BlockSpec(array.shape, lambda i, r: (0,) * array.ndim)
    small = [gain, bias, dispatch, *heads, *weights]
    return pl.pallas_call(
        functools.partial(middle_kernel, len(heads)),
        grid_spec=pltpu.PrefetchScalarGridSpec(
            num_scalar_prefetch=1,
            grid=(1,),
            in_specs=[pl.BlockSpec((shard, width), lambda i, r: (r[0], 0))]
            + [fixed(array) for array in small],
            out_specs=(
                pl.BlockSpec((shard, width), lambda i, r: (0, 0)),
                pl.BlockSpec((count, width), lambda i, r: (0, 0)),
            ),
        ),
        out_shape=(
            jax.ShapeDtypeStruct((shard, width), f32),
            jax.ShapeDtypeStruct((count, width), bf16),
        ),
        name="middle",
        cost_estimate=COST,
    )(rank, tokens, *small)


def turn_kernel(
    count, lens_ref, rank_ref, dispatch_ref, back_ref, residual_ref, cotangent_ref,
    gain_ref, *refs
):
    head_refs, weight_refs = refs[:count], refs[count : 2 * count]
    grad_ref, sums_ref, kept_ref, sent_ref = refs[2 * count : 2 * count + 4]
    part_refs = refs[2 * count + 4 :]
    shard = residual_ref.shape[0]
    grad_normed = contract_rows(dispatch_ref[...], back_ref[...])
    values = residual_ref[...]
    centred = values - jnp.mean(values, axis=-1, keepdims=True)
    inverse = lax.rsqrt(jnp.mean(centred * centred, axis=-1, keepdims=True) + EPSILON)
    normed = centred * inverse
    sums_ref[0:1] = jnp.sum(grad_normed * normed, axis=0, keepdims=True)
    sums_ref[1:2] = jnp.sum(grad_normed, axis=0, keepdims=True)
    scaled = grad_normed * gain_ref[...][None]
    grad = cotangent_ref[...].astype(f32) + inverse * (
        scaled
        - jnp.mean(scaled, axis=-1, keepdims=True)
        - normed * jnp.mean(scaled * normed, axis=-1, keepdims=True)
    )
    grad_ref[...] = grad
    low = grad.astype(bf16)
    place = rank_ref[0, 0] * shard + lax.broadcasted_iota(jnp.int32, (1, shard), 1)
    alive = place < item_ends(lens_ref)[-1]
    for weight_ref, part_ref in zip(weight_refs, part_refs):
        part_ref[...] = jnp.where(alive, across(weight_ref[...], low), 0.0).astype(bf16)
    for j, head_ref in enumerate(head_refs):
        made = jnp.dot(head_ref[...], low, preferred_element_type=f32)
        (kept_ref, sent_ref)[j % 2][j // 2] = made.astype(bf16)


def turn(lens, rank, dispatch, back, residual, cotangent, gain, heads, weights):
    shard, width = residual.shape
    cols = weights[0].shape[0]
    count = len(weights)
    return pl.pallas_call(
        functools.partial(turn_kernel, count),
        out_shape=(
            jax.ShapeDtypeStruct((shard, width), f32),
            jax.ShapeDtypeStruct((2, width), f32),
            jax.ShapeDtypeStruct((count // 2, cols, width), bf16),
            jax.ShapeDtypeStruct((count // 2, cols, width), bf16),
        )
        + (jax.ShapeDtypeStruct((cols, shard), bf16),) * count,
        in_specs=[SMEM, SMEM] + [VMEM] * (5 + 2 * count),
        out_specs=(VMEM,) * (4 + count),
        name="turn",
        cost_estimate=COST,
    )(lens, rank, dispatch, back, residual, cotangent, gain, *heads, *weights)


def output_sum_kernel(kept_ref, core_ref, first_ref, near_ref, far_ref):
    cols = near_ref.shape[0]
    total = [
        (kept_ref[j].astype(f32) + core_ref[j].astype(f32)).astype(bf16) for j in range(2)
    ]
    near_ref[...] = total[0]
    far_ref[:cols, :] = total[1]
    far_ref[cols:, :] = first_ref[...]


def output_sums(kept, core, first):
    slots, cols, width = kept.shape
    return pl.pallas_call(
        output_sum_kernel,
        out_shape=(
            jax.ShapeDtypeStruct((cols, width), bf16),
            jax.ShapeDtypeStruct((cols + first.shape[0], width), bf16),
        ),
        in_specs=[VMEM] * 3,
        out_specs=(VMEM, VMEM),
        name="output_sums",
        cost_estimate=LONG,
    )(kept, core, first)


def gelu_parts(values):
    below = 0.5 + 0.5 * lax.erf(values * (0.5**0.5))
    density = jnp.exp(-0.5 * values * values) * (0.5 / jnp.pi) ** 0.5
    return values * below, below + values * density


def part_at(step, parts, rank):
    half = parts // 2
    return (2 * (step % half) + step // half) ^ rank


def expert_kernel(
    rank_ref, in_ref, grad_act_ref, up_ref,
    act_kept_ref, pre_kept_ref, act_sent_ref, pre_sent_ref, mid_ref, sum_ref,
):
    step = pl.program_id(0)
    pre = jnp.dot(in_ref[...], up_ref[...], preferred_element_type=f32)
    act, slope = gelu_parts(pre)
    act = act.astype(bf16)
    grad_pre = (grad_act_ref[...] * slope).astype(bf16)
    half = pl.num_programs(0) // 2

    @pl.when(step < half)
    def keep():
        act_kept_ref[...] = act
        pre_kept_ref[...] = grad_pre

    @pl.when(step >= half)
    def send():
        act_sent_ref[...] = act
        pre_sent_ref[...] = grad_pre

    mid = across(grad_pre, up_ref[...])

    @pl.when(step == 0)
    def first():
        sum_ref[...] = mid

    @pl.when(step > 0)
    def later():
        sum_ref[...] += mid

    @pl.when(step == pl.num_programs(0) - 1)
    def last():
        mid_ref[...] = sum_ref[...].astype(bf16)


def expert(rank, rows, grad_act, up, parts):
    count, width = rows.shape
    hidden = up.shape[1]
    size = min(256, hidden // parts)
    cuts = hidden // parts // size
    steps = parts * cuts
    column = lambda i, r: (0, part_at(i // cuts, parts, r[0]) * cuts + i % cuts)
    kept = pl.BlockSpec((count, size), lambda i, r: (0, jnp.minimum(i, steps // 2 - 1)))
    sent = pl.BlockSpec((count, size), lambda i, r: (0, jnp.maximum(i - steps // 2, 0)))
    fixed = pl.BlockSpec((count, width), lambda i, r: (0, 0))
    return pl.pallas_call(
        expert_kernel,
        grid_spec=pltpu.PrefetchScalarGridSpec(
            num_scalar_prefetch=1,
            grid=(steps,),
            in_specs=[
                fixed,
                pl.BlockSpec((count, size), column),
                pl.BlockSpec((width, size), column),
            ],
            out_specs=(kept, kept, sent, sent, fixed),
            scratch_shapes=[pltpu.VMEM((count, width), f32)],
        ),
        out_shape=(jax.ShapeDtypeStruct((count, hidden // 2), bf16),) * 4
        + (jax.ShapeDtypeStruct((count, width), bf16),),
        name="expert",
        cost_estimate=COST,
    )(rank, rows, grad_act, up)


def product_kernel(rank_ref, kept_ref, sent_ref, down_ref, out_ref, sum_ref):
    step = pl.program_id(0)
    steps = pl.num_programs(0)
    act = jnp.where(step < steps // 2, kept_ref[...], sent_ref[...])
    made = jnp.dot(act, down_ref[...], preferred_element_type=f32)

    @pl.when(step == 0)
    def first():
        sum_ref[...] = made

    @pl.when(step > 0)
    def later():
        sum_ref[...] += made

    @pl.when(step == steps - 1)
    def last():
        out_ref[...] = sum_ref[...].astype(bf16)


def product(rank, kept, sent, down, parts):
    count = kept.shape[0]
    hidden, width = down.shape
    size = hidden // parts
    return pl.pallas_call(
        product_kernel,
        grid_spec=pltpu.PrefetchScalarGridSpec(
            num_scalar_prefetch=1,
            grid=(parts,),
            in_specs=[
                pl.BlockSpec((count, size), lambda i, r: (0, jnp.minimum(i, parts // 2 - 1))),
                pl.BlockSpec((count, size), lambda i, r: (0, jnp.maximum(i - parts // 2, 0))),
                pl.BlockSpec((size, width), lambda i, r: (part_at(i, parts, r[0]), 0)),
            ],
            out_specs=pl.BlockSpec((count, width), lambda i, r: (0, 0)),
            scratch_shapes=[pltpu.VMEM((count, width), f32)],
        ),
        out_shape=jax.ShapeDtypeStruct((count, width), bf16),
        name="product",
        cost_estimate=COST,
    )(rank, kept, sent, down)


def weight_kernel(groups, *refs):
    first_ref, rest_ref, up_ref, down_ref = refs[-4:]
    dup = ddown = 0.0
    for g in range(groups):
        in_ref, grad_ref, act_ref, pre_ref = refs[4 * g : 4 * g + 4]
        dup = dup + contract_rows(in_ref[...], pre_ref[...])
        ddown = ddown + contract_rows(act_ref[...], grad_ref[...])
    cut = first_ref.shape[0]

    @pl.when(pl.program_id(0) == 0)
    def far():
        first_ref[...] = dup[:cut].astype(bf16)
        rest_ref[: dup.shape[0] - cut, :] = dup[cut:].astype(bf16)
        rest_ref[dup.shape[0] - cut :, :] = ddown.astype(bf16)

    @pl.when(pl.program_id(0) == 1)
    def near():
        up_ref[...] = dup
        down_ref[...] = ddown


def expert_weights(groups):
    count, width = groups[0][0].shape
    size = groups[0][2].shape[1] // 2
    fixed = pl.BlockSpec((count, width), lambda i: (0, 0))
    columns = pl.BlockSpec((count, size), lambda i: (0, 1 - i))
    cut = (width + size) // 4
    shapes = ((cut, size), (width + size - cut, size), (width, size), (size, width))
    return pl.pallas_call(
        functools.partial(weight_kernel, len(groups)),
        grid=(2,),
        in_specs=[fixed, fixed, columns, columns] * len(groups),
        out_specs=tuple(pl.BlockSpec(shape, lambda i: (0, 0)) for shape in shapes),
        out_shape=tuple(
            jax.ShapeDtypeStruct(shape, bf16 if k < 2 else f32)
            for k, shape in enumerate(shapes)
        ),
        name="expert_weights",
        compiler_params=pltpu.CompilerParams(vmem_limit_bytes=60 * 2**20),
        cost_estimate=COST,
    )(*[values for group in groups for values in group])


def expert_sum_kernel(near_up_ref, near_down_ref, first_ref, rest_ref, up_ref, down_ref):
    step = pl.program_id(0)
    half = pl.num_programs(0) // 2
    far = jnp.where(step < half // 2, first_ref[...], rest_ref[...]).astype(f32)

    @pl.when(step < half)
    def upper():
        up_ref[...] = near_up_ref[...] + far

    @pl.when(step >= half)
    def lower():
        down_ref[...] = near_down_ref[...] + far


def expert_sums(near_up, near_down, first, rest):
    count, width = near_up.shape
    steps = 8
    half = steps // 2
    size = count // half
    head = steps // 4
    skip = first.shape[0] // size - head
    block = lambda place: pl.BlockSpec((size, width), lambda i: (place(i), 0))
    upper = block(lambda i: jnp.minimum(i, half - 1))
    lower = block(lambda i: jnp.maximum(i - half, 0))
    return pl.pallas_call(
        expert_sum_kernel,
        grid=(steps,),
        out_shape=(jax.ShapeDtypeStruct((count, width), f32),) * 2,
        in_specs=[
            upper,
            lower,
            block(lambda i: jnp.minimum(i, head - 1) + skip),
            block(lambda i: jnp.maximum(i - head, 0)),
        ],
        out_specs=(upper, lower),
        name="expert_sums",
        cost_estimate=COST,
    )(near_up, near_down, first, rest)


def input_grad_kernel(groups, qw_ref, kw_ref, vw_ref, *refs):
    joint_refs = refs[: len(groups)]
    kept_ref, sent_ref, turned_ref = refs[len(groups) :]
    step = pl.program_id(0)

    @pl.when(step == 0)
    def stack():
        start = 0
        for first_head, heads in groups:
            for at, weight_ref, first, size in stacked_parts(
                first_head, heads, qw_ref, kw_ref, vw_ref
            ):
                turned_ref[start + at : start + at + size, :] = weight_ref[
                    first : first + size, :
                ]
            start += 3 * heads * HEAD_DIM

    total = 0.0
    at = 0
    for joint_ref in joint_refs:
        rows = slice(at, at + joint_ref.shape[1])
        total = total + jnp.dot(
            joint_ref[...], turned_ref[rows, :], preferred_element_type=f32
        )
        at += joint_ref.shape[1]

    @pl.when(step % 2 == 0)
    def keep():
        kept_ref[0] = total.astype(bf16)

    @pl.when(step % 2 == 1)
    def send():
        sent_ref[0] = total.astype(bf16)


def input_grad(groups, weights, joints, first, count, size):
    cols, width = weights[0].shape
    fixed = pl.BlockSpec((cols, width), lambda i: (0, 0))
    return pl.pallas_call(
        functools.partial(input_grad_kernel, groups),
        grid=(count,),
        out_shape=(jax.ShapeDtypeStruct((count // 2, size, width), bf16),) * 2,
        in_specs=[fixed] * 3
        + [
            pl.BlockSpec((size, joint.shape[1]), lambda i: (first + i, 0))
            for joint in joints
        ],
        out_specs=(pl.BlockSpec((1, size, width), lambda i: (i // 2, 0, 0)),) * 2,
        scratch_shapes=[pltpu.VMEM((3 * cols, width), bf16)],
        name="input_grad",
        cost_estimate=COST,
    )(*weights, *joints)


def close_kernel(rank_ref, tokens_ref, gain_ref, grad_ref, *refs):
    *part_refs, out_ref = refs
    grad_in = 0.0
    for part_ref in part_refs:
        grad_in = grad_in + part_ref[...].reshape(out_ref.shape).astype(f32)
    values = tokens_ref[...].astype(f32)
    centred = values - jnp.mean(values, axis=-1, keepdims=True)
    inverse = lax.rsqrt(jnp.mean(centred * centred, axis=-1, keepdims=True) + EPSILON)
    normed = centred * inverse
    scaled = grad_in * gain_ref[...][None]
    out_ref[...] = grad_ref[...] + inverse * (
        scaled
        - jnp.mean(scaled, axis=-1, keepdims=True)
        - normed * jnp.mean(scaled * normed, axis=-1, keepdims=True)
    )


def close(rank, tokens, gain, grad, parts):
    shard, width = grad.shape
    size = shard // 2
    rows = lambda i, r: (i, 0)
    return pl.pallas_call(
        close_kernel,
        grid_spec=pltpu.PrefetchScalarGridSpec(
            num_scalar_prefetch=1,
            grid=(2,),
            in_specs=[
                pl.BlockSpec((size, width), lambda i, r: (2 * r[0] + i, 0)),
                pl.BlockSpec((width,), lambda i, r: (0,)),
                pl.BlockSpec((size, width), rows),
            ]
            + [pl.BlockSpec((1, size, width), lambda i, r: (0, i, 0))] * len(parts),
            out_specs=pl.BlockSpec((size, width), rows),
        ),
        out_shape=jax.ShapeDtypeStruct((shard, width), f32),
        name="close",
        cost_estimate=COST,
    )(rank, tokens, gain, grad, *parts)


def add_low(a, b):
    return (a.astype(f32) + b.astype(f32)).astype(bf16)


def tie(*values):
    return lax.optimization_barrier(values)


def finish_kernel(groups, bit_ref, *refs):
    pieces, refs = refs[: 2 * len(groups)], refs[2 * len(groups) :]
    query_ref, key_ref, value_ref = refs[:3]
    bit = bit_ref[0, 0]
    for g, ((first_head, heads), whole_ref) in enumerate(zip(groups, refs[3:])):
        half = whole_ref.shape[0] // 2
        for piece_ref, at in ((pieces[2 * g], bit), (pieces[2 * g + 1], 1 - bit)):
            whole_ref[rows_at(at, half), :] = piece_ref[0:half, :].astype(f32)
        for at, target_ref, first, size in stacked_parts(
            first_head, heads, query_ref, key_ref, value_ref
        ):
            target_ref[first : first + size, :] = whole_ref[at : at + size, :]


def finish(groups, bit, pieces):
    width = pieces[0].shape[1]
    cols = sum(heads for first_head, heads in groups) * HEAD_DIM
    return pl.pallas_call(
        functools.partial(finish_kernel, groups),
        out_shape=(jax.ShapeDtypeStruct((cols, width), f32),) * 3,
        in_specs=[SMEM] + [VMEM] * len(pieces),
        out_specs=(VMEM,) * 3,
        scratch_shapes=[
            pltpu.VMEM((3 * heads * HEAD_DIM, width), f32) for first_head, heads in groups
        ],
        name="finish",
        cost_estimate=COST,
    )(bit, *pieces)


def on_device(
    tokens,
    first_gain,
    first_bias,
    query_weight,
    key_weight,
    value_weight,
    output_weight,
    second_gain,
    second_bias,
    expert_up,
    expert_down,
    item_lengths,
    routes,
    slot_order,
    cotangent,
):
    slots_all, width = tokens.shape
    members = lax.axis_size("tensor")
    shard_rows = slots_all // members
    rank = lax.axis_index("tensor")
    sources = lax.axis_size("dp")
    experts_all = sources * expert_up.shape[0]
    capacity = shard_rows // experts_all
    head_cols = query_weight.shape[1]
    heads = head_cols // HEAD_DIM
    up_matrix = expert_up[0]
    down_matrix = expert_down[0]
    rank_cell = rank.astype(jnp.int32).reshape(1, 1)

    def exchange(rows):
        return lax.all_to_all(
            rows.reshape(sources, -1, width), "dp", split_axis=0, concat_axis=0, tiled=True
        ).reshape(-1, width)

    qw, kw, vw = query_weight.T, key_weight.T, value_weight.T

    dispatch, grad_slots = plan(
        item_lengths, rank_cell, routes, slot_order, cotangent, capacity, experts_all
    )
    flat_grad = exchange(grad_slots)
    tokens, grad_slots = tie(tokens, grad_slots)
    normed_in, qt, kt, vt = project(
        rank_cell[0], tokens, first_gain, first_bias, qw, kw, vw, members
    )
    outputs = [output_weight] + [
        swap(output_weight, "tensor", k) for k in range(1, members)
    ]
    far = members // 2
    *far_heads, far_logs = attend(
        item_lengths, rank_cell, qt, kt, vt, members, far, members - far
    )
    far_heads, kt = tie(far_heads, kt)
    far_arrived = [swap(far_heads[j - far], "tensor", j) for j in range(far, members)]
    *near_heads, near_logs = attend(item_lengths, rank_cell, qt, kt, vt, members, 0, far)
    near_heads, far_arrived, outputs = tie(near_heads, far_arrived, outputs)
    own_heads = near_heads + far_heads
    logs = (near_logs, far_logs)
    all_heads = (
        near_heads[:1]
        + [swap(near_heads[j], "tensor", j) for j in range(1, far)]
        + far_arrived
    )
    residual, outgoing = middle(
        rank_cell[0], tokens, second_gain, second_bias, dispatch, all_heads, outputs
    )
    flat_in = exchange(outgoing)

    flat_grad, outgoing = tie(flat_grad, outgoing)
    grad_act = across(flat_grad, down_matrix)
    near_grads = swap(flat_grad, "tensor", 1)
    flat_in, grad_act, near_grads = tie(flat_in, grad_act, near_grads)
    near_rows = swap(flat_in, "tensor", 1)
    act, grad_pre, act_sent, pre_sent, grad_mid = expert(
        rank_cell[0], flat_in, grad_act, up_matrix, members
    )
    grad_mid, act, near_rows = tie(grad_mid, act, near_rows)
    grad_back = exchange(grad_mid)

    act, act_sent, pre_sent, grad_mid = tie(act, act_sent, pre_sent, grad_mid)
    near_act = swap(act_sent, "tensor", 1)
    near_pre = swap(pre_sent, "tensor", 1)
    made = product(rank_cell[0], act, act_sent, down_matrix, members)
    made, near_act, near_pre = tie(made, near_act, near_pre)
    *expert_far, expert_up_near, expert_down_near = expert_weights(
        [(flat_in, flat_grad, act, grad_pre), (near_rows, near_grads, near_act, near_pre)]
    )
    grad_back, made, expert_far = tie(grad_back, made, expert_far)

    steps = steps_of(members)
    grad_res, sums_second, kept, sent, *grad_heads = turn(
        item_lengths, rank_cell, dispatch, grad_back, residual, cotangent,
        second_gain, all_heads, outputs,
    )
    grad_parts = [grad_heads[0]] + [
        swap(grad_heads[j], "tensor", j) for j in range(1, members)
    ]
    output_near, output_far = output_sums(kept, swap(sent, "tensor", 1), expert_far[0])
    made, grad_heads = tie(made, grad_heads)
    returned = exchange(made)
    grad_parts, output_near, output_far = tie(grad_parts, output_near, output_far)

    bit_cell = (lax.axis_index("dp") & 1).astype(jnp.int32).reshape(1, 1)
    weights = (qw, kw, vw)
    dp_steps = steps_of(sources)
    back = functools.partial(
        attend_back, lens=item_lengths, rank=rank_cell, bit=bit_cell, qt=qt, kt=kt, vt=vt,
        logs=logs, weights=weights, normed=normed_in, outs=own_heads,
    )
    groups = ((0, heads - 1), (heads - 1, 1))
    joint_a, sums_a, own_a, away_a = back(*groups[0], extras=(), grads=grad_parts)
    output_got = swap(output_far, "tensor", 2)
    joint_a, own_a, away_a, output_got, grad_parts, expert_rest, returned = tie(
        joint_a, own_a, away_a, output_got, grad_parts, expert_far[1], returned
    )
    expert_got = swap(expert_rest, "tensor", 2)
    output_sum = add_low(output_near, output_got[: output_near.shape[0]])
    own_a = add_low(own_a, swap(away_a, "dp", 1))
    output_sum = add_low(output_sum, swap(output_sum, "dp", dp_steps[-1]))
    joint_b, unused, own_b, away_b = back(
        *groups[1], extras=(sums_a, sums_second), grads=grad_parts
    )
    joint_b, own_a, own_b, away_b, output_sum = tie(
        joint_b, own_a, own_b, away_b, output_sum
    )

    far_kept, far_sent = input_grad(
        groups, weights, (joint_a, joint_b), far, members - far, shard_rows
    )
    near_kept, near_sent = input_grad(
        groups, weights, (joint_a, joint_b), 0, far, shard_rows
    )
    own_b = add_parts(own_b, swap(away_b, "dp", 1))
    far_kept = add_low(far_kept, swap(far_sent, "tensor", 1))
    far_kept, own_b, output_sum, near_sent = tie(far_kept, own_b, output_sum, near_sent)
    near_core = swap(near_sent, "tensor", 1)
    near_far = swap(far_kept, "tensor", 2)
    for step in dp_steps[1:]:
        own_a = add_low(own_a, swap(own_a, "dp", step))
        own_b = add_parts(own_b, swap(own_b, "dp", step))
        if step == dp_steps[1]:
            own_b, expert_got = tie(own_b, expert_got)
    up_grad, down_grad = expert_sums(
        expert_up_near, expert_down_near, output_got, expert_got
    )
    own_b, up_grad, down_grad, near_far = tie(own_b, up_grad, down_grad, near_far)
    norm_sums = own_b[-SUM_ROWS:].astype(f32)
    norm_sums = norm_sums[: SUM_ROWS // 2] + norm_sums[SUM_ROWS // 2 :]
    for step in steps:
        norm_sums = norm_sums + swap(norm_sums, "tensor", step)
    pieces = (own_a, swap(own_a, "dp", 1), own_b, swap(own_b, "dp", 1))
    token_grad = close(
        rank_cell[0], tokens, first_gain, grad_res, (near_kept, near_core, near_far)
    )
    for step in dp_steps[:-1]:
        output_sum = add_low(output_sum, swap(output_sum, "dp", step))

    block_out = residual + contract_rows(dispatch, returned)
    query_grad, key_grad, value_grad = finish(groups, bit_cell, pieces)
    return (
        block_out,
        token_grad,
        (norm_sums[0] - first_bias * norm_sums[1]) / first_gain,
        norm_sums[1],
        query_grad.T,
        key_grad.T,
        value_grad.T,
        output_sum.astype(f32),
        norm_sums[2],
        norm_sums[3],
        up_grad[None],
        down_grad[None],
    )


def solution(mesh):
    in_specs = (
        P("dp", None),
        P(),
        P(),
        P(None, "tensor"),
        P(None, "tensor"),
        P(None, "tensor"),
        P("tensor", None),
        P(),
        P(),
        P("dp", None, None),
        P("dp", None, None),
        P("dp", None),
        P(("dp", "tensor"), None),
        P(("dp", "tensor"), None),
        P(("dp", "tensor"), None),
    )
    out_specs = (
        P(("dp", "tensor"), None),
        P(("dp", "tensor"), None),
        P(),
        P(),
        P(None, "tensor"),
        P(None, "tensor"),
        P(None, "tensor"),
        P("tensor", None),
        P(),
        P(),
        P("dp", None, "tensor"),
        P("dp", "tensor", None),
    )
    return jax.shard_map(
        on_device, mesh=mesh, in_specs=in_specs, out_specs=out_specs, check_vma=False
    )
```

```python
import functools

import jax
import jax.numpy as jnp
from jax import lax
from jax.experimental import pallas as pl
from jax.experimental.pallas import tpu as pltpu
from jax.sharding import PartitionSpec as P

HEAD_DIM = 64
EPSILON = 1e-05
NEGATIVE = -1e30
f32 = jnp.float32
bf16 = jnp.bfloat16
VMEM = pl.BlockSpec(memory_space=pltpu.VMEM)
SMEM = pl.BlockSpec(memory_space=pltpu.SMEM)
SUM_ROWS = 16
COST = pl.CostEstimate(flops=2**20, bytes_accessed=2**20, transcendentals=0)
LONG = pl.CostEstimate(flops=2**34, bytes_accessed=2**24, transcendentals=0)


def layer_norm(values, gain, shift):
    average = jnp.mean(values, axis=-1, keepdims=True)
    centred = values - average
    variance = jnp.mean(centred * centred, axis=-1, keepdims=True)
    return centred * lax.rsqrt(variance + EPSILON) * gain + shift


def contract_rows(left, right):
    return lax.dot_general(
        left, right, (((0,), (0,)), ((), ())), preferred_element_type=f32
    )


def swap(values, axis, step):
    count = lax.axis_size(axis)
    return lax.ppermute(values, axis, [(i, i ^ step) for i in range(count)])


def steps_of(count):
    steps = []
    step = 1
    while step < count:
        steps.append(step)
        step *= 2
    return steps


def normalized(values):
    average = jnp.mean(values, axis=-1, keepdims=True)
    centred = values - average
    variance = jnp.mean(centred * centred, axis=-1, keepdims=True)
    return centred * lax.rsqrt(variance + EPSILON)


def project_kernel(
    rank_ref, tokens_ref, gain_ref, bias_ref, qw_ref, kw_ref, vw_ref,
    normed_ref, qt_ref, kt_ref, vt_ref,
):
    values = tokens_ref[...].astype(f32)
    normed = (normalized(values) * gain_ref[...][None] + bias_ref[...][None]).astype(bf16)
    normed_ref[...] = normed
    for weight_ref, out_ref, factor in (
        (qw_ref, qt_ref, HEAD_DIM ** (-0.5)), (kw_ref, kt_ref, None), (vw_ref, vt_ref, None)
    ):
        made = lax.dot_general(
            weight_ref[...], normed, (((1,), (1,)), ((), ())), preferred_element_type=f32
        ).astype(bf16)
        if factor is not None:
            made = made * jnp.asarray(factor, bf16)
        out_ref[...] = made


def project(rank, tokens, gain, bias, qw, kw, vw, blocks):
    slots, width = tokens.shape
    cols = qw.shape[0]
    size = slots // blocks
    fixed = lambda i, r: (0, 0)
    line = pl.BlockSpec((width,), lambda i, r: (0,))
    return pl.pallas_call(
        project_kernel,
        grid_spec=pltpu.PrefetchScalarGridSpec(
            num_scalar_prefetch=1,
            grid=(blocks,),
            in_specs=[
                pl.BlockSpec((size, width), lambda i, r: (i ^ r[0], 0)),
                line,
                line,
                pl.BlockSpec((cols, width), fixed),
                pl.BlockSpec((cols, width), fixed),
                pl.BlockSpec((cols, width), fixed),
            ],
            out_specs=(
                pl.BlockSpec((size, width), lambda i, r: (i, 0)),
                pl.BlockSpec((cols, size), lambda i, r: (0, i)),
                pl.BlockSpec((cols, size), lambda i, r: (0, i)),
                pl.BlockSpec((cols, size), lambda i, r: (0, i)),
            ),
        ),
        out_shape=(jax.ShapeDtypeStruct((slots, width), bf16),)
        + (jax.ShapeDtypeStruct((cols, slots), bf16),) * 3,
        name="project",
        compiler_params=pltpu.CompilerParams(vmem_limit_bytes=12 * 2**20),
        cost_estimate=COST,
    )(rank, tokens, gain, bias, qw, kw, vw)


def item_ends(lens_ref):
    ends = []
    total = jnp.int32(0)
    for i in range(lens_ref.shape[1]):
        total = total + lens_ref[0, i]
        ends.append(total)
    return ends


def segments_at(place, ends):
    segment = jnp.zeros_like(place)
    for end in ends:
        segment = segment + (place >= end).astype(jnp.int32)
    return segment


def block_span(first, size, unit, ends):
    last = jnp.minimum(first + size, ends[-1]) - 1
    low = jnp.int32(0)
    high = ends[-1]
    for end in ends:
        low = jnp.where(first >= end, end, low)
    for end in reversed(ends):
        high = jnp.where(last < end, end, high)
    empty = first >= ends[-1]
    low_block = jnp.where(empty, 0, low // unit)
    high_block = jnp.where(empty, 0, (high + unit - 1) // unit)
    return low_block, high_block


def rows_at(block, size):
    return pl.ds(pl.multiple_of(block * size, size), size)


def fill_segments(row_ref, col_ref, shard, rank, ends):
    slots = row_ref.shape[1]
    at = lax.broadcasted_iota(jnp.int32, (1, slots), 1)
    place = ((at // shard) ^ rank) * shard + at % shard
    segments = segments_at(place, ends)
    row_ref[...] = segments
    col_ref[...] = jnp.transpose(jnp.broadcast_to(segments, (128, slots)), (1, 0))


def block_bias(row_ref, col_ref, rows, cols):
    return jnp.where(col_ref[rows, 0:1] == row_ref[:, cols], 0.0, NEGATIVE)


def lane_masked(values, head):
    lane = lax.broadcasted_iota(jnp.int32, values.shape, 1)
    inside = (lane >= head * HEAD_DIM) & (lane < (head + 1) * HEAD_DIM)
    return jnp.where(inside, values, jnp.zeros_like(values))


def forward_kernel(
    first, blocks, lens_ref, rank_ref, qt_ref, kt_ref, vt_ref, *refs
):
    *out_refs, log_ref, masked_ref, out_ref, row_ref, col_ref, score_ref = refs
    count, width, size = out_ref.shape
    heads = width // HEAD_DIM
    shard = size
    rank = rank_ref[0, 0]
    ends = item_ends(lens_ref)
    fill_segments(row_ref, col_ref, shard, rank, ends)
    keys = jnp.transpose(kt_ref[...], (1, 0))
    for h in range(heads):
        masked_ref[h] = lane_masked(keys, h)

    def query_block(b, unused):
        at = first + b
        i = at ^ rank
        cols = rows_at(at, size)
        queries = qt_ref[:, cols]

        def score_block(j, carry):
            rows = rows_at(j ^ rank, shard)
            bias = block_bias(row_ref, col_ref, rows, cols)
            result = []
            for h in range(heads):
                scores = jnp.dot(
                    masked_ref[h, rows, :], queries, preferred_element_type=f32
                )
                scores = scores + bias
                score_ref[h, rows_at(j, shard), :] = scores
                part = jnp.max(scores.reshape(-1, 8, size), axis=0)
                result.append(jnp.maximum(carry[h], part))
            return tuple(result)

        low, high = block_span(i * size, size, shard, ends)
        peaks = lax.fori_loop(
            low, high, score_block, (jnp.full((8, size), NEGATIVE, f32),) * heads
        )
        peaks = [jnp.max(peak, axis=0, keepdims=True) for peak in peaks]

        def key_block(j, carry):
            rows = rows_at(j ^ rank, shard)
            result = []
            for h in range(heads):
                summed, total = carry[h]
                soft = jnp.exp(score_ref[h, rows_at(j, shard), :] - peaks[h])
                summed = summed + jnp.sum(soft.reshape(-1, 8, size), axis=0)
                total = total + jnp.dot(
                    vt_ref[pl.ds(h * HEAD_DIM, HEAD_DIM), rows],
                    soft.astype(bf16),
                    preferred_element_type=f32,
                )
                result.append((summed, total))
            return tuple(result)

        start = ((jnp.zeros((8, size), f32), jnp.zeros((HEAD_DIM, size), f32)),) * heads
        done = lax.fori_loop(low, high, key_block, start)
        live = row_ref[:, cols] < len(ends)
        for h in range(heads):
            summed, total = done[h]
            summed = jnp.sum(summed, axis=0, keepdims=True)
            highest = peaks[h]
            summed = jnp.where(live, summed, 1.0)
            result = jnp.where(live, total / summed, 0.0).astype(bf16)
            logs = jnp.where(live, highest + jnp.log(summed), -NEGATIVE)
            out_ref[b, pl.ds(h * HEAD_DIM, HEAD_DIM), :] = result
            log_ref[h, :, rows_at(b, size)] = logs
        return unused

    lax.fori_loop(0, count, query_block, 0)
    for b in range(count):
        out_refs[b][...] = out_ref[b]


def attend(lens, rank, qt, kt, vt, blocks, first, count):
    width, slots = qt.shape
    size = slots // blocks
    heads = width // HEAD_DIM
    return pl.pallas_call(
        functools.partial(forward_kernel, first, blocks),
        out_shape=(jax.ShapeDtypeStruct((width, size), bf16),) * count
        + (jax.ShapeDtypeStruct((heads, 1, count * size), f32),),
        in_specs=[SMEM, SMEM, VMEM, VMEM, VMEM],
        out_specs=(VMEM,) * (count + 1),
        scratch_shapes=[
            pltpu.VMEM((heads, slots, width), bf16),
            pltpu.VMEM((count, width, size), bf16),
            pltpu.VMEM((1, slots), jnp.int32),
            pltpu.VMEM((slots, 128), jnp.int32),
            pltpu.VMEM((heads, slots, size), f32),
        ],
        name="attend",
        compiler_params=pltpu.CompilerParams(vmem_limit_bytes=26 * 2**20),
        cost_estimate=COST,
    )(lens, rank, qt, kt, vt)


def split_rows(values):
    high = values.astype(bf16)
    return jnp.concatenate([high, (values - high.astype(f32)).astype(bf16)], axis=0)


def add_kernel(a_ref, b_ref, out_ref):
    half = out_ref.shape[0] - SUM_ROWS
    line = SUM_ROWS // 2
    total = a_ref[...].astype(f32) + b_ref[...].astype(f32)
    out_ref[:half, :] = total[:half].astype(bf16)
    out_ref[half:, :] = split_rows(total[half : half + line] + total[half + line :])


def add_parts(a, b):
    return pl.pallas_call(
        add_kernel,
        out_shape=jax.ShapeDtypeStruct(a.shape, bf16),
        in_specs=[VMEM, VMEM],
        out_specs=VMEM,
        name="add_parts",
        compiler_params=pltpu.CompilerParams(vmem_limit_bytes=4 * 2**20),
        cost_estimate=COST,
    )(a, b)


def stacked_parts(first_head, heads, query, key, value):
    dim = HEAD_DIM
    parts = []
    for n in range(heads):
        first = (first_head + n) * dim
        parts += [(2 * n * dim, key, first, dim), ((2 * n + 1) * dim, value, first, dim)]
    return parts + [(2 * heads * dim, query, first_head * dim, heads * dim)]


def backward_kernel(
    first_head, heads, blocks, extras, lens_ref, rank_ref, bit_ref, qt_ref, kt_ref, vt_ref,
    near_ref, far_ref, qw_ref, kw_ref, vw_ref, normed_ref, *rest
):
    extra_refs, rest = rest[:extras], rest[extras:]
    width, slots = qt_ref.shape
    shard = slots // blocks
    dim = HEAD_DIM
    out_refs, grad_refs = rest[:blocks], rest[blocks : 2 * blocks]
    joint_ref, sums_ref, own_ref, away_ref = rest[2 * blocks : 2 * blocks + 4]
    kv_ref, q0_ref, og_ref, right_ref, inner_ref, dq_ref, made_ref = rest[-13:-6]
    log_ref = rest[-6]
    row_ref, col_ref = rest[-5:-3]
    turned_ref, rows_ref, copied = rest[-3:]
    fetch = pltpu.make_async_copy(normed_ref, rows_ref, copied)
    fetch.start()
    unit = shard // 2
    rank = rank_ref[0, 0]
    ends = item_ends(lens_ref)
    fill_segments(row_ref, col_ref, shard, rank, ends)
    near = near_ref.shape[2]
    log_ref[:, :, :near] = near_ref[...]
    log_ref[:, :, near:] = far_ref[...]
    zero = jnp.zeros((dim, slots), bf16)
    for n in range(heads):
        part = slice((first_head + n) * dim, (first_head + n + 1) * dim)
        both = jnp.concatenate([kt_ref[part, :], vt_ref[part, :]], axis=0)
        kv_ref[n] = jnp.transpose(both, (1, 0))
        padded = jnp.concatenate([qt_ref[part, :], zero], axis=0)
        q0_ref[n] = jnp.transpose(padded, (1, 0))
        right_ref[n, 0] = padded
        for b in range(blocks):
            grad = grad_refs[b][part, :]
            cols = slice(b * shard, (b + 1) * shard)
            padded = jnp.concatenate([zero[:, :shard], grad], axis=0)
            og_ref[n, cols, :] = jnp.transpose(padded, (1, 0))
            right_ref[n, 1, :, cols] = padded
            inner_ref[n, :, cols] = jnp.sum(
                out_refs[b][part, :].astype(f32) * grad.astype(f32), axis=0, keepdims=True
            )
    dq_ref[...] = jnp.zeros_like(dq_ref)

    def key_block(j, unused):
        at_key = ((j // 2) ^ rank) * 2 + j % 2
        rows = rows_at(at_key, unit)

        def query_block(i, totals):
            at = i ^ rank
            cols = rows_at(at, shard)
            same = col_ref[rows, 0:1] == row_ref[:, cols]
            result = []
            for n in range(heads):
                head = first_head + n
                kv = kv_ref[n, rows, :]
                scores = jnp.dot(kv, right_ref[n, 0, :, cols], preferred_element_type=f32)
                grad_soft = jnp.dot(kv, right_ref[n, 1, :, cols], preferred_element_type=f32)
                soft = jnp.where(same, jnp.exp(scores - log_ref[head, :, cols]), 0.0)
                grad_scores = (soft * (grad_soft - inner_ref[n, :, cols])).astype(bf16)
                total = totals[n] + jnp.dot(
                    soft.astype(bf16), og_ref[n, cols, :], preferred_element_type=f32
                )
                total = total + jnp.dot(
                    grad_scores, q0_ref[n, cols, :], preferred_element_type=f32
                )
                dq_ref[n, :, cols] += jnp.dot(
                    kt_ref[pl.ds(head * dim, dim), rows], grad_scores,
                    preferred_element_type=f32,
                )
                result.append(total)
            return tuple(result)

        low, high = block_span(j * unit, unit, shard, ends)
        start = (jnp.zeros((unit, 2 * dim), f32),) * heads
        totals = lax.fori_loop(low, high, query_block, start)
        for n in range(heads):
            part = slice(2 * dim * n, 2 * dim * (n + 1))
            total = totals[n].astype(bf16)
            joint_ref[rows, part] = total
            turned_ref[part, rows] = jnp.transpose(total, (1, 0))
        return unused

    lax.fori_loop(0, 2 * blocks, key_block, 0)
    dq = (dq_ref[...] * dim ** (-0.5)).astype(bf16).reshape(heads * dim, slots)
    turned_ref[2 * dim * heads :, :] = dq
    joint_ref[:, 2 * dim * heads :] = jnp.transpose(dq, (1, 0))
    fetch.wait()
    made_ref[...] = jnp.dot(turned_ref[...], rows_ref[...], preferred_element_type=f32)
    gains = jnp.zeros((1, rows_ref.shape[1]), f32)
    shifts = jnp.zeros((1, rows_ref.shape[1]), f32)
    for at, weight_ref, first, size in stacked_parts(
        first_head, heads, qw_ref, kw_ref, vw_ref
    ):
        weight = weight_ref[first : first + size, :].astype(f32)
        gains += jnp.sum(weight * made_ref[at : at + size, :], axis=0, keepdims=True)
        total = jnp.sum(turned_ref[at : at + size, :].astype(f32), axis=1, keepdims=True)
        shifts += jnp.sum(weight * total, axis=0, keepdims=True)
    sums_ref[0:1] = gains
    sums_ref[1:2] = shifts
    half = made_ref.shape[0] // 2
    bit = bit_ref[0, 0]
    for part_ref, at in ((own_ref, bit), (away_ref, 1 - bit)):
        part_ref[0:half, :] = made_ref[rows_at(at, half), :].astype(bf16)
        if extras:
            lines = [sums_ref[...] + extra_refs[0][...], extra_refs[1][...]]
            lines.append(jnp.zeros((SUM_ROWS // 2 - 4, gains.shape[1]), f32))
            part_ref[half:, :] = split_rows(jnp.concatenate(lines, axis=0))


def attend_back(
    first_head, heads, extras, lens, rank, bit, qt, kt, vt, logs, weights, normed, outs, grads
):
    slots, width = normed.shape
    blocks = len(outs)
    dim = HEAD_DIM
    cols = 3 * dim * heads
    rows = cols // 2 + (SUM_ROWS if extras else 0)
    return pl.pallas_call(
        functools.partial(backward_kernel, first_head, heads, blocks, len(extras)),
        out_shape=(
            jax.ShapeDtypeStruct((slots, cols), bf16),
            jax.ShapeDtypeStruct((2, width), f32),
        )
        + (jax.ShapeDtypeStruct((rows, width), bf16),) * 2,
        in_specs=[SMEM, SMEM, SMEM]
        + [VMEM] * 8
        + [pl.BlockSpec(memory_space=pl.ANY)]
        + [VMEM] * (len(extras) + 2 * blocks),
        out_specs=(VMEM,) * 4,
        scratch_shapes=[pltpu.VMEM((heads, slots, 2 * dim), bf16)] * 3
        + [
            pltpu.VMEM((heads, 2, 2 * dim, slots), bf16),
            pltpu.VMEM((heads, 1, slots), f32),
            pltpu.VMEM((heads, dim, slots), f32),
            pltpu.VMEM((cols, width), f32),
            pltpu.VMEM((qt.shape[0] // dim, 1, slots), f32),
            pltpu.VMEM((1, slots), jnp.int32),
            pltpu.VMEM((slots, 128), jnp.int32),
            pltpu.VMEM((cols, slots), bf16),
            pltpu.VMEM((slots, width), bf16),
            pltpu.SemaphoreType.DMA,
        ],
        name="attend_back",
        compiler_params=pltpu.CompilerParams(vmem_limit_bytes=28 * 2**20),
        cost_estimate=COST,
    )(lens, rank, bit, qt, kt, vt, *logs, *weights, normed, *extras, *outs, *grads)


def plan_kernel(capacity, lens_ref, rank_ref, routes_ref, order_ref, grad_ref,
                dispatch_ref, slots_ref):
    shard = routes_ref.shape[1]
    first = rank_ref[0, 0] * shard
    ends = item_ends(lens_ref)
    chosen_row = routes_ref[...]
    chosen_col = jnp.transpose(jnp.broadcast_to(chosen_row, (128, shard)), (1, 0))[:, 0:1]
    order_row = order_ref[...]
    order_col = jnp.transpose(jnp.broadcast_to(order_row, (128, shard)), (1, 0))[:, 0:1]
    alive_row = segments_at(
        first + lax.broadcasted_iota(jnp.int32, (1, shard), 1), ends
    ) < len(ends)
    alive_col = segments_at(
        first + lax.broadcasted_iota(jnp.int32, (shard, 1), 0), ends
    ) < len(ends)
    ahead = (chosen_col == chosen_row) & (order_col < order_row) & alive_col
    ranked = jnp.sum(ahead.astype(jnp.int32), axis=0, keepdims=True)
    kept = alive_row & (ranked < capacity)
    slot = jnp.where(kept, chosen_row * capacity + ranked, -1)
    dispatch = (
        lax.broadcasted_iota(jnp.int32, dispatch_ref.shape, 0) == slot
    ).astype(f32).astype(bf16)
    dispatch_ref[...] = dispatch
    slots_ref[...] = jnp.dot(
        dispatch, grad_ref[...], preferred_element_type=f32
    ).astype(bf16)


def plan(lens, rank, routes, order, grads, capacity, experts_all):
    shard, width = grads.shape
    count = experts_all * capacity
    return pl.pallas_call(
        functools.partial(plan_kernel, capacity),
        out_shape=(
            jax.ShapeDtypeStruct((count, shard), bf16),
            jax.ShapeDtypeStruct((count, width), bf16),
        ),
        in_specs=[SMEM, SMEM, VMEM, VMEM, VMEM],
        out_specs=(VMEM, VMEM),
        name="plan",
        compiler_params=pltpu.CompilerParams(vmem_limit_bytes=6 * 2**20),
        cost_estimate=COST,
    )(lens, rank, routes.reshape(1, -1), order, grads)


def across(left, right):
    return lax.dot_general(
        left, right, (((1,), (1,)), ((), ())), preferred_element_type=f32
    )


def middle_kernel(count, rank_ref, tokens_ref, gain_ref, bias_ref, dispatch_ref, *refs):
    head_refs, weight_refs = refs[:count], refs[count : 2 * count]
    residual_ref, rows_ref = refs[2 * count :]
    residual = tokens_ref[...].astype(f32)
    for head_ref, weight_ref in zip(head_refs, weight_refs):
        residual = residual + contract_rows(head_ref[...], weight_ref[...])
    residual_ref[...] = residual
    normed = (normalized(residual) * gain_ref[...][None] + bias_ref[...][None]).astype(bf16)
    rows_ref[...] = jnp.dot(
        dispatch_ref[...], normed, preferred_element_type=f32
    ).astype(bf16)


def middle(rank, tokens, gain, bias, dispatch, heads, weights):
    count, shard = dispatch.shape
    width = tokens.shape[1]
    fixed = lambda array: pl.BlockSpec(array.shape, lambda i, r: (0,) * array.ndim)
    small = [gain, bias, dispatch, *heads, *weights]
    return pl.pallas_call(
        functools.partial(middle_kernel, len(heads)),
        grid_spec=pltpu.PrefetchScalarGridSpec(
            num_scalar_prefetch=1,
            grid=(1,),
            in_specs=[pl.BlockSpec((shard, width), lambda i, r: (r[0], 0))]
            + [fixed(array) for array in small],
            out_specs=(
                pl.BlockSpec((shard, width), lambda i, r: (0, 0)),
                pl.BlockSpec((count, width), lambda i, r: (0, 0)),
            ),
        ),
        out_shape=(
            jax.ShapeDtypeStruct((shard, width), f32),
            jax.ShapeDtypeStruct((count, width), bf16),
        ),
        name="middle",
        compiler_params=pltpu.CompilerParams(vmem_limit_bytes=10 * 2**20),
        cost_estimate=COST,
    )(rank, tokens, *small)


def turn_kernel(
    count, lens_ref, rank_ref, dispatch_ref, back_ref, residual_ref, cotangent_ref,
    gain_ref, *refs
):
    head_refs, weight_refs = refs[:count], refs[count : 2 * count]
    grad_ref, sums_ref, kept_ref, sent_ref = refs[2 * count : 2 * count + 4]
    part_refs = refs[2 * count + 4 :]
    shard = residual_ref.shape[0]
    grad_normed = contract_rows(dispatch_ref[...], back_ref[...])
    values = residual_ref[...]
    centred = values - jnp.mean(values, axis=-1, keepdims=True)
    inverse = lax.rsqrt(jnp.mean(centred * centred, axis=-1, keepdims=True) + EPSILON)
    normed = centred * inverse
    sums_ref[0:1] = jnp.sum(grad_normed * normed, axis=0, keepdims=True)
    sums_ref[1:2] = jnp.sum(grad_normed, axis=0, keepdims=True)
    scaled = grad_normed * gain_ref[...][None]
    grad = cotangent_ref[...].astype(f32) + inverse * (
        scaled
        - jnp.mean(scaled, axis=-1, keepdims=True)
        - normed * jnp.mean(scaled * normed, axis=-1, keepdims=True)
    )
    grad_ref[...] = grad
    low = grad.astype(bf16)
    place = rank_ref[0, 0] * shard + lax.broadcasted_iota(jnp.int32, (1, shard), 1)
    alive = place < item_ends(lens_ref)[-1]
    for weight_ref, part_ref in zip(weight_refs, part_refs):
        part_ref[...] = jnp.where(alive, across(weight_ref[...], low), 0.0).astype(bf16)
    for j, head_ref in enumerate(head_refs):
        made = jnp.dot(head_ref[...], low, preferred_element_type=f32)
        (kept_ref, sent_ref)[j % 2][j // 2] = made.astype(bf16)


def turn(lens, rank, dispatch, back, residual, cotangent, gain, heads, weights):
    shard, width = residual.shape
    cols = weights[0].shape[0]
    count = len(weights)
    return pl.pallas_call(
        functools.partial(turn_kernel, count),
        out_shape=(
            jax.ShapeDtypeStruct((shard, width), f32),
            jax.ShapeDtypeStruct((2, width), f32),
            jax.ShapeDtypeStruct((count // 2, cols, width), bf16),
            jax.ShapeDtypeStruct((count // 2, cols, width), bf16),
        )
        + (jax.ShapeDtypeStruct((cols, shard), bf16),) * count,
        in_specs=[SMEM, SMEM] + [VMEM] * (5 + 2 * count),
        out_specs=(VMEM,) * (4 + count),
        name="turn",
        compiler_params=pltpu.CompilerParams(vmem_limit_bytes=16 * 2**20),
        cost_estimate=COST,
    )(lens, rank, dispatch, back, residual, cotangent, gain, *heads, *weights)


def output_sum_kernel(kept_ref, core_ref, first_ref, near_ref, far_ref):
    cols = near_ref.shape[0]
    total = [
        (kept_ref[j].astype(f32) + core_ref[j].astype(f32)).astype(bf16) for j in range(2)
    ]
    near_ref[...] = total[0]
    far_ref[:cols, :] = total[1]
    far_ref[cols:, :] = first_ref[...]


def output_sums(kept, core, first):
    slots, cols, width = kept.shape
    return pl.pallas_call(
        output_sum_kernel,
        out_shape=(
            jax.ShapeDtypeStruct((cols, width), bf16),
            jax.ShapeDtypeStruct((cols + first.shape[0], width), bf16),
        ),
        in_specs=[VMEM] * 3,
        out_specs=(VMEM, VMEM),
        name="output_sums",
        compiler_params=pltpu.CompilerParams(vmem_limit_bytes=6 * 2**20),
        cost_estimate=LONG,
    )(kept, core, first)


def gelu_parts(values):
    below = 0.5 + 0.5 * lax.erf(values * (0.5**0.5))
    density = jnp.exp(-0.5 * values * values) * (0.5 / jnp.pi) ** 0.5
    return values * below, below + values * density


def part_at(step, parts, rank):
    half = parts // 2
    return (2 * (step % half) + step // half) ^ rank


def expert_kernel(
    rank_ref, in_ref, grad_act_ref, up_ref,
    act_kept_ref, pre_kept_ref, act_sent_ref, pre_sent_ref, mid_ref, sum_ref,
):
    step = pl.program_id(0)
    pre = jnp.dot(in_ref[...], up_ref[...], preferred_element_type=f32)
    act, slope = gelu_parts(pre)
    act = act.astype(bf16)
    grad_pre = (grad_act_ref[...] * slope).astype(bf16)
    half = pl.num_programs(0) // 2

    @pl.when(step < half)
    def keep():
        act_kept_ref[...] = act
        pre_kept_ref[...] = grad_pre

    @pl.when(step >= half)
    def send():
        act_sent_ref[...] = act
        pre_sent_ref[...] = grad_pre

    mid = across(grad_pre, up_ref[...])

    @pl.when(step == 0)
    def first():
        sum_ref[...] = mid

    @pl.when(step > 0)
    def later():
        sum_ref[...] += mid

    @pl.when(step == pl.num_programs(0) - 1)
    def last():
        mid_ref[...] = sum_ref[...].astype(bf16)


def expert(rank, rows, grad_act, up, parts):
    count, width = rows.shape
    hidden = up.shape[1]
    size = min(768, hidden // parts)
    cuts = hidden // parts // size
    steps = parts * cuts
    column = lambda i, r: (0, part_at(i // cuts, parts, r[0]) * cuts + i % cuts)
    kept = pl.BlockSpec((count, size), lambda i, r: (0, jnp.minimum(i, steps // 2 - 1)))
    sent = pl.BlockSpec((count, size), lambda i, r: (0, jnp.maximum(i - steps // 2, 0)))
    fixed = pl.BlockSpec((count, width), lambda i, r: (0, 0))
    return pl.pallas_call(
        expert_kernel,
        grid_spec=pltpu.PrefetchScalarGridSpec(
            num_scalar_prefetch=1,
            grid=(steps,),
            in_specs=[
                fixed,
                pl.BlockSpec((count, size), column),
                pl.BlockSpec((width, size), column),
            ],
            out_specs=(kept, kept, sent, sent, fixed),
            scratch_shapes=[pltpu.VMEM((count, width), f32)],
        ),
        out_shape=(jax.ShapeDtypeStruct((count, hidden // 2), bf16),) * 4
        + (jax.ShapeDtypeStruct((count, width), bf16),),
        name="expert",
        compiler_params=pltpu.CompilerParams(vmem_limit_bytes=40 * 2**20),
        cost_estimate=COST,
    )(rank, rows, grad_act, up)


def product_kernel(rank_ref, kept_ref, sent_ref, down_ref, out_ref, sum_ref):
    step = pl.program_id(0)
    steps = pl.num_programs(0)
    act = jnp.where(step < steps // 2, kept_ref[...], sent_ref[...])
    made = jnp.dot(act, down_ref[...], preferred_element_type=f32)

    @pl.when(step == 0)
    def first():
        sum_ref[...] = made

    @pl.when(step > 0)
    def later():
        sum_ref[...] += made

    @pl.when(step == steps - 1)
    def last():
        out_ref[...] = sum_ref[...].astype(bf16)


def product(rank, kept, sent, down, parts):
    count = kept.shape[0]
    hidden, width = down.shape
    size = hidden // parts
    return pl.pallas_call(
        product_kernel,
        grid_spec=pltpu.PrefetchScalarGridSpec(
            num_scalar_prefetch=1,
            grid=(parts,),
            in_specs=[
                pl.BlockSpec((count, size), lambda i, r: (0, jnp.minimum(i, parts // 2 - 1))),
                pl.BlockSpec((count, size), lambda i, r: (0, jnp.maximum(i - parts // 2, 0))),
                pl.BlockSpec((size, width), lambda i, r: (part_at(i, parts, r[0]), 0)),
            ],
            out_specs=pl.BlockSpec((count, width), lambda i, r: (0, 0)),
            scratch_shapes=[pltpu.VMEM((count, width), f32)],
        ),
        out_shape=jax.ShapeDtypeStruct((count, width), bf16),
        name="product",
        compiler_params=pltpu.CompilerParams(vmem_limit_bytes=14 * 2**20),
        cost_estimate=COST,
    )(rank, kept, sent, down)


def weight_kernel(groups, *refs):
    first_ref, rest_ref, up_ref, down_ref = refs[-4:]
    dup = ddown = 0.0
    for g in range(groups):
        in_ref, grad_ref, act_ref, pre_ref = refs[4 * g : 4 * g + 4]
        dup = dup + contract_rows(in_ref[...], pre_ref[...])
        ddown = ddown + contract_rows(act_ref[...], grad_ref[...])
    cut = first_ref.shape[0]

    @pl.when(pl.program_id(0) == 0)
    def far():
        first_ref[...] = dup[:cut].astype(bf16)
        rest_ref[: dup.shape[0] - cut, :] = dup[cut:].astype(bf16)
        rest_ref[dup.shape[0] - cut :, :] = ddown.astype(bf16)

    @pl.when(pl.program_id(0) == 1)
    def near():
        up_ref[...] = dup
        down_ref[...] = ddown


def expert_weights(groups):
    count, width = groups[0][0].shape
    size = groups[0][2].shape[1] // 2
    fixed = pl.BlockSpec((count, width), lambda i: (0, 0))
    columns = pl.BlockSpec((count, size), lambda i: (0, 1 - i))
    cut = (width + size) // 4
    shapes = ((cut, size), (width + size - cut, size), (width, size), (size, width))
    return pl.pallas_call(
        functools.partial(weight_kernel, len(groups)),
        grid=(2,),
        in_specs=[fixed, fixed, columns, columns] * len(groups),
        out_specs=tuple(pl.BlockSpec(shape, lambda i: (0, 0)) for shape in shapes),
        out_shape=tuple(
            jax.ShapeDtypeStruct(shape, bf16 if k < 2 else f32)
            for k, shape in enumerate(shapes)
        ),
        name="expert_weights",
        compiler_params=pltpu.CompilerParams(vmem_limit_bytes=28 * 2**20),
        cost_estimate=COST,
    )(*[values for group in groups for values in group])


def expert_sum_kernel(near_up_ref, near_down_ref, first_ref, rest_ref, up_ref, down_ref):
    step = pl.program_id(0)
    half = pl.num_programs(0) // 2
    far = jnp.where(step < half // 2, first_ref[...], rest_ref[...]).astype(f32)

    @pl.when(step < half)
    def upper():
        up_ref[...] = near_up_ref[...] + far

    @pl.when(step >= half)
    def lower():
        down_ref[...] = near_down_ref[...] + far


def expert_sums(near_up, near_down, first, rest):
    count, width = near_up.shape
    steps = 8
    half = steps // 2
    size = count // half
    head = steps // 4
    skip = first.shape[0] // size - head
    block = lambda place: pl.BlockSpec((size, width), lambda i: (place(i), 0))
    upper = block(lambda i: jnp.minimum(i, half - 1))
    lower = block(lambda i: jnp.maximum(i - half, 0))
    return pl.pallas_call(
        expert_sum_kernel,
        grid=(steps,),
        out_shape=(jax.ShapeDtypeStruct((count, width), f32),) * 2,
        in_specs=[
            upper,
            lower,
            block(lambda i: jnp.minimum(i, head - 1) + skip),
            block(lambda i: jnp.maximum(i - head, 0)),
        ],
        out_specs=(upper, lower),
        name="expert_sums",
        compiler_params=pltpu.CompilerParams(vmem_limit_bytes=10 * 2**20),
        cost_estimate=COST,
    )(near_up, near_down, first, rest)


def input_grad_kernel(groups, qw_ref, kw_ref, vw_ref, *refs):
    joint_refs = refs[: len(groups)]
    kept_ref, sent_ref, turned_ref = refs[len(groups) :]
    step = pl.program_id(0)

    @pl.when(step == 0)
    def stack():
        start = 0
        for first_head, heads in groups:
            for at, weight_ref, first, size in stacked_parts(
                first_head, heads, qw_ref, kw_ref, vw_ref
            ):
                turned_ref[start + at : start + at + size, :] = weight_ref[
                    first : first + size, :
                ]
            start += 3 * heads * HEAD_DIM

    total = 0.0
    at = 0
    for joint_ref in joint_refs:
        rows = slice(at, at + joint_ref.shape[1])
        total = total + jnp.dot(
            joint_ref[...], turned_ref[rows, :], preferred_element_type=f32
        )
        at += joint_ref.shape[1]

    @pl.when(step % 2 == 0)
    def keep():
        kept_ref[0] = total.astype(bf16)

    @pl.when(step % 2 == 1)
    def send():
        sent_ref[0] = total.astype(bf16)


def input_grad(groups, weights, joints, first, count, size):
    cols, width = weights[0].shape
    fixed = pl.BlockSpec((cols, width), lambda i: (0, 0))
    return pl.pallas_call(
        functools.partial(input_grad_kernel, groups),
        grid=(count,),
        out_shape=(jax.ShapeDtypeStruct((count // 2, size, width), bf16),) * 2,
        in_specs=[fixed] * 3
        + [
            pl.BlockSpec((size, joint.shape[1]), lambda i: (first + i, 0))
            for joint in joints
        ],
        out_specs=(pl.BlockSpec((1, size, width), lambda i: (i // 2, 0, 0)),) * 2,
        scratch_shapes=[pltpu.VMEM((3 * cols, width), bf16)],
        name="input_grad",
        compiler_params=pltpu.CompilerParams(vmem_limit_bytes=12 * 2**20),
        cost_estimate=COST,
    )(*weights, *joints)


def close_kernel(rank_ref, tokens_ref, gain_ref, grad_ref, *refs):
    *part_refs, out_ref = refs
    grad_in = 0.0
    for part_ref in part_refs:
        grad_in = grad_in + part_ref[...].reshape(out_ref.shape).astype(f32)
    values = tokens_ref[...].astype(f32)
    centred = values - jnp.mean(values, axis=-1, keepdims=True)
    inverse = lax.rsqrt(jnp.mean(centred * centred, axis=-1, keepdims=True) + EPSILON)
    normed = centred * inverse
    scaled = grad_in * gain_ref[...][None]
    out_ref[...] = grad_ref[...] + inverse * (
        scaled
        - jnp.mean(scaled, axis=-1, keepdims=True)
        - normed * jnp.mean(scaled * normed, axis=-1, keepdims=True)
    )


def close(rank, tokens, gain, grad, parts):
    shard, width = grad.shape
    size = shard // 2
    rows = lambda i, r: (i, 0)
    return pl.pallas_call(
        close_kernel,
        grid_spec=pltpu.PrefetchScalarGridSpec(
            num_scalar_prefetch=1,
            grid=(2,),
            in_specs=[
                pl.BlockSpec((size, width), lambda i, r: (2 * r[0] + i, 0)),
                pl.BlockSpec((width,), lambda i, r: (0,)),
                pl.BlockSpec((size, width), rows),
            ]
            + [pl.BlockSpec((1, size, width), lambda i, r: (0, i, 0))] * len(parts),
            out_specs=pl.BlockSpec((size, width), rows),
        ),
        out_shape=jax.ShapeDtypeStruct((shard, width), f32),
        name="close",
        compiler_params=pltpu.CompilerParams(vmem_limit_bytes=12 * 2**20),
        cost_estimate=COST,
    )(rank, tokens, gain, grad, *parts)


def add_low(a, b):
    return (a.astype(f32) + b.astype(f32)).astype(bf16)


def tie(*values):
    return lax.optimization_barrier(values)


def finish_kernel(groups, bit_ref, *refs):
    pieces, refs = refs[: 2 * len(groups)], refs[2 * len(groups) :]
    query_ref, key_ref, value_ref = refs[:3]
    bit = bit_ref[0, 0]
    for g, ((first_head, heads), whole_ref) in enumerate(zip(groups, refs[3:])):
        half = whole_ref.shape[0] // 2
        for piece_ref, at in ((pieces[2 * g], bit), (pieces[2 * g + 1], 1 - bit)):
            whole_ref[rows_at(at, half), :] = piece_ref[0:half, :].astype(f32)
        for at, target_ref, first, size in stacked_parts(
            first_head, heads, query_ref, key_ref, value_ref
        ):
            target_ref[first : first + size, :] = whole_ref[at : at + size, :]


def finish(groups, bit, pieces):
    width = pieces[0].shape[1]
    cols = sum(heads for first_head, heads in groups) * HEAD_DIM
    return pl.pallas_call(
        functools.partial(finish_kernel, groups),
        out_shape=(jax.ShapeDtypeStruct((cols, width), f32),) * 3,
        in_specs=[SMEM] + [VMEM] * len(pieces),
        out_specs=(VMEM,) * 3,
        scratch_shapes=[
            pltpu.VMEM((3 * heads * HEAD_DIM, width), f32) for first_head, heads in groups
        ],
        name="finish",
        compiler_params=pltpu.CompilerParams(vmem_limit_bytes=8 * 2**20),
        cost_estimate=COST,
    )(bit, *pieces)


def on_device(
    tokens,
    first_gain,
    first_bias,
    query_weight,
    key_weight,
    value_weight,
    output_weight,
    second_gain,
    second_bias,
    expert_up,
    expert_down,
    item_lengths,
    routes,
    slot_order,
    cotangent,
):
    slots_all, width = tokens.shape
    members = lax.axis_size("tensor")
    shard_rows = slots_all // members
    rank = lax.axis_index("tensor")
    sources = lax.axis_size("dp")
    experts_all = sources * expert_up.shape[0]
    capacity = shard_rows // experts_all
    head_cols = query_weight.shape[1]
    heads = head_cols // HEAD_DIM
    up_matrix = expert_up[0]
    down_matrix = expert_down[0]
    rank_cell = rank.astype(jnp.int32).reshape(1, 1)

    def exchange(rows):
        return lax.all_to_all(
            rows.reshape(sources, -1, width), "dp", split_axis=0, concat_axis=0, tiled=True
        ).reshape(-1, width)

    qw, kw, vw = query_weight.T, key_weight.T, value_weight.T

    dispatch, grad_slots = plan(
        item_lengths, rank_cell, routes, slot_order, cotangent, capacity, experts_all
    )
    flat_grad = exchange(grad_slots)
    tokens, grad_slots = tie(tokens, grad_slots)
    normed_in, qt, kt, vt = project(
        rank_cell[0], tokens, first_gain, first_bias, qw, kw, vw, members
    )
    outputs = [output_weight] + [
        swap(output_weight, "tensor", k) for k in range(1, members)
    ]
    far = members // 2
    *far_heads, far_logs = attend(
        item_lengths, rank_cell, qt, kt, vt, members, far, members - far
    )
    far_heads, kt = tie(far_heads, kt)
    far_arrived = [swap(far_heads[j - far], "tensor", j) for j in range(far, members)]
    *near_heads, near_logs = attend(item_lengths, rank_cell, qt, kt, vt, members, 0, far)
    near_heads, far_arrived, outputs = tie(near_heads, far_arrived, outputs)
    own_heads = near_heads + far_heads
    logs = (near_logs, far_logs)
    all_heads = (
        near_heads[:1]
        + [swap(near_heads[j], "tensor", j) for j in range(1, far)]
        + far_arrived
    )
    residual, outgoing = middle(
        rank_cell[0], tokens, second_gain, second_bias, dispatch, all_heads, outputs
    )
    flat_in = exchange(outgoing)

    flat_grad, outgoing = tie(flat_grad, outgoing)
    grad_act = across(flat_grad, down_matrix)
    near_grads = swap(flat_grad, "tensor", 1)
    flat_in, grad_act, near_grads = tie(flat_in, grad_act, near_grads)
    near_rows = swap(flat_in, "tensor", 1)
    act, grad_pre, act_sent, pre_sent, grad_mid = expert(
        rank_cell[0], flat_in, grad_act, up_matrix, members
    )
    grad_mid, act, near_rows = tie(grad_mid, act, near_rows)
    grad_back = exchange(grad_mid)

    act, act_sent, pre_sent, grad_mid = tie(act, act_sent, pre_sent, grad_mid)
    near_act = swap(act_sent, "tensor", 1)
    near_pre = swap(pre_sent, "tensor", 1)
    made = product(rank_cell[0], act, act_sent, down_matrix, members)
    made, near_act, near_pre = tie(made, near_act, near_pre)
    *expert_far, expert_up_near, expert_down_near = expert_weights(
        [(flat_in, flat_grad, act, grad_pre), (near_rows, near_grads, near_act, near_pre)]
    )
    grad_back, made, expert_far = tie(grad_back, made, expert_far)

    steps = steps_of(members)
    grad_res, sums_second, kept, sent, *grad_heads = turn(
        item_lengths, rank_cell, dispatch, grad_back, residual, cotangent,
        second_gain, all_heads, outputs,
    )
    grad_parts = [grad_heads[0]] + [
        swap(grad_heads[j], "tensor", j) for j in range(1, members)
    ]
    output_near, output_far = output_sums(kept, swap(sent, "tensor", 1), expert_far[0])
    made, grad_heads = tie(made, grad_heads)
    returned = exchange(made)
    grad_parts, output_near, output_far = tie(grad_parts, output_near, output_far)

    bit_cell = (lax.axis_index("dp") & 1).astype(jnp.int32).reshape(1, 1)
    weights = (qw, kw, vw)
    dp_steps = steps_of(sources)
    back = functools.partial(
        attend_back, lens=item_lengths, rank=rank_cell, bit=bit_cell, qt=qt, kt=kt, vt=vt,
        logs=logs, weights=weights, normed=normed_in, outs=own_heads,
    )
    groups = ((0, heads - 1), (heads - 1, 1))
    joint_a, sums_a, own_a, away_a = back(*groups[0], extras=(), grads=grad_parts)
    output_got = swap(output_far, "tensor", 2)
    joint_a, own_a, away_a, output_got, grad_parts, expert_rest, returned = tie(
        joint_a, own_a, away_a, output_got, grad_parts, expert_far[1], returned
    )
    expert_got = swap(expert_rest, "tensor", 2)
    output_sum = add_low(output_near, output_got[: output_near.shape[0]])
    own_a = add_low(own_a, swap(away_a, "dp", 1))
    output_sum = add_low(output_sum, swap(output_sum, "dp", dp_steps[-1]))
    joint_b, unused, own_b, away_b = back(
        *groups[1], extras=(sums_a, sums_second), grads=grad_parts
    )
    joint_b, own_a, own_b, away_b, output_sum = tie(
        joint_b, own_a, own_b, away_b, output_sum
    )

    far_kept, far_sent = input_grad(
        groups, weights, (joint_a, joint_b), far, members - far, shard_rows
    )
    near_kept, near_sent = input_grad(
        groups, weights, (joint_a, joint_b), 0, far, shard_rows
    )
    own_b = add_parts(own_b, swap(away_b, "dp", 1))
    far_kept = add_low(far_kept, swap(far_sent, "tensor", 1))
    far_kept, own_b, output_sum, near_sent = tie(far_kept, own_b, output_sum, near_sent)
    near_core = swap(near_sent, "tensor", 1)
    near_far = swap(far_kept, "tensor", 2)
    for step in dp_steps[1:]:
        own_a = add_low(own_a, swap(own_a, "dp", step))
        own_b = add_parts(own_b, swap(own_b, "dp", step))
        if step == dp_steps[1]:
            own_b, expert_got = tie(own_b, expert_got)
    up_grad, down_grad = expert_sums(
        expert_up_near, expert_down_near, output_got, expert_got
    )
    own_b, up_grad, down_grad, near_far = tie(own_b, up_grad, down_grad, near_far)
    norm_sums = own_b[-SUM_ROWS:].astype(f32)
    norm_sums = norm_sums[: SUM_ROWS // 2] + norm_sums[SUM_ROWS // 2 :]
    for step in steps:
        norm_sums = norm_sums + swap(norm_sums, "tensor", step)
    pieces = (own_a, swap(own_a, "dp", 1), own_b, swap(own_b, "dp", 1))
    token_grad = close(
        rank_cell[0], tokens, first_gain, grad_res, (near_kept, near_core, near_far)
    )
    for step in dp_steps[:-1]:
        output_sum = add_low(output_sum, swap(output_sum, "dp", step))

    block_out = residual + contract_rows(dispatch, returned)
    query_grad, key_grad, value_grad = finish(groups, bit_cell, pieces)
    return (
        block_out,
        token_grad,
        (norm_sums[0] - first_bias * norm_sums[1]) / first_gain,
        norm_sums[1],
        query_grad.T,
        key_grad.T,
        value_grad.T,
        output_sum.astype(f32),
        norm_sums[2],
        norm_sums[3],
        up_grad[None],
        down_grad[None],
    )


def solution(mesh):
    in_specs = (
        P("dp", None),
        P(),
        P(),
        P(None, "tensor"),
        P(None, "tensor"),
        P(None, "tensor"),
        P("tensor", None),
        P(),
        P(),
        P("dp", None, None),
        P("dp", None, None),
        P("dp", None),
        P(("dp", "tensor"), None),
        P(("dp", "tensor"), None),
        P(("dp", "tensor"), None),
    )
    out_specs = (
        P(("dp", "tensor"), None),
        P(("dp", "tensor"), None),
        P(),
        P(),
        P(None, "tensor"),
        P(None, "tensor"),
        P(None, "tensor"),
        P("tensor", None),
        P(),
        P(),
        P("dp", None, "tensor"),
        P("dp", "tensor", None),
    )
    return jax.shard_map(
        on_device, mesh=mesh, in_specs=in_specs, out_specs=out_specs, check_vma=False
    )
```

```python
import functools

import jax
import jax.numpy as jnp
from jax import lax
from jax.experimental import pallas as pl
from jax.experimental.pallas import tpu as pltpu
from jax.sharding import PartitionSpec as P

HEAD_DIM = 64
EPSILON = 1e-05
NEGATIVE = -1e30
f32 = jnp.float32
bf16 = jnp.bfloat16
VMEM = pl.BlockSpec(memory_space=pltpu.VMEM)
HBM = pl.BlockSpec(memory_space=pltpu.MemorySpace.HBM)
SMEM = pl.BlockSpec(memory_space=pltpu.SMEM)
SUM_ROWS = 16
COST = pl.CostEstimate(flops=2**20, bytes_accessed=2**20, transcendentals=0)
LONG = pl.CostEstimate(flops=2**34, bytes_accessed=2**24, transcendentals=0)


def layer_norm(values, gain, shift):
    average = jnp.mean(values, axis=-1, keepdims=True)
    centred = values - average
    variance = jnp.mean(centred * centred, axis=-1, keepdims=True)
    return centred * lax.rsqrt(variance + EPSILON) * gain + shift


def contract_rows(left, right):
    return lax.dot_general(
        left, right, (((0,), (0,)), ((), ())), preferred_element_type=f32
    )


def swap(values, axis, step):
    count = lax.axis_size(axis)
    return lax.ppermute(values, axis, [(i, i ^ step) for i in range(count)])


def steps_of(count):
    steps = []
    step = 1
    while step < count:
        steps.append(step)
        step *= 2
    return steps


def normalized(values):
    average = jnp.mean(values, axis=-1, keepdims=True)
    centred = values - average
    variance = jnp.mean(centred * centred, axis=-1, keepdims=True)
    return centred * lax.rsqrt(variance + EPSILON)


def project_kernel(
    rank_ref, tokens_ref, gain_ref, bias_ref, qw_ref, kw_ref, vw_ref,
    normed_ref, qt_ref, kt_ref, vt_ref,
):
    values = tokens_ref[...].astype(f32)
    normed = (normalized(values) * gain_ref[...][None] + bias_ref[...][None]).astype(bf16)
    normed_ref[...] = normed
    for weight_ref, out_ref, factor in (
        (qw_ref, qt_ref, HEAD_DIM ** (-0.5)), (kw_ref, kt_ref, None), (vw_ref, vt_ref, None)
    ):
        made = lax.dot_general(
            weight_ref[...], normed, (((1,), (1,)), ((), ())), preferred_element_type=f32
        ).astype(bf16)
        if factor is not None:
            made = made * jnp.asarray(factor, bf16)
        out_ref[...] = made


def project(rank, tokens, gain, bias, qw, kw, vw, blocks):
    slots, width = tokens.shape
    cols = qw.shape[0]
    size = slots // blocks
    fixed = lambda i, r: (0, 0)
    line = pl.BlockSpec((width,), lambda i, r: (0,))
    return pl.pallas_call(
        project_kernel,
        grid_spec=pltpu.PrefetchScalarGridSpec(
            num_scalar_prefetch=1,
            grid=(blocks,),
            in_specs=[
                pl.BlockSpec((size, width), lambda i, r: (i ^ r[0], 0)),
                line,
                line,
                pl.BlockSpec((cols, width), fixed),
                pl.BlockSpec((cols, width), fixed),
                pl.BlockSpec((cols, width), fixed),
            ],
            out_specs=(
                pl.BlockSpec((size, width), lambda i, r: (i, 0)),
                pl.BlockSpec((cols, size), lambda i, r: (0, i)),
                pl.BlockSpec((cols, size), lambda i, r: (0, i)),
                pl.BlockSpec((cols, size), lambda i, r: (0, i)),
            ),
        ),
        out_shape=(jax.ShapeDtypeStruct((slots, width), bf16),)
        + (jax.ShapeDtypeStruct((cols, slots), bf16),) * 3,
        name="project",
        cost_estimate=COST,
    )(rank, tokens, gain, bias, qw, kw, vw)


def item_ends(lens_ref):
    ends = []
    total = jnp.int32(0)
    for i in range(lens_ref.shape[1]):
        total = total + lens_ref[0, i]
        ends.append(total)
    return ends


def segments_at(place, ends):
    segment = jnp.zeros_like(place)
    for end in ends:
        segment = segment + (place >= end).astype(jnp.int32)
    return segment


def block_span(first, size, unit, ends):
    last = jnp.minimum(first + size, ends[-1]) - 1
    low = jnp.int32(0)
    high = ends[-1]
    for end in ends:
        low = jnp.where(first >= end, end, low)
    for end in reversed(ends):
        high = jnp.where(last < end, end, high)
    empty = first >= ends[-1]
    low_block = jnp.where(empty, 0, low // unit)
    high_block = jnp.where(empty, 0, (high + unit - 1) // unit)
    return low_block, high_block


def rows_at(block, size):
    return pl.ds(pl.multiple_of(block * size, size), size)


def fill_segments(row_ref, col_ref, shard, rank, ends):
    slots = row_ref.shape[1]
    at = lax.broadcasted_iota(jnp.int32, (1, slots), 1)
    place = ((at // shard) ^ rank) * shard + at % shard
    segments = segments_at(place, ends)
    row_ref[...] = segments
    col_ref[...] = jnp.transpose(jnp.broadcast_to(segments, (128, slots)), (1, 0))


def block_bias(row_ref, col_ref, rows, cols):
    return jnp.where(col_ref[rows, 0:1] == row_ref[:, cols], 0.0, NEGATIVE)


def lane_masked(values, head):
    lane = lax.broadcasted_iota(jnp.int32, values.shape, 1)
    inside = (lane >= head * HEAD_DIM) & (lane < (head + 1) * HEAD_DIM)
    return jnp.where(inside, values, jnp.zeros_like(values))


def forward_kernel(
    first, blocks, lens_ref, rank_ref, qt_ref, kt_ref, vt_ref, *refs
):
    *out_refs, log_ref, masked_ref, out_ref, row_ref, col_ref, score_ref = refs
    count, width, size = out_ref.shape
    heads = width // HEAD_DIM
    shard = size
    rank = rank_ref[0, 0]
    ends = item_ends(lens_ref)
    fill_segments(row_ref, col_ref, shard, rank, ends)
    keys = jnp.transpose(kt_ref[...], (1, 0))
    for h in range(heads):
        masked_ref[h] = lane_masked(keys, h)

    def query_block(b, unused):
        at = first + b
        i = at ^ rank
        cols = rows_at(at, size)
        queries = qt_ref[:, cols]

        def score_block(j, carry):
            rows = rows_at(j ^ rank, shard)
            bias = block_bias(row_ref, col_ref, rows, cols)
            result = []
            for h in range(heads):
                scores = jnp.dot(
                    masked_ref[h, rows, :], queries, preferred_element_type=f32
                )
                scores = scores + bias
                score_ref[h, rows_at(j, shard), :] = scores
                part = jnp.max(scores.reshape(-1, 8, size), axis=0)
                result.append(jnp.maximum(carry[h], part))
            return tuple(result)

        low, high = block_span(i * size, size, shard, ends)
        peaks = lax.fori_loop(
            low, high, score_block, (jnp.full((8, size), NEGATIVE, f32),) * heads
        )
        peaks = [jnp.max(peak, axis=0, keepdims=True) for peak in peaks]

        def key_block(j, carry):
            rows = rows_at(j ^ rank, shard)
            result = []
            for h in range(heads):
                summed, total = carry[h]
                soft = jnp.exp(score_ref[h, rows_at(j, shard), :] - peaks[h])
                summed = summed + jnp.sum(soft.reshape(-1, 8, size), axis=0)
                total = total + jnp.dot(
                    vt_ref[pl.ds(h * HEAD_DIM, HEAD_DIM), rows],
                    soft.astype(bf16),
                    preferred_element_type=f32,
                )
                result.append((summed, total))
            return tuple(result)

        start = ((jnp.zeros((8, size), f32), jnp.zeros((HEAD_DIM, size), f32)),) * heads
        done = lax.fori_loop(low, high, key_block, start)
        live = row_ref[:, cols] < len(ends)
        for h in range(heads):
            summed, total = done[h]
            summed = jnp.sum(summed, axis=0, keepdims=True)
            highest = peaks[h]
            summed = jnp.where(live, summed, 1.0)
            result = jnp.where(live, total / summed, 0.0).astype(bf16)
            logs = jnp.where(live, highest + jnp.log(summed), -NEGATIVE)
            out_ref[b, pl.ds(h * HEAD_DIM, HEAD_DIM), :] = result
            log_ref[h, :, rows_at(b, size)] = logs
        return unused

    lax.fori_loop(0, count, query_block, 0)
    for b in range(count):
        out_refs[b][...] = out_ref[b]


def attend(lens, rank, qt, kt, vt, blocks, first, count):
    width, slots = qt.shape
    size = slots // blocks
    heads = width // HEAD_DIM
    return pl.pallas_call(
        functools.partial(forward_kernel, first, blocks),
        out_shape=(jax.ShapeDtypeStruct((width, size), bf16),) * count
        + (jax.ShapeDtypeStruct((heads, 1, count * size), f32),),
        in_specs=[SMEM, SMEM, VMEM, VMEM, VMEM],
        out_specs=(VMEM,) * (count + 1),
        scratch_shapes=[
            pltpu.VMEM((heads, slots, width), bf16),
            pltpu.VMEM((count, width, size), bf16),
            pltpu.VMEM((1, slots), jnp.int32),
            pltpu.VMEM((slots, 128), jnp.int32),
            pltpu.VMEM((heads, slots, size), f32),
        ],
        name="attend",
        compiler_params=pltpu.CompilerParams(vmem_limit_bytes=60 * 2**20),
        cost_estimate=COST,
    )(lens, rank, qt, kt, vt)


def split_rows(values):
    high = values.astype(bf16)
    return jnp.concatenate([high, (values - high.astype(f32)).astype(bf16)], axis=0)


def add_kernel(a_ref, b_ref, out_ref):
    half = out_ref.shape[0] - SUM_ROWS
    line = SUM_ROWS // 2
    total = a_ref[...].astype(f32) + b_ref[...].astype(f32)
    out_ref[:half, :] = total[:half].astype(bf16)
    out_ref[half:, :] = split_rows(total[half : half + line] + total[half + line :])


def add_parts(a, b):
    return pl.pallas_call(
        add_kernel,
        out_shape=jax.ShapeDtypeStruct(a.shape, bf16),
        in_specs=[VMEM, VMEM],
        out_specs=VMEM,
        name="add_parts",
        compiler_params=pltpu.CompilerParams(vmem_limit_bytes=5 * 2**20),
        cost_estimate=COST,
    )(a, b)


def stacked_parts(first_head, heads, query, key, value):
    dim = HEAD_DIM
    parts = []
    for n in range(heads):
        first = (first_head + n) * dim
        parts += [(2 * n * dim, key, first, dim), ((2 * n + 1) * dim, value, first, dim)]
    return parts + [(2 * heads * dim, query, first_head * dim, heads * dim)]


def backward_kernel(
    first_head, heads, blocks, extras, lens_ref, rank_ref, bit_ref, qt_ref, kt_ref, vt_ref,
    near_ref, far_ref, qw_ref, kw_ref, vw_ref, normed_ref, *rest
):
    extra_refs, rest = rest[:extras], rest[extras:]
    width, slots = qt_ref.shape
    shard = slots // blocks
    dim = HEAD_DIM
    out_refs, grad_refs = rest[:blocks], rest[blocks : 2 * blocks]
    joint_ref, sums_ref, own_ref, away_ref = rest[2 * blocks : 2 * blocks + 4]
    kv_ref, q0_ref, og_ref, right_ref, inner_ref, dq_ref, made_ref = rest[-13:-6]
    log_ref = rest[-6]
    row_ref, col_ref = rest[-5:-3]
    turned_ref, rows_ref, copied = rest[-3:]
    fetch = pltpu.make_async_copy(normed_ref, rows_ref, copied)
    fetch.start()
    unit = shard // 2
    rank = rank_ref[0, 0]
    ends = item_ends(lens_ref)
    fill_segments(row_ref, col_ref, shard, rank, ends)
    near = near_ref.shape[2]
    log_ref[:, :, :near] = near_ref[...]
    log_ref[:, :, near:] = far_ref[...]
    zero = jnp.zeros((dim, slots), bf16)
    for n in range(heads):
        part = slice((first_head + n) * dim, (first_head + n + 1) * dim)
        both = jnp.concatenate([kt_ref[part, :], vt_ref[part, :]], axis=0)
        kv_ref[n] = jnp.transpose(both, (1, 0))
        padded = jnp.concatenate([qt_ref[part, :], zero], axis=0)
        q0_ref[n] = jnp.transpose(padded, (1, 0))
        right_ref[n, 0] = padded
        for b in range(blocks):
            grad = grad_refs[b][part, :]
            cols = slice(b * shard, (b + 1) * shard)
            padded = jnp.concatenate([zero[:, :shard], grad], axis=0)
            og_ref[n, cols, :] = jnp.transpose(padded, (1, 0))
            right_ref[n, 1, :, cols] = padded
            inner_ref[n, :, cols] = jnp.sum(
                out_refs[b][part, :].astype(f32) * grad.astype(f32), axis=0, keepdims=True
            )
    dq_ref[...] = jnp.zeros_like(dq_ref)

    def key_block(j, unused):
        at_key = ((j // 2) ^ rank) * 2 + j % 2
        rows = rows_at(at_key, unit)

        def query_block(i, totals):
            at = i ^ rank
            cols = rows_at(at, shard)
            same = col_ref[rows, 0:1] == row_ref[:, cols]
            result = []
            for n in range(heads):
                head = first_head + n
                kv = kv_ref[n, rows, :]
                scores = jnp.dot(kv, right_ref[n, 0, :, cols], preferred_element_type=f32)
                grad_soft = jnp.dot(kv, right_ref[n, 1, :, cols], preferred_element_type=f32)
                soft = jnp.where(same, jnp.exp(scores - log_ref[head, :, cols]), 0.0)
                grad_scores = (soft * (grad_soft - inner_ref[n, :, cols])).astype(bf16)
                total = totals[n] + jnp.dot(
                    soft.astype(bf16), og_ref[n, cols, :], preferred_element_type=f32
                )
                total = total + jnp.dot(
                    grad_scores, q0_ref[n, cols, :], preferred_element_type=f32
                )
                dq_ref[n, :, cols] += jnp.dot(
                    kt_ref[pl.ds(head * dim, dim), rows], grad_scores,
                    preferred_element_type=f32,
                )
                result.append(total)
            return tuple(result)

        low, high = block_span(j * unit, unit, shard, ends)
        start = (jnp.zeros((unit, 2 * dim), f32),) * heads
        totals = lax.fori_loop(low, high, query_block, start)
        for n in range(heads):
            part = slice(2 * dim * n, 2 * dim * (n + 1))
            total = totals[n].astype(bf16)
            joint_ref[rows, part] = total
            turned_ref[part, rows] = jnp.transpose(total, (1, 0))
        return unused

    lax.fori_loop(0, 2 * blocks, key_block, 0)
    dq = (dq_ref[...] * dim ** (-0.5)).astype(bf16).reshape(heads * dim, slots)
    turned_ref[2 * dim * heads :, :] = dq
    joint_ref[:, 2 * dim * heads :] = jnp.transpose(dq, (1, 0))
    fetch.wait()
    made_ref[...] = jnp.dot(turned_ref[...], rows_ref[...], preferred_element_type=f32)
    gains = jnp.zeros((1, rows_ref.shape[1]), f32)
    shifts = jnp.zeros((1, rows_ref.shape[1]), f32)
    for at, weight_ref, first, size in stacked_parts(
        first_head, heads, qw_ref, kw_ref, vw_ref
    ):
        weight = weight_ref[first : first + size, :].astype(f32)
        gains += jnp.sum(weight * made_ref[at : at + size, :], axis=0, keepdims=True)
        total = jnp.sum(turned_ref[at : at + size, :].astype(f32), axis=1, keepdims=True)
        shifts += jnp.sum(weight * total, axis=0, keepdims=True)
    sums_ref[0:1] = gains
    sums_ref[1:2] = shifts
    half = made_ref.shape[0] // 2
    bit = bit_ref[0, 0]
    for part_ref, at in ((own_ref, bit), (away_ref, 1 - bit)):
        part_ref[0:half, :] = made_ref[rows_at(at, half), :].astype(bf16)
        if extras:
            lines = [sums_ref[...] + extra_refs[0][...], extra_refs[1][...]]
            lines.append(jnp.zeros((SUM_ROWS // 2 - 4, gains.shape[1]), f32))
            part_ref[half:, :] = split_rows(jnp.concatenate(lines, axis=0))


def attend_back(
    first_head, heads, extras, lens, rank, bit, qt, kt, vt, logs, weights, normed, outs, grads
):
    slots, width = normed.shape
    blocks = len(outs)
    dim = HEAD_DIM
    cols = 3 * dim * heads
    rows = cols // 2 + (SUM_ROWS if extras else 0)
    return pl.pallas_call(
        functools.partial(backward_kernel, first_head, heads, blocks, len(extras)),
        out_shape=(
            jax.ShapeDtypeStruct((slots, cols), bf16),
            jax.ShapeDtypeStruct((2, width), f32),
        )
        + (jax.ShapeDtypeStruct((rows, width), bf16),) * 2,
        in_specs=[SMEM, SMEM, SMEM]
        + [VMEM] * 8
        + [pl.BlockSpec(memory_space=pl.ANY)]
        + [VMEM] * (len(extras) + 2 * blocks),
        out_specs=(VMEM,) * 4,
        scratch_shapes=[pltpu.VMEM((heads, slots, 2 * dim), bf16)] * 3
        + [
            pltpu.VMEM((heads, 2, 2 * dim, slots), bf16),
            pltpu.VMEM((heads, 1, slots), f32),
            pltpu.VMEM((heads, dim, slots), f32),
            pltpu.VMEM((cols, width), f32),
            pltpu.VMEM((qt.shape[0] // dim, 1, slots), f32),
            pltpu.VMEM((1, slots), jnp.int32),
            pltpu.VMEM((slots, 128), jnp.int32),
            pltpu.VMEM((cols, slots), bf16),
            pltpu.VMEM((slots, width), bf16),
            pltpu.SemaphoreType.DMA,
        ],
        name="attend_back",
        compiler_params=pltpu.CompilerParams(vmem_limit_bytes=60 * 2**20),
        cost_estimate=COST,
    )(lens, rank, bit, qt, kt, vt, *logs, *weights, normed, *extras, *outs, *grads)


def plan_kernel(capacity, lens_ref, rank_ref, routes_ref, order_ref, grad_ref,
                dispatch_ref, slots_ref):
    shard = routes_ref.shape[1]
    first = rank_ref[0, 0] * shard
    ends = item_ends(lens_ref)
    chosen_row = routes_ref[...]
    chosen_col = jnp.transpose(jnp.broadcast_to(chosen_row, (128, shard)), (1, 0))[:, 0:1]
    order_row = order_ref[...]
    order_col = jnp.transpose(jnp.broadcast_to(order_row, (128, shard)), (1, 0))[:, 0:1]
    alive_row = segments_at(
        first + lax.broadcasted_iota(jnp.int32, (1, shard), 1), ends
    ) < len(ends)
    alive_col = segments_at(
        first + lax.broadcasted_iota(jnp.int32, (shard, 1), 0), ends
    ) < len(ends)
    ahead = (chosen_col == chosen_row) & (order_col < order_row) & alive_col
    ranked = jnp.sum(ahead.astype(jnp.int32), axis=0, keepdims=True)
    kept = alive_row & (ranked < capacity)
    slot = jnp.where(kept, chosen_row * capacity + ranked, -1)
    dispatch = (
        lax.broadcasted_iota(jnp.int32, dispatch_ref.shape, 0) == slot
    ).astype(f32).astype(bf16)
    dispatch_ref[...] = dispatch
    slots_ref[...] = jnp.dot(
        dispatch, grad_ref[...], preferred_element_type=f32
    ).astype(bf16)


def plan(lens, rank, routes, order, grads, capacity, experts_all):
    shard, width = grads.shape
    count = experts_all * capacity
    return pl.pallas_call(
        functools.partial(plan_kernel, capacity),
        out_shape=(
            jax.ShapeDtypeStruct((count, shard), bf16),
            jax.ShapeDtypeStruct((count, width), bf16),
        ),
        in_specs=[SMEM, SMEM, VMEM, VMEM, VMEM],
        out_specs=(VMEM, VMEM),
        name="plan",
        cost_estimate=COST,
    )(lens, rank, routes.reshape(1, -1), order, grads)


def across(left, right):
    return lax.dot_general(
        left, right, (((1,), (1,)), ((), ())), preferred_element_type=f32
    )


def middle_kernel(count, rank_ref, tokens_ref, gain_ref, bias_ref, dispatch_ref, *refs):
    head_refs, weight_refs = refs[:count], refs[count : 2 * count]
    residual_ref, rows_ref = refs[2 * count :]
    residual = tokens_ref[...].astype(f32)
    for head_ref, weight_ref in zip(head_refs, weight_refs):
        residual = residual + contract_rows(head_ref[...], weight_ref[...])
    residual_ref[...] = residual
    normed = (normalized(residual) * gain_ref[...][None] + bias_ref[...][None]).astype(bf16)
    rows_ref[...] = jnp.dot(
        dispatch_ref[...], normed, preferred_element_type=f32
    ).astype(bf16)


def middle(rank, tokens, gain, bias, dispatch, heads, weights):
    count, shard = dispatch.shape
    width = tokens.shape[1]
    fixed = lambda array: pl.BlockSpec(array.shape, lambda i, r: (0,) * array.ndim)
    small = [gain, bias, dispatch, *heads, *weights]
    return pl.pallas_call(
        functools.partial(middle_kernel, len(heads)),
        grid_spec=pltpu.PrefetchScalarGridSpec(
            num_scalar_prefetch=1,
            grid=(1,),
            in_specs=[pl.BlockSpec((shard, width), lambda i, r: (r[0], 0))]
            + [fixed(array) for array in small],
            out_specs=(
                pl.BlockSpec((shard, width), lambda i, r: (0, 0)),
                pl.BlockSpec((count, width), lambda i, r: (0, 0)),
            ),
        ),
        out_shape=(
            jax.ShapeDtypeStruct((shard, width), f32),
            jax.ShapeDtypeStruct((count, width), bf16),
        ),
        name="middle",
        cost_estimate=COST,
    )(rank, tokens, *small)


def turn_kernel(
    count, lens_ref, rank_ref, dispatch_ref, back_ref, residual_ref, cotangent_ref,
    gain_ref, *refs
):
    head_refs, weight_refs = refs[:count], refs[count : 2 * count]
    grad_ref, sums_ref, kept_ref, sent_ref = refs[2 * count : 2 * count + 4]
    part_refs = refs[2 * count + 4 :]
    shard = residual_ref.shape[0]
    grad_normed = contract_rows(dispatch_ref[...], back_ref[...])
    values = residual_ref[...]
    centred = values - jnp.mean(values, axis=-1, keepdims=True)
    inverse = lax.rsqrt(jnp.mean(centred * centred, axis=-1, keepdims=True) + EPSILON)
    normed = centred * inverse
    sums_ref[0:1] = jnp.sum(grad_normed * normed, axis=0, keepdims=True)
    sums_ref[1:2] = jnp.sum(grad_normed, axis=0, keepdims=True)
    scaled = grad_normed * gain_ref[...][None]
    grad = cotangent_ref[...].astype(f32) + inverse * (
        scaled
        - jnp.mean(scaled, axis=-1, keepdims=True)
        - normed * jnp.mean(scaled * normed, axis=-1, keepdims=True)
    )
    grad_ref[...] = grad
    low = grad.astype(bf16)
    place = rank_ref[0, 0] * shard + lax.broadcasted_iota(jnp.int32, (1, shard), 1)
    alive = place < item_ends(lens_ref)[-1]
    for weight_ref, part_ref in zip(weight_refs, part_refs):
        part_ref[...] = jnp.where(alive, across(weight_ref[...], low), 0.0).astype(bf16)
    for j, head_ref in enumerate(head_refs):
        made = jnp.dot(head_ref[...], low, preferred_element_type=f32)
        (kept_ref, sent_ref)[j % 2][j // 2] = made.astype(bf16)


def turn(lens, rank, dispatch, back, residual, cotangent, gain, heads, weights):
    shard, width = residual.shape
    cols = weights[0].shape[0]
    count = len(weights)
    return pl.pallas_call(
        functools.partial(turn_kernel, count),
        out_shape=(
            jax.ShapeDtypeStruct((shard, width), f32),
            jax.ShapeDtypeStruct((2, width), f32),
            jax.ShapeDtypeStruct((count // 2, cols, width), bf16),
            jax.ShapeDtypeStruct((count // 2, cols, width), bf16),
        )
        + (jax.ShapeDtypeStruct((cols, shard), bf16),) * count,
        in_specs=[SMEM, SMEM] + [VMEM] * (5 + 2 * count),
        out_specs=(VMEM,) * (4 + count),
        name="turn",
        cost_estimate=COST,
    )(lens, rank, dispatch, back, residual, cotangent, gain, *heads, *weights)


def output_sum_kernel(kept_ref, core_ref, first_ref, near_ref, far_ref):
    cols = near_ref.shape[0]
    total = [
        (kept_ref[j].astype(f32) + core_ref[j].astype(f32)).astype(bf16) for j in range(2)
    ]
    near_ref[...] = total[0]
    far_ref[:cols, :] = total[1]
    far_ref[cols:, :] = first_ref[...]


def output_sums(kept, core, first):
    slots, cols, width = kept.shape
    return pl.pallas_call(
        output_sum_kernel,
        out_shape=(
            jax.ShapeDtypeStruct((cols, width), bf16),
            jax.ShapeDtypeStruct((cols + first.shape[0], width), bf16),
        ),
        in_specs=[VMEM] * 3,
        out_specs=(VMEM, VMEM),
        name="output_sums",
        cost_estimate=LONG,
    )(kept, core, first)


def gelu_parts(values):
    below = 0.5 + 0.5 * lax.erf(values * (0.5**0.5))
    density = jnp.exp(-0.5 * values * values) * (0.5 / jnp.pi) ** 0.5
    return values * below, below + values * density


def part_at(step, parts, rank):
    half = parts // 2
    return (2 * (step % half) + step // half) ^ rank


def expert_kernel(
    parts, rank_ref, in_ref, grad_act_ref, up_ref,
    act_kept_ref, pre_kept_ref, act_sent_ref, pre_sent_ref, mid_ref,
    grads_ref, ups_ref, acts_ref, pres_ref, sum_ref, fetched, stored,
):
    rank = rank_ref[0, 0]
    size = ups_ref.shape[2]
    half = parts // 2

    def fetch(p):
        cols = rows_at(part_at(p, parts, rank), size)
        return (
            pltpu.make_async_copy(up_ref.at[:, cols], ups_ref.at[p], fetched.at[0, p]),
            pltpu.make_async_copy(grad_act_ref.at[:, cols], grads_ref.at[p], fetched.at[1, p]),
        )

    def store(p, act_out_ref, pre_out_ref):
        cols = rows_at(p % half, size)
        return (
            pltpu.make_async_copy(acts_ref.at[p], act_out_ref.at[:, cols], stored.at[0, p]),
            pltpu.make_async_copy(pres_ref.at[p], pre_out_ref.at[:, cols], stored.at[1, p]),
        )

    for p in range(parts):
        for copy in fetch(p):
            copy.start()
    sum_ref[...] = jnp.zeros_like(sum_ref)

    def part(p, unused):
        for copy in fetch(p):
            copy.wait()
        pre = jnp.dot(in_ref[...], ups_ref[p], preferred_element_type=f32)
        act, slope = gelu_parts(pre)
        acts_ref[p] = act.astype(bf16)
        grad_pre = (grads_ref[p].astype(f32) * slope).astype(bf16)
        pres_ref[p] = grad_pre
        sum_ref[...] += across(grad_pre, ups_ref[p])

        @pl.when(p < half)
        def keep():
            for copy in store(p, act_kept_ref, pre_kept_ref):
                copy.start()

        @pl.when(p >= half)
        def send():
            for copy in store(p, act_sent_ref, pre_sent_ref):
                copy.start()

        return unused

    lax.fori_loop(0, parts, part, 0)
    mid_ref[...] = sum_ref[...].astype(bf16)
    for p in range(parts):
        outs = (act_kept_ref, pre_kept_ref) if p < half else (act_sent_ref, pre_sent_ref)
        for copy in store(p, *outs):
            copy.wait()


def expert(rank, rows, grad_act, up, parts):
    count, width = rows.shape
    hidden = up.shape[1]
    size = hidden // parts
    return pl.pallas_call(
        functools.partial(expert_kernel, parts),
        out_shape=(jax.ShapeDtypeStruct((count, hidden // 2), bf16),) * 4
        + (jax.ShapeDtypeStruct((count, width), bf16),),
        in_specs=[SMEM, VMEM, HBM, HBM],
        out_specs=(HBM,) * 4 + (VMEM,),
        scratch_shapes=[
            pltpu.VMEM((parts, count, size), grad_act.dtype),
            pltpu.VMEM((parts, width, size), bf16),
            pltpu.VMEM((parts, count, size), bf16),
            pltpu.VMEM((parts, count, size), bf16),
            pltpu.VMEM((count, width), f32),
            pltpu.SemaphoreType.DMA((2, parts)),
            pltpu.SemaphoreType.DMA((2, parts)),
        ],
        name="expert",
        compiler_params=pltpu.CompilerParams(vmem_limit_bytes=60 * 2**20),
        cost_estimate=COST,
    )(rank.reshape(1, 1), rows, grad_act, up)


def product_kernel(parts, rank_ref, kept_ref, sent_ref, down_ref, out_ref,
                   acts_ref, downs_ref, sum_ref, fetched):
    rank = rank_ref[0, 0]
    size = downs_ref.shape[1]
    half = parts // 2

    def fetch(p):
        rows = rows_at(part_at(p, parts, rank), size)
        source = kept_ref if p < half else sent_ref
        cols = slice((p % half) * size, (p % half + 1) * size)
        return (
            pltpu.make_async_copy(down_ref.at[rows, :], downs_ref.at[p], fetched.at[0, p]),
            pltpu.make_async_copy(source.at[:, cols], acts_ref.at[p], fetched.at[1, p]),
        )

    for p in range(parts):
        for copy in fetch(p):
            copy.start()
    sum_ref[...] = jnp.zeros_like(sum_ref)
    for p in range(parts):
        for copy in fetch(p):
            copy.wait()
        sum_ref[...] += jnp.dot(acts_ref[p], downs_ref[p], preferred_element_type=f32)
    out_ref[...] = sum_ref[...].astype(bf16)


def product(rank, kept, sent, down, parts):
    count = kept.shape[0]
    hidden, width = down.shape
    size = hidden // parts
    return pl.pallas_call(
        functools.partial(product_kernel, parts),
        out_shape=jax.ShapeDtypeStruct((count, width), bf16),
        in_specs=[SMEM, HBM, HBM, HBM],
        out_specs=VMEM,
        scratch_shapes=[
            pltpu.VMEM((parts, count, size), bf16),
            pltpu.VMEM((parts, size, width), bf16),
            pltpu.VMEM((count, width), f32),
            pltpu.SemaphoreType.DMA((2, parts)),
        ],
        name="product",
        cost_estimate=COST,
    )(rank.reshape(1, 1), kept, sent, down)


def weight_kernel(groups, *refs):
    first_ref, rest_ref, up_ref, down_ref = refs[-4:]
    dup = ddown = 0.0
    for g in range(groups):
        in_ref, grad_ref, act_ref, pre_ref = refs[4 * g : 4 * g + 4]
        dup = dup + contract_rows(in_ref[...], pre_ref[...])
        ddown = ddown + contract_rows(act_ref[...], grad_ref[...])
    cut = first_ref.shape[0]

    @pl.when(pl.program_id(0) == 0)
    def far():
        first_ref[...] = dup[:cut].astype(bf16)
        rest_ref[: dup.shape[0] - cut, :] = dup[cut:].astype(bf16)
        rest_ref[dup.shape[0] - cut :, :] = ddown.astype(bf16)

    @pl.when(pl.program_id(0) == 1)
    def near():
        up_ref[...] = dup
        down_ref[...] = ddown


def expert_weights(groups):
    count, width = groups[0][0].shape
    size = groups[0][2].shape[1] // 2
    fixed = pl.BlockSpec((count, width), lambda i: (0, 0))
    columns = pl.BlockSpec((count, size), lambda i: (0, 1 - i))
    cut = (width + size) // 4
    shapes = ((cut, size), (width + size - cut, size), (width, size), (size, width))
    return pl.pallas_call(
        functools.partial(weight_kernel, len(groups)),
        grid=(2,),
        in_specs=[fixed, fixed, columns, columns] * len(groups),
        out_specs=tuple(pl.BlockSpec(shape, lambda i: (0, 0)) for shape in shapes),
        out_shape=tuple(
            jax.ShapeDtypeStruct(shape, bf16 if k < 2 else f32)
            for k, shape in enumerate(shapes)
        ),
        name="expert_weights",
        compiler_params=pltpu.CompilerParams(vmem_limit_bytes=60 * 2**20),
        cost_estimate=COST,
    )(*[values for group in groups for values in group])


def expert_sum_kernel(near_up_ref, near_down_ref, first_ref, rest_ref, up_ref, down_ref):
    step = pl.program_id(0)
    half = pl.num_programs(0) // 2
    far = jnp.where(step < half // 2, first_ref[...], rest_ref[...]).astype(f32)

    @pl.when(step < half)
    def upper():
        up_ref[...] = near_up_ref[...] + far

    @pl.when(step >= half)
    def lower():
        down_ref[...] = near_down_ref[...] + far


def expert_sums(near_up, near_down, first, rest):
    count, width = near_up.shape
    steps = 8
    half = steps // 2
    size = count // half
    head = steps // 4
    skip = first.shape[0] // size - head
    block = lambda place: pl.BlockSpec((size, width), lambda i: (place(i), 0))
    upper = block(lambda i: jnp.minimum(i, half - 1))
    lower = block(lambda i: jnp.maximum(i - half, 0))
    return pl.pallas_call(
        expert_sum_kernel,
        grid=(steps,),
        out_shape=(jax.ShapeDtypeStruct((count, width), f32),) * 2,
        in_specs=[
            upper,
            lower,
            block(lambda i: jnp.minimum(i, head - 1) + skip),
            block(lambda i: jnp.maximum(i - head, 0)),
        ],
        out_specs=(upper, lower),
        name="expert_sums",
        compiler_params=pltpu.CompilerParams(vmem_limit_bytes=10 * 2**20),
        cost_estimate=COST,
    )(near_up, near_down, first, rest)


def input_grad_kernel(groups, qw_ref, kw_ref, vw_ref, *refs):
    joint_refs = refs[: len(groups)]
    kept_ref, sent_ref, turned_ref = refs[len(groups) :]
    step = pl.program_id(0)

    @pl.when(step == 0)
    def stack():
        start = 0
        for first_head, heads in groups:
            for at, weight_ref, first, size in stacked_parts(
                first_head, heads, qw_ref, kw_ref, vw_ref
            ):
                turned_ref[start + at : start + at + size, :] = weight_ref[
                    first : first + size, :
                ]
            start += 3 * heads * HEAD_DIM

    total = 0.0
    at = 0
    for joint_ref in joint_refs:
        rows = slice(at, at + joint_ref.shape[1])
        total = total + jnp.dot(
            joint_ref[...], turned_ref[rows, :], preferred_element_type=f32
        )
        at += joint_ref.shape[1]

    @pl.when(step % 2 == 0)
    def keep():
        kept_ref[0] = total.astype(bf16)

    @pl.when(step % 2 == 1)
    def send():
        sent_ref[0] = total.astype(bf16)


def input_grad(groups, weights, joints, first, count, size):
    cols, width = weights[0].shape
    fixed = pl.BlockSpec((cols, width), lambda i: (0, 0))
    return pl.pallas_call(
        functools.partial(input_grad_kernel, groups),
        grid=(count,),
        out_shape=(jax.ShapeDtypeStruct((count // 2, size, width), bf16),) * 2,
        in_specs=[fixed] * 3
        + [
            pl.BlockSpec((size, joint.shape[1]), lambda i: (first + i, 0))
            for joint in joints
        ],
        out_specs=(pl.BlockSpec((1, size, width), lambda i: (i // 2, 0, 0)),) * 2,
        scratch_shapes=[pltpu.VMEM((3 * cols, width), bf16)],
        name="input_grad",
        compiler_params=pltpu.CompilerParams(vmem_limit_bytes=12 * 2**20),
        cost_estimate=COST,
    )(*weights, *joints)


def close_kernel(rank_ref, tokens_ref, gain_ref, grad_ref, *refs):
    *part_refs, out_ref = refs
    grad_in = 0.0
    for part_ref in part_refs:
        grad_in = grad_in + part_ref[...].reshape(out_ref.shape).astype(f32)
    values = tokens_ref[...].astype(f32)
    centred = values - jnp.mean(values, axis=-1, keepdims=True)
    inverse = lax.rsqrt(jnp.mean(centred * centred, axis=-1, keepdims=True) + EPSILON)
    normed = centred * inverse
    scaled = grad_in * gain_ref[...][None]
    out_ref[...] = grad_ref[...] + inverse * (
        scaled
        - jnp.mean(scaled, axis=-1, keepdims=True)
        - normed * jnp.mean(scaled * normed, axis=-1, keepdims=True)
    )


def close(rank, tokens, gain, grad, parts):
    shard, width = grad.shape
    size = shard // 2
    rows = lambda i, r: (i, 0)
    return pl.pallas_call(
        close_kernel,
        grid_spec=pltpu.PrefetchScalarGridSpec(
            num_scalar_prefetch=1,
            grid=(2,),
            in_specs=[
                pl.BlockSpec((size, width), lambda i, r: (2 * r[0] + i, 0)),
                pl.BlockSpec((width,), lambda i, r: (0,)),
                pl.BlockSpec((size, width), rows),
            ]
            + [pl.BlockSpec((1, size, width), lambda i, r: (0, i, 0))] * len(parts),
            out_specs=pl.BlockSpec((size, width), rows),
        ),
        out_shape=jax.ShapeDtypeStruct((shard, width), f32),
        name="close",
        compiler_params=pltpu.CompilerParams(vmem_limit_bytes=12 * 2**20),
        cost_estimate=COST,
    )(rank, tokens, gain, grad, *parts)


def add_low(a, b):
    return (a.astype(f32) + b.astype(f32)).astype(bf16)


def tie(*values):
    return lax.optimization_barrier(values)


def finish_kernel(groups, bit_ref, *refs):
    pieces, refs = refs[: 2 * len(groups)], refs[2 * len(groups) :]
    query_ref, key_ref, value_ref = refs[:3]
    bit = bit_ref[0, 0]
    for g, ((first_head, heads), whole_ref) in enumerate(zip(groups, refs[3:])):
        half = whole_ref.shape[0] // 2
        for piece_ref, at in ((pieces[2 * g], bit), (pieces[2 * g + 1], 1 - bit)):
            whole_ref[rows_at(at, half), :] = piece_ref[0:half, :].astype(f32)
        for at, target_ref, first, size in stacked_parts(
            first_head, heads, query_ref, key_ref, value_ref
        ):
            target_ref[first : first + size, :] = whole_ref[at : at + size, :]


def finish(groups, bit, pieces):
    width = pieces[0].shape[1]
    cols = sum(heads for first_head, heads in groups) * HEAD_DIM
    return pl.pallas_call(
        functools.partial(finish_kernel, groups),
        out_shape=(jax.ShapeDtypeStruct((cols, width), f32),) * 3,
        in_specs=[SMEM] + [VMEM] * len(pieces),
        out_specs=(VMEM,) * 3,
        scratch_shapes=[
            pltpu.VMEM((3 * heads * HEAD_DIM, width), f32) for first_head, heads in groups
        ],
        name="finish",
        compiler_params=pltpu.CompilerParams(vmem_limit_bytes=10 * 2**20),
        cost_estimate=COST,
    )(bit, *pieces)


def on_device(
    tokens,
    first_gain,
    first_bias,
    query_weight,
    key_weight,
    value_weight,
    output_weight,
    second_gain,
    second_bias,
    expert_up,
    expert_down,
    item_lengths,
    routes,
    slot_order,
    cotangent,
):
    slots_all, width = tokens.shape
    members = lax.axis_size("tensor")
    shard_rows = slots_all // members
    rank = lax.axis_index("tensor")
    sources = lax.axis_size("dp")
    experts_all = sources * expert_up.shape[0]
    capacity = shard_rows // experts_all
    head_cols = query_weight.shape[1]
    heads = head_cols // HEAD_DIM
    up_matrix = expert_up[0]
    down_matrix = expert_down[0]
    rank_cell = rank.astype(jnp.int32).reshape(1, 1)

    def exchange(rows):
        return lax.all_to_all(
            rows.reshape(sources, -1, width), "dp", split_axis=0, concat_axis=0, tiled=True
        ).reshape(-1, width)

    qw, kw, vw = query_weight.T, key_weight.T, value_weight.T

    dispatch, grad_slots = plan(
        item_lengths, rank_cell, routes, slot_order, cotangent, capacity, experts_all
    )
    flat_grad = exchange(grad_slots)
    tokens, grad_slots = tie(tokens, grad_slots)
    normed_in, qt, kt, vt = project(
        rank_cell[0], tokens, first_gain, first_bias, qw, kw, vw, members
    )
    outputs = [output_weight] + [
        swap(output_weight, "tensor", k) for k in range(1, members)
    ]
    far = members // 2
    *far_heads, far_logs = attend(
        item_lengths, rank_cell, qt, kt, vt, members, far, members - far
    )
    far_heads, kt = tie(far_heads, kt)
    far_arrived = [swap(far_heads[j - far], "tensor", j) for j in range(far, members)]
    *near_heads, near_logs = attend(item_lengths, rank_cell, qt, kt, vt, members, 0, far)
    near_heads, far_arrived, outputs = tie(near_heads, far_arrived, outputs)
    own_heads = near_heads + far_heads
    logs = (near_logs, far_logs)
    all_heads = (
        near_heads[:1]
        + [swap(near_heads[j], "tensor", j) for j in range(1, far)]
        + far_arrived
    )
    residual, outgoing = middle(
        rank_cell[0], tokens, second_gain, second_bias, dispatch, all_heads, outputs
    )
    flat_in = exchange(outgoing)

    flat_grad, outgoing = tie(flat_grad, outgoing)
    grad_act = across(flat_grad, down_matrix).astype(bf16)
    near_grads = swap(flat_grad, "tensor", 1)
    flat_in, grad_act, near_grads = tie(flat_in, grad_act, near_grads)
    near_rows = swap(flat_in, "tensor", 1)
    act, grad_pre, act_sent, pre_sent, grad_mid = expert(
        rank_cell[0], flat_in, grad_act, up_matrix, members
    )
    grad_mid, act, near_rows = tie(grad_mid, act, near_rows)
    grad_back = exchange(grad_mid)

    act, act_sent, pre_sent, grad_mid = tie(act, act_sent, pre_sent, grad_mid)
    near_act = swap(act_sent, "tensor", 1)
    near_pre = swap(pre_sent, "tensor", 1)
    made = product(rank_cell[0], act, act_sent, down_matrix, members)
    made, near_act, near_pre = tie(made, near_act, near_pre)
    *expert_far, expert_up_near, expert_down_near = expert_weights(
        [(flat_in, flat_grad, act, grad_pre), (near_rows, near_grads, near_act, near_pre)]
    )
    grad_back, made, expert_far = tie(grad_back, made, expert_far)

    steps = steps_of(members)
    grad_res, sums_second, kept, sent, *grad_heads = turn(
        item_lengths, rank_cell, dispatch, grad_back, residual, cotangent,
        second_gain, all_heads, outputs,
    )
    grad_parts = [grad_heads[0]] + [
        swap(grad_heads[j], "tensor", j) for j in range(1, members)
    ]
    output_near, output_far = output_sums(kept, swap(sent, "tensor", 1), expert_far[0])
    made, grad_heads = tie(made, grad_heads)
    returned = exchange(made)
    grad_parts, output_near, output_far = tie(grad_parts, output_near, output_far)

    bit_cell = (lax.axis_index("dp") & 1).astype(jnp.int32).reshape(1, 1)
    weights = (qw, kw, vw)
    dp_steps = steps_of(sources)
    back = functools.partial(
        attend_back, lens=item_lengths, rank=rank_cell, bit=bit_cell, qt=qt, kt=kt, vt=vt,
        logs=logs, weights=weights, normed=normed_in, outs=own_heads,
    )
    groups = ((0, heads - 1), (heads - 1, 1))
    joint_a, sums_a, own_a, away_a = back(*groups[0], extras=(), grads=grad_parts)
    output_got = swap(output_far, "tensor", 2)
    joint_a, own_a, away_a, output_got, grad_parts, expert_rest, returned = tie(
        joint_a, own_a, away_a, output_got, grad_parts, expert_far[1], returned
    )
    expert_got = swap(expert_rest, "tensor", 2)
    output_sum = add_low(output_near, output_got[: output_near.shape[0]])
    own_a = add_low(own_a, swap(away_a, "dp", 1))
    output_sum = add_low(output_sum, swap(output_sum, "dp", dp_steps[-1]))
    joint_b, unused, own_b, away_b = back(
        *groups[1], extras=(sums_a, sums_second), grads=grad_parts
    )
    joint_b, own_a, own_b, away_b, output_sum = tie(
        joint_b, own_a, own_b, away_b, output_sum
    )

    far_kept, far_sent = input_grad(
        groups, weights, (joint_a, joint_b), far, members - far, shard_rows
    )
    near_kept, near_sent = input_grad(
        groups, weights, (joint_a, joint_b), 0, far, shard_rows
    )
    own_b = add_parts(own_b, swap(away_b, "dp", 1))
    far_kept = add_low(far_kept, swap(far_sent, "tensor", 1))
    far_kept, own_b, output_sum, near_sent = tie(far_kept, own_b, output_sum, near_sent)
    near_core = swap(near_sent, "tensor", 1)
    near_far = swap(far_kept, "tensor", 2)
    for step in dp_steps[1:]:
        own_a = add_low(own_a, swap(own_a, "dp", step))
        own_b = add_parts(own_b, swap(own_b, "dp", step))
        if step == dp_steps[1]:
            own_b, expert_got = tie(own_b, expert_got)
    up_grad, down_grad = expert_sums(
        expert_up_near, expert_down_near, output_got, expert_got
    )
    own_b, up_grad, down_grad, near_far = tie(own_b, up_grad, down_grad, near_far)
    norm_sums = own_b[-SUM_ROWS:].astype(f32)
    norm_sums = norm_sums[: SUM_ROWS // 2] + norm_sums[SUM_ROWS // 2 :]
    for step in steps:
        norm_sums = norm_sums + swap(norm_sums, "tensor", step)
    pieces = (own_a, swap(own_a, "dp", 1), own_b, swap(own_b, "dp", 1))
    token_grad = close(
        rank_cell[0], tokens, first_gain, grad_res, (near_kept, near_core, near_far)
    )
    for step in dp_steps[:-1]:
        output_sum = add_low(output_sum, swap(output_sum, "dp", step))

    block_out = residual + contract_rows(dispatch, returned)
    query_grad, key_grad, value_grad = finish(groups, bit_cell, pieces)
    return (
        block_out,
        token_grad,
        (norm_sums[0] - first_bias * norm_sums[1]) / first_gain,
        norm_sums[1],
        query_grad.T,
        key_grad.T,
        value_grad.T,
        output_sum.astype(f32),
        norm_sums[2],
        norm_sums[3],
        up_grad[None],
        down_grad[None],
    )


def solution(mesh):
    in_specs = (
        P("dp", None),
        P(),
        P(),
        P(None, "tensor"),
        P(None, "tensor"),
        P(None, "tensor"),
        P("tensor", None),
        P(),
        P(),
        P("dp", None, None),
        P("dp", None, None),
        P("dp", None),
        P(("dp", "tensor"), None),
        P(("dp", "tensor"), None),
        P(("dp", "tensor"), None),
    )
    out_specs = (
        P(("dp", "tensor"), None),
        P(("dp", "tensor"), None),
        P(),
        P(),
        P(None, "tensor"),
        P(None, "tensor"),
        P(None, "tensor"),
        P("tensor", None),
        P(),
        P(),
        P("dp", None, "tensor"),
        P("dp", "tensor", None),
    )
    return jax.shard_map(
        on_device, mesh=mesh, in_specs=in_specs, out_specs=out_specs, check_vma=False
    )
```

```python
import functools

import jax
import jax.numpy as jnp
from jax import lax
from jax.experimental import pallas as pl
from jax.experimental.pallas import tpu as pltpu
from jax.sharding import PartitionSpec as P

HEAD_DIM = 64
EPSILON = 1e-05
NEGATIVE = -1e30
f32 = jnp.float32
bf16 = jnp.bfloat16
VMEM = pl.BlockSpec(memory_space=pltpu.VMEM)
HBM = pl.BlockSpec(memory_space=pltpu.MemorySpace.HBM)
SMEM = pl.BlockSpec(memory_space=pltpu.SMEM)
SUM_ROWS = 16
COST = pl.CostEstimate(flops=2**20, bytes_accessed=2**20, transcendentals=0)
LONG = pl.CostEstimate(flops=2**34, bytes_accessed=2**24, transcendentals=0)


def layer_norm(values, gain, shift):
    average = jnp.mean(values, axis=-1, keepdims=True)
    centred = values - average
    variance = jnp.mean(centred * centred, axis=-1, keepdims=True)
    return centred * lax.rsqrt(variance + EPSILON) * gain + shift


def contract_rows(left, right):
    return lax.dot_general(
        left, right, (((0,), (0,)), ((), ())), preferred_element_type=f32
    )


def swap(values, axis, step):
    count = lax.axis_size(axis)
    return lax.ppermute(values, axis, [(i, i ^ step) for i in range(count)])


def steps_of(count):
    steps = []
    step = 1
    while step < count:
        steps.append(step)
        step *= 2
    return steps


def normalized(values):
    average = jnp.mean(values, axis=-1, keepdims=True)
    centred = values - average
    variance = jnp.mean(centred * centred, axis=-1, keepdims=True)
    return centred * lax.rsqrt(variance + EPSILON)


def project_kernel(
    rank_ref, tokens_ref, gain_ref, bias_ref, qw_ref, kw_ref, vw_ref,
    normed_ref, qt_ref, kt_ref, vt_ref,
):
    values = tokens_ref[...].astype(f32)
    normed = (normalized(values) * gain_ref[...][None] + bias_ref[...][None]).astype(bf16)
    normed_ref[...] = normed
    for weight_ref, out_ref, factor in (
        (qw_ref, qt_ref, HEAD_DIM ** (-0.5)), (kw_ref, kt_ref, None), (vw_ref, vt_ref, None)
    ):
        made = lax.dot_general(
            weight_ref[...], normed, (((1,), (1,)), ((), ())), preferred_element_type=f32
        ).astype(bf16)
        if factor is not None:
            made = made * jnp.asarray(factor, bf16)
        out_ref[...] = made


def project(rank, tokens, gain, bias, qw, kw, vw, blocks):
    slots, width = tokens.shape
    cols = qw.shape[0]
    size = slots // blocks
    fixed = lambda i, r: (0, 0)
    line = pl.BlockSpec((width,), lambda i, r: (0,))
    return pl.pallas_call(
        project_kernel,
        grid_spec=pltpu.PrefetchScalarGridSpec(
            num_scalar_prefetch=1,
            grid=(blocks,),
            in_specs=[
                pl.BlockSpec((size, width), lambda i, r: (i ^ r[0], 0)),
                line,
                line,
                pl.BlockSpec((cols, width), fixed),
                pl.BlockSpec((cols, width), fixed),
                pl.BlockSpec((cols, width), fixed),
            ],
            out_specs=(
                pl.BlockSpec((size, width), lambda i, r: (i, 0)),
                pl.BlockSpec((cols, size), lambda i, r: (0, i)),
                pl.BlockSpec((cols, size), lambda i, r: (0, i)),
                pl.BlockSpec((cols, size), lambda i, r: (0, i)),
            ),
        ),
        out_shape=(jax.ShapeDtypeStruct((slots, width), bf16),)
        + (jax.ShapeDtypeStruct((cols, slots), bf16),) * 3,
        name="project",
        cost_estimate=COST,
    )(rank, tokens, gain, bias, qw, kw, vw)


def item_ends(lens_ref):
    ends = []
    total = jnp.int32(0)
    for i in range(lens_ref.shape[1]):
        total = total + lens_ref[0, i]
        ends.append(total)
    return ends


def segments_at(place, ends):
    segment = jnp.zeros_like(place)
    for end in ends:
        segment = segment + (place >= end).astype(jnp.int32)
    return segment


def block_span(first, size, unit, ends):
    last = jnp.minimum(first + size, ends[-1]) - 1
    low = jnp.int32(0)
    high = ends[-1]
    for end in ends:
        low = jnp.where(first >= end, end, low)
    for end in reversed(ends):
        high = jnp.where(last < end, end, high)
    empty = first >= ends[-1]
    low_block = jnp.where(empty, 0, low // unit)
    high_block = jnp.where(empty, 0, (high + unit - 1) // unit)
    return low_block, high_block


def rows_at(block, size):
    return pl.ds(pl.multiple_of(block * size, size), size)


def fill_segments(row_ref, col_ref, shard, rank, ends):
    slots = row_ref.shape[1]
    at = lax.broadcasted_iota(jnp.int32, (1, slots), 1)
    place = ((at // shard) ^ rank) * shard + at % shard
    segments = segments_at(place, ends)
    row_ref[...] = segments
    col_ref[...] = jnp.transpose(jnp.broadcast_to(segments, (128, slots)), (1, 0))


def block_bias(row_ref, col_ref, rows, cols):
    return jnp.where(col_ref[rows, 0:1] == row_ref[:, cols], 0.0, NEGATIVE)


def lane_masked(values, head):
    lane = lax.broadcasted_iota(jnp.int32, values.shape, 1)
    inside = (lane >= head * HEAD_DIM) & (lane < (head + 1) * HEAD_DIM)
    return jnp.where(inside, values, jnp.zeros_like(values))


def forward_kernel(
    first, blocks, lens_ref, rank_ref, qt_ref, kt_ref, vt_ref, *refs
):
    *out_refs, log_ref, masked_ref, out_ref, row_ref, col_ref, score_ref = refs
    count, width, size = out_ref.shape
    heads = width // HEAD_DIM
    shard = size
    rank = rank_ref[0, 0]
    ends = item_ends(lens_ref)
    fill_segments(row_ref, col_ref, shard, rank, ends)
    keys = jnp.transpose(kt_ref[...], (1, 0))
    for h in range(heads):
        masked_ref[h] = lane_masked(keys, h)

    def query_block(b, unused):
        at = first + b
        i = at ^ rank
        cols = rows_at(at, size)
        queries = qt_ref[:, cols]

        def score_block(j, carry):
            rows = rows_at(j ^ rank, shard)
            bias = block_bias(row_ref, col_ref, rows, cols)
            result = []
            for h in range(heads):
                scores = jnp.dot(
                    masked_ref[h, rows, :], queries, preferred_element_type=f32
                )
                scores = scores + bias
                score_ref[h, rows_at(j, shard), :] = scores
                part = jnp.max(scores.reshape(-1, 8, size), axis=0)
                result.append(jnp.maximum(carry[h], part))
            return tuple(result)

        low, high = block_span(i * size, size, shard, ends)
        peaks = lax.fori_loop(
            low, high, score_block, (jnp.full((8, size), NEGATIVE, f32),) * heads
        )
        peaks = [jnp.max(peak, axis=0, keepdims=True) for peak in peaks]

        def key_block(j, carry):
            rows = rows_at(j ^ rank, shard)
            result = []
            for h in range(heads):
                summed, total = carry[h]
                soft = jnp.exp(score_ref[h, rows_at(j, shard), :] - peaks[h])
                summed = summed + jnp.sum(soft.reshape(-1, 8, size), axis=0)
                total = total + jnp.dot(
                    vt_ref[pl.ds(h * HEAD_DIM, HEAD_DIM), rows],
                    soft.astype(bf16),
                    preferred_element_type=f32,
                )
                result.append((summed, total))
            return tuple(result)

        start = ((jnp.zeros((8, size), f32), jnp.zeros((HEAD_DIM, size), f32)),) * heads
        done = lax.fori_loop(low, high, key_block, start)
        live = row_ref[:, cols] < len(ends)
        for h in range(heads):
            summed, total = done[h]
            summed = jnp.sum(summed, axis=0, keepdims=True)
            highest = peaks[h]
            summed = jnp.where(live, summed, 1.0)
            result = jnp.where(live, total / summed, 0.0).astype(bf16)
            logs = jnp.where(live, highest + jnp.log(summed), -NEGATIVE)
            out_ref[b, pl.ds(h * HEAD_DIM, HEAD_DIM), :] = result
            log_ref[h, :, rows_at(b, size)] = logs
        return unused

    lax.fori_loop(0, count, query_block, 0)
    for b in range(count):
        out_refs[b][...] = out_ref[b]


def attend(lens, rank, qt, kt, vt, blocks, first, count):
    width, slots = qt.shape
    size = slots // blocks
    heads = width // HEAD_DIM
    return pl.pallas_call(
        functools.partial(forward_kernel, first, blocks),
        out_shape=(jax.ShapeDtypeStruct((width, size), bf16),) * count
        + (jax.ShapeDtypeStruct((heads, 1, count * size), f32),),
        in_specs=[SMEM, SMEM, VMEM, VMEM, VMEM],
        out_specs=(VMEM,) * (count + 1),
        scratch_shapes=[
            pltpu.VMEM((heads, slots, width), bf16),
            pltpu.VMEM((count, width, size), bf16),
            pltpu.VMEM((1, slots), jnp.int32),
            pltpu.VMEM((slots, 128), jnp.int32),
            pltpu.VMEM((heads, slots, size), f32),
        ],
        name="attend",
        compiler_params=pltpu.CompilerParams(vmem_limit_bytes=60 * 2**20),
        cost_estimate=COST,
    )(lens, rank, qt, kt, vt)


def split_rows(values):
    high = values.astype(bf16)
    return jnp.concatenate([high, (values - high.astype(f32)).astype(bf16)], axis=0)


def add_kernel(a_ref, b_ref, out_ref):
    half = out_ref.shape[0] - SUM_ROWS
    line = SUM_ROWS // 2
    total = a_ref[...].astype(f32) + b_ref[...].astype(f32)
    out_ref[:half, :] = total[:half].astype(bf16)
    out_ref[half:, :] = split_rows(total[half : half + line] + total[half + line :])


def add_parts(a, b):
    return pl.pallas_call(
        add_kernel,
        out_shape=jax.ShapeDtypeStruct(a.shape, bf16),
        in_specs=[VMEM, VMEM],
        out_specs=VMEM,
        name="add_parts",
        compiler_params=pltpu.CompilerParams(vmem_limit_bytes=5 * 2**20),
        cost_estimate=COST,
    )(a, b)


def stacked_parts(first_head, heads, query, key, value):
    dim = HEAD_DIM
    parts = []
    for n in range(heads):
        first = (first_head + n) * dim
        parts += [(2 * n * dim, key, first, dim), ((2 * n + 1) * dim, value, first, dim)]
    return parts + [(2 * heads * dim, query, first_head * dim, heads * dim)]


def backward_kernel(
    first_head, heads, blocks, extras, lens_ref, rank_ref, bit_ref, qt_ref, kt_ref, vt_ref,
    near_ref, far_ref, qw_ref, kw_ref, vw_ref, normed_ref, *rest
):
    extra_refs, rest = rest[:extras], rest[extras:]
    width, slots = qt_ref.shape
    shard = slots // blocks
    dim = HEAD_DIM
    out_refs, grad_refs = rest[:blocks], rest[blocks : 2 * blocks]
    joint_ref, sums_ref, own_ref, away_ref = rest[2 * blocks : 2 * blocks + 4]
    kv_ref, q0_ref, og_ref, right_ref, inner_ref, dq_ref, made_ref = rest[-13:-6]
    log_ref = rest[-6]
    row_ref, col_ref = rest[-5:-3]
    turned_ref, rows_ref, copied = rest[-3:]
    fetch = pltpu.make_async_copy(normed_ref, rows_ref, copied)
    fetch.start()
    unit = shard // 2
    rank = rank_ref[0, 0]
    ends = item_ends(lens_ref)
    fill_segments(row_ref, col_ref, shard, rank, ends)
    near = near_ref.shape[2]
    log_ref[:, :, :near] = near_ref[...]
    log_ref[:, :, near:] = far_ref[...]
    zero = jnp.zeros((dim, slots), bf16)
    for n in range(heads):
        part = slice((first_head + n) * dim, (first_head + n + 1) * dim)
        both = jnp.concatenate([kt_ref[part, :], vt_ref[part, :]], axis=0)
        kv_ref[n] = jnp.transpose(both, (1, 0))
        padded = jnp.concatenate([qt_ref[part, :], zero], axis=0)
        q0_ref[n] = jnp.transpose(padded, (1, 0))
        right_ref[n, 0] = padded
        for b in range(blocks):
            grad = grad_refs[b][part, :]
            cols = slice(b * shard, (b + 1) * shard)
            padded = jnp.concatenate([zero[:, :shard], grad], axis=0)
            og_ref[n, cols, :] = jnp.transpose(padded, (1, 0))
            right_ref[n, 1, :, cols] = padded
            inner_ref[n, :, cols] = jnp.sum(
                out_refs[b][part, :].astype(f32) * grad.astype(f32), axis=0, keepdims=True
            )
    dq_ref[...] = jnp.zeros_like(dq_ref)

    def key_block(j, unused):
        at_key = ((j // 2) ^ rank) * 2 + j % 2
        rows = rows_at(at_key, unit)

        def query_block(i, totals):
            at = i ^ rank
            cols = rows_at(at, shard)
            same = col_ref[rows, 0:1] == row_ref[:, cols]
            result = []
            for n in range(heads):
                head = first_head + n
                kv = kv_ref[n, rows, :]
                scores = jnp.dot(kv, right_ref[n, 0, :, cols], preferred_element_type=f32)
                grad_soft = jnp.dot(kv, right_ref[n, 1, :, cols], preferred_element_type=f32)
                soft = jnp.where(same, jnp.exp(scores - log_ref[head, :, cols]), 0.0)
                grad_scores = (soft * (grad_soft - inner_ref[n, :, cols])).astype(bf16)
                total = totals[n] + jnp.dot(
                    soft.astype(bf16), og_ref[n, cols, :], preferred_element_type=f32
                )
                total = total + jnp.dot(
                    grad_scores, q0_ref[n, cols, :], preferred_element_type=f32
                )
                dq_ref[n, :, cols] += jnp.dot(
                    kt_ref[pl.ds(head * dim, dim), rows], grad_scores,
                    preferred_element_type=f32,
                )
                result.append(total)
            return tuple(result)

        low, high = block_span(j * unit, unit, shard, ends)
        start = (jnp.zeros((unit, 2 * dim), f32),) * heads
        totals = lax.fori_loop(low, high, query_block, start)
        for n in range(heads):
            part = slice(2 * dim * n, 2 * dim * (n + 1))
            total = totals[n].astype(bf16)
            joint_ref[rows, part] = total
            turned_ref[part, rows] = jnp.transpose(total, (1, 0))
        return unused

    lax.fori_loop(0, 2 * blocks, key_block, 0)
    dq = (dq_ref[...] * dim ** (-0.5)).astype(bf16).reshape(heads * dim, slots)
    turned_ref[2 * dim * heads :, :] = dq
    joint_ref[:, 2 * dim * heads :] = jnp.transpose(dq, (1, 0))
    fetch.wait()
    made_ref[...] = jnp.dot(turned_ref[...], rows_ref[...], preferred_element_type=f32)
    gains = jnp.zeros((1, rows_ref.shape[1]), f32)
    shifts = jnp.zeros((1, rows_ref.shape[1]), f32)
    for at, weight_ref, first, size in stacked_parts(
        first_head, heads, qw_ref, kw_ref, vw_ref
    ):
        weight = weight_ref[first : first + size, :].astype(f32)
        gains += jnp.sum(weight * made_ref[at : at + size, :], axis=0, keepdims=True)
        total = jnp.sum(turned_ref[at : at + size, :].astype(f32), axis=1, keepdims=True)
        shifts += jnp.sum(weight * total, axis=0, keepdims=True)
    sums_ref[0:1] = gains
    sums_ref[1:2] = shifts
    half = made_ref.shape[0] // 2
    bit = bit_ref[0, 0]
    for part_ref, at in ((own_ref, bit), (away_ref, 1 - bit)):
        part_ref[0:half, :] = made_ref[rows_at(at, half), :].astype(bf16)
        if extras:
            lines = [sums_ref[...] + extra_refs[0][...], extra_refs[1][...]]
            lines.append(jnp.zeros((SUM_ROWS // 2 - 4, gains.shape[1]), f32))
            part_ref[half:, :] = split_rows(jnp.concatenate(lines, axis=0))


def attend_back(
    first_head, heads, extras, lens, rank, bit, qt, kt, vt, logs, weights, normed, outs, grads
):
    slots, width = normed.shape
    blocks = len(outs)
    dim = HEAD_DIM
    cols = 3 * dim * heads
    rows = cols // 2 + (SUM_ROWS if extras else 0)
    return pl.pallas_call(
        functools.partial(backward_kernel, first_head, heads, blocks, len(extras)),
        out_shape=(
            jax.ShapeDtypeStruct((slots, cols), bf16),
            jax.ShapeDtypeStruct((2, width), f32),
        )
        + (jax.ShapeDtypeStruct((rows, width), bf16),) * 2,
        in_specs=[SMEM, SMEM, SMEM]
        + [VMEM] * 8
        + [pl.BlockSpec(memory_space=pl.ANY)]
        + [VMEM] * (len(extras) + 2 * blocks),
        out_specs=(VMEM,) * 4,
        scratch_shapes=[pltpu.VMEM((heads, slots, 2 * dim), bf16)] * 3
        + [
            pltpu.VMEM((heads, 2, 2 * dim, slots), bf16),
            pltpu.VMEM((heads, 1, slots), f32),
            pltpu.VMEM((heads, dim, slots), f32),
            pltpu.VMEM((cols, width), f32),
            pltpu.VMEM((qt.shape[0] // dim, 1, slots), f32),
            pltpu.VMEM((1, slots), jnp.int32),
            pltpu.VMEM((slots, 128), jnp.int32),
            pltpu.VMEM((cols, slots), bf16),
            pltpu.VMEM((slots, width), bf16),
            pltpu.SemaphoreType.DMA,
        ],
        name="attend_back",
        compiler_params=pltpu.CompilerParams(vmem_limit_bytes=60 * 2**20),
        cost_estimate=COST,
    )(lens, rank, bit, qt, kt, vt, *logs, *weights, normed, *extras, *outs, *grads)


def plan_kernel(capacity, lens_ref, rank_ref, routes_ref, order_ref, grad_ref,
                dispatch_ref, slots_ref):
    shard = routes_ref.shape[1]
    first = rank_ref[0, 0] * shard
    ends = item_ends(lens_ref)
    chosen_row = routes_ref[...]
    chosen_col = jnp.transpose(jnp.broadcast_to(chosen_row, (128, shard)), (1, 0))[:, 0:1]
    order_row = order_ref[...]
    order_col = jnp.transpose(jnp.broadcast_to(order_row, (128, shard)), (1, 0))[:, 0:1]
    alive_row = segments_at(
        first + lax.broadcasted_iota(jnp.int32, (1, shard), 1), ends
    ) < len(ends)
    alive_col = segments_at(
        first + lax.broadcasted_iota(jnp.int32, (shard, 1), 0), ends
    ) < len(ends)
    ahead = (chosen_col == chosen_row) & (order_col < order_row) & alive_col
    ranked = jnp.sum(ahead.astype(jnp.int32), axis=0, keepdims=True)
    kept = alive_row & (ranked < capacity)
    slot = jnp.where(kept, chosen_row * capacity + ranked, -1)
    dispatch = (
        lax.broadcasted_iota(jnp.int32, dispatch_ref.shape, 0) == slot
    ).astype(f32).astype(bf16)
    dispatch_ref[...] = dispatch
    slots_ref[...] = jnp.dot(
        dispatch, grad_ref[...], preferred_element_type=f32
    ).astype(bf16)


def plan(lens, rank, routes, order, grads, capacity, experts_all):
    shard, width = grads.shape
    count = experts_all * capacity
    return pl.pallas_call(
        functools.partial(plan_kernel, capacity),
        out_shape=(
            jax.ShapeDtypeStruct((count, shard), bf16),
            jax.ShapeDtypeStruct((count, width), bf16),
        ),
        in_specs=[SMEM, SMEM, VMEM, VMEM, VMEM],
        out_specs=(VMEM, VMEM),
        name="plan",
        cost_estimate=COST,
    )(lens, rank, routes.reshape(1, -1), order, grads)


def across(left, right):
    return lax.dot_general(
        left, right, (((1,), (1,)), ((), ())), preferred_element_type=f32
    )


def middle_kernel(count, rank_ref, tokens_ref, gain_ref, bias_ref, dispatch_ref, *refs):
    head_refs, weight_refs = refs[:count], refs[count : 2 * count]
    residual_ref, rows_ref = refs[2 * count :]
    residual = tokens_ref[...].astype(f32)
    for head_ref, weight_ref in zip(head_refs, weight_refs):
        residual = residual + contract_rows(head_ref[...], weight_ref[...])
    residual_ref[...] = residual
    normed = (normalized(residual) * gain_ref[...][None] + bias_ref[...][None]).astype(bf16)
    rows_ref[...] = jnp.dot(
        dispatch_ref[...], normed, preferred_element_type=f32
    ).astype(bf16)


def middle(rank, tokens, gain, bias, dispatch, heads, weights):
    count, shard = dispatch.shape
    width = tokens.shape[1]
    fixed = lambda array: pl.BlockSpec(array.shape, lambda i, r: (0,) * array.ndim)
    small = [gain, bias, dispatch, *heads, *weights]
    return pl.pallas_call(
        functools.partial(middle_kernel, len(heads)),
        grid_spec=pltpu.PrefetchScalarGridSpec(
            num_scalar_prefetch=1,
            grid=(1,),
            in_specs=[pl.BlockSpec((shard, width), lambda i, r: (r[0], 0))]
            + [fixed(array) for array in small],
            out_specs=(
                pl.BlockSpec((shard, width), lambda i, r: (0, 0)),
                pl.BlockSpec((count, width), lambda i, r: (0, 0)),
            ),
        ),
        out_shape=(
            jax.ShapeDtypeStruct((shard, width), f32),
            jax.ShapeDtypeStruct((count, width), bf16),
        ),
        name="middle",
        cost_estimate=COST,
    )(rank, tokens, *small)


def turn_kernel(
    count, lens_ref, rank_ref, dispatch_ref, back_ref, residual_ref, cotangent_ref,
    gain_ref, *refs
):
    head_refs, weight_refs = refs[:count], refs[count : 2 * count]
    grad_ref, sums_ref, kept_ref, sent_ref = refs[2 * count : 2 * count + 4]
    part_refs = refs[2 * count + 4 :]
    shard = residual_ref.shape[0]
    grad_normed = contract_rows(dispatch_ref[...], back_ref[...])
    values = residual_ref[...]
    centred = values - jnp.mean(values, axis=-1, keepdims=True)
    inverse = lax.rsqrt(jnp.mean(centred * centred, axis=-1, keepdims=True) + EPSILON)
    normed = centred * inverse
    sums_ref[0:1] = jnp.sum(grad_normed * normed, axis=0, keepdims=True)
    sums_ref[1:2] = jnp.sum(grad_normed, axis=0, keepdims=True)
    scaled = grad_normed * gain_ref[...][None]
    grad = cotangent_ref[...].astype(f32) + inverse * (
        scaled
        - jnp.mean(scaled, axis=-1, keepdims=True)
        - normed * jnp.mean(scaled * normed, axis=-1, keepdims=True)
    )
    grad_ref[...] = grad
    low = grad.astype(bf16)
    place = rank_ref[0, 0] * shard + lax.broadcasted_iota(jnp.int32, (1, shard), 1)
    alive = place < item_ends(lens_ref)[-1]
    for weight_ref, part_ref in zip(weight_refs, part_refs):
        part_ref[...] = jnp.where(alive, across(weight_ref[...], low), 0.0).astype(bf16)
    for j, head_ref in enumerate(head_refs):
        made = jnp.dot(head_ref[...], low, preferred_element_type=f32)
        (kept_ref, sent_ref)[j % 2][j // 2] = made.astype(bf16)


def turn(lens, rank, dispatch, back, residual, cotangent, gain, heads, weights):
    shard, width = residual.shape
    cols = weights[0].shape[0]
    count = len(weights)
    return pl.pallas_call(
        functools.partial(turn_kernel, count),
        out_shape=(
            jax.ShapeDtypeStruct((shard, width), f32),
            jax.ShapeDtypeStruct((2, width), f32),
            jax.ShapeDtypeStruct((count // 2, cols, width), bf16),
            jax.ShapeDtypeStruct((count // 2, cols, width), bf16),
        )
        + (jax.ShapeDtypeStruct((cols, shard), bf16),) * count,
        in_specs=[SMEM, SMEM] + [VMEM] * (5 + 2 * count),
        out_specs=(VMEM,) * (4 + count),
        name="turn",
        cost_estimate=COST,
    )(lens, rank, dispatch, back, residual, cotangent, gain, *heads, *weights)


def output_sum_kernel(kept_ref, core_ref, first_ref, near_ref, far_ref):
    cols = near_ref.shape[0]
    total = [
        (kept_ref[j].astype(f32) + core_ref[j].astype(f32)).astype(bf16) for j in range(2)
    ]
    near_ref[...] = total[0]
    far_ref[:cols, :] = total[1]
    far_ref[cols:, :] = first_ref[...]


def output_sums(kept, core, first):
    slots, cols, width = kept.shape
    return pl.pallas_call(
        output_sum_kernel,
        out_shape=(
            jax.ShapeDtypeStruct((cols, width), bf16),
            jax.ShapeDtypeStruct((cols + first.shape[0], width), bf16),
        ),
        in_specs=[VMEM] * 3,
        out_specs=(VMEM, VMEM),
        name="output_sums",
        cost_estimate=LONG,
    )(kept, core, first)


def gelu_parts(values):
    below = 0.5 + 0.5 * lax.erf(values * (0.5**0.5))
    density = jnp.exp(-0.5 * values * values) * (0.5 / jnp.pi) ** 0.5
    return values * below, below + values * density


def part_at(step, parts, rank):
    half = parts // 2
    return (2 * (step % half) + step // half) ^ rank


def expert_kernel(
    parts, rank_ref, in_ref, grad_act_ref, up_ref,
    act_kept_ref, pre_kept_ref, act_sent_ref, pre_sent_ref, mid_ref,
    grads_ref, ups_ref, acts_ref, pres_ref, sum_ref, fetched, stored,
):
    rank = rank_ref[0, 0]
    size = ups_ref.shape[2]
    half = parts // 2

    def fetch(p):
        cols = rows_at(part_at(p, parts, rank), size)
        return (
            pltpu.make_async_copy(up_ref.at[:, cols], ups_ref.at[p], fetched.at[0, p]),
            pltpu.make_async_copy(grad_act_ref.at[:, cols], grads_ref.at[p], fetched.at[1, p]),
        )

    def store(p, act_out_ref, pre_out_ref):
        cols = rows_at(p % half, size)
        return (
            pltpu.make_async_copy(acts_ref.at[p], act_out_ref.at[:, cols], stored.at[0, p]),
            pltpu.make_async_copy(pres_ref.at[p], pre_out_ref.at[:, cols], stored.at[1, p]),
        )

    for p in range(parts):
        for copy in fetch(p):
            copy.start()
    sum_ref[...] = jnp.zeros_like(sum_ref)

    def part(p, unused):
        for copy in fetch(p):
            copy.wait()
        pre = jnp.dot(in_ref[...], ups_ref[p], preferred_element_type=f32)
        act, slope = gelu_parts(pre)
        acts_ref[p] = act.astype(bf16)
        grad_pre = (grads_ref[p].astype(f32) * slope).astype(bf16)
        pres_ref[p] = grad_pre
        sum_ref[...] += across(grad_pre, ups_ref[p])

        @pl.when(p < half)
        def keep():
            for copy in store(p, act_kept_ref, pre_kept_ref):
                copy.start()

        @pl.when(p >= half)
        def send():
            for copy in store(p, act_sent_ref, pre_sent_ref):
                copy.start()

        return unused

    lax.fori_loop(0, parts, part, 0)
    mid_ref[...] = sum_ref[...].astype(bf16)
    for p in range(parts):
        outs = (act_kept_ref, pre_kept_ref) if p < half else (act_sent_ref, pre_sent_ref)
        for copy in store(p, *outs):
            copy.wait()


def expert(rank, rows, grad_act, up, parts):
    count, width = rows.shape
    hidden = up.shape[1]
    size = hidden // parts
    return pl.pallas_call(
        functools.partial(expert_kernel, parts),
        out_shape=(jax.ShapeDtypeStruct((count, hidden // 2), bf16),) * 4
        + (jax.ShapeDtypeStruct((count, width), bf16),),
        in_specs=[SMEM, VMEM, HBM, HBM],
        out_specs=(HBM,) * 4 + (VMEM,),
        scratch_shapes=[
            pltpu.VMEM((parts, count, size), grad_act.dtype),
            pltpu.VMEM((parts, width, size), bf16),
            pltpu.VMEM((parts, count, size), bf16),
            pltpu.VMEM((parts, count, size), bf16),
            pltpu.VMEM((count, width), f32),
            pltpu.SemaphoreType.DMA((2, parts)),
            pltpu.SemaphoreType.DMA((2, parts)),
        ],
        name="expert",
        compiler_params=pltpu.CompilerParams(vmem_limit_bytes=60 * 2**20),
        cost_estimate=COST,
    )(rank.reshape(1, 1), rows, grad_act, up)


def product_kernel(parts, rank_ref, kept_ref, sent_ref, down_ref, out_ref,
                   acts_ref, downs_ref, sum_ref, fetched):
    rank = rank_ref[0, 0]
    size = downs_ref.shape[1]
    half = parts // 2

    def fetch(p):
        rows = rows_at(part_at(p, parts, rank), size)
        source = kept_ref if p < half else sent_ref
        cols = slice((p % half) * size, (p % half + 1) * size)
        return (
            pltpu.make_async_copy(down_ref.at[rows, :], downs_ref.at[p], fetched.at[0, p]),
            pltpu.make_async_copy(source.at[:, cols], acts_ref.at[p], fetched.at[1, p]),
        )

    for p in range(parts):
        for copy in fetch(p):
            copy.start()
    sum_ref[...] = jnp.zeros_like(sum_ref)
    for p in range(parts):
        for copy in fetch(p):
            copy.wait()
        sum_ref[...] += jnp.dot(acts_ref[p], downs_ref[p], preferred_element_type=f32)
    out_ref[...] = sum_ref[...].astype(bf16)


def product(rank, kept, sent, down, parts):
    count = kept.shape[0]
    hidden, width = down.shape
    size = hidden // parts
    return pl.pallas_call(
        functools.partial(product_kernel, parts),
        out_shape=jax.ShapeDtypeStruct((count, width), bf16),
        in_specs=[SMEM, HBM, HBM, HBM],
        out_specs=VMEM,
        scratch_shapes=[
            pltpu.VMEM((parts, count, size), bf16),
            pltpu.VMEM((parts, size, width), bf16),
            pltpu.VMEM((count, width), f32),
            pltpu.SemaphoreType.DMA((2, parts)),
        ],
        name="product",
        cost_estimate=COST,
    )(rank.reshape(1, 1), kept, sent, down)


def weight_kernel(groups, *refs):
    first_ref, second_ref, third_ref, up_ref, down_ref = refs[-5:]
    dup = ddown = 0.0
    for g in range(groups):
        in_ref, grad_ref, act_ref, pre_ref = refs[4 * g : 4 * g + 4]
        dup = dup + contract_rows(in_ref[...], pre_ref[...])
        ddown = ddown + contract_rows(act_ref[...], grad_ref[...])
    cut = first_ref.shape[0]

    @pl.when(pl.program_id(0) == 0)
    def far():
        first_ref[...] = dup[:cut].astype(bf16)
        second_ref[...] = dup[cut:].astype(bf16)
        third_ref[...] = ddown.astype(bf16)

    @pl.when(pl.program_id(0) == 1)
    def near():
        up_ref[...] = dup
        down_ref[...] = ddown


def expert_weights(groups):
    count, width = groups[0][0].shape
    size = groups[0][2].shape[1] // 2
    fixed = pl.BlockSpec((count, width), lambda i: (0, 0))
    columns = pl.BlockSpec((count, size), lambda i: (0, 1 - i))
    half = (width // 2, size)
    shapes = (half, half, (size, width), (width, size), (size, width))
    return pl.pallas_call(
        functools.partial(weight_kernel, len(groups)),
        grid=(2,),
        in_specs=[fixed, fixed, columns, columns] * len(groups),
        out_specs=tuple(pl.BlockSpec(shape, lambda i: (0, 0)) for shape in shapes),
        out_shape=tuple(
            jax.ShapeDtypeStruct(shape, bf16 if k < 3 else f32)
            for k, shape in enumerate(shapes)
        ),
        name="expert_weights",
        compiler_params=pltpu.CompilerParams(vmem_limit_bytes=60 * 2**20),
        cost_estimate=COST,
    )(*[values for group in groups for values in group])


def expert_sum_kernel(
    near_up_ref, near_down_ref, first_ref, second_ref, third_ref, up_ref, down_ref
):
    step = pl.program_id(0)
    half = pl.num_programs(0) // 2

    @pl.when(step < half)
    def upper():
        far = jnp.where(step < half // 2, first_ref[...], second_ref[...]).astype(f32)
        up_ref[...] = near_up_ref[...] + far

    @pl.when(step >= half)
    def lower():
        down_ref[...] = near_down_ref[...] + third_ref[...].astype(f32)


def expert_sums(near_up, near_down, first, second, third):
    count, width = near_up.shape
    steps = 8
    half = steps // 2
    size = count // half
    head = half // 2
    skip = first.shape[0] // size - head
    block = lambda place: pl.BlockSpec((size, width), lambda i: (place(i), 0))
    upper = block(lambda i: jnp.minimum(i, half - 1))
    lower = block(lambda i: jnp.maximum(i - half, 0))
    return pl.pallas_call(
        expert_sum_kernel,
        grid=(steps,),
        out_shape=(jax.ShapeDtypeStruct((count, width), f32),) * 2,
        in_specs=[
            upper,
            lower,
            block(lambda i: jnp.minimum(i, head - 1) + skip),
            block(lambda i: jnp.clip(i - head, 0, head - 1)),
            lower,
        ],
        out_specs=(upper, lower),
        name="expert_sums",
        compiler_params=pltpu.CompilerParams(vmem_limit_bytes=10 * 2**20),
        cost_estimate=COST,
    )(near_up, near_down, first, second, third)


def input_grad_kernel(groups, qw_ref, kw_ref, vw_ref, *refs):
    joint_refs = refs[: len(groups)]
    kept_ref, sent_ref, turned_ref = refs[len(groups) :]
    step = pl.program_id(0)

    @pl.when(step == 0)
    def stack():
        start = 0
        for first_head, heads in groups:
            for at, weight_ref, first, size in stacked_parts(
                first_head, heads, qw_ref, kw_ref, vw_ref
            ):
                turned_ref[start + at : start + at + size, :] = weight_ref[
                    first : first + size, :
                ]
            start += 3 * heads * HEAD_DIM

    total = 0.0
    at = 0
    for joint_ref in joint_refs:
        rows = slice(at, at + joint_ref.shape[1])
        total = total + jnp.dot(
            joint_ref[...], turned_ref[rows, :], preferred_element_type=f32
        )
        at += joint_ref.shape[1]

    @pl.when(step % 2 == 0)
    def keep():
        kept_ref[0] = total.astype(bf16)

    @pl.when(step % 2 == 1)
    def send():
        sent_ref[0] = total.astype(bf16)


def input_grad(groups, weights, joints, first, count, size):
    cols, width = weights[0].shape
    fixed = pl.BlockSpec((cols, width), lambda i: (0, 0))
    return pl.pallas_call(
        functools.partial(input_grad_kernel, groups),
        grid=(count,),
        out_shape=(jax.ShapeDtypeStruct((count // 2, size, width), bf16),) * 2,
        in_specs=[fixed] * 3
        + [
            pl.BlockSpec((size, joint.shape[1]), lambda i: (first + i, 0))
            for joint in joints
        ],
        out_specs=(pl.BlockSpec((1, size, width), lambda i: (i // 2, 0, 0)),) * 2,
        scratch_shapes=[pltpu.VMEM((3 * cols, width), bf16)],
        name="input_grad",
        compiler_params=pltpu.CompilerParams(vmem_limit_bytes=12 * 2**20),
        cost_estimate=COST,
    )(*weights, *joints)


def close_kernel(rank_ref, tokens_ref, gain_ref, grad_ref, *refs):
    *part_refs, out_ref = refs
    grad_in = 0.0
    for part_ref in part_refs:
        grad_in = grad_in + part_ref[...].reshape(out_ref.shape).astype(f32)
    values = tokens_ref[...].astype(f32)
    centred = values - jnp.mean(values, axis=-1, keepdims=True)
    inverse = lax.rsqrt(jnp.mean(centred * centred, axis=-1, keepdims=True) + EPSILON)
    normed = centred * inverse
    scaled = grad_in * gain_ref[...][None]
    out_ref[...] = grad_ref[...] + inverse * (
        scaled
        - jnp.mean(scaled, axis=-1, keepdims=True)
        - normed * jnp.mean(scaled * normed, axis=-1, keepdims=True)
    )


def close(rank, tokens, gain, grad, parts):
    shard, width = grad.shape
    size = shard // 2
    rows = lambda i, r: (i, 0)
    return pl.pallas_call(
        close_kernel,
        grid_spec=pltpu.PrefetchScalarGridSpec(
            num_scalar_prefetch=1,
            grid=(2,),
            in_specs=[
                pl.BlockSpec((size, width), lambda i, r: (2 * r[0] + i, 0)),
                pl.BlockSpec((width,), lambda i, r: (0,)),
                pl.BlockSpec((size, width), rows),
            ]
            + [pl.BlockSpec((1, size, width), lambda i, r: (0, i, 0))] * len(parts),
            out_specs=pl.BlockSpec((size, width), rows),
        ),
        out_shape=jax.ShapeDtypeStruct((shard, width), f32),
        name="close",
        compiler_params=pltpu.CompilerParams(vmem_limit_bytes=12 * 2**20),
        cost_estimate=COST,
    )(rank, tokens, gain, grad, *parts)


def add_low(a, b):
    return (a.astype(f32) + b.astype(f32)).astype(bf16)


def after(value, *others):
    return lax.optimization_barrier((value, *others))[0]


def tie(*values):
    return lax.optimization_barrier(values)


def finish_kernel(groups, bit_ref, *refs):
    pieces, refs = refs[: 2 * len(groups)], refs[2 * len(groups) :]
    query_ref, key_ref, value_ref = refs[:3]
    bit = bit_ref[0, 0]
    for g, ((first_head, heads), whole_ref) in enumerate(zip(groups, refs[3:])):
        half = whole_ref.shape[0] // 2
        for piece_ref, at in ((pieces[2 * g], bit), (pieces[2 * g + 1], 1 - bit)):
            whole_ref[rows_at(at, half), :] = piece_ref[0:half, :].astype(f32)
        for at, target_ref, first, size in stacked_parts(
            first_head, heads, query_ref, key_ref, value_ref
        ):
            target_ref[first : first + size, :] = whole_ref[at : at + size, :]


def finish(groups, bit, pieces):
    width = pieces[0].shape[1]
    cols = sum(heads for first_head, heads in groups) * HEAD_DIM
    return pl.pallas_call(
        functools.partial(finish_kernel, groups),
        out_shape=(jax.ShapeDtypeStruct((cols, width), f32),) * 3,
        in_specs=[SMEM] + [VMEM] * len(pieces),
        out_specs=(VMEM,) * 3,
        scratch_shapes=[
            pltpu.VMEM((3 * heads * HEAD_DIM, width), f32) for first_head, heads in groups
        ],
        name="finish",
        compiler_params=pltpu.CompilerParams(vmem_limit_bytes=10 * 2**20),
        cost_estimate=COST,
    )(bit, *pieces)


def on_device(
    tokens,
    first_gain,
    first_bias,
    query_weight,
    key_weight,
    value_weight,
    output_weight,
    second_gain,
    second_bias,
    expert_up,
    expert_down,
    item_lengths,
    routes,
    slot_order,
    cotangent,
):
    slots_all, width = tokens.shape
    members = lax.axis_size("tensor")
    shard_rows = slots_all // members
    rank = lax.axis_index("tensor")
    sources = lax.axis_size("dp")
    experts_all = sources * expert_up.shape[0]
    capacity = shard_rows // experts_all
    head_cols = query_weight.shape[1]
    heads = head_cols // HEAD_DIM
    up_matrix = expert_up[0]
    down_matrix = expert_down[0]
    rank_cell = rank.astype(jnp.int32).reshape(1, 1)

    def exchange(rows):
        return lax.all_to_all(
            rows.reshape(sources, -1, width), "dp", split_axis=0, concat_axis=0, tiled=True
        ).reshape(-1, width)

    qw, kw, vw = query_weight.T, key_weight.T, value_weight.T

    dispatch, grad_slots = plan(
        item_lengths, rank_cell, routes, slot_order, cotangent, capacity, experts_all
    )
    flat_grad = exchange(grad_slots)
    tokens, grad_slots = tie(tokens, grad_slots)
    normed_in, qt, kt, vt = project(
        rank_cell[0], tokens, first_gain, first_bias, qw, kw, vw, members
    )
    outputs = [output_weight] + [
        swap(output_weight, "tensor", k) for k in range(1, members)
    ]
    far = members // 2
    *far_heads, far_logs = attend(
        item_lengths, rank_cell, qt, kt, vt, members, far, members - far
    )
    far_heads, kt = tie(far_heads, kt)
    far_arrived = [swap(far_heads[j - far], "tensor", j) for j in range(far, members)]
    *near_heads, near_logs = attend(item_lengths, rank_cell, qt, kt, vt, members, 0, far)
    near_heads, far_arrived, outputs = tie(near_heads, far_arrived, outputs)
    own_heads = near_heads + far_heads
    logs = (near_logs, far_logs)
    all_heads = (
        near_heads[:1]
        + [swap(near_heads[j], "tensor", j) for j in range(1, far)]
        + far_arrived
    )
    residual, outgoing = middle(
        rank_cell[0], tokens, second_gain, second_bias, dispatch, all_heads, outputs
    )
    flat_in = exchange(outgoing)

    flat_grad, outgoing = tie(flat_grad, outgoing)
    grad_act = across(flat_grad, down_matrix).astype(bf16)
    near_grads = swap(flat_grad, "tensor", 1)
    flat_in, grad_act, near_grads = tie(flat_in, grad_act, near_grads)
    near_rows = swap(flat_in, "tensor", 1)
    act, grad_pre, act_sent, pre_sent, grad_mid = expert(
        rank_cell[0], flat_in, grad_act, up_matrix, members
    )
    grad_mid, act, near_rows = tie(grad_mid, act, near_rows)
    grad_back = exchange(grad_mid)

    act, act_sent, pre_sent, grad_mid = tie(act, act_sent, pre_sent, grad_mid)
    near_act = swap(act_sent, "tensor", 1)
    near_pre = swap(pre_sent, "tensor", 1)
    made = product(rank_cell[0], act, act_sent, down_matrix, members)
    made, near_act, near_pre = tie(made, near_act, near_pre)
    *expert_far, expert_up_near, expert_down_near = expert_weights(
        [(flat_in, flat_grad, act, grad_pre), (near_rows, near_grads, near_act, near_pre)]
    )
    grad_back, made, expert_far = tie(grad_back, made, expert_far)

    steps = steps_of(members)
    grad_res, sums_second, kept, sent, *grad_heads = turn(
        item_lengths, rank_cell, dispatch, grad_back, residual, cotangent,
        second_gain, all_heads, outputs,
    )
    grad_parts = [grad_heads[0]] + [
        swap(grad_heads[j], "tensor", j) for j in range(1, members)
    ]
    output_near, output_far = output_sums(kept, swap(sent, "tensor", 1), expert_far[0])
    made, grad_heads = tie(made, grad_heads)
    returned = exchange(made)
    grad_parts, output_near, output_far = tie(grad_parts, output_near, output_far)

    bit_cell = (lax.axis_index("dp") & 1).astype(jnp.int32).reshape(1, 1)
    weights = (qw, kw, vw)
    dp_steps = steps_of(sources)
    back = functools.partial(
        attend_back, lens=item_lengths, rank=rank_cell, bit=bit_cell, qt=qt, kt=kt, vt=vt,
        logs=logs, weights=weights, normed=normed_in, outs=own_heads,
    )
    groups = ((0, heads - 1), (heads - 1, 1))
    joint_a, sums_a, own_a, away_a = back(*groups[0], extras=(), grads=grad_parts)
    output_got = swap(output_far, "tensor", 2)
    joint_a, own_a, away_a, output_got, grad_parts, expert_far, returned = tie(
        joint_a, own_a, away_a, output_got, grad_parts, expert_far, returned
    )
    expert_second = swap(expert_far[1], "tensor", 2)
    output_sum = add_low(output_near, output_got[: output_near.shape[0]])
    own_a = add_low(own_a, swap(away_a, "dp", 1))
    output_sum = add_low(output_sum, swap(output_sum, "dp", dp_steps[-1]))
    joint_b, unused, own_b, away_b = back(
        *groups[1], extras=(sums_a, sums_second), grads=grad_parts
    )
    joint_b, own_a, own_b, away_b, output_sum, expert_second, expert_third = tie(
        joint_b, own_a, own_b, away_b, output_sum, expert_second, expert_far[2]
    )

    expert_third = swap(expert_third, "tensor", 2)
    far_kept, far_sent = input_grad(
        groups, weights, (joint_a, joint_b), far, members - far, shard_rows
    )
    near_kept, near_sent = input_grad(
        groups, weights, (joint_a, joint_b), 0, far, shard_rows
    )
    own_b = add_parts(own_b, swap(away_b, "dp", 1))
    far_kept = add_low(far_kept, swap(far_sent, "tensor", 1))
    far_kept, own_b, output_sum, near_sent = tie(far_kept, own_b, output_sum, near_sent)
    near_core = swap(near_sent, "tensor", 1)
    near_far = swap(far_kept, "tensor", 2)
    for step in dp_steps[1:]:
        got_a = swap(own_a, "dp", step)
        own_b = add_parts(own_b, swap(own_b, "dp", step))
        own_a = add_low(own_a, got_a if step == dp_steps[1] else after(got_a, own_b))
    own_b, near_far, expert_third, returned = tie(
        own_b, near_far, expert_third, returned
    )
    up_grad, down_grad = expert_sums(
        expert_up_near, expert_down_near, output_got, expert_second, expert_third
    )
    norm_sums = own_b[-SUM_ROWS:].astype(f32)
    norm_sums = norm_sums[: SUM_ROWS // 2] + norm_sums[SUM_ROWS // 2 :]
    for step in steps:
        norm_sums = norm_sums + swap(norm_sums, "tensor", step)
    pieces = (own_a, swap(own_a, "dp", 1), own_b, swap(own_b, "dp", 1))
    token_grad = close(
        rank_cell[0], tokens, first_gain, grad_res, (near_kept, near_core, near_far)
    )
    for step in dp_steps[:-1]:
        output_sum = add_low(output_sum, swap(output_sum, "dp", step))
    block_out = residual + contract_rows(dispatch, returned)
    query_grad, key_grad, value_grad = finish(groups, bit_cell, pieces)
    return (
        block_out,
        token_grad,
        (norm_sums[0] - first_bias * norm_sums[1]) / first_gain,
        norm_sums[1],
        query_grad.T,
        key_grad.T,
        value_grad.T,
        output_sum.astype(f32),
        norm_sums[2],
        norm_sums[3],
        up_grad[None],
        down_grad[None],
    )


def solution(mesh):
    in_specs = (
        P("dp", None),
        P(),
        P(),
        P(None, "tensor"),
        P(None, "tensor"),
        P(None, "tensor"),
        P("tensor", None),
        P(),
        P(),
        P("dp", None, None),
        P("dp", None, None),
        P("dp", None),
        P(("dp", "tensor"), None),
        P(("dp", "tensor"), None),
        P(("dp", "tensor"), None),
    )
    out_specs = (
        P(("dp", "tensor"), None),
        P(("dp", "tensor"), None),
        P(),
        P(),
        P(None, "tensor"),
        P(None, "tensor"),
        P(None, "tensor"),
        P("tensor", None),
        P(),
        P(),
        P("dp", None, "tensor"),
        P("dp", "tensor", None),
    )
    return jax.shard_map(
        on_device, mesh=mesh, in_specs=in_specs, out_specs=out_specs, check_vma=False
    )
```

```python
import functools

import jax
import jax.numpy as jnp
from jax import lax
from jax.experimental import pallas as pl
from jax.experimental.pallas import tpu as pltpu
from jax.sharding import PartitionSpec as P

HEAD_DIM = 64
EPSILON = 1e-05
NEGATIVE = -1e30
f32 = jnp.float32
bf16 = jnp.bfloat16
VMEM = pl.BlockSpec(memory_space=pltpu.VMEM)
HBM = pl.BlockSpec(memory_space=pltpu.MemorySpace.HBM)
SMEM = pl.BlockSpec(memory_space=pltpu.SMEM)
SUM_ROWS = 16
COST = pl.CostEstimate(flops=2**20, bytes_accessed=2**20, transcendentals=0)
LONG = pl.CostEstimate(flops=2**34, bytes_accessed=2**24, transcendentals=0)


def layer_norm(values, gain, shift):
    average = jnp.mean(values, axis=-1, keepdims=True)
    centred = values - average
    variance = jnp.mean(centred * centred, axis=-1, keepdims=True)
    return centred * lax.rsqrt(variance + EPSILON) * gain + shift


def contract_rows(left, right):
    return lax.dot_general(
        left, right, (((0,), (0,)), ((), ())), preferred_element_type=f32
    )


def swap(values, axis, step):
    count = lax.axis_size(axis)
    return lax.ppermute(values, axis, [(i, i ^ step) for i in range(count)])


def steps_of(count):
    steps = []
    step = 1
    while step < count:
        steps.append(step)
        step *= 2
    return steps


def normalized(values):
    average = jnp.mean(values, axis=-1, keepdims=True)
    centred = values - average
    variance = jnp.mean(centred * centred, axis=-1, keepdims=True)
    return centred * lax.rsqrt(variance + EPSILON)


def project_kernel(
    rank_ref, tokens_ref, gain_ref, bias_ref, qw_ref, kw_ref, vw_ref,
    normed_ref, qt_ref, kt_ref, vt_ref,
):
    values = tokens_ref[...].astype(f32)
    normed = (normalized(values) * gain_ref[...][None] + bias_ref[...][None]).astype(bf16)
    normed_ref[...] = normed
    for weight_ref, out_ref, factor in (
        (qw_ref, qt_ref, HEAD_DIM ** (-0.5)), (kw_ref, kt_ref, None), (vw_ref, vt_ref, None)
    ):
        made = lax.dot_general(
            weight_ref[...], normed, (((1,), (1,)), ((), ())), preferred_element_type=f32
        ).astype(bf16)
        if factor is not None:
            made = made * jnp.asarray(factor, bf16)
        out_ref[...] = made


def project(rank, tokens, gain, bias, qw, kw, vw, blocks):
    slots, width = tokens.shape
    cols = qw.shape[0]
    size = slots // blocks
    fixed = lambda i, r: (0, 0)
    line = pl.BlockSpec((width,), lambda i, r: (0,))
    return pl.pallas_call(
        project_kernel,
        grid_spec=pltpu.PrefetchScalarGridSpec(
            num_scalar_prefetch=1,
            grid=(blocks,),
            in_specs=[
                pl.BlockSpec((size, width), lambda i, r: (i ^ r[0], 0)),
                line,
                line,
                pl.BlockSpec((cols, width), fixed),
                pl.BlockSpec((cols, width), fixed),
                pl.BlockSpec((cols, width), fixed),
            ],
            out_specs=(
                pl.BlockSpec((size, width), lambda i, r: (i, 0)),
                pl.BlockSpec((cols, size), lambda i, r: (0, i)),
                pl.BlockSpec((cols, size), lambda i, r: (0, i)),
                pl.BlockSpec((cols, size), lambda i, r: (0, i)),
            ),
        ),
        out_shape=(jax.ShapeDtypeStruct((slots, width), bf16),)
        + (jax.ShapeDtypeStruct((cols, slots), bf16),) * 3,
        name="project",
        cost_estimate=COST,
    )(rank, tokens, gain, bias, qw, kw, vw)


def item_ends(lens_ref):
    ends = []
    total = jnp.int32(0)
    for i in range(lens_ref.shape[1]):
        total = total + lens_ref[0, i]
        ends.append(total)
    return ends


def segments_at(place, ends):
    segment = jnp.zeros_like(place)
    for end in ends:
        segment = segment + (place >= end).astype(jnp.int32)
    return segment


def block_span(first, size, unit, ends):
    last = jnp.minimum(first + size, ends[-1]) - 1
    low = jnp.int32(0)
    high = ends[-1]
    for end in ends:
        low = jnp.where(first >= end, end, low)
    for end in reversed(ends):
        high = jnp.where(last < end, end, high)
    empty = first >= ends[-1]
    low_block = jnp.where(empty, 0, low // unit)
    high_block = jnp.where(empty, 0, (high + unit - 1) // unit)
    return low_block, high_block


def rows_at(block, size):
    return pl.ds(pl.multiple_of(block * size, size), size)


def fill_segments(row_ref, col_ref, shard, rank, ends):
    slots = row_ref.shape[1]
    at = lax.broadcasted_iota(jnp.int32, (1, slots), 1)
    place = ((at // shard) ^ rank) * shard + at % shard
    segments = segments_at(place, ends)
    row_ref[...] = segments
    col_ref[...] = jnp.transpose(jnp.broadcast_to(segments, (128, slots)), (1, 0))


def block_bias(row_ref, col_ref, rows, cols):
    return jnp.where(col_ref[rows, 0:1] == row_ref[:, cols], 0.0, NEGATIVE)


def lane_masked(values, head):
    lane = lax.broadcasted_iota(jnp.int32, values.shape, 1)
    inside = (lane >= head * HEAD_DIM) & (lane < (head + 1) * HEAD_DIM)
    return jnp.where(inside, values, jnp.zeros_like(values))


def forward_kernel(
    first, blocks, lens_ref, rank_ref, qt_ref, kt_ref, vt_ref, *refs
):
    *out_refs, log_ref, masked_ref, out_ref, row_ref, col_ref, score_ref = refs
    count, width, size = out_ref.shape
    heads = width // HEAD_DIM
    shard = size
    rank = rank_ref[0, 0]
    ends = item_ends(lens_ref)
    fill_segments(row_ref, col_ref, shard, rank, ends)
    keys = jnp.transpose(kt_ref[...], (1, 0))
    for h in range(heads):
        masked_ref[h] = lane_masked(keys, h)

    def query_block(b, unused):
        at = first + b
        i = at ^ rank
        cols = rows_at(at, size)
        queries = qt_ref[:, cols]

        def score_block(j, carry):
            rows = rows_at(j ^ rank, shard)
            bias = block_bias(row_ref, col_ref, rows, cols)
            result = []
            for h in range(heads):
                scores = jnp.dot(
                    masked_ref[h, rows, :], queries, preferred_element_type=f32
                )
                scores = scores + bias
                score_ref[h, rows_at(j, shard), :] = scores
                part = jnp.max(scores.reshape(-1, 8, size), axis=0)
                result.append(jnp.maximum(carry[h], part))
            return tuple(result)

        low, high = block_span(i * size, size, shard, ends)
        peaks = lax.fori_loop(
            low, high, score_block, (jnp.full((8, size), NEGATIVE, f32),) * heads
        )
        peaks = [jnp.max(peak, axis=0, keepdims=True) for peak in peaks]

        def key_block(j, carry):
            rows = rows_at(j ^ rank, shard)
            result = []
            for h in range(heads):
                summed, total = carry[h]
                soft = jnp.exp(score_ref[h, rows_at(j, shard), :] - peaks[h])
                summed = summed + jnp.sum(soft.reshape(-1, 8, size), axis=0)
                total = total + jnp.dot(
                    vt_ref[pl.ds(h * HEAD_DIM, HEAD_DIM), rows],
                    soft.astype(bf16),
                    preferred_element_type=f32,
                )
                result.append((summed, total))
            return tuple(result)

        start = ((jnp.zeros((8, size), f32), jnp.zeros((HEAD_DIM, size), f32)),) * heads
        done = lax.fori_loop(low, high, key_block, start)
        live = row_ref[:, cols] < len(ends)
        for h in range(heads):
            summed, total = done[h]
            summed = jnp.sum(summed, axis=0, keepdims=True)
            highest = peaks[h]
            summed = jnp.where(live, summed, 1.0)
            result = jnp.where(live, total / summed, 0.0).astype(bf16)
            logs = jnp.where(live, highest + jnp.log(summed), -NEGATIVE)
            out_ref[b, pl.ds(h * HEAD_DIM, HEAD_DIM), :] = result
            log_ref[h, :, rows_at(b, size)] = logs
        return unused

    lax.fori_loop(0, count, query_block, 0)
    for b in range(count):
        out_refs[b][...] = out_ref[b]


def attend(lens, rank, qt, kt, vt, blocks, first, count):
    width, slots = qt.shape
    size = slots // blocks
    heads = width // HEAD_DIM
    return pl.pallas_call(
        functools.partial(forward_kernel, first, blocks),
        out_shape=(jax.ShapeDtypeStruct((width, size), bf16),) * count
        + (jax.ShapeDtypeStruct((heads, 1, count * size), f32),),
        in_specs=[SMEM, SMEM, VMEM, VMEM, VMEM],
        out_specs=(VMEM,) * (count + 1),
        scratch_shapes=[
            pltpu.VMEM((heads, slots, width), bf16),
            pltpu.VMEM((count, width, size), bf16),
            pltpu.VMEM((1, slots), jnp.int32),
            pltpu.VMEM((slots, 128), jnp.int32),
            pltpu.VMEM((heads, slots, size), f32),
        ],
        name="attend",
        compiler_params=pltpu.CompilerParams(vmem_limit_bytes=60 * 2**20),
        cost_estimate=COST,
    )(lens, rank, qt, kt, vt)


def split_rows(values):
    high = values.astype(bf16)
    return jnp.concatenate([high, (values - high.astype(f32)).astype(bf16)], axis=0)


def add_kernel(a_ref, b_ref, out_ref):
    half = out_ref.shape[0] - SUM_ROWS
    line = SUM_ROWS // 2
    total = a_ref[...].astype(f32) + b_ref[...].astype(f32)
    out_ref[:half, :] = total[:half].astype(bf16)
    out_ref[half:, :] = split_rows(total[half : half + line] + total[half + line :])


def add_parts(a, b):
    return pl.pallas_call(
        add_kernel,
        out_shape=jax.ShapeDtypeStruct(a.shape, bf16),
        in_specs=[VMEM, VMEM],
        out_specs=VMEM,
        name="add_parts",
        compiler_params=pltpu.CompilerParams(vmem_limit_bytes=5 * 2**20),
        cost_estimate=COST,
    )(a, b)


def stacked_parts(first_head, heads, query, key, value):
    dim = HEAD_DIM
    parts = []
    for n in range(heads):
        first = (first_head + n) * dim
        parts += [(2 * n * dim, key, first, dim), ((2 * n + 1) * dim, value, first, dim)]
    return parts + [(2 * heads * dim, query, first_head * dim, heads * dim)]


def backward_kernel(
    first_head, heads, blocks, extras, lens_ref, rank_ref, bit_ref, qt_ref, kt_ref, vt_ref,
    near_ref, far_ref, qw_ref, kw_ref, vw_ref, normed_ref, *rest
):
    extra_refs, rest = rest[:extras], rest[extras:]
    width, slots = qt_ref.shape
    shard = slots // blocks
    dim = HEAD_DIM
    out_refs, grad_refs = rest[:blocks], rest[blocks : 2 * blocks]
    joint_ref, sums_ref, own_ref, away_ref = rest[2 * blocks : 2 * blocks + 4]
    kv_ref, q0_ref, og_ref, right_ref, inner_ref, dq_ref, made_ref = rest[-13:-6]
    log_ref = rest[-6]
    row_ref, col_ref = rest[-5:-3]
    turned_ref, rows_ref, copied = rest[-3:]
    fetch = pltpu.make_async_copy(normed_ref, rows_ref, copied)
    fetch.start()
    unit = shard // 2
    rank = rank_ref[0, 0]
    ends = item_ends(lens_ref)
    fill_segments(row_ref, col_ref, shard, rank, ends)
    near = near_ref.shape[2]
    log_ref[:, :, :near] = near_ref[...]
    log_ref[:, :, near:] = far_ref[...]
    zero = jnp.zeros((dim, slots), bf16)
    for n in range(heads):
        part = slice((first_head + n) * dim, (first_head + n + 1) * dim)
        both = jnp.concatenate([kt_ref[part, :], vt_ref[part, :]], axis=0)
        kv_ref[n] = jnp.transpose(both, (1, 0))
        padded = jnp.concatenate([qt_ref[part, :], zero], axis=0)
        q0_ref[n] = jnp.transpose(padded, (1, 0))
        right_ref[n, 0] = padded
        for b in range(blocks):
            grad = grad_refs[b][part, :]
            cols = slice(b * shard, (b + 1) * shard)
            padded = jnp.concatenate([zero[:, :shard], grad], axis=0)
            og_ref[n, cols, :] = jnp.transpose(padded, (1, 0))
            right_ref[n, 1, :, cols] = padded
            inner_ref[n, :, cols] = jnp.sum(
                out_refs[b][part, :].astype(f32) * grad.astype(f32), axis=0, keepdims=True
            )
    dq_ref[...] = jnp.zeros_like(dq_ref)

    def key_block(j, unused):
        at_key = ((j // 2) ^ rank) * 2 + j % 2
        rows = rows_at(at_key, unit)

        def query_block(i, totals):
            at = i ^ rank
            cols = rows_at(at, shard)
            same = col_ref[rows, 0:1] == row_ref[:, cols]
            result = []
            for n in range(heads):
                head = first_head + n
                kv = kv_ref[n, rows, :]
                scores = jnp.dot(kv, right_ref[n, 0, :, cols], preferred_element_type=f32)
                grad_soft = jnp.dot(kv, right_ref[n, 1, :, cols], preferred_element_type=f32)
                soft = jnp.where(same, jnp.exp(scores - log_ref[head, :, cols]), 0.0)
                grad_scores = (soft * (grad_soft - inner_ref[n, :, cols])).astype(bf16)
                total = totals[n] + jnp.dot(
                    soft.astype(bf16), og_ref[n, cols, :], preferred_element_type=f32
                )
                total = total + jnp.dot(
                    grad_scores, q0_ref[n, cols, :], preferred_element_type=f32
                )
                dq_ref[n, :, cols] += jnp.dot(
                    kt_ref[pl.ds(head * dim, dim), rows], grad_scores,
                    preferred_element_type=f32,
                )
                result.append(total)
            return tuple(result)

        low, high = block_span(j * unit, unit, shard, ends)
        start = (jnp.zeros((unit, 2 * dim), f32),) * heads
        totals = lax.fori_loop(low, high, query_block, start)
        for n in range(heads):
            part = slice(2 * dim * n, 2 * dim * (n + 1))
            total = totals[n].astype(bf16)
            joint_ref[rows, part] = total
            turned_ref[part, rows] = jnp.transpose(total, (1, 0))
        return unused

    lax.fori_loop(0, 2 * blocks, key_block, 0)
    dq = (dq_ref[...] * dim ** (-0.5)).astype(bf16).reshape(heads * dim, slots)
    turned_ref[2 * dim * heads :, :] = dq
    joint_ref[:, 2 * dim * heads :] = jnp.transpose(dq, (1, 0))
    fetch.wait()
    made_ref[...] = jnp.dot(turned_ref[...], rows_ref[...], preferred_element_type=f32)
    gains = jnp.zeros((1, rows_ref.shape[1]), f32)
    shifts = jnp.zeros((1, rows_ref.shape[1]), f32)
    for at, weight_ref, first, size in stacked_parts(
        first_head, heads, qw_ref, kw_ref, vw_ref
    ):
        weight = weight_ref[first : first + size, :].astype(f32)
        gains += jnp.sum(weight * made_ref[at : at + size, :], axis=0, keepdims=True)
        total = jnp.sum(turned_ref[at : at + size, :].astype(f32), axis=1, keepdims=True)
        shifts += jnp.sum(weight * total, axis=0, keepdims=True)
    sums_ref[0:1] = gains
    sums_ref[1:2] = shifts
    half = made_ref.shape[0] // 2
    bit = bit_ref[0, 0]
    for part_ref, at in ((own_ref, bit), (away_ref, 1 - bit)):
        part_ref[0:half, :] = made_ref[rows_at(at, half), :].astype(bf16)
        if extras:
            lines = [sums_ref[...] + extra_refs[0][...], extra_refs[1][...]]
            lines.append(jnp.zeros((SUM_ROWS // 2 - 4, gains.shape[1]), f32))
            part_ref[half:, :] = split_rows(jnp.concatenate(lines, axis=0))


def attend_back(
    first_head, heads, extras, lens, rank, bit, qt, kt, vt, logs, weights, normed, outs, grads
):
    slots, width = normed.shape
    blocks = len(outs)
    dim = HEAD_DIM
    cols = 3 * dim * heads
    rows = cols // 2 + (SUM_ROWS if extras else 0)
    return pl.pallas_call(
        functools.partial(backward_kernel, first_head, heads, blocks, len(extras)),
        out_shape=(
            jax.ShapeDtypeStruct((slots, cols), bf16),
            jax.ShapeDtypeStruct((2, width), f32),
        )
        + (jax.ShapeDtypeStruct((rows, width), bf16),) * 2,
        in_specs=[SMEM, SMEM, SMEM]
        + [VMEM] * 8
        + [pl.BlockSpec(memory_space=pl.ANY)]
        + [VMEM] * (len(extras) + 2 * blocks),
        out_specs=(VMEM,) * 4,
        scratch_shapes=[pltpu.VMEM((heads, slots, 2 * dim), bf16)] * 3
        + [
            pltpu.VMEM((heads, 2, 2 * dim, slots), bf16),
            pltpu.VMEM((heads, 1, slots), f32),
            pltpu.VMEM((heads, dim, slots), f32),
            pltpu.VMEM((cols, width), f32),
            pltpu.VMEM((qt.shape[0] // dim, 1, slots), f32),
            pltpu.VMEM((1, slots), jnp.int32),
            pltpu.VMEM((slots, 128), jnp.int32),
            pltpu.VMEM((cols, slots), bf16),
            pltpu.VMEM((slots, width), bf16),
            pltpu.SemaphoreType.DMA,
        ],
        name="attend_back",
        compiler_params=pltpu.CompilerParams(vmem_limit_bytes=60 * 2**20),
        cost_estimate=COST,
    )(lens, rank, bit, qt, kt, vt, *logs, *weights, normed, *extras, *outs, *grads)


def plan_kernel(capacity, lens_ref, rank_ref, routes_ref, order_ref, grad_ref,
                dispatch_ref, slots_ref):
    shard = routes_ref.shape[1]
    first = rank_ref[0, 0] * shard
    ends = item_ends(lens_ref)
    chosen_row = routes_ref[...]
    chosen_col = jnp.transpose(jnp.broadcast_to(chosen_row, (128, shard)), (1, 0))[:, 0:1]
    order_row = order_ref[...]
    order_col = jnp.transpose(jnp.broadcast_to(order_row, (128, shard)), (1, 0))[:, 0:1]
    alive_row = segments_at(
        first + lax.broadcasted_iota(jnp.int32, (1, shard), 1), ends
    ) < len(ends)
    alive_col = segments_at(
        first + lax.broadcasted_iota(jnp.int32, (shard, 1), 0), ends
    ) < len(ends)
    ahead = (chosen_col == chosen_row) & (order_col < order_row) & alive_col
    ranked = jnp.sum(ahead.astype(jnp.int32), axis=0, keepdims=True)
    kept = alive_row & (ranked < capacity)
    slot = jnp.where(kept, chosen_row * capacity + ranked, -1)
    dispatch = (
        lax.broadcasted_iota(jnp.int32, dispatch_ref.shape, 0) == slot
    ).astype(f32).astype(bf16)
    dispatch_ref[...] = dispatch
    slots_ref[...] = jnp.dot(
        dispatch, grad_ref[...], preferred_element_type=f32
    ).astype(bf16)


def plan(lens, rank, routes, order, grads, capacity, experts_all):
    shard, width = grads.shape
    count = experts_all * capacity
    return pl.pallas_call(
        functools.partial(plan_kernel, capacity),
        out_shape=(
            jax.ShapeDtypeStruct((count, shard), bf16),
            jax.ShapeDtypeStruct((count, width), bf16),
        ),
        in_specs=[SMEM, SMEM, VMEM, VMEM, VMEM],
        out_specs=(VMEM, VMEM),
        name="plan",
        cost_estimate=COST,
    )(lens, rank, routes.reshape(1, -1), order, grads)


def across(left, right):
    return lax.dot_general(
        left, right, (((1,), (1,)), ((), ())), preferred_element_type=f32
    )


def middle_kernel(count, rank_ref, tokens_ref, gain_ref, bias_ref, dispatch_ref, *refs):
    head_refs, weight_refs = refs[:count], refs[count : 2 * count]
    residual_ref, rows_ref = refs[2 * count :]
    residual = tokens_ref[...].astype(f32)
    for head_ref, weight_ref in zip(head_refs, weight_refs):
        residual = residual + contract_rows(head_ref[...], weight_ref[...])
    residual_ref[...] = residual
    normed = (normalized(residual) * gain_ref[...][None] + bias_ref[...][None]).astype(bf16)
    rows_ref[...] = jnp.dot(
        dispatch_ref[...], normed, preferred_element_type=f32
    ).astype(bf16)


def middle(rank, tokens, gain, bias, dispatch, heads, weights):
    count, shard = dispatch.shape
    width = tokens.shape[1]
    fixed = lambda array: pl.BlockSpec(array.shape, lambda i, r: (0,) * array.ndim)
    small = [gain, bias, dispatch, *heads, *weights]
    return pl.pallas_call(
        functools.partial(middle_kernel, len(heads)),
        grid_spec=pltpu.PrefetchScalarGridSpec(
            num_scalar_prefetch=1,
            grid=(1,),
            in_specs=[pl.BlockSpec((shard, width), lambda i, r: (r[0], 0))]
            + [fixed(array) for array in small],
            out_specs=(
                pl.BlockSpec((shard, width), lambda i, r: (0, 0)),
                pl.BlockSpec((count, width), lambda i, r: (0, 0)),
            ),
        ),
        out_shape=(
            jax.ShapeDtypeStruct((shard, width), f32),
            jax.ShapeDtypeStruct((count, width), bf16),
        ),
        name="middle",
        cost_estimate=COST,
    )(rank, tokens, *small)


def turn_kernel(
    count, lens_ref, rank_ref, dispatch_ref, back_ref, residual_ref, cotangent_ref,
    gain_ref, *refs
):
    head_refs, weight_refs = refs[:count], refs[count : 2 * count]
    grad_ref, sums_ref, kept_ref, sent_ref = refs[2 * count : 2 * count + 4]
    part_refs = refs[2 * count + 4 :]
    shard = residual_ref.shape[0]
    grad_normed = contract_rows(dispatch_ref[...], back_ref[...])
    values = residual_ref[...]
    centred = values - jnp.mean(values, axis=-1, keepdims=True)
    inverse = lax.rsqrt(jnp.mean(centred * centred, axis=-1, keepdims=True) + EPSILON)
    normed = centred * inverse
    sums_ref[0:1] = jnp.sum(grad_normed * normed, axis=0, keepdims=True)
    sums_ref[1:2] = jnp.sum(grad_normed, axis=0, keepdims=True)
    scaled = grad_normed * gain_ref[...][None]
    grad = cotangent_ref[...].astype(f32) + inverse * (
        scaled
        - jnp.mean(scaled, axis=-1, keepdims=True)
        - normed * jnp.mean(scaled * normed, axis=-1, keepdims=True)
    )
    grad_ref[...] = grad
    low = grad.astype(bf16)
    place = rank_ref[0, 0] * shard + lax.broadcasted_iota(jnp.int32, (1, shard), 1)
    alive = place < item_ends(lens_ref)[-1]
    for weight_ref, part_ref in zip(weight_refs, part_refs):
        part_ref[...] = jnp.where(alive, across(weight_ref[...], low), 0.0).astype(bf16)
    for j, head_ref in enumerate(head_refs):
        made = jnp.dot(head_ref[...], low, preferred_element_type=f32)
        (kept_ref, sent_ref)[j % 2][j // 2] = made.astype(bf16)


def turn(lens, rank, dispatch, back, residual, cotangent, gain, heads, weights):
    shard, width = residual.shape
    cols = weights[0].shape[0]
    count = len(weights)
    return pl.pallas_call(
        functools.partial(turn_kernel, count),
        out_shape=(
            jax.ShapeDtypeStruct((shard, width), f32),
            jax.ShapeDtypeStruct((2, width), f32),
            jax.ShapeDtypeStruct((count // 2, cols, width), bf16),
            jax.ShapeDtypeStruct((count // 2, cols, width), bf16),
        )
        + (jax.ShapeDtypeStruct((cols, shard), bf16),) * count,
        in_specs=[SMEM, SMEM] + [VMEM] * (5 + 2 * count),
        out_specs=(VMEM,) * (4 + count),
        name="turn",
        cost_estimate=COST,
    )(lens, rank, dispatch, back, residual, cotangent, gain, *heads, *weights)


def output_sum_kernel(kept_ref, core_ref, first_ref, near_ref, far_ref):
    cols = near_ref.shape[0]
    total = [
        (kept_ref[j].astype(f32) + core_ref[j].astype(f32)).astype(bf16) for j in range(2)
    ]
    near_ref[...] = total[0]
    far_ref[:cols, :] = total[1]
    far_ref[cols:, :] = first_ref[...]


def output_sums(kept, core, first):
    slots, cols, width = kept.shape
    return pl.pallas_call(
        output_sum_kernel,
        out_shape=(
            jax.ShapeDtypeStruct((cols, width), bf16),
            jax.ShapeDtypeStruct((cols + first.shape[0], width), bf16),
        ),
        in_specs=[VMEM] * 3,
        out_specs=(VMEM, VMEM),
        name="output_sums",
        cost_estimate=LONG,
    )(kept, core, first)


def gelu_parts(values):
    below = 0.5 + 0.5 * lax.erf(values * (0.5**0.5))
    density = jnp.exp(-0.5 * values * values) * (0.5 / jnp.pi) ** 0.5
    return values * below, below + values * density


def part_at(step, parts, rank):
    half = parts // 2
    return (2 * (step % half) + step // half) ^ rank


def activation_kernel(grad_ref, down_ref, out_ref):
    out_ref[...] = across(grad_ref[...], down_ref[...]).astype(bf16)


def activation_grads(grads, down, parts):
    count, width = grads.shape
    hidden = down.shape[0]
    size = hidden // parts
    return pl.pallas_call(
        activation_kernel,
        grid=(parts,),
        out_shape=jax.ShapeDtypeStruct((count, hidden), bf16),
        in_specs=[
            pl.BlockSpec((count, width), lambda i: (0, 0)),
            pl.BlockSpec((size, width), lambda i: (i, 0)),
        ],
        out_specs=pl.BlockSpec((count, size), lambda i: (0, i)),
        name="activation_grads",
        cost_estimate=COST,
    )(grads, down)


def expert_kernel(
    parts, rank_ref, in_ref, grad_act_ref, up_ref,
    act_kept_ref, pre_kept_ref, act_sent_ref, pre_sent_ref, mid_ref,
    grads_ref, ups_ref, acts_ref, pres_ref, sum_ref, fetched, stored,
):
    rank = rank_ref[0, 0]
    size = ups_ref.shape[2]
    half = parts // 2

    def fetch(p):
        cols = rows_at(part_at(p, parts, rank), size)
        return (
            pltpu.make_async_copy(up_ref.at[:, cols], ups_ref.at[p], fetched.at[0, p]),
            pltpu.make_async_copy(grad_act_ref.at[:, cols], grads_ref.at[p], fetched.at[1, p]),
        )

    def store(p, act_out_ref, pre_out_ref):
        cols = rows_at(p % half, size)
        return (
            pltpu.make_async_copy(acts_ref.at[p], act_out_ref.at[:, cols], stored.at[0, p]),
            pltpu.make_async_copy(pres_ref.at[p], pre_out_ref.at[:, cols], stored.at[1, p]),
        )

    for p in range(parts):
        for copy in fetch(p):
            copy.start()
    sum_ref[...] = jnp.zeros_like(sum_ref)

    def part(p, unused):
        for copy in fetch(p):
            copy.wait()
        pre = jnp.dot(in_ref[...], ups_ref[p], preferred_element_type=f32)
        act, slope = gelu_parts(pre)
        acts_ref[p] = act.astype(bf16)
        grad_pre = (grads_ref[p].astype(f32) * slope).astype(bf16)
        pres_ref[p] = grad_pre
        sum_ref[...] += across(grad_pre, ups_ref[p])

        @pl.when(p < half)
        def keep():
            for copy in store(p, act_kept_ref, pre_kept_ref):
                copy.start()

        @pl.when(p >= half)
        def send():
            for copy in store(p, act_sent_ref, pre_sent_ref):
                copy.start()

        return unused

    lax.fori_loop(0, parts, part, 0)
    mid_ref[...] = sum_ref[...].astype(bf16)
    for p in range(parts):
        outs = (act_kept_ref, pre_kept_ref) if p < half else (act_sent_ref, pre_sent_ref)
        for copy in store(p, *outs):
            copy.wait()


def expert(rank, rows, grad_act, up, parts):
    count, width = rows.shape
    hidden = up.shape[1]
    size = hidden // parts
    return pl.pallas_call(
        functools.partial(expert_kernel, parts),
        out_shape=(jax.ShapeDtypeStruct((count, hidden // 2), bf16),) * 4
        + (jax.ShapeDtypeStruct((count, width), bf16),),
        in_specs=[SMEM, VMEM, HBM, HBM],
        out_specs=(HBM,) * 4 + (VMEM,),
        scratch_shapes=[
            pltpu.VMEM((parts, count, size), grad_act.dtype),
            pltpu.VMEM((parts, width, size), bf16),
            pltpu.VMEM((parts, count, size), bf16),
            pltpu.VMEM((parts, count, size), bf16),
            pltpu.VMEM((count, width), f32),
            pltpu.SemaphoreType.DMA((2, parts)),
            pltpu.SemaphoreType.DMA((2, parts)),
        ],
        name="expert",
        compiler_params=pltpu.CompilerParams(vmem_limit_bytes=60 * 2**20),
        cost_estimate=COST,
    )(rank.reshape(1, 1), rows, grad_act, up)


def product_kernel(parts, rank_ref, kept_ref, sent_ref, down_ref, out_ref,
                   acts_ref, downs_ref, sum_ref, fetched):
    rank = rank_ref[0, 0]
    size = downs_ref.shape[1]
    half = parts // 2

    def fetch(p):
        rows = rows_at(part_at(p, parts, rank), size)
        source = kept_ref if p < half else sent_ref
        cols = slice((p % half) * size, (p % half + 1) * size)
        return (
            pltpu.make_async_copy(down_ref.at[rows, :], downs_ref.at[p], fetched.at[0, p]),
            pltpu.make_async_copy(source.at[:, cols], acts_ref.at[p], fetched.at[1, p]),
        )

    for p in range(parts):
        for copy in fetch(p):
            copy.start()
    sum_ref[...] = jnp.zeros_like(sum_ref)
    for p in range(parts):
        for copy in fetch(p):
            copy.wait()
        sum_ref[...] += jnp.dot(acts_ref[p], downs_ref[p], preferred_element_type=f32)
    out_ref[...] = sum_ref[...].astype(bf16)


def product(rank, kept, sent, down, parts):
    count = kept.shape[0]
    hidden, width = down.shape
    size = hidden // parts
    return pl.pallas_call(
        functools.partial(product_kernel, parts),
        out_shape=jax.ShapeDtypeStruct((count, width), bf16),
        in_specs=[SMEM, HBM, HBM, HBM],
        out_specs=VMEM,
        scratch_shapes=[
            pltpu.VMEM((parts, count, size), bf16),
            pltpu.VMEM((parts, size, width), bf16),
            pltpu.VMEM((count, width), f32),
            pltpu.SemaphoreType.DMA((2, parts)),
        ],
        name="product",
        cost_estimate=COST,
    )(rank.reshape(1, 1), kept, sent, down)


def weight_kernel(groups, *refs):
    first_ref, rest_ref, up_ref, down_ref = refs[-4:]
    dup = ddown = 0.0
    for g in range(groups):
        in_ref, grad_ref, act_ref, pre_ref = refs[4 * g : 4 * g + 4]
        dup = dup + contract_rows(in_ref[...], pre_ref[...])
        ddown = ddown + contract_rows(act_ref[...], grad_ref[...])
    cut = first_ref.shape[0]

    @pl.when(pl.program_id(0) == 0)
    def far():
        first_ref[...] = dup[:cut].astype(bf16)
        rest_ref[: dup.shape[0] - cut, :] = dup[cut:].astype(bf16)
        rest_ref[dup.shape[0] - cut :, :] = ddown.astype(bf16)

    @pl.when(pl.program_id(0) == 1)
    def near():
        up_ref[...] = dup
        down_ref[...] = ddown


def expert_weights(groups):
    count, width = groups[0][0].shape
    size = groups[0][2].shape[1] // 2
    fixed = pl.BlockSpec((count, width), lambda i: (0, 0))
    columns = pl.BlockSpec((count, size), lambda i: (0, 1 - i))
    cut = (width + size) // 4
    shapes = ((cut, size), (width + size - cut, size), (width, size), (size, width))
    return pl.pallas_call(
        functools.partial(weight_kernel, len(groups)),
        grid=(2,),
        in_specs=[fixed, fixed, columns, columns] * len(groups),
        out_specs=tuple(pl.BlockSpec(shape, lambda i: (0, 0)) for shape in shapes),
        out_shape=tuple(
            jax.ShapeDtypeStruct(shape, bf16 if k < 2 else f32)
            for k, shape in enumerate(shapes)
        ),
        name="expert_weights",
        compiler_params=pltpu.CompilerParams(vmem_limit_bytes=60 * 2**20),
        cost_estimate=COST,
    )(*[values for group in groups for values in group])


def expert_sum_kernel(near_up_ref, near_down_ref, first_ref, rest_ref, up_ref, down_ref):
    step = pl.program_id(0)
    half = pl.num_programs(0) // 2
    far = jnp.where(step < half // 2, first_ref[...], rest_ref[...]).astype(f32)

    @pl.when(step < half)
    def upper():
        up_ref[...] = near_up_ref[...] + far

    @pl.when(step >= half)
    def lower():
        down_ref[...] = near_down_ref[...] + far


def expert_sums(near_up, near_down, first, rest):
    count, width = near_up.shape
    steps = 8
    half = steps // 2
    size = count // half
    head = steps // 4
    skip = first.shape[0] // size - head
    block = lambda place: pl.BlockSpec((size, width), lambda i: (place(i), 0))
    upper = block(lambda i: jnp.minimum(i, half - 1))
    lower = block(lambda i: jnp.maximum(i - half, 0))
    return pl.pallas_call(
        expert_sum_kernel,
        grid=(steps,),
        out_shape=(jax.ShapeDtypeStruct((count, width), f32),) * 2,
        in_specs=[
            upper,
            lower,
            block(lambda i: jnp.minimum(i, head - 1) + skip),
            block(lambda i: jnp.maximum(i - head, 0)),
        ],
        out_specs=(upper, lower),
        name="expert_sums",
        compiler_params=pltpu.CompilerParams(vmem_limit_bytes=10 * 2**20),
        cost_estimate=COST,
    )(near_up, near_down, first, rest)


def input_grad_kernel(groups, qw_ref, kw_ref, vw_ref, *refs):
    joint_refs = refs[: len(groups)]
    kept_ref, sent_ref, turned_ref = refs[len(groups) :]
    step = pl.program_id(0)

    @pl.when(step == 0)
    def stack():
        start = 0
        for first_head, heads in groups:
            for at, weight_ref, first, size in stacked_parts(
                first_head, heads, qw_ref, kw_ref, vw_ref
            ):
                turned_ref[start + at : start + at + size, :] = weight_ref[
                    first : first + size, :
                ]
            start += 3 * heads * HEAD_DIM

    total = 0.0
    at = 0
    for joint_ref in joint_refs:
        rows = slice(at, at + joint_ref.shape[1])
        total = total + jnp.dot(
            joint_ref[...], turned_ref[rows, :], preferred_element_type=f32
        )
        at += joint_ref.shape[1]

    @pl.when(step % 2 == 0)
    def keep():
        kept_ref[0] = total.astype(bf16)

    @pl.when(step % 2 == 1)
    def send():
        sent_ref[0] = total.astype(bf16)


def input_grad(groups, weights, joints, first, count, size):
    cols, width = weights[0].shape
    fixed = pl.BlockSpec((cols, width), lambda i: (0, 0))
    return pl.pallas_call(
        functools.partial(input_grad_kernel, groups),
        grid=(count,),
        out_shape=(jax.ShapeDtypeStruct((count // 2, size, width), bf16),) * 2,
        in_specs=[fixed] * 3
        + [
            pl.BlockSpec((size, joint.shape[1]), lambda i: (first + i, 0))
            for joint in joints
        ],
        out_specs=(pl.BlockSpec((1, size, width), lambda i: (i // 2, 0, 0)),) * 2,
        scratch_shapes=[pltpu.VMEM((3 * cols, width), bf16)],
        name="input_grad",
        compiler_params=pltpu.CompilerParams(vmem_limit_bytes=10 * 2**20),
        cost_estimate=COST,
    )(*weights, *joints)


def block_kernel(residual_ref, dispatch_ref, back_ref, out_ref):
    out_ref[...] = residual_ref[...] + contract_rows(dispatch_ref[...], back_ref[...])


def block_output(residual, dispatch, back):
    return pl.pallas_call(
        block_kernel,
        out_shape=jax.ShapeDtypeStruct(residual.shape, f32),
        in_specs=[VMEM] * 3,
        out_specs=VMEM,
        name="block_output",
        compiler_params=pltpu.CompilerParams(vmem_limit_bytes=9 * 2**20),
        cost_estimate=COST,
    )(residual, dispatch, back)


def close_kernel(rank_ref, tokens_ref, gain_ref, grad_ref, *refs):
    *part_refs, out_ref = refs
    grad_in = 0.0
    for part_ref in part_refs:
        grad_in = grad_in + part_ref[...].reshape(out_ref.shape).astype(f32)
    values = tokens_ref[...].astype(f32)
    centred = values - jnp.mean(values, axis=-1, keepdims=True)
    inverse = lax.rsqrt(jnp.mean(centred * centred, axis=-1, keepdims=True) + EPSILON)
    normed = centred * inverse
    scaled = grad_in * gain_ref[...][None]
    out_ref[...] = grad_ref[...] + inverse * (
        scaled
        - jnp.mean(scaled, axis=-1, keepdims=True)
        - normed * jnp.mean(scaled * normed, axis=-1, keepdims=True)
    )


def close(rank, tokens, gain, grad, parts):
    shard, width = grad.shape
    size = shard // 2
    rows = lambda i, r: (i, 0)
    return pl.pallas_call(
        close_kernel,
        grid_spec=pltpu.PrefetchScalarGridSpec(
            num_scalar_prefetch=1,
            grid=(2,),
            in_specs=[
                pl.BlockSpec((size, width), lambda i, r: (2 * r[0] + i, 0)),
                pl.BlockSpec((width,), lambda i, r: (0,)),
                pl.BlockSpec((size, width), rows),
            ]
            + [pl.BlockSpec((1, size, width), lambda i, r: (0, i, 0))] * len(parts),
            out_specs=pl.BlockSpec((size, width), rows),
        ),
        out_shape=jax.ShapeDtypeStruct((shard, width), f32),
        name="close",
        compiler_params=pltpu.CompilerParams(vmem_limit_bytes=12 * 2**20),
        cost_estimate=COST,
    )(rank, tokens, gain, grad, *parts)


def add_low_kernel(a_ref, b_ref, out_ref):
    out_ref[...] = (a_ref[...].astype(f32) + b_ref[...].astype(f32)).astype(bf16)


def add_low(a, b):
    block = pl.BlockSpec(a.shape, lambda i: (0,) * a.ndim)
    return pl.pallas_call(
        add_low_kernel,
        grid=(1,),
        out_shape=jax.ShapeDtypeStruct(a.shape, bf16),
        in_specs=[block, block],
        out_specs=block,
        name="add_low",
        compiler_params=pltpu.CompilerParams(vmem_limit_bytes=6 * 2**20),
        cost_estimate=COST,
    )(a, b)


def tie(*values):
    return lax.optimization_barrier(values)


def finish_kernel(groups, bit_ref, *refs):
    pieces, refs = refs[: 2 * len(groups)], refs[2 * len(groups) :]
    query_ref, key_ref, value_ref = refs[:3]
    bit = bit_ref[0, 0]
    for g, ((first_head, heads), whole_ref) in enumerate(zip(groups, refs[3:])):
        half = whole_ref.shape[0] // 2
        for piece_ref, at in ((pieces[2 * g], bit), (pieces[2 * g + 1], 1 - bit)):
            whole_ref[rows_at(at, half), :] = piece_ref[0:half, :].astype(f32)
        for at, target_ref, first, size in stacked_parts(
            first_head, heads, query_ref, key_ref, value_ref
        ):
            target_ref[first : first + size, :] = whole_ref[at : at + size, :]


def finish(groups, bit, pieces):
    width = pieces[0].shape[1]
    cols = sum(heads for first_head, heads in groups) * HEAD_DIM
    return pl.pallas_call(
        functools.partial(finish_kernel, groups),
        out_shape=(jax.ShapeDtypeStruct((cols, width), f32),) * 3,
        in_specs=[SMEM] + [VMEM] * len(pieces),
        out_specs=(VMEM,) * 3,
        scratch_shapes=[
            pltpu.VMEM((3 * heads * HEAD_DIM, width), f32) for first_head, heads in groups
        ],
        name="finish",
        compiler_params=pltpu.CompilerParams(vmem_limit_bytes=10 * 2**20),
        cost_estimate=COST,
    )(bit, *pieces)


def on_device(
    tokens,
    first_gain,
    first_bias,
    query_weight,
    key_weight,
    value_weight,
    output_weight,
    second_gain,
    second_bias,
    expert_up,
    expert_down,
    item_lengths,
    routes,
    slot_order,
    cotangent,
):
    slots_all, width = tokens.shape
    members = lax.axis_size("tensor")
    shard_rows = slots_all // members
    rank = lax.axis_index("tensor")
    sources = lax.axis_size("dp")
    experts_all = sources * expert_up.shape[0]
    capacity = shard_rows // experts_all
    head_cols = query_weight.shape[1]
    heads = head_cols // HEAD_DIM
    up_matrix = expert_up[0]
    down_matrix = expert_down[0]
    rank_cell = rank.astype(jnp.int32).reshape(1, 1)

    def exchange(rows):
        return lax.all_to_all(
            rows.reshape(sources, -1, width), "dp", split_axis=0, concat_axis=0, tiled=True
        ).reshape(-1, width)

    qw, kw, vw = query_weight.T, key_weight.T, value_weight.T

    dispatch, grad_slots = plan(
        item_lengths, rank_cell, routes, slot_order, cotangent, capacity, experts_all
    )
    flat_grad = exchange(grad_slots)
    tokens, grad_slots = tie(tokens, grad_slots)
    normed_in, qt, kt, vt = project(
        rank_cell[0], tokens, first_gain, first_bias, qw, kw, vw, members
    )
    outputs = [output_weight] + [
        swap(output_weight, "tensor", k) for k in range(1, members)
    ]
    far = members // 2
    *far_heads, far_logs = attend(
        item_lengths, rank_cell, qt, kt, vt, members, far, members - far
    )
    far_heads, kt = tie(far_heads, kt)
    far_arrived = [swap(far_heads[j - far], "tensor", j) for j in range(far, members)]
    *near_heads, near_logs = attend(item_lengths, rank_cell, qt, kt, vt, members, 0, far)
    near_heads, far_arrived, outputs = tie(near_heads, far_arrived, outputs)
    own_heads = near_heads + far_heads
    logs = (near_logs, far_logs)
    all_heads = (
        near_heads[:1]
        + [swap(near_heads[j], "tensor", j) for j in range(1, far)]
        + far_arrived
    )
    residual, outgoing = middle(
        rank_cell[0], tokens, second_gain, second_bias, dispatch, all_heads, outputs
    )
    flat_in = exchange(outgoing)

    flat_grad, outgoing = tie(flat_grad, outgoing)
    grad_act = activation_grads(flat_grad, down_matrix, members)
    near_grads = swap(flat_grad, "tensor", 1)
    flat_in, grad_act, near_grads = tie(flat_in, grad_act, near_grads)
    near_rows = swap(flat_in, "tensor", 1)
    act, grad_pre, act_sent, pre_sent, grad_mid = expert(
        rank_cell[0], flat_in, grad_act, up_matrix, members
    )
    grad_mid, act, near_rows = tie(grad_mid, act, near_rows)
    grad_back = exchange(grad_mid)

    act, act_sent, pre_sent, grad_mid = tie(act, act_sent, pre_sent, grad_mid)
    near_act = swap(act_sent, "tensor", 1)
    near_pre = swap(pre_sent, "tensor", 1)
    made = product(rank_cell[0], act, act_sent, down_matrix, members)
    made, near_act, near_pre = tie(made, near_act, near_pre)
    *expert_far, expert_up_near, expert_down_near = expert_weights(
        [(flat_in, flat_grad, act, grad_pre), (near_rows, near_grads, near_act, near_pre)]
    )
    grad_back, made, expert_far = tie(grad_back, made, expert_far)

    steps = steps_of(members)
    grad_res, sums_second, kept, sent, *grad_heads = turn(
        item_lengths, rank_cell, dispatch, grad_back, residual, cotangent,
        second_gain, all_heads, outputs,
    )
    grad_parts = [grad_heads[0]] + [
        swap(grad_heads[j], "tensor", j) for j in range(1, members)
    ]
    output_near, output_far = output_sums(kept, swap(sent, "tensor", 1), expert_far[0])
    made, grad_heads = tie(made, grad_heads)
    returned = exchange(made)
    grad_parts, output_near, output_far = tie(grad_parts, output_near, output_far)

    bit_cell = (lax.axis_index("dp") & 1).astype(jnp.int32).reshape(1, 1)
    weights = (qw, kw, vw)
    dp_steps = steps_of(sources)
    back = functools.partial(
        attend_back, lens=item_lengths, rank=rank_cell, bit=bit_cell, qt=qt, kt=kt, vt=vt,
        logs=logs, weights=weights, normed=normed_in, outs=own_heads,
    )
    groups = ((0, heads - 1), (heads - 1, 1))
    joint_a, sums_a, own_a, away_a = back(*groups[0], extras=(), grads=grad_parts)
    output_got = swap(output_far, "tensor", 2)
    joint_a, own_a, away_a, output_got, grad_parts, expert_rest, returned = tie(
        joint_a, own_a, away_a, output_got, grad_parts, expert_far[1], returned
    )
    expert_got = swap(expert_rest, "tensor", 2)
    output_sum = add_low(output_near, output_got)
    own_a = add_low(own_a, swap(away_a, "dp", 1))
    output_sum = add_low(output_sum, swap(output_sum, "dp", dp_steps[-1]))
    joint_b, unused, own_b, away_b = back(
        *groups[1], extras=(sums_a, sums_second), grads=grad_parts
    )
    joint_b, own_a, own_b, away_b, output_sum = tie(
        joint_b, own_a, own_b, away_b, output_sum
    )

    far_kept, far_sent = input_grad(
        groups, weights, (joint_a, joint_b), far, members - far, shard_rows
    )
    near_kept, near_sent = input_grad(
        groups, weights, (joint_a, joint_b), 0, far, shard_rows
    )
    own_b = add_parts(own_b, swap(away_b, "dp", 1))
    far_kept = add_low(far_kept, swap(far_sent, "tensor", 1))
    far_kept, own_b, output_sum, near_sent = tie(far_kept, own_b, output_sum, near_sent)
    near_core = swap(near_sent, "tensor", 1)
    near_far = swap(far_kept, "tensor", 2)
    for step in dp_steps[1:]:
        own_a = add_low(own_a, swap(own_a, "dp", step))
        own_b = add_parts(own_b, swap(own_b, "dp", step))
        if step == dp_steps[1]:
            own_b, expert_got = tie(own_b, expert_got)
    up_grad, down_grad = expert_sums(
        expert_up_near, expert_down_near, output_got, expert_got
    )
    own_b, up_grad, down_grad, near_far = tie(own_b, up_grad, down_grad, near_far)
    norm_sums = own_b[-SUM_ROWS:].astype(f32)
    norm_sums = norm_sums[: SUM_ROWS // 2] + norm_sums[SUM_ROWS // 2 :]
    for step in steps:
        norm_sums = norm_sums + swap(norm_sums, "tensor", step)
    pieces = (own_a, swap(own_a, "dp", 1), own_b, swap(own_b, "dp", 1))
    token_grad = close(
        rank_cell[0], tokens, first_gain, grad_res, (near_kept, near_core, near_far)
    )
    for step in dp_steps[:-1]:
        output_sum = add_low(output_sum, swap(output_sum, "dp", step))

    block_out = block_output(residual, dispatch, returned)
    query_grad, key_grad, value_grad = finish(groups, bit_cell, pieces)
    return (
        block_out,
        token_grad,
        (norm_sums[0] - first_bias * norm_sums[1]) / first_gain,
        norm_sums[1],
        query_grad.T,
        key_grad.T,
        value_grad.T,
        output_sum.astype(f32),
        norm_sums[2],
        norm_sums[3],
        up_grad[None],
        down_grad[None],
    )


def solution(mesh):
    in_specs = (
        P("dp", None),
        P(),
        P(),
        P(None, "tensor"),
        P(None, "tensor"),
        P(None, "tensor"),
        P("tensor", None),
        P(),
        P(),
        P("dp", None, None),
        P("dp", None, None),
        P("dp", None),
        P(("dp", "tensor"), None),
        P(("dp", "tensor"), None),
        P(("dp", "tensor"), None),
    )
    out_specs = (
        P(("dp", "tensor"), None),
        P(("dp", "tensor"), None),
        P(),
        P(),
        P(None, "tensor"),
        P(None, "tensor"),
        P(None, "tensor"),
        P("tensor", None),
        P(),
        P(),
        P("dp", None, "tensor"),
        P("dp", "tensor", None),
    )
    return jax.shard_map(
        on_device, mesh=mesh, in_specs=in_specs, out_specs=out_specs, check_vma=False
    )
```

```python
import functools

import jax
import jax.numpy as jnp
from jax import lax
from jax.experimental import pallas as pl
from jax.experimental.pallas import tpu as pltpu
from jax.sharding import PartitionSpec as P

HEAD_DIM = 64
EPSILON = 1e-05
NEGATIVE = -1e30
f32 = jnp.float32
bf16 = jnp.bfloat16
VMEM = pl.BlockSpec(memory_space=pltpu.VMEM)
HBM = pl.BlockSpec(memory_space=pltpu.MemorySpace.HBM)
SMEM = pl.BlockSpec(memory_space=pltpu.SMEM)
SUM_ROWS = 16
COST = pl.CostEstimate(flops=2**20, bytes_accessed=2**20, transcendentals=0)
LONG = pl.CostEstimate(flops=2**34, bytes_accessed=2**24, transcendentals=0)


def layer_norm(values, gain, shift):
    average = jnp.mean(values, axis=-1, keepdims=True)
    centred = values - average
    variance = jnp.mean(centred * centred, axis=-1, keepdims=True)
    return centred * lax.rsqrt(variance + EPSILON) * gain + shift


def contract_rows(left, right):
    return lax.dot_general(
        left, right, (((0,), (0,)), ((), ())), preferred_element_type=f32
    )


def swap(values, axis, step):
    count = lax.axis_size(axis)
    return lax.ppermute(values, axis, [(i, i ^ step) for i in range(count)])


def steps_of(count):
    steps = []
    step = 1
    while step < count:
        steps.append(step)
        step *= 2
    return steps


def normalized(values):
    average = jnp.mean(values, axis=-1, keepdims=True)
    centred = values - average
    variance = jnp.mean(centred * centred, axis=-1, keepdims=True)
    return centred * lax.rsqrt(variance + EPSILON)


def project_kernel(
    rank_ref, tokens_ref, gain_ref, bias_ref, qw_ref, kw_ref, vw_ref,
    normed_ref, qt_ref, kt_ref, vt_ref,
):
    values = tokens_ref[...].astype(f32)
    normed = (normalized(values) * gain_ref[...][None] + bias_ref[...][None]).astype(bf16)
    normed_ref[...] = normed
    for weight_ref, out_ref, factor in (
        (qw_ref, qt_ref, HEAD_DIM ** (-0.5)), (kw_ref, kt_ref, None), (vw_ref, vt_ref, None)
    ):
        made = lax.dot_general(
            weight_ref[...], normed, (((1,), (1,)), ((), ())), preferred_element_type=f32
        ).astype(bf16)
        if factor is not None:
            made = made * jnp.asarray(factor, bf16)
        out_ref[...] = made


def project(rank, tokens, gain, bias, qw, kw, vw, blocks):
    slots, width = tokens.shape
    cols = qw.shape[0]
    size = slots // blocks
    fixed = lambda i, r: (0, 0)
    line = pl.BlockSpec((width,), lambda i, r: (0,))
    return pl.pallas_call(
        project_kernel,
        grid_spec=pltpu.PrefetchScalarGridSpec(
            num_scalar_prefetch=1,
            grid=(blocks,),
            in_specs=[
                pl.BlockSpec((size, width), lambda i, r: (i ^ r[0], 0)),
                line,
                line,
                pl.BlockSpec((cols, width), fixed),
                pl.BlockSpec((cols, width), fixed),
                pl.BlockSpec((cols, width), fixed),
            ],
            out_specs=(
                pl.BlockSpec((size, width), lambda i, r: (i, 0)),
                pl.BlockSpec((cols, size), lambda i, r: (0, i)),
                pl.BlockSpec((cols, size), lambda i, r: (0, i)),
                pl.BlockSpec((cols, size), lambda i, r: (0, i)),
            ),
        ),
        out_shape=(jax.ShapeDtypeStruct((slots, width), bf16),)
        + (jax.ShapeDtypeStruct((cols, slots), bf16),) * 3,
        name="project",
        cost_estimate=COST,
    )(rank, tokens, gain, bias, qw, kw, vw)


def item_ends(lens_ref):
    ends = []
    total = jnp.int32(0)
    for i in range(lens_ref.shape[1]):
        total = total + lens_ref[0, i]
        ends.append(total)
    return ends


def segments_at(place, ends):
    segment = jnp.zeros_like(place)
    for end in ends:
        segment = segment + (place >= end).astype(jnp.int32)
    return segment


def block_span(first, size, unit, ends):
    last = jnp.minimum(first + size, ends[-1]) - 1
    low = jnp.int32(0)
    high = ends[-1]
    for end in ends:
        low = jnp.where(first >= end, end, low)
    for end in reversed(ends):
        high = jnp.where(last < end, end, high)
    empty = first >= ends[-1]
    low_block = jnp.where(empty, 0, low // unit)
    high_block = jnp.where(empty, 0, (high + unit - 1) // unit)
    return low_block, high_block


def rows_at(block, size):
    return pl.ds(pl.multiple_of(block * size, size), size)


def fill_segments(row_ref, col_ref, shard, rank, ends):
    slots = row_ref.shape[1]
    at = lax.broadcasted_iota(jnp.int32, (1, slots), 1)
    place = ((at // shard) ^ rank) * shard + at % shard
    segments = segments_at(place, ends)
    row_ref[...] = segments
    col_ref[...] = jnp.transpose(jnp.broadcast_to(segments, (128, slots)), (1, 0))


def block_bias(row_ref, col_ref, rows, cols):
    return jnp.where(col_ref[rows, 0:1] == row_ref[:, cols], 0.0, NEGATIVE)


def lane_masked(values, head):
    lane = lax.broadcasted_iota(jnp.int32, values.shape, 1)
    inside = (lane >= head * HEAD_DIM) & (lane < (head + 1) * HEAD_DIM)
    return jnp.where(inside, values, jnp.zeros_like(values))


def forward_kernel(
    first, blocks, lens_ref, rank_ref, qt_ref, kt_ref, vt_ref, *refs
):
    *out_refs, log_ref, masked_ref, out_ref, row_ref, col_ref, score_ref = refs
    count, width, size = out_ref.shape
    heads = width // HEAD_DIM
    shard = size
    rank = rank_ref[0, 0]
    ends = item_ends(lens_ref)
    fill_segments(row_ref, col_ref, shard, rank, ends)
    keys = jnp.transpose(kt_ref[...], (1, 0))
    for h in range(heads):
        masked_ref[h] = lane_masked(keys, h)

    def query_block(b, unused):
        at = first + b
        i = at ^ rank
        cols = rows_at(at, size)
        queries = qt_ref[:, cols]

        def score_block(j, carry):
            rows = rows_at(j ^ rank, shard)
            bias = block_bias(row_ref, col_ref, rows, cols)
            result = []
            for h in range(heads):
                scores = jnp.dot(
                    masked_ref[h, rows, :], queries, preferred_element_type=f32
                )
                scores = scores + bias
                score_ref[h, rows_at(j, shard), :] = scores
                part = jnp.max(scores.reshape(-1, 8, size), axis=0)
                result.append(jnp.maximum(carry[h], part))
            return tuple(result)

        low, high = block_span(i * size, size, shard, ends)
        peaks = lax.fori_loop(
            low, high, score_block, (jnp.full((8, size), NEGATIVE, f32),) * heads
        )
        peaks = [jnp.max(peak, axis=0, keepdims=True) for peak in peaks]

        def key_block(j, carry):
            rows = rows_at(j ^ rank, shard)
            result = []
            for h in range(heads):
                summed, total = carry[h]
                soft = jnp.exp(score_ref[h, rows_at(j, shard), :] - peaks[h])
                summed = summed + jnp.sum(soft.reshape(-1, 8, size), axis=0)
                total = total + jnp.dot(
                    vt_ref[pl.ds(h * HEAD_DIM, HEAD_DIM), rows],
                    soft.astype(bf16),
                    preferred_element_type=f32,
                )
                result.append((summed, total))
            return tuple(result)

        start = ((jnp.zeros((8, size), f32), jnp.zeros((HEAD_DIM, size), f32)),) * heads
        done = lax.fori_loop(low, high, key_block, start)
        live = row_ref[:, cols] < len(ends)
        for h in range(heads):
            summed, total = done[h]
            summed = jnp.sum(summed, axis=0, keepdims=True)
            highest = peaks[h]
            summed = jnp.where(live, summed, 1.0)
            result = jnp.where(live, total / summed, 0.0).astype(bf16)
            logs = jnp.where(live, highest + jnp.log(summed), -NEGATIVE)
            out_ref[b, pl.ds(h * HEAD_DIM, HEAD_DIM), :] = result
            log_ref[h, :, rows_at(b, size)] = logs
        return unused

    lax.fori_loop(0, count, query_block, 0)
    for b in range(count):
        out_refs[b][...] = out_ref[b]


def attend(lens, rank, qt, kt, vt, blocks, first, count):
    width, slots = qt.shape
    size = slots // blocks
    heads = width // HEAD_DIM
    return pl.pallas_call(
        functools.partial(forward_kernel, first, blocks),
        out_shape=(jax.ShapeDtypeStruct((width, size), bf16),) * count
        + (jax.ShapeDtypeStruct((heads, 1, count * size), f32),),
        in_specs=[SMEM, SMEM, VMEM, VMEM, VMEM],
        out_specs=(VMEM,) * (count + 1),
        scratch_shapes=[
            pltpu.VMEM((heads, slots, width), bf16),
            pltpu.VMEM((count, width, size), bf16),
            pltpu.VMEM((1, slots), jnp.int32),
            pltpu.VMEM((slots, 128), jnp.int32),
            pltpu.VMEM((heads, slots, size), f32),
        ],
        name="attend",
        compiler_params=pltpu.CompilerParams(vmem_limit_bytes=60 * 2**20),
        cost_estimate=COST,
    )(lens, rank, qt, kt, vt)


def split_rows(values):
    high = values.astype(bf16)
    return jnp.concatenate([high, (values - high.astype(f32)).astype(bf16)], axis=0)


def add_kernel(a_ref, b_ref, out_ref):
    half = out_ref.shape[0] - SUM_ROWS
    line = SUM_ROWS // 2
    total = a_ref[...].astype(f32) + b_ref[...].astype(f32)
    out_ref[:half, :] = total[:half].astype(bf16)
    out_ref[half:, :] = split_rows(total[half : half + line] + total[half + line :])


def add_parts(a, b):
    return pl.pallas_call(
        add_kernel,
        out_shape=jax.ShapeDtypeStruct(a.shape, bf16),
        in_specs=[VMEM, VMEM],
        out_specs=VMEM,
        name="add_parts",
        compiler_params=pltpu.CompilerParams(vmem_limit_bytes=5 * 2**20),
        cost_estimate=COST,
    )(a, b)


def stacked_parts(first_head, heads, query, key, value):
    dim = HEAD_DIM
    parts = []
    for n in range(heads):
        first = (first_head + n) * dim
        parts += [(2 * n * dim, key, first, dim), ((2 * n + 1) * dim, value, first, dim)]
    return parts + [(2 * heads * dim, query, first_head * dim, heads * dim)]


def backward_kernel(
    first_head, heads, blocks, extras, lens_ref, rank_ref, bit_ref, qt_ref, kt_ref, vt_ref,
    near_ref, far_ref, qw_ref, kw_ref, vw_ref, normed_ref, *rest
):
    extra_refs, rest = rest[:extras], rest[extras:]
    width, slots = qt_ref.shape
    shard = slots // blocks
    dim = HEAD_DIM
    out_refs, grad_refs = rest[:blocks], rest[blocks : 2 * blocks]
    joint_ref, sums_ref, own_ref, away_ref = rest[2 * blocks : 2 * blocks + 4]
    kv_ref, q0_ref, og_ref, right_ref, inner_ref, dq_ref, made_ref = rest[-13:-6]
    log_ref = rest[-6]
    row_ref, col_ref = rest[-5:-3]
    turned_ref, rows_ref, copied = rest[-3:]
    fetch = pltpu.make_async_copy(normed_ref, rows_ref, copied)
    fetch.start()
    unit = shard // 2
    rank = rank_ref[0, 0]
    ends = item_ends(lens_ref)
    fill_segments(row_ref, col_ref, shard, rank, ends)
    near = near_ref.shape[2]
    log_ref[:, :, :near] = near_ref[...]
    log_ref[:, :, near:] = far_ref[...]
    zero = jnp.zeros((dim, slots), bf16)
    for n in range(heads):
        part = slice((first_head + n) * dim, (first_head + n + 1) * dim)
        both = jnp.concatenate([kt_ref[part, :], vt_ref[part, :]], axis=0)
        kv_ref[n] = jnp.transpose(both, (1, 0))
        padded = jnp.concatenate([qt_ref[part, :], zero], axis=0)
        q0_ref[n] = jnp.transpose(padded, (1, 0))
        right_ref[n, 0] = padded
        for b in range(blocks):
            grad = grad_refs[b][part, :]
            cols = slice(b * shard, (b + 1) * shard)
            padded = jnp.concatenate([zero[:, :shard], grad], axis=0)
            og_ref[n, cols, :] = jnp.transpose(padded, (1, 0))
            right_ref[n, 1, :, cols] = padded
            inner_ref[n, :, cols] = jnp.sum(
                out_refs[b][part, :].astype(f32) * grad.astype(f32), axis=0, keepdims=True
            )
    dq_ref[...] = jnp.zeros_like(dq_ref)

    def key_block(j, unused):
        at_key = ((j // 2) ^ rank) * 2 + j % 2
        rows = rows_at(at_key, unit)

        def query_block(i, totals):
            at = i ^ rank
            cols = rows_at(at, shard)
            same = col_ref[rows, 0:1] == row_ref[:, cols]
            result = []
            for n in range(heads):
                head = first_head + n
                kv = kv_ref[n, rows, :]
                scores = jnp.dot(kv, right_ref[n, 0, :, cols], preferred_element_type=f32)
                grad_soft = jnp.dot(kv, right_ref[n, 1, :, cols], preferred_element_type=f32)
                soft = jnp.where(same, jnp.exp(scores - log_ref[head, :, cols]), 0.0)
                grad_scores = (soft * (grad_soft - inner_ref[n, :, cols])).astype(bf16)
                total = totals[n] + jnp.dot(
                    soft.astype(bf16), og_ref[n, cols, :], preferred_element_type=f32
                )
                total = total + jnp.dot(
                    grad_scores, q0_ref[n, cols, :], preferred_element_type=f32
                )
                dq_ref[n, :, cols] += jnp.dot(
                    kt_ref[pl.ds(head * dim, dim), rows], grad_scores,
                    preferred_element_type=f32,
                )
                result.append(total)
            return tuple(result)

        low, high = block_span(j * unit, unit, shard, ends)
        start = (jnp.zeros((unit, 2 * dim), f32),) * heads
        totals = lax.fori_loop(low, high, query_block, start)
        for n in range(heads):
            part = slice(2 * dim * n, 2 * dim * (n + 1))
            total = totals[n].astype(bf16)
            joint_ref[rows, part] = total
            turned_ref[part, rows] = jnp.transpose(total, (1, 0))
        return unused

    lax.fori_loop(0, 2 * blocks, key_block, 0)
    dq = (dq_ref[...] * dim ** (-0.5)).astype(bf16).reshape(heads * dim, slots)
    turned_ref[2 * dim * heads :, :] = dq
    joint_ref[:, 2 * dim * heads :] = jnp.transpose(dq, (1, 0))
    fetch.wait()
    made_ref[...] = jnp.dot(turned_ref[...], rows_ref[...], preferred_element_type=f32)
    gains = jnp.zeros((1, rows_ref.shape[1]), f32)
    shifts = jnp.zeros((1, rows_ref.shape[1]), f32)
    for at, weight_ref, first, size in stacked_parts(
        first_head, heads, qw_ref, kw_ref, vw_ref
    ):
        weight = weight_ref[first : first + size, :].astype(f32)
        gains += jnp.sum(weight * made_ref[at : at + size, :], axis=0, keepdims=True)
        total = jnp.sum(turned_ref[at : at + size, :].astype(f32), axis=1, keepdims=True)
        shifts += jnp.sum(weight * total, axis=0, keepdims=True)
    sums_ref[0:1] = gains
    sums_ref[1:2] = shifts
    half = made_ref.shape[0] // 2
    bit = bit_ref[0, 0]
    for part_ref, at in ((own_ref, bit), (away_ref, 1 - bit)):
        part_ref[0:half, :] = made_ref[rows_at(at, half), :].astype(bf16)
        if extras:
            lines = [sums_ref[...] + extra_refs[0][...], extra_refs[1][...]]
            lines.append(jnp.zeros((SUM_ROWS // 2 - 4, gains.shape[1]), f32))
            part_ref[half:, :] = split_rows(jnp.concatenate(lines, axis=0))


def attend_back(
    first_head, heads, extras, lens, rank, bit, qt, kt, vt, logs, weights, normed, outs, grads
):
    slots, width = normed.shape
    blocks = len(outs)
    dim = HEAD_DIM
    cols = 3 * dim * heads
    rows = cols // 2 + (SUM_ROWS if extras else 0)
    return pl.pallas_call(
        functools.partial(backward_kernel, first_head, heads, blocks, len(extras)),
        out_shape=(
            jax.ShapeDtypeStruct((slots, cols), bf16),
            jax.ShapeDtypeStruct((2, width), f32),
        )
        + (jax.ShapeDtypeStruct((rows, width), bf16),) * 2,
        in_specs=[SMEM, SMEM, SMEM]
        + [VMEM] * 8
        + [pl.BlockSpec(memory_space=pl.ANY)]
        + [VMEM] * (len(extras) + 2 * blocks),
        out_specs=(VMEM,) * 4,
        scratch_shapes=[pltpu.VMEM((heads, slots, 2 * dim), bf16)] * 3
        + [
            pltpu.VMEM((heads, 2, 2 * dim, slots), bf16),
            pltpu.VMEM((heads, 1, slots), f32),
            pltpu.VMEM((heads, dim, slots), f32),
            pltpu.VMEM((cols, width), f32),
            pltpu.VMEM((qt.shape[0] // dim, 1, slots), f32),
            pltpu.VMEM((1, slots), jnp.int32),
            pltpu.VMEM((slots, 128), jnp.int32),
            pltpu.VMEM((cols, slots), bf16),
            pltpu.VMEM((slots, width), bf16),
            pltpu.SemaphoreType.DMA,
        ],
        name="attend_back",
        compiler_params=pltpu.CompilerParams(vmem_limit_bytes=60 * 2**20),
        cost_estimate=COST,
    )(lens, rank, bit, qt, kt, vt, *logs, *weights, normed, *extras, *outs, *grads)


def plan_kernel(capacity, lens_ref, rank_ref, routes_ref, order_ref, grad_ref,
                dispatch_ref, slots_ref):
    shard = routes_ref.shape[1]
    first = rank_ref[0, 0] * shard
    ends = item_ends(lens_ref)
    chosen_row = routes_ref[...]
    chosen_col = jnp.transpose(jnp.broadcast_to(chosen_row, (128, shard)), (1, 0))[:, 0:1]
    order_row = order_ref[...]
    order_col = jnp.transpose(jnp.broadcast_to(order_row, (128, shard)), (1, 0))[:, 0:1]
    alive_row = segments_at(
        first + lax.broadcasted_iota(jnp.int32, (1, shard), 1), ends
    ) < len(ends)
    alive_col = segments_at(
        first + lax.broadcasted_iota(jnp.int32, (shard, 1), 0), ends
    ) < len(ends)
    ahead = (chosen_col == chosen_row) & (order_col < order_row) & alive_col
    ranked = jnp.sum(ahead.astype(jnp.int32), axis=0, keepdims=True)
    kept = alive_row & (ranked < capacity)
    slot = jnp.where(kept, chosen_row * capacity + ranked, -1)
    dispatch = (
        lax.broadcasted_iota(jnp.int32, dispatch_ref.shape, 0) == slot
    ).astype(f32).astype(bf16)
    dispatch_ref[...] = dispatch
    slots_ref[...] = jnp.dot(
        dispatch, grad_ref[...], preferred_element_type=f32
    ).astype(bf16)


def plan(lens, rank, routes, order, grads, capacity, experts_all):
    shard, width = grads.shape
    count = experts_all * capacity
    return pl.pallas_call(
        functools.partial(plan_kernel, capacity),
        out_shape=(
            jax.ShapeDtypeStruct((count, shard), bf16),
            jax.ShapeDtypeStruct((count, width), bf16),
        ),
        in_specs=[SMEM, SMEM, VMEM, VMEM, VMEM],
        out_specs=(VMEM, VMEM),
        name="plan",
        cost_estimate=COST,
    )(lens, rank, routes.reshape(1, -1), order, grads)


def across(left, right):
    return lax.dot_general(
        left, right, (((1,), (1,)), ((), ())), preferred_element_type=f32
    )


def middle_kernel(count, rank_ref, tokens_ref, gain_ref, bias_ref, dispatch_ref, *refs):
    head_refs, weight_refs = refs[:count], refs[count : 2 * count]
    residual_ref, rows_ref = refs[2 * count :]
    residual = tokens_ref[...].astype(f32)
    for head_ref, weight_ref in zip(head_refs, weight_refs):
        residual = residual + contract_rows(head_ref[...], weight_ref[...])
    residual_ref[...] = residual
    normed = (normalized(residual) * gain_ref[...][None] + bias_ref[...][None]).astype(bf16)
    rows_ref[...] = jnp.dot(
        dispatch_ref[...], normed, preferred_element_type=f32
    ).astype(bf16)


def middle(rank, tokens, gain, bias, dispatch, heads, weights):
    count, shard = dispatch.shape
    width = tokens.shape[1]
    fixed = lambda array: pl.BlockSpec(array.shape, lambda i, r: (0,) * array.ndim)
    small = [gain, bias, dispatch, *heads, *weights]
    return pl.pallas_call(
        functools.partial(middle_kernel, len(heads)),
        grid_spec=pltpu.PrefetchScalarGridSpec(
            num_scalar_prefetch=1,
            grid=(1,),
            in_specs=[pl.BlockSpec((shard, width), lambda i, r: (r[0], 0))]
            + [fixed(array) for array in small],
            out_specs=(
                pl.BlockSpec((shard, width), lambda i, r: (0, 0)),
                pl.BlockSpec((count, width), lambda i, r: (0, 0)),
            ),
        ),
        out_shape=(
            jax.ShapeDtypeStruct((shard, width), f32),
            jax.ShapeDtypeStruct((count, width), bf16),
        ),
        name="middle",
        cost_estimate=COST,
    )(rank, tokens, *small)


def turn_kernel(
    count, lens_ref, rank_ref, dispatch_ref, back_ref, residual_ref, cotangent_ref,
    gain_ref, *refs
):
    head_refs, weight_refs = refs[:count], refs[count : 2 * count]
    grad_ref, sums_ref, kept_ref, sent_ref = refs[2 * count : 2 * count + 4]
    part_refs = refs[2 * count + 4 :]
    shard = residual_ref.shape[0]
    grad_normed = contract_rows(dispatch_ref[...], back_ref[...])
    values = residual_ref[...]
    centred = values - jnp.mean(values, axis=-1, keepdims=True)
    inverse = lax.rsqrt(jnp.mean(centred * centred, axis=-1, keepdims=True) + EPSILON)
    normed = centred * inverse
    sums_ref[0:1] = jnp.sum(grad_normed * normed, axis=0, keepdims=True)
    sums_ref[1:2] = jnp.sum(grad_normed, axis=0, keepdims=True)
    scaled = grad_normed * gain_ref[...][None]
    grad = cotangent_ref[...].astype(f32) + inverse * (
        scaled
        - jnp.mean(scaled, axis=-1, keepdims=True)
        - normed * jnp.mean(scaled * normed, axis=-1, keepdims=True)
    )
    grad_ref[...] = grad
    low = grad.astype(bf16)
    place = rank_ref[0, 0] * shard + lax.broadcasted_iota(jnp.int32, (1, shard), 1)
    alive = place < item_ends(lens_ref)[-1]
    for weight_ref, part_ref in zip(weight_refs, part_refs):
        part_ref[...] = jnp.where(alive, across(weight_ref[...], low), 0.0).astype(bf16)
    for j, head_ref in enumerate(head_refs):
        made = jnp.dot(head_ref[...], low, preferred_element_type=f32)
        (kept_ref, sent_ref)[j % 2][j // 2] = made.astype(bf16)


def turn(lens, rank, dispatch, back, residual, cotangent, gain, heads, weights):
    shard, width = residual.shape
    cols = weights[0].shape[0]
    count = len(weights)
    return pl.pallas_call(
        functools.partial(turn_kernel, count),
        out_shape=(
            jax.ShapeDtypeStruct((shard, width), f32),
            jax.ShapeDtypeStruct((2, width), f32),
            jax.ShapeDtypeStruct((count // 2, cols, width), bf16),
            jax.ShapeDtypeStruct((count // 2, cols, width), bf16),
        )
        + (jax.ShapeDtypeStruct((cols, shard), bf16),) * count,
        in_specs=[SMEM, SMEM] + [VMEM] * (5 + 2 * count),
        out_specs=(VMEM,) * (4 + count),
        name="turn",
        cost_estimate=COST,
    )(lens, rank, dispatch, back, residual, cotangent, gain, *heads, *weights)


def output_sum_kernel(kept_ref, core_ref, first_ref, near_ref, far_ref):
    cols = near_ref.shape[0]
    total = [
        (kept_ref[j].astype(f32) + core_ref[j].astype(f32)).astype(bf16) for j in range(2)
    ]
    near_ref[...] = total[0]
    far_ref[:cols, :] = total[1]
    far_ref[cols:, :] = first_ref[...]


def output_sums(kept, core, first):
    slots, cols, width = kept.shape
    return pl.pallas_call(
        output_sum_kernel,
        out_shape=(
            jax.ShapeDtypeStruct((cols, width), bf16),
            jax.ShapeDtypeStruct((cols + first.shape[0], width), bf16),
        ),
        in_specs=[VMEM] * 3,
        out_specs=(VMEM, VMEM),
        name="output_sums",
        compiler_params=pltpu.CompilerParams(vmem_limit_bytes=52 * 2**20),
        cost_estimate=LONG,
    )(kept, core, first)


def gelu_parts(values):
    below = 0.5 + 0.5 * lax.erf(values * (0.5**0.5))
    density = jnp.exp(-0.5 * values * values) * (0.5 / jnp.pi) ** 0.5
    return values * below, below + values * density


def part_at(step, parts, rank):
    half = parts // 2
    return (2 * (step % half) + step // half) ^ rank


def activation_kernel(grad_ref, down_ref, out_ref):
    out_ref[...] = across(grad_ref[...], down_ref[...]).astype(bf16)


def activation_grads(grads, down, parts):
    count, width = grads.shape
    hidden = down.shape[0]
    size = hidden // parts
    return pl.pallas_call(
        activation_kernel,
        grid=(parts,),
        out_shape=jax.ShapeDtypeStruct((count, hidden), bf16),
        in_specs=[
            pl.BlockSpec((count, width), lambda i: (0, 0)),
            pl.BlockSpec((size, width), lambda i: (i, 0)),
        ],
        out_specs=pl.BlockSpec((count, size), lambda i: (0, i)),
        name="activation_grads",
        cost_estimate=COST,
    )(grads, down)


def expert_kernel(
    parts, rank_ref, in_ref, grad_act_ref, up_ref,
    act_kept_ref, pre_kept_ref, act_sent_ref, pre_sent_ref, mid_ref,
    grads_ref, ups_ref, acts_ref, pres_ref, sum_ref, fetched, stored,
):
    rank = rank_ref[0, 0]
    size = ups_ref.shape[2]
    half = parts // 2

    def fetch(p):
        cols = rows_at(part_at(p, parts, rank), size)
        return (
            pltpu.make_async_copy(up_ref.at[:, cols], ups_ref.at[p], fetched.at[0, p]),
            pltpu.make_async_copy(grad_act_ref.at[:, cols], grads_ref.at[p], fetched.at[1, p]),
        )

    def store(p, act_out_ref, pre_out_ref):
        cols = rows_at(p % half, size)
        return (
            pltpu.make_async_copy(acts_ref.at[p], act_out_ref.at[:, cols], stored.at[0, p]),
            pltpu.make_async_copy(pres_ref.at[p], pre_out_ref.at[:, cols], stored.at[1, p]),
        )

    for p in range(parts):
        for copy in fetch(p):
            copy.start()
    sum_ref[...] = jnp.zeros_like(sum_ref)

    def part(p, unused):
        for copy in fetch(p):
            copy.wait()
        pre = jnp.dot(in_ref[...], ups_ref[p], preferred_element_type=f32)
        act, slope = gelu_parts(pre)
        acts_ref[p] = act.astype(bf16)
        grad_pre = (grads_ref[p].astype(f32) * slope).astype(bf16)
        pres_ref[p] = grad_pre
        sum_ref[...] += across(grad_pre, ups_ref[p])

        @pl.when(p < half)
        def keep():
            for copy in store(p, act_kept_ref, pre_kept_ref):
                copy.start()

        @pl.when(p >= half)
        def send():
            for copy in store(p, act_sent_ref, pre_sent_ref):
                copy.start()

        return unused

    lax.fori_loop(0, parts, part, 0)
    mid_ref[...] = sum_ref[...].astype(bf16)
    for p in range(parts):
        outs = (act_kept_ref, pre_kept_ref) if p < half else (act_sent_ref, pre_sent_ref)
        for copy in store(p, *outs):
            copy.wait()


def expert(rank, rows, grad_act, up, parts):
    count, width = rows.shape
    hidden = up.shape[1]
    size = hidden // parts
    return pl.pallas_call(
        functools.partial(expert_kernel, parts),
        out_shape=(jax.ShapeDtypeStruct((count, hidden // 2), bf16),) * 4
        + (jax.ShapeDtypeStruct((count, width), bf16),),
        in_specs=[SMEM, VMEM, HBM, HBM],
        out_specs=(HBM,) * 4 + (VMEM,),
        scratch_shapes=[
            pltpu.VMEM((parts, count, size), grad_act.dtype),
            pltpu.VMEM((parts, width, size), bf16),
            pltpu.VMEM((parts, count, size), bf16),
            pltpu.VMEM((parts, count, size), bf16),
            pltpu.VMEM((count, width), f32),
            pltpu.SemaphoreType.DMA((2, parts)),
            pltpu.SemaphoreType.DMA((2, parts)),
        ],
        name="expert",
        compiler_params=pltpu.CompilerParams(vmem_limit_bytes=52 * 2**20),
        cost_estimate=COST,
    )(rank.reshape(1, 1), rows, grad_act, up)


def product_kernel(parts, rank_ref, kept_ref, sent_ref, down_ref, out_ref,
                   acts_ref, downs_ref, sum_ref, fetched):
    rank = rank_ref[0, 0]
    size = downs_ref.shape[1]
    half = parts // 2

    def fetch(p):
        rows = rows_at(part_at(p, parts, rank), size)
        source = kept_ref if p < half else sent_ref
        cols = slice((p % half) * size, (p % half + 1) * size)
        return (
            pltpu.make_async_copy(down_ref.at[rows, :], downs_ref.at[p], fetched.at[0, p]),
            pltpu.make_async_copy(source.at[:, cols], acts_ref.at[p], fetched.at[1, p]),
        )

    for p in range(parts):
        for copy in fetch(p):
            copy.start()
    sum_ref[...] = jnp.zeros_like(sum_ref)
    for p in range(parts):
        for copy in fetch(p):
            copy.wait()
        sum_ref[...] += jnp.dot(acts_ref[p], downs_ref[p], preferred_element_type=f32)
    out_ref[...] = sum_ref[...].astype(bf16)


def product(rank, kept, sent, down, parts):
    count = kept.shape[0]
    hidden, width = down.shape
    size = hidden // parts
    return pl.pallas_call(
        functools.partial(product_kernel, parts),
        out_shape=jax.ShapeDtypeStruct((count, width), bf16),
        in_specs=[SMEM, HBM, HBM, HBM],
        out_specs=VMEM,
        scratch_shapes=[
            pltpu.VMEM((parts, count, size), bf16),
            pltpu.VMEM((parts, size, width), bf16),
            pltpu.VMEM((count, width), f32),
            pltpu.SemaphoreType.DMA((2, parts)),
        ],
        name="product",
        cost_estimate=COST,
    )(rank.reshape(1, 1), kept, sent, down)


def weight_kernel(groups, *refs):
    first_ref, rest_ref, up_ref, down_ref = refs[-4:]
    dup = ddown = 0.0
    for g in range(groups):
        in_ref, grad_ref, act_ref, pre_ref = refs[4 * g : 4 * g + 4]
        dup = dup + contract_rows(in_ref[...], pre_ref[...])
        ddown = ddown + contract_rows(act_ref[...], grad_ref[...])
    cut = first_ref.shape[0]

    @pl.when(pl.program_id(0) == 0)
    def far():
        first_ref[...] = dup[:cut].astype(bf16)
        rest_ref[: dup.shape[0] - cut, :] = dup[cut:].astype(bf16)
        rest_ref[dup.shape[0] - cut :, :] = ddown.astype(bf16)

    @pl.when(pl.program_id(0) == 1)
    def near():
        up_ref[...] = dup
        down_ref[...] = ddown


def expert_weights(groups):
    count, width = groups[0][0].shape
    size = groups[0][2].shape[1] // 2
    fixed = pl.BlockSpec((count, width), lambda i: (0, 0))
    columns = pl.BlockSpec((count, size), lambda i: (0, 1 - i))
    cut = (width + size) // 4
    shapes = ((cut, size), (width + size - cut, size), (width, size), (size, width))
    return pl.pallas_call(
        functools.partial(weight_kernel, len(groups)),
        grid=(2,),
        in_specs=[fixed, fixed, columns, columns] * len(groups),
        out_specs=tuple(pl.BlockSpec(shape, lambda i: (0, 0)) for shape in shapes),
        out_shape=tuple(
            jax.ShapeDtypeStruct(shape, bf16 if k < 2 else f32)
            for k, shape in enumerate(shapes)
        ),
        name="expert_weights",
        compiler_params=pltpu.CompilerParams(vmem_limit_bytes=60 * 2**20),
        cost_estimate=COST,
    )(*[values for group in groups for values in group])


def expert_sum_kernel(near_up_ref, near_down_ref, first_ref, rest_ref, up_ref, down_ref):
    step = pl.program_id(0)
    half = pl.num_programs(0) // 2
    far = jnp.where(step < half // 2, first_ref[...], rest_ref[...]).astype(f32)

    @pl.when(step < half)
    def upper():
        up_ref[...] = near_up_ref[...] + far

    @pl.when(step >= half)
    def lower():
        down_ref[...] = near_down_ref[...] + far


def expert_sums(near_up, near_down, first, rest):
    count, width = near_up.shape
    steps = 8
    half = steps // 2
    size = count // half
    head = steps // 4
    skip = first.shape[0] // size - head
    block = lambda place: pl.BlockSpec((size, width), lambda i: (place(i), 0))
    upper = block(lambda i: jnp.minimum(i, half - 1))
    lower = block(lambda i: jnp.maximum(i - half, 0))
    return pl.pallas_call(
        expert_sum_kernel,
        grid=(steps,),
        out_shape=(jax.ShapeDtypeStruct((count, width), f32),) * 2,
        in_specs=[
            upper,
            lower,
            block(lambda i: jnp.minimum(i, head - 1) + skip),
            block(lambda i: jnp.maximum(i - head, 0)),
        ],
        out_specs=(upper, lower),
        name="expert_sums",
        compiler_params=pltpu.CompilerParams(vmem_limit_bytes=10 * 2**20),
        cost_estimate=COST,
    )(near_up, near_down, first, rest)


def input_grad_kernel(groups, qw_ref, kw_ref, vw_ref, *refs):
    joint_refs = refs[: len(groups)]
    kept_ref, sent_ref, turned_ref = refs[len(groups) :]
    step = pl.program_id(0)

    @pl.when(step == 0)
    def stack():
        start = 0
        for first_head, heads in groups:
            for at, weight_ref, first, size in stacked_parts(
                first_head, heads, qw_ref, kw_ref, vw_ref
            ):
                turned_ref[start + at : start + at + size, :] = weight_ref[
                    first : first + size, :
                ]
            start += 3 * heads * HEAD_DIM

    total = 0.0
    at = 0
    for joint_ref in joint_refs:
        rows = slice(at, at + joint_ref.shape[1])
        total = total + jnp.dot(
            joint_ref[...], turned_ref[rows, :], preferred_element_type=f32
        )
        at += joint_ref.shape[1]

    @pl.when(step % 2 == 0)
    def keep():
        kept_ref[0] = total.astype(bf16)

    @pl.when(step % 2 == 1)
    def send():
        sent_ref[0] = total.astype(bf16)


def input_grad(groups, weights, joints, first, count, size):
    cols, width = weights[0].shape
    fixed = pl.BlockSpec((cols, width), lambda i: (0, 0))
    return pl.pallas_call(
        functools.partial(input_grad_kernel, groups),
        grid=(count,),
        out_shape=(jax.ShapeDtypeStruct((count // 2, size, width), bf16),) * 2,
        in_specs=[fixed] * 3
        + [
            pl.BlockSpec((size, joint.shape[1]), lambda i: (first + i, 0))
            for joint in joints
        ],
        out_specs=(pl.BlockSpec((1, size, width), lambda i: (i // 2, 0, 0)),) * 2,
        scratch_shapes=[pltpu.VMEM((3 * cols, width), bf16)],
        name="input_grad",
        compiler_params=pltpu.CompilerParams(vmem_limit_bytes=10 * 2**20),
        cost_estimate=COST,
    )(*weights, *joints)


def block_kernel(residual_ref, dispatch_ref, back_ref, out_ref):
    out_ref[...] = residual_ref[...] + contract_rows(dispatch_ref[...], back_ref[...])


def block_output(residual, dispatch, back):
    return pl.pallas_call(
        block_kernel,
        out_shape=jax.ShapeDtypeStruct(residual.shape, f32),
        in_specs=[VMEM] * 3,
        out_specs=VMEM,
        name="block_output",
        compiler_params=pltpu.CompilerParams(vmem_limit_bytes=9 * 2**20),
        cost_estimate=COST,
    )(residual, dispatch, back)


def close_kernel(rank_ref, tokens_ref, gain_ref, grad_ref, *refs):
    *part_refs, out_ref = refs
    grad_in = 0.0
    for part_ref in part_refs:
        grad_in = grad_in + part_ref[...].reshape(out_ref.shape).astype(f32)
    values = tokens_ref[...].astype(f32)
    centred = values - jnp.mean(values, axis=-1, keepdims=True)
    inverse = lax.rsqrt(jnp.mean(centred * centred, axis=-1, keepdims=True) + EPSILON)
    normed = centred * inverse
    scaled = grad_in * gain_ref[...][None]
    out_ref[...] = grad_ref[...] + inverse * (
        scaled
        - jnp.mean(scaled, axis=-1, keepdims=True)
        - normed * jnp.mean(scaled * normed, axis=-1, keepdims=True)
    )


def close(rank, tokens, gain, grad, parts):
    shard, width = grad.shape
    size = shard // 2
    rows = lambda i, r: (i, 0)
    return pl.pallas_call(
        close_kernel,
        grid_spec=pltpu.PrefetchScalarGridSpec(
            num_scalar_prefetch=1,
            grid=(2,),
            in_specs=[
                pl.BlockSpec((size, width), lambda i, r: (2 * r[0] + i, 0)),
                pl.BlockSpec((width,), lambda i, r: (0,)),
                pl.BlockSpec((size, width), rows),
            ]
            + [pl.BlockSpec((1, size, width), lambda i, r: (0, i, 0))] * len(parts),
            out_specs=pl.BlockSpec((size, width), rows),
        ),
        out_shape=jax.ShapeDtypeStruct((shard, width), f32),
        name="close",
        compiler_params=pltpu.CompilerParams(vmem_limit_bytes=12 * 2**20),
        cost_estimate=COST,
    )(rank, tokens, gain, grad, *parts)


def add_low_kernel(a_ref, b_ref, out_ref):
    out_ref[...] = (a_ref[...].astype(f32) + b_ref[...].astype(f32)).astype(bf16)


def add_low(a, b):
    block = pl.BlockSpec(a.shape, lambda i: (0,) * a.ndim)
    return pl.pallas_call(
        add_low_kernel,
        grid=(1,),
        out_shape=jax.ShapeDtypeStruct(a.shape, bf16),
        in_specs=[block, block],
        out_specs=block,
        name="add_low",
        compiler_params=pltpu.CompilerParams(vmem_limit_bytes=6 * 2**20),
        cost_estimate=COST,
    )(a, b)


def tie(*values):
    return lax.optimization_barrier(values)


def finish_kernel(groups, bit_ref, *refs):
    pieces, refs = refs[: 2 * len(groups)], refs[2 * len(groups) :]
    query_ref, key_ref, value_ref = refs[:3]
    bit = bit_ref[0, 0]
    for g, ((first_head, heads), whole_ref) in enumerate(zip(groups, refs[3:])):
        half = whole_ref.shape[0] // 2
        for piece_ref, at in ((pieces[2 * g], bit), (pieces[2 * g + 1], 1 - bit)):
            whole_ref[rows_at(at, half), :] = piece_ref[0:half, :].astype(f32)
        for at, target_ref, first, size in stacked_parts(
            first_head, heads, query_ref, key_ref, value_ref
        ):
            target_ref[first : first + size, :] = whole_ref[at : at + size, :]


def finish(groups, bit, pieces):
    width = pieces[0].shape[1]
    cols = sum(heads for first_head, heads in groups) * HEAD_DIM
    return pl.pallas_call(
        functools.partial(finish_kernel, groups),
        out_shape=(jax.ShapeDtypeStruct((cols, width), f32),) * 3,
        in_specs=[SMEM] + [VMEM] * len(pieces),
        out_specs=(VMEM,) * 3,
        scratch_shapes=[
            pltpu.VMEM((3 * heads * HEAD_DIM, width), f32) for first_head, heads in groups
        ],
        name="finish",
        compiler_params=pltpu.CompilerParams(vmem_limit_bytes=10 * 2**20),
        cost_estimate=COST,
    )(bit, *pieces)


def on_device(
    tokens,
    first_gain,
    first_bias,
    query_weight,
    key_weight,
    value_weight,
    output_weight,
    second_gain,
    second_bias,
    expert_up,
    expert_down,
    item_lengths,
    routes,
    slot_order,
    cotangent,
):
    slots_all, width = tokens.shape
    members = lax.axis_size("tensor")
    shard_rows = slots_all // members
    rank = lax.axis_index("tensor")
    sources = lax.axis_size("dp")
    experts_all = sources * expert_up.shape[0]
    capacity = shard_rows // experts_all
    head_cols = query_weight.shape[1]
    heads = head_cols // HEAD_DIM
    up_matrix = expert_up[0]
    down_matrix = expert_down[0]
    rank_cell = rank.astype(jnp.int32).reshape(1, 1)

    def exchange(rows):
        return lax.all_to_all(
            rows.reshape(sources, -1, width), "dp", split_axis=0, concat_axis=0, tiled=True
        ).reshape(-1, width)

    qw, kw, vw = query_weight.T, key_weight.T, value_weight.T

    dispatch, grad_slots = plan(
        item_lengths, rank_cell, routes, slot_order, cotangent, capacity, experts_all
    )
    flat_grad = exchange(grad_slots)
    tokens, grad_slots = tie(tokens, grad_slots)
    normed_in, qt, kt, vt = project(
        rank_cell[0], tokens, first_gain, first_bias, qw, kw, vw, members
    )
    outputs = [output_weight] + [
        swap(output_weight, "tensor", k) for k in range(1, members)
    ]
    far = members // 2
    *far_heads, far_logs = attend(
        item_lengths, rank_cell, qt, kt, vt, members, far, members - far
    )
    far_heads, kt = tie(far_heads, kt)
    far_arrived = [swap(far_heads[j - far], "tensor", j) for j in range(far, members)]
    *near_heads, near_logs = attend(item_lengths, rank_cell, qt, kt, vt, members, 0, far)
    near_heads, far_arrived, outputs = tie(near_heads, far_arrived, outputs)
    own_heads = near_heads + far_heads
    logs = (near_logs, far_logs)
    all_heads = (
        near_heads[:1]
        + [swap(near_heads[j], "tensor", j) for j in range(1, far)]
        + far_arrived
    )
    residual, outgoing = middle(
        rank_cell[0], tokens, second_gain, second_bias, dispatch, all_heads, outputs
    )
    flat_in = exchange(outgoing)

    flat_grad, outgoing = tie(flat_grad, outgoing)
    grad_act = activation_grads(flat_grad, down_matrix, members)
    near_grads = swap(flat_grad, "tensor", 1)
    flat_in, grad_act, near_grads = tie(flat_in, grad_act, near_grads)
    near_rows = swap(flat_in, "tensor", 1)
    act, grad_pre, act_sent, pre_sent, grad_mid = expert(
        rank_cell[0], flat_in, grad_act, up_matrix, members
    )
    grad_mid, act, near_rows = tie(grad_mid, act, near_rows)
    grad_back = exchange(grad_mid)

    act, act_sent, pre_sent, grad_mid = tie(act, act_sent, pre_sent, grad_mid)
    near_act = swap(act_sent, "tensor", 1)
    near_pre = swap(pre_sent, "tensor", 1)
    made = product(rank_cell[0], act, act_sent, down_matrix, members)
    made, near_act, near_pre = tie(made, near_act, near_pre)
    *expert_far, expert_up_near, expert_down_near = expert_weights(
        [(flat_in, flat_grad, act, grad_pre), (near_rows, near_grads, near_act, near_pre)]
    )
    grad_back, made, expert_far = tie(grad_back, made, expert_far)

    steps = steps_of(members)
    grad_res, sums_second, kept, sent, *grad_heads = turn(
        item_lengths, rank_cell, dispatch, grad_back, residual, cotangent,
        second_gain, all_heads, outputs,
    )
    grad_parts = [grad_heads[0]] + [
        swap(grad_heads[j], "tensor", j) for j in range(1, members)
    ]
    output_near, output_far = output_sums(kept, swap(sent, "tensor", 1), expert_far[0])
    made, grad_heads = tie(made, grad_heads)
    returned = exchange(made)
    grad_parts, output_near, output_far = tie(grad_parts, output_near, output_far)

    bit_cell = (lax.axis_index("dp") & 1).astype(jnp.int32).reshape(1, 1)
    weights = (qw, kw, vw)
    dp_steps = steps_of(sources)
    back = functools.partial(
        attend_back, lens=item_lengths, rank=rank_cell, bit=bit_cell, qt=qt, kt=kt, vt=vt,
        logs=logs, weights=weights, normed=normed_in, outs=own_heads,
    )
    groups = ((0, heads - 1), (heads - 1, 1))
    joint_a, sums_a, own_a, away_a = back(*groups[0], extras=(), grads=grad_parts)
    output_got = swap(output_far, "tensor", 2)
    joint_a, own_a, away_a, output_got, grad_parts, expert_rest, returned = tie(
        joint_a, own_a, away_a, output_got, grad_parts, expert_far[1], returned
    )
    expert_got = swap(expert_rest, "tensor", 2)
    output_sum = add_low(output_near, output_got)
    own_a = add_low(own_a, swap(away_a, "dp", 1))
    output_sum = add_low(output_sum, swap(output_sum, "dp", dp_steps[-1]))
    joint_b, unused, own_b, away_b = back(
        *groups[1], extras=(sums_a, sums_second), grads=grad_parts
    )
    joint_b, own_a, own_b, away_b, output_sum = tie(
        joint_b, own_a, own_b, away_b, output_sum
    )

    far_kept, far_sent = input_grad(
        groups, weights, (joint_a, joint_b), far, members - far, shard_rows
    )
    got_a = swap(own_a, "dp", dp_steps[1])
    got_b = swap(away_b, "dp", 1)
    joint_b, got_a, got_b = tie(joint_b, got_a, got_b)
    near_kept, near_sent = input_grad(
        groups, weights, (joint_a, joint_b), 0, far, shard_rows
    )
    own_b = add_parts(own_b, got_b)
    far_kept = add_low(far_kept, swap(far_sent, "tensor", 1))
    own_a = add_low(own_a, got_a)
    far_kept, own_b, output_sum, own_a = tie(far_kept, own_b, output_sum, own_a)
    near_core = swap(near_sent, "tensor", 1)
    near_far = swap(far_kept, "tensor", 2)
    for step in dp_steps[1:]:
        if step != dp_steps[1]:
            own_a = add_low(own_a, swap(own_a, "dp", step))
        own_b = add_parts(own_b, swap(own_b, "dp", step))
        if step == dp_steps[1]:
            own_b, expert_got = tie(own_b, expert_got)
    up_grad, down_grad = expert_sums(
        expert_up_near, expert_down_near, output_got, expert_got
    )
    own_b, up_grad, down_grad, near_far = tie(own_b, up_grad, down_grad, near_far)
    norm_sums = own_b[-SUM_ROWS:].astype(f32)
    norm_sums = norm_sums[: SUM_ROWS // 2] + norm_sums[SUM_ROWS // 2 :]
    for step in steps:
        norm_sums = norm_sums + swap(norm_sums, "tensor", step)
    pieces = (own_a, swap(own_a, "dp", 1), own_b, swap(own_b, "dp", 1))
    token_grad = close(
        rank_cell[0], tokens, first_gain, grad_res, (near_kept, near_core, near_far)
    )
    for step in dp_steps[:-1]:
        output_sum = add_low(output_sum, swap(output_sum, "dp", step))

    block_out = block_output(residual, dispatch, returned)
    query_grad, key_grad, value_grad = finish(groups, bit_cell, pieces)
    return (
        block_out,
        token_grad,
        (norm_sums[0] - first_bias * norm_sums[1]) / first_gain,
        norm_sums[1],
        query_grad.T,
        key_grad.T,
        value_grad.T,
        output_sum.astype(f32),
        norm_sums[2],
        norm_sums[3],
        up_grad[None],
        down_grad[None],
    )


def solution(mesh):
    in_specs = (
        P("dp", None),
        P(),
        P(),
        P(None, "tensor"),
        P(None, "tensor"),
        P(None, "tensor"),
        P("tensor", None),
        P(),
        P(),
        P("dp", None, None),
        P("dp", None, None),
        P("dp", None),
        P(("dp", "tensor"), None),
        P(("dp", "tensor"), None),
        P(("dp", "tensor"), None),
    )
    out_specs = (
        P(("dp", "tensor"), None),
        P(("dp", "tensor"), None),
        P(),
        P(),
        P(None, "tensor"),
        P(None, "tensor"),
        P(None, "tensor"),
        P("tensor", None),
        P(),
        P(),
        P("dp", None, "tensor"),
        P("dp", "tensor", None),
    )
    return jax.shard_map(
        on_device, mesh=mesh, in_specs=in_specs, out_specs=out_specs, check_vma=False
    )
```

```python
import functools

import jax
import jax.numpy as jnp
from jax import lax
from jax.experimental import pallas as pl
from jax.experimental.pallas import tpu as pltpu
from jax.sharding import PartitionSpec as P

HEAD_DIM = 64
EPSILON = 1e-05
NEGATIVE = -1e30
f32 = jnp.float32
bf16 = jnp.bfloat16
VMEM = pl.BlockSpec(memory_space=pltpu.VMEM)
HBM = pl.BlockSpec(memory_space=pltpu.MemorySpace.HBM)
SMEM = pl.BlockSpec(memory_space=pltpu.SMEM)
SUM_ROWS = 16
COST = pl.CostEstimate(flops=2**20, bytes_accessed=2**20, transcendentals=0)
LONG = pl.CostEstimate(flops=2**34, bytes_accessed=2**24, transcendentals=0)


def layer_norm(values, gain, shift):
    average = jnp.mean(values, axis=-1, keepdims=True)
    centred = values - average
    variance = jnp.mean(centred * centred, axis=-1, keepdims=True)
    return centred * lax.rsqrt(variance + EPSILON) * gain + shift


def contract_rows(left, right):
    return lax.dot_general(
        left, right, (((0,), (0,)), ((), ())), preferred_element_type=f32
    )


def swap(values, axis, step):
    count = lax.axis_size(axis)
    return lax.ppermute(values, axis, [(i, i ^ step) for i in range(count)])


def steps_of(count):
    steps = []
    step = 1
    while step < count:
        steps.append(step)
        step *= 2
    return steps


def normalized(values):
    average = jnp.mean(values, axis=-1, keepdims=True)
    centred = values - average
    variance = jnp.mean(centred * centred, axis=-1, keepdims=True)
    return centred * lax.rsqrt(variance + EPSILON)


def project_kernel(
    rank_ref, tokens_ref, gain_ref, bias_ref, qw_ref, kw_ref, vw_ref,
    normed_ref, qt_ref, kt_ref, vt_ref,
):
    values = tokens_ref[...].astype(f32)
    normed = (normalized(values) * gain_ref[...][None] + bias_ref[...][None]).astype(bf16)
    normed_ref[...] = normed
    for weight_ref, out_ref, factor in (
        (qw_ref, qt_ref, HEAD_DIM ** (-0.5)), (kw_ref, kt_ref, None), (vw_ref, vt_ref, None)
    ):
        made = lax.dot_general(
            weight_ref[...], normed, (((1,), (1,)), ((), ())), preferred_element_type=f32
        ).astype(bf16)
        if factor is not None:
            made = made * jnp.asarray(factor, bf16)
        out_ref[...] = made


def project(rank, tokens, gain, bias, qw, kw, vw, blocks):
    slots, width = tokens.shape
    cols = qw.shape[0]
    size = slots // blocks
    fixed = lambda i, r: (0, 0)
    line = pl.BlockSpec((width,), lambda i, r: (0,))
    return pl.pallas_call(
        project_kernel,
        grid_spec=pltpu.PrefetchScalarGridSpec(
            num_scalar_prefetch=1,
            grid=(blocks,),
            in_specs=[
                pl.BlockSpec((size, width), lambda i, r: (i ^ r[0], 0)),
                line,
                line,
                pl.BlockSpec((cols, width), fixed),
                pl.BlockSpec((cols, width), fixed),
                pl.BlockSpec((cols, width), fixed),
            ],
            out_specs=(
                pl.BlockSpec((size, width), lambda i, r: (i, 0)),
                pl.BlockSpec((cols, size), lambda i, r: (0, i)),
                pl.BlockSpec((cols, size), lambda i, r: (0, i)),
                pl.BlockSpec((cols, size), lambda i, r: (0, i)),
            ),
        ),
        out_shape=(jax.ShapeDtypeStruct((slots, width), bf16),)
        + (jax.ShapeDtypeStruct((cols, slots), bf16),) * 3,
        name="project",
        cost_estimate=COST,
    )(rank, tokens, gain, bias, qw, kw, vw)


def item_ends(lens_ref):
    ends = []
    total = jnp.int32(0)
    for i in range(lens_ref.shape[1]):
        total = total + lens_ref[0, i]
        ends.append(total)
    return ends


def segments_at(place, ends):
    segment = jnp.zeros_like(place)
    for end in ends:
        segment = segment + (place >= end).astype(jnp.int32)
    return segment


def block_span(first, size, unit, ends):
    last = jnp.minimum(first + size, ends[-1]) - 1
    low = jnp.int32(0)
    high = ends[-1]
    for end in ends:
        low = jnp.where(first >= end, end, low)
    for end in reversed(ends):
        high = jnp.where(last < end, end, high)
    empty = first >= ends[-1]
    low_block = jnp.where(empty, 0, low // unit)
    high_block = jnp.where(empty, 0, (high + unit - 1) // unit)
    return low_block, high_block


def rows_at(block, size):
    return pl.ds(pl.multiple_of(block * size, size), size)


def fill_segments(row_ref, col_ref, shard, rank, ends):
    slots = row_ref.shape[1]
    at = lax.broadcasted_iota(jnp.int32, (1, slots), 1)
    place = ((at // shard) ^ rank) * shard + at % shard
    segments = segments_at(place, ends)
    row_ref[...] = segments
    col_ref[...] = jnp.transpose(jnp.broadcast_to(segments, (128, slots)), (1, 0))


def block_bias(row_ref, col_ref, rows, cols):
    return jnp.where(col_ref[rows, 0:1] == row_ref[:, cols], 0.0, NEGATIVE)


def lane_masked(values, head):
    lane = lax.broadcasted_iota(jnp.int32, values.shape, 1)
    inside = (lane >= head * HEAD_DIM) & (lane < (head + 1) * HEAD_DIM)
    return jnp.where(inside, values, jnp.zeros_like(values))


def forward_kernel(
    first, blocks, lens_ref, rank_ref, qt_ref, kt_ref, vt_ref, *refs
):
    *out_refs, log_ref, masked_ref, out_ref, row_ref, col_ref, score_ref = refs
    count, width, size = out_ref.shape
    heads = width // HEAD_DIM
    shard = size
    rank = rank_ref[0, 0]
    ends = item_ends(lens_ref)
    fill_segments(row_ref, col_ref, shard, rank, ends)
    keys = jnp.transpose(kt_ref[...], (1, 0))
    for h in range(heads):
        masked_ref[h] = lane_masked(keys, h)

    def query_block(b, unused):
        at = first + b
        i = at ^ rank
        cols = rows_at(at, size)
        queries = qt_ref[:, cols]

        def score_block(j, carry):
            rows = rows_at(j ^ rank, shard)
            bias = block_bias(row_ref, col_ref, rows, cols)
            result = []
            for h in range(heads):
                scores = jnp.dot(
                    masked_ref[h, rows, :], queries, preferred_element_type=f32
                )
                scores = scores + bias
                score_ref[h, rows_at(j, shard), :] = scores
                part = jnp.max(scores.reshape(-1, 8, size), axis=0)
                result.append(jnp.maximum(carry[h], part))
            return tuple(result)

        low, high = block_span(i * size, size, shard, ends)
        peaks = lax.fori_loop(
            low, high, score_block, (jnp.full((8, size), NEGATIVE, f32),) * heads
        )
        peaks = [jnp.max(peak, axis=0, keepdims=True) for peak in peaks]

        def key_block(j, carry):
            rows = rows_at(j ^ rank, shard)
            result = []
            for h in range(heads):
                summed, total = carry[h]
                soft = jnp.exp(score_ref[h, rows_at(j, shard), :] - peaks[h])
                summed = summed + jnp.sum(soft.reshape(-1, 8, size), axis=0)
                total = total + jnp.dot(
                    vt_ref[pl.ds(h * HEAD_DIM, HEAD_DIM), rows],
                    soft.astype(bf16),
                    preferred_element_type=f32,
                )
                result.append((summed, total))
            return tuple(result)

        start = ((jnp.zeros((8, size), f32), jnp.zeros((HEAD_DIM, size), f32)),) * heads
        done = lax.fori_loop(low, high, key_block, start)
        live = row_ref[:, cols] < len(ends)
        for h in range(heads):
            summed, total = done[h]
            summed = jnp.sum(summed, axis=0, keepdims=True)
            highest = peaks[h]
            summed = jnp.where(live, summed, 1.0)
            result = jnp.where(live, total / summed, 0.0).astype(bf16)
            logs = jnp.where(live, highest + jnp.log(summed), -NEGATIVE)
            out_ref[b, pl.ds(h * HEAD_DIM, HEAD_DIM), :] = result
            log_ref[h, :, rows_at(b, size)] = logs
        return unused

    lax.fori_loop(0, count, query_block, 0)
    for b in range(count):
        out_refs[b][...] = out_ref[b]


def attend(lens, rank, qt, kt, vt, blocks, first, count):
    width, slots = qt.shape
    size = slots // blocks
    heads = width // HEAD_DIM
    return pl.pallas_call(
        functools.partial(forward_kernel, first, blocks),
        out_shape=(jax.ShapeDtypeStruct((width, size), bf16),) * count
        + (jax.ShapeDtypeStruct((heads, 1, count * size), f32),),
        in_specs=[SMEM, SMEM, VMEM, VMEM, VMEM],
        out_specs=(VMEM,) * (count + 1),
        scratch_shapes=[
            pltpu.VMEM((heads, slots, width), bf16),
            pltpu.VMEM((count, width, size), bf16),
            pltpu.VMEM((1, slots), jnp.int32),
            pltpu.VMEM((slots, 128), jnp.int32),
            pltpu.VMEM((heads, slots, size), f32),
        ],
        name="attend",
        compiler_params=pltpu.CompilerParams(vmem_limit_bytes=60 * 2**20),
        cost_estimate=COST,
    )(lens, rank, qt, kt, vt)


def split_rows(values):
    high = values.astype(bf16)
    return jnp.concatenate([high, (values - high.astype(f32)).astype(bf16)], axis=0)


def add_kernel(a_ref, b_ref, out_ref):
    half = out_ref.shape[0] - SUM_ROWS
    line = SUM_ROWS // 2
    total = a_ref[...].astype(f32) + b_ref[...].astype(f32)
    out_ref[:half, :] = total[:half].astype(bf16)
    out_ref[half:, :] = split_rows(total[half : half + line] + total[half + line :])


def add_parts(a, b):
    return pl.pallas_call(
        add_kernel,
        out_shape=jax.ShapeDtypeStruct(a.shape, bf16),
        in_specs=[VMEM, VMEM],
        out_specs=VMEM,
        name="add_parts",
        compiler_params=pltpu.CompilerParams(vmem_limit_bytes=5 * 2**20),
        cost_estimate=COST,
    )(a, b)


def stacked_parts(first_head, heads, query, key, value):
    dim = HEAD_DIM
    parts = []
    for n in range(heads):
        first = (first_head + n) * dim
        parts += [(2 * n * dim, key, first, dim), ((2 * n + 1) * dim, value, first, dim)]
    return parts + [(2 * heads * dim, query, first_head * dim, heads * dim)]


def backward_kernel(
    first_head, heads, blocks, extras, lens_ref, rank_ref, bit_ref, qt_ref, kt_ref, vt_ref,
    near_ref, far_ref, qw_ref, kw_ref, vw_ref, normed_ref, *rest
):
    extra_refs, rest = rest[:extras], rest[extras:]
    width, slots = qt_ref.shape
    shard = slots // blocks
    dim = HEAD_DIM
    out_refs, grad_refs = rest[:blocks], rest[blocks : 2 * blocks]
    joint_ref, sums_ref, own_ref, away_ref = rest[2 * blocks : 2 * blocks + 4]
    kv_ref, q0_ref, og_ref, right_ref, inner_ref, dq_ref, made_ref = rest[-13:-6]
    log_ref = rest[-6]
    row_ref, col_ref = rest[-5:-3]
    turned_ref, rows_ref, copied = rest[-3:]
    fetch = pltpu.make_async_copy(normed_ref, rows_ref, copied)
    fetch.start()
    unit = shard // 2
    rank = rank_ref[0, 0]
    ends = item_ends(lens_ref)
    fill_segments(row_ref, col_ref, shard, rank, ends)
    near = near_ref.shape[2]
    log_ref[:, :, :near] = near_ref[...]
    log_ref[:, :, near:] = far_ref[...]
    zero = jnp.zeros((dim, slots), bf16)
    for n in range(heads):
        part = slice((first_head + n) * dim, (first_head + n + 1) * dim)
        both = jnp.concatenate([kt_ref[part, :], vt_ref[part, :]], axis=0)
        kv_ref[n] = jnp.transpose(both, (1, 0))
        padded = jnp.concatenate([qt_ref[part, :], zero], axis=0)
        q0_ref[n] = jnp.transpose(padded, (1, 0))
        right_ref[n, 0] = padded
        for b in range(blocks):
            grad = grad_refs[b][part, :]
            cols = slice(b * shard, (b + 1) * shard)
            padded = jnp.concatenate([zero[:, :shard], grad], axis=0)
            og_ref[n, cols, :] = jnp.transpose(padded, (1, 0))
            right_ref[n, 1, :, cols] = padded
            inner_ref[n, :, cols] = jnp.sum(
                out_refs[b][part, :].astype(f32) * grad.astype(f32), axis=0, keepdims=True
            )
    dq_ref[...] = jnp.zeros_like(dq_ref)

    def key_block(j, unused):
        at_key = ((j // 2) ^ rank) * 2 + j % 2
        rows = rows_at(at_key, unit)

        def query_block(i, totals):
            at = i ^ rank
            cols = rows_at(at, shard)
            same = col_ref[rows, 0:1] == row_ref[:, cols]
            result = []
            for n in range(heads):
                head = first_head + n
                kv = kv_ref[n, rows, :]
                scores = jnp.dot(kv, right_ref[n, 0, :, cols], preferred_element_type=f32)
                grad_soft = jnp.dot(kv, right_ref[n, 1, :, cols], preferred_element_type=f32)
                soft = jnp.where(same, jnp.exp(scores - log_ref[head, :, cols]), 0.0)
                grad_scores = (soft * (grad_soft - inner_ref[n, :, cols])).astype(bf16)
                total = totals[n] + jnp.dot(
                    soft.astype(bf16), og_ref[n, cols, :], preferred_element_type=f32
                )
                total = total + jnp.dot(
                    grad_scores, q0_ref[n, cols, :], preferred_element_type=f32
                )
                dq_ref[n, :, cols] += jnp.dot(
                    kt_ref[pl.ds(head * dim, dim), rows], grad_scores,
                    preferred_element_type=f32,
                )
                result.append(total)
            return tuple(result)

        low, high = block_span(j * unit, unit, shard, ends)
        start = (jnp.zeros((unit, 2 * dim), f32),) * heads
        totals = lax.fori_loop(low, high, query_block, start)
        for n in range(heads):
            part = slice(2 * dim * n, 2 * dim * (n + 1))
            total = totals[n].astype(bf16)
            joint_ref[rows, part] = total
            turned_ref[part, rows] = jnp.transpose(total, (1, 0))
        return unused

    lax.fori_loop(0, 2 * blocks, key_block, 0)
    dq = (dq_ref[...] * dim ** (-0.5)).astype(bf16).reshape(heads * dim, slots)
    turned_ref[2 * dim * heads :, :] = dq
    joint_ref[:, 2 * dim * heads :] = jnp.transpose(dq, (1, 0))
    fetch.wait()
    made_ref[...] = jnp.dot(turned_ref[...], rows_ref[...], preferred_element_type=f32)
    gains = jnp.zeros((1, rows_ref.shape[1]), f32)
    shifts = jnp.zeros((1, rows_ref.shape[1]), f32)
    for at, weight_ref, first, size in stacked_parts(
        first_head, heads, qw_ref, kw_ref, vw_ref
    ):
        weight = weight_ref[first : first + size, :].astype(f32)
        gains += jnp.sum(weight * made_ref[at : at + size, :], axis=0, keepdims=True)
        total = jnp.sum(turned_ref[at : at + size, :].astype(f32), axis=1, keepdims=True)
        shifts += jnp.sum(weight * total, axis=0, keepdims=True)
    sums_ref[0:1] = gains
    sums_ref[1:2] = shifts
    half = made_ref.shape[0] // 2
    bit = bit_ref[0, 0]
    for part_ref, at in ((own_ref, bit), (away_ref, 1 - bit)):
        part_ref[0:half, :] = made_ref[rows_at(at, half), :].astype(bf16)
        if extras:
            lines = [sums_ref[...] + extra_refs[0][...], extra_refs[1][...]]
            lines.append(jnp.zeros((SUM_ROWS // 2 - 4, gains.shape[1]), f32))
            part_ref[half:, :] = split_rows(jnp.concatenate(lines, axis=0))


def attend_back(
    first_head, heads, extras, lens, rank, bit, qt, kt, vt, logs, weights, normed, outs, grads
):
    slots, width = normed.shape
    blocks = len(outs)
    dim = HEAD_DIM
    cols = 3 * dim * heads
    rows = cols // 2 + (SUM_ROWS if extras else 0)
    return pl.pallas_call(
        functools.partial(backward_kernel, first_head, heads, blocks, len(extras)),
        out_shape=(
            jax.ShapeDtypeStruct((slots, cols), bf16),
            jax.ShapeDtypeStruct((2, width), f32),
        )
        + (jax.ShapeDtypeStruct((rows, width), bf16),) * 2,
        in_specs=[SMEM, SMEM, SMEM]
        + [VMEM] * 8
        + [pl.BlockSpec(memory_space=pl.ANY)]
        + [VMEM] * (len(extras) + 2 * blocks),
        out_specs=(VMEM,) * 4,
        scratch_shapes=[pltpu.VMEM((heads, slots, 2 * dim), bf16)] * 3
        + [
            pltpu.VMEM((heads, 2, 2 * dim, slots), bf16),
            pltpu.VMEM((heads, 1, slots), f32),
            pltpu.VMEM((heads, dim, slots), f32),
            pltpu.VMEM((cols, width), f32),
            pltpu.VMEM((qt.shape[0] // dim, 1, slots), f32),
            pltpu.VMEM((1, slots), jnp.int32),
            pltpu.VMEM((slots, 128), jnp.int32),
            pltpu.VMEM((cols, slots), bf16),
            pltpu.VMEM((slots, width), bf16),
            pltpu.SemaphoreType.DMA,
        ],
        name="attend_back",
        compiler_params=pltpu.CompilerParams(vmem_limit_bytes=60 * 2**20),
        cost_estimate=COST,
    )(lens, rank, bit, qt, kt, vt, *logs, *weights, normed, *extras, *outs, *grads)


def plan_kernel(capacity, lens_ref, rank_ref, routes_ref, order_ref, grad_ref,
                dispatch_ref, slots_ref):
    shard = routes_ref.shape[1]
    first = rank_ref[0, 0] * shard
    ends = item_ends(lens_ref)
    chosen_row = routes_ref[...]
    chosen_col = jnp.transpose(jnp.broadcast_to(chosen_row, (128, shard)), (1, 0))[:, 0:1]
    order_row = order_ref[...]
    order_col = jnp.transpose(jnp.broadcast_to(order_row, (128, shard)), (1, 0))[:, 0:1]
    alive_row = segments_at(
        first + lax.broadcasted_iota(jnp.int32, (1, shard), 1), ends
    ) < len(ends)
    alive_col = segments_at(
        first + lax.broadcasted_iota(jnp.int32, (shard, 1), 0), ends
    ) < len(ends)
    ahead = (chosen_col == chosen_row) & (order_col < order_row) & alive_col
    ranked = jnp.sum(ahead.astype(jnp.int32), axis=0, keepdims=True)
    kept = alive_row & (ranked < capacity)
    slot = jnp.where(kept, chosen_row * capacity + ranked, -1)
    dispatch = (
        lax.broadcasted_iota(jnp.int32, dispatch_ref.shape, 0) == slot
    ).astype(f32).astype(bf16)
    dispatch_ref[...] = dispatch
    slots_ref[...] = jnp.dot(
        dispatch, grad_ref[...], preferred_element_type=f32
    ).astype(bf16)


def plan(lens, rank, routes, order, grads, capacity, experts_all):
    shard, width = grads.shape
    count = experts_all * capacity
    return pl.pallas_call(
        functools.partial(plan_kernel, capacity),
        out_shape=(
            jax.ShapeDtypeStruct((count, shard), bf16),
            jax.ShapeDtypeStruct((count, width), bf16),
        ),
        in_specs=[SMEM, SMEM, VMEM, VMEM, VMEM],
        out_specs=(VMEM, VMEM),
        name="plan",
        cost_estimate=COST,
    )(lens, rank, routes.reshape(1, -1), order, grads)


def across(left, right):
    return lax.dot_general(
        left, right, (((1,), (1,)), ((), ())), preferred_element_type=f32
    )


def middle_kernel(count, rank_ref, tokens_ref, gain_ref, bias_ref, dispatch_ref, *refs):
    head_refs, weight_refs = refs[:count], refs[count : 2 * count]
    residual_ref, rows_ref = refs[2 * count :]
    residual = tokens_ref[...].astype(f32)
    for head_ref, weight_ref in zip(head_refs, weight_refs):
        residual = residual + contract_rows(head_ref[...], weight_ref[...])
    residual_ref[...] = residual
    normed = (normalized(residual) * gain_ref[...][None] + bias_ref[...][None]).astype(bf16)
    rows_ref[...] = jnp.dot(
        dispatch_ref[...], normed, preferred_element_type=f32
    ).astype(bf16)


def middle(rank, tokens, gain, bias, dispatch, heads, weights):
    count, shard = dispatch.shape
    width = tokens.shape[1]
    fixed = lambda array: pl.BlockSpec(array.shape, lambda i, r: (0,) * array.ndim)
    small = [gain, bias, dispatch, *heads, *weights]
    return pl.pallas_call(
        functools.partial(middle_kernel, len(heads)),
        grid_spec=pltpu.PrefetchScalarGridSpec(
            num_scalar_prefetch=1,
            grid=(1,),
            in_specs=[pl.BlockSpec((shard, width), lambda i, r: (r[0], 0))]
            + [fixed(array) for array in small],
            out_specs=(
                pl.BlockSpec((shard, width), lambda i, r: (0, 0)),
                pl.BlockSpec((count, width), lambda i, r: (0, 0)),
            ),
        ),
        out_shape=(
            jax.ShapeDtypeStruct((shard, width), f32),
            jax.ShapeDtypeStruct((count, width), bf16),
        ),
        name="middle",
        cost_estimate=COST,
    )(rank, tokens, *small)


def turn_kernel(
    count, lens_ref, rank_ref, dispatch_ref, back_ref, residual_ref, cotangent_ref,
    gain_ref, *refs
):
    head_refs, weight_refs = refs[:count], refs[count : 2 * count]
    grad_ref, sums_ref, kept_ref, sent_ref = refs[2 * count : 2 * count + 4]
    part_refs = refs[2 * count + 4 :]
    shard = residual_ref.shape[0]
    grad_normed = contract_rows(dispatch_ref[...], back_ref[...])
    values = residual_ref[...]
    centred = values - jnp.mean(values, axis=-1, keepdims=True)
    inverse = lax.rsqrt(jnp.mean(centred * centred, axis=-1, keepdims=True) + EPSILON)
    normed = centred * inverse
    sums_ref[0:1] = jnp.sum(grad_normed * normed, axis=0, keepdims=True)
    sums_ref[1:2] = jnp.sum(grad_normed, axis=0, keepdims=True)
    scaled = grad_normed * gain_ref[...][None]
    grad = cotangent_ref[...].astype(f32) + inverse * (
        scaled
        - jnp.mean(scaled, axis=-1, keepdims=True)
        - normed * jnp.mean(scaled * normed, axis=-1, keepdims=True)
    )
    grad_ref[...] = grad
    low = grad.astype(bf16)
    place = rank_ref[0, 0] * shard + lax.broadcasted_iota(jnp.int32, (1, shard), 1)
    alive = place < item_ends(lens_ref)[-1]
    for weight_ref, part_ref in zip(weight_refs, part_refs):
        part_ref[...] = jnp.where(alive, across(weight_ref[...], low), 0.0).astype(bf16)
    for j, head_ref in enumerate(head_refs):
        made = jnp.dot(head_ref[...], low, preferred_element_type=f32)
        (kept_ref, sent_ref)[j % 2][j // 2] = made.astype(bf16)


def turn(lens, rank, dispatch, back, residual, cotangent, gain, heads, weights):
    shard, width = residual.shape
    cols = weights[0].shape[0]
    count = len(weights)
    return pl.pallas_call(
        functools.partial(turn_kernel, count),
        out_shape=(
            jax.ShapeDtypeStruct((shard, width), f32),
            jax.ShapeDtypeStruct((2, width), f32),
            jax.ShapeDtypeStruct((count // 2, cols, width), bf16),
            jax.ShapeDtypeStruct((count // 2, cols, width), bf16),
        )
        + (jax.ShapeDtypeStruct((cols, shard), bf16),) * count,
        in_specs=[SMEM, SMEM] + [VMEM] * (5 + 2 * count),
        out_specs=(VMEM,) * (4 + count),
        name="turn",
        cost_estimate=COST,
    )(lens, rank, dispatch, back, residual, cotangent, gain, *heads, *weights)


def output_sum_kernel(kept_ref, core_ref, first_ref, near_ref, far_ref):
    cols = near_ref.shape[0]
    total = [
        (kept_ref[j].astype(f32) + core_ref[j].astype(f32)).astype(bf16) for j in range(2)
    ]
    near_ref[...] = total[0]
    far_ref[:cols, :] = total[1]
    far_ref[cols:, :] = first_ref[...]


def output_sums(kept, core, first):
    slots, cols, width = kept.shape
    return pl.pallas_call(
        output_sum_kernel,
        out_shape=(
            jax.ShapeDtypeStruct((cols, width), bf16),
            jax.ShapeDtypeStruct((cols + first.shape[0], width), bf16),
        ),
        in_specs=[VMEM] * 3,
        out_specs=(VMEM, VMEM),
        name="output_sums",
        compiler_params=pltpu.CompilerParams(vmem_limit_bytes=52 * 2**20),
        cost_estimate=LONG,
    )(kept, core, first)


def gelu_parts(values):
    below = 0.5 + 0.5 * lax.erf(values * (0.5**0.5))
    density = jnp.exp(-0.5 * values * values) * (0.5 / jnp.pi) ** 0.5
    return values * below, below + values * density


def part_at(step, parts, rank):
    half = parts // 2
    return (2 * (step % half) + step // half) ^ rank


def activation_kernel(grad_ref, down_ref, out_ref):
    out_ref[...] = across(grad_ref[...], down_ref[...]).astype(bf16)


def activation_grads(grads, down, parts):
    count, width = grads.shape
    hidden = down.shape[0]
    size = hidden // parts
    return pl.pallas_call(
        activation_kernel,
        grid=(parts,),
        out_shape=jax.ShapeDtypeStruct((count, hidden), bf16),
        in_specs=[
            pl.BlockSpec((count, width), lambda i: (0, 0)),
            pl.BlockSpec((size, width), lambda i: (i, 0)),
        ],
        out_specs=pl.BlockSpec((count, size), lambda i: (0, i)),
        name="activation_grads",
        cost_estimate=COST,
    )(grads, down)


def expert_kernel(
    parts, rank_ref, in_ref, grad_act_ref, up_ref,
    act_kept_ref, pre_kept_ref, act_sent_ref, pre_sent_ref, mid_ref,
    grads_ref, ups_ref, acts_ref, pres_ref, sum_ref, fetched, stored,
):
    rank = rank_ref[0, 0]
    size = ups_ref.shape[2]
    half = parts // 2

    def fetch(p):
        cols = rows_at(part_at(p, parts, rank), size)
        return (
            pltpu.make_async_copy(up_ref.at[:, cols], ups_ref.at[p], fetched.at[0, p]),
            pltpu.make_async_copy(grad_act_ref.at[:, cols], grads_ref.at[p], fetched.at[1, p]),
        )

    def store(p, act_out_ref, pre_out_ref):
        cols = rows_at(p % half, size)
        return (
            pltpu.make_async_copy(acts_ref.at[p], act_out_ref.at[:, cols], stored.at[0, p]),
            pltpu.make_async_copy(pres_ref.at[p], pre_out_ref.at[:, cols], stored.at[1, p]),
        )

    for p in range(parts):
        for copy in fetch(p):
            copy.start()
    sum_ref[...] = jnp.zeros_like(sum_ref)

    def part(p, unused):
        for copy in fetch(p):
            copy.wait()
        pre = jnp.dot(in_ref[...], ups_ref[p], preferred_element_type=f32)
        act, slope = gelu_parts(pre)
        acts_ref[p] = act.astype(bf16)
        grad_pre = (grads_ref[p].astype(f32) * slope).astype(bf16)
        pres_ref[p] = grad_pre
        sum_ref[...] += across(grad_pre, ups_ref[p])

        @pl.when(p < half)
        def keep():
            for copy in store(p, act_kept_ref, pre_kept_ref):
                copy.start()

        @pl.when(p >= half)
        def send():
            for copy in store(p, act_sent_ref, pre_sent_ref):
                copy.start()

        return unused

    lax.fori_loop(0, parts, part, 0)
    mid_ref[...] = sum_ref[...].astype(bf16)
    for p in range(parts):
        outs = (act_kept_ref, pre_kept_ref) if p < half else (act_sent_ref, pre_sent_ref)
        for copy in store(p, *outs):
            copy.wait()


def expert(rank, rows, grad_act, up, parts):
    count, width = rows.shape
    hidden = up.shape[1]
    size = hidden // parts
    return pl.pallas_call(
        functools.partial(expert_kernel, parts),
        out_shape=(jax.ShapeDtypeStruct((count, hidden // 2), bf16),) * 4
        + (jax.ShapeDtypeStruct((count, width), bf16),),
        in_specs=[SMEM, VMEM, HBM, HBM],
        out_specs=(HBM,) * 4 + (VMEM,),
        scratch_shapes=[
            pltpu.VMEM((parts, count, size), grad_act.dtype),
            pltpu.VMEM((parts, width, size), bf16),
            pltpu.VMEM((parts, count, size), bf16),
            pltpu.VMEM((parts, count, size), bf16),
            pltpu.VMEM((count, width), f32),
            pltpu.SemaphoreType.DMA((2, parts)),
            pltpu.SemaphoreType.DMA((2, parts)),
        ],
        name="expert",
        compiler_params=pltpu.CompilerParams(vmem_limit_bytes=52 * 2**20),
        cost_estimate=COST,
    )(rank.reshape(1, 1), rows, grad_act, up)


def product_kernel(parts, rank_ref, kept_ref, sent_ref, down_ref, out_ref,
                   acts_ref, downs_ref, sum_ref, fetched):
    rank = rank_ref[0, 0]
    size = downs_ref.shape[1]
    half = parts // 2

    def fetch(p):
        rows = rows_at(part_at(p, parts, rank), size)
        source = kept_ref if p < half else sent_ref
        cols = slice((p % half) * size, (p % half + 1) * size)
        return (
            pltpu.make_async_copy(down_ref.at[rows, :], downs_ref.at[p], fetched.at[0, p]),
            pltpu.make_async_copy(source.at[:, cols], acts_ref.at[p], fetched.at[1, p]),
        )

    for p in range(parts):
        for copy in fetch(p):
            copy.start()
    sum_ref[...] = jnp.zeros_like(sum_ref)
    for p in range(parts):
        for copy in fetch(p):
            copy.wait()
        sum_ref[...] += jnp.dot(acts_ref[p], downs_ref[p], preferred_element_type=f32)
    out_ref[...] = sum_ref[...].astype(bf16)


def product(rank, kept, sent, down, parts):
    count = kept.shape[0]
    hidden, width = down.shape
    size = hidden // parts
    return pl.pallas_call(
        functools.partial(product_kernel, parts),
        out_shape=jax.ShapeDtypeStruct((count, width), bf16),
        in_specs=[SMEM, HBM, HBM, HBM],
        out_specs=VMEM,
        scratch_shapes=[
            pltpu.VMEM((parts, count, size), bf16),
            pltpu.VMEM((parts, size, width), bf16),
            pltpu.VMEM((count, width), f32),
            pltpu.SemaphoreType.DMA((2, parts)),
        ],
        name="product",
        cost_estimate=COST,
    )(rank.reshape(1, 1), kept, sent, down)


def weight_kernel(groups, *refs):
    first_ref, rest_ref, up_ref, down_ref = refs[-4:]
    dup = ddown = 0.0
    for g in range(groups):
        in_ref, grad_ref, act_ref, pre_ref = refs[4 * g : 4 * g + 4]
        dup = dup + contract_rows(in_ref[...], pre_ref[...])
        ddown = ddown + contract_rows(act_ref[...], grad_ref[...])
    cut = first_ref.shape[0]

    @pl.when(pl.program_id(0) == 0)
    def far():
        first_ref[...] = dup[:cut].astype(bf16)
        rest_ref[: dup.shape[0] - cut, :] = dup[cut:].astype(bf16)
        rest_ref[dup.shape[0] - cut :, :] = ddown.astype(bf16)

    @pl.when(pl.program_id(0) == 1)
    def near():
        up_ref[...] = dup
        down_ref[...] = ddown


def expert_weights(groups):
    count, width = groups[0][0].shape
    size = groups[0][2].shape[1] // 2
    fixed = pl.BlockSpec((count, width), lambda i: (0, 0))
    columns = pl.BlockSpec((count, size), lambda i: (0, 1 - i))
    cut = (width + size) // 4
    shapes = ((cut, size), (width + size - cut, size), (width, size), (size, width))
    return pl.pallas_call(
        functools.partial(weight_kernel, len(groups)),
        grid=(2,),
        in_specs=[fixed, fixed, columns, columns] * len(groups),
        out_specs=tuple(pl.BlockSpec(shape, lambda i: (0, 0)) for shape in shapes),
        out_shape=tuple(
            jax.ShapeDtypeStruct(shape, bf16 if k < 2 else f32)
            for k, shape in enumerate(shapes)
        ),
        name="expert_weights",
        compiler_params=pltpu.CompilerParams(vmem_limit_bytes=60 * 2**20),
        cost_estimate=COST,
    )(*[values for group in groups for values in group])


def expert_sum_kernel(near_up_ref, near_down_ref, first_ref, rest_ref, up_ref, down_ref):
    step = pl.program_id(0)
    half = pl.num_programs(0) // 2
    far = jnp.where(step < half // 2, first_ref[...], rest_ref[...]).astype(f32)

    @pl.when(step < half)
    def upper():
        up_ref[...] = near_up_ref[...] + far

    @pl.when(step >= half)
    def lower():
        down_ref[...] = near_down_ref[...] + far


def expert_sums(near_up, near_down, first, rest):
    count, width = near_up.shape
    steps = 8
    half = steps // 2
    size = count // half
    head = steps // 4
    skip = first.shape[0] // size - head
    block = lambda place: pl.BlockSpec((size, width), lambda i: (place(i), 0))
    upper = block(lambda i: jnp.minimum(i, half - 1))
    lower = block(lambda i: jnp.maximum(i - half, 0))
    return pl.pallas_call(
        expert_sum_kernel,
        grid=(steps,),
        out_shape=(jax.ShapeDtypeStruct((count, width), f32),) * 2,
        in_specs=[
            upper,
            lower,
            block(lambda i: jnp.minimum(i, head - 1) + skip),
            block(lambda i: jnp.maximum(i - head, 0)),
        ],
        out_specs=(upper, lower),
        name="expert_sums",
        compiler_params=pltpu.CompilerParams(vmem_limit_bytes=10 * 2**20),
        cost_estimate=COST,
    )(near_up, near_down, first, rest)


def input_grad_kernel(groups, qw_ref, kw_ref, vw_ref, *refs):
    joint_refs = refs[: len(groups)]
    kept_ref, sent_ref, turned_ref = refs[len(groups) :]
    step = pl.program_id(0)

    @pl.when(step == 0)
    def stack():
        start = 0
        for first_head, heads in groups:
            for at, weight_ref, first, size in stacked_parts(
                first_head, heads, qw_ref, kw_ref, vw_ref
            ):
                turned_ref[start + at : start + at + size, :] = weight_ref[
                    first : first + size, :
                ]
            start += 3 * heads * HEAD_DIM

    total = 0.0
    at = 0
    for joint_ref in joint_refs:
        rows = slice(at, at + joint_ref.shape[1])
        total = total + jnp.dot(
            joint_ref[...], turned_ref[rows, :], preferred_element_type=f32
        )
        at += joint_ref.shape[1]

    @pl.when(step % 2 == 0)
    def keep():
        kept_ref[0] = total.astype(bf16)

    @pl.when(step % 2 == 1)
    def send():
        sent_ref[0] = total.astype(bf16)


def input_grad(groups, weights, joints, first, count, size):
    cols, width = weights[0].shape
    fixed = pl.BlockSpec((cols, width), lambda i: (0, 0))
    return pl.pallas_call(
        functools.partial(input_grad_kernel, groups),
        grid=(count,),
        out_shape=(jax.ShapeDtypeStruct((count // 2, size, width), bf16),) * 2,
        in_specs=[fixed] * 3
        + [
            pl.BlockSpec((size, joint.shape[1]), lambda i: (first + i, 0))
            for joint in joints
        ],
        out_specs=(pl.BlockSpec((1, size, width), lambda i: (i // 2, 0, 0)),) * 2,
        scratch_shapes=[pltpu.VMEM((3 * cols, width), bf16)],
        name="input_grad",
        compiler_params=pltpu.CompilerParams(vmem_limit_bytes=10 * 2**20),
        cost_estimate=COST,
    )(*weights, *joints)


def close_kernel(
    rank_ref, tokens_ref, gain_ref, grad_ref, residual_ref, dispatch_ref, back_ref, *refs
):
    *part_refs, out_ref, block_ref = refs
    block_ref[...] = residual_ref[...] + contract_rows(dispatch_ref[...], back_ref[...])
    grad_in = 0.0
    for part_ref in part_refs:
        grad_in = grad_in + part_ref[...].reshape(out_ref.shape).astype(f32)
    values = tokens_ref[...].astype(f32)
    centred = values - jnp.mean(values, axis=-1, keepdims=True)
    inverse = lax.rsqrt(jnp.mean(centred * centred, axis=-1, keepdims=True) + EPSILON)
    normed = centred * inverse
    scaled = grad_in * gain_ref[...][None]
    out_ref[...] = grad_ref[...] + inverse * (
        scaled
        - jnp.mean(scaled, axis=-1, keepdims=True)
        - normed * jnp.mean(scaled * normed, axis=-1, keepdims=True)
    )


def close(rank, tokens, gain, grad, residual, dispatch, back, parts):
    shard, width = grad.shape
    count = dispatch.shape[0]
    size = shard // 2
    rows = pl.BlockSpec((size, width), lambda i, r: (i, 0))
    return pl.pallas_call(
        close_kernel,
        grid_spec=pltpu.PrefetchScalarGridSpec(
            num_scalar_prefetch=1,
            grid=(2,),
            in_specs=[
                pl.BlockSpec((size, width), lambda i, r: (2 * r[0] + i, 0)),
                pl.BlockSpec((width,), lambda i, r: (0,)),
                rows,
                rows,
                pl.BlockSpec((count, size), lambda i, r: (0, i)),
                pl.BlockSpec((count, width), lambda i, r: (0, 0)),
            ]
            + [pl.BlockSpec((1, size, width), lambda i, r: (0, i, 0))] * len(parts),
            out_specs=(rows, rows),
        ),
        out_shape=(jax.ShapeDtypeStruct((shard, width), f32),) * 2,
        name="close",
        compiler_params=pltpu.CompilerParams(vmem_limit_bytes=16 * 2**20),
        cost_estimate=COST,
    )(rank, tokens, gain, grad, residual, dispatch, back, *parts)


def add_low_kernel(a_ref, b_ref, out_ref):
    out_ref[...] = (a_ref[...].astype(f32) + b_ref[...].astype(f32)).astype(bf16)


def add_low(a, b):
    block = pl.BlockSpec(a.shape, lambda i: (0,) * a.ndim)
    return pl.pallas_call(
        add_low_kernel,
        grid=(1,),
        out_shape=jax.ShapeDtypeStruct(a.shape, bf16),
        in_specs=[block, block],
        out_specs=block,
        name="add_low",
        compiler_params=pltpu.CompilerParams(vmem_limit_bytes=6 * 2**20),
        cost_estimate=COST,
    )(a, b)


def after(value, *others):
    return lax.optimization_barrier((value, *others))[0]


def tie(*values):
    return lax.optimization_barrier(values)


def finish_kernel(groups, bit_ref, *refs):
    pieces, refs = refs[: 2 * len(groups)], refs[2 * len(groups) :]
    query_ref, key_ref, value_ref = refs[:3]
    bit = bit_ref[0, 0]
    for g, ((first_head, heads), whole_ref) in enumerate(zip(groups, refs[3:])):
        half = whole_ref.shape[0] // 2
        for piece_ref, at in ((pieces[2 * g], bit), (pieces[2 * g + 1], 1 - bit)):
            whole_ref[rows_at(at, half), :] = piece_ref[0:half, :].astype(f32)
        for at, target_ref, first, size in stacked_parts(
            first_head, heads, query_ref, key_ref, value_ref
        ):
            target_ref[first : first + size, :] = whole_ref[at : at + size, :]


def finish(groups, bit, pieces):
    width = pieces[0].shape[1]
    cols = sum(heads for first_head, heads in groups) * HEAD_DIM
    return pl.pallas_call(
        functools.partial(finish_kernel, groups),
        out_shape=(jax.ShapeDtypeStruct((cols, width), f32),) * 3,
        in_specs=[SMEM] + [VMEM] * len(pieces),
        out_specs=(VMEM,) * 3,
        scratch_shapes=[
            pltpu.VMEM((3 * heads * HEAD_DIM, width), f32) for first_head, heads in groups
        ],
        name="finish",
        compiler_params=pltpu.CompilerParams(vmem_limit_bytes=10 * 2**20),
        cost_estimate=COST,
    )(bit, *pieces)


def on_device(
    tokens,
    first_gain,
    first_bias,
    query_weight,
    key_weight,
    value_weight,
    output_weight,
    second_gain,
    second_bias,
    expert_up,
    expert_down,
    item_lengths,
    routes,
    slot_order,
    cotangent,
):
    slots_all, width = tokens.shape
    members = lax.axis_size("tensor")
    shard_rows = slots_all // members
    rank = lax.axis_index("tensor")
    sources = lax.axis_size("dp")
    experts_all = sources * expert_up.shape[0]
    capacity = shard_rows // experts_all
    head_cols = query_weight.shape[1]
    heads = head_cols // HEAD_DIM
    up_matrix = expert_up[0]
    down_matrix = expert_down[0]
    rank_cell = rank.astype(jnp.int32).reshape(1, 1)

    def exchange(rows):
        return lax.all_to_all(
            rows.reshape(sources, -1, width), "dp", split_axis=0, concat_axis=0, tiled=True
        ).reshape(-1, width)

    qw, kw, vw = query_weight.T, key_weight.T, value_weight.T

    dispatch, grad_slots = plan(
        item_lengths, rank_cell, routes, slot_order, cotangent, capacity, experts_all
    )
    flat_grad = exchange(grad_slots)
    tokens, grad_slots = tie(tokens, grad_slots)
    normed_in, qt, kt, vt = project(
        rank_cell[0], tokens, first_gain, first_bias, qw, kw, vw, members
    )
    outputs = [output_weight] + [
        swap(output_weight, "tensor", k) for k in range(1, members)
    ]
    far = members // 2
    *far_heads, far_logs = attend(
        item_lengths, rank_cell, qt, kt, vt, members, far, members - far
    )
    far_heads, kt = tie(far_heads, kt)
    far_arrived = [swap(far_heads[j - far], "tensor", j) for j in range(far, members)]
    *near_heads, near_logs = attend(item_lengths, rank_cell, qt, kt, vt, members, 0, far)
    near_heads, far_arrived, outputs = tie(near_heads, far_arrived, outputs)
    own_heads = near_heads + far_heads
    logs = (near_logs, far_logs)
    all_heads = (
        near_heads[:1]
        + [swap(near_heads[j], "tensor", j) for j in range(1, far)]
        + far_arrived
    )
    residual, outgoing = middle(
        rank_cell[0], tokens, second_gain, second_bias, dispatch, all_heads, outputs
    )
    flat_in = exchange(outgoing)

    flat_grad, outgoing = tie(flat_grad, outgoing)
    grad_act = activation_grads(flat_grad, down_matrix, members)
    near_grads = swap(flat_grad, "tensor", 1)
    flat_in, grad_act, near_grads = tie(flat_in, grad_act, near_grads)
    near_rows = swap(flat_in, "tensor", 1)
    act, grad_pre, act_sent, pre_sent, grad_mid = expert(
        rank_cell[0], flat_in, grad_act, up_matrix, members
    )
    grad_mid, act, near_rows = tie(grad_mid, act, near_rows)
    grad_back = exchange(grad_mid)

    act, act_sent, pre_sent, grad_mid = tie(act, act_sent, pre_sent, grad_mid)
    near_act = swap(act_sent, "tensor", 1)
    near_pre = swap(pre_sent, "tensor", 1)
    made = product(rank_cell[0], act, act_sent, down_matrix, members)
    made, near_act, near_pre = tie(made, near_act, near_pre)
    *expert_far, expert_up_near, expert_down_near = expert_weights(
        [(flat_in, flat_grad, act, grad_pre), (near_rows, near_grads, near_act, near_pre)]
    )
    grad_back, made, expert_far = tie(grad_back, made, expert_far)

    steps = steps_of(members)
    grad_res, sums_second, kept, sent, *grad_heads = turn(
        item_lengths, rank_cell, dispatch, grad_back, residual, cotangent,
        second_gain, all_heads, outputs,
    )
    grad_parts = [grad_heads[0]] + [
        swap(grad_heads[j], "tensor", j) for j in range(1, members)
    ]
    output_near, output_far = output_sums(kept, swap(sent, "tensor", 1), expert_far[0])
    made, grad_heads = tie(made, grad_heads)
    returned = exchange(made)
    grad_parts, output_near, output_far = tie(grad_parts, output_near, output_far)

    bit_cell = (lax.axis_index("dp") & 1).astype(jnp.int32).reshape(1, 1)
    weights = (qw, kw, vw)
    dp_steps = steps_of(sources)
    back = functools.partial(
        attend_back, lens=item_lengths, rank=rank_cell, bit=bit_cell, qt=qt, kt=kt, vt=vt,
        logs=logs, weights=weights, normed=normed_in, outs=own_heads,
    )
    groups = ((0, heads - 1), (heads - 1, 1))
    joint_a, sums_a, own_a, away_a = back(*groups[0], extras=(), grads=grad_parts)
    output_got = swap(output_far, "tensor", 2)
    joint_a, own_a, away_a, output_got, grad_parts, expert_rest, returned = tie(
        joint_a, own_a, away_a, output_got, grad_parts, expert_far[1], returned
    )
    expert_got = swap(expert_rest, "tensor", 2)
    output_sum = add_low(output_near, output_got)
    own_a = add_low(own_a, swap(away_a, "dp", 1))
    output_sum = add_low(output_sum, swap(output_sum, "dp", dp_steps[-1]))
    joint_b, unused, own_b, away_b = back(
        *groups[1], extras=(sums_a, sums_second), grads=grad_parts
    )
    joint_b, own_a, own_b, away_b, output_sum = tie(
        joint_b, own_a, own_b, away_b, output_sum
    )

    far_kept, far_sent = input_grad(
        groups, weights, (joint_a, joint_b), far, members - far, shard_rows
    )
    got_a = swap(own_a, "dp", dp_steps[1])
    got_b = swap(away_b, "dp", 1)
    joint_b, got_a, got_b = tie(joint_b, got_a, got_b)
    near_kept, near_sent = input_grad(
        groups, weights, (joint_a, joint_b), 0, far, shard_rows
    )
    own_b = add_parts(own_b, got_b)
    far_kept = add_low(far_kept, swap(far_sent, "tensor", 1))
    own_a = add_low(own_a, got_a)
    far_kept, own_b, output_sum, own_a = tie(far_kept, own_b, output_sum, own_a)
    near_core = swap(near_sent, "tensor", 1)
    near_far = swap(far_kept, "tensor", 2)
    for step in dp_steps[1:]:
        if step != dp_steps[1]:
            own_a = add_low(own_a, swap(own_a, "dp", step))
        own_b = add_parts(own_b, swap(own_b, "dp", step))
        if step == dp_steps[1]:
            own_b, expert_got = tie(own_b, expert_got)
    up_grad, down_grad = expert_sums(
        expert_up_near, expert_down_near, output_got, expert_got
    )
    own_b, up_grad, down_grad, near_far = tie(own_b, up_grad, down_grad, near_far)
    pieces = (own_a, swap(own_a, "dp", 1), own_b, swap(own_b, "dp", 1))
    token_grad, block_out = close(
        rank_cell[0], tokens, first_gain, grad_res, residual, dispatch, returned,
        (near_kept, near_core, near_far),
    )
    norm_sums = own_b[-SUM_ROWS:].astype(f32)
    norm_sums = norm_sums[: SUM_ROWS // 2] + norm_sums[SUM_ROWS // 2 :]
    for step in steps:
        norm_sums = norm_sums + swap(norm_sums, "tensor", step)
    for step in dp_steps[:-1]:
        output_sum = add_low(output_sum, swap(output_sum, "dp", step))
    query_grad, key_grad, value_grad = finish(groups, bit_cell, pieces)
    return (
        block_out,
        token_grad,
        (norm_sums[0] - first_bias * norm_sums[1]) / first_gain,
        norm_sums[1],
        query_grad.T,
        key_grad.T,
        value_grad.T,
        output_sum.astype(f32),
        norm_sums[2],
        norm_sums[3],
        up_grad[None],
        down_grad[None],
    )


def solution(mesh):
    in_specs = (
        P("dp", None),
        P(),
        P(),
        P(None, "tensor"),
        P(None, "tensor"),
        P(None, "tensor"),
        P("tensor", None),
        P(),
        P(),
        P("dp", None, None),
        P("dp", None, None),
        P("dp", None),
        P(("dp", "tensor"), None),
        P(("dp", "tensor"), None),
        P(("dp", "tensor"), None),
    )
    out_specs = (
        P(("dp", "tensor"), None),
        P(("dp", "tensor"), None),
        P(),
        P(),
        P(None, "tensor"),
        P(None, "tensor"),
        P(None, "tensor"),
        P("tensor", None),
        P(),
        P(),
        P("dp", None, "tensor"),
        P("dp", "tensor", None),
    )
    return jax.shard_map(
        on_device, mesh=mesh, in_specs=in_specs, out_specs=out_specs, check_vma=False
    )
```

```python
import functools

import jax
import jax.numpy as jnp
from jax import lax
from jax.experimental import pallas as pl
from jax.experimental.pallas import tpu as pltpu
from jax.sharding import PartitionSpec as P

HEAD_DIM = 64
EPSILON = 1e-05
NEGATIVE = -1e30
f32 = jnp.float32
bf16 = jnp.bfloat16
VMEM = pl.BlockSpec(memory_space=pltpu.VMEM)
HBM = pl.BlockSpec(memory_space=pltpu.MemorySpace.HBM)
SMEM = pl.BlockSpec(memory_space=pltpu.SMEM)
SUM_ROWS = 16
COST = pl.CostEstimate(flops=2**20, bytes_accessed=2**20, transcendentals=0)
LONG = pl.CostEstimate(flops=2**34, bytes_accessed=2**24, transcendentals=0)


def layer_norm(values, gain, shift):
    average = jnp.mean(values, axis=-1, keepdims=True)
    centred = values - average
    variance = jnp.mean(centred * centred, axis=-1, keepdims=True)
    return centred * lax.rsqrt(variance + EPSILON) * gain + shift


def contract_rows(left, right):
    return lax.dot_general(
        left, right, (((0,), (0,)), ((), ())), preferred_element_type=f32
    )


def swap(values, axis, step):
    count = lax.axis_size(axis)
    return lax.ppermute(values, axis, [(i, i ^ step) for i in range(count)])


def steps_of(count):
    steps = []
    step = 1
    while step < count:
        steps.append(step)
        step *= 2
    return steps


def normalized(values):
    average = jnp.mean(values, axis=-1, keepdims=True)
    centred = values - average
    variance = jnp.mean(centred * centred, axis=-1, keepdims=True)
    return centred * lax.rsqrt(variance + EPSILON)


def project_kernel(
    rank_ref, tokens_ref, gain_ref, bias_ref, qw_ref, kw_ref, vw_ref,
    normed_ref, qt_ref, kt_ref, vt_ref,
):
    values = tokens_ref[...].astype(f32)
    normed = (normalized(values) * gain_ref[...][None] + bias_ref[...][None]).astype(bf16)
    normed_ref[...] = normed
    for weight_ref, out_ref, factor in (
        (qw_ref, qt_ref, HEAD_DIM ** (-0.5)), (kw_ref, kt_ref, None), (vw_ref, vt_ref, None)
    ):
        made = lax.dot_general(
            weight_ref[...], normed, (((1,), (1,)), ((), ())), preferred_element_type=f32
        ).astype(bf16)
        if factor is not None:
            made = made * jnp.asarray(factor, bf16)
        out_ref[...] = made


def project(rank, tokens, gain, bias, qw, kw, vw, blocks):
    slots, width = tokens.shape
    cols = qw.shape[0]
    size = slots // blocks
    fixed = lambda i, r: (0, 0)
    line = pl.BlockSpec((width,), lambda i, r: (0,))
    return pl.pallas_call(
        project_kernel,
        grid_spec=pltpu.PrefetchScalarGridSpec(
            num_scalar_prefetch=1,
            grid=(blocks,),
            in_specs=[
                pl.BlockSpec((size, width), lambda i, r: (i ^ r[0], 0)),
                line,
                line,
                pl.BlockSpec((cols, width), fixed),
                pl.BlockSpec((cols, width), fixed),
                pl.BlockSpec((cols, width), fixed),
            ],
            out_specs=(
                pl.BlockSpec((size, width), lambda i, r: (i, 0)),
                pl.BlockSpec((cols, size), lambda i, r: (0, i)),
                pl.BlockSpec((cols, size), lambda i, r: (0, i)),
                pl.BlockSpec((cols, size), lambda i, r: (0, i)),
            ),
        ),
        out_shape=(jax.ShapeDtypeStruct((slots, width), bf16),)
        + (jax.ShapeDtypeStruct((cols, slots), bf16),) * 3,
        name="project",
        cost_estimate=COST,
    )(rank, tokens, gain, bias, qw, kw, vw)


def item_ends(lens_ref):
    ends = []
    total = jnp.int32(0)
    for i in range(lens_ref.shape[1]):
        total = total + lens_ref[0, i]
        ends.append(total)
    return ends


def segments_at(place, ends):
    segment = jnp.zeros_like(place)
    for end in ends:
        segment = segment + (place >= end).astype(jnp.int32)
    return segment


def block_span(first, size, unit, ends):
    last = jnp.minimum(first + size, ends[-1]) - 1
    low = jnp.int32(0)
    high = ends[-1]
    for end in ends:
        low = jnp.where(first >= end, end, low)
    for end in reversed(ends):
        high = jnp.where(last < end, end, high)
    empty = first >= ends[-1]
    low_block = jnp.where(empty, 0, low // unit)
    high_block = jnp.where(empty, 0, (high + unit - 1) // unit)
    return low_block, high_block


def rows_at(block, size):
    return pl.ds(pl.multiple_of(block * size, size), size)


def fill_segments(row_ref, col_ref, shard, rank, ends):
    slots = row_ref.shape[1]
    at = lax.broadcasted_iota(jnp.int32, (1, slots), 1)
    place = ((at // shard) ^ rank) * shard + at % shard
    segments = segments_at(place, ends)
    row_ref[...] = segments
    col_ref[...] = jnp.transpose(jnp.broadcast_to(segments, (128, slots)), (1, 0))


def block_bias(row_ref, col_ref, rows, cols):
    return jnp.where(col_ref[rows, 0:1] == row_ref[:, cols], 0.0, NEGATIVE)


def lane_masked(values, head):
    lane = lax.broadcasted_iota(jnp.int32, values.shape, 1)
    inside = (lane >= head * HEAD_DIM) & (lane < (head + 1) * HEAD_DIM)
    return jnp.where(inside, values, jnp.zeros_like(values))


def forward_kernel(
    first, blocks, lens_ref, rank_ref, qt_ref, kt_ref, vt_ref, *refs
):
    *out_refs, log_ref, masked_ref, out_ref, row_ref, col_ref, score_ref = refs
    count, width, size = out_ref.shape
    heads = width // HEAD_DIM
    shard = size
    rank = rank_ref[0, 0]
    ends = item_ends(lens_ref)
    fill_segments(row_ref, col_ref, shard, rank, ends)
    keys = jnp.transpose(kt_ref[...], (1, 0))
    for h in range(heads):
        masked_ref[h] = lane_masked(keys, h)

    def query_block(b, unused):
        at = first + b
        i = at ^ rank
        cols = rows_at(at, size)
        queries = qt_ref[:, cols]

        def score_block(j, carry):
            rows = rows_at(j ^ rank, shard)
            bias = block_bias(row_ref, col_ref, rows, cols)
            result = []
            for h in range(heads):
                scores = jnp.dot(
                    masked_ref[h, rows, :], queries, preferred_element_type=f32
                )
                scores = scores + bias
                score_ref[h, rows_at(j, shard), :] = scores
                part = jnp.max(scores.reshape(-1, 8, size), axis=0)
                result.append(jnp.maximum(carry[h], part))
            return tuple(result)

        low, high = block_span(i * size, size, shard, ends)
        peaks = lax.fori_loop(
            low, high, score_block, (jnp.full((8, size), NEGATIVE, f32),) * heads
        )
        peaks = [jnp.max(peak, axis=0, keepdims=True) for peak in peaks]

        def key_block(j, carry):
            rows = rows_at(j ^ rank, shard)
            result = []
            for h in range(heads):
                summed, total = carry[h]
                soft = jnp.exp(score_ref[h, rows_at(j, shard), :] - peaks[h])
                summed = summed + jnp.sum(soft.reshape(-1, 8, size), axis=0)
                total = total + jnp.dot(
                    vt_ref[pl.ds(h * HEAD_DIM, HEAD_DIM), rows],
                    soft.astype(bf16),
                    preferred_element_type=f32,
                )
                result.append((summed, total))
            return tuple(result)

        start = ((jnp.zeros((8, size), f32), jnp.zeros((HEAD_DIM, size), f32)),) * heads
        done = lax.fori_loop(low, high, key_block, start)
        live = row_ref[:, cols] < len(ends)
        for h in range(heads):
            summed, total = done[h]
            summed = jnp.sum(summed, axis=0, keepdims=True)
            highest = peaks[h]
            summed = jnp.where(live, summed, 1.0)
            result = jnp.where(live, total / summed, 0.0).astype(bf16)
            logs = jnp.where(live, highest + jnp.log(summed), -NEGATIVE)
            out_ref[b, pl.ds(h * HEAD_DIM, HEAD_DIM), :] = result
            log_ref[h, :, rows_at(b, size)] = logs
        return unused

    lax.fori_loop(0, count, query_block, 0)
    for b in range(count):
        out_refs[b][...] = out_ref[b]


def attend(lens, rank, qt, kt, vt, blocks, first, count):
    width, slots = qt.shape
    size = slots // blocks
    heads = width // HEAD_DIM
    return pl.pallas_call(
        functools.partial(forward_kernel, first, blocks),
        out_shape=(jax.ShapeDtypeStruct((width, size), bf16),) * count
        + (jax.ShapeDtypeStruct((heads, 1, count * size), f32),),
        in_specs=[SMEM, SMEM, VMEM, VMEM, VMEM],
        out_specs=(VMEM,) * (count + 1),
        scratch_shapes=[
            pltpu.VMEM((heads, slots, width), bf16),
            pltpu.VMEM((count, width, size), bf16),
            pltpu.VMEM((1, slots), jnp.int32),
            pltpu.VMEM((slots, 128), jnp.int32),
            pltpu.VMEM((heads, slots, size), f32),
        ],
        name="attend",
        compiler_params=pltpu.CompilerParams(vmem_limit_bytes=60 * 2**20),
        cost_estimate=COST,
    )(lens, rank, qt, kt, vt)


def split_rows(values):
    high = values.astype(bf16)
    return jnp.concatenate([high, (values - high.astype(f32)).astype(bf16)], axis=0)


def add_kernel(a_ref, b_ref, out_ref):
    half = out_ref.shape[0] - SUM_ROWS
    line = SUM_ROWS // 2
    total = a_ref[...].astype(f32) + b_ref[...].astype(f32)
    out_ref[:half, :] = total[:half].astype(bf16)
    out_ref[half:, :] = split_rows(total[half : half + line] + total[half + line :])


def add_parts(a, b):
    return pl.pallas_call(
        add_kernel,
        out_shape=jax.ShapeDtypeStruct(a.shape, bf16),
        in_specs=[VMEM, VMEM],
        out_specs=VMEM,
        name="add_parts",
        compiler_params=pltpu.CompilerParams(vmem_limit_bytes=5 * 2**20),
        cost_estimate=COST,
    )(a, b)


def stacked_parts(first_head, heads, query, key, value):
    dim = HEAD_DIM
    parts = []
    for n in range(heads):
        first = (first_head + n) * dim
        parts += [(2 * n * dim, key, first, dim), ((2 * n + 1) * dim, value, first, dim)]
    return parts + [(2 * heads * dim, query, first_head * dim, heads * dim)]


def backward_kernel(
    first_head, heads, blocks, extras, lens_ref, rank_ref, bit_ref, qt_ref, kt_ref, vt_ref,
    near_ref, far_ref, qw_ref, kw_ref, vw_ref, normed_ref, *rest
):
    extra_refs, rest = rest[:extras], rest[extras:]
    width, slots = qt_ref.shape
    shard = slots // blocks
    dim = HEAD_DIM
    out_refs, grad_refs = rest[:blocks], rest[blocks : 2 * blocks]
    joint_ref, sums_ref, own_ref, away_ref = rest[2 * blocks : 2 * blocks + 4]
    kv_ref, q0_ref, og_ref, right_ref, inner_ref, dq_ref, made_ref = rest[-13:-6]
    log_ref = rest[-6]
    row_ref, col_ref = rest[-5:-3]
    turned_ref, rows_ref, copied = rest[-3:]
    fetch = pltpu.make_async_copy(normed_ref, rows_ref, copied)
    fetch.start()
    unit = shard // 2
    rank = rank_ref[0, 0]
    ends = item_ends(lens_ref)
    fill_segments(row_ref, col_ref, shard, rank, ends)
    near = near_ref.shape[2]
    log_ref[:, :, :near] = near_ref[...]
    log_ref[:, :, near:] = far_ref[...]
    zero = jnp.zeros((dim, slots), bf16)
    for n in range(heads):
        part = slice((first_head + n) * dim, (first_head + n + 1) * dim)
        both = jnp.concatenate([kt_ref[part, :], vt_ref[part, :]], axis=0)
        kv_ref[n] = jnp.transpose(both, (1, 0))
        padded = jnp.concatenate([qt_ref[part, :], zero], axis=0)
        q0_ref[n] = jnp.transpose(padded, (1, 0))
        right_ref[n, 0] = padded
        for b in range(blocks):
            grad = grad_refs[b][part, :]
            cols = slice(b * shard, (b + 1) * shard)
            padded = jnp.concatenate([zero[:, :shard], grad], axis=0)
            og_ref[n, cols, :] = jnp.transpose(padded, (1, 0))
            right_ref[n, 1, :, cols] = padded
            inner_ref[n, :, cols] = jnp.sum(
                out_refs[b][part, :].astype(f32) * grad.astype(f32), axis=0, keepdims=True
            )
    dq_ref[...] = jnp.zeros_like(dq_ref)

    def key_block(j, unused):
        at_key = ((j // 2) ^ rank) * 2 + j % 2
        rows = rows_at(at_key, unit)

        def query_block(i, totals):
            at = i ^ rank
            cols = rows_at(at, shard)
            same = col_ref[rows, 0:1] == row_ref[:, cols]
            result = []
            for n in range(heads):
                head = first_head + n
                kv = kv_ref[n, rows, :]
                scores = jnp.dot(kv, right_ref[n, 0, :, cols], preferred_element_type=f32)
                grad_soft = jnp.dot(kv, right_ref[n, 1, :, cols], preferred_element_type=f32)
                soft = jnp.where(same, jnp.exp(scores - log_ref[head, :, cols]), 0.0)
                grad_scores = (soft * (grad_soft - inner_ref[n, :, cols])).astype(bf16)
                total = totals[n] + jnp.dot(
                    soft.astype(bf16), og_ref[n, cols, :], preferred_element_type=f32
                )
                total = total + jnp.dot(
                    grad_scores, q0_ref[n, cols, :], preferred_element_type=f32
                )
                dq_ref[n, :, cols] += jnp.dot(
                    kt_ref[pl.ds(head * dim, dim), rows], grad_scores,
                    preferred_element_type=f32,
                )
                result.append(total)
            return tuple(result)

        low, high = block_span(j * unit, unit, shard, ends)
        start = (jnp.zeros((unit, 2 * dim), f32),) * heads
        totals = lax.fori_loop(low, high, query_block, start)
        for n in range(heads):
            part = slice(2 * dim * n, 2 * dim * (n + 1))
            total = totals[n].astype(bf16)
            joint_ref[rows, part] = total
            turned_ref[part, rows] = jnp.transpose(total, (1, 0))
        return unused

    lax.fori_loop(0, 2 * blocks, key_block, 0)
    dq = (dq_ref[...] * dim ** (-0.5)).astype(bf16).reshape(heads * dim, slots)
    turned_ref[2 * dim * heads :, :] = dq
    joint_ref[:, 2 * dim * heads :] = jnp.transpose(dq, (1, 0))
    fetch.wait()
    made_ref[...] = jnp.dot(turned_ref[...], rows_ref[...], preferred_element_type=f32)
    gains = jnp.zeros((1, rows_ref.shape[1]), f32)
    shifts = jnp.zeros((1, rows_ref.shape[1]), f32)
    for at, weight_ref, first, size in stacked_parts(
        first_head, heads, qw_ref, kw_ref, vw_ref
    ):
        weight = weight_ref[first : first + size, :].astype(f32)
        gains += jnp.sum(weight * made_ref[at : at + size, :], axis=0, keepdims=True)
        total = jnp.sum(turned_ref[at : at + size, :].astype(f32), axis=1, keepdims=True)
        shifts += jnp.sum(weight * total, axis=0, keepdims=True)
    sums_ref[0:1] = gains
    sums_ref[1:2] = shifts
    half = made_ref.shape[0] // 2
    bit = bit_ref[0, 0]
    for part_ref, at in ((own_ref, bit), (away_ref, 1 - bit)):
        part_ref[0:half, :] = made_ref[rows_at(at, half), :].astype(bf16)
        if extras:
            lines = [sums_ref[...] + extra_refs[0][...], extra_refs[1][...]]
            lines.append(jnp.zeros((SUM_ROWS // 2 - 4, gains.shape[1]), f32))
            part_ref[half:, :] = split_rows(jnp.concatenate(lines, axis=0))


def attend_back(
    first_head, heads, extras, lens, rank, bit, qt, kt, vt, logs, weights, normed, outs, grads
):
    slots, width = normed.shape
    blocks = len(outs)
    dim = HEAD_DIM
    cols = 3 * dim * heads
    rows = cols // 2 + (SUM_ROWS if extras else 0)
    return pl.pallas_call(
        functools.partial(backward_kernel, first_head, heads, blocks, len(extras)),
        out_shape=(
            jax.ShapeDtypeStruct((slots, cols), bf16),
            jax.ShapeDtypeStruct((2, width), f32),
        )
        + (jax.ShapeDtypeStruct((rows, width), bf16),) * 2,
        in_specs=[SMEM, SMEM, SMEM]
        + [VMEM] * 8
        + [pl.BlockSpec(memory_space=pl.ANY)]
        + [VMEM] * (len(extras) + 2 * blocks),
        out_specs=(VMEM,) * 4,
        scratch_shapes=[pltpu.VMEM((heads, slots, 2 * dim), bf16)] * 3
        + [
            pltpu.VMEM((heads, 2, 2 * dim, slots), bf16),
            pltpu.VMEM((heads, 1, slots), f32),
            pltpu.VMEM((heads, dim, slots), f32),
            pltpu.VMEM((cols, width), f32),
            pltpu.VMEM((qt.shape[0] // dim, 1, slots), f32),
            pltpu.VMEM((1, slots), jnp.int32),
            pltpu.VMEM((slots, 128), jnp.int32),
            pltpu.VMEM((cols, slots), bf16),
            pltpu.VMEM((slots, width), bf16),
            pltpu.SemaphoreType.DMA,
        ],
        name="attend_back",
        compiler_params=pltpu.CompilerParams(vmem_limit_bytes=60 * 2**20),
        cost_estimate=COST,
    )(lens, rank, bit, qt, kt, vt, *logs, *weights, normed, *extras, *outs, *grads)


def plan_kernel(capacity, lens_ref, rank_ref, routes_ref, order_ref, grad_ref,
                dispatch_ref, slots_ref):
    shard = routes_ref.shape[1]
    first = rank_ref[0, 0] * shard
    ends = item_ends(lens_ref)
    chosen_row = routes_ref[...]
    chosen_col = jnp.transpose(jnp.broadcast_to(chosen_row, (128, shard)), (1, 0))[:, 0:1]
    order_row = order_ref[...]
    order_col = jnp.transpose(jnp.broadcast_to(order_row, (128, shard)), (1, 0))[:, 0:1]
    alive_row = segments_at(
        first + lax.broadcasted_iota(jnp.int32, (1, shard), 1), ends
    ) < len(ends)
    alive_col = segments_at(
        first + lax.broadcasted_iota(jnp.int32, (shard, 1), 0), ends
    ) < len(ends)
    ahead = (chosen_col == chosen_row) & (order_col < order_row) & alive_col
    ranked = jnp.sum(ahead.astype(jnp.int32), axis=0, keepdims=True)
    kept = alive_row & (ranked < capacity)
    slot = jnp.where(kept, chosen_row * capacity + ranked, -1)
    dispatch = (
        lax.broadcasted_iota(jnp.int32, dispatch_ref.shape, 0) == slot
    ).astype(f32).astype(bf16)
    dispatch_ref[...] = dispatch
    slots_ref[...] = jnp.dot(
        dispatch, grad_ref[...], preferred_element_type=f32
    ).astype(bf16)


def plan(lens, rank, routes, order, grads, capacity, experts_all):
    shard, width = grads.shape
    count = experts_all * capacity
    return pl.pallas_call(
        functools.partial(plan_kernel, capacity),
        out_shape=(
            jax.ShapeDtypeStruct((count, shard), bf16),
            jax.ShapeDtypeStruct((count, width), bf16),
        ),
        in_specs=[SMEM, SMEM, VMEM, VMEM, VMEM],
        out_specs=(VMEM, VMEM),
        name="plan",
        cost_estimate=COST,
    )(lens, rank, routes.reshape(1, -1), order, grads)


def across(left, right):
    return lax.dot_general(
        left, right, (((1,), (1,)), ((), ())), preferred_element_type=f32
    )


def middle_kernel(count, rank_ref, tokens_ref, gain_ref, bias_ref, dispatch_ref, *refs):
    head_refs, weight_refs = refs[:count], refs[count : 2 * count]
    residual_ref, rows_ref = refs[2 * count :]
    residual = tokens_ref[...].astype(f32)
    for head_ref, weight_ref in zip(head_refs, weight_refs):
        residual = residual + contract_rows(head_ref[...], weight_ref[...])
    residual_ref[...] = residual
    normed = (normalized(residual) * gain_ref[...][None] + bias_ref[...][None]).astype(bf16)
    rows_ref[...] = jnp.dot(
        dispatch_ref[...], normed, preferred_element_type=f32
    ).astype(bf16)


def middle(rank, tokens, gain, bias, dispatch, heads, weights):
    count, shard = dispatch.shape
    width = tokens.shape[1]
    fixed = lambda array: pl.BlockSpec(array.shape, lambda i, r: (0,) * array.ndim)
    small = [gain, bias, dispatch, *heads, *weights]
    return pl.pallas_call(
        functools.partial(middle_kernel, len(heads)),
        grid_spec=pltpu.PrefetchScalarGridSpec(
            num_scalar_prefetch=1,
            grid=(1,),
            in_specs=[pl.BlockSpec((shard, width), lambda i, r: (r[0], 0))]
            + [fixed(array) for array in small],
            out_specs=(
                pl.BlockSpec((shard, width), lambda i, r: (0, 0)),
                pl.BlockSpec((count, width), lambda i, r: (0, 0)),
            ),
        ),
        out_shape=(
            jax.ShapeDtypeStruct((shard, width), f32),
            jax.ShapeDtypeStruct((count, width), bf16),
        ),
        name="middle",
        cost_estimate=COST,
    )(rank, tokens, *small)


def turn_kernel(
    count, lens_ref, rank_ref, dispatch_ref, back_ref, residual_ref, cotangent_ref,
    gain_ref, *refs
):
    head_refs, weight_refs = refs[:count], refs[count : 2 * count]
    grad_ref, sums_ref, kept_ref, sent_ref = refs[2 * count : 2 * count + 4]
    part_refs = refs[2 * count + 4 :]
    shard = residual_ref.shape[0]
    grad_normed = contract_rows(dispatch_ref[...], back_ref[...])
    values = residual_ref[...]
    centred = values - jnp.mean(values, axis=-1, keepdims=True)
    inverse = lax.rsqrt(jnp.mean(centred * centred, axis=-1, keepdims=True) + EPSILON)
    normed = centred * inverse
    sums_ref[0:1] = jnp.sum(grad_normed * normed, axis=0, keepdims=True)
    sums_ref[1:2] = jnp.sum(grad_normed, axis=0, keepdims=True)
    scaled = grad_normed * gain_ref[...][None]
    grad = cotangent_ref[...].astype(f32) + inverse * (
        scaled
        - jnp.mean(scaled, axis=-1, keepdims=True)
        - normed * jnp.mean(scaled * normed, axis=-1, keepdims=True)
    )
    grad_ref[...] = grad
    low = grad.astype(bf16)
    place = rank_ref[0, 0] * shard + lax.broadcasted_iota(jnp.int32, (1, shard), 1)
    alive = place < item_ends(lens_ref)[-1]
    for weight_ref, part_ref in zip(weight_refs, part_refs):
        part_ref[...] = jnp.where(alive, across(weight_ref[...], low), 0.0).astype(bf16)
    for j, head_ref in enumerate(head_refs):
        made = jnp.dot(head_ref[...], low, preferred_element_type=f32)
        (kept_ref, sent_ref)[j % 2][j // 2] = made.astype(bf16)


def turn(lens, rank, dispatch, back, residual, cotangent, gain, heads, weights):
    shard, width = residual.shape
    cols = weights[0].shape[0]
    count = len(weights)
    return pl.pallas_call(
        functools.partial(turn_kernel, count),
        out_shape=(
            jax.ShapeDtypeStruct((shard, width), f32),
            jax.ShapeDtypeStruct((2, width), f32),
            jax.ShapeDtypeStruct((count // 2, cols, width), bf16),
            jax.ShapeDtypeStruct((count // 2, cols, width), bf16),
        )
        + (jax.ShapeDtypeStruct((cols, shard), bf16),) * count,
        in_specs=[SMEM, SMEM] + [VMEM] * (5 + 2 * count),
        out_specs=(VMEM,) * (4 + count),
        name="turn",
        cost_estimate=COST,
    )(lens, rank, dispatch, back, residual, cotangent, gain, *heads, *weights)


def output_sum_kernel(kept_ref, core_ref, first_ref, near_ref, far_ref):
    cols = near_ref.shape[0]
    total = [
        (kept_ref[j].astype(f32) + core_ref[j].astype(f32)).astype(bf16) for j in range(2)
    ]
    near_ref[...] = total[0]
    far_ref[:cols, :] = total[1]
    far_ref[cols:, :] = first_ref[...]


def output_sums(kept, core, first):
    slots, cols, width = kept.shape
    return pl.pallas_call(
        output_sum_kernel,
        out_shape=(
            jax.ShapeDtypeStruct((cols, width), bf16),
            jax.ShapeDtypeStruct((cols + first.shape[0], width), bf16),
        ),
        in_specs=[VMEM] * 3,
        out_specs=(VMEM, VMEM),
        name="output_sums",
        compiler_params=pltpu.CompilerParams(vmem_limit_bytes=52 * 2**20),
        cost_estimate=LONG,
    )(kept, core, first)


def gelu_parts(values):
    below = 0.5 + 0.5 * lax.erf(values * (0.5**0.5))
    density = jnp.exp(-0.5 * values * values) * (0.5 / jnp.pi) ** 0.5
    return values * below, below + values * density


def part_at(step, parts, rank):
    half = parts // 2
    return (2 * (step % half) + step // half) ^ rank


def activation_kernel(grad_ref, down_ref, out_ref):
    out_ref[...] = across(grad_ref[...], down_ref[...]).astype(bf16)


def activation_grads(grads, down, parts):
    count, width = grads.shape
    hidden = down.shape[0]
    size = hidden // parts
    return pl.pallas_call(
        activation_kernel,
        grid=(parts,),
        out_shape=jax.ShapeDtypeStruct((count, hidden), bf16),
        in_specs=[
            pl.BlockSpec((count, width), lambda i: (0, 0)),
            pl.BlockSpec((size, width), lambda i: (i, 0)),
        ],
        out_specs=pl.BlockSpec((count, size), lambda i: (0, i)),
        name="activation_grads",
        cost_estimate=COST,
    )(grads, down)


def expert_kernel(
    parts, rank_ref, in_ref, grad_act_ref, up_ref,
    act_kept_ref, pre_kept_ref, act_sent_ref, pre_sent_ref, mid_ref,
    grads_ref, ups_ref, acts_ref, pres_ref, sum_ref, fetched, stored,
):
    rank = rank_ref[0, 0]
    size = ups_ref.shape[2]
    half = parts // 2

    def fetch(p):
        cols = rows_at(part_at(p, parts, rank), size)
        return (
            pltpu.make_async_copy(up_ref.at[:, cols], ups_ref.at[p], fetched.at[0, p]),
            pltpu.make_async_copy(grad_act_ref.at[:, cols], grads_ref.at[p], fetched.at[1, p]),
        )

    def store(p, act_out_ref, pre_out_ref):
        cols = rows_at(p % half, size)
        return (
            pltpu.make_async_copy(acts_ref.at[p], act_out_ref.at[:, cols], stored.at[0, p]),
            pltpu.make_async_copy(pres_ref.at[p], pre_out_ref.at[:, cols], stored.at[1, p]),
        )

    for p in range(parts):
        for copy in fetch(p):
            copy.start()
    sum_ref[...] = jnp.zeros_like(sum_ref)

    def part(p, unused):
        for copy in fetch(p):
            copy.wait()
        pre = jnp.dot(in_ref[...], ups_ref[p], preferred_element_type=f32)
        act, slope = gelu_parts(pre)
        acts_ref[p] = act.astype(bf16)
        grad_pre = (grads_ref[p].astype(f32) * slope).astype(bf16)
        pres_ref[p] = grad_pre
        sum_ref[...] += across(grad_pre, ups_ref[p])

        @pl.when(p < half)
        def keep():
            for copy in store(p, act_kept_ref, pre_kept_ref):
                copy.start()

        @pl.when(p >= half)
        def send():
            for copy in store(p, act_sent_ref, pre_sent_ref):
                copy.start()

        return unused

    lax.fori_loop(0, parts, part, 0)
    mid_ref[...] = sum_ref[...].astype(bf16)
    for p in range(parts):
        outs = (act_kept_ref, pre_kept_ref) if p < half else (act_sent_ref, pre_sent_ref)
        for copy in store(p, *outs):
            copy.wait()


def expert(rank, rows, grad_act, up, parts):
    count, width = rows.shape
    hidden = up.shape[1]
    size = hidden // parts
    return pl.pallas_call(
        functools.partial(expert_kernel, parts),
        out_shape=(jax.ShapeDtypeStruct((count, hidden // 2), bf16),) * 4
        + (jax.ShapeDtypeStruct((count, width), bf16),),
        in_specs=[SMEM, VMEM, HBM, HBM],
        out_specs=(HBM,) * 4 + (VMEM,),
        scratch_shapes=[
            pltpu.VMEM((parts, count, size), grad_act.dtype),
            pltpu.VMEM((parts, width, size), bf16),
            pltpu.VMEM((parts, count, size), bf16),
            pltpu.VMEM((parts, count, size), bf16),
            pltpu.VMEM((count, width), f32),
            pltpu.SemaphoreType.DMA((2, parts)),
            pltpu.SemaphoreType.DMA((2, parts)),
        ],
        name="expert",
        compiler_params=pltpu.CompilerParams(vmem_limit_bytes=52 * 2**20),
        cost_estimate=COST,
    )(rank.reshape(1, 1), rows, grad_act, up)


def product_kernel(parts, rank_ref, kept_ref, sent_ref, down_ref, out_ref,
                   acts_ref, downs_ref, sum_ref, fetched):
    rank = rank_ref[0, 0]
    size = downs_ref.shape[1]
    half = parts // 2

    def fetch(p):
        rows = rows_at(part_at(p, parts, rank), size)
        source = kept_ref if p < half else sent_ref
        cols = slice((p % half) * size, (p % half + 1) * size)
        return (
            pltpu.make_async_copy(down_ref.at[rows, :], downs_ref.at[p], fetched.at[0, p]),
            pltpu.make_async_copy(source.at[:, cols], acts_ref.at[p], fetched.at[1, p]),
        )

    for p in range(parts):
        for copy in fetch(p):
            copy.start()
    sum_ref[...] = jnp.zeros_like(sum_ref)
    for p in range(parts):
        for copy in fetch(p):
            copy.wait()
        sum_ref[...] += jnp.dot(acts_ref[p], downs_ref[p], preferred_element_type=f32)
    out_ref[...] = sum_ref[...].astype(bf16)


def product(rank, kept, sent, down, parts):
    count = kept.shape[0]
    hidden, width = down.shape
    size = hidden // parts
    return pl.pallas_call(
        functools.partial(product_kernel, parts),
        out_shape=jax.ShapeDtypeStruct((count, width), bf16),
        in_specs=[SMEM, HBM, HBM, HBM],
        out_specs=VMEM,
        scratch_shapes=[
            pltpu.VMEM((parts, count, size), bf16),
            pltpu.VMEM((parts, size, width), bf16),
            pltpu.VMEM((count, width), f32),
            pltpu.SemaphoreType.DMA((2, parts)),
        ],
        name="product",
        cost_estimate=COST,
    )(rank.reshape(1, 1), kept, sent, down)


def group_sums(refs, groups):
    dup = ddown = 0.0
    for g in range(groups):
        in_ref, grad_ref, act_ref, pre_ref = refs[4 * g : 4 * g + 4]
        dup = dup + contract_rows(in_ref[...], pre_ref[...])
        ddown = ddown + contract_rows(act_ref[...], grad_ref[...])
    return dup, ddown


def group_specs(groups, part):
    count, width = groups[0][0].shape
    size = groups[0][2].shape[1] // 2
    fixed = pl.BlockSpec((count, width), lambda i: (0, 0))
    columns = pl.BlockSpec((count, size), lambda i: (0, part))
    return [fixed, fixed, columns, columns] * len(groups)


def far_weight_kernel(groups, *refs):
    first_ref, rest_ref = refs[-2:]
    dup, ddown = group_sums(refs, groups)
    cut = first_ref.shape[0]
    first_ref[...] = dup[:cut].astype(bf16)
    rest_ref[: dup.shape[0] - cut, :] = dup[cut:].astype(bf16)
    rest_ref[dup.shape[0] - cut :, :] = ddown.astype(bf16)


def far_weights(groups):
    width = groups[0][0].shape[1]
    size = groups[0][2].shape[1] // 2
    cut = (width + size) // 4
    shapes = ((cut, size), (width + size - cut, size))
    return pl.pallas_call(
        functools.partial(far_weight_kernel, len(groups)),
        grid=(1,),
        in_specs=group_specs(groups, 1),
        out_specs=tuple(pl.BlockSpec(shape, lambda i: (0, 0)) for shape in shapes),
        out_shape=tuple(jax.ShapeDtypeStruct(shape, bf16) for shape in shapes),
        name="far_weights",
        cost_estimate=COST,
    )(*[values for group in groups for values in group])


def near_weight_kernel(groups, skip, *refs):
    first_ref, rest_ref, up_ref, down_ref = refs[-4:]
    dup, ddown = group_sums(refs, groups)
    cut = first_ref.shape[0] - skip
    down_at = dup.shape[0] - cut
    up_ref[:cut, :] = dup[:cut] + first_ref[skip:, :].astype(f32)
    up_ref[cut:, :] = dup[cut:] + rest_ref[:down_at, :].astype(f32)
    down_ref[...] = ddown + rest_ref[down_at:, :].astype(f32)


def near_weights(groups, first, rest):
    width = groups[0][0].shape[1]
    size = groups[0][2].shape[1] // 2
    skip = first.shape[0] + rest.shape[0] - width - size
    whole = lambda shape: pl.BlockSpec(shape, lambda i: (0, 0))
    return pl.pallas_call(
        functools.partial(near_weight_kernel, len(groups), skip),
        grid=(1,),
        in_specs=group_specs(groups, 0) + [whole(first.shape), whole(rest.shape)],
        out_specs=(whole((width, size)), whole((size, width))),
        out_shape=(
            jax.ShapeDtypeStruct((width, size), f32),
            jax.ShapeDtypeStruct((size, width), f32),
        ),
        name="near_weights",
        compiler_params=pltpu.CompilerParams(vmem_limit_bytes=52 * 2**20),
        cost_estimate=COST,
    )(*[values for group in groups for values in group], first, rest)


def input_grad_kernel(groups, qw_ref, kw_ref, vw_ref, *refs):
    joint_refs = refs[: len(groups)]
    kept_ref, sent_ref, turned_ref = refs[len(groups) :]
    step = pl.program_id(0)

    @pl.when(step == 0)
    def stack():
        start = 0
        for first_head, heads in groups:
            for at, weight_ref, first, size in stacked_parts(
                first_head, heads, qw_ref, kw_ref, vw_ref
            ):
                turned_ref[start + at : start + at + size, :] = weight_ref[
                    first : first + size, :
                ]
            start += 3 * heads * HEAD_DIM

    total = 0.0
    at = 0
    for joint_ref in joint_refs:
        rows = slice(at, at + joint_ref.shape[1])
        total = total + jnp.dot(
            joint_ref[...], turned_ref[rows, :], preferred_element_type=f32
        )
        at += joint_ref.shape[1]

    @pl.when(step % 2 == 0)
    def keep():
        kept_ref[0] = total.astype(bf16)

    @pl.when(step % 2 == 1)
    def send():
        sent_ref[0] = total.astype(bf16)


def input_grad(groups, weights, joints, first, count, size):
    cols, width = weights[0].shape
    fixed = pl.BlockSpec((cols, width), lambda i: (0, 0))
    return pl.pallas_call(
        functools.partial(input_grad_kernel, groups),
        grid=(count,),
        out_shape=(jax.ShapeDtypeStruct((count // 2, size, width), bf16),) * 2,
        in_specs=[fixed] * 3
        + [
            pl.BlockSpec((size, joint.shape[1]), lambda i: (first + i, 0))
            for joint in joints
        ],
        out_specs=(pl.BlockSpec((1, size, width), lambda i: (i // 2, 0, 0)),) * 2,
        scratch_shapes=[pltpu.VMEM((3 * cols, width), bf16)],
        name="input_grad",
        compiler_params=pltpu.CompilerParams(vmem_limit_bytes=10 * 2**20),
        cost_estimate=COST,
    )(*weights, *joints)


def close_kernel(
    rank_ref, tokens_ref, gain_ref, grad_ref, residual_ref, dispatch_ref, back_ref, *refs
):
    *part_refs, out_ref, block_ref = refs
    block_ref[...] = residual_ref[...] + contract_rows(dispatch_ref[...], back_ref[...])
    grad_in = 0.0
    for part_ref in part_refs:
        grad_in = grad_in + part_ref[...].reshape(out_ref.shape).astype(f32)
    values = tokens_ref[...].astype(f32)
    centred = values - jnp.mean(values, axis=-1, keepdims=True)
    inverse = lax.rsqrt(jnp.mean(centred * centred, axis=-1, keepdims=True) + EPSILON)
    normed = centred * inverse
    scaled = grad_in * gain_ref[...][None]
    out_ref[...] = grad_ref[...] + inverse * (
        scaled
        - jnp.mean(scaled, axis=-1, keepdims=True)
        - normed * jnp.mean(scaled * normed, axis=-1, keepdims=True)
    )


def close(rank, tokens, gain, grad, residual, dispatch, back, parts):
    shard, width = grad.shape
    count = dispatch.shape[0]
    size = shard // 2
    rows = pl.BlockSpec((size, width), lambda i, r: (i, 0))
    return pl.pallas_call(
        close_kernel,
        grid_spec=pltpu.PrefetchScalarGridSpec(
            num_scalar_prefetch=1,
            grid=(2,),
            in_specs=[
                pl.BlockSpec((size, width), lambda i, r: (2 * r[0] + i, 0)),
                pl.BlockSpec((width,), lambda i, r: (0,)),
                rows,
                rows,
                pl.BlockSpec((count, size), lambda i, r: (0, i)),
                pl.BlockSpec((count, width), lambda i, r: (0, 0)),
            ]
            + [pl.BlockSpec((1, size, width), lambda i, r: (0, i, 0))] * len(parts),
            out_specs=(rows, rows),
        ),
        out_shape=(jax.ShapeDtypeStruct((shard, width), f32),) * 2,
        name="close",
        compiler_params=pltpu.CompilerParams(vmem_limit_bytes=16 * 2**20),
        cost_estimate=COST,
    )(rank, tokens, gain, grad, residual, dispatch, back, *parts)


def add_low_kernel(a_ref, b_ref, out_ref):
    out_ref[...] = (a_ref[...].astype(f32) + b_ref[...].astype(f32)).astype(bf16)


def add_low(a, b):
    block = pl.BlockSpec(a.shape, lambda i: (0,) * a.ndim)
    return pl.pallas_call(
        add_low_kernel,
        grid=(1,),
        out_shape=jax.ShapeDtypeStruct(a.shape, bf16),
        in_specs=[block, block],
        out_specs=block,
        name="add_low",
        compiler_params=pltpu.CompilerParams(vmem_limit_bytes=6 * 2**20),
        cost_estimate=COST,
    )(a, b)


def after(value, *others):
    return lax.optimization_barrier((value, *others))[0]


def tie(*values):
    return lax.optimization_barrier(values)


def finish_kernel(groups, bit_ref, *refs):
    pieces, refs = refs[: 2 * len(groups)], refs[2 * len(groups) :]
    query_ref, key_ref, value_ref = refs[:3]
    bit = bit_ref[0, 0]
    for g, ((first_head, heads), whole_ref) in enumerate(zip(groups, refs[3:])):
        half = whole_ref.shape[0] // 2
        for piece_ref, at in ((pieces[2 * g], bit), (pieces[2 * g + 1], 1 - bit)):
            whole_ref[rows_at(at, half), :] = piece_ref[0:half, :].astype(f32)
        for at, target_ref, first, size in stacked_parts(
            first_head, heads, query_ref, key_ref, value_ref
        ):
            target_ref[first : first + size, :] = whole_ref[at : at + size, :]


def finish(groups, bit, pieces):
    width = pieces[0].shape[1]
    cols = sum(heads for first_head, heads in groups) * HEAD_DIM
    return pl.pallas_call(
        functools.partial(finish_kernel, groups),
        out_shape=(jax.ShapeDtypeStruct((cols, width), f32),) * 3,
        in_specs=[SMEM] + [VMEM] * len(pieces),
        out_specs=(VMEM,) * 3,
        scratch_shapes=[
            pltpu.VMEM((3 * heads * HEAD_DIM, width), f32) for first_head, heads in groups
        ],
        name="finish",
        compiler_params=pltpu.CompilerParams(vmem_limit_bytes=10 * 2**20),
        cost_estimate=COST,
    )(bit, *pieces)


def on_device(
    tokens,
    first_gain,
    first_bias,
    query_weight,
    key_weight,
    value_weight,
    output_weight,
    second_gain,
    second_bias,
    expert_up,
    expert_down,
    item_lengths,
    routes,
    slot_order,
    cotangent,
):
    slots_all, width = tokens.shape
    members = lax.axis_size("tensor")
    shard_rows = slots_all // members
    rank = lax.axis_index("tensor")
    sources = lax.axis_size("dp")
    experts_all = sources * expert_up.shape[0]
    capacity = shard_rows // experts_all
    head_cols = query_weight.shape[1]
    heads = head_cols // HEAD_DIM
    up_matrix = expert_up[0]
    down_matrix = expert_down[0]
    rank_cell = rank.astype(jnp.int32).reshape(1, 1)

    def exchange(rows):
        return lax.all_to_all(
            rows.reshape(sources, -1, width), "dp", split_axis=0, concat_axis=0, tiled=True
        ).reshape(-1, width)

    qw, kw, vw = query_weight.T, key_weight.T, value_weight.T

    dispatch, grad_slots = plan(
        item_lengths, rank_cell, routes, slot_order, cotangent, capacity, experts_all
    )
    flat_grad = exchange(grad_slots)
    tokens, grad_slots = tie(tokens, grad_slots)
    normed_in, qt, kt, vt = project(
        rank_cell[0], tokens, first_gain, first_bias, qw, kw, vw, members
    )
    outputs = [output_weight] + [
        swap(output_weight, "tensor", k) for k in range(1, members)
    ]
    far = members // 2
    *far_heads, far_logs = attend(
        item_lengths, rank_cell, qt, kt, vt, members, far, members - far
    )
    far_heads, kt = tie(far_heads, kt)
    far_arrived = [swap(far_heads[j - far], "tensor", j) for j in range(far, members)]
    *near_heads, near_logs = attend(item_lengths, rank_cell, qt, kt, vt, members, 0, far)
    near_heads, far_arrived, outputs = tie(near_heads, far_arrived, outputs)
    own_heads = near_heads + far_heads
    logs = (near_logs, far_logs)
    all_heads = (
        near_heads[:1]
        + [swap(near_heads[j], "tensor", j) for j in range(1, far)]
        + far_arrived
    )
    residual, outgoing = middle(
        rank_cell[0], tokens, second_gain, second_bias, dispatch, all_heads, outputs
    )
    flat_in = exchange(outgoing)

    flat_grad, outgoing = tie(flat_grad, outgoing)
    grad_act = activation_grads(flat_grad, down_matrix, members)
    near_grads = swap(flat_grad, "tensor", 1)
    flat_in, grad_act, near_grads = tie(flat_in, grad_act, near_grads)
    near_rows = swap(flat_in, "tensor", 1)
    act, grad_pre, act_sent, pre_sent, grad_mid = expert(
        rank_cell[0], flat_in, grad_act, up_matrix, members
    )
    grad_mid, act, near_rows = tie(grad_mid, act, near_rows)
    grad_back = exchange(grad_mid)

    act, act_sent, pre_sent, grad_mid = tie(act, act_sent, pre_sent, grad_mid)
    near_act = swap(act_sent, "tensor", 1)
    near_pre = swap(pre_sent, "tensor", 1)
    made = product(rank_cell[0], act, act_sent, down_matrix, members)
    made, near_act, near_pre = tie(made, near_act, near_pre)
    expert_groups = [
        (flat_in, flat_grad, act, grad_pre), (near_rows, near_grads, near_act, near_pre)
    ]
    expert_far = list(far_weights(expert_groups))
    grad_back, made, expert_far = tie(grad_back, made, expert_far)

    steps = steps_of(members)
    grad_res, sums_second, kept, sent, *grad_heads = turn(
        item_lengths, rank_cell, dispatch, grad_back, residual, cotangent,
        second_gain, all_heads, outputs,
    )
    grad_parts = [grad_heads[0]] + [
        swap(grad_heads[j], "tensor", j) for j in range(1, members)
    ]
    output_near, output_far = output_sums(kept, swap(sent, "tensor", 1), expert_far[0])
    made, grad_heads = tie(made, grad_heads)
    returned = exchange(made)
    grad_parts, output_near, output_far = tie(grad_parts, output_near, output_far)

    bit_cell = (lax.axis_index("dp") & 1).astype(jnp.int32).reshape(1, 1)
    weights = (qw, kw, vw)
    dp_steps = steps_of(sources)
    back = functools.partial(
        attend_back, lens=item_lengths, rank=rank_cell, bit=bit_cell, qt=qt, kt=kt, vt=vt,
        logs=logs, weights=weights, normed=normed_in, outs=own_heads,
    )
    groups = ((0, heads - 1), (heads - 1, 1))
    joint_a, sums_a, own_a, away_a = back(*groups[0], extras=(), grads=grad_parts)
    output_got = swap(output_far, "tensor", 2)
    joint_a, own_a, away_a, output_got, grad_parts, expert_rest, returned = tie(
        joint_a, own_a, away_a, output_got, grad_parts, expert_far[1], returned
    )
    expert_got = swap(expert_rest, "tensor", 2)
    output_sum = add_low(output_near, output_got)
    own_a = add_low(own_a, swap(away_a, "dp", 1))
    output_sum = add_low(output_sum, swap(output_sum, "dp", dp_steps[-1]))
    joint_b, unused, own_b, away_b = back(
        *groups[1], extras=(sums_a, sums_second), grads=grad_parts
    )
    joint_b, own_a, own_b, away_b, output_sum = tie(
        joint_b, own_a, own_b, away_b, output_sum
    )

    far_kept, far_sent = input_grad(
        groups, weights, (joint_a, joint_b), far, members - far, shard_rows
    )
    got_a = swap(own_a, "dp", dp_steps[1])
    got_b = swap(away_b, "dp", 1)
    joint_b, got_a, got_b = tie(joint_b, got_a, got_b)
    near_kept, near_sent = input_grad(
        groups, weights, (joint_a, joint_b), 0, far, shard_rows
    )
    own_b = add_parts(own_b, got_b)
    far_kept = add_low(far_kept, swap(far_sent, "tensor", 1))
    own_a = add_low(own_a, got_a)
    far_kept, own_b, output_sum, own_a = tie(far_kept, own_b, output_sum, own_a)
    near_core = swap(near_sent, "tensor", 1)
    near_far = swap(far_kept, "tensor", 2)
    for step in dp_steps[1:]:
        if step != dp_steps[1]:
            own_a = add_low(own_a, swap(own_a, "dp", step))
        own_b = add_parts(own_b, swap(own_b, "dp", step))
        if step == dp_steps[1]:
            own_b, expert_got = tie(own_b, expert_got)
    up_grad, down_grad = near_weights(expert_groups, output_got, expert_got)
    own_b, up_grad, down_grad, near_far = tie(own_b, up_grad, down_grad, near_far)
    pieces = (own_a, swap(own_a, "dp", 1), own_b, swap(own_b, "dp", 1))
    token_grad, block_out = close(
        rank_cell[0], tokens, first_gain, grad_res, residual, dispatch, returned,
        (near_kept, near_core, near_far),
    )
    norm_sums = own_b[-SUM_ROWS:].astype(f32)
    norm_sums = norm_sums[: SUM_ROWS // 2] + norm_sums[SUM_ROWS // 2 :]
    for step in steps:
        norm_sums = norm_sums + swap(norm_sums, "tensor", step)
    for step in dp_steps[:-1]:
        output_sum = add_low(output_sum, swap(output_sum, "dp", step))
    query_grad, key_grad, value_grad = finish(groups, bit_cell, pieces)
    return (
        block_out,
        token_grad,
        (norm_sums[0] - first_bias * norm_sums[1]) / first_gain,
        norm_sums[1],
        query_grad.T,
        key_grad.T,
        value_grad.T,
        output_sum.astype(f32),
        norm_sums[2],
        norm_sums[3],
        up_grad[None],
        down_grad[None],
    )


def solution(mesh):
    in_specs = (
        P("dp", None),
        P(),
        P(),
        P(None, "tensor"),
        P(None, "tensor"),
        P(None, "tensor"),
        P("tensor", None),
        P(),
        P(),
        P("dp", None, None),
        P("dp", None, None),
        P("dp", None),
        P(("dp", "tensor"), None),
        P(("dp", "tensor"), None),
        P(("dp", "tensor"), None),
    )
    out_specs = (
        P(("dp", "tensor"), None),
        P(("dp", "tensor"), None),
        P(),
        P(),
        P(None, "tensor"),
        P(None, "tensor"),
        P(None, "tensor"),
        P("tensor", None),
        P(),
        P(),
        P("dp", None, "tensor"),
        P("dp", "tensor", None),
    )
    return jax.shard_map(
        on_device, mesh=mesh, in_specs=in_specs, out_specs=out_specs, check_vma=False
    )
```

```python
import functools

import jax
import jax.numpy as jnp
from jax import lax
from jax.experimental import pallas as pl
from jax.experimental.pallas import tpu as pltpu
from jax.sharding import PartitionSpec as P

HEAD_DIM = 64
EPSILON = 1e-05
NEGATIVE = -1e30
f32 = jnp.float32
bf16 = jnp.bfloat16
VMEM = pl.BlockSpec(memory_space=pltpu.VMEM)
HBM = pl.BlockSpec(memory_space=pltpu.MemorySpace.HBM)
SMEM = pl.BlockSpec(memory_space=pltpu.SMEM)
SUM_ROWS = 16
COST = pl.CostEstimate(flops=2**20, bytes_accessed=2**20, transcendentals=0)
LONG = pl.CostEstimate(flops=2**34, bytes_accessed=2**24, transcendentals=0)


def layer_norm(values, gain, shift):
    average = jnp.mean(values, axis=-1, keepdims=True)
    centred = values - average
    variance = jnp.mean(centred * centred, axis=-1, keepdims=True)
    return centred * lax.rsqrt(variance + EPSILON) * gain + shift


def contract_rows(left, right):
    return lax.dot_general(
        left, right, (((0,), (0,)), ((), ())), preferred_element_type=f32
    )


def swap(values, axis, step):
    count = lax.axis_size(axis)
    return lax.ppermute(values, axis, [(i, i ^ step) for i in range(count)])


def steps_of(count):
    steps = []
    step = 1
    while step < count:
        steps.append(step)
        step *= 2
    return steps


def normalized(values):
    average = jnp.mean(values, axis=-1, keepdims=True)
    centred = values - average
    variance = jnp.mean(centred * centred, axis=-1, keepdims=True)
    return centred * lax.rsqrt(variance + EPSILON)


def project_kernel(
    rank_ref, tokens_ref, gain_ref, bias_ref, qw_ref, kw_ref, vw_ref,
    normed_ref, qt_ref, kt_ref, vt_ref,
):
    values = tokens_ref[...].astype(f32)
    normed = (normalized(values) * gain_ref[...][None] + bias_ref[...][None]).astype(bf16)
    normed_ref[...] = normed
    for weight_ref, out_ref, factor in (
        (qw_ref, qt_ref, HEAD_DIM ** (-0.5)), (kw_ref, kt_ref, None), (vw_ref, vt_ref, None)
    ):
        made = lax.dot_general(
            weight_ref[...], normed, (((1,), (1,)), ((), ())), preferred_element_type=f32
        ).astype(bf16)
        if factor is not None:
            made = made * jnp.asarray(factor, bf16)
        out_ref[...] = made


def project(rank, tokens, gain, bias, qw, kw, vw, blocks):
    slots, width = tokens.shape
    cols = qw.shape[0]
    size = slots // blocks
    fixed = lambda i, r: (0, 0)
    line = pl.BlockSpec((width,), lambda i, r: (0,))
    return pl.pallas_call(
        project_kernel,
        grid_spec=pltpu.PrefetchScalarGridSpec(
            num_scalar_prefetch=1,
            grid=(blocks,),
            in_specs=[
                pl.BlockSpec((size, width), lambda i, r: (i ^ r[0], 0)),
                line,
                line,
                pl.BlockSpec((cols, width), fixed),
                pl.BlockSpec((cols, width), fixed),
                pl.BlockSpec((cols, width), fixed),
            ],
            out_specs=(
                pl.BlockSpec((size, width), lambda i, r: (i, 0)),
                pl.BlockSpec((cols, size), lambda i, r: (0, i)),
                pl.BlockSpec((cols, size), lambda i, r: (0, i)),
                pl.BlockSpec((cols, size), lambda i, r: (0, i)),
            ),
        ),
        out_shape=(jax.ShapeDtypeStruct((slots, width), bf16),)
        + (jax.ShapeDtypeStruct((cols, slots), bf16),) * 3,
        name="project",
        cost_estimate=COST,
    )(rank, tokens, gain, bias, qw, kw, vw)


def item_ends(lens_ref):
    ends = []
    total = jnp.int32(0)
    for i in range(lens_ref.shape[1]):
        total = total + lens_ref[0, i]
        ends.append(total)
    return ends


def segments_at(place, ends):
    segment = jnp.zeros_like(place)
    for end in ends:
        segment = segment + (place >= end).astype(jnp.int32)
    return segment


def block_span(first, size, unit, ends):
    last = jnp.minimum(first + size, ends[-1]) - 1
    low = jnp.int32(0)
    high = ends[-1]
    for end in ends:
        low = jnp.where(first >= end, end, low)
    for end in reversed(ends):
        high = jnp.where(last < end, end, high)
    empty = first >= ends[-1]
    low_block = jnp.where(empty, 0, low // unit)
    high_block = jnp.where(empty, 0, (high + unit - 1) // unit)
    return low_block, high_block


def rows_at(block, size):
    return pl.ds(pl.multiple_of(block * size, size), size)


def fill_segments(row_ref, col_ref, shard, rank, ends):
    slots = row_ref.shape[1]
    at = lax.broadcasted_iota(jnp.int32, (1, slots), 1)
    place = ((at // shard) ^ rank) * shard + at % shard
    segments = segments_at(place, ends)
    row_ref[...] = segments
    col_ref[...] = jnp.transpose(jnp.broadcast_to(segments, (128, slots)), (1, 0))


def block_bias(row_ref, col_ref, rows, cols):
    return jnp.where(col_ref[rows, 0:1] == row_ref[:, cols], 0.0, NEGATIVE)


def lane_masked(values, head):
    lane = lax.broadcasted_iota(jnp.int32, values.shape, 1)
    inside = (lane >= head * HEAD_DIM) & (lane < (head + 1) * HEAD_DIM)
    return jnp.where(inside, values, jnp.zeros_like(values))


def forward_kernel(
    first, blocks, lens_ref, rank_ref, qt_ref, kt_ref, vt_ref, *refs
):
    *out_refs, log_ref, masked_ref, out_ref, row_ref, col_ref, score_ref = refs
    count, width, size = out_ref.shape
    heads = width // HEAD_DIM
    shard = size
    rank = rank_ref[0, 0]
    ends = item_ends(lens_ref)
    fill_segments(row_ref, col_ref, shard, rank, ends)
    keys = jnp.transpose(kt_ref[...], (1, 0))
    for h in range(heads):
        masked_ref[h] = lane_masked(keys, h)

    def query_block(b, unused):
        at = first + b
        i = at ^ rank
        cols = rows_at(at, size)
        queries = qt_ref[:, cols]

        def score_block(j, carry):
            rows = rows_at(j ^ rank, shard)
            bias = block_bias(row_ref, col_ref, rows, cols)
            result = []
            for h in range(heads):
                scores = jnp.dot(
                    masked_ref[h, rows, :], queries, preferred_element_type=f32
                )
                scores = scores + bias
                score_ref[h, rows_at(j, shard), :] = scores
                part = jnp.max(scores.reshape(-1, 8, size), axis=0)
                result.append(jnp.maximum(carry[h], part))
            return tuple(result)

        low, high = block_span(i * size, size, shard, ends)
        peaks = lax.fori_loop(
            low, high, score_block, (jnp.full((8, size), NEGATIVE, f32),) * heads
        )
        peaks = [jnp.max(peak, axis=0, keepdims=True) for peak in peaks]

        def key_block(j, carry):
            rows = rows_at(j ^ rank, shard)
            result = []
            for h in range(heads):
                summed, total = carry[h]
                soft = jnp.exp(score_ref[h, rows_at(j, shard), :] - peaks[h])
                summed = summed + jnp.sum(soft.reshape(-1, 8, size), axis=0)
                total = total + jnp.dot(
                    vt_ref[pl.ds(h * HEAD_DIM, HEAD_DIM), rows],
                    soft.astype(bf16),
                    preferred_element_type=f32,
                )
                result.append((summed, total))
            return tuple(result)

        start = ((jnp.zeros((8, size), f32), jnp.zeros((HEAD_DIM, size), f32)),) * heads
        done = lax.fori_loop(low, high, key_block, start)
        live = row_ref[:, cols] < len(ends)
        for h in range(heads):
            summed, total = done[h]
            summed = jnp.sum(summed, axis=0, keepdims=True)
            highest = peaks[h]
            summed = jnp.where(live, summed, 1.0)
            result = jnp.where(live, total / summed, 0.0).astype(bf16)
            logs = jnp.where(live, highest + jnp.log(summed), -NEGATIVE)
            out_ref[b, pl.ds(h * HEAD_DIM, HEAD_DIM), :] = result
            log_ref[h, :, rows_at(b, size)] = logs
        return unused

    lax.fori_loop(0, count, query_block, 0)
    for b in range(count):
        out_refs[b][...] = out_ref[b]


def attend(lens, rank, qt, kt, vt, blocks, first, count):
    width, slots = qt.shape
    size = slots // blocks
    heads = width // HEAD_DIM
    return pl.pallas_call(
        functools.partial(forward_kernel, first, blocks),
        out_shape=(jax.ShapeDtypeStruct((width, size), bf16),) * count
        + (jax.ShapeDtypeStruct((heads, 1, count * size), f32),),
        in_specs=[SMEM, SMEM, VMEM, VMEM, VMEM],
        out_specs=(VMEM,) * (count + 1),
        scratch_shapes=[
            pltpu.VMEM((heads, slots, width), bf16),
            pltpu.VMEM((count, width, size), bf16),
            pltpu.VMEM((1, slots), jnp.int32),
            pltpu.VMEM((slots, 128), jnp.int32),
            pltpu.VMEM((heads, slots, size), f32),
        ],
        name="attend",
        compiler_params=pltpu.CompilerParams(vmem_limit_bytes=60 * 2**20),
        cost_estimate=COST,
    )(lens, rank, qt, kt, vt)


def split_rows(values):
    high = values.astype(bf16)
    return jnp.concatenate([high, (values - high.astype(f32)).astype(bf16)], axis=0)


def add_kernel(a_ref, b_ref, out_ref):
    half = out_ref.shape[0] - SUM_ROWS
    line = SUM_ROWS // 2
    total = a_ref[...].astype(f32) + b_ref[...].astype(f32)
    out_ref[:half, :] = total[:half].astype(bf16)
    out_ref[half:, :] = split_rows(total[half : half + line] + total[half + line :])


def add_parts(a, b):
    return pl.pallas_call(
        add_kernel,
        out_shape=jax.ShapeDtypeStruct(a.shape, bf16),
        in_specs=[VMEM, VMEM],
        out_specs=VMEM,
        name="add_parts",
        compiler_params=pltpu.CompilerParams(vmem_limit_bytes=5 * 2**20),
        cost_estimate=COST,
    )(a, b)


def stacked_parts(first_head, heads, query, key, value):
    dim = HEAD_DIM
    parts = []
    for n in range(heads):
        first = (first_head + n) * dim
        parts += [(2 * n * dim, key, first, dim), ((2 * n + 1) * dim, value, first, dim)]
    return parts + [(2 * heads * dim, query, first_head * dim, heads * dim)]


def backward_kernel(
    first_head, heads, blocks, extras, lens_ref, rank_ref, bit_ref, qt_ref, kt_ref, vt_ref,
    near_ref, far_ref, qw_ref, kw_ref, vw_ref, normed_ref, *rest
):
    extra_refs, rest = rest[:extras], rest[extras:]
    width, slots = qt_ref.shape
    shard = slots // blocks
    dim = HEAD_DIM
    out_refs, grad_refs = rest[:blocks], rest[blocks : 2 * blocks]
    joint_ref, sums_ref, own_ref, away_ref = rest[2 * blocks : 2 * blocks + 4]
    kv_ref, q0_ref, og_ref, right_ref, inner_ref, dq_ref, made_ref = rest[-13:-6]
    log_ref = rest[-6]
    row_ref, col_ref = rest[-5:-3]
    turned_ref, rows_ref, copied = rest[-3:]
    fetch = pltpu.make_async_copy(normed_ref, rows_ref, copied)
    fetch.start()
    unit = shard // 2
    rank = rank_ref[0, 0]
    ends = item_ends(lens_ref)
    fill_segments(row_ref, col_ref, shard, rank, ends)
    near = near_ref.shape[2]
    log_ref[:, :, :near] = near_ref[...]
    log_ref[:, :, near:] = far_ref[...]
    zero = jnp.zeros((dim, slots), bf16)
    for n in range(heads):
        part = slice((first_head + n) * dim, (first_head + n + 1) * dim)
        both = jnp.concatenate([kt_ref[part, :], vt_ref[part, :]], axis=0)
        kv_ref[n] = jnp.transpose(both, (1, 0))
        padded = jnp.concatenate([qt_ref[part, :], zero], axis=0)
        q0_ref[n] = jnp.transpose(padded, (1, 0))
        right_ref[n, 0] = padded
        for b in range(blocks):
            grad = grad_refs[b][part, :]
            cols = slice(b * shard, (b + 1) * shard)
            padded = jnp.concatenate([zero[:, :shard], grad], axis=0)
            og_ref[n, cols, :] = jnp.transpose(padded, (1, 0))
            right_ref[n, 1, :, cols] = padded
            inner_ref[n, :, cols] = jnp.sum(
                out_refs[b][part, :].astype(f32) * grad.astype(f32), axis=0, keepdims=True
            )
    dq_ref[...] = jnp.zeros_like(dq_ref)

    def key_block(j, unused):
        at_key = ((j // 2) ^ rank) * 2 + j % 2
        rows = rows_at(at_key, unit)

        def query_block(i, totals):
            at = i ^ rank
            cols = rows_at(at, shard)
            same = col_ref[rows, 0:1] == row_ref[:, cols]
            result = []
            for n in range(heads):
                head = first_head + n
                kv = kv_ref[n, rows, :]
                scores = jnp.dot(kv, right_ref[n, 0, :, cols], preferred_element_type=f32)
                grad_soft = jnp.dot(kv, right_ref[n, 1, :, cols], preferred_element_type=f32)
                soft = jnp.where(same, jnp.exp(scores - log_ref[head, :, cols]), 0.0)
                grad_scores = (soft * (grad_soft - inner_ref[n, :, cols])).astype(bf16)
                total = totals[n] + jnp.dot(
                    soft.astype(bf16), og_ref[n, cols, :], preferred_element_type=f32
                )
                total = total + jnp.dot(
                    grad_scores, q0_ref[n, cols, :], preferred_element_type=f32
                )
                dq_ref[n, :, cols] += jnp.dot(
                    kt_ref[pl.ds(head * dim, dim), rows], grad_scores,
                    preferred_element_type=f32,
                )
                result.append(total)
            return tuple(result)

        low, high = block_span(j * unit, unit, shard, ends)
        start = (jnp.zeros((unit, 2 * dim), f32),) * heads
        totals = lax.fori_loop(low, high, query_block, start)
        for n in range(heads):
            part = slice(2 * dim * n, 2 * dim * (n + 1))
            total = totals[n].astype(bf16)
            joint_ref[rows, part] = total
            turned_ref[part, rows] = jnp.transpose(total, (1, 0))
        return unused

    lax.fori_loop(0, 2 * blocks, key_block, 0)
    dq = (dq_ref[...] * dim ** (-0.5)).astype(bf16).reshape(heads * dim, slots)
    turned_ref[2 * dim * heads :, :] = dq
    joint_ref[:, 2 * dim * heads :] = jnp.transpose(dq, (1, 0))
    fetch.wait()
    made_ref[...] = jnp.dot(turned_ref[...], rows_ref[...], preferred_element_type=f32)
    gains = jnp.zeros((1, rows_ref.shape[1]), f32)
    shifts = jnp.zeros((1, rows_ref.shape[1]), f32)
    for at, weight_ref, first, size in stacked_parts(
        first_head, heads, qw_ref, kw_ref, vw_ref
    ):
        weight = weight_ref[first : first + size, :].astype(f32)
        gains += jnp.sum(weight * made_ref[at : at + size, :], axis=0, keepdims=True)
        total = jnp.sum(turned_ref[at : at + size, :].astype(f32), axis=1, keepdims=True)
        shifts += jnp.sum(weight * total, axis=0, keepdims=True)
    sums_ref[0:1] = gains
    sums_ref[1:2] = shifts
    half = made_ref.shape[0] // 2
    bit = bit_ref[0, 0]
    for part_ref, at in ((own_ref, bit), (away_ref, 1 - bit)):
        part_ref[0:half, :] = made_ref[rows_at(at, half), :].astype(bf16)
        if extras:
            lines = [sums_ref[...] + extra_refs[0][...], extra_refs[1][...]]
            lines.append(jnp.zeros((SUM_ROWS // 2 - 4, gains.shape[1]), f32))
            part_ref[half:, :] = split_rows(jnp.concatenate(lines, axis=0))


def attend_back(
    first_head, heads, extras, lens, rank, bit, qt, kt, vt, logs, weights, normed, outs, grads
):
    slots, width = normed.shape
    blocks = len(outs)
    dim = HEAD_DIM
    cols = 3 * dim * heads
    rows = cols // 2 + (SUM_ROWS if extras else 0)
    return pl.pallas_call(
        functools.partial(backward_kernel, first_head, heads, blocks, len(extras)),
        out_shape=(
            jax.ShapeDtypeStruct((slots, cols), bf16),
            jax.ShapeDtypeStruct((2, width), f32),
        )
        + (jax.ShapeDtypeStruct((rows, width), bf16),) * 2,
        in_specs=[SMEM, SMEM, SMEM]
        + [VMEM] * 8
        + [pl.BlockSpec(memory_space=pl.ANY)]
        + [VMEM] * (len(extras) + 2 * blocks),
        out_specs=(VMEM,) * 4,
        scratch_shapes=[pltpu.VMEM((heads, slots, 2 * dim), bf16)] * 3
        + [
            pltpu.VMEM((heads, 2, 2 * dim, slots), bf16),
            pltpu.VMEM((heads, 1, slots), f32),
            pltpu.VMEM((heads, dim, slots), f32),
            pltpu.VMEM((cols, width), f32),
            pltpu.VMEM((qt.shape[0] // dim, 1, slots), f32),
            pltpu.VMEM((1, slots), jnp.int32),
            pltpu.VMEM((slots, 128), jnp.int32),
            pltpu.VMEM((cols, slots), bf16),
            pltpu.VMEM((slots, width), bf16),
            pltpu.SemaphoreType.DMA,
        ],
        name="attend_back",
        compiler_params=pltpu.CompilerParams(vmem_limit_bytes=60 * 2**20),
        cost_estimate=COST,
    )(lens, rank, bit, qt, kt, vt, *logs, *weights, normed, *extras, *outs, *grads)


def plan_kernel(capacity, lens_ref, rank_ref, routes_ref, order_ref, grad_ref,
                dispatch_ref, slots_ref):
    shard = routes_ref.shape[1]
    first = rank_ref[0, 0] * shard
    ends = item_ends(lens_ref)
    chosen_row = routes_ref[...]
    chosen_col = jnp.transpose(jnp.broadcast_to(chosen_row, (128, shard)), (1, 0))[:, 0:1]
    order_row = order_ref[...]
    order_col = jnp.transpose(jnp.broadcast_to(order_row, (128, shard)), (1, 0))[:, 0:1]
    alive_row = segments_at(
        first + lax.broadcasted_iota(jnp.int32, (1, shard), 1), ends
    ) < len(ends)
    alive_col = segments_at(
        first + lax.broadcasted_iota(jnp.int32, (shard, 1), 0), ends
    ) < len(ends)
    ahead = (chosen_col == chosen_row) & (order_col < order_row) & alive_col
    ranked = jnp.sum(ahead.astype(jnp.int32), axis=0, keepdims=True)
    kept = alive_row & (ranked < capacity)
    slot = jnp.where(kept, chosen_row * capacity + ranked, -1)
    dispatch = (
        lax.broadcasted_iota(jnp.int32, dispatch_ref.shape, 0) == slot
    ).astype(f32).astype(bf16)
    dispatch_ref[...] = dispatch
    slots_ref[...] = jnp.dot(
        dispatch, grad_ref[...], preferred_element_type=f32
    ).astype(bf16)


def plan(lens, rank, routes, order, grads, capacity, experts_all):
    shard, width = grads.shape
    count = experts_all * capacity
    return pl.pallas_call(
        functools.partial(plan_kernel, capacity),
        out_shape=(
            jax.ShapeDtypeStruct((count, shard), bf16),
            jax.ShapeDtypeStruct((count, width), bf16),
        ),
        in_specs=[SMEM, SMEM, VMEM, VMEM, VMEM],
        out_specs=(VMEM, VMEM),
        name="plan",
        cost_estimate=COST,
    )(lens, rank, routes.reshape(1, -1), order, grads)


def across(left, right):
    return lax.dot_general(
        left, right, (((1,), (1,)), ((), ())), preferred_element_type=f32
    )


def middle_kernel(count, rank_ref, tokens_ref, gain_ref, bias_ref, dispatch_ref, *refs):
    head_refs, weight_refs = refs[:count], refs[count : 2 * count]
    residual_ref, rows_ref = refs[2 * count :]
    residual = tokens_ref[...].astype(f32)
    for head_ref, weight_ref in zip(head_refs, weight_refs):
        residual = residual + contract_rows(head_ref[...], weight_ref[...])
    residual_ref[...] = residual
    normed = (normalized(residual) * gain_ref[...][None] + bias_ref[...][None]).astype(bf16)
    rows_ref[...] = jnp.dot(
        dispatch_ref[...], normed, preferred_element_type=f32
    ).astype(bf16)


def middle(rank, tokens, gain, bias, dispatch, heads, weights):
    count, shard = dispatch.shape
    width = tokens.shape[1]
    fixed = lambda array: pl.BlockSpec(array.shape, lambda i, r: (0,) * array.ndim)
    small = [gain, bias, dispatch, *heads, *weights]
    return pl.pallas_call(
        functools.partial(middle_kernel, len(heads)),
        grid_spec=pltpu.PrefetchScalarGridSpec(
            num_scalar_prefetch=1,
            grid=(1,),
            in_specs=[pl.BlockSpec((shard, width), lambda i, r: (r[0], 0))]
            + [fixed(array) for array in small],
            out_specs=(
                pl.BlockSpec((shard, width), lambda i, r: (0, 0)),
                pl.BlockSpec((count, width), lambda i, r: (0, 0)),
            ),
        ),
        out_shape=(
            jax.ShapeDtypeStruct((shard, width), f32),
            jax.ShapeDtypeStruct((count, width), bf16),
        ),
        name="middle",
        cost_estimate=COST,
    )(rank, tokens, *small)


def turn_kernel(
    count, lens_ref, rank_ref, dispatch_ref, back_ref, residual_ref, cotangent_ref,
    gain_ref, *refs
):
    head_refs, weight_refs = refs[:count], refs[count : 2 * count]
    grad_ref, sums_ref, kept_ref, sent_ref = refs[2 * count : 2 * count + 4]
    part_refs = refs[2 * count + 4 :]
    shard = residual_ref.shape[0]
    grad_normed = contract_rows(dispatch_ref[...], back_ref[...])
    values = residual_ref[...]
    centred = values - jnp.mean(values, axis=-1, keepdims=True)
    inverse = lax.rsqrt(jnp.mean(centred * centred, axis=-1, keepdims=True) + EPSILON)
    normed = centred * inverse
    sums_ref[0:1] = jnp.sum(grad_normed * normed, axis=0, keepdims=True)
    sums_ref[1:2] = jnp.sum(grad_normed, axis=0, keepdims=True)
    scaled = grad_normed * gain_ref[...][None]
    grad = cotangent_ref[...].astype(f32) + inverse * (
        scaled
        - jnp.mean(scaled, axis=-1, keepdims=True)
        - normed * jnp.mean(scaled * normed, axis=-1, keepdims=True)
    )
    grad_ref[...] = grad
    low = grad.astype(bf16)
    place = rank_ref[0, 0] * shard + lax.broadcasted_iota(jnp.int32, (1, shard), 1)
    alive = place < item_ends(lens_ref)[-1]
    for weight_ref, part_ref in zip(weight_refs, part_refs):
        part_ref[...] = jnp.where(alive, across(weight_ref[...], low), 0.0).astype(bf16)
    for j, head_ref in enumerate(head_refs):
        made = jnp.dot(head_ref[...], low, preferred_element_type=f32)
        (kept_ref, sent_ref)[j % 2][j // 2] = made.astype(bf16)


def turn(lens, rank, dispatch, back, residual, cotangent, gain, heads, weights):
    shard, width = residual.shape
    cols = weights[0].shape[0]
    count = len(weights)
    return pl.pallas_call(
        functools.partial(turn_kernel, count),
        out_shape=(
            jax.ShapeDtypeStruct((shard, width), f32),
            jax.ShapeDtypeStruct((2, width), f32),
            jax.ShapeDtypeStruct((count // 2, cols, width), bf16),
            jax.ShapeDtypeStruct((count // 2, cols, width), bf16),
        )
        + (jax.ShapeDtypeStruct((cols, shard), bf16),) * count,
        in_specs=[SMEM, SMEM] + [VMEM] * (5 + 2 * count),
        out_specs=(VMEM,) * (4 + count),
        name="turn",
        cost_estimate=COST,
    )(lens, rank, dispatch, back, residual, cotangent, gain, *heads, *weights)


def output_sum_kernel(kept_ref, core_ref, first_ref, near_ref, far_ref):
    cols = near_ref.shape[0]
    total = [
        (kept_ref[j].astype(f32) + core_ref[j].astype(f32)).astype(bf16) for j in range(2)
    ]
    near_ref[...] = total[0]
    far_ref[:cols, :] = total[1]
    far_ref[cols:, :] = first_ref[...]


def output_sums(kept, core, first):
    slots, cols, width = kept.shape
    return pl.pallas_call(
        output_sum_kernel,
        out_shape=(
            jax.ShapeDtypeStruct((cols, width), bf16),
            jax.ShapeDtypeStruct((cols + first.shape[0], width), bf16),
        ),
        in_specs=[VMEM] * 3,
        out_specs=(VMEM, VMEM),
        name="output_sums",
        compiler_params=pltpu.CompilerParams(vmem_limit_bytes=52 * 2**20),
        cost_estimate=LONG,
    )(kept, core, first)


def gelu_parts(values):
    below = 0.5 + 0.5 * lax.erf(values * (0.5**0.5))
    density = jnp.exp(-0.5 * values * values) * (0.5 / jnp.pi) ** 0.5
    return values * below, below + values * density


def part_at(step, parts, rank):
    half = parts // 2
    return (2 * (step % half) + step // half) ^ rank


def activation_kernel(grad_ref, down_ref, out_ref):
    out_ref[...] = across(grad_ref[...], down_ref[...]).astype(bf16)


def activation_grads(grads, down, parts):
    count, width = grads.shape
    hidden = down.shape[0]
    size = hidden // parts
    return pl.pallas_call(
        activation_kernel,
        grid=(parts,),
        out_shape=jax.ShapeDtypeStruct((count, hidden), bf16),
        in_specs=[
            pl.BlockSpec((count, width), lambda i: (0, 0)),
            pl.BlockSpec((size, width), lambda i: (i, 0)),
        ],
        out_specs=pl.BlockSpec((count, size), lambda i: (0, i)),
        name="activation_grads",
        cost_estimate=COST,
    )(grads, down)


def expert_kernel(
    parts, rank_ref, in_ref, grad_act_ref, up_ref,
    act_kept_ref, pre_kept_ref, act_sent_ref, pre_sent_ref, mid_ref,
    grads_ref, ups_ref, acts_ref, pres_ref, sum_ref, fetched, stored,
):
    rank = rank_ref[0, 0]
    size = ups_ref.shape[2]
    half = parts // 2

    def fetch(p):
        cols = rows_at(part_at(p, parts, rank), size)
        return (
            pltpu.make_async_copy(up_ref.at[:, cols], ups_ref.at[p], fetched.at[0, p]),
            pltpu.make_async_copy(grad_act_ref.at[:, cols], grads_ref.at[p], fetched.at[1, p]),
        )

    def store(p, act_out_ref, pre_out_ref):
        cols = rows_at(p % half, size)
        return (
            pltpu.make_async_copy(acts_ref.at[p], act_out_ref.at[:, cols], stored.at[0, p]),
            pltpu.make_async_copy(pres_ref.at[p], pre_out_ref.at[:, cols], stored.at[1, p]),
        )

    for p in range(parts):
        for copy in fetch(p):
            copy.start()
    sum_ref[...] = jnp.zeros_like(sum_ref)

    def part(p, unused):
        for copy in fetch(p):
            copy.wait()
        pre = jnp.dot(in_ref[...], ups_ref[p], preferred_element_type=f32)
        act, slope = gelu_parts(pre)
        acts_ref[p] = act.astype(bf16)
        grad_pre = (grads_ref[p].astype(f32) * slope).astype(bf16)
        pres_ref[p] = grad_pre
        sum_ref[...] += across(grad_pre, ups_ref[p])

        @pl.when(p < half)
        def keep():
            for copy in store(p, act_kept_ref, pre_kept_ref):
                copy.start()

        @pl.when(p >= half)
        def send():
            for copy in store(p, act_sent_ref, pre_sent_ref):
                copy.start()

        return unused

    lax.fori_loop(0, parts, part, 0)
    mid_ref[...] = sum_ref[...].astype(bf16)
    for p in range(parts):
        outs = (act_kept_ref, pre_kept_ref) if p < half else (act_sent_ref, pre_sent_ref)
        for copy in store(p, *outs):
            copy.wait()


def expert(rank, rows, grad_act, up, parts):
    count, width = rows.shape
    hidden = up.shape[1]
    size = hidden // parts
    return pl.pallas_call(
        functools.partial(expert_kernel, parts),
        out_shape=(jax.ShapeDtypeStruct((count, hidden // 2), bf16),) * 4
        + (jax.ShapeDtypeStruct((count, width), bf16),),
        in_specs=[SMEM, VMEM, HBM, HBM],
        out_specs=(HBM,) * 4 + (VMEM,),
        scratch_shapes=[
            pltpu.VMEM((parts, count, size), grad_act.dtype),
            pltpu.VMEM((parts, width, size), bf16),
            pltpu.VMEM((parts, count, size), bf16),
            pltpu.VMEM((parts, count, size), bf16),
            pltpu.VMEM((count, width), f32),
            pltpu.SemaphoreType.DMA((2, parts)),
            pltpu.SemaphoreType.DMA((2, parts)),
        ],
        name="expert",
        compiler_params=pltpu.CompilerParams(vmem_limit_bytes=52 * 2**20),
        cost_estimate=COST,
    )(rank.reshape(1, 1), rows, grad_act, up)


def product_kernel(parts, rank_ref, kept_ref, sent_ref, down_ref, out_ref,
                   acts_ref, downs_ref, sum_ref, fetched):
    rank = rank_ref[0, 0]
    size = downs_ref.shape[1]
    half = parts // 2

    def fetch(p):
        rows = rows_at(part_at(p, parts, rank), size)
        source = kept_ref if p < half else sent_ref
        cols = slice((p % half) * size, (p % half + 1) * size)
        return (
            pltpu.make_async_copy(down_ref.at[rows, :], downs_ref.at[p], fetched.at[0, p]),
            pltpu.make_async_copy(source.at[:, cols], acts_ref.at[p], fetched.at[1, p]),
        )

    for p in range(parts):
        for copy in fetch(p):
            copy.start()
    sum_ref[...] = jnp.zeros_like(sum_ref)
    for p in range(parts):
        for copy in fetch(p):
            copy.wait()
        sum_ref[...] += jnp.dot(acts_ref[p], downs_ref[p], preferred_element_type=f32)
    out_ref[...] = sum_ref[...].astype(bf16)


def product(rank, kept, sent, down, parts):
    count = kept.shape[0]
    hidden, width = down.shape
    size = hidden // parts
    return pl.pallas_call(
        functools.partial(product_kernel, parts),
        out_shape=jax.ShapeDtypeStruct((count, width), bf16),
        in_specs=[SMEM, HBM, HBM, HBM],
        out_specs=VMEM,
        scratch_shapes=[
            pltpu.VMEM((parts, count, size), bf16),
            pltpu.VMEM((parts, size, width), bf16),
            pltpu.VMEM((count, width), f32),
            pltpu.SemaphoreType.DMA((2, parts)),
        ],
        name="product",
        cost_estimate=COST,
    )(rank.reshape(1, 1), kept, sent, down)


def group_sums(refs, groups):
    dup = ddown = 0.0
    for g in range(groups):
        in_ref, grad_ref, act_ref, pre_ref = refs[4 * g : 4 * g + 4]
        dup = dup + contract_rows(in_ref[...], pre_ref[...])
        ddown = ddown + contract_rows(act_ref[...], grad_ref[...])
    return dup, ddown


def group_specs(groups, part):
    count, width = groups[0][0].shape
    size = groups[0][2].shape[1] // 2
    fixed = pl.BlockSpec((count, width), lambda i: (0, 0))
    columns = pl.BlockSpec((count, size), lambda i: (0, part))
    return [fixed, fixed, columns, columns] * len(groups)


def far_weight_kernel(groups, *refs):
    first_ref, rest_ref = refs[-2:]
    dup, ddown = group_sums(refs, groups)
    cut = first_ref.shape[0]
    first_ref[...] = dup[:cut].astype(bf16)
    rest_ref[: dup.shape[0] - cut, :] = dup[cut:].astype(bf16)
    rest_ref[dup.shape[0] - cut :, :] = ddown.astype(bf16)


def far_weights(groups):
    width = groups[0][0].shape[1]
    size = groups[0][2].shape[1] // 2
    cut = (width + size) // 4
    shapes = ((cut, size), (width + size - cut, size))
    return pl.pallas_call(
        functools.partial(far_weight_kernel, len(groups)),
        grid=(1,),
        in_specs=group_specs(groups, 1),
        out_specs=tuple(pl.BlockSpec(shape, lambda i: (0, 0)) for shape in shapes),
        out_shape=tuple(jax.ShapeDtypeStruct(shape, bf16) for shape in shapes),
        name="far_weights",
        cost_estimate=COST,
    )(*[values for group in groups for values in group])


def near_weight_kernel(groups, skip, *refs):
    first_ref, rest_ref, up_ref, down_ref = refs[-4:]
    dup, ddown = group_sums(refs, groups)
    cut = first_ref.shape[0] - skip
    down_at = dup.shape[0] - cut
    up_ref[:cut, :] = dup[:cut] + first_ref[skip:, :].astype(f32)
    up_ref[cut:, :] = dup[cut:] + rest_ref[:down_at, :].astype(f32)
    down_ref[...] = ddown + rest_ref[down_at:, :].astype(f32)


def near_weights(groups, first, rest):
    width = groups[0][0].shape[1]
    size = groups[0][2].shape[1] // 2
    skip = first.shape[0] + rest.shape[0] - width - size
    whole = lambda shape: pl.BlockSpec(shape, lambda i: (0, 0))
    return pl.pallas_call(
        functools.partial(near_weight_kernel, len(groups), skip),
        grid=(1,),
        in_specs=group_specs(groups, 0) + [whole(first.shape), whole(rest.shape)],
        out_specs=(whole((width, size)), whole((size, width))),
        out_shape=(
            jax.ShapeDtypeStruct((width, size), f32),
            jax.ShapeDtypeStruct((size, width), f32),
        ),
        name="near_weights",
        compiler_params=pltpu.CompilerParams(vmem_limit_bytes=52 * 2**20),
        cost_estimate=COST,
    )(*[values for group in groups for values in group], first, rest)


def input_grad_kernel(groups, qw_ref, kw_ref, vw_ref, *refs):
    joint_refs = refs[: len(groups)]
    kept_ref, sent_ref, turned_ref = refs[len(groups) :]
    step = pl.program_id(0)

    @pl.when(step == 0)
    def stack():
        start = 0
        for first_head, heads in groups:
            for at, weight_ref, first, size in stacked_parts(
                first_head, heads, qw_ref, kw_ref, vw_ref
            ):
                turned_ref[start + at : start + at + size, :] = weight_ref[
                    first : first + size, :
                ]
            start += 3 * heads * HEAD_DIM

    total = 0.0
    at = 0
    for joint_ref in joint_refs:
        rows = slice(at, at + joint_ref.shape[1])
        total = total + jnp.dot(
            joint_ref[...], turned_ref[rows, :], preferred_element_type=f32
        )
        at += joint_ref.shape[1]

    @pl.when(step % 2 == 0)
    def keep():
        kept_ref[0] = total.astype(bf16)

    @pl.when(step % 2 == 1)
    def send():
        sent_ref[0] = total.astype(bf16)


def input_grad(groups, weights, joints, first, count, size):
    cols, width = weights[0].shape
    fixed = pl.BlockSpec((cols, width), lambda i: (0, 0))
    return pl.pallas_call(
        functools.partial(input_grad_kernel, groups),
        grid=(count,),
        out_shape=(jax.ShapeDtypeStruct((count // 2, size, width), bf16),) * 2,
        in_specs=[fixed] * 3
        + [
            pl.BlockSpec((size, joint.shape[1]), lambda i: (first + i, 0))
            for joint in joints
        ],
        out_specs=(pl.BlockSpec((1, size, width), lambda i: (i // 2, 0, 0)),) * 2,
        scratch_shapes=[pltpu.VMEM((3 * cols, width), bf16)],
        name="input_grad",
        compiler_params=pltpu.CompilerParams(vmem_limit_bytes=10 * 2**20),
        cost_estimate=COST,
    )(*weights, *joints)


def close_kernel(
    rank_ref, tokens_ref, gain_ref, grad_ref, residual_ref, dispatch_ref, back_ref, *refs
):
    *part_refs, out_ref, block_ref = refs
    block_ref[...] = residual_ref[...] + contract_rows(dispatch_ref[...], back_ref[...])
    grad_in = 0.0
    for part_ref in part_refs:
        grad_in = grad_in + part_ref[...].reshape(out_ref.shape).astype(f32)
    values = tokens_ref[...].astype(f32)
    centred = values - jnp.mean(values, axis=-1, keepdims=True)
    inverse = lax.rsqrt(jnp.mean(centred * centred, axis=-1, keepdims=True) + EPSILON)
    normed = centred * inverse
    scaled = grad_in * gain_ref[...][None]
    out_ref[...] = grad_ref[...] + inverse * (
        scaled
        - jnp.mean(scaled, axis=-1, keepdims=True)
        - normed * jnp.mean(scaled * normed, axis=-1, keepdims=True)
    )


def close(rank, tokens, gain, grad, residual, dispatch, back, parts):
    shard, width = grad.shape
    count = dispatch.shape[0]
    size = shard // 2
    rows = pl.BlockSpec((size, width), lambda i, r: (i, 0))
    return pl.pallas_call(
        close_kernel,
        grid_spec=pltpu.PrefetchScalarGridSpec(
            num_scalar_prefetch=1,
            grid=(2,),
            in_specs=[
                pl.BlockSpec((size, width), lambda i, r: (2 * r[0] + i, 0)),
                pl.BlockSpec((width,), lambda i, r: (0,)),
                rows,
                rows,
                pl.BlockSpec((count, size), lambda i, r: (0, i)),
                pl.BlockSpec((count, width), lambda i, r: (0, 0)),
            ]
            + [pl.BlockSpec((1, size, width), lambda i, r: (0, i, 0))] * len(parts),
            out_specs=(rows, rows),
        ),
        out_shape=(jax.ShapeDtypeStruct((shard, width), f32),) * 2,
        name="close",
        compiler_params=pltpu.CompilerParams(vmem_limit_bytes=16 * 2**20),
        cost_estimate=COST,
    )(rank, tokens, gain, grad, residual, dispatch, back, *parts)


def add_low_kernel(a_ref, b_ref, out_ref):
    out_ref[...] = (a_ref[...].astype(f32) + b_ref[...].astype(f32)).astype(bf16)


def add_low(a, b):
    block = pl.BlockSpec(a.shape, lambda i: (0,) * a.ndim)
    return pl.pallas_call(
        add_low_kernel,
        grid=(1,),
        out_shape=jax.ShapeDtypeStruct(a.shape, bf16),
        in_specs=[block, block],
        out_specs=block,
        name="add_low",
        compiler_params=pltpu.CompilerParams(vmem_limit_bytes=6 * 2**20),
        cost_estimate=COST,
    )(a, b)


def after(value, *others):
    return lax.optimization_barrier((value, *others))[0]


def tie(*values):
    return lax.optimization_barrier(values)


def finish_kernel(groups, bit_ref, *refs):
    pieces, refs = refs[: 2 * len(groups)], refs[2 * len(groups) :]
    query_ref, key_ref, value_ref = refs[:3]
    bit = bit_ref[0, 0]
    for g, ((first_head, heads), whole_ref) in enumerate(zip(groups, refs[3:])):
        half = whole_ref.shape[0] // 2
        for piece_ref, at in ((pieces[2 * g], bit), (pieces[2 * g + 1], 1 - bit)):
            whole_ref[rows_at(at, half), :] = piece_ref[0:half, :].astype(f32)
        for at, target_ref, first, size in stacked_parts(
            first_head, heads, query_ref, key_ref, value_ref
        ):
            target_ref[first : first + size, :] = whole_ref[at : at + size, :]


def finish(groups, bit, pieces):
    width = pieces[0].shape[1]
    cols = sum(heads for first_head, heads in groups) * HEAD_DIM
    return pl.pallas_call(
        functools.partial(finish_kernel, groups),
        out_shape=(jax.ShapeDtypeStruct((cols, width), f32),) * 3,
        in_specs=[SMEM] + [VMEM] * len(pieces),
        out_specs=(VMEM,) * 3,
        scratch_shapes=[
            pltpu.VMEM((3 * heads * HEAD_DIM, width), f32) for first_head, heads in groups
        ],
        name="finish",
        compiler_params=pltpu.CompilerParams(vmem_limit_bytes=10 * 2**20),
        cost_estimate=COST,
    )(bit, *pieces)


def on_device(
    tokens,
    first_gain,
    first_bias,
    query_weight,
    key_weight,
    value_weight,
    output_weight,
    second_gain,
    second_bias,
    expert_up,
    expert_down,
    item_lengths,
    routes,
    slot_order,
    cotangent,
):
    slots_all, width = tokens.shape
    members = lax.axis_size("tensor")
    shard_rows = slots_all // members
    rank = lax.axis_index("tensor")
    sources = lax.axis_size("dp")
    experts_all = sources * expert_up.shape[0]
    capacity = shard_rows // experts_all
    head_cols = query_weight.shape[1]
    heads = head_cols // HEAD_DIM
    up_matrix = expert_up[0]
    down_matrix = expert_down[0]
    rank_cell = rank.astype(jnp.int32).reshape(1, 1)

    def exchange(rows):
        return lax.all_to_all(
            rows.reshape(sources, -1, width), "dp", split_axis=0, concat_axis=0, tiled=True
        ).reshape(-1, width)

    qw, kw, vw = query_weight.T, key_weight.T, value_weight.T

    dispatch, grad_slots = plan(
        item_lengths, rank_cell, routes, slot_order, cotangent, capacity, experts_all
    )
    flat_grad = exchange(grad_slots)
    tokens, grad_slots = tie(tokens, grad_slots)
    normed_in, qt, kt, vt = project(
        rank_cell[0], tokens, first_gain, first_bias, qw, kw, vw, members
    )
    outputs = [output_weight] + [
        swap(output_weight, "tensor", k) for k in range(1, members)
    ]
    far = members // 2
    *far_heads, far_logs = attend(
        item_lengths, rank_cell, qt, kt, vt, members, far, members - far
    )
    far_heads, kt = tie(far_heads, kt)
    far_arrived = [swap(far_heads[j - far], "tensor", j) for j in range(far, members)]
    *near_heads, near_logs = attend(item_lengths, rank_cell, qt, kt, vt, members, 0, far)
    near_heads, far_arrived, outputs = tie(near_heads, far_arrived, outputs)
    own_heads = near_heads + far_heads
    logs = (near_logs, far_logs)
    all_heads = (
        near_heads[:1]
        + [swap(near_heads[j], "tensor", j) for j in range(1, far)]
        + far_arrived
    )
    residual, outgoing = middle(
        rank_cell[0], tokens, second_gain, second_bias, dispatch, all_heads, outputs
    )
    flat_in = exchange(outgoing)

    flat_grad, outgoing = tie(flat_grad, outgoing)
    grad_act = activation_grads(flat_grad, down_matrix, members)
    near_grads = swap(flat_grad, "tensor", 1)
    flat_in, grad_act, near_grads = tie(flat_in, grad_act, near_grads)
    near_rows = swap(flat_in, "tensor", 1)
    act, grad_pre, act_sent, pre_sent, grad_mid = expert(
        rank_cell[0], flat_in, grad_act, up_matrix, members
    )
    grad_mid, act, near_rows = tie(grad_mid, act, near_rows)
    grad_back = exchange(grad_mid)

    act, act_sent, pre_sent, grad_mid = tie(act, act_sent, pre_sent, grad_mid)
    near_act = swap(act_sent, "tensor", 1)
    near_pre = swap(pre_sent, "tensor", 1)
    made = product(rank_cell[0], act, act_sent, down_matrix, members)
    made, near_act, near_pre = tie(made, near_act, near_pre)
    expert_groups = [
        (flat_in, flat_grad, act, grad_pre), (near_rows, near_grads, near_act, near_pre)
    ]
    expert_far = list(far_weights(expert_groups))
    grad_back, made, expert_far = tie(grad_back, made, expert_far)

    steps = steps_of(members)
    grad_res, sums_second, kept, sent, *grad_heads = turn(
        item_lengths, rank_cell, dispatch, grad_back, residual, cotangent,
        second_gain, all_heads, outputs,
    )
    grad_parts = [grad_heads[0]] + [
        swap(grad_heads[j], "tensor", j) for j in range(1, members)
    ]
    output_near, output_far = output_sums(kept, swap(sent, "tensor", 1), expert_far[0])
    made, grad_heads = tie(made, grad_heads)
    returned = exchange(made)
    grad_parts, output_near, output_far = tie(grad_parts, output_near, output_far)

    bit_cell = (lax.axis_index("dp") & 1).astype(jnp.int32).reshape(1, 1)
    weights = (qw, kw, vw)
    dp_steps = steps_of(sources)
    back = functools.partial(
        attend_back, lens=item_lengths, rank=rank_cell, bit=bit_cell, qt=qt, kt=kt, vt=vt,
        logs=logs, weights=weights, normed=normed_in, outs=own_heads,
    )
    groups = ((0, heads - 1), (heads - 1, 1))
    joint_a, sums_a, own_a, away_a = back(*groups[0], extras=(), grads=grad_parts)
    output_got = swap(output_far, "tensor", 2)
    joint_a, own_a, away_a, output_got, grad_parts, expert_rest, returned = tie(
        joint_a, own_a, away_a, output_got, grad_parts, expert_far[1], returned
    )
    expert_got = swap(expert_rest, "tensor", 2)
    output_sum = add_low(output_near, output_got)
    own_a = add_low(own_a, swap(away_a, "dp", 1))
    output_sum = add_low(output_sum, swap(output_sum, "dp", dp_steps[-1]))
    joint_b, unused, own_b, away_b = back(
        *groups[1], extras=(sums_a, sums_second), grads=grad_parts
    )
    joint_b, own_a, own_b, away_b, output_sum = tie(
        joint_b, own_a, own_b, away_b, output_sum
    )

    far_kept, far_sent = input_grad(
        groups, weights, (joint_a, joint_b), far, members - far, shard_rows
    )
    got_a = swap(own_a, "dp", dp_steps[1])
    got_b = swap(away_b, "dp", 1)
    joint_b, got_a, got_b = tie(joint_b, got_a, got_b)
    near_kept, near_sent = input_grad(
        groups, weights, (joint_a, joint_b), 0, far, shard_rows
    )
    own_b = add_parts(own_b, got_b)
    far_kept = add_low(far_kept, swap(far_sent, "tensor", 1))
    own_a = add_low(own_a, got_a)
    far_kept, own_b, output_sum, own_a = tie(far_kept, own_b, output_sum, own_a)
    near_core = swap(near_sent, "tensor", 1)
    near_far = swap(far_kept, "tensor", 2)
    for step in dp_steps[1:]:
        if step != dp_steps[1]:
            own_a = add_low(own_a, swap(own_a, "dp", step))
        own_b = add_parts(own_b, swap(own_b, "dp", step))
        if step == dp_steps[1]:
            own_b, expert_got = tie(own_b, expert_got)
    up_grad, down_grad = near_weights(expert_groups, output_got, expert_got)
    own_b, up_grad, down_grad, near_far = tie(own_b, up_grad, down_grad, near_far)
    pieces = (own_a, swap(own_a, "dp", 1), own_b, swap(own_b, "dp", 1))
    token_grad, block_out = close(
        rank_cell[0], tokens, first_gain, grad_res, residual, dispatch, returned,
        (near_kept, near_core, near_far),
    )
    norm_sums = own_b[-SUM_ROWS:].astype(f32)
    norm_sums = norm_sums[: SUM_ROWS // 2] + norm_sums[SUM_ROWS // 2 :]
    for step in steps:
        norm_sums = norm_sums + swap(norm_sums, "tensor", step)
    for step in dp_steps[:-1]:
        output_sum = add_low(output_sum, swap(output_sum, "dp", step))
    output_sum = after(output_sum, token_grad)
    query_grad, key_grad, value_grad = finish(groups, bit_cell, pieces)
    return (
        block_out,
        token_grad,
        (norm_sums[0] - first_bias * norm_sums[1]) / first_gain,
        norm_sums[1],
        query_grad.T,
        key_grad.T,
        value_grad.T,
        output_sum.astype(f32),
        norm_sums[2],
        norm_sums[3],
        up_grad[None],
        down_grad[None],
    )


def solution(mesh):
    in_specs = (
        P("dp", None),
        P(),
        P(),
        P(None, "tensor"),
        P(None, "tensor"),
        P(None, "tensor"),
        P("tensor", None),
        P(),
        P(),
        P("dp", None, None),
        P("dp", None, None),
        P("dp", None),
        P(("dp", "tensor"), None),
        P(("dp", "tensor"), None),
        P(("dp", "tensor"), None),
    )
    out_specs = (
        P(("dp", "tensor"), None),
        P(("dp", "tensor"), None),
        P(),
        P(),
        P(None, "tensor"),
        P(None, "tensor"),
        P(None, "tensor"),
        P("tensor", None),
        P(),
        P(),
        P("dp", None, "tensor"),
        P("dp", "tensor", None),
    )
    return jax.shard_map(
        on_device, mesh=mesh, in_specs=in_specs, out_specs=out_specs, check_vma=False
    )
```

```python
import functools

import jax
import jax.numpy as jnp
from jax import lax
from jax.experimental import pallas as pl
from jax.experimental.pallas import tpu as pltpu
from jax.sharding import PartitionSpec as P

HEAD_DIM = 64
EPSILON = 1e-05
NEGATIVE = -1e30
f32 = jnp.float32
bf16 = jnp.bfloat16
VMEM = pl.BlockSpec(memory_space=pltpu.VMEM)
HBM = pl.BlockSpec(memory_space=pltpu.MemorySpace.HBM)
SMEM = pl.BlockSpec(memory_space=pltpu.SMEM)
SUM_ROWS = 16
COST = pl.CostEstimate(flops=2**20, bytes_accessed=2**20, transcendentals=0)
LONG = pl.CostEstimate(flops=2**34, bytes_accessed=2**24, transcendentals=0)


def layer_norm(values, gain, shift):
    average = jnp.mean(values, axis=-1, keepdims=True)
    centred = values - average
    variance = jnp.mean(centred * centred, axis=-1, keepdims=True)
    return centred * lax.rsqrt(variance + EPSILON) * gain + shift


def contract_rows(left, right):
    return lax.dot_general(
        left, right, (((0,), (0,)), ((), ())), preferred_element_type=f32
    )


def swap(values, axis, step):
    count = lax.axis_size(axis)
    return lax.ppermute(values, axis, [(i, i ^ step) for i in range(count)])


def steps_of(count):
    steps = []
    step = 1
    while step < count:
        steps.append(step)
        step *= 2
    return steps


def normalized(values):
    average = jnp.mean(values, axis=-1, keepdims=True)
    centred = values - average
    variance = jnp.mean(centred * centred, axis=-1, keepdims=True)
    return centred * lax.rsqrt(variance + EPSILON)


def project_kernel(
    rank_ref, tokens_ref, gain_ref, bias_ref, qw_ref, kw_ref, vw_ref,
    normed_ref, qt_ref, kt_ref, vt_ref,
):
    values = tokens_ref[...].astype(f32)
    normed = (normalized(values) * gain_ref[...][None] + bias_ref[...][None]).astype(bf16)
    normed_ref[...] = normed
    for weight_ref, out_ref, factor in (
        (qw_ref, qt_ref, HEAD_DIM ** (-0.5)), (kw_ref, kt_ref, None), (vw_ref, vt_ref, None)
    ):
        made = lax.dot_general(
            weight_ref[...], normed, (((1,), (1,)), ((), ())), preferred_element_type=f32
        ).astype(bf16)
        if factor is not None:
            made = made * jnp.asarray(factor, bf16)
        out_ref[...] = made


def project(rank, tokens, gain, bias, qw, kw, vw, blocks):
    slots, width = tokens.shape
    cols = qw.shape[0]
    size = slots // blocks
    fixed = lambda i, r: (0, 0)
    line = pl.BlockSpec((width,), lambda i, r: (0,))
    return pl.pallas_call(
        project_kernel,
        grid_spec=pltpu.PrefetchScalarGridSpec(
            num_scalar_prefetch=1,
            grid=(blocks,),
            in_specs=[
                pl.BlockSpec((size, width), lambda i, r: (i ^ r[0], 0)),
                line,
                line,
                pl.BlockSpec((cols, width), fixed),
                pl.BlockSpec((cols, width), fixed),
                pl.BlockSpec((cols, width), fixed),
            ],
            out_specs=(
                pl.BlockSpec((size, width), lambda i, r: (i, 0)),
                pl.BlockSpec((cols, size), lambda i, r: (0, i)),
                pl.BlockSpec((cols, size), lambda i, r: (0, i)),
                pl.BlockSpec((cols, size), lambda i, r: (0, i)),
            ),
        ),
        out_shape=(jax.ShapeDtypeStruct((slots, width), bf16),)
        + (jax.ShapeDtypeStruct((cols, slots), bf16),) * 3,
        name="project",
        cost_estimate=COST,
    )(rank, tokens, gain, bias, qw, kw, vw)


def item_ends(lens_ref):
    ends = []
    total = jnp.int32(0)
    for i in range(lens_ref.shape[1]):
        total = total + lens_ref[0, i]
        ends.append(total)
    return ends


def segments_at(place, ends):
    segment = jnp.zeros_like(place)
    for end in ends:
        segment = segment + (place >= end).astype(jnp.int32)
    return segment


def block_span(first, size, unit, ends):
    last = jnp.minimum(first + size, ends[-1]) - 1
    low = jnp.int32(0)
    high = ends[-1]
    for end in ends:
        low = jnp.where(first >= end, end, low)
    for end in reversed(ends):
        high = jnp.where(last < end, end, high)
    empty = first >= ends[-1]
    low_block = jnp.where(empty, 0, low // unit)
    high_block = jnp.where(empty, 0, (high + unit - 1) // unit)
    return low_block, high_block


def rows_at(block, size):
    return pl.ds(pl.multiple_of(block * size, size), size)


def fill_segments(row_ref, col_ref, shard, rank, ends):
    slots = row_ref.shape[1]
    at = lax.broadcasted_iota(jnp.int32, (1, slots), 1)
    place = ((at // shard) ^ rank) * shard + at % shard
    segments = segments_at(place, ends)
    row_ref[...] = segments
    col_ref[...] = jnp.transpose(jnp.broadcast_to(segments, (128, slots)), (1, 0))


def block_bias(row_ref, col_ref, rows, cols):
    return jnp.where(col_ref[rows, 0:1] == row_ref[:, cols], 0.0, NEGATIVE)


def lane_masked(values, head):
    lane = lax.broadcasted_iota(jnp.int32, values.shape, 1)
    inside = (lane >= head * HEAD_DIM) & (lane < (head + 1) * HEAD_DIM)
    return jnp.where(inside, values, jnp.zeros_like(values))


def forward_kernel(
    first, blocks, lens_ref, rank_ref, qt_ref, kt_ref, vt_ref, *refs
):
    *out_refs, log_ref, masked_ref, out_ref, row_ref, col_ref, score_ref = refs
    count, width, size = out_ref.shape
    heads = width // HEAD_DIM
    shard = size
    rank = rank_ref[0, 0]
    ends = item_ends(lens_ref)
    fill_segments(row_ref, col_ref, shard, rank, ends)
    keys = jnp.transpose(kt_ref[...], (1, 0))
    for h in range(heads):
        masked_ref[h] = lane_masked(keys, h)

    def query_block(b, unused):
        at = first + b
        i = at ^ rank
        cols = rows_at(at, size)
        queries = qt_ref[:, cols]

        def score_block(j, carry):
            rows = rows_at(j ^ rank, shard)
            bias = block_bias(row_ref, col_ref, rows, cols)
            result = []
            for h in range(heads):
                scores = jnp.dot(
                    masked_ref[h, rows, :], queries, preferred_element_type=f32
                )
                scores = scores + bias
                score_ref[h, rows_at(j, shard), :] = scores
                part = jnp.max(scores.reshape(-1, 8, size), axis=0)
                result.append(jnp.maximum(carry[h], part))
            return tuple(result)

        low, high = block_span(i * size, size, shard, ends)
        peaks = lax.fori_loop(
            low, high, score_block, (jnp.full((8, size), NEGATIVE, f32),) * heads
        )
        peaks = [jnp.max(peak, axis=0, keepdims=True) for peak in peaks]

        def key_block(j, carry):
            rows = rows_at(j ^ rank, shard)
            result = []
            for h in range(heads):
                summed, total = carry[h]
                soft = jnp.exp(score_ref[h, rows_at(j, shard), :] - peaks[h])
                summed = summed + jnp.sum(soft.reshape(-1, 8, size), axis=0)
                total = total + jnp.dot(
                    vt_ref[pl.ds(h * HEAD_DIM, HEAD_DIM), rows],
                    soft.astype(bf16),
                    preferred_element_type=f32,
                )
                result.append((summed, total))
            return tuple(result)

        start = ((jnp.zeros((8, size), f32), jnp.zeros((HEAD_DIM, size), f32)),) * heads
        done = lax.fori_loop(low, high, key_block, start)
        live = row_ref[:, cols] < len(ends)
        for h in range(heads):
            summed, total = done[h]
            summed = jnp.sum(summed, axis=0, keepdims=True)
            highest = peaks[h]
            summed = jnp.where(live, summed, 1.0)
            result = jnp.where(live, total / summed, 0.0).astype(bf16)
            logs = jnp.where(live, highest + jnp.log(summed), -NEGATIVE)
            out_ref[b, pl.ds(h * HEAD_DIM, HEAD_DIM), :] = result
            log_ref[h, :, rows_at(b, size)] = logs
        return unused

    lax.fori_loop(0, count, query_block, 0)
    for b in range(count):
        out_refs[b][...] = out_ref[b]


def attend(lens, rank, qt, kt, vt, blocks, first, count):
    width, slots = qt.shape
    size = slots // blocks
    heads = width // HEAD_DIM
    return pl.pallas_call(
        functools.partial(forward_kernel, first, blocks),
        out_shape=(jax.ShapeDtypeStruct((width, size), bf16),) * count
        + (jax.ShapeDtypeStruct((heads, 1, count * size), f32),),
        in_specs=[SMEM, SMEM, VMEM, VMEM, VMEM],
        out_specs=(VMEM,) * (count + 1),
        scratch_shapes=[
            pltpu.VMEM((heads, slots, width), bf16),
            pltpu.VMEM((count, width, size), bf16),
            pltpu.VMEM((1, slots), jnp.int32),
            pltpu.VMEM((slots, 128), jnp.int32),
            pltpu.VMEM((heads, slots, size), f32),
        ],
        name="attend",
        compiler_params=pltpu.CompilerParams(vmem_limit_bytes=60 * 2**20),
        cost_estimate=COST,
    )(lens, rank, qt, kt, vt)


def split_rows(values):
    high = values.astype(bf16)
    return jnp.concatenate([high, (values - high.astype(f32)).astype(bf16)], axis=0)


def add_kernel(a_ref, b_ref, out_ref):
    half = out_ref.shape[0] - SUM_ROWS
    line = SUM_ROWS // 2
    total = a_ref[...].astype(f32) + b_ref[...].astype(f32)
    out_ref[:half, :] = total[:half].astype(bf16)
    out_ref[half:, :] = split_rows(total[half : half + line] + total[half + line :])


def add_parts(a, b):
    return pl.pallas_call(
        add_kernel,
        out_shape=jax.ShapeDtypeStruct(a.shape, bf16),
        in_specs=[VMEM, VMEM],
        out_specs=VMEM,
        name="add_parts",
        compiler_params=pltpu.CompilerParams(vmem_limit_bytes=5 * 2**20),
        cost_estimate=COST,
    )(a, b)


def stacked_parts(first_head, heads, query, key, value):
    dim = HEAD_DIM
    parts = []
    for n in range(heads):
        first = (first_head + n) * dim
        parts += [(2 * n * dim, key, first, dim), ((2 * n + 1) * dim, value, first, dim)]
    return parts + [(2 * heads * dim, query, first_head * dim, heads * dim)]


def backward_kernel(
    first_head, heads, blocks, extras, lens_ref, rank_ref, bit_ref, qt_ref, kt_ref, vt_ref,
    near_ref, far_ref, qw_ref, kw_ref, vw_ref, normed_ref, *rest
):
    extra_refs, rest = rest[:extras], rest[extras:]
    width, slots = qt_ref.shape
    shard = slots // blocks
    dim = HEAD_DIM
    out_refs, grad_refs = rest[:blocks], rest[blocks : 2 * blocks]
    joint_ref, sums_ref, own_ref, away_ref = rest[2 * blocks : 2 * blocks + 4]
    kv_ref, q0_ref, og_ref, right_ref, inner_ref, dq_ref, made_ref = rest[-13:-6]
    log_ref = rest[-6]
    row_ref, col_ref = rest[-5:-3]
    turned_ref, rows_ref, copied = rest[-3:]
    fetch = pltpu.make_async_copy(normed_ref, rows_ref, copied)
    fetch.start()
    unit = shard // 2
    rank = rank_ref[0, 0]
    ends = item_ends(lens_ref)
    fill_segments(row_ref, col_ref, shard, rank, ends)
    near = near_ref.shape[2]
    log_ref[:, :, :near] = near_ref[...]
    log_ref[:, :, near:] = far_ref[...]
    zero = jnp.zeros((dim, slots), bf16)
    for n in range(heads):
        part = slice((first_head + n) * dim, (first_head + n + 1) * dim)
        both = jnp.concatenate([kt_ref[part, :], vt_ref[part, :]], axis=0)
        kv_ref[n] = jnp.transpose(both, (1, 0))
        padded = jnp.concatenate([qt_ref[part, :], zero], axis=0)
        q0_ref[n] = jnp.transpose(padded, (1, 0))
        right_ref[n, 0] = padded
        for b in range(blocks):
            grad = grad_refs[b][part, :]
            cols = slice(b * shard, (b + 1) * shard)
            padded = jnp.concatenate([zero[:, :shard], grad], axis=0)
            og_ref[n, cols, :] = jnp.transpose(padded, (1, 0))
            right_ref[n, 1, :, cols] = padded
            inner_ref[n, :, cols] = jnp.sum(
                out_refs[b][part, :].astype(f32) * grad.astype(f32), axis=0, keepdims=True
            )
    dq_ref[...] = jnp.zeros_like(dq_ref)

    def key_block(j, unused):
        at_key = ((j // 2) ^ rank) * 2 + j % 2
        rows = rows_at(at_key, unit)

        def query_block(i, totals):
            at = i ^ rank
            cols = rows_at(at, shard)
            same = col_ref[rows, 0:1] == row_ref[:, cols]
            result = []
            for n in range(heads):
                head = first_head + n
                kv = kv_ref[n, rows, :]
                scores = jnp.dot(kv, right_ref[n, 0, :, cols], preferred_element_type=f32)
                grad_soft = jnp.dot(kv, right_ref[n, 1, :, cols], preferred_element_type=f32)
                soft = jnp.where(same, jnp.exp(scores - log_ref[head, :, cols]), 0.0)
                grad_scores = (soft * (grad_soft - inner_ref[n, :, cols])).astype(bf16)
                total = totals[n] + jnp.dot(
                    soft.astype(bf16), og_ref[n, cols, :], preferred_element_type=f32
                )
                total = total + jnp.dot(
                    grad_scores, q0_ref[n, cols, :], preferred_element_type=f32
                )
                dq_ref[n, :, cols] += jnp.dot(
                    kt_ref[pl.ds(head * dim, dim), rows], grad_scores,
                    preferred_element_type=f32,
                )
                result.append(total)
            return tuple(result)

        low, high = block_span(j * unit, unit, shard, ends)
        start = (jnp.zeros((unit, 2 * dim), f32),) * heads
        totals = lax.fori_loop(low, high, query_block, start)
        for n in range(heads):
            part = slice(2 * dim * n, 2 * dim * (n + 1))
            total = totals[n].astype(bf16)
            joint_ref[rows, part] = total
            turned_ref[part, rows] = jnp.transpose(total, (1, 0))
        return unused

    lax.fori_loop(0, 2 * blocks, key_block, 0)
    dq = (dq_ref[...] * dim ** (-0.5)).astype(bf16).reshape(heads * dim, slots)
    turned_ref[2 * dim * heads :, :] = dq
    joint_ref[:, 2 * dim * heads :] = jnp.transpose(dq, (1, 0))
    fetch.wait()
    made_ref[...] = jnp.dot(turned_ref[...], rows_ref[...], preferred_element_type=f32)
    gains = jnp.zeros((1, rows_ref.shape[1]), f32)
    shifts = jnp.zeros((1, rows_ref.shape[1]), f32)
    for at, weight_ref, first, size in stacked_parts(
        first_head, heads, qw_ref, kw_ref, vw_ref
    ):
        weight = weight_ref[first : first + size, :].astype(f32)
        gains += jnp.sum(weight * made_ref[at : at + size, :], axis=0, keepdims=True)
        total = jnp.sum(turned_ref[at : at + size, :].astype(f32), axis=1, keepdims=True)
        shifts += jnp.sum(weight * total, axis=0, keepdims=True)
    sums_ref[0:1] = gains
    sums_ref[1:2] = shifts
    half = made_ref.shape[0] // 2
    bit = bit_ref[0, 0]
    for part_ref, at in ((own_ref, bit), (away_ref, 1 - bit)):
        part_ref[0:half, :] = made_ref[rows_at(at, half), :].astype(bf16)
        if extras:
            lines = [sums_ref[...] + extra_refs[0][...], extra_refs[1][...]]
            lines.append(jnp.zeros((SUM_ROWS // 2 - 4, gains.shape[1]), f32))
            part_ref[half:, :] = split_rows(jnp.concatenate(lines, axis=0))


def attend_back(
    first_head, heads, extras, lens, rank, bit, qt, kt, vt, logs, weights, normed, outs, grads
):
    slots, width = normed.shape
    blocks = len(outs)
    dim = HEAD_DIM
    cols = 3 * dim * heads
    rows = cols // 2 + (SUM_ROWS if extras else 0)
    return pl.pallas_call(
        functools.partial(backward_kernel, first_head, heads, blocks, len(extras)),
        out_shape=(
            jax.ShapeDtypeStruct((slots, cols), bf16),
            jax.ShapeDtypeStruct((2, width), f32),
        )
        + (jax.ShapeDtypeStruct((rows, width), bf16),) * 2,
        in_specs=[SMEM, SMEM, SMEM]
        + [VMEM] * 8
        + [pl.BlockSpec(memory_space=pl.ANY)]
        + [VMEM] * (len(extras) + 2 * blocks),
        out_specs=(VMEM,) * 4,
        scratch_shapes=[pltpu.VMEM((heads, slots, 2 * dim), bf16)] * 3
        + [
            pltpu.VMEM((heads, 2, 2 * dim, slots), bf16),
            pltpu.VMEM((heads, 1, slots), f32),
            pltpu.VMEM((heads, dim, slots), f32),
            pltpu.VMEM((cols, width), f32),
            pltpu.VMEM((qt.shape[0] // dim, 1, slots), f32),
            pltpu.VMEM((1, slots), jnp.int32),
            pltpu.VMEM((slots, 128), jnp.int32),
            pltpu.VMEM((cols, slots), bf16),
            pltpu.VMEM((slots, width), bf16),
            pltpu.SemaphoreType.DMA,
        ],
        name="attend_back",
        compiler_params=pltpu.CompilerParams(vmem_limit_bytes=60 * 2**20),
        cost_estimate=COST,
    )(lens, rank, bit, qt, kt, vt, *logs, *weights, normed, *extras, *outs, *grads)


def plan_kernel(capacity, lens_ref, rank_ref, routes_ref, order_ref, grad_ref,
                dispatch_ref, slots_ref):
    shard = routes_ref.shape[1]
    first = rank_ref[0, 0] * shard
    ends = item_ends(lens_ref)
    chosen_row = routes_ref[...]
    chosen_col = jnp.transpose(jnp.broadcast_to(chosen_row, (128, shard)), (1, 0))[:, 0:1]
    order_row = order_ref[...]
    order_col = jnp.transpose(jnp.broadcast_to(order_row, (128, shard)), (1, 0))[:, 0:1]
    alive_row = segments_at(
        first + lax.broadcasted_iota(jnp.int32, (1, shard), 1), ends
    ) < len(ends)
    alive_col = segments_at(
        first + lax.broadcasted_iota(jnp.int32, (shard, 1), 0), ends
    ) < len(ends)
    ahead = (chosen_col == chosen_row) & (order_col < order_row) & alive_col
    ranked = jnp.sum(ahead.astype(jnp.int32), axis=0, keepdims=True)
    kept = alive_row & (ranked < capacity)
    slot = jnp.where(kept, chosen_row * capacity + ranked, -1)
    dispatch = (
        lax.broadcasted_iota(jnp.int32, dispatch_ref.shape, 0) == slot
    ).astype(f32).astype(bf16)
    dispatch_ref[...] = dispatch
    slots_ref[...] = jnp.dot(
        dispatch, grad_ref[...], preferred_element_type=f32
    ).astype(bf16)


def plan(lens, rank, routes, order, grads, capacity, experts_all):
    shard, width = grads.shape
    count = experts_all * capacity
    return pl.pallas_call(
        functools.partial(plan_kernel, capacity),
        out_shape=(
            jax.ShapeDtypeStruct((count, shard), bf16),
            jax.ShapeDtypeStruct((count, width), bf16),
        ),
        in_specs=[SMEM, SMEM, VMEM, VMEM, VMEM],
        out_specs=(VMEM, VMEM),
        name="plan",
        cost_estimate=COST,
    )(lens, rank, routes.reshape(1, -1), order, grads)


def across(left, right):
    return lax.dot_general(
        left, right, (((1,), (1,)), ((), ())), preferred_element_type=f32
    )


def middle_kernel(count, rank_ref, tokens_ref, gain_ref, bias_ref, dispatch_ref, *refs):
    head_refs, weight_refs = refs[:count], refs[count : 2 * count]
    residual_ref, rows_ref = refs[2 * count :]
    residual = tokens_ref[...].astype(f32)
    for head_ref, weight_ref in zip(head_refs, weight_refs):
        residual = residual + contract_rows(head_ref[...], weight_ref[...])
    residual_ref[...] = residual
    normed = (normalized(residual) * gain_ref[...][None] + bias_ref[...][None]).astype(bf16)
    rows_ref[...] = jnp.dot(
        dispatch_ref[...], normed, preferred_element_type=f32
    ).astype(bf16)


def middle(rank, tokens, gain, bias, dispatch, heads, weights):
    count, shard = dispatch.shape
    width = tokens.shape[1]
    fixed = lambda array: pl.BlockSpec(array.shape, lambda i, r: (0,) * array.ndim)
    small = [gain, bias, dispatch, *heads, *weights]
    return pl.pallas_call(
        functools.partial(middle_kernel, len(heads)),
        grid_spec=pltpu.PrefetchScalarGridSpec(
            num_scalar_prefetch=1,
            grid=(1,),
            in_specs=[pl.BlockSpec((shard, width), lambda i, r: (r[0], 0))]
            + [fixed(array) for array in small],
            out_specs=(
                pl.BlockSpec((shard, width), lambda i, r: (0, 0)),
                pl.BlockSpec((count, width), lambda i, r: (0, 0)),
            ),
        ),
        out_shape=(
            jax.ShapeDtypeStruct((shard, width), f32),
            jax.ShapeDtypeStruct((count, width), bf16),
        ),
        name="middle",
        cost_estimate=COST,
    )(rank, tokens, *small)


def turn_kernel(
    count, lens_ref, rank_ref, dispatch_ref, back_ref, residual_ref, cotangent_ref,
    gain_ref, *refs
):
    head_refs, weight_refs = refs[:count], refs[count : 2 * count]
    grad_ref, sums_ref, kept_ref, sent_ref = refs[2 * count : 2 * count + 4]
    part_refs = refs[2 * count + 4 :]
    shard = residual_ref.shape[0]
    grad_normed = contract_rows(dispatch_ref[...], back_ref[...])
    values = residual_ref[...]
    centred = values - jnp.mean(values, axis=-1, keepdims=True)
    inverse = lax.rsqrt(jnp.mean(centred * centred, axis=-1, keepdims=True) + EPSILON)
    normed = centred * inverse
    sums_ref[0:1] = jnp.sum(grad_normed * normed, axis=0, keepdims=True)
    sums_ref[1:2] = jnp.sum(grad_normed, axis=0, keepdims=True)
    scaled = grad_normed * gain_ref[...][None]
    grad = cotangent_ref[...].astype(f32) + inverse * (
        scaled
        - jnp.mean(scaled, axis=-1, keepdims=True)
        - normed * jnp.mean(scaled * normed, axis=-1, keepdims=True)
    )
    grad_ref[...] = grad
    low = grad.astype(bf16)
    place = rank_ref[0, 0] * shard + lax.broadcasted_iota(jnp.int32, (1, shard), 1)
    alive = place < item_ends(lens_ref)[-1]
    for weight_ref, part_ref in zip(weight_refs, part_refs):
        part_ref[...] = jnp.where(alive, across(weight_ref[...], low), 0.0).astype(bf16)
    for j, head_ref in enumerate(head_refs):
        made = jnp.dot(head_ref[...], low, preferred_element_type=f32)
        (kept_ref, sent_ref)[j % 2][j // 2] = made.astype(bf16)


def turn(lens, rank, dispatch, back, residual, cotangent, gain, heads, weights):
    shard, width = residual.shape
    cols = weights[0].shape[0]
    count = len(weights)
    return pl.pallas_call(
        functools.partial(turn_kernel, count),
        out_shape=(
            jax.ShapeDtypeStruct((shard, width), f32),
            jax.ShapeDtypeStruct((2, width), f32),
            jax.ShapeDtypeStruct((count // 2, cols, width), bf16),
            jax.ShapeDtypeStruct((count // 2, cols, width), bf16),
        )
        + (jax.ShapeDtypeStruct((cols, shard), bf16),) * count,
        in_specs=[SMEM, SMEM] + [VMEM] * (5 + 2 * count),
        out_specs=(VMEM,) * (4 + count),
        name="turn",
        cost_estimate=COST,
    )(lens, rank, dispatch, back, residual, cotangent, gain, *heads, *weights)


def output_sum_kernel(kept_ref, core_ref, first_ref, near_ref, far_ref):
    cols = near_ref.shape[0]
    total = [
        (kept_ref[j].astype(f32) + core_ref[j].astype(f32)).astype(bf16) for j in range(2)
    ]
    near_ref[...] = total[0]
    far_ref[:cols, :] = total[1]
    far_ref[cols:, :] = first_ref[...]


def output_sums(kept, core, first):
    slots, cols, width = kept.shape
    return pl.pallas_call(
        output_sum_kernel,
        out_shape=(
            jax.ShapeDtypeStruct((cols, width), bf16),
            jax.ShapeDtypeStruct((cols + first.shape[0], width), bf16),
        ),
        in_specs=[VMEM] * 3,
        out_specs=(VMEM, VMEM),
        name="output_sums",
        compiler_params=pltpu.CompilerParams(vmem_limit_bytes=52 * 2**20),
        cost_estimate=LONG,
    )(kept, core, first)


def gelu_parts(values):
    below = 0.5 + 0.5 * lax.erf(values * (0.5**0.5))
    density = jnp.exp(-0.5 * values * values) * (0.5 / jnp.pi) ** 0.5
    return values * below, below + values * density


def part_at(step, parts, rank):
    half = parts // 2
    return (2 * (step % half) + step // half) ^ rank


def activation_kernel(grad_ref, down_ref, out_ref):
    out_ref[...] = across(grad_ref[...], down_ref[...]).astype(bf16)


def activation_grads(grads, down, parts):
    count, width = grads.shape
    hidden = down.shape[0]
    size = hidden // parts
    return pl.pallas_call(
        activation_kernel,
        grid=(parts,),
        out_shape=jax.ShapeDtypeStruct((count, hidden), bf16),
        in_specs=[
            pl.BlockSpec((count, width), lambda i: (0, 0)),
            pl.BlockSpec((size, width), lambda i: (i, 0)),
        ],
        out_specs=pl.BlockSpec((count, size), lambda i: (0, i)),
        name="activation_grads",
        cost_estimate=COST,
    )(grads, down)


def expert_kernel(
    parts, rank_ref, in_ref, grad_act_ref, up_ref,
    act_kept_ref, pre_kept_ref, act_sent_ref, pre_sent_ref, mid_ref,
    grads_ref, ups_ref, acts_ref, pres_ref, sum_ref, fetched, stored,
):
    rank = rank_ref[0, 0]
    size = ups_ref.shape[2]
    half = parts // 2

    def fetch(p):
        cols = rows_at(part_at(p, parts, rank), size)
        return (
            pltpu.make_async_copy(up_ref.at[:, cols], ups_ref.at[p], fetched.at[0, p]),
            pltpu.make_async_copy(grad_act_ref.at[:, cols], grads_ref.at[p], fetched.at[1, p]),
        )

    def store(p, act_out_ref, pre_out_ref):
        cols = rows_at(p % half, size)
        return (
            pltpu.make_async_copy(acts_ref.at[p], act_out_ref.at[:, cols], stored.at[0, p]),
            pltpu.make_async_copy(pres_ref.at[p], pre_out_ref.at[:, cols], stored.at[1, p]),
        )

    for p in range(parts):
        for copy in fetch(p):
            copy.start()
    sum_ref[...] = jnp.zeros_like(sum_ref)

    def part(p, unused):
        for copy in fetch(p):
            copy.wait()
        pre = jnp.dot(in_ref[...], ups_ref[p], preferred_element_type=f32)
        act, slope = gelu_parts(pre)
        acts_ref[p] = act.astype(bf16)
        grad_pre = (grads_ref[p].astype(f32) * slope).astype(bf16)
        pres_ref[p] = grad_pre
        sum_ref[...] += across(grad_pre, ups_ref[p])

        @pl.when(p < half)
        def keep():
            for copy in store(p, act_kept_ref, pre_kept_ref):
                copy.start()

        @pl.when(p >= half)
        def send():
            for copy in store(p, act_sent_ref, pre_sent_ref):
                copy.start()

        return unused

    lax.fori_loop(0, parts, part, 0)
    mid_ref[...] = sum_ref[...].astype(bf16)
    for p in range(parts):
        outs = (act_kept_ref, pre_kept_ref) if p < half else (act_sent_ref, pre_sent_ref)
        for copy in store(p, *outs):
            copy.wait()


def expert(rank, rows, grad_act, up, parts):
    count, width = rows.shape
    hidden = up.shape[1]
    size = hidden // parts
    return pl.pallas_call(
        functools.partial(expert_kernel, parts),
        out_shape=(jax.ShapeDtypeStruct((count, hidden // 2), bf16),) * 4
        + (jax.ShapeDtypeStruct((count, width), bf16),),
        in_specs=[SMEM, VMEM, HBM, HBM],
        out_specs=(HBM,) * 4 + (VMEM,),
        scratch_shapes=[
            pltpu.VMEM((parts, count, size), grad_act.dtype),
            pltpu.VMEM((parts, width, size), bf16),
            pltpu.VMEM((parts, count, size), bf16),
            pltpu.VMEM((parts, count, size), bf16),
            pltpu.VMEM((count, width), f32),
            pltpu.SemaphoreType.DMA((2, parts)),
            pltpu.SemaphoreType.DMA((2, parts)),
        ],
        name="expert",
        compiler_params=pltpu.CompilerParams(vmem_limit_bytes=52 * 2**20),
        cost_estimate=COST,
    )(rank.reshape(1, 1), rows, grad_act, up)


def product_kernel(parts, rank_ref, kept_ref, sent_ref, down_ref, out_ref,
                   acts_ref, downs_ref, sum_ref, fetched):
    rank = rank_ref[0, 0]
    size = downs_ref.shape[1]
    half = parts // 2

    def fetch(p):
        rows = rows_at(part_at(p, parts, rank), size)
        source = kept_ref if p < half else sent_ref
        cols = slice((p % half) * size, (p % half + 1) * size)
        return (
            pltpu.make_async_copy(down_ref.at[rows, :], downs_ref.at[p], fetched.at[0, p]),
            pltpu.make_async_copy(source.at[:, cols], acts_ref.at[p], fetched.at[1, p]),
        )

    for p in range(parts):
        for copy in fetch(p):
            copy.start()
    sum_ref[...] = jnp.zeros_like(sum_ref)
    for p in range(parts):
        for copy in fetch(p):
            copy.wait()
        sum_ref[...] += jnp.dot(acts_ref[p], downs_ref[p], preferred_element_type=f32)
    out_ref[...] = sum_ref[...].astype(bf16)


def product(rank, kept, sent, down, parts):
    count = kept.shape[0]
    hidden, width = down.shape
    size = hidden // parts
    return pl.pallas_call(
        functools.partial(product_kernel, parts),
        out_shape=jax.ShapeDtypeStruct((count, width), bf16),
        in_specs=[SMEM, HBM, HBM, HBM],
        out_specs=VMEM,
        scratch_shapes=[
            pltpu.VMEM((parts, count, size), bf16),
            pltpu.VMEM((parts, size, width), bf16),
            pltpu.VMEM((count, width), f32),
            pltpu.SemaphoreType.DMA((2, parts)),
        ],
        name="product",
        compiler_params=pltpu.CompilerParams(vmem_limit_bytes=54 * 2**20),
        cost_estimate=COST,
    )(rank.reshape(1, 1), kept, sent, down)


def group_sums(refs, groups):
    dup = ddown = 0.0
    for g in range(groups):
        in_ref, grad_ref, act_ref, pre_ref = refs[4 * g : 4 * g + 4]
        dup = dup + contract_rows(in_ref[...], pre_ref[...])
        ddown = ddown + contract_rows(act_ref[...], grad_ref[...])
    return dup, ddown


def group_specs(groups, part):
    count, width = groups[0][0].shape
    size = groups[0][2].shape[1] // 2
    fixed = pl.BlockSpec((count, width), lambda i: (0, 0))
    columns = pl.BlockSpec((count, size), lambda i: (0, part))
    return [fixed, fixed, columns, columns] * len(groups)


def far_weight_kernel(groups, *refs):
    first_ref, rest_ref = refs[-2:]
    dup, ddown = group_sums(refs, groups)
    cut = first_ref.shape[0]
    first_ref[...] = dup[:cut].astype(bf16)
    rest_ref[: dup.shape[0] - cut, :] = dup[cut:].astype(bf16)
    rest_ref[dup.shape[0] - cut :, :] = ddown.astype(bf16)


def far_weights(groups):
    width = groups[0][0].shape[1]
    size = groups[0][2].shape[1] // 2
    cut = (width + size) // 4
    shapes = ((cut, size), (width + size - cut, size))
    return pl.pallas_call(
        functools.partial(far_weight_kernel, len(groups)),
        grid=(1,),
        in_specs=group_specs(groups, 1),
        out_specs=tuple(pl.BlockSpec(shape, lambda i: (0, 0)) for shape in shapes),
        out_shape=tuple(jax.ShapeDtypeStruct(shape, bf16) for shape in shapes),
        name="far_weights",
        compiler_params=pltpu.CompilerParams(vmem_limit_bytes=52 * 2**20),
        cost_estimate=COST,
    )(*[values for group in groups for values in group])


def near_weight_kernel(groups, skip, *refs):
    first_ref, rest_ref, up_ref, down_ref = refs[-4:]
    dup, ddown = group_sums(refs, groups)
    cut = first_ref.shape[0] - skip
    down_at = dup.shape[0] - cut
    up_ref[:cut, :] = dup[:cut] + first_ref[skip:, :].astype(f32)
    up_ref[cut:, :] = dup[cut:] + rest_ref[:down_at, :].astype(f32)
    down_ref[...] = ddown + rest_ref[down_at:, :].astype(f32)


def near_weights(groups, first, rest):
    width = groups[0][0].shape[1]
    size = groups[0][2].shape[1] // 2
    skip = first.shape[0] + rest.shape[0] - width - size
    whole = lambda shape: pl.BlockSpec(shape, lambda i: (0, 0))
    return pl.pallas_call(
        functools.partial(near_weight_kernel, len(groups), skip),
        grid=(1,),
        in_specs=group_specs(groups, 0) + [whole(first.shape), whole(rest.shape)],
        out_specs=(whole((width, size)), whole((size, width))),
        out_shape=(
            jax.ShapeDtypeStruct((width, size), f32),
            jax.ShapeDtypeStruct((size, width), f32),
        ),
        name="near_weights",
        compiler_params=pltpu.CompilerParams(vmem_limit_bytes=52 * 2**20),
        cost_estimate=COST,
    )(*[values for group in groups for values in group], first, rest)


def input_grad_kernel(groups, qw_ref, kw_ref, vw_ref, *refs):
    joint_refs = refs[: len(groups)]
    kept_ref, sent_ref, turned_ref = refs[len(groups) :]
    step = pl.program_id(0)

    @pl.when(step == 0)
    def stack():
        start = 0
        for first_head, heads in groups:
            for at, weight_ref, first, size in stacked_parts(
                first_head, heads, qw_ref, kw_ref, vw_ref
            ):
                turned_ref[start + at : start + at + size, :] = weight_ref[
                    first : first + size, :
                ]
            start += 3 * heads * HEAD_DIM

    total = 0.0
    at = 0
    for joint_ref in joint_refs:
        rows = slice(at, at + joint_ref.shape[1])
        total = total + jnp.dot(
            joint_ref[...], turned_ref[rows, :], preferred_element_type=f32
        )
        at += joint_ref.shape[1]

    @pl.when(step % 2 == 0)
    def keep():
        kept_ref[0] = total.astype(bf16)

    @pl.when(step % 2 == 1)
    def send():
        sent_ref[0] = total.astype(bf16)


def input_grad(groups, weights, joints, first, count, size):
    cols, width = weights[0].shape
    fixed = pl.BlockSpec((cols, width), lambda i: (0, 0))
    return pl.pallas_call(
        functools.partial(input_grad_kernel, groups),
        grid=(count,),
        out_shape=(jax.ShapeDtypeStruct((count // 2, size, width), bf16),) * 2,
        in_specs=[fixed] * 3
        + [
            pl.BlockSpec((size, joint.shape[1]), lambda i: (first + i, 0))
            for joint in joints
        ],
        out_specs=(pl.BlockSpec((1, size, width), lambda i: (i // 2, 0, 0)),) * 2,
        scratch_shapes=[pltpu.VMEM((3 * cols, width), bf16)],
        name="input_grad",
        compiler_params=pltpu.CompilerParams(vmem_limit_bytes=10 * 2**20),
        cost_estimate=COST,
    )(*weights, *joints)


def close_kernel(
    rank_ref, tokens_ref, gain_ref, grad_ref, residual_ref, dispatch_ref, back_ref, *refs
):
    *part_refs, out_ref, block_ref = refs
    block_ref[...] = residual_ref[...] + contract_rows(dispatch_ref[...], back_ref[...])
    grad_in = 0.0
    for part_ref in part_refs:
        grad_in = grad_in + part_ref[...].reshape(out_ref.shape).astype(f32)
    values = tokens_ref[...].astype(f32)
    centred = values - jnp.mean(values, axis=-1, keepdims=True)
    inverse = lax.rsqrt(jnp.mean(centred * centred, axis=-1, keepdims=True) + EPSILON)
    normed = centred * inverse
    scaled = grad_in * gain_ref[...][None]
    out_ref[...] = grad_ref[...] + inverse * (
        scaled
        - jnp.mean(scaled, axis=-1, keepdims=True)
        - normed * jnp.mean(scaled * normed, axis=-1, keepdims=True)
    )


def close(rank, tokens, gain, grad, residual, dispatch, back, parts):
    shard, width = grad.shape
    count = dispatch.shape[0]
    size = shard // 2
    rows = pl.BlockSpec((size, width), lambda i, r: (i, 0))
    return pl.pallas_call(
        close_kernel,
        grid_spec=pltpu.PrefetchScalarGridSpec(
            num_scalar_prefetch=1,
            grid=(2,),
            in_specs=[
                pl.BlockSpec((size, width), lambda i, r: (2 * r[0] + i, 0)),
                pl.BlockSpec((width,), lambda i, r: (0,)),
                rows,
                rows,
                pl.BlockSpec((count, size), lambda i, r: (0, i)),
                pl.BlockSpec((count, width), lambda i, r: (0, 0)),
            ]
            + [pl.BlockSpec((1, size, width), lambda i, r: (0, i, 0))] * len(parts),
            out_specs=(rows, rows),
        ),
        out_shape=(jax.ShapeDtypeStruct((shard, width), f32),) * 2,
        name="close",
        compiler_params=pltpu.CompilerParams(vmem_limit_bytes=16 * 2**20),
        cost_estimate=COST,
    )(rank, tokens, gain, grad, residual, dispatch, back, *parts)


def add_low_kernel(a_ref, b_ref, out_ref):
    out_ref[...] = (a_ref[...].astype(f32) + b_ref[...].astype(f32)).astype(bf16)


def add_low(a, b):
    block = pl.BlockSpec(a.shape, lambda i: (0,) * a.ndim)
    return pl.pallas_call(
        add_low_kernel,
        grid=(1,),
        out_shape=jax.ShapeDtypeStruct(a.shape, bf16),
        in_specs=[block, block],
        out_specs=block,
        name="add_low",
        compiler_params=pltpu.CompilerParams(vmem_limit_bytes=6 * 2**20),
        cost_estimate=COST,
    )(a, b)


def after(value, *others):
    return lax.optimization_barrier((value, *others))[0]


def tie(*values):
    return lax.optimization_barrier(values)


def finish_kernel(groups, bit_ref, *refs):
    pieces, refs = refs[: 2 * len(groups)], refs[2 * len(groups) :]
    query_ref, key_ref, value_ref = refs[:3]
    bit = bit_ref[0, 0]
    for g, ((first_head, heads), whole_ref) in enumerate(zip(groups, refs[3:])):
        half = whole_ref.shape[0] // 2
        for piece_ref, at in ((pieces[2 * g], bit), (pieces[2 * g + 1], 1 - bit)):
            whole_ref[rows_at(at, half), :] = piece_ref[0:half, :].astype(f32)
        for at, target_ref, first, size in stacked_parts(
            first_head, heads, query_ref, key_ref, value_ref
        ):
            target_ref[first : first + size, :] = whole_ref[at : at + size, :]


def finish(groups, bit, pieces):
    width = pieces[0].shape[1]
    cols = sum(heads for first_head, heads in groups) * HEAD_DIM
    return pl.pallas_call(
        functools.partial(finish_kernel, groups),
        out_shape=(jax.ShapeDtypeStruct((cols, width), f32),) * 3,
        in_specs=[SMEM] + [VMEM] * len(pieces),
        out_specs=(VMEM,) * 3,
        scratch_shapes=[
            pltpu.VMEM((3 * heads * HEAD_DIM, width), f32) for first_head, heads in groups
        ],
        name="finish",
        compiler_params=pltpu.CompilerParams(vmem_limit_bytes=10 * 2**20),
        cost_estimate=COST,
    )(bit, *pieces)


def on_device(
    tokens,
    first_gain,
    first_bias,
    query_weight,
    key_weight,
    value_weight,
    output_weight,
    second_gain,
    second_bias,
    expert_up,
    expert_down,
    item_lengths,
    routes,
    slot_order,
    cotangent,
):
    slots_all, width = tokens.shape
    members = lax.axis_size("tensor")
    shard_rows = slots_all // members
    rank = lax.axis_index("tensor")
    sources = lax.axis_size("dp")
    experts_all = sources * expert_up.shape[0]
    capacity = shard_rows // experts_all
    head_cols = query_weight.shape[1]
    heads = head_cols // HEAD_DIM
    up_matrix = expert_up[0]
    down_matrix = expert_down[0]
    rank_cell = rank.astype(jnp.int32).reshape(1, 1)

    def exchange(rows):
        return lax.all_to_all(
            rows.reshape(sources, -1, width), "dp", split_axis=0, concat_axis=0, tiled=True
        ).reshape(-1, width)

    qw, kw, vw = query_weight.T, key_weight.T, value_weight.T

    dispatch, grad_slots = plan(
        item_lengths, rank_cell, routes, slot_order, cotangent, capacity, experts_all
    )
    flat_grad = exchange(grad_slots)
    tokens, grad_slots = tie(tokens, grad_slots)
    normed_in, qt, kt, vt = project(
        rank_cell[0], tokens, first_gain, first_bias, qw, kw, vw, members
    )
    outputs = [output_weight] + [
        swap(output_weight, "tensor", k) for k in range(1, members)
    ]
    far = members // 2
    *far_heads, far_logs = attend(
        item_lengths, rank_cell, qt, kt, vt, members, far, members - far
    )
    far_heads, kt = tie(far_heads, kt)
    far_arrived = [swap(far_heads[j - far], "tensor", j) for j in range(far, members)]
    *near_heads, near_logs = attend(item_lengths, rank_cell, qt, kt, vt, members, 0, far)
    near_heads, far_arrived, outputs = tie(near_heads, far_arrived, outputs)
    own_heads = near_heads + far_heads
    logs = (near_logs, far_logs)
    all_heads = (
        near_heads[:1]
        + [swap(near_heads[j], "tensor", j) for j in range(1, far)]
        + far_arrived
    )
    residual, outgoing = middle(
        rank_cell[0], tokens, second_gain, second_bias, dispatch, all_heads, outputs
    )
    flat_in = exchange(outgoing)

    flat_grad, outgoing = tie(flat_grad, outgoing)
    grad_act = activation_grads(flat_grad, down_matrix, members)
    near_grads = swap(flat_grad, "tensor", 1)
    flat_in, grad_act, near_grads = tie(flat_in, grad_act, near_grads)
    near_rows = swap(flat_in, "tensor", 1)
    act, grad_pre, act_sent, pre_sent, grad_mid = expert(
        rank_cell[0], flat_in, grad_act, up_matrix, members
    )
    grad_mid, act, near_rows = tie(grad_mid, act, near_rows)
    grad_back = exchange(grad_mid)

    act, act_sent, pre_sent, grad_mid = tie(act, act_sent, pre_sent, grad_mid)
    near_act = swap(act_sent, "tensor", 1)
    near_pre = swap(pre_sent, "tensor", 1)
    made = product(rank_cell[0], act, act_sent, down_matrix, members)
    made, near_act, near_pre = tie(made, near_act, near_pre)
    expert_groups = [
        (flat_in, flat_grad, act, grad_pre), (near_rows, near_grads, near_act, near_pre)
    ]
    expert_far = list(far_weights(expert_groups))
    grad_back, made, expert_far = tie(grad_back, made, expert_far)

    steps = steps_of(members)
    grad_res, sums_second, kept, sent, *grad_heads = turn(
        item_lengths, rank_cell, dispatch, grad_back, residual, cotangent,
        second_gain, all_heads, outputs,
    )
    grad_parts = [grad_heads[0]] + [
        swap(grad_heads[j], "tensor", j) for j in range(1, members)
    ]
    output_near, output_far = output_sums(kept, swap(sent, "tensor", 1), expert_far[0])
    made, grad_heads = tie(made, grad_heads)
    returned = exchange(made)
    grad_parts, output_near, output_far = tie(grad_parts, output_near, output_far)

    bit_cell = (lax.axis_index("dp") & 1).astype(jnp.int32).reshape(1, 1)
    weights = (qw, kw, vw)
    dp_steps = steps_of(sources)
    back = functools.partial(
        attend_back, lens=item_lengths, rank=rank_cell, bit=bit_cell, qt=qt, kt=kt, vt=vt,
        logs=logs, weights=weights, normed=normed_in, outs=own_heads,
    )
    groups = ((0, heads - 1), (heads - 1, 1))
    joint_a, sums_a, own_a, away_a = back(*groups[0], extras=(), grads=grad_parts)
    output_got = swap(output_far, "tensor", 2)
    joint_a, own_a, away_a, output_got, grad_parts, expert_rest, returned = tie(
        joint_a, own_a, away_a, output_got, grad_parts, expert_far[1], returned
    )
    expert_got = swap(expert_rest, "tensor", 2)
    output_sum = add_low(output_near, output_got)
    own_a = add_low(own_a, swap(away_a, "dp", 1))
    output_sum = add_low(output_sum, swap(output_sum, "dp", dp_steps[-1]))
    joint_b, unused, own_b, away_b = back(
        *groups[1], extras=(sums_a, sums_second), grads=grad_parts
    )
    joint_b, own_a, own_b, away_b, output_sum = tie(
        joint_b, own_a, own_b, away_b, output_sum
    )

    far_kept, far_sent = input_grad(
        groups, weights, (joint_a, joint_b), far, members - far, shard_rows
    )
    got_a = swap(own_a, "dp", dp_steps[1])
    got_b = swap(away_b, "dp", 1)
    joint_b, got_a, got_b = tie(joint_b, got_a, got_b)
    near_kept, near_sent = input_grad(
        groups, weights, (joint_a, joint_b), 0, far, shard_rows
    )
    own_b = add_parts(own_b, got_b)
    far_kept = add_low(far_kept, swap(far_sent, "tensor", 1))
    own_a = add_low(own_a, got_a)
    far_kept, own_b, output_sum, own_a = tie(far_kept, own_b, output_sum, own_a)
    near_core = swap(near_sent, "tensor", 1)
    near_far = swap(far_kept, "tensor", 2)
    for step in dp_steps[1:]:
        if step != dp_steps[1]:
            own_a = add_low(own_a, swap(own_a, "dp", step))
        own_b = add_parts(own_b, swap(own_b, "dp", step))
        if step == dp_steps[1]:
            own_b, expert_got = tie(own_b, expert_got)
    up_grad, down_grad = near_weights(expert_groups, output_got, expert_got)
    own_b, up_grad, down_grad, near_far = tie(own_b, up_grad, down_grad, near_far)
    pieces = (own_a, swap(own_a, "dp", 1), own_b, swap(own_b, "dp", 1))
    token_grad, block_out = close(
        rank_cell[0], tokens, first_gain, grad_res, residual, dispatch, returned,
        (near_kept, near_core, near_far),
    )
    norm_sums = own_b[-SUM_ROWS:].astype(f32)
    norm_sums = norm_sums[: SUM_ROWS // 2] + norm_sums[SUM_ROWS // 2 :]
    for step in steps:
        norm_sums = norm_sums + swap(norm_sums, "tensor", step)
    for step in dp_steps[:-1]:
        output_sum = add_low(output_sum, swap(output_sum, "dp", step))
    output_sum = after(output_sum, token_grad)
    query_grad, key_grad, value_grad = finish(groups, bit_cell, pieces)
    return (
        block_out,
        token_grad,
        (norm_sums[0] - first_bias * norm_sums[1]) / first_gain,
        norm_sums[1],
        query_grad.T,
        key_grad.T,
        value_grad.T,
        output_sum.astype(f32),
        norm_sums[2],
        norm_sums[3],
        up_grad[None],
        down_grad[None],
    )


def solution(mesh):
    in_specs = (
        P("dp", None),
        P(),
        P(),
        P(None, "tensor"),
        P(None, "tensor"),
        P(None, "tensor"),
        P("tensor", None),
        P(),
        P(),
        P("dp", None, None),
        P("dp", None, None),
        P("dp", None),
        P(("dp", "tensor"), None),
        P(("dp", "tensor"), None),
        P(("dp", "tensor"), None),
    )
    out_specs = (
        P(("dp", "tensor"), None),
        P(("dp", "tensor"), None),
        P(),
        P(),
        P(None, "tensor"),
        P(None, "tensor"),
        P(None, "tensor"),
        P("tensor", None),
        P(),
        P(),
        P("dp", None, "tensor"),
        P("dp", "tensor", None),
    )
    return jax.shard_map(
        on_device, mesh=mesh, in_specs=in_specs, out_specs=out_specs, check_vma=False
    )
```

```python
import functools

import jax
import jax.numpy as jnp
from jax import lax
from jax.experimental import pallas as pl
from jax.experimental.pallas import tpu as pltpu
from jax.sharding import PartitionSpec as P

HEAD_DIM = 64
EPSILON = 1e-05
NEGATIVE = -1e30
f32 = jnp.float32
bf16 = jnp.bfloat16
VMEM = pl.BlockSpec(memory_space=pltpu.VMEM)
HBM = pl.BlockSpec(memory_space=pltpu.MemorySpace.HBM)
SMEM = pl.BlockSpec(memory_space=pltpu.SMEM)
SUM_ROWS = 16
COST = pl.CostEstimate(flops=2**20, bytes_accessed=2**20, transcendentals=0)
LONG = pl.CostEstimate(flops=2**34, bytes_accessed=2**24, transcendentals=0)


def layer_norm(values, gain, shift):
    average = jnp.mean(values, axis=-1, keepdims=True)
    centred = values - average
    variance = jnp.mean(centred * centred, axis=-1, keepdims=True)
    return centred * lax.rsqrt(variance + EPSILON) * gain + shift


def contract_rows(left, right):
    return lax.dot_general(
        left, right, (((0,), (0,)), ((), ())), preferred_element_type=f32
    )


def swap(values, axis, step):
    count = lax.axis_size(axis)
    return lax.ppermute(values, axis, [(i, i ^ step) for i in range(count)])


def steps_of(count):
    steps = []
    step = 1
    while step < count:
        steps.append(step)
        step *= 2
    return steps


def normalized(values):
    average = jnp.mean(values, axis=-1, keepdims=True)
    centred = values - average
    variance = jnp.mean(centred * centred, axis=-1, keepdims=True)
    return centred * lax.rsqrt(variance + EPSILON)


def project_kernel(
    rank_ref, tokens_ref, gain_ref, bias_ref, qw_ref, kw_ref, vw_ref,
    normed_ref, qt_ref, kt_ref, vt_ref,
):
    values = tokens_ref[...].astype(f32)
    normed = (normalized(values) * gain_ref[...][None] + bias_ref[...][None]).astype(bf16)
    normed_ref[...] = normed
    for weight_ref, out_ref, factor in (
        (qw_ref, qt_ref, HEAD_DIM ** (-0.5)), (kw_ref, kt_ref, None), (vw_ref, vt_ref, None)
    ):
        made = lax.dot_general(
            weight_ref[...], normed, (((1,), (1,)), ((), ())), preferred_element_type=f32
        ).astype(bf16)
        if factor is not None:
            made = made * jnp.asarray(factor, bf16)
        out_ref[...] = made


def project(rank, tokens, gain, bias, qw, kw, vw, blocks):
    slots, width = tokens.shape
    cols = qw.shape[0]
    size = slots // blocks
    fixed = lambda i, r: (0, 0)
    line = pl.BlockSpec((width,), lambda i, r: (0,))
    return pl.pallas_call(
        project_kernel,
        grid_spec=pltpu.PrefetchScalarGridSpec(
            num_scalar_prefetch=1,
            grid=(blocks,),
            in_specs=[
                pl.BlockSpec((size, width), lambda i, r: (i ^ r[0], 0)),
                line,
                line,
                pl.BlockSpec((cols, width), fixed),
                pl.BlockSpec((cols, width), fixed),
                pl.BlockSpec((cols, width), fixed),
            ],
            out_specs=(
                pl.BlockSpec((size, width), lambda i, r: (i, 0)),
                pl.BlockSpec((cols, size), lambda i, r: (0, i)),
                pl.BlockSpec((cols, size), lambda i, r: (0, i)),
                pl.BlockSpec((cols, size), lambda i, r: (0, i)),
            ),
        ),
        out_shape=(jax.ShapeDtypeStruct((slots, width), bf16),)
        + (jax.ShapeDtypeStruct((cols, slots), bf16),) * 3,
        name="project",
        cost_estimate=COST,
    )(rank, tokens, gain, bias, qw, kw, vw)


def item_ends(lens_ref):
    ends = []
    total = jnp.int32(0)
    for i in range(lens_ref.shape[1]):
        total = total + lens_ref[0, i]
        ends.append(total)
    return ends


def segments_at(place, ends):
    segment = jnp.zeros_like(place)
    for end in ends:
        segment = segment + (place >= end).astype(jnp.int32)
    return segment


def block_span(first, size, unit, ends):
    last = jnp.minimum(first + size, ends[-1]) - 1
    low = jnp.int32(0)
    high = ends[-1]
    for end in ends:
        low = jnp.where(first >= end, end, low)
    for end in reversed(ends):
        high = jnp.where(last < end, end, high)
    empty = first >= ends[-1]
    low_block = jnp.where(empty, 0, low // unit)
    high_block = jnp.where(empty, 0, (high + unit - 1) // unit)
    return low_block, high_block


def rows_at(block, size):
    return pl.ds(pl.multiple_of(block * size, size), size)


def fill_segments(row_ref, col_ref, shard, rank, ends):
    slots = row_ref.shape[1]
    at = lax.broadcasted_iota(jnp.int32, (1, slots), 1)
    place = ((at // shard) ^ rank) * shard + at % shard
    segments = segments_at(place, ends)
    row_ref[...] = segments
    col_ref[...] = jnp.transpose(jnp.broadcast_to(segments, (128, slots)), (1, 0))


def block_bias(row_ref, col_ref, rows, cols):
    return jnp.where(col_ref[rows, 0:1] == row_ref[:, cols], 0.0, NEGATIVE)


def lane_masked(values, head):
    lane = lax.broadcasted_iota(jnp.int32, values.shape, 1)
    inside = (lane >= head * HEAD_DIM) & (lane < (head + 1) * HEAD_DIM)
    return jnp.where(inside, values, jnp.zeros_like(values))


def forward_kernel(
    first, blocks, lens_ref, rank_ref, qt_ref, kt_ref, vt_ref, *refs
):
    *out_refs, log_ref, masked_ref, out_ref, row_ref, col_ref, score_ref = refs
    count, width, size = out_ref.shape
    heads = width // HEAD_DIM
    shard = size
    rank = rank_ref[0, 0]
    ends = item_ends(lens_ref)
    fill_segments(row_ref, col_ref, shard, rank, ends)
    keys = jnp.transpose(kt_ref[...], (1, 0))
    for h in range(heads):
        masked_ref[h] = lane_masked(keys, h)

    def query_block(b, unused):
        at = first + b
        i = at ^ rank
        cols = rows_at(at, size)
        queries = qt_ref[:, cols]

        def score_block(j, carry):
            rows = rows_at(j ^ rank, shard)
            bias = block_bias(row_ref, col_ref, rows, cols)
            result = []
            for h in range(heads):
                scores = jnp.dot(
                    masked_ref[h, rows, :], queries, preferred_element_type=f32
                )
                scores = scores + bias
                score_ref[h, rows_at(j, shard), :] = scores
                part = jnp.max(scores.reshape(-1, 8, size), axis=0)
                result.append(jnp.maximum(carry[h], part))
            return tuple(result)

        low, high = block_span(i * size, size, shard, ends)
        peaks = lax.fori_loop(
            low, high, score_block, (jnp.full((8, size), NEGATIVE, f32),) * heads
        )
        peaks = [jnp.max(peak, axis=0, keepdims=True) for peak in peaks]

        def key_block(j, carry):
            rows = rows_at(j ^ rank, shard)
            result = []
            for h in range(heads):
                summed, total = carry[h]
                soft = jnp.exp(score_ref[h, rows_at(j, shard), :] - peaks[h])
                summed = summed + jnp.sum(soft.reshape(-1, 8, size), axis=0)
                total = total + jnp.dot(
                    vt_ref[pl.ds(h * HEAD_DIM, HEAD_DIM), rows],
                    soft.astype(bf16),
                    preferred_element_type=f32,
                )
                result.append((summed, total))
            return tuple(result)

        start = ((jnp.zeros((8, size), f32), jnp.zeros((HEAD_DIM, size), f32)),) * heads
        done = lax.fori_loop(low, high, key_block, start)
        live = row_ref[:, cols] < len(ends)
        for h in range(heads):
            summed, total = done[h]
            summed = jnp.sum(summed, axis=0, keepdims=True)
            highest = peaks[h]
            summed = jnp.where(live, summed, 1.0)
            result = jnp.where(live, total / summed, 0.0).astype(bf16)
            logs = jnp.where(live, highest + jnp.log(summed), -NEGATIVE)
            out_ref[b, pl.ds(h * HEAD_DIM, HEAD_DIM), :] = result
            log_ref[h, :, rows_at(b, size)] = logs
        return unused

    lax.fori_loop(0, count, query_block, 0)
    for b in range(count):
        out_refs[b][...] = out_ref[b]


def attend(lens, rank, qt, kt, vt, blocks, first, count):
    width, slots = qt.shape
    size = slots // blocks
    heads = width // HEAD_DIM
    return pl.pallas_call(
        functools.partial(forward_kernel, first, blocks),
        out_shape=(jax.ShapeDtypeStruct((width, size), bf16),) * count
        + (jax.ShapeDtypeStruct((heads, 1, count * size), f32),),
        in_specs=[SMEM, SMEM, VMEM, VMEM, VMEM],
        out_specs=(VMEM,) * (count + 1),
        scratch_shapes=[
            pltpu.VMEM((heads, slots, width), bf16),
            pltpu.VMEM((count, width, size), bf16),
            pltpu.VMEM((1, slots), jnp.int32),
            pltpu.VMEM((slots, 128), jnp.int32),
            pltpu.VMEM((heads, slots, size), f32),
        ],
        name="attend",
        compiler_params=pltpu.CompilerParams(vmem_limit_bytes=60 * 2**20),
        cost_estimate=COST,
    )(lens, rank, qt, kt, vt)


def split_rows(values):
    high = values.astype(bf16)
    return jnp.concatenate([high, (values - high.astype(f32)).astype(bf16)], axis=0)


def add_kernel(a_ref, b_ref, out_ref):
    half = out_ref.shape[0] - SUM_ROWS
    line = SUM_ROWS // 2
    total = a_ref[...].astype(f32) + b_ref[...].astype(f32)
    out_ref[:half, :] = total[:half].astype(bf16)
    out_ref[half:, :] = split_rows(total[half : half + line] + total[half + line :])


def add_parts(a, b):
    return pl.pallas_call(
        add_kernel,
        out_shape=jax.ShapeDtypeStruct(a.shape, bf16),
        in_specs=[VMEM, VMEM],
        out_specs=VMEM,
        name="add_parts",
        compiler_params=pltpu.CompilerParams(vmem_limit_bytes=5 * 2**20),
        cost_estimate=COST,
    )(a, b)


def stacked_parts(first_head, heads, query, key, value):
    dim = HEAD_DIM
    parts = []
    for n in range(heads):
        first = (first_head + n) * dim
        parts += [(2 * n * dim, key, first, dim), ((2 * n + 1) * dim, value, first, dim)]
    return parts + [(2 * heads * dim, query, first_head * dim, heads * dim)]


def backward_kernel(
    first_head, heads, blocks, extras, lens_ref, rank_ref, bit_ref, qt_ref, kt_ref, vt_ref,
    near_ref, far_ref, qw_ref, kw_ref, vw_ref, normed_ref, *rest
):
    extra_refs, rest = rest[:extras], rest[extras:]
    width, slots = qt_ref.shape
    shard = slots // blocks
    dim = HEAD_DIM
    out_refs, grad_refs = rest[:blocks], rest[blocks : 2 * blocks]
    joint_ref, sums_ref, own_ref, away_ref = rest[2 * blocks : 2 * blocks + 4]
    kv_ref, q0_ref, og_ref, right_ref, inner_ref, dq_ref, made_ref = rest[-13:-6]
    log_ref = rest[-6]
    row_ref, col_ref = rest[-5:-3]
    turned_ref, rows_ref, copied = rest[-3:]
    fetch = pltpu.make_async_copy(normed_ref, rows_ref, copied)
    fetch.start()
    unit = shard // 2
    rank = rank_ref[0, 0]
    ends = item_ends(lens_ref)
    fill_segments(row_ref, col_ref, shard, rank, ends)
    near = near_ref.shape[2]
    log_ref[:, :, :near] = near_ref[...]
    log_ref[:, :, near:] = far_ref[...]
    zero = jnp.zeros((dim, slots), bf16)
    for n in range(heads):
        part = slice((first_head + n) * dim, (first_head + n + 1) * dim)
        both = jnp.concatenate([kt_ref[part, :], vt_ref[part, :]], axis=0)
        kv_ref[n] = jnp.transpose(both, (1, 0))
        padded = jnp.concatenate([qt_ref[part, :], zero], axis=0)
        q0_ref[n] = jnp.transpose(padded, (1, 0))
        right_ref[n, 0] = padded
        for b in range(blocks):
            grad = grad_refs[b][part, :]
            cols = slice(b * shard, (b + 1) * shard)
            padded = jnp.concatenate([zero[:, :shard], grad], axis=0)
            og_ref[n, cols, :] = jnp.transpose(padded, (1, 0))
            right_ref[n, 1, :, cols] = padded
            inner_ref[n, :, cols] = jnp.sum(
                out_refs[b][part, :].astype(f32) * grad.astype(f32), axis=0, keepdims=True
            )
    dq_ref[...] = jnp.zeros_like(dq_ref)

    def key_block(j, unused):
        at_key = ((j // 2) ^ rank) * 2 + j % 2
        rows = rows_at(at_key, unit)

        def query_block(i, totals):
            at = i ^ rank
            cols = rows_at(at, shard)
            same = col_ref[rows, 0:1] == row_ref[:, cols]
            result = []
            for n in range(heads):
                head = first_head + n
                kv = kv_ref[n, rows, :]
                scores = jnp.dot(kv, right_ref[n, 0, :, cols], preferred_element_type=f32)
                grad_soft = jnp.dot(kv, right_ref[n, 1, :, cols], preferred_element_type=f32)
                soft = jnp.where(same, jnp.exp(scores - log_ref[head, :, cols]), 0.0)
                grad_scores = (soft * (grad_soft - inner_ref[n, :, cols])).astype(bf16)
                total = totals[n] + jnp.dot(
                    soft.astype(bf16), og_ref[n, cols, :], preferred_element_type=f32
                )
                total = total + jnp.dot(
                    grad_scores, q0_ref[n, cols, :], preferred_element_type=f32
                )
                dq_ref[n, :, cols] += jnp.dot(
                    kt_ref[pl.ds(head * dim, dim), rows], grad_scores,
                    preferred_element_type=f32,
                )
                result.append(total)
            return tuple(result)

        low, high = block_span(j * unit, unit, shard, ends)
        start = (jnp.zeros((unit, 2 * dim), f32),) * heads
        totals = lax.fori_loop(low, high, query_block, start)
        for n in range(heads):
            part = slice(2 * dim * n, 2 * dim * (n + 1))
            total = totals[n].astype(bf16)
            joint_ref[rows, part] = total
            turned_ref[part, rows] = jnp.transpose(total, (1, 0))
        return unused

    lax.fori_loop(0, 2 * blocks, key_block, 0)
    dq = (dq_ref[...] * dim ** (-0.5)).astype(bf16).reshape(heads * dim, slots)
    turned_ref[2 * dim * heads :, :] = dq
    joint_ref[:, 2 * dim * heads :] = jnp.transpose(dq, (1, 0))
    fetch.wait()
    made_ref[...] = jnp.dot(turned_ref[...], rows_ref[...], preferred_element_type=f32)
    gains = jnp.zeros((1, rows_ref.shape[1]), f32)
    shifts = jnp.zeros((1, rows_ref.shape[1]), f32)
    for at, weight_ref, first, size in stacked_parts(
        first_head, heads, qw_ref, kw_ref, vw_ref
    ):
        weight = weight_ref[first : first + size, :].astype(f32)
        gains += jnp.sum(weight * made_ref[at : at + size, :], axis=0, keepdims=True)
        total = jnp.sum(turned_ref[at : at + size, :].astype(f32), axis=1, keepdims=True)
        shifts += jnp.sum(weight * total, axis=0, keepdims=True)
    sums_ref[0:1] = gains
    sums_ref[1:2] = shifts
    half = made_ref.shape[0] // 2
    bit = bit_ref[0, 0]
    for part_ref, at in ((own_ref, bit), (away_ref, 1 - bit)):
        part_ref[0:half, :] = made_ref[rows_at(at, half), :].astype(bf16)
        if extras:
            lines = [sums_ref[...] + extra_refs[0][...], extra_refs[1][...]]
            lines.append(jnp.zeros((SUM_ROWS // 2 - 4, gains.shape[1]), f32))
            part_ref[half:, :] = split_rows(jnp.concatenate(lines, axis=0))


def attend_back(
    first_head, heads, extras, lens, rank, bit, qt, kt, vt, logs, weights, normed, outs, grads
):
    slots, width = normed.shape
    blocks = len(outs)
    dim = HEAD_DIM
    cols = 3 * dim * heads
    rows = cols // 2 + (SUM_ROWS if extras else 0)
    return pl.pallas_call(
        functools.partial(backward_kernel, first_head, heads, blocks, len(extras)),
        out_shape=(
            jax.ShapeDtypeStruct((slots, cols), bf16),
            jax.ShapeDtypeStruct((2, width), f32),
        )
        + (jax.ShapeDtypeStruct((rows, width), bf16),) * 2,
        in_specs=[SMEM, SMEM, SMEM]
        + [VMEM] * 8
        + [pl.BlockSpec(memory_space=pl.ANY)]
        + [VMEM] * (len(extras) + 2 * blocks),
        out_specs=(VMEM,) * 4,
        scratch_shapes=[pltpu.VMEM((heads, slots, 2 * dim), bf16)] * 3
        + [
            pltpu.VMEM((heads, 2, 2 * dim, slots), bf16),
            pltpu.VMEM((heads, 1, slots), f32),
            pltpu.VMEM((heads, dim, slots), f32),
            pltpu.VMEM((cols, width), f32),
            pltpu.VMEM((qt.shape[0] // dim, 1, slots), f32),
            pltpu.VMEM((1, slots), jnp.int32),
            pltpu.VMEM((slots, 128), jnp.int32),
            pltpu.VMEM((cols, slots), bf16),
            pltpu.VMEM((slots, width), bf16),
            pltpu.SemaphoreType.DMA,
        ],
        name="attend_back",
        compiler_params=pltpu.CompilerParams(vmem_limit_bytes=60 * 2**20),
        cost_estimate=COST,
    )(lens, rank, bit, qt, kt, vt, *logs, *weights, normed, *extras, *outs, *grads)


def plan_kernel(capacity, lens_ref, rank_ref, routes_ref, order_ref, grad_ref,
                dispatch_ref, slots_ref):
    shard = routes_ref.shape[1]
    first = rank_ref[0, 0] * shard
    ends = item_ends(lens_ref)
    chosen_row = routes_ref[...]
    chosen_col = jnp.transpose(jnp.broadcast_to(chosen_row, (128, shard)), (1, 0))[:, 0:1]
    order_row = order_ref[...]
    order_col = jnp.transpose(jnp.broadcast_to(order_row, (128, shard)), (1, 0))[:, 0:1]
    alive_row = segments_at(
        first + lax.broadcasted_iota(jnp.int32, (1, shard), 1), ends
    ) < len(ends)
    alive_col = segments_at(
        first + lax.broadcasted_iota(jnp.int32, (shard, 1), 0), ends
    ) < len(ends)
    ahead = (chosen_col == chosen_row) & (order_col < order_row) & alive_col
    ranked = jnp.sum(ahead.astype(jnp.int32), axis=0, keepdims=True)
    kept = alive_row & (ranked < capacity)
    slot = jnp.where(kept, chosen_row * capacity + ranked, -1)
    dispatch = (
        lax.broadcasted_iota(jnp.int32, dispatch_ref.shape, 0) == slot
    ).astype(f32).astype(bf16)
    dispatch_ref[...] = dispatch
    slots_ref[...] = jnp.dot(
        dispatch, grad_ref[...], preferred_element_type=f32
    ).astype(bf16)


def plan(lens, rank, routes, order, grads, capacity, experts_all):
    shard, width = grads.shape
    count = experts_all * capacity
    return pl.pallas_call(
        functools.partial(plan_kernel, capacity),
        out_shape=(
            jax.ShapeDtypeStruct((count, shard), bf16),
            jax.ShapeDtypeStruct((count, width), bf16),
        ),
        in_specs=[SMEM, SMEM, VMEM, VMEM, VMEM],
        out_specs=(VMEM, VMEM),
        name="plan",
        cost_estimate=COST,
    )(lens, rank, routes.reshape(1, -1), order, grads)


def across(left, right):
    return lax.dot_general(
        left, right, (((1,), (1,)), ((), ())), preferred_element_type=f32
    )


def middle_kernel(count, rank_ref, tokens_ref, gain_ref, bias_ref, dispatch_ref, *refs):
    head_refs, weight_refs = refs[:count], refs[count : 2 * count]
    residual_ref, rows_ref = refs[2 * count :]
    residual = tokens_ref[...].astype(f32)
    for head_ref, weight_ref in zip(head_refs, weight_refs):
        residual = residual + contract_rows(head_ref[...], weight_ref[...])
    residual_ref[...] = residual
    normed = (normalized(residual) * gain_ref[...][None] + bias_ref[...][None]).astype(bf16)
    rows_ref[...] = jnp.dot(
        dispatch_ref[...], normed, preferred_element_type=f32
    ).astype(bf16)


def middle(rank, tokens, gain, bias, dispatch, heads, weights):
    count, shard = dispatch.shape
    width = tokens.shape[1]
    fixed = lambda array: pl.BlockSpec(array.shape, lambda i, r: (0,) * array.ndim)
    small = [gain, bias, dispatch, *heads, *weights]
    return pl.pallas_call(
        functools.partial(middle_kernel, len(heads)),
        grid_spec=pltpu.PrefetchScalarGridSpec(
            num_scalar_prefetch=1,
            grid=(1,),
            in_specs=[pl.BlockSpec((shard, width), lambda i, r: (r[0], 0))]
            + [fixed(array) for array in small],
            out_specs=(
                pl.BlockSpec((shard, width), lambda i, r: (0, 0)),
                pl.BlockSpec((count, width), lambda i, r: (0, 0)),
            ),
        ),
        out_shape=(
            jax.ShapeDtypeStruct((shard, width), f32),
            jax.ShapeDtypeStruct((count, width), bf16),
        ),
        name="middle",
        compiler_params=pltpu.CompilerParams(vmem_limit_bytes=54 * 2**20),
        cost_estimate=COST,
    )(rank, tokens, *small)


def turn_kernel(
    count, lens_ref, rank_ref, dispatch_ref, back_ref, residual_ref, cotangent_ref,
    gain_ref, *refs
):
    head_refs, weight_refs = refs[:count], refs[count : 2 * count]
    grad_ref, sums_ref, kept_ref, sent_ref = refs[2 * count : 2 * count + 4]
    part_refs = refs[2 * count + 4 :]
    shard = residual_ref.shape[0]
    grad_normed = contract_rows(dispatch_ref[...], back_ref[...])
    values = residual_ref[...]
    centred = values - jnp.mean(values, axis=-1, keepdims=True)
    inverse = lax.rsqrt(jnp.mean(centred * centred, axis=-1, keepdims=True) + EPSILON)
    normed = centred * inverse
    sums_ref[0:1] = jnp.sum(grad_normed * normed, axis=0, keepdims=True)
    sums_ref[1:2] = jnp.sum(grad_normed, axis=0, keepdims=True)
    scaled = grad_normed * gain_ref[...][None]
    grad = cotangent_ref[...].astype(f32) + inverse * (
        scaled
        - jnp.mean(scaled, axis=-1, keepdims=True)
        - normed * jnp.mean(scaled * normed, axis=-1, keepdims=True)
    )
    grad_ref[...] = grad
    low = grad.astype(bf16)
    place = rank_ref[0, 0] * shard + lax.broadcasted_iota(jnp.int32, (1, shard), 1)
    alive = place < item_ends(lens_ref)[-1]
    for weight_ref, part_ref in zip(weight_refs, part_refs):
        part_ref[...] = jnp.where(alive, across(weight_ref[...], low), 0.0).astype(bf16)
    for j, head_ref in enumerate(head_refs):
        made = jnp.dot(head_ref[...], low, preferred_element_type=f32)
        (kept_ref, sent_ref)[j % 2][j // 2] = made.astype(bf16)


def turn(lens, rank, dispatch, back, residual, cotangent, gain, heads, weights):
    shard, width = residual.shape
    cols = weights[0].shape[0]
    count = len(weights)
    return pl.pallas_call(
        functools.partial(turn_kernel, count),
        out_shape=(
            jax.ShapeDtypeStruct((shard, width), f32),
            jax.ShapeDtypeStruct((2, width), f32),
            jax.ShapeDtypeStruct((count // 2, cols, width), bf16),
            jax.ShapeDtypeStruct((count // 2, cols, width), bf16),
        )
        + (jax.ShapeDtypeStruct((cols, shard), bf16),) * count,
        in_specs=[SMEM, SMEM] + [VMEM] * (5 + 2 * count),
        out_specs=(VMEM,) * (4 + count),
        name="turn",
        cost_estimate=COST,
    )(lens, rank, dispatch, back, residual, cotangent, gain, *heads, *weights)


def output_sum_kernel(kept_ref, core_ref, first_ref, near_ref, far_ref):
    cols = near_ref.shape[0]
    total = [
        (kept_ref[j].astype(f32) + core_ref[j].astype(f32)).astype(bf16) for j in range(2)
    ]
    near_ref[...] = total[0]
    far_ref[:cols, :] = total[1]
    far_ref[cols:, :] = first_ref[...]


def output_sums(kept, core, first):
    slots, cols, width = kept.shape
    return pl.pallas_call(
        output_sum_kernel,
        out_shape=(
            jax.ShapeDtypeStruct((cols, width), bf16),
            jax.ShapeDtypeStruct((cols + first.shape[0], width), bf16),
        ),
        in_specs=[VMEM] * 3,
        out_specs=(VMEM, VMEM),
        name="output_sums",
        compiler_params=pltpu.CompilerParams(vmem_limit_bytes=52 * 2**20),
        cost_estimate=LONG,
    )(kept, core, first)


def gelu_parts(values):
    below = 0.5 + 0.5 * lax.erf(values * (0.5**0.5))
    density = jnp.exp(-0.5 * values * values) * (0.5 / jnp.pi) ** 0.5
    return values * below, below + values * density


def part_at(step, parts, rank):
    half = parts // 2
    return (2 * (step % half) + step // half) ^ rank


def activation_kernel(grad_ref, down_ref, out_ref):
    out_ref[...] = across(grad_ref[...], down_ref[...]).astype(bf16)


def activation_grads(grads, down, parts):
    count, width = grads.shape
    hidden = down.shape[0]
    size = hidden // parts
    return pl.pallas_call(
        activation_kernel,
        grid=(parts,),
        out_shape=jax.ShapeDtypeStruct((count, hidden), bf16),
        in_specs=[
            pl.BlockSpec((count, width), lambda i: (0, 0)),
            pl.BlockSpec((size, width), lambda i: (i, 0)),
        ],
        out_specs=pl.BlockSpec((count, size), lambda i: (0, i)),
        name="activation_grads",
        cost_estimate=COST,
    )(grads, down)


def expert_kernel(
    parts, rank_ref, in_ref, grad_act_ref, up_ref,
    act_kept_ref, pre_kept_ref, act_sent_ref, pre_sent_ref, mid_ref,
    grads_ref, ups_ref, acts_ref, pres_ref, sum_ref, fetched, stored,
):
    rank = rank_ref[0, 0]
    size = ups_ref.shape[2]
    half = parts // 2

    def fetch(p):
        cols = rows_at(part_at(p, parts, rank), size)
        return (
            pltpu.make_async_copy(up_ref.at[:, cols], ups_ref.at[p], fetched.at[0, p]),
            pltpu.make_async_copy(grad_act_ref.at[:, cols], grads_ref.at[p], fetched.at[1, p]),
        )

    def store(p, act_out_ref, pre_out_ref):
        cols = rows_at(p % half, size)
        return (
            pltpu.make_async_copy(acts_ref.at[p], act_out_ref.at[:, cols], stored.at[0, p]),
            pltpu.make_async_copy(pres_ref.at[p], pre_out_ref.at[:, cols], stored.at[1, p]),
        )

    for p in range(parts):
        for copy in fetch(p):
            copy.start()
    sum_ref[...] = jnp.zeros_like(sum_ref)

    def part(p, unused):
        for copy in fetch(p):
            copy.wait()
        pre = jnp.dot(in_ref[...], ups_ref[p], preferred_element_type=f32)
        act, slope = gelu_parts(pre)
        acts_ref[p] = act.astype(bf16)
        grad_pre = (grads_ref[p].astype(f32) * slope).astype(bf16)
        pres_ref[p] = grad_pre
        sum_ref[...] += across(grad_pre, ups_ref[p])

        @pl.when(p < half)
        def keep():
            for copy in store(p, act_kept_ref, pre_kept_ref):
                copy.start()

        @pl.when(p >= half)
        def send():
            for copy in store(p, act_sent_ref, pre_sent_ref):
                copy.start()

        return unused

    lax.fori_loop(0, parts, part, 0)
    mid_ref[...] = sum_ref[...].astype(bf16)
    for p in range(parts):
        outs = (act_kept_ref, pre_kept_ref) if p < half else (act_sent_ref, pre_sent_ref)
        for copy in store(p, *outs):
            copy.wait()


def expert(rank, rows, grad_act, up, parts):
    count, width = rows.shape
    hidden = up.shape[1]
    size = hidden // parts
    return pl.pallas_call(
        functools.partial(expert_kernel, parts),
        out_shape=(jax.ShapeDtypeStruct((count, hidden // 2), bf16),) * 4
        + (jax.ShapeDtypeStruct((count, width), bf16),),
        in_specs=[SMEM, VMEM, HBM, HBM],
        out_specs=(HBM,) * 4 + (VMEM,),
        scratch_shapes=[
            pltpu.VMEM((parts, count, size), grad_act.dtype),
            pltpu.VMEM((parts, width, size), bf16),
            pltpu.VMEM((parts, count, size), bf16),
            pltpu.VMEM((parts, count, size), bf16),
            pltpu.VMEM((count, width), f32),
            pltpu.SemaphoreType.DMA((2, parts)),
            pltpu.SemaphoreType.DMA((2, parts)),
        ],
        name="expert",
        compiler_params=pltpu.CompilerParams(vmem_limit_bytes=52 * 2**20),
        cost_estimate=COST,
    )(rank.reshape(1, 1), rows, grad_act, up)


def product_kernel(parts, rank_ref, kept_ref, sent_ref, down_ref, out_ref,
                   acts_ref, downs_ref, sum_ref, fetched):
    rank = rank_ref[0, 0]
    size = downs_ref.shape[1]
    half = parts // 2

    def fetch(p):
        rows = rows_at(part_at(p, parts, rank), size)
        source = kept_ref if p < half else sent_ref
        cols = slice((p % half) * size, (p % half + 1) * size)
        return (
            pltpu.make_async_copy(down_ref.at[rows, :], downs_ref.at[p], fetched.at[0, p]),
            pltpu.make_async_copy(source.at[:, cols], acts_ref.at[p], fetched.at[1, p]),
        )

    for p in range(parts):
        for copy in fetch(p):
            copy.start()
    sum_ref[...] = jnp.zeros_like(sum_ref)
    for p in range(parts):
        for copy in fetch(p):
            copy.wait()
        sum_ref[...] += jnp.dot(acts_ref[p], downs_ref[p], preferred_element_type=f32)
    out_ref[...] = sum_ref[...].astype(bf16)


def product(rank, kept, sent, down, parts):
    count = kept.shape[0]
    hidden, width = down.shape
    size = hidden // parts
    return pl.pallas_call(
        functools.partial(product_kernel, parts),
        out_shape=jax.ShapeDtypeStruct((count, width), bf16),
        in_specs=[SMEM, HBM, HBM, HBM],
        out_specs=VMEM,
        scratch_shapes=[
            pltpu.VMEM((parts, count, size), bf16),
            pltpu.VMEM((parts, size, width), bf16),
            pltpu.VMEM((count, width), f32),
            pltpu.SemaphoreType.DMA((2, parts)),
        ],
        name="product",
        compiler_params=pltpu.CompilerParams(vmem_limit_bytes=54 * 2**20),
        cost_estimate=COST,
    )(rank.reshape(1, 1), kept, sent, down)


def group_sums(refs, groups):
    dup = ddown = 0.0
    for g in range(groups):
        in_ref, grad_ref, act_ref, pre_ref = refs[4 * g : 4 * g + 4]
        dup = dup + contract_rows(in_ref[...], pre_ref[...])
        ddown = ddown + contract_rows(act_ref[...], grad_ref[...])
    return dup, ddown


def group_specs(groups, part):
    count, width = groups[0][0].shape
    size = groups[0][2].shape[1] // 2
    fixed = pl.BlockSpec((count, width), lambda i: (0, 0))
    columns = pl.BlockSpec((count, size), lambda i: (0, part))
    return [fixed, fixed, columns, columns] * len(groups)


def far_weight_kernel(groups, *refs):
    first_ref, rest_ref = refs[-2:]
    dup, ddown = group_sums(refs, groups)
    cut = first_ref.shape[0]
    first_ref[...] = dup[:cut].astype(bf16)
    rest_ref[: dup.shape[0] - cut, :] = dup[cut:].astype(bf16)
    rest_ref[dup.shape[0] - cut :, :] = ddown.astype(bf16)


def far_weights(groups):
    width = groups[0][0].shape[1]
    size = groups[0][2].shape[1] // 2
    cut = (width + size) // 4
    shapes = ((cut, size), (width + size - cut, size))
    return pl.pallas_call(
        functools.partial(far_weight_kernel, len(groups)),
        grid=(1,),
        in_specs=group_specs(groups, 1),
        out_specs=tuple(pl.BlockSpec(shape, lambda i: (0, 0)) for shape in shapes),
        out_shape=tuple(jax.ShapeDtypeStruct(shape, bf16) for shape in shapes),
        name="far_weights",
        compiler_params=pltpu.CompilerParams(vmem_limit_bytes=52 * 2**20),
        cost_estimate=COST,
    )(*[values for group in groups for values in group])


def near_weight_kernel(groups, skip, *refs):
    first_ref, rest_ref, up_ref, down_ref = refs[-4:]
    dup, ddown = group_sums(refs, groups)
    cut = first_ref.shape[0] - skip
    down_at = dup.shape[0] - cut
    up_ref[:cut, :] = dup[:cut] + first_ref[skip:, :].astype(f32)
    up_ref[cut:, :] = dup[cut:] + rest_ref[:down_at, :].astype(f32)
    down_ref[...] = ddown + rest_ref[down_at:, :].astype(f32)


def near_weights(groups, first, rest):
    width = groups[0][0].shape[1]
    size = groups[0][2].shape[1] // 2
    skip = first.shape[0] + rest.shape[0] - width - size
    whole = lambda shape: pl.BlockSpec(shape, lambda i: (0, 0))
    return pl.pallas_call(
        functools.partial(near_weight_kernel, len(groups), skip),
        grid=(1,),
        in_specs=group_specs(groups, 0) + [whole(first.shape), whole(rest.shape)],
        out_specs=(whole((width, size)), whole((size, width))),
        out_shape=(
            jax.ShapeDtypeStruct((width, size), f32),
            jax.ShapeDtypeStruct((size, width), f32),
        ),
        name="near_weights",
        compiler_params=pltpu.CompilerParams(vmem_limit_bytes=52 * 2**20),
        cost_estimate=COST,
    )(*[values for group in groups for values in group], first, rest)


def input_grad_kernel(groups, qw_ref, kw_ref, vw_ref, *refs):
    joint_refs = refs[: len(groups)]
    kept_ref, sent_ref, turned_ref = refs[len(groups) :]
    step = pl.program_id(0)

    @pl.when(step == 0)
    def stack():
        start = 0
        for first_head, heads in groups:
            for at, weight_ref, first, size in stacked_parts(
                first_head, heads, qw_ref, kw_ref, vw_ref
            ):
                turned_ref[start + at : start + at + size, :] = weight_ref[
                    first : first + size, :
                ]
            start += 3 * heads * HEAD_DIM

    total = 0.0
    at = 0
    for joint_ref in joint_refs:
        rows = slice(at, at + joint_ref.shape[1])
        total = total + jnp.dot(
            joint_ref[...], turned_ref[rows, :], preferred_element_type=f32
        )
        at += joint_ref.shape[1]

    @pl.when(step % 2 == 0)
    def keep():
        kept_ref[0] = total.astype(bf16)

    @pl.when(step % 2 == 1)
    def send():
        sent_ref[0] = total.astype(bf16)


def input_grad(groups, weights, joints, first, count, size):
    cols, width = weights[0].shape
    fixed = pl.BlockSpec((cols, width), lambda i: (0, 0))
    return pl.pallas_call(
        functools.partial(input_grad_kernel, groups),
        grid=(count,),
        out_shape=(jax.ShapeDtypeStruct((count // 2, size, width), bf16),) * 2,
        in_specs=[fixed] * 3
        + [
            pl.BlockSpec((size, joint.shape[1]), lambda i: (first + i, 0))
            for joint in joints
        ],
        out_specs=(pl.BlockSpec((1, size, width), lambda i: (i // 2, 0, 0)),) * 2,
        scratch_shapes=[pltpu.VMEM((3 * cols, width), bf16)],
        name="input_grad",
        compiler_params=pltpu.CompilerParams(vmem_limit_bytes=10 * 2**20),
        cost_estimate=COST,
    )(*weights, *joints)


def close_kernel(
    rank_ref, tokens_ref, gain_ref, grad_ref, residual_ref, dispatch_ref, back_ref, *refs
):
    *part_refs, out_ref, block_ref = refs
    block_ref[...] = residual_ref[...] + contract_rows(dispatch_ref[...], back_ref[...])
    grad_in = 0.0
    for part_ref in part_refs:
        grad_in = grad_in + part_ref[...].reshape(out_ref.shape).astype(f32)
    values = tokens_ref[...].astype(f32)
    centred = values - jnp.mean(values, axis=-1, keepdims=True)
    inverse = lax.rsqrt(jnp.mean(centred * centred, axis=-1, keepdims=True) + EPSILON)
    normed = centred * inverse
    scaled = grad_in * gain_ref[...][None]
    out_ref[...] = grad_ref[...] + inverse * (
        scaled
        - jnp.mean(scaled, axis=-1, keepdims=True)
        - normed * jnp.mean(scaled * normed, axis=-1, keepdims=True)
    )


def close(rank, tokens, gain, grad, residual, dispatch, back, parts):
    shard, width = grad.shape
    count = dispatch.shape[0]
    size = shard // 2
    rows = pl.BlockSpec((size, width), lambda i, r: (i, 0))
    return pl.pallas_call(
        close_kernel,
        grid_spec=pltpu.PrefetchScalarGridSpec(
            num_scalar_prefetch=1,
            grid=(2,),
            in_specs=[
                pl.BlockSpec((size, width), lambda i, r: (2 * r[0] + i, 0)),
                pl.BlockSpec((width,), lambda i, r: (0,)),
                rows,
                rows,
                pl.BlockSpec((count, size), lambda i, r: (0, i)),
                pl.BlockSpec((count, width), lambda i, r: (0, 0)),
            ]
            + [pl.BlockSpec((1, size, width), lambda i, r: (0, i, 0))] * len(parts),
            out_specs=(rows, rows),
        ),
        out_shape=(jax.ShapeDtypeStruct((shard, width), f32),) * 2,
        name="close",
        compiler_params=pltpu.CompilerParams(vmem_limit_bytes=16 * 2**20),
        cost_estimate=COST,
    )(rank, tokens, gain, grad, residual, dispatch, back, *parts)


def add_low_kernel(a_ref, b_ref, out_ref):
    out_ref[...] = (a_ref[...].astype(f32) + b_ref[...].astype(f32)).astype(bf16)


def add_low(a, b):
    block = pl.BlockSpec(a.shape, lambda i: (0,) * a.ndim)
    return pl.pallas_call(
        add_low_kernel,
        grid=(1,),
        out_shape=jax.ShapeDtypeStruct(a.shape, bf16),
        in_specs=[block, block],
        out_specs=block,
        name="add_low",
        compiler_params=pltpu.CompilerParams(vmem_limit_bytes=6 * 2**20),
        cost_estimate=COST,
    )(a, b)


def after(value, *others):
    return lax.optimization_barrier((value, *others))[0]


def tie(*values):
    return lax.optimization_barrier(values)


def finish_kernel(groups, bit_ref, *refs):
    pieces, refs = refs[: 2 * len(groups)], refs[2 * len(groups) :]
    query_ref, key_ref, value_ref = refs[:3]
    bit = bit_ref[0, 0]
    for g, ((first_head, heads), whole_ref) in enumerate(zip(groups, refs[3:])):
        half = whole_ref.shape[0] // 2
        for piece_ref, at in ((pieces[2 * g], bit), (pieces[2 * g + 1], 1 - bit)):
            whole_ref[rows_at(at, half), :] = piece_ref[0:half, :].astype(f32)
        for at, target_ref, first, size in stacked_parts(
            first_head, heads, query_ref, key_ref, value_ref
        ):
            target_ref[first : first + size, :] = whole_ref[at : at + size, :]


def finish(groups, bit, pieces):
    width = pieces[0].shape[1]
    cols = sum(heads for first_head, heads in groups) * HEAD_DIM
    return pl.pallas_call(
        functools.partial(finish_kernel, groups),
        out_shape=(jax.ShapeDtypeStruct((cols, width), f32),) * 3,
        in_specs=[SMEM] + [VMEM] * len(pieces),
        out_specs=(VMEM,) * 3,
        scratch_shapes=[
            pltpu.VMEM((3 * heads * HEAD_DIM, width), f32) for first_head, heads in groups
        ],
        name="finish",
        compiler_params=pltpu.CompilerParams(vmem_limit_bytes=10 * 2**20),
        cost_estimate=COST,
    )(bit, *pieces)


def on_device(
    tokens,
    first_gain,
    first_bias,
    query_weight,
    key_weight,
    value_weight,
    output_weight,
    second_gain,
    second_bias,
    expert_up,
    expert_down,
    item_lengths,
    routes,
    slot_order,
    cotangent,
):
    slots_all, width = tokens.shape
    members = lax.axis_size("tensor")
    shard_rows = slots_all // members
    rank = lax.axis_index("tensor")
    sources = lax.axis_size("dp")
    experts_all = sources * expert_up.shape[0]
    capacity = shard_rows // experts_all
    head_cols = query_weight.shape[1]
    heads = head_cols // HEAD_DIM
    up_matrix = expert_up[0]
    down_matrix = expert_down[0]
    rank_cell = rank.astype(jnp.int32).reshape(1, 1)

    def exchange(rows):
        return lax.all_to_all(
            rows.reshape(sources, -1, width), "dp", split_axis=0, concat_axis=0, tiled=True
        ).reshape(-1, width)

    qw, kw, vw = query_weight.T, key_weight.T, value_weight.T

    dispatch, grad_slots = plan(
        item_lengths, rank_cell, routes, slot_order, cotangent, capacity, experts_all
    )
    flat_grad = exchange(grad_slots)
    tokens, grad_slots = tie(tokens, grad_slots)
    normed_in, qt, kt, vt = project(
        rank_cell[0], tokens, first_gain, first_bias, qw, kw, vw, members
    )
    outputs = [output_weight] + [
        swap(output_weight, "tensor", k) for k in range(1, members)
    ]
    far = members // 2
    *far_heads, far_logs = attend(
        item_lengths, rank_cell, qt, kt, vt, members, far, members - far
    )
    far_heads, kt = tie(far_heads, kt)
    far_arrived = [swap(far_heads[j - far], "tensor", j) for j in range(far, members)]
    *near_heads, near_logs = attend(item_lengths, rank_cell, qt, kt, vt, members, 0, far)
    near_heads, far_arrived, outputs = tie(near_heads, far_arrived, outputs)
    own_heads = near_heads + far_heads
    logs = (near_logs, far_logs)
    all_heads = (
        near_heads[:1]
        + [swap(near_heads[j], "tensor", j) for j in range(1, far)]
        + far_arrived
    )
    residual, outgoing = middle(
        rank_cell[0], tokens, second_gain, second_bias, dispatch, all_heads, outputs
    )
    flat_in = exchange(outgoing)

    flat_grad, outgoing = tie(flat_grad, outgoing)
    grad_act = activation_grads(flat_grad, down_matrix, members)
    near_grads = swap(flat_grad, "tensor", 1)
    flat_in, grad_act, near_grads = tie(flat_in, grad_act, near_grads)
    near_rows = swap(flat_in, "tensor", 1)
    act, grad_pre, act_sent, pre_sent, grad_mid = expert(
        rank_cell[0], flat_in, grad_act, up_matrix, members
    )
    grad_mid, act, near_rows = tie(grad_mid, act, near_rows)
    grad_back = exchange(grad_mid)

    act, act_sent, pre_sent, grad_mid = tie(act, act_sent, pre_sent, grad_mid)
    near_act = swap(act_sent, "tensor", 1)
    near_pre = swap(pre_sent, "tensor", 1)
    made = product(rank_cell[0], act, act_sent, down_matrix, members)
    made, near_act, near_pre = tie(made, near_act, near_pre)
    expert_groups = [
        (flat_in, flat_grad, act, grad_pre), (near_rows, near_grads, near_act, near_pre)
    ]
    expert_far = list(far_weights(expert_groups))
    grad_back, made, expert_far = tie(grad_back, made, expert_far)

    steps = steps_of(members)
    grad_res, sums_second, kept, sent, *grad_heads = turn(
        item_lengths, rank_cell, dispatch, grad_back, residual, cotangent,
        second_gain, all_heads, outputs,
    )
    grad_parts = [grad_heads[0]] + [
        swap(grad_heads[j], "tensor", j) for j in range(1, members)
    ]
    output_near, output_far = output_sums(kept, swap(sent, "tensor", 1), expert_far[0])
    made, grad_heads = tie(made, grad_heads)
    returned = exchange(made)
    grad_parts, output_near, output_far = tie(grad_parts, output_near, output_far)

    bit_cell = (lax.axis_index("dp") & 1).astype(jnp.int32).reshape(1, 1)
    weights = (qw, kw, vw)
    dp_steps = steps_of(sources)
    back = functools.partial(
        attend_back, lens=item_lengths, rank=rank_cell, bit=bit_cell, qt=qt, kt=kt, vt=vt,
        logs=logs, weights=weights, normed=normed_in, outs=own_heads,
    )
    groups = ((0, heads - 1), (heads - 1, 1))
    joint_a, sums_a, own_a, away_a = back(*groups[0], extras=(), grads=grad_parts)
    output_got = swap(output_far, "tensor", 2)
    joint_a, own_a, away_a, output_got, grad_parts, expert_rest, returned = tie(
        joint_a, own_a, away_a, output_got, grad_parts, expert_far[1], returned
    )
    expert_got = swap(expert_rest, "tensor", 2)
    output_sum = add_low(output_near, output_got)
    own_a = add_low(own_a, swap(away_a, "dp", 1))
    output_sum = add_low(output_sum, swap(output_sum, "dp", dp_steps[-1]))
    joint_b, unused, own_b, away_b = back(
        *groups[1], extras=(sums_a, sums_second), grads=grad_parts
    )
    joint_b, own_a, own_b, away_b, output_sum = tie(
        joint_b, own_a, own_b, away_b, output_sum
    )

    far_kept, far_sent = input_grad(
        groups, weights, (joint_a, joint_b), far, members - far, shard_rows
    )
    got_a = swap(own_a, "dp", dp_steps[1])
    got_b = swap(away_b, "dp", 1)
    joint_b, got_a, got_b = tie(joint_b, got_a, got_b)
    near_kept, near_sent = input_grad(
        groups, weights, (joint_a, joint_b), 0, far, shard_rows
    )
    own_b = add_parts(own_b, got_b)
    far_kept = add_low(far_kept, swap(far_sent, "tensor", 1))
    own_a = add_low(own_a, got_a)
    far_kept, own_b, output_sum, own_a = tie(far_kept, own_b, output_sum, own_a)
    near_core = swap(near_sent, "tensor", 1)
    near_far = swap(far_kept, "tensor", 2)
    for step in dp_steps[1:]:
        if step != dp_steps[1]:
            own_a = add_low(own_a, swap(own_a, "dp", step))
        own_b = add_parts(own_b, swap(own_b, "dp", step))
        if step == dp_steps[1]:
            own_b, expert_got = tie(own_b, expert_got)
    up_grad, down_grad = near_weights(expert_groups, output_got, expert_got)
    own_b, up_grad, down_grad, near_far = tie(own_b, up_grad, down_grad, near_far)
    pieces = (own_a, swap(own_a, "dp", 1), own_b, swap(own_b, "dp", 1))
    token_grad, block_out = close(
        rank_cell[0], tokens, first_gain, grad_res, residual, dispatch, returned,
        (near_kept, near_core, near_far),
    )
    norm_sums = own_b[-SUM_ROWS:].astype(f32)
    norm_sums = norm_sums[: SUM_ROWS // 2] + norm_sums[SUM_ROWS // 2 :]
    for step in steps:
        norm_sums = norm_sums + swap(norm_sums, "tensor", step)
    for step in dp_steps[:-1]:
        output_sum = add_low(output_sum, swap(output_sum, "dp", step))
    output_sum = after(output_sum, token_grad)
    query_grad, key_grad, value_grad = finish(groups, bit_cell, pieces)
    return (
        block_out,
        token_grad,
        (norm_sums[0] - first_bias * norm_sums[1]) / first_gain,
        norm_sums[1],
        query_grad.T,
        key_grad.T,
        value_grad.T,
        output_sum.astype(f32),
        norm_sums[2],
        norm_sums[3],
        up_grad[None],
        down_grad[None],
    )


def solution(mesh):
    in_specs = (
        P("dp", None),
        P(),
        P(),
        P(None, "tensor"),
        P(None, "tensor"),
        P(None, "tensor"),
        P("tensor", None),
        P(),
        P(),
        P("dp", None, None),
        P("dp", None, None),
        P("dp", None),
        P(("dp", "tensor"), None),
        P(("dp", "tensor"), None),
        P(("dp", "tensor"), None),
    )
    out_specs = (
        P(("dp", "tensor"), None),
        P(("dp", "tensor"), None),
        P(),
        P(),
        P(None, "tensor"),
        P(None, "tensor"),
        P(None, "tensor"),
        P("tensor", None),
        P(),
        P(),
        P("dp", None, "tensor"),
        P("dp", "tensor", None),
    )
    return jax.shard_map(
        on_device, mesh=mesh, in_specs=in_specs, out_specs=out_specs, check_vma=False
    )
```
